32 devices in a mesh: ctx: 8 (over y, x, core), sp: 4 (over z).
Axes of the slice: x: 2, y: 2, z: 4, core: 2. Of those that a mesh axis runs over, the one named last changes fastest.
Arguments:
- enc_in: bfloat16 [2048, 768], P(('ctx', 'sp')), may hold values from -6 to 6
- dec_in: bfloat16 [2048, 768], P(('ctx', 'sp')), may hold values from -6 to 6
- enc_cot: bfloat16 [2048, 768], P(('ctx', 'sp')), may hold values from -6 to 6
- dec_cot: bfloat16 [2048, 768], P(('ctx', 'sp')), may hold values from -6 to 6
- enc_segments: int32 [2048], replicated, may hold values from 0 to 15, as said below
- dec_segments: int32 [2048], replicated, may hold values from 0 to 15, as said below
- buckets: int32 [2, 257], replicated, may hold values from 0 to 31
- enc_norm1: bfloat16 [768], P('ctx'), may hold values from 0.5 to 1.5
- enc_query: bfloat16 [768, 768], P('ctx'), may hold values from -0.0546875 to 0.0546875
- enc_key: bfloat16 [768, 768], P('ctx'), may hold values from -0.21875 to 0.21875
- enc_value: bfloat16 [768, 768], P('ctx'), may hold values from -0.21875 to 0.21875
- enc_proj: bfloat16 [768, 768], P('ctx'), may hold values from -3 to 3
- enc_rel: bfloat16 [384], P('ctx'), may hold values from -4 to 4
- enc_norm2: bfloat16 [768], P('ctx'), may hold values from 0.5 to 1.5
- enc_gate: bfloat16 [768, 2048], P('ctx'), may hold values from -0.21875 to 0.21875
- enc_up: bfloat16 [768, 2048], P('ctx'), may hold values from -0.21875 to 0.21875
- enc_down: bfloat16 [2048, 768], P('ctx'), may hold values from -0.125 to 0.125
- enc_final: bfloat16 [768], P('ctx'), may hold values from 0.5 to 1.5
- dec_norm1: bfloat16 [768], P('ctx'), may hold values from 0.5 to 1.5
- dec_query: bfloat16 [768, 768], P('ctx'), may hold values from -0.0546875 to 0.0546875
- dec_key: bfloat16 [768, 768], P('ctx'), may hold values from -0.21875 to 0.21875
- dec_value: bfloat16 [768, 768], P('ctx'), may hold values from -0.21875 to 0.21875
- dec_proj: bfloat16 [768, 768], P('ctx'), may hold values from -3 to 3
- dec_rel: bfloat16 [384], P('ctx'), may hold values from -4 to 4
- dec_norm2: bfloat16 [768], P('ctx'), may hold values from 0.5 to 1.5
- cross_query: bfloat16 [768, 768], P('ctx'), may hold values from -0.0546875 to 0.0546875
- cross_key: bfloat16 [768, 768], P('ctx'), may hold values from -0.21875 to 0.21875
- cross_value: bfloat16 [768, 768], P('ctx'), may hold values from -0.21875 to 0.21875
- cross_proj: bfloat16 [768, 768], P('ctx'), may hold values from -3 to 3
- dec_norm3: bfloat16 [768], P('ctx'), may hold values from 0.5 to 1.5
- dec_gate: bfloat16 [768, 2048], P('ctx'), may hold values from -0.21875 to 0.21875
- dec_up: bfloat16 [768, 2048], P('ctx'), may hold values from -0.21875 to 0.21875
- dec_down: bfloat16 [2048, 768], P('ctx'), may hold values from -0.125 to 0.125
Outputs:
- enc_out: float32 [2048, 768], P(('ctx', 'sp'))
- dec_out: float32 [2048, 768], P(('ctx', 'sp'))
- enc_in_grad: float32 [2048, 768], P(('ctx', 'sp'))
- dec_in_grad: float32 [2048, 768], P(('ctx', 'sp'))
- enc_norm1_grad: float32 [768], P('ctx')
- enc_query_grad: float32 [768, 768], P('ctx')
- enc_key_grad: float32 [768, 768], P('ctx')
- enc_value_grad: float32 [768, 768], P('ctx')
- enc_proj_grad: float32 [768, 768], P('ctx')
- enc_rel_grad: float32 [384], P('ctx')
- enc_norm2_grad: float32 [768], P('ctx')
- enc_gate_grad: float32 [768, 2048], P('ctx')
- enc_up_grad: float32 [768, 2048], P('ctx')
- enc_down_grad: float32 [2048, 768], P('ctx')
- enc_final_grad: float32 [768], P('ctx')
- dec_norm1_grad: float32 [768], P('ctx')
- dec_query_grad: float32 [768, 768], P('ctx')
- dec_key_grad: float32 [768, 768], P('ctx')
- dec_value_grad: float32 [768, 768], P('ctx')
- dec_proj_grad: float32 [768, 768], P('ctx')
- dec_rel_grad: float32 [384], P('ctx')
- dec_norm2_grad: float32 [768], P('ctx')
- cross_query_grad: float32 [768, 768], P('ctx')
- cross_key_grad: float32 [768, 768], P('ctx')
- cross_value_grad: float32 [768, 768], P('ctx')
- cross_proj_grad: float32 [768, 768], P('ctx')
- dec_norm3_grad: float32 [768], P('ctx')
- dec_gate_grad: float32 [768, 2048], P('ctx')
- dec_up_grad: float32 [768, 2048], P('ctx')
- dec_down_grad: float32 [2048, 768], P('ctx')
The draws below stay inside these ranges and needn't reach their ends.
Inputs may be any that keep to these rules, and one draw needn't show every extreme that they name: `enc_segments`: numbers never fall along a sequence and every number from 0 to 15 labels a nonempty document; one document starts within the first 256 tokens and ends within the last 256 tokens, and every other lies within the first or the last 256 tokens. `dec_segments`: as for enc_segments; a decoder token attends to the encoder tokens of the same number.
All inputs are finite; a program needn't handle non-finite values.
Results may differ from the reference program's by a relative error of at most 0.04.
Values may be sent and summed in bfloat16 or wider, within the bound.
A program may use at most 576 MiB of HBM per device.

```python
import math
import jax
import jax.numpy as jnp
from jax import lax

D = 768
HEADS = 12
HD = 64
FF = 2048
NB = 32
MAXD = 128
DOCS = 16
SEQ = 2048
CH = 256


def document_ids(key):
    positions = jnp.arange(SEQ, dtype=jnp.int32)
    inside = (positions >= 1) & (positions < CH) | (positions > SEQ - CH)
    weights = jax.random.randint(key, (SEQ,), 1, 4096, dtype=jnp.int32)
    scores = jnp.where(inside, weights * SEQ + positions, -1 - positions)
    chosen = lax.top_k(scores, DOCS - 1)[1]
    flags = jnp.zeros((SEQ,), jnp.int32).at[chosen].set(1)
    return jnp.cumsum(flags).astype(jnp.int32)


def draw_enc_segments(key, part):
    return document_ids(jax.random.fold_in(key, 17))


def draw_dec_segments(key, part):
    return document_ids(jax.random.fold_in(key, 23))


def plant(array, stream_key, least, high):
    extent = array.shape
    index_at = [jax.random.randint(jax.random.fold_in(stream_key, axis), (), 0, extent[axis]) for axis in range(len(extent))]
    array = array.at[tuple(index_at)].set(least)
    longest = extent.index(max(extent))
    index_at[longest] = (index_at[longest] + 1) % extent[longest]
    return array.at[tuple(index_at)].set(high)


def block_scale(key, shape, pieces, low, largest):
    level, own = 1.0, jax.random.fold_in(key, 6)
    for axis_at, blocks in pieces:
        draws = jnp.exp(jax.random.uniform(jax.random.fold_in(own, axis_at), (blocks,), jnp.float32, low / len(pieces), largest / len(pieces)))
        level = level * jnp.repeat(draws, shape[axis_at] // blocks).reshape([-1 if axis == axis_at else 1 for axis in range(len(shape))])
    return level


def gaussian(rng, extent, spread, most, split=(), held_as=jnp.bfloat16):
    entries = jax.random.normal(rng, extent, jnp.float32) * spread
    if len(split) > 0:
        entries = block_scale(rng, extent, split, -0.22, 0.18) * entries
    return jnp.clip(entries, min=-most, max=most).astype(held_as)


def setup_inputs(seed: int = 0) -> dict:
    keys = jax.random.split(jax.random.key(seed), 34)
    enc_in = gaussian(keys[0], (SEQ, D), 1.0, 6.0, ((0, 32),))
    dec_in = gaussian(keys[1], (SEQ, D), 1.0, 6.0, ((0, 32),))
    enc_cot = gaussian(keys[2], (SEQ, D), 1.0, 6.0, ((0, 32),))
    dec_cot = gaussian(keys[3], (SEQ, D), 1.0, 6.0, ((0, 32),))
    enc_segments = draw_enc_segments(jax.random.fold_in(keys[33], 71), 0)
    dec_segments = draw_dec_segments(jax.random.fold_in(keys[33], 71), 0)
    buckets = plant(jax.random.randint(keys[6], (2, 2 * MAXD + 1), 0, NB), jax.random.fold_in(keys[6], 1), 0, NB - 1).astype(jnp.int32)
    enc_norm1 = jnp.clip(1.0 + 0.1 * jax.random.normal(keys[7], (D,), jnp.float32), 0.5, 1.5).astype(jnp.bfloat16)
    enc_query = gaussian(keys[8], (D, D), (16 * D) ** -0.5, 0.0546875, ((0, 8),))
    enc_key = gaussian(keys[9], (D, D), D ** -0.5, 0.21875, ((0, 8),))
    enc_value = gaussian(keys[10], (D, D), D ** -0.5, 0.21875, ((0, 8),))
    enc_proj = gaussian(keys[11], (D, D), 4 ** -0.5, 3.0, ((0, 8),))
    enc_rel = gaussian(keys[12], (NB * HEADS,), 1.0, 4.0, ((0, 8),))
    enc_norm2 = jnp.clip(1.0 + 0.1 * jax.random.normal(keys[13], (D,), jnp.float32), 0.5, 1.5).astype(jnp.bfloat16)
    enc_gate = gaussian(keys[14], (D, FF), D ** -0.5, 0.21875, ((0, 8),))
    enc_up = gaussian(keys[15], (D, FF), D ** -0.5, 0.21875, ((0, 8),))
    enc_down = gaussian(keys[16], (FF, D), FF ** -0.5, 0.125, ((0, 8),))
    enc_final = jnp.clip(1.0 + 0.1 * jax.random.normal(keys[17], (D,), jnp.float32), 0.5, 1.5).astype(jnp.bfloat16)
    dec_norm1 = jnp.clip(1.0 + 0.1 * jax.random.normal(keys[18], (D,), jnp.float32), 0.5, 1.5).astype(jnp.bfloat16)
    dec_query = gaussian(keys[19], (D, D), (16 * D) ** -0.5, 0.0546875, ((0, 8),))
    dec_key = gaussian(keys[20], (D, D), D ** -0.5, 0.21875, ((0, 8),))
    dec_value = gaussian(keys[21], (D, D), D ** -0.5, 0.21875, ((0, 8),))
    dec_proj = gaussian(keys[22], (D, D), 4 ** -0.5, 3.0, ((0, 8),))
    dec_rel = gaussian(keys[23], (NB * HEADS,), 1.0, 4.0, ((0, 8),))
    dec_norm2 = jnp.clip(1.0 + 0.1 * jax.random.normal(keys[24], (D,), jnp.float32), 0.5, 1.5).astype(jnp.bfloat16)
    cross_query = gaussian(keys[25], (D, D), (16 * D) ** -0.5, 0.0546875, ((0, 8),))
    cross_key = gaussian(keys[26], (D, D), D ** -0.5, 0.21875, ((0, 8),))
    cross_value = gaussian(keys[27], (D, D), D ** -0.5, 0.21875, ((0, 8),))
    cross_proj = gaussian(keys[28], (D, D), 4 ** -0.5, 3.0, ((0, 8),))
    dec_norm3 = jnp.clip(1.0 + 0.1 * jax.random.normal(keys[29], (D,), jnp.float32), 0.5, 1.5).astype(jnp.bfloat16)
    dec_gate = gaussian(keys[30], (D, FF), D ** -0.5, 0.21875, ((0, 8),))
    dec_up = gaussian(keys[31], (D, FF), D ** -0.5, 0.21875, ((0, 8),))
    dec_down = gaussian(keys[32], (FF, D), FF ** -0.5, 0.125, ((0, 8),))
    return dict(enc_in=enc_in, dec_in=dec_in, enc_cot=enc_cot, dec_cot=dec_cot, enc_segments=enc_segments, dec_segments=dec_segments, buckets=buckets, enc_norm1=enc_norm1, enc_query=enc_query, enc_key=enc_key, enc_value=enc_value, enc_proj=enc_proj, enc_rel=enc_rel, enc_norm2=enc_norm2, enc_gate=enc_gate, enc_up=enc_up, enc_down=enc_down, enc_final=enc_final, dec_norm1=dec_norm1, dec_query=dec_query, dec_key=dec_key, dec_value=dec_value, dec_proj=dec_proj, dec_rel=dec_rel, dec_norm2=dec_norm2, cross_query=cross_query, cross_key=cross_key, cross_value=cross_value, cross_proj=cross_proj, dec_norm3=dec_norm3, dec_gate=dec_gate, dec_up=dec_up, dec_down=dec_down)


EPSILON = 1e-06
NEGATIVE = -1e+30
HIGHEST = lax.Precision.HIGHEST

@jax.custom_vjp
def low(v):
    return lax.optimization_barrier(v.astype(jnp.bfloat16)).astype(jnp.float32)

@jax.custom_vjp
def low_back(v):
    return v

def low_keep(v):
    return (low(v), None)

def low_pass(kept, grad):
    return (grad,)

def back_keep(v):
    return (v, None)

def back_low(kept, grad):
    return (low(grad),)
low.defvjp(low_keep, low_pass)
low_back.defvjp(back_keep, back_low)

def matmul(left, right):
    return jnp.dot(left, right, precision=HIGHEST)

def rms_norm(values, norm_gain):
    return values * lax.rsqrt(lax.optimization_barrier(jnp.mean(values * values, axis=-1, keepdims=True)) + EPSILON) * norm_gain

def bias_table(relative, table_row):
    return relative.reshape(NB, HEADS)[table_row].T

def attend(query_proj, key_proj, value_proj, query_ids, key_ids, head_bias, causal):
    length = query_proj.shape[0]
    key_len = key_proj.shape[0]
    heads_q = query_proj.reshape(length, HEADS, HD)
    heads_k = key_proj.reshape(key_len, HEADS, HD)
    heads_v = value_proj.reshape(key_len, HEADS, HD)
    block_rows = math.gcd(512, length)
    col_ids = jnp.arange(key_len, dtype=jnp.int32)

    def one_block(offset):
        rows_q = lax.dynamic_slice_in_dim(heads_q, offset, block_rows, 0)
        row_ids = offset + jnp.arange(block_rows, dtype=jnp.int32)
        ids_q = lax.dynamic_slice_in_dim(query_ids, offset, block_rows, 0)
        scores = jnp.einsum('qhd,khd->hqk', rows_q, heads_k, precision=HIGHEST)
        allowed = ids_q[:, None] == key_ids[None, :]
        if causal:
            allowed = allowed & (col_ids[None, :] <= row_ids[:, None])
        if head_bias is not None:
            where_at = jnp.clip(col_ids[None, :] - row_ids[:, None], -MAXD, MAXD) + MAXD
            scores = scores + jnp.take(head_bias, where_at, axis=1)
        scores = low_back(scores)
        scores = jnp.where(allowed[None], scores, NEGATIVE)
        probabilities = low(jax.nn.softmax(scores, axis=-1))
        return jnp.einsum('hqk,khd->qhd', probabilities, heads_v, precision=HIGHEST)
    offsets = jnp.arange(length // block_rows, dtype=jnp.int32) * block_rows
    results = lax.map(jax.checkpoint(one_block), offsets)
    return results.reshape(length, HEADS * HD)

def heads_of(normed, weight):
    return low(low_back(matmul(normed, weight)))

def attention_block(residual, source, norm_gain, w_query, w_key, w_value, w_proj, query_ids, key_ids, head_bias, causal):
    normed = low(rms_norm(residual, norm_gain))
    kv_input = normed if source is None else source
    query_proj = heads_of(normed, w_query)
    key_proj = heads_of(kv_input, w_key)
    value_proj = heads_of(kv_input, w_value)
    mixed_heads = low(low_back(attend(query_proj, key_proj, value_proj, query_ids, key_ids, head_bias, causal)))
    return residual + low_back(matmul(mixed_heads, w_proj))

def feed_forward(residual, norm_gain, w_gate, w_up, w_down):
    normed = low(rms_norm(residual, norm_gain))
    gate_val = low_back(matmul(normed, w_gate))
    up_val = low_back(matmul(normed, w_up))
    hidden = low(jax.nn.gelu(gate_val, approximate=True) * up_val)
    return residual + low_back(matmul(hidden, w_down))

def reference(enc_in, dec_in, enc_cot, dec_cot, enc_segments, dec_segments, buckets, enc_norm1, enc_query, enc_key, enc_value, enc_proj, enc_rel, enc_norm2, enc_gate, enc_up, enc_down, enc_final, dec_norm1, dec_query, dec_key, dec_value, dec_proj, dec_rel, dec_norm2, cross_query, cross_key, cross_value, cross_proj, dec_norm3, dec_gate, dec_up, dec_down):
    weights = (enc_norm1, enc_query, enc_key, enc_value, enc_proj, enc_rel, enc_norm2, enc_gate, enc_up, enc_down, enc_final, dec_norm1, dec_query, dec_key, dec_value, dec_proj, dec_rel, dec_norm2, cross_query, cross_key, cross_value, cross_proj, dec_norm3, dec_gate, dec_up, dec_down)
    weights = tuple((entry.astype(jnp.float32) for entry in weights))

    def forward(enc_x, dec_x, params):
        e_norm1, e_query, e_key, e_value, e_proj, e_rel, e_norm2, e_gate, e_up, e_down, e_final, d_norm1, d_query, d_key, d_value, d_proj, d_rel, d_norm2, c_query, c_key, c_value, c_proj, d_norm3, d_gate, d_up, d_down = params
        enc_table = bias_table(e_rel, buckets[0])
        dec_table = bias_table(d_rel, buckets[1])
        enc_mid = attention_block(enc_x, None, e_norm1, e_query, e_key, e_value, e_proj, enc_segments, enc_segments, enc_table, False)
        enc_result = feed_forward(enc_mid, e_norm2, e_gate, e_up, e_down)
        memory = low(rms_norm(enc_result, e_final))
        dec_mid = attention_block(dec_x, None, d_norm1, d_query, d_key, d_value, d_proj, dec_segments, dec_segments, dec_table, True)
        dec_cross = attention_block(dec_mid, memory, d_norm2, c_query, c_key, c_value, c_proj, dec_segments, enc_segments, None, False)
        dec_result = feed_forward(dec_cross, d_norm3, d_gate, d_up, d_down)
        return (enc_result, dec_result)
    (enc_result, dec_result), pullback = jax.vjp(forward, enc_in.astype(jnp.float32), dec_in.astype(jnp.float32), weights)
    grad_enc, grad_dec, grads = pullback((enc_cot.astype(jnp.float32), dec_cot.astype(jnp.float32)))
    return (enc_result, dec_result, grad_enc, grad_dec, grads[0], grads[1], grads[2], grads[3], grads[4], grads[5], grads[6], grads[7], grads[8], grads[9], grads[10], grads[11], grads[12], grads[13], grads[14], grads[15], grads[16], grads[17], grads[18], grads[19], grads[20], grads[21], grads[22], grads[23], grads[24], grads[25])
```

```python
import math

import jax
import jax.numpy as jnp
import numpy as np
from jax import lax
from jax.experimental import pallas as pl
from jax.experimental.pallas import tpu as pltpu
from jax.sharding import Mesh
from jax.sharding import PartitionSpec as P

HEADS = 12
HD = 64


EPSILON = 1e-06
NEGATIVE = -1e30
HIGHEST = lax.Precision.HIGHEST


def rms_norm(values, norm_gain):
    return (
        values * lax.rsqrt(jnp.mean(values * values, axis=-1, keepdims=True) + EPSILON) * norm_gain
    )


def norm_pullback(values, norm_gain, grad_normed):
    _, pullback = jax.vjp(rms_norm, values, norm_gain)
    return pullback(grad_normed)


def gated(gate_val, up_val):
    return jax.nn.gelu(gate_val, approximate=True) * up_val


def project(left, right):
    return jnp.dot(left, right, preferred_element_type=jnp.float32)


def weight_grad(left, right):
    return jnp.einsum("td,te->de", left, right, preferred_element_type=jnp.float32)


def input_grad(grad_out, weight):
    return jnp.einsum("te,de->td", grad_out, weight, preferred_element_type=jnp.float32)


def head_table(relative, table_row, heads_here):
    bucket_count = relative.shape[0] // HEADS
    onehot = (table_row[:, None] == jnp.arange(bucket_count, dtype=jnp.int32)[None, :]).astype(
        jnp.float32
    )
    bias_grid = relative.astype(jnp.float32).reshape(bucket_count, HEADS)
    full_table = jnp.dot(onehot, bias_grid, precision=HIGHEST).T
    first_head = lax.axis_index("sp") * heads_here
    return (lax.dynamic_slice_in_dim(full_table, first_head, heads_here, 0), onehot)


def table_grad(grad_table, onehot, heads_here):
    full_grad = jnp.zeros((HEADS, onehot.shape[0]), jnp.float32)
    full_grad = lax.dynamic_update_slice_in_dim(
        full_grad, grad_table, lax.axis_index("sp") * heads_here, 0
    )
    return jnp.dot(onehot.T, full_grad.T, precision=HIGHEST).reshape(-1)


def bias_block(head_bias, pad_len, offset_q, rows, offset_k, cols):
    head_count, table_len = head_bias.shape
    reach_len = (table_len - 1) // 2
    left_edge = jnp.broadcast_to(head_bias[:, :1], (head_count, pad_len))
    right_edge = jnp.broadcast_to(head_bias[:, -1:], (head_count, pad_len))
    padded = jnp.concatenate([left_edge, head_bias, right_edge], axis=1)
    band_width = rows + cols - 1
    start = offset_k - offset_q - (rows - 1) + reach_len + pad_len
    band = lax.dynamic_slice_in_dim(padded, start, band_width, 1)
    tiled = jnp.broadcast_to(band[:, None, :], (head_count, rows, band_width)).reshape(
        head_count, rows * band_width
    )
    skewed = tiled[:, rows - 1 : rows - 1 + rows * (band_width - 1)].reshape(
        head_count, rows, band_width - 1
    )
    return skewed[:, :, :cols]


def make_frame(query_local, query_ids, key_ids, head_bias, causal):
    local_len = query_local.shape[0]
    heads_here = query_local.shape[1] // HD
    offset_q = lax.axis_index("ctx") * local_len
    ids_q = lax.dynamic_slice_in_dim(query_ids, offset_q, local_len, 0)
    row_ids = offset_q + jnp.arange(local_len, dtype=jnp.int32)
    query_heads = query_local.reshape(local_len, heads_here, HD)
    pad_len = query_ids.shape[0] + key_ids.shape[0]

    def bias_of(entries, offset_k, length):
        return bias_block(entries, pad_len, offset_q, local_len, offset_k, length)

    def scores_of(key_block, offset_k):
        length = key_block.shape[0]
        key_heads = key_block.reshape(length, heads_here, HD)
        raw_scores = jnp.einsum(
            "qhd,khd->hqk", query_heads, key_heads, preferred_element_type=jnp.float32
        )
        col_ids = offset_k + jnp.arange(length, dtype=jnp.int32)
        ids_k = lax.dynamic_slice_in_dim(key_ids, offset_k, length, 0)
        allowed = ids_q[:, None] == ids_k[None, :]
        if causal:
            allowed = allowed & (col_ids[None, :] <= row_ids[:, None])
        if head_bias is not None:
            raw_scores = raw_scores + bias_of(head_bias, offset_k, length)
        return (raw_scores, allowed)

    def touches(offset_k, length):
        first_id = lax.dynamic_slice_in_dim(key_ids, offset_k, 1, 0)[0]
        last_id = lax.dynamic_slice_in_dim(key_ids, offset_k + length - 1, 1, 0)[0]
        touched = (ids_q[0] <= last_id) & (first_id <= ids_q[-1])
        if causal:
            touched = touched & (offset_k <= offset_q + local_len - 1)
        return touched

    return (query_heads, scores_of, touches, bias_of)


def sweep(keys_gathered, local_len, step_fn, carry_state):
    key_all, value_all = keys_gathered
    block_len = local_len * math.gcd(4, lax.axis_size("ctx"))

    def sweep_loop_body(number, running):
        offset_k = number * block_len
        key_block = lax.dynamic_slice_in_dim(key_all, offset_k, block_len, 0)
        value_block = lax.dynamic_slice_in_dim(value_all, offset_k, block_len, 0)
        return step_fn(running, key_block, value_block, offset_k)

    return lax.fori_loop(0, key_all.shape[0] // block_len, sweep_loop_body, carry_state)


def whole_keys(key_local, value_local):
    return (
        lax.all_gather(key_local, "ctx", axis=0, tiled=True),
        lax.all_gather(value_local, "ctx", axis=0, tiled=True),
    )


def attention_forward(query_proj, key_proj, value_proj, query_ids, key_ids, head_bias, causal):
    query_local, key_local, value_local = (
        lax.all_to_all(query_proj, "sp", split_axis=1, concat_axis=0, tiled=True),
        lax.all_to_all(key_proj, "sp", split_axis=1, concat_axis=0, tiled=True),
        lax.all_to_all(value_proj, "sp", split_axis=1, concat_axis=0, tiled=True),
    )
    local_len = query_local.shape[0]
    heads_here = query_local.shape[1] // HD
    query_heads, scores_of, touches, _ = make_frame(
        query_local, query_ids, key_ids, head_bias, causal
    )
    key_block = lax.all_gather(key_local, "ctx", axis=0, tiled=True)
    value_block = lax.all_gather(value_local, "ctx", axis=0, tiled=True)
    offset_k = jnp.int32(0)
    length = key_block.shape[0]
    row_top = jnp.full((heads_here, local_len), NEGATIVE, jnp.float32)
    weighted = jnp.zeros((local_len, heads_here, HD), jnp.float32)
    raw_scores, allowed = scores_of(key_block, offset_k)
    masked = jnp.where(allowed[None], raw_scores, NEGATIVE)
    new_top = jnp.maximum(row_top, jnp.max(masked, axis=-1))
    weights = jnp.where(allowed[None], jnp.exp(masked - new_top[..., None]), 0.0)
    rescale = jnp.exp(row_top - new_top)
    value_heads = value_block.reshape(length, heads_here, HD)
    increment = jnp.einsum(
        "hqk,khd->qhd",
        weights.astype(jnp.bfloat16),
        value_heads,
        preferred_element_type=jnp.float32,
    )
    row_top, row_total, weighted = (
        new_top,
        jnp.sum(weights, axis=-1),
        weighted * rescale.T[:, :, None] + increment,
    )
    mixed_heads = weighted / row_total.T[:, :, None]
    log_total = row_top + jnp.log(row_total)
    mixed_low = mixed_heads.reshape(local_len, heads_here * HD).astype(jnp.bfloat16)
    mixed_tokens = lax.all_to_all(mixed_low, "sp", split_axis=0, concat_axis=1, tiled=True)
    retained = (
        query_local,
        key_local,
        value_local,
        mixed_heads,
        log_total,
        None,
        query_ids,
        key_ids,
        head_bias,
        causal,
    )
    return (mixed_tokens, retained)


def attention_backward(grad_mixed, retained):
    (
        query_local,
        key_local,
        value_local,
        mixed_heads,
        log_total,
        gathered,
        query_ids,
        key_ids,
        head_bias,
        causal,
    ) = retained
    grad_local = lax.all_to_all(grad_mixed, "sp", split_axis=1, concat_axis=0, tiled=True)
    local_len = query_local.shape[0]
    heads_here = query_local.shape[1] // HD
    width = heads_here * HD
    query_heads, scores_of, touches, bias_of = make_frame(
        query_local, query_ids, key_ids, head_bias, causal
    )
    grad_heads = grad_local.reshape(local_len, heads_here, HD)
    row_inner = jnp.einsum("qhd,qhd->hq", grad_heads.astype(jnp.float32), mixed_heads)
    gathered = whole_keys(key_local, value_local)
    table_zero = jnp.zeros(head_bias.shape if head_bias is not None else (1,), jnp.float32)

    def gradients_of(key_block, value_block, offset_k):
        length = key_block.shape[0]
        raw_scores, allowed = scores_of(key_block, offset_k)
        probabilities = jnp.where(allowed[None], jnp.exp(raw_scores - log_total[..., None]), 0.0)
        value_heads = value_block.reshape(length, heads_here, HD)
        grad_probs = jnp.einsum(
            "qhd,khd->hqk", grad_heads, value_heads, preferred_element_type=jnp.float32
        )
        grad_scores = (probabilities * (grad_probs - row_inner[..., None])).astype(jnp.bfloat16)
        return (probabilities, grad_scores)

    def table_part(grad_scores, offset_k, length):
        if head_bias is None:
            return table_zero
        _, pullback = jax.vjp(lambda entries: bias_of(entries, offset_k, length), head_bias)
        return pullback(grad_scores.astype(jnp.float32))[0]

    def key_terms_of(probabilities, grad_scores, length):
        grad_key = jnp.einsum(
            "hqk,qhd->khd", grad_scores, query_heads, preferred_element_type=jnp.float32
        )
        grad_value = jnp.einsum(
            "hqk,qhd->khd",
            probabilities.astype(jnp.bfloat16),
            grad_heads,
            preferred_element_type=jnp.float32,
        )
        return jnp.concatenate(
            [grad_key.reshape(length, width), grad_value.reshape(length, width)], axis=1
        )

    def query_part(grad_scores, key_block):
        length = key_block.shape[0]
        key_heads = key_block.reshape(length, heads_here, HD)
        return jnp.einsum(
            "hqk,khd->qhd", grad_scores, key_heads, preferred_element_type=jnp.float32
        )

    def query_step(running, key_block, value_block, offset_k):
        length = key_block.shape[0]
        grad_query, grad_table = running
        probabilities, grad_scores = gradients_of(key_block, value_block, offset_k)
        return (
            grad_query + query_part(grad_scores, key_block),
            grad_table + table_part(grad_scores, offset_k, length),
        )

    query_zero = jnp.zeros((local_len, heads_here, HD), jnp.float32)
    block_len = local_len * math.gcd(4, lax.axis_size("ctx"))
    grad_query, grad_table = sweep(gathered, local_len, query_step, (query_zero, table_zero))
    key_all, value_all = gathered
    step_len = math.gcd(lax.axis_size("ctx") * local_len, block_len)

    def term_loop_body(number, rows_acc):
        offset_b = number * step_len
        key_block = lax.dynamic_slice_in_dim(key_all, offset_b, step_len, 0)
        value_block = lax.dynamic_slice_in_dim(value_all, offset_b, step_len, 0)
        probabilities, grad_scores = gradients_of(key_block, value_block, offset_b)
        return lax.dynamic_update_slice_in_dim(
            rows_acc, key_terms_of(probabilities, grad_scores, step_len), number * step_len, 0
        )

    own_rows = lax.psum_scatter(
        lax.fori_loop(
            0,
            lax.axis_size("ctx") * local_len // step_len,
            term_loop_body,
            jnp.zeros((lax.axis_size("ctx") * local_len, 2 * width), jnp.float32),
        ),
        "ctx",
        scatter_dimension=0,
        tiled=True,
    )
    grad_q_low = grad_query.reshape(local_len, width).astype(jnp.bfloat16)
    grad_k_low = own_rows[:, :width].astype(jnp.bfloat16)
    grad_v_low = own_rows[:, width:].astype(jnp.bfloat16)
    grad_q_tok, grad_k_tok, grad_v_tok = (
        lax.all_to_all(grad_q_low, "sp", split_axis=0, concat_axis=1, tiled=True),
        lax.all_to_all(grad_k_low, "sp", split_axis=0, concat_axis=1, tiled=True),
        lax.all_to_all(grad_v_low, "sp", split_axis=0, concat_axis=1, tiled=True),
    )
    return (grad_q_tok, grad_k_tok, grad_v_tok, grad_table)


def attention_layer(
    residual,
    source,
    norm_gain,
    w_query,
    w_key,
    w_value,
    w_proj,
    query_ids,
    key_ids,
    head_bias,
    causal,
):
    normed = rms_norm(residual, norm_gain).astype(jnp.bfloat16)
    kv_input = normed if source is None else source
    query_proj = project(normed, w_query).astype(jnp.bfloat16)
    key_proj = project(kv_input, w_key).astype(jnp.bfloat16)
    value_proj = project(kv_input, w_value).astype(jnp.bfloat16)
    mixed_tokens, retained = attention_forward(
        query_proj, key_proj, value_proj, query_ids, key_ids, head_bias, causal
    )
    result = residual + project(mixed_tokens, w_proj)
    return (result, (residual, normed, kv_input, mixed_tokens, retained))


def attention_layer_back(grad_out, saved, norm_gain, w_query, w_key, w_value, w_proj, is_cross):
    residual, normed, kv_input, mixed_tokens, retained = saved
    grad_low = grad_out.astype(jnp.bfloat16)
    grad_proj = weight_grad(mixed_tokens, grad_low)
    grad_mixed = input_grad(grad_low, w_proj).astype(jnp.bfloat16)
    grad_q_tok, grad_k_tok, grad_v_tok, grad_table = attention_backward(grad_mixed, retained)
    grad_wq = weight_grad(normed, grad_q_tok)
    grad_wk = weight_grad(kv_input, grad_k_tok)
    grad_wv = weight_grad(kv_input, grad_v_tok)
    grad_source = input_grad(grad_k_tok, w_key) + input_grad(grad_v_tok, w_value)
    grad_normed = input_grad(grad_q_tok, w_query)
    if not is_cross:
        grad_normed = grad_normed + grad_source
        grad_source = None
    grad_resid, grad_gain = norm_pullback(residual, norm_gain, grad_normed)
    return (
        grad_out + grad_resid,
        grad_source,
        (grad_gain, grad_wq, grad_wk, grad_wv, grad_proj, grad_table),
    )


def feed_layer(residual, norm_gain, w_gate, w_up, w_down):
    normed = rms_norm(residual, norm_gain).astype(jnp.bfloat16)
    gate_val = project(normed, w_gate)
    up_val = project(normed, w_up)
    hidden = gated(gate_val, up_val).astype(jnp.bfloat16)
    return (residual + project(hidden, w_down), (residual, normed, gate_val, up_val, hidden))


def feed_layer_back(grad_out, saved, norm_gain, w_gate, w_up, w_down):
    residual, normed, gate_val, up_val, hidden = saved
    grad_low = grad_out.astype(jnp.bfloat16)
    grad_down = weight_grad(hidden, grad_low)
    grad_hidden = input_grad(grad_low, w_down)
    _, pullback = jax.vjp(gated, gate_val, up_val)
    grad_gate, grad_up = pullback(grad_hidden)
    grad_gate = grad_gate.astype(jnp.bfloat16)
    grad_up = grad_up.astype(jnp.bfloat16)
    grad_wg = weight_grad(normed, grad_gate)
    grad_wu = weight_grad(normed, grad_up)
    grad_normed = input_grad(grad_gate, w_gate) + input_grad(grad_up, w_up)
    grad_resid, grad_gain = norm_pullback(residual, norm_gain, grad_normed)
    return (grad_out + grad_resid, (grad_gain, grad_wg, grad_wu, grad_down))


def per_device(
    enc_in,
    dec_in,
    enc_cot,
    dec_cot,
    enc_segments,
    dec_segments,
    buckets,
    enc_norm1,
    enc_query,
    enc_key,
    enc_value,
    enc_proj,
    enc_rel,
    enc_norm2,
    enc_gate,
    enc_up,
    enc_down,
    enc_final,
    dec_norm1,
    dec_query,
    dec_key,
    dec_value,
    dec_proj,
    dec_rel,
    dec_norm2,
    cross_query,
    cross_key,
    cross_value,
    cross_proj,
    dec_norm3,
    dec_gate,
    dec_up,
    dec_down,
):
    (
        enc_norm1,
        enc_query,
        enc_key,
        enc_value,
        enc_proj,
        enc_rel,
        enc_norm2,
        enc_gate,
        enc_up,
        enc_down,
        enc_final,
        dec_norm1,
        dec_query,
        dec_key,
        dec_value,
        dec_proj,
        dec_rel,
        dec_norm2,
        cross_query,
        cross_key,
        cross_value,
        cross_proj,
        dec_norm3,
        dec_gate,
        dec_up,
        dec_down,
    ) = (
        lax.all_gather(enc_norm1, "ctx", axis=0, tiled=True),
        lax.all_gather(enc_query, "ctx", axis=0, tiled=True),
        lax.all_gather(enc_key, "ctx", axis=0, tiled=True),
        lax.all_gather(enc_value, "ctx", axis=0, tiled=True),
        lax.all_gather(enc_proj, "ctx", axis=0, tiled=True),
        lax.all_gather(enc_rel, "ctx", axis=0, tiled=True),
        lax.all_gather(enc_norm2, "ctx", axis=0, tiled=True),
        lax.all_gather(enc_gate, "ctx", axis=0, tiled=True),
        lax.all_gather(enc_up, "ctx", axis=0, tiled=True),
        lax.all_gather(enc_down, "ctx", axis=0, tiled=True),
        lax.all_gather(enc_final, "ctx", axis=0, tiled=True),
        lax.all_gather(dec_norm1, "ctx", axis=0, tiled=True),
        lax.all_gather(dec_query, "ctx", axis=0, tiled=True),
        lax.all_gather(dec_key, "ctx", axis=0, tiled=True),
        lax.all_gather(dec_value, "ctx", axis=0, tiled=True),
        lax.all_gather(dec_proj, "ctx", axis=0, tiled=True),
        lax.all_gather(dec_rel, "ctx", axis=0, tiled=True),
        lax.all_gather(dec_norm2, "ctx", axis=0, tiled=True),
        lax.all_gather(cross_query, "ctx", axis=0, tiled=True),
        lax.all_gather(cross_key, "ctx", axis=0, tiled=True),
        lax.all_gather(cross_value, "ctx", axis=0, tiled=True),
        lax.all_gather(cross_proj, "ctx", axis=0, tiled=True),
        lax.all_gather(dec_norm3, "ctx", axis=0, tiled=True),
        lax.all_gather(dec_gate, "ctx", axis=0, tiled=True),
        lax.all_gather(dec_up, "ctx", axis=0, tiled=True),
        lax.all_gather(dec_down, "ctx", axis=0, tiled=True),
    )
    enc_norm1 = enc_norm1.astype(jnp.float32)
    enc_norm2 = enc_norm2.astype(jnp.float32)
    enc_final = enc_final.astype(jnp.float32)
    dec_norm1 = dec_norm1.astype(jnp.float32)
    dec_norm2 = dec_norm2.astype(jnp.float32)
    dec_norm3 = dec_norm3.astype(jnp.float32)
    heads_here = HEADS // lax.axis_size("sp")
    enc_table, enc_onehot = head_table(enc_rel, buckets[0], heads_here)
    dec_table, dec_onehot = head_table(dec_rel, buckets[1], heads_here)
    enc_x = enc_in.astype(jnp.float32)
    enc_mid, enc_saved_a = attention_layer(
        enc_x,
        None,
        enc_norm1,
        enc_query,
        enc_key,
        enc_value,
        enc_proj,
        enc_segments,
        enc_segments,
        enc_table,
        False,
    )
    enc_result, enc_saved_f = feed_layer(enc_mid, enc_norm2, enc_gate, enc_up, enc_down)
    memory = rms_norm(enc_result, enc_final).astype(jnp.bfloat16)
    dec_x = dec_in.astype(jnp.float32)
    dec_mid, dec_saved_a = attention_layer(
        dec_x,
        None,
        dec_norm1,
        dec_query,
        dec_key,
        dec_value,
        dec_proj,
        dec_segments,
        dec_segments,
        dec_table,
        True,
    )
    dec_cross, dec_saved_c = attention_layer(
        dec_mid,
        memory,
        dec_norm2,
        cross_query,
        cross_key,
        cross_value,
        cross_proj,
        dec_segments,
        enc_segments,
        None,
        False,
    )
    dec_result, dec_saved_f = feed_layer(dec_cross, dec_norm3, dec_gate, dec_up, dec_down)
    grad_dec, dec_ff_grads = feed_layer_back(
        dec_cot.astype(jnp.float32), dec_saved_f, dec_norm3, dec_gate, dec_up, dec_down
    )
    grad_dec, grad_memory, cross_grads = attention_layer_back(
        grad_dec, dec_saved_c, dec_norm2, cross_query, cross_key, cross_value, cross_proj, True
    )
    grad_dec, _, dec_self_grads = attention_layer_back(
        grad_dec, dec_saved_a, dec_norm1, dec_query, dec_key, dec_value, dec_proj, False
    )
    grad_enc_out, grad_final = norm_pullback(enc_result, enc_final, grad_memory)
    grad_enc, enc_ff_grads = feed_layer_back(
        enc_cot.astype(jnp.float32) + grad_enc_out,
        enc_saved_f,
        enc_norm2,
        enc_gate,
        enc_up,
        enc_down,
    )
    grad_enc, _, enc_self_grads = attention_layer_back(
        grad_enc, enc_saved_a, enc_norm1, enc_query, enc_key, enc_value, enc_proj, False
    )
    e_gain1, e_wq, e_wk, e_wv, e_wo, e_table = enc_self_grads
    e_gain2, e_wg, e_wu, e_wd = enc_ff_grads
    d_gain1, d_wq, d_wk, d_wv, d_wo, d_table = dec_self_grads
    c_gain, c_wq, c_wk, c_wv, c_wo, _ = cross_grads
    d_gain3, d_wg, d_wu, d_wd = dec_ff_grads
    e_rel = table_grad(e_table, enc_onehot, heads_here)
    d_rel = table_grad(d_table, dec_onehot, heads_here)
    shards = (
        lax.psum_scatter(e_gain1, "ctx", scatter_dimension=0, tiled=True),
        lax.psum_scatter(e_wq, "ctx", scatter_dimension=0, tiled=True),
        lax.psum_scatter(e_wk, "ctx", scatter_dimension=0, tiled=True),
        lax.psum_scatter(e_wv, "ctx", scatter_dimension=0, tiled=True),
        lax.psum_scatter(e_wo, "ctx", scatter_dimension=0, tiled=True),
        lax.psum_scatter(e_rel, "ctx", scatter_dimension=0, tiled=True),
        lax.psum_scatter(e_gain2, "ctx", scatter_dimension=0, tiled=True),
        lax.psum_scatter(e_wg, "ctx", scatter_dimension=0, tiled=True),
        lax.psum_scatter(e_wu, "ctx", scatter_dimension=0, tiled=True),
        lax.psum_scatter(e_wd, "ctx", scatter_dimension=0, tiled=True),
        lax.psum_scatter(grad_final, "ctx", scatter_dimension=0, tiled=True),
        lax.psum_scatter(d_gain1, "ctx", scatter_dimension=0, tiled=True),
        lax.psum_scatter(d_wq, "ctx", scatter_dimension=0, tiled=True),
        lax.psum_scatter(d_wk, "ctx", scatter_dimension=0, tiled=True),
        lax.psum_scatter(d_wv, "ctx", scatter_dimension=0, tiled=True),
        lax.psum_scatter(d_wo, "ctx", scatter_dimension=0, tiled=True),
        lax.psum_scatter(d_rel, "ctx", scatter_dimension=0, tiled=True),
        lax.psum_scatter(c_gain, "ctx", scatter_dimension=0, tiled=True),
        lax.psum_scatter(c_wq, "ctx", scatter_dimension=0, tiled=True),
        lax.psum_scatter(c_wk, "ctx", scatter_dimension=0, tiled=True),
        lax.psum_scatter(c_wv, "ctx", scatter_dimension=0, tiled=True),
        lax.psum_scatter(c_wo, "ctx", scatter_dimension=0, tiled=True),
        lax.psum_scatter(d_gain3, "ctx", scatter_dimension=0, tiled=True),
        lax.psum_scatter(d_wg, "ctx", scatter_dimension=0, tiled=True),
        lax.psum_scatter(d_wu, "ctx", scatter_dimension=0, tiled=True),
        lax.psum_scatter(d_wd, "ctx", scatter_dimension=0, tiled=True),
    )
    (
        s_gain1,
        s_wq,
        s_wk,
        s_wv,
        s_wo,
        s_rel,
        s_gain2,
        s_wg,
        s_wu,
        s_wd,
        s_final,
        t_gain1,
        t_wq,
        t_wk,
        t_wv,
        t_wo,
        t_rel,
        t_gain2,
        t_cq,
        t_ck,
        t_cv,
        t_co,
        t_gain3,
        t_wg,
        t_wu,
        t_wd,
    ) = shards
    reduced = (
        lax.psum(s_gain1.astype(jnp.bfloat16), "sp").astype(jnp.float32),
        lax.psum(s_wq.astype(jnp.bfloat16), "sp").astype(jnp.float32),
        lax.psum(s_wk.astype(jnp.bfloat16), "sp").astype(jnp.float32),
        lax.psum(s_wv.astype(jnp.bfloat16), "sp").astype(jnp.float32),
        lax.psum(s_wo.astype(jnp.bfloat16), "sp").astype(jnp.float32),
        lax.psum(s_rel.astype(jnp.bfloat16), "sp").astype(jnp.float32),
        lax.psum(s_gain2.astype(jnp.bfloat16), "sp").astype(jnp.float32),
        lax.psum(s_wg.astype(jnp.bfloat16), "sp").astype(jnp.float32),
        lax.psum(s_wu.astype(jnp.bfloat16), "sp").astype(jnp.float32),
        lax.psum(s_wd.astype(jnp.bfloat16), "sp").astype(jnp.float32),
        lax.psum(s_final.astype(jnp.bfloat16), "sp").astype(jnp.float32),
        lax.psum(t_gain1.astype(jnp.bfloat16), "sp").astype(jnp.float32),
        lax.psum(t_wq.astype(jnp.bfloat16), "sp").astype(jnp.float32),
        lax.psum(t_wk.astype(jnp.bfloat16), "sp").astype(jnp.float32),
        lax.psum(t_wv.astype(jnp.bfloat16), "sp").astype(jnp.float32),
        lax.psum(t_wo.astype(jnp.bfloat16), "sp").astype(jnp.float32),
        lax.psum(t_rel.astype(jnp.bfloat16), "sp").astype(jnp.float32),
        lax.psum(t_gain2.astype(jnp.bfloat16), "sp").astype(jnp.float32),
        lax.psum(t_cq.astype(jnp.bfloat16), "sp").astype(jnp.float32),
        lax.psum(t_ck.astype(jnp.bfloat16), "sp").astype(jnp.float32),
        lax.psum(t_cv.astype(jnp.bfloat16), "sp").astype(jnp.float32),
        lax.psum(t_co.astype(jnp.bfloat16), "sp").astype(jnp.float32),
        lax.psum(t_gain3.astype(jnp.bfloat16), "sp").astype(jnp.float32),
        lax.psum(t_wg.astype(jnp.bfloat16), "sp").astype(jnp.float32),
        lax.psum(t_wu.astype(jnp.bfloat16), "sp").astype(jnp.float32),
        lax.psum(t_wd.astype(jnp.bfloat16), "sp").astype(jnp.float32),
    )
    return (enc_result, dec_result, grad_enc, grad_dec) + tuple(reduced)


HG, CORE, SP = "hg", "core", "sp"
BLOCK_PAD = 128


def nt(left, right):
    return lax.dot_general(left, right, (((1,), (1,)), ((), ())), preferred_element_type=jnp.float32)


def tn(left, right):
    return lax.dot_general(left, right, (((0,), (0,)), ((), ())), preferred_element_type=jnp.float32)


def nn(left, right):
    return jnp.dot(left, right, preferred_element_type=jnp.float32)


def identity(size):
    rows = lax.broadcasted_iota(jnp.int32, (size, size), 0)
    cols = lax.broadcasted_iota(jnp.int32, (size, size), 1)
    return jnp.where(rows == cols, 1.0, 0.0).astype(jnp.bfloat16)


def only_head(array, head):
    lanes = lax.broadcasted_iota(jnp.int32, array.shape, 1)
    keep = (lanes >= head * HD) & (lanes < (head + 1) * HD)
    return jnp.where(keep, array, jnp.zeros_like(array))


def bias_mask_kernel(heads, block, causal, starts_ref, tables_ref, kdoc_ref, qdoc_ref, qpos_ref, qstart_ref, out_ref):
    rows_total, lanes = out_ref.shape[1], out_ref.shape[2]
    key_len = kdoc_ref.shape[0]
    strip = block + 2 * BLOCK_PAD
    for head in range(heads):
        if tables_ref is not None:
            row = tables_ref[head : head + 1, :]
            width = row.shape[1]
            left, right = tables_ref[head : head + 1, width - 2 : width - 1], tables_ref[head : head + 1, 0:1]
            places = lax.broadcasted_iota(jnp.int32, (rows_total, lanes), 0)
            fill = jnp.where(places < qstart_ref[...], left, right)
            out_ref[head] = fill.astype(jnp.bfloat16)
            wide = jnp.broadcast_to(row, (strip, width))
            for number in range(lanes // block):
                at = (number * block) % 128
                turned = pltpu.roll(wide, (width - (strip - 1) + at) % width, 1, stride=1, stride_axis=0)
                out_ref[head, pl.ds(pl.multiple_of(starts_ref[number], block), strip), number * block : (number + 1) * block] = turned[:, at : at + block].astype(jnp.bfloat16)
        allowed = kdoc_ref[...] == qdoc_ref[...]
        if causal:
            places = lax.broadcasted_iota(jnp.int32, (key_len, lanes), 0)
            allowed = allowed & (places <= qpos_ref[...])
        inside = pl.ds(BLOCK_PAD, key_len)
        if tables_ref is not None:
            out_ref[head, inside, :] = jnp.where(allowed, out_ref[head, inside, :].astype(jnp.float32), NEGATIVE).astype(jnp.bfloat16)
        else:
            out_ref[head, inside, :] = jnp.where(allowed, 0.0, NEGATIVE).astype(jnp.bfloat16)


def bias_mask(starts, tables, kdoc, qdoc, qpos, block, causal):
    key_len, lanes = kdoc.shape[0], qdoc.shape[1]
    heads = tables.shape[0] if tables is not None else 1
    qstart = jnp.repeat(starts, block)[None, :]
    operands = [starts] + ([tables] if tables is not None else []) + [kdoc, qdoc, qpos, qstart]

    def body(*refs):
        refs = list(refs)
        if tables is None:
            refs.insert(1, None)
        bias_mask_kernel(heads, block, causal, *refs)

    return pl.pallas_call(
        body,
        out_shape=jax.ShapeDtypeStruct((heads, key_len + 2 * BLOCK_PAD, lanes), jnp.bfloat16),
        in_specs=[pl.BlockSpec(memory_space=pltpu.SMEM)] + [pl.BlockSpec(memory_space=pltpu.VMEM)] * (len(operands) - 1),
        out_specs=pl.BlockSpec(memory_space=pltpu.VMEM),
        compiler_params=pltpu.CompilerParams(vmem_limit_bytes=VMEM_BYTES),
    )(*operands)


VMEM_BYTES = 56 << 20
ROWS = 512


def head_scores(k_ref, masked_q, bm_ref, head, at):
    bias_head = head if bm_ref.shape[0] > 1 else 0
    bias = bm_ref[bias_head, pl.ds(pl.multiple_of(BLOCK_PAD + at, 128), ROWS), :].astype(jnp.float32)
    return nt(k_ref[pl.ds(at, ROWS), :], masked_q) + bias


def mix_kernel(q_ref, k_ref, v_ref, bm_ref, o_ref, lse_ref, s_ref, p_ref, ot_ref):
    key_len, width = k_ref.shape
    lanes = q_ref.shape[0]
    vt = nt(identity(width), v_ref[...]).astype(jnp.bfloat16)
    for head in range(width // HD):
        masked_q = only_head(q_ref[...], head)

        def first(number, top):
            at = pl.multiple_of(number * ROWS, ROWS)
            scores = head_scores(k_ref, masked_q, bm_ref, head, at)
            s_ref[pl.ds(at, ROWS), :] = scores
            return jnp.maximum(top, jnp.max(scores, axis=0, keepdims=True))

        top = lax.fori_loop(0, key_len // ROWS, first, jnp.full((1, lanes), NEGATIVE, jnp.float32))

        def second(number, total):
            at = pl.multiple_of(number * ROWS, ROWS)
            weights = jnp.exp(s_ref[pl.ds(at, ROWS), :] - top)
            p_ref[pl.ds(at, ROWS), :] = weights.astype(jnp.bfloat16)
            return total + jnp.sum(weights, axis=0, keepdims=True)

        total = lax.fori_loop(0, key_len // ROWS, second, jnp.zeros((1, lanes), jnp.float32))
        lse_ref[:, head * lanes : (head + 1) * lanes] = top + jnp.log(total)
        mixed = nn(vt[head * HD : (head + 1) * HD], p_ref[...])
        ot_ref[head * HD : (head + 1) * HD, :] = (mixed / total).astype(jnp.bfloat16)
    o_ref[...] = nt(identity(lanes), ot_ref[...]).astype(jnp.bfloat16)


def mix(q, k, v, bm):
    lanes, width = q.shape
    heads = width // HD
    return pl.pallas_call(
        mix_kernel,
        out_shape=(
            jax.ShapeDtypeStruct((lanes, width), jnp.bfloat16),
            jax.ShapeDtypeStruct((1, heads * lanes), jnp.float32),
        ),
        in_specs=[pl.BlockSpec(memory_space=pltpu.VMEM)] * 4,
        out_specs=(pl.BlockSpec(memory_space=pltpu.VMEM),) * 2,
        scratch_shapes=[
            pltpu.VMEM((k.shape[0], lanes), jnp.float32),
            pltpu.VMEM((k.shape[0], lanes), jnp.bfloat16),
            pltpu.VMEM((width, lanes), jnp.bfloat16),
        ],
        compiler_params=pltpu.CompilerParams(vmem_limit_bytes=VMEM_BYTES),
    )(q, k, v, bm)


def mix_back_kernel(block, starts_ref, q_ref, k_ref, v_ref, do_ref, lse_ref, bm_ref, qstart_ref, dq_ref, dk_ref, dv_ref, strip_ref, edge_ref, p_ref, dp_ref, ds_ref, pb_ref, ot_ref):
    key_len, width = k_ref.shape
    lanes = q_ref.shape[0]
    heads = width // HD
    biased = strip_ref is not None
    strip = block + 2 * BLOCK_PAD
    kt = nt(identity(width), k_ref[...]).astype(jnp.bfloat16)
    if biased:
        none = jnp.zeros((BLOCK_PAD, heads * lanes), jnp.bfloat16)
        ds_ref[0:BLOCK_PAD, :] = none
        ds_ref[BLOCK_PAD + key_len :, :] = none
    for head in range(heads):
        masked_q = only_head(q_ref[...], head)
        masked_do = only_head(do_ref[...], head)
        across = slice(head * lanes, (head + 1) * lanes)

        def first(number, inner):
            at = pl.multiple_of(number * ROWS, ROWS)
            p = jnp.exp(head_scores(k_ref, masked_q, bm_ref, head, at) - lse_ref[:, across])
            dp = nt(v_ref[pl.ds(at, ROWS), :], masked_do)
            p_ref[pl.ds(at, ROWS), :] = p
            dp_ref[pl.ds(at, ROWS), :] = dp
            pb_ref[pl.ds(at, ROWS), across] = p.astype(jnp.bfloat16)
            return inner + jnp.sum(p * dp, axis=0, keepdims=True)

        inner = lax.fori_loop(0, key_len // ROWS, first, jnp.zeros((1, lanes), jnp.float32))

        def second(number, sums):
            at = pl.multiple_of(number * ROWS, ROWS)
            ds = (p_ref[pl.ds(at, ROWS), :] * (dp_ref[pl.ds(at, ROWS), :] - inner)).astype(jnp.bfloat16)
            ds_ref[pl.ds(BLOCK_PAD + at, ROWS), across] = ds
            if not biased:
                return sums
            wide = ds.astype(jnp.float32)
            places = lax.broadcasted_iota(jnp.int32, wide.shape, 0) + (at + BLOCK_PAD)
            left = jnp.sum(jnp.where(places < qstart_ref[...], wide, 0.0), axis=0, keepdims=True)
            right = jnp.sum(jnp.where(places >= qstart_ref[...] + strip, wide, 0.0), axis=0, keepdims=True)
            return (sums[0] + left, sums[1] + right)

        nothing = jnp.zeros((1, lanes), jnp.float32)
        left, right = lax.fori_loop(0, key_len // ROWS, second, (nothing, nothing))
        if biased:
            edge_ref[2 * head : 2 * head + 1, :] = left
            edge_ref[2 * head + 1 : 2 * head + 2, :] = right
            total = jnp.zeros((strip, block), jnp.float32)
            for number in range(lanes // block):
                low = head * lanes + number * block
                rows = pl.ds(pl.multiple_of(starts_ref[number], block), strip)
                total = total + ds_ref[rows, low : low + block].astype(jnp.float32)
            strip_ref[head] = total
        back = nn(kt[head * HD : (head + 1) * HD], ds_ref[BLOCK_PAD : BLOCK_PAD + key_len, across])
        ot_ref[head * HD : (head + 1) * HD, :] = back.astype(jnp.bfloat16)
    dq_ref[...] = nt(identity(lanes), ot_ref[...]).astype(jnp.bfloat16)
    stacked_q = jnp.concatenate([only_head(q_ref[...], head) for head in range(heads)], axis=0)
    stacked_do = jnp.concatenate([only_head(do_ref[...], head) for head in range(heads)], axis=0)

    @pl.loop(0, key_len // ROWS)
    def _(number):
        at = pl.multiple_of(number * ROWS, ROWS)
        dk_ref[pl.ds(at, ROWS), :] = nn(ds_ref[pl.ds(BLOCK_PAD + at, ROWS), :], stacked_q).astype(dk_ref.dtype)
        dv_ref[pl.ds(at, ROWS), :] = nn(pb_ref[pl.ds(at, ROWS), :], stacked_do).astype(dv_ref.dtype)


def mix_back(starts, q, k, v, do, lse, bm, block, biased):
    lanes, width = q.shape
    key_len = k.shape[0]
    heads = width // HD
    qstart = jnp.repeat(starts, block)[None, :]
    shapes = [
        jax.ShapeDtypeStruct((lanes, width), jnp.bfloat16),
        jax.ShapeDtypeStruct((key_len, width), jnp.bfloat16),
        jax.ShapeDtypeStruct((key_len, width), jnp.bfloat16),
    ]
    if biased:
        shapes.append(jax.ShapeDtypeStruct((heads, block + 2 * BLOCK_PAD, block), jnp.float32))
        shapes.append(jax.ShapeDtypeStruct((2 * heads, lanes), jnp.float32))

    def body(*refs):
        refs = list(refs)
        if not biased:
            refs[11:11] = [None, None]
        mix_back_kernel(block, *refs)

    return pl.pallas_call(
        body,
        out_shape=tuple(shapes),
        in_specs=[pl.BlockSpec(memory_space=pltpu.SMEM)] + [pl.BlockSpec(memory_space=pltpu.VMEM)] * 7,
        out_specs=(pl.BlockSpec(memory_space=pltpu.VMEM),) * len(shapes),
        scratch_shapes=[
            pltpu.VMEM((key_len, lanes), jnp.float32),
            pltpu.VMEM((key_len, lanes), jnp.float32),
            pltpu.VMEM((key_len + 2 * BLOCK_PAD, heads * lanes), jnp.bfloat16),
            pltpu.VMEM((key_len, heads * lanes), jnp.bfloat16),
            pltpu.VMEM((width, lanes), jnp.bfloat16),
        ],
        compiler_params=pltpu.CompilerParams(vmem_limit_bytes=VMEM_BYTES),
    )(starts, q, k, v, do, lse, bm, qstart)


def fast_device(
    enc_in, dec_in, enc_cot, dec_cot, enc_segments, dec_segments, buckets,
    enc_norm1, enc_query, enc_key, enc_value, enc_proj, enc_rel, enc_norm2, enc_gate, enc_up, enc_down, enc_final,
    dec_norm1, dec_query, dec_key, dec_value, dec_proj, dec_rel, dec_norm2, cross_query, cross_key, cross_value, cross_proj,
    dec_norm3, dec_gate, dec_up, dec_down,
):
    groups, cores, parts = lax.axis_size(HG), lax.axis_size(CORE), lax.axis_size(SP)
    my_group, my_core, my_part = lax.axis_index(HG), lax.axis_index(CORE), lax.axis_index(SP)
    block, model = enc_in.shape
    share = model // (groups * cores)
    width = HEADS // groups * HD
    heads = HEADS // groups
    reach = (buckets.shape[1] - 1) // 2
    bf16, f32 = jnp.bfloat16, jnp.float32

    def columns(*weights):
        cut = [w.reshape(w.shape[0], groups, w.shape[1] // groups) for w in weights]
        packed = jnp.concatenate(cut, axis=2).transpose(1, 0, 2)
        moved = lax.all_to_all(packed, HG, split_axis=0, concat_axis=0, tiled=True)
        both = lax.all_gather(moved, CORE, axis=1)
        return both.reshape(model, -1)

    def both_rows(weight):
        return lax.all_gather(weight, CORE, axis=0, tiled=True)

    self_cols = columns(enc_query, enc_key, enc_value, dec_query, dec_key, dec_value)
    enc_qkv, dec_qkv = self_cols[:, : 3 * width], self_cols[:, 3 * width :]
    enc_gu = columns(enc_gate, enc_up)
    cross_qkv = columns(cross_query, cross_key, cross_value)
    cross_q, cross_kv = cross_qkv[:, :width], cross_qkv[:, width:]
    dec_gu = columns(dec_gate, dec_up)
    enc_wo, dec_wo, cross_wo = both_rows(enc_proj), both_rows(dec_proj), both_rows(cross_proj)
    enc_wd, dec_wd = both_rows(enc_down), both_rows(dec_down)
    small = jnp.concatenate([enc_norm1, enc_norm2, enc_final, dec_norm1, dec_norm2, dec_norm3, enc_rel, dec_rel])
    small = lax.all_gather(small, (HG, CORE), axis=0)
    gains = [small[:, i * share : (i + 1) * share].reshape(1, model).astype(f32) for i in range(6)]
    g_e1, g_e2, g_ef, g_d1, g_d2, g_d3 = gains
    rel_len = enc_rel.shape[0]
    rels = [small[:, 6 * share + i * rel_len : 6 * share + (i + 1) * rel_len].reshape(-1, HEADS).astype(f32) for i in range(2)]

    def table_of(relative, row):
        onehot = (row[:, None] == jnp.arange(relative.shape[0], dtype=jnp.int32)[None, :]).astype(f32)
        full = jnp.dot(onehot, relative, precision=HIGHEST).T
        here = lax.dynamic_slice_in_dim(full, my_group * heads, heads, 0)
        return here, onehot

    def turned(table):
        edge = block - 1
        long = jnp.concatenate(
            [jnp.broadcast_to(table[:, :1], (heads, edge)), table, jnp.broadcast_to(table[:, -1:], (heads, edge))], axis=1
        )
        flipped = long[:, ::-1]
        pad = -flipped.shape[1] % 128
        return jnp.pad(flipped, ((0, 0), (0, pad)))

    enc_table, enc_onehot = table_of(rels[0], buckets[0])
    dec_table, dec_onehot = table_of(rels[1], buckets[1])
    firsts = ((cores * jnp.arange(groups, dtype=jnp.int32) + my_core) * parts + my_part) * block
    qpos = (firsts[:, None] + jnp.arange(block, dtype=jnp.int32)[None, :]).reshape(1, -1)

    def mine(ids):
        return lax.dynamic_index_in_dim(
            lax.dynamic_index_in_dim(ids.reshape(groups, cores, parts, block), my_core, 1, False), my_part, 1, False
        ).reshape(1, -1)

    enc_q_ids, dec_q_ids = mine(enc_segments), mine(dec_segments)
    enc_k_ids, dec_k_ids = enc_segments[:, None], dec_segments[:, None]
    enc_bm = bias_mask(firsts, turned(enc_table), enc_k_ids, enc_q_ids, qpos, block, False)
    dec_bm = bias_mask(firsts, turned(dec_table), dec_k_ids, dec_q_ids, qpos, block, True)
    cross_bm = bias_mask(firsts, None, enc_k_ids, dec_q_ids, qpos, block, False)

    def spread(own):
        return lax.all_gather(own, HG, axis=0, tiled=True)

    def collect(partial):
        return lax.psum_scatter(partial.astype(bf16), HG, scatter_dimension=0, tiled=True).astype(f32)

    def all_keys(kv):
        every = lax.all_gather(kv, (CORE, SP), axis=0)
        every = every.reshape(cores, parts, groups, block, -1).transpose(2, 0, 1, 3, 4)
        return every.reshape(cores * parts * groups * block, -1)

    def own_keys(dkv):
        cut = dkv.reshape(groups, cores, parts, block, -1).transpose(1, 2, 0, 3, 4)
        return lax.psum_scatter(cut.reshape(cores * parts * groups * block, -1), (CORE, SP), scatter_dimension=0, tiled=True)

    def attend(n_query, w_query, kv, bm):
        q = nn(n_query, w_query).astype(bf16)
        every = all_keys(kv)
        k, v = every[:, :width], every[:, width:]
        o, lse = mix(q, k, v, bm)
        return o, (q, k, v, o, lse)

    def attend_back(dyb, kept, bm, w_proj, biased):
        q, k, v, o, lse = kept
        do = nt(dyb, w_proj).astype(bf16)
        d_proj = tn(o, dyb)
        got = mix_back(firsts, q, k, v, do, lse, bm, block, biased)
        dq, dk, dv = got[:3]
        dkv = own_keys(jnp.concatenate([dk, dv], axis=1)).astype(bf16)
        return d_proj, dq, dkv, got[3:]

    def normed(x, g):
        return rms_norm(x, g).astype(bf16)

    def norm_back(x, g, dn):
        r = lax.rsqrt(jnp.mean(x * x, axis=-1, keepdims=True) + EPSILON)
        w = dn * g
        dx = r * w - x * (r * r * r) * jnp.mean(w * x, axis=-1, keepdims=True)
        return dx, jnp.sum(dn * x * r, axis=0)

    enc_x, dec_x = enc_in.astype(f32), dec_in.astype(f32)
    en1, dn1 = spread(normed(enc_x, g_e1)), spread(normed(dec_x, g_d1))
    enc_o, enc_kept = attend(en1, enc_qkv[:, :width], nn(en1, enc_qkv[:, width:]).astype(bf16), enc_bm)
    dec_o, dec_kept = attend(dn1, dec_qkv[:, :width], nn(dn1, dec_qkv[:, width:]).astype(bf16), dec_bm)
    ex = enc_x + collect(nn(enc_o, enc_wo))
    dx = dec_x + collect(nn(dec_o, dec_wo))
    hidden = enc_wd.shape[0]

    def feed(n, w_gu, w_d):
        gu = nn(n, w_gu)
        g, u = gu[:, :hidden], gu[:, hidden:]
        h = gated(g, u).astype(bf16)
        return g, u, h, collect(nn(h, w_d))

    def feed_back(n, g, u, h, dyb, w_gu, w_d):
        dh = nt(dyb, w_d)
        d_down = tn(h, dyb)
        _, pullback = jax.vjp(gated, g, u)
        dg, du = pullback(dh)
        dgu = jnp.concatenate([dg, du], axis=1).astype(bf16)
        return tn(n, dgu), d_down, collect(nt(dgu, w_gu))

    en2 = spread(normed(ex, g_e2))
    e_g, e_u, e_h, y = feed(en2, enc_gu, enc_wd)
    enc_out = ex + y
    memory = spread(normed(enc_out, g_ef))
    dn2 = spread(normed(dx, g_d2))
    cross_o, cross_kept = attend(dn2, cross_q, nn(memory, cross_kv).astype(bf16), cross_bm)
    cx = dx + collect(nn(cross_o, cross_wo))
    dn3 = spread(normed(cx, g_d3))
    d_g, d_u, d_h, y = feed(dn3, dec_gu, dec_wd)
    dec_out = cx + y

    d_cot, e_cot = dec_cot.astype(f32), enc_cot.astype(f32)
    dyb = spread(dec_cot)
    dw_dgu, dw_ddown, dn = feed_back(dn3, d_g, d_u, d_h, dyb, dec_gu, dec_wd)
    back, dg_d3 = norm_back(cx, g_d3, dn)
    grad_dec = d_cot + back
    dyb = spread(grad_dec.astype(bf16))
    dw_cproj, dq, dkv, _ = attend_back(dyb, cross_kept, cross_bm, cross_wo, False)
    dw_cq = tn(dn2, dq)
    dw_ckv = tn(memory, dkv)
    dn, dmem = collect(nt(dq, cross_q)), collect(nt(dkv, cross_kv))
    back, dg_d2 = norm_back(dx, g_d2, dn)
    grad_dec = grad_dec + back
    dyb = spread(grad_dec.astype(bf16))
    dw_dproj, dq, dkv, dec_tab = attend_back(dyb, dec_kept, dec_bm, dec_wo, True)
    dqkv = jnp.concatenate([dq, dkv], axis=1)
    dw_dqkv = tn(dn1, dqkv)
    back, dg_d1 = norm_back(dec_x, g_d1, collect(nt(dqkv, dec_qkv)))
    dec_in_grad = grad_dec + back
    back, dg_ef = norm_back(enc_out, g_ef, dmem)
    grad_enc = e_cot + back
    dyb = spread(grad_enc.astype(bf16))
    dw_egu, dw_edown, dn = feed_back(en2, e_g, e_u, e_h, dyb, enc_gu, enc_wd)
    back, dg_e2 = norm_back(ex, g_e2, dn)
    grad_enc = grad_enc + back
    dyb = spread(grad_enc.astype(bf16))
    dw_eproj, dq, dkv, enc_tab = attend_back(dyb, enc_kept, enc_bm, enc_wo, True)
    dqkv = jnp.concatenate([dq, dkv], axis=1)
    dw_eqkv = tn(en1, dqkv)
    back, dg_e1 = norm_back(enc_x, g_e1, collect(nt(dqkv, enc_qkv)))
    enc_in_grad = grad_enc + back

    def rows_back(grad, pieces):
        n = grad.shape[1]
        cut = grad.reshape(groups, cores, share, n).transpose(1, 0, 2, 3).reshape(cores * groups * share, n)
        half = lax.psum_scatter(cut.astype(bf16), CORE, scatter_dimension=0, tiled=True).reshape(groups, share, n)
        moved = lax.all_to_all(half, HG, split_axis=0, concat_axis=0, tiled=True)
        whole = lax.psum(moved, SP).astype(f32)
        each = n // pieces
        return [whole[:, :, i * each : (i + 1) * each].transpose(1, 0, 2).reshape(share, groups * each) for i in range(pieces)]

    def rows_kept(grad):
        half = lax.psum_scatter(grad.astype(bf16), CORE, scatter_dimension=0, tiled=True)
        return lax.psum(half, SP).astype(f32)

    e_wq, e_wk, e_wv = rows_back(dw_eqkv, 3)
    e_wg, e_wu = rows_back(dw_egu, 2)
    d_wq, d_wk, d_wv = rows_back(dw_dqkv, 3)
    c_wq, c_wk, c_wv = rows_back(jnp.concatenate([dw_cq, dw_ckv], axis=1), 3)
    d_wg, d_wu = rows_back(dw_dgu, 2)
    e_wo, d_wo, c_wo = rows_kept(dw_eproj), rows_kept(dw_dproj), rows_kept(dw_cproj)
    e_wd, d_wd = rows_kept(dw_edown), rows_kept(dw_ddown)

    def fold(tab, onehot):
        strips, edges = tab
        keys = strips.shape[1]
        flipped = strips[:, :, ::-1].transpose(0, 2, 1)
        span = keys + block
        wide = jnp.pad(flipped, ((0, 0), (0, 0), (0, block)))
        flat = wide.reshape(heads, block * span)[:, : block * (span - 1)]
        by_distance = jnp.sum(flat.reshape(heads, block, span - 1), axis=1)
        shift = block - 1 + BLOCK_PAD - reach
        size = 2 * reach + 1
        inner = by_distance[:, shift : shift + size]
        low = jnp.sum(by_distance[:, :shift], axis=1)
        high = jnp.sum(by_distance[:, shift + size :], axis=1)
        sides = jnp.sum(edges, axis=1).reshape(heads, 2)
        inner = inner.at[:, 0].add(low + sides[:, 0]).at[:, -1].add(high + sides[:, 1])
        full = jnp.zeros((HEADS, size), f32)
        full = lax.dynamic_update_slice_in_dim(full, inner, my_group * heads, 0)
        return jnp.dot(onehot.T, full.T, precision=HIGHEST).reshape(-1)

    small_grads = [dg_e1, dg_e2, dg_ef, dg_d1, dg_d2, dg_d3, fold(enc_tab, enc_onehot), fold(dec_tab, dec_onehot)]
    packed = jnp.concatenate([v.reshape(groups * cores, -1) for v in small_grads], axis=1)
    summed = lax.psum(packed, (HG, CORE, SP))
    own = lax.dynamic_index_in_dim(summed, my_group * cores + my_core, 0, False)
    s = [own[i * share : (i + 1) * share] for i in range(6)]
    e_rel, d_rel = own[6 * share : 6 * share + rel_len], own[6 * share + rel_len :]
    return (
        enc_out, dec_out, enc_in_grad, dec_in_grad,
        s[0], e_wq, e_wk, e_wv, e_wo, e_rel, s[1], e_wg, e_wu, e_wd, s[2],
        s[3], d_wq, d_wk, d_wv, d_wo, d_rel, s[4], c_wq, c_wk, c_wv, c_wo, s[5], d_wg, d_wu, d_wd,
    )


def general_plan(mesh):
    placed = (
        P(("ctx", "sp"), None),
        P(("ctx", "sp"), None),
        P(("ctx", "sp"), None),
        P(("ctx", "sp"), None),
        P(),
        P(),
        P(),
        P("ctx"),
        P("ctx", None),
        P("ctx", None),
        P("ctx", None),
        P("ctx", None),
        P("ctx"),
        P("ctx"),
        P("ctx", None),
        P("ctx", None),
        P("ctx", None),
        P("ctx"),
        P("ctx"),
        P("ctx", None),
        P("ctx", None),
        P("ctx", None),
        P("ctx", None),
        P("ctx"),
        P("ctx"),
        P("ctx", None),
        P("ctx", None),
        P("ctx", None),
        P("ctx", None),
        P("ctx"),
        P("ctx", None),
        P("ctx", None),
        P("ctx", None),
    )
    return jax.shard_map(
        per_device,
        mesh=mesh,
        in_specs=placed,
        out_specs=(
            P(("ctx", "sp"), None),
            P(("ctx", "sp"), None),
            P(("ctx", "sp"), None),
            P(("ctx", "sp"), None),
            P("ctx"),
            P("ctx", None),
            P("ctx", None),
            P("ctx", None),
            P("ctx", None),
            P("ctx"),
            P("ctx"),
            P("ctx", None),
            P("ctx", None),
            P("ctx", None),
            P("ctx"),
            P("ctx"),
            P("ctx", None),
            P("ctx", None),
            P("ctx", None),
            P("ctx", None),
            P("ctx"),
            P("ctx"),
            P("ctx", None),
            P("ctx", None),
            P("ctx", None),
            P("ctx", None),
            P("ctx"),
            P("ctx", None),
            P("ctx", None),
            P("ctx", None),
        ),
        check_vma=False,
    )


def split_plan(mesh, groups):
    cut = Mesh(np.asarray(mesh.devices).reshape(groups, 2, mesh.shape["sp"]), (HG, CORE, SP))
    tokens, rows, gain, same = P((HG, CORE, SP), None), P((HG, CORE), None), P((HG, CORE)), P()
    attention = (gain, rows, rows, rows, rows, gain)
    feed = (gain, rows, rows, rows)
    weights = attention + feed + (gain,) + attention + (gain, rows, rows, rows, rows) + feed
    return jax.shard_map(
        fast_device,
        mesh=cut,
        in_specs=(tokens,) * 4 + (same,) * 3 + weights,
        out_specs=(tokens,) * 4 + weights,
        check_vma=False,
    )


def solution(mesh):
    groups, odd = divmod(mesh.shape["ctx"], 2)
    if odd or HEADS % groups:
        return general_plan(mesh)
    return split_plan(mesh, groups)
```

```python
import functools
import math

import jax
import jax.numpy as jnp
import numpy as np
from jax import lax
from jax.experimental import pallas as pl
from jax.experimental.pallas import tpu as pltpu
from jax.sharding import Mesh
from jax.sharding import PartitionSpec as P

HEADS = 12
HD = 64


EPSILON = 1e-06
NEGATIVE = -1e30
HIGHEST = lax.Precision.HIGHEST


def rms_norm(values, norm_gain):
    return (
        values * lax.rsqrt(jnp.mean(values * values, axis=-1, keepdims=True) + EPSILON) * norm_gain
    )


def norm_pullback(values, norm_gain, grad_normed):
    _, pullback = jax.vjp(rms_norm, values, norm_gain)
    return pullback(grad_normed)


def gated(gate_val, up_val):
    return jax.nn.gelu(gate_val, approximate=True) * up_val


def project(left, right):
    return jnp.dot(left, right, preferred_element_type=jnp.float32)


def weight_grad(left, right):
    return jnp.einsum("td,te->de", left, right, preferred_element_type=jnp.float32)


def input_grad(grad_out, weight):
    return jnp.einsum("te,de->td", grad_out, weight, preferred_element_type=jnp.float32)


def head_table(relative, table_row, heads_here):
    bucket_count = relative.shape[0] // HEADS
    onehot = (table_row[:, None] == jnp.arange(bucket_count, dtype=jnp.int32)[None, :]).astype(
        jnp.float32
    )
    bias_grid = relative.astype(jnp.float32).reshape(bucket_count, HEADS)
    full_table = jnp.dot(onehot, bias_grid, precision=HIGHEST).T
    first_head = lax.axis_index("sp") * heads_here
    return (lax.dynamic_slice_in_dim(full_table, first_head, heads_here, 0), onehot)


def table_grad(grad_table, onehot, heads_here):
    full_grad = jnp.zeros((HEADS, onehot.shape[0]), jnp.float32)
    full_grad = lax.dynamic_update_slice_in_dim(
        full_grad, grad_table, lax.axis_index("sp") * heads_here, 0
    )
    return jnp.dot(onehot.T, full_grad.T, precision=HIGHEST).reshape(-1)


def bias_block(head_bias, pad_len, offset_q, rows, offset_k, cols):
    head_count, table_len = head_bias.shape
    reach_len = (table_len - 1) // 2
    left_edge = jnp.broadcast_to(head_bias[:, :1], (head_count, pad_len))
    right_edge = jnp.broadcast_to(head_bias[:, -1:], (head_count, pad_len))
    padded = jnp.concatenate([left_edge, head_bias, right_edge], axis=1)
    band_width = rows + cols - 1
    start = offset_k - offset_q - (rows - 1) + reach_len + pad_len
    band = lax.dynamic_slice_in_dim(padded, start, band_width, 1)
    tiled = jnp.broadcast_to(band[:, None, :], (head_count, rows, band_width)).reshape(
        head_count, rows * band_width
    )
    skewed = tiled[:, rows - 1 : rows - 1 + rows * (band_width - 1)].reshape(
        head_count, rows, band_width - 1
    )
    return skewed[:, :, :cols]


def make_frame(query_local, query_ids, key_ids, head_bias, causal):
    local_len = query_local.shape[0]
    heads_here = query_local.shape[1] // HD
    offset_q = lax.axis_index("ctx") * local_len
    ids_q = lax.dynamic_slice_in_dim(query_ids, offset_q, local_len, 0)
    row_ids = offset_q + jnp.arange(local_len, dtype=jnp.int32)
    query_heads = query_local.reshape(local_len, heads_here, HD)
    pad_len = query_ids.shape[0] + key_ids.shape[0]

    def bias_of(entries, offset_k, length):
        return bias_block(entries, pad_len, offset_q, local_len, offset_k, length)

    def scores_of(key_block, offset_k):
        length = key_block.shape[0]
        key_heads = key_block.reshape(length, heads_here, HD)
        raw_scores = jnp.einsum(
            "qhd,khd->hqk", query_heads, key_heads, preferred_element_type=jnp.float32
        )
        col_ids = offset_k + jnp.arange(length, dtype=jnp.int32)
        ids_k = lax.dynamic_slice_in_dim(key_ids, offset_k, length, 0)
        allowed = ids_q[:, None] == ids_k[None, :]
        if causal:
            allowed = allowed & (col_ids[None, :] <= row_ids[:, None])
        if head_bias is not None:
            raw_scores = raw_scores + bias_of(head_bias, offset_k, length)
        return (raw_scores, allowed)

    def touches(offset_k, length):
        first_id = lax.dynamic_slice_in_dim(key_ids, offset_k, 1, 0)[0]
        last_id = lax.dynamic_slice_in_dim(key_ids, offset_k + length - 1, 1, 0)[0]
        touched = (ids_q[0] <= last_id) & (first_id <= ids_q[-1])
        if causal:
            touched = touched & (offset_k <= offset_q + local_len - 1)
        return touched

    return (query_heads, scores_of, touches, bias_of)


def sweep(keys_gathered, local_len, step_fn, carry_state):
    key_all, value_all = keys_gathered
    block_len = local_len * math.gcd(4, lax.axis_size("ctx"))

    def sweep_loop_body(number, running):
        offset_k = number * block_len
        key_block = lax.dynamic_slice_in_dim(key_all, offset_k, block_len, 0)
        value_block = lax.dynamic_slice_in_dim(value_all, offset_k, block_len, 0)
        return step_fn(running, key_block, value_block, offset_k)

    return lax.fori_loop(0, key_all.shape[0] // block_len, sweep_loop_body, carry_state)


def whole_keys(key_local, value_local):
    return (
        lax.all_gather(key_local, "ctx", axis=0, tiled=True),
        lax.all_gather(value_local, "ctx", axis=0, tiled=True),
    )


def attention_forward(query_proj, key_proj, value_proj, query_ids, key_ids, head_bias, causal):
    query_local, key_local, value_local = (
        lax.all_to_all(query_proj, "sp", split_axis=1, concat_axis=0, tiled=True),
        lax.all_to_all(key_proj, "sp", split_axis=1, concat_axis=0, tiled=True),
        lax.all_to_all(value_proj, "sp", split_axis=1, concat_axis=0, tiled=True),
    )
    local_len = query_local.shape[0]
    heads_here = query_local.shape[1] // HD
    query_heads, scores_of, touches, _ = make_frame(
        query_local, query_ids, key_ids, head_bias, causal
    )
    key_block = lax.all_gather(key_local, "ctx", axis=0, tiled=True)
    value_block = lax.all_gather(value_local, "ctx", axis=0, tiled=True)
    offset_k = jnp.int32(0)
    length = key_block.shape[0]
    row_top = jnp.full((heads_here, local_len), NEGATIVE, jnp.float32)
    weighted = jnp.zeros((local_len, heads_here, HD), jnp.float32)
    raw_scores, allowed = scores_of(key_block, offset_k)
    masked = jnp.where(allowed[None], raw_scores, NEGATIVE)
    new_top = jnp.maximum(row_top, jnp.max(masked, axis=-1))
    weights = jnp.where(allowed[None], jnp.exp(masked - new_top[..., None]), 0.0)
    rescale = jnp.exp(row_top - new_top)
    value_heads = value_block.reshape(length, heads_here, HD)
    increment = jnp.einsum(
        "hqk,khd->qhd",
        weights.astype(jnp.bfloat16),
        value_heads,
        preferred_element_type=jnp.float32,
    )
    row_top, row_total, weighted = (
        new_top,
        jnp.sum(weights, axis=-1),
        weighted * rescale.T[:, :, None] + increment,
    )
    mixed_heads = weighted / row_total.T[:, :, None]
    log_total = row_top + jnp.log(row_total)
    mixed_low = mixed_heads.reshape(local_len, heads_here * HD).astype(jnp.bfloat16)
    mixed_tokens = lax.all_to_all(mixed_low, "sp", split_axis=0, concat_axis=1, tiled=True)
    retained = (
        query_local,
        key_local,
        value_local,
        mixed_heads,
        log_total,
        None,
        query_ids,
        key_ids,
        head_bias,
        causal,
    )
    return (mixed_tokens, retained)


def attention_backward(grad_mixed, retained):
    (
        query_local,
        key_local,
        value_local,
        mixed_heads,
        log_total,
        gathered,
        query_ids,
        key_ids,
        head_bias,
        causal,
    ) = retained
    grad_local = lax.all_to_all(grad_mixed, "sp", split_axis=1, concat_axis=0, tiled=True)
    local_len = query_local.shape[0]
    heads_here = query_local.shape[1] // HD
    width = heads_here * HD
    query_heads, scores_of, touches, bias_of = make_frame(
        query_local, query_ids, key_ids, head_bias, causal
    )
    grad_heads = grad_local.reshape(local_len, heads_here, HD)
    row_inner = jnp.einsum("qhd,qhd->hq", grad_heads.astype(jnp.float32), mixed_heads)
    gathered = whole_keys(key_local, value_local)
    table_zero = jnp.zeros(head_bias.shape if head_bias is not None else (1,), jnp.float32)

    def gradients_of(key_block, value_block, offset_k):
        length = key_block.shape[0]
        raw_scores, allowed = scores_of(key_block, offset_k)
        probabilities = jnp.where(allowed[None], jnp.exp(raw_scores - log_total[..., None]), 0.0)
        value_heads = value_block.reshape(length, heads_here, HD)
        grad_probs = jnp.einsum(
            "qhd,khd->hqk", grad_heads, value_heads, preferred_element_type=jnp.float32
        )
        grad_scores = (probabilities * (grad_probs - row_inner[..., None])).astype(jnp.bfloat16)
        return (probabilities, grad_scores)

    def table_part(grad_scores, offset_k, length):
        if head_bias is None:
            return table_zero
        _, pullback = jax.vjp(lambda entries: bias_of(entries, offset_k, length), head_bias)
        return pullback(grad_scores.astype(jnp.float32))[0]

    def key_terms_of(probabilities, grad_scores, length):
        grad_key = jnp.einsum(
            "hqk,qhd->khd", grad_scores, query_heads, preferred_element_type=jnp.float32
        )
        grad_value = jnp.einsum(
            "hqk,qhd->khd",
            probabilities.astype(jnp.bfloat16),
            grad_heads,
            preferred_element_type=jnp.float32,
        )
        return jnp.concatenate(
            [grad_key.reshape(length, width), grad_value.reshape(length, width)], axis=1
        )

    def query_part(grad_scores, key_block):
        length = key_block.shape[0]
        key_heads = key_block.reshape(length, heads_here, HD)
        return jnp.einsum(
            "hqk,khd->qhd", grad_scores, key_heads, preferred_element_type=jnp.float32
        )

    def query_step(running, key_block, value_block, offset_k):
        length = key_block.shape[0]
        grad_query, grad_table = running
        probabilities, grad_scores = gradients_of(key_block, value_block, offset_k)
        return (
            grad_query + query_part(grad_scores, key_block),
            grad_table + table_part(grad_scores, offset_k, length),
        )

    query_zero = jnp.zeros((local_len, heads_here, HD), jnp.float32)
    block_len = local_len * math.gcd(4, lax.axis_size("ctx"))
    grad_query, grad_table = sweep(gathered, local_len, query_step, (query_zero, table_zero))
    key_all, value_all = gathered
    step_len = math.gcd(lax.axis_size("ctx") * local_len, block_len)

    def term_loop_body(number, rows_acc):
        offset_b = number * step_len
        key_block = lax.dynamic_slice_in_dim(key_all, offset_b, step_len, 0)
        value_block = lax.dynamic_slice_in_dim(value_all, offset_b, step_len, 0)
        probabilities, grad_scores = gradients_of(key_block, value_block, offset_b)
        return lax.dynamic_update_slice_in_dim(
            rows_acc, key_terms_of(probabilities, grad_scores, step_len), number * step_len, 0
        )

    own_rows = lax.psum_scatter(
        lax.fori_loop(
            0,
            lax.axis_size("ctx") * local_len // step_len,
            term_loop_body,
            jnp.zeros((lax.axis_size("ctx") * local_len, 2 * width), jnp.float32),
        ),
        "ctx",
        scatter_dimension=0,
        tiled=True,
    )
    grad_q_low = grad_query.reshape(local_len, width).astype(jnp.bfloat16)
    grad_k_low = own_rows[:, :width].astype(jnp.bfloat16)
    grad_v_low = own_rows[:, width:].astype(jnp.bfloat16)
    grad_q_tok, grad_k_tok, grad_v_tok = (
        lax.all_to_all(grad_q_low, "sp", split_axis=0, concat_axis=1, tiled=True),
        lax.all_to_all(grad_k_low, "sp", split_axis=0, concat_axis=1, tiled=True),
        lax.all_to_all(grad_v_low, "sp", split_axis=0, concat_axis=1, tiled=True),
    )
    return (grad_q_tok, grad_k_tok, grad_v_tok, grad_table)


def attention_layer(
    residual,
    source,
    norm_gain,
    w_query,
    w_key,
    w_value,
    w_proj,
    query_ids,
    key_ids,
    head_bias,
    causal,
):
    normed = rms_norm(residual, norm_gain).astype(jnp.bfloat16)
    kv_input = normed if source is None else source
    query_proj = project(normed, w_query).astype(jnp.bfloat16)
    key_proj = project(kv_input, w_key).astype(jnp.bfloat16)
    value_proj = project(kv_input, w_value).astype(jnp.bfloat16)
    mixed_tokens, retained = attention_forward(
        query_proj, key_proj, value_proj, query_ids, key_ids, head_bias, causal
    )
    result = residual + project(mixed_tokens, w_proj)
    return (result, (residual, normed, kv_input, mixed_tokens, retained))


def attention_layer_back(grad_out, saved, norm_gain, w_query, w_key, w_value, w_proj, is_cross):
    residual, normed, kv_input, mixed_tokens, retained = saved
    grad_low = grad_out.astype(jnp.bfloat16)
    grad_proj = weight_grad(mixed_tokens, grad_low)
    grad_mixed = input_grad(grad_low, w_proj).astype(jnp.bfloat16)
    grad_q_tok, grad_k_tok, grad_v_tok, grad_table = attention_backward(grad_mixed, retained)
    grad_wq = weight_grad(normed, grad_q_tok)
    grad_wk = weight_grad(kv_input, grad_k_tok)
    grad_wv = weight_grad(kv_input, grad_v_tok)
    grad_source = input_grad(grad_k_tok, w_key) + input_grad(grad_v_tok, w_value)
    grad_normed = input_grad(grad_q_tok, w_query)
    if not is_cross:
        grad_normed = grad_normed + grad_source
        grad_source = None
    grad_resid, grad_gain = norm_pullback(residual, norm_gain, grad_normed)
    return (
        grad_out + grad_resid,
        grad_source,
        (grad_gain, grad_wq, grad_wk, grad_wv, grad_proj, grad_table),
    )


def feed_layer(residual, norm_gain, w_gate, w_up, w_down):
    normed = rms_norm(residual, norm_gain).astype(jnp.bfloat16)
    gate_val = project(normed, w_gate)
    up_val = project(normed, w_up)
    hidden = gated(gate_val, up_val).astype(jnp.bfloat16)
    return (residual + project(hidden, w_down), (residual, normed, gate_val, up_val, hidden))


def feed_layer_back(grad_out, saved, norm_gain, w_gate, w_up, w_down):
    residual, normed, gate_val, up_val, hidden = saved
    grad_low = grad_out.astype(jnp.bfloat16)
    grad_down = weight_grad(hidden, grad_low)
    grad_hidden = input_grad(grad_low, w_down)
    _, pullback = jax.vjp(gated, gate_val, up_val)
    grad_gate, grad_up = pullback(grad_hidden)
    grad_gate = grad_gate.astype(jnp.bfloat16)
    grad_up = grad_up.astype(jnp.bfloat16)
    grad_wg = weight_grad(normed, grad_gate)
    grad_wu = weight_grad(normed, grad_up)
    grad_normed = input_grad(grad_gate, w_gate) + input_grad(grad_up, w_up)
    grad_resid, grad_gain = norm_pullback(residual, norm_gain, grad_normed)
    return (grad_out + grad_resid, (grad_gain, grad_wg, grad_wu, grad_down))


def per_device(
    enc_in,
    dec_in,
    enc_cot,
    dec_cot,
    enc_segments,
    dec_segments,
    buckets,
    enc_norm1,
    enc_query,
    enc_key,
    enc_value,
    enc_proj,
    enc_rel,
    enc_norm2,
    enc_gate,
    enc_up,
    enc_down,
    enc_final,
    dec_norm1,
    dec_query,
    dec_key,
    dec_value,
    dec_proj,
    dec_rel,
    dec_norm2,
    cross_query,
    cross_key,
    cross_value,
    cross_proj,
    dec_norm3,
    dec_gate,
    dec_up,
    dec_down,
):
    (
        enc_norm1,
        enc_query,
        enc_key,
        enc_value,
        enc_proj,
        enc_rel,
        enc_norm2,
        enc_gate,
        enc_up,
        enc_down,
        enc_final,
        dec_norm1,
        dec_query,
        dec_key,
        dec_value,
        dec_proj,
        dec_rel,
        dec_norm2,
        cross_query,
        cross_key,
        cross_value,
        cross_proj,
        dec_norm3,
        dec_gate,
        dec_up,
        dec_down,
    ) = (
        lax.all_gather(enc_norm1, "ctx", axis=0, tiled=True),
        lax.all_gather(enc_query, "ctx", axis=0, tiled=True),
        lax.all_gather(enc_key, "ctx", axis=0, tiled=True),
        lax.all_gather(enc_value, "ctx", axis=0, tiled=True),
        lax.all_gather(enc_proj, "ctx", axis=0, tiled=True),
        lax.all_gather(enc_rel, "ctx", axis=0, tiled=True),
        lax.all_gather(enc_norm2, "ctx", axis=0, tiled=True),
        lax.all_gather(enc_gate, "ctx", axis=0, tiled=True),
        lax.all_gather(enc_up, "ctx", axis=0, tiled=True),
        lax.all_gather(enc_down, "ctx", axis=0, tiled=True),
        lax.all_gather(enc_final, "ctx", axis=0, tiled=True),
        lax.all_gather(dec_norm1, "ctx", axis=0, tiled=True),
        lax.all_gather(dec_query, "ctx", axis=0, tiled=True),
        lax.all_gather(dec_key, "ctx", axis=0, tiled=True),
        lax.all_gather(dec_value, "ctx", axis=0, tiled=True),
        lax.all_gather(dec_proj, "ctx", axis=0, tiled=True),
        lax.all_gather(dec_rel, "ctx", axis=0, tiled=True),
        lax.all_gather(dec_norm2, "ctx", axis=0, tiled=True),
        lax.all_gather(cross_query, "ctx", axis=0, tiled=True),
        lax.all_gather(cross_key, "ctx", axis=0, tiled=True),
        lax.all_gather(cross_value, "ctx", axis=0, tiled=True),
        lax.all_gather(cross_proj, "ctx", axis=0, tiled=True),
        lax.all_gather(dec_norm3, "ctx", axis=0, tiled=True),
        lax.all_gather(dec_gate, "ctx", axis=0, tiled=True),
        lax.all_gather(dec_up, "ctx", axis=0, tiled=True),
        lax.all_gather(dec_down, "ctx", axis=0, tiled=True),
    )
    enc_norm1 = enc_norm1.astype(jnp.float32)
    enc_norm2 = enc_norm2.astype(jnp.float32)
    enc_final = enc_final.astype(jnp.float32)
    dec_norm1 = dec_norm1.astype(jnp.float32)
    dec_norm2 = dec_norm2.astype(jnp.float32)
    dec_norm3 = dec_norm3.astype(jnp.float32)
    heads_here = HEADS // lax.axis_size("sp")
    enc_table, enc_onehot = head_table(enc_rel, buckets[0], heads_here)
    dec_table, dec_onehot = head_table(dec_rel, buckets[1], heads_here)
    enc_x = enc_in.astype(jnp.float32)
    enc_mid, enc_saved_a = attention_layer(
        enc_x,
        None,
        enc_norm1,
        enc_query,
        enc_key,
        enc_value,
        enc_proj,
        enc_segments,
        enc_segments,
        enc_table,
        False,
    )
    enc_result, enc_saved_f = feed_layer(enc_mid, enc_norm2, enc_gate, enc_up, enc_down)
    memory = rms_norm(enc_result, enc_final).astype(jnp.bfloat16)
    dec_x = dec_in.astype(jnp.float32)
    dec_mid, dec_saved_a = attention_layer(
        dec_x,
        None,
        dec_norm1,
        dec_query,
        dec_key,
        dec_value,
        dec_proj,
        dec_segments,
        dec_segments,
        dec_table,
        True,
    )
    dec_cross, dec_saved_c = attention_layer(
        dec_mid,
        memory,
        dec_norm2,
        cross_query,
        cross_key,
        cross_value,
        cross_proj,
        dec_segments,
        enc_segments,
        None,
        False,
    )
    dec_result, dec_saved_f = feed_layer(dec_cross, dec_norm3, dec_gate, dec_up, dec_down)
    grad_dec, dec_ff_grads = feed_layer_back(
        dec_cot.astype(jnp.float32), dec_saved_f, dec_norm3, dec_gate, dec_up, dec_down
    )
    grad_dec, grad_memory, cross_grads = attention_layer_back(
        grad_dec, dec_saved_c, dec_norm2, cross_query, cross_key, cross_value, cross_proj, True
    )
    grad_dec, _, dec_self_grads = attention_layer_back(
        grad_dec, dec_saved_a, dec_norm1, dec_query, dec_key, dec_value, dec_proj, False
    )
    grad_enc_out, grad_final = norm_pullback(enc_result, enc_final, grad_memory)
    grad_enc, enc_ff_grads = feed_layer_back(
        enc_cot.astype(jnp.float32) + grad_enc_out,
        enc_saved_f,
        enc_norm2,
        enc_gate,
        enc_up,
        enc_down,
    )
    grad_enc, _, enc_self_grads = attention_layer_back(
        grad_enc, enc_saved_a, enc_norm1, enc_query, enc_key, enc_value, enc_proj, False
    )
    e_gain1, e_wq, e_wk, e_wv, e_wo, e_table = enc_self_grads
    e_gain2, e_wg, e_wu, e_wd = enc_ff_grads
    d_gain1, d_wq, d_wk, d_wv, d_wo, d_table = dec_self_grads
    c_gain, c_wq, c_wk, c_wv, c_wo, _ = cross_grads
    d_gain3, d_wg, d_wu, d_wd = dec_ff_grads
    e_rel = table_grad(e_table, enc_onehot, heads_here)
    d_rel = table_grad(d_table, dec_onehot, heads_here)
    shards = (
        lax.psum_scatter(e_gain1, "ctx", scatter_dimension=0, tiled=True),
        lax.psum_scatter(e_wq, "ctx", scatter_dimension=0, tiled=True),
        lax.psum_scatter(e_wk, "ctx", scatter_dimension=0, tiled=True),
        lax.psum_scatter(e_wv, "ctx", scatter_dimension=0, tiled=True),
        lax.psum_scatter(e_wo, "ctx", scatter_dimension=0, tiled=True),
        lax.psum_scatter(e_rel, "ctx", scatter_dimension=0, tiled=True),
        lax.psum_scatter(e_gain2, "ctx", scatter_dimension=0, tiled=True),
        lax.psum_scatter(e_wg, "ctx", scatter_dimension=0, tiled=True),
        lax.psum_scatter(e_wu, "ctx", scatter_dimension=0, tiled=True),
        lax.psum_scatter(e_wd, "ctx", scatter_dimension=0, tiled=True),
        lax.psum_scatter(grad_final, "ctx", scatter_dimension=0, tiled=True),
        lax.psum_scatter(d_gain1, "ctx", scatter_dimension=0, tiled=True),
        lax.psum_scatter(d_wq, "ctx", scatter_dimension=0, tiled=True),
        lax.psum_scatter(d_wk, "ctx", scatter_dimension=0, tiled=True),
        lax.psum_scatter(d_wv, "ctx", scatter_dimension=0, tiled=True),
        lax.psum_scatter(d_wo, "ctx", scatter_dimension=0, tiled=True),
        lax.psum_scatter(d_rel, "ctx", scatter_dimension=0, tiled=True),
        lax.psum_scatter(c_gain, "ctx", scatter_dimension=0, tiled=True),
        lax.psum_scatter(c_wq, "ctx", scatter_dimension=0, tiled=True),
        lax.psum_scatter(c_wk, "ctx", scatter_dimension=0, tiled=True),
        lax.psum_scatter(c_wv, "ctx", scatter_dimension=0, tiled=True),
        lax.psum_scatter(c_wo, "ctx", scatter_dimension=0, tiled=True),
        lax.psum_scatter(d_gain3, "ctx", scatter_dimension=0, tiled=True),
        lax.psum_scatter(d_wg, "ctx", scatter_dimension=0, tiled=True),
        lax.psum_scatter(d_wu, "ctx", scatter_dimension=0, tiled=True),
        lax.psum_scatter(d_wd, "ctx", scatter_dimension=0, tiled=True),
    )
    (
        s_gain1,
        s_wq,
        s_wk,
        s_wv,
        s_wo,
        s_rel,
        s_gain2,
        s_wg,
        s_wu,
        s_wd,
        s_final,
        t_gain1,
        t_wq,
        t_wk,
        t_wv,
        t_wo,
        t_rel,
        t_gain2,
        t_cq,
        t_ck,
        t_cv,
        t_co,
        t_gain3,
        t_wg,
        t_wu,
        t_wd,
    ) = shards
    reduced = (
        lax.psum(s_gain1.astype(jnp.bfloat16), "sp").astype(jnp.float32),
        lax.psum(s_wq.astype(jnp.bfloat16), "sp").astype(jnp.float32),
        lax.psum(s_wk.astype(jnp.bfloat16), "sp").astype(jnp.float32),
        lax.psum(s_wv.astype(jnp.bfloat16), "sp").astype(jnp.float32),
        lax.psum(s_wo.astype(jnp.bfloat16), "sp").astype(jnp.float32),
        lax.psum(s_rel.astype(jnp.bfloat16), "sp").astype(jnp.float32),
        lax.psum(s_gain2.astype(jnp.bfloat16), "sp").astype(jnp.float32),
        lax.psum(s_wg.astype(jnp.bfloat16), "sp").astype(jnp.float32),
        lax.psum(s_wu.astype(jnp.bfloat16), "sp").astype(jnp.float32),
        lax.psum(s_wd.astype(jnp.bfloat16), "sp").astype(jnp.float32),
        lax.psum(s_final.astype(jnp.bfloat16), "sp").astype(jnp.float32),
        lax.psum(t_gain1.astype(jnp.bfloat16), "sp").astype(jnp.float32),
        lax.psum(t_wq.astype(jnp.bfloat16), "sp").astype(jnp.float32),
        lax.psum(t_wk.astype(jnp.bfloat16), "sp").astype(jnp.float32),
        lax.psum(t_wv.astype(jnp.bfloat16), "sp").astype(jnp.float32),
        lax.psum(t_wo.astype(jnp.bfloat16), "sp").astype(jnp.float32),
        lax.psum(t_rel.astype(jnp.bfloat16), "sp").astype(jnp.float32),
        lax.psum(t_gain2.astype(jnp.bfloat16), "sp").astype(jnp.float32),
        lax.psum(t_cq.astype(jnp.bfloat16), "sp").astype(jnp.float32),
        lax.psum(t_ck.astype(jnp.bfloat16), "sp").astype(jnp.float32),
        lax.psum(t_cv.astype(jnp.bfloat16), "sp").astype(jnp.float32),
        lax.psum(t_co.astype(jnp.bfloat16), "sp").astype(jnp.float32),
        lax.psum(t_gain3.astype(jnp.bfloat16), "sp").astype(jnp.float32),
        lax.psum(t_wg.astype(jnp.bfloat16), "sp").astype(jnp.float32),
        lax.psum(t_wu.astype(jnp.bfloat16), "sp").astype(jnp.float32),
        lax.psum(t_wd.astype(jnp.bfloat16), "sp").astype(jnp.float32),
    )
    return (enc_result, dec_result, grad_enc, grad_dec) + tuple(reduced)


HG, CORE, SP = "hg", "core", "sp"
BLOCK_PAD = 128


def nt(left, right):
    return lax.dot_general(left, right, (((1,), (1,)), ((), ())), preferred_element_type=jnp.float32)


def tn(left, right):
    return lax.dot_general(left, right, (((0,), (0,)), ((), ())), preferred_element_type=jnp.float32)


def nn(left, right):
    return jnp.dot(left, right, preferred_element_type=jnp.float32)


def identity(size):
    rows = lax.broadcasted_iota(jnp.int32, (size, size), 0)
    cols = lax.broadcasted_iota(jnp.int32, (size, size), 1)
    return jnp.where(rows == cols, 1.0, 0.0).astype(jnp.bfloat16)


def only_head(array, head):
    lanes = lax.broadcasted_iota(jnp.int32, array.shape, 1)
    keep = (lanes >= head * HD) & (lanes < (head + 1) * HD)
    return jnp.where(keep, array, jnp.zeros_like(array))


def bias_mask_kernel(heads, block, causal, starts_ref, tables_ref, kdoc_ref, qdoc_ref, qpos_ref, qstart_ref, out_ref):
    rows_total, lanes = out_ref.shape[1], out_ref.shape[2]
    key_len = kdoc_ref.shape[0]
    strip = block + 2 * BLOCK_PAD
    for head in range(heads):
        if tables_ref is not None:
            row = tables_ref[head : head + 1, :]
            width = row.shape[1]
            left, right = tables_ref[head : head + 1, width - 2 : width - 1], tables_ref[head : head + 1, 0:1]
            places = lax.broadcasted_iota(jnp.int32, (rows_total, lanes), 0)
            fill = jnp.where(places < qstart_ref[...], left, right)
            out_ref[head] = fill.astype(jnp.bfloat16)
            wide = jnp.broadcast_to(row, (strip, width))
            for number in range(lanes // block):
                at = (number * block) % 128
                turned = pltpu.roll(wide, (width - (strip - 1) + at) % width, 1, stride=1, stride_axis=0)
                out_ref[head, pl.ds(pl.multiple_of(starts_ref[number], block), strip), number * block : (number + 1) * block] = turned[:, at : at + block].astype(jnp.bfloat16)
        allowed = kdoc_ref[...] == qdoc_ref[...]
        if causal:
            places = lax.broadcasted_iota(jnp.int32, (key_len, lanes), 0)
            allowed = allowed & (places <= qpos_ref[...])
        inside = pl.ds(BLOCK_PAD, key_len)
        if tables_ref is not None:
            out_ref[head, inside, :] = jnp.where(allowed, out_ref[head, inside, :].astype(jnp.float32), NEGATIVE).astype(jnp.bfloat16)
        else:
            out_ref[head, inside, :] = jnp.where(allowed, 0.0, NEGATIVE).astype(jnp.bfloat16)


def bias_mask(starts, tables, kdoc, qdoc, qpos, block, causal):
    key_len, lanes = kdoc.shape[0], qdoc.shape[1]
    heads = tables.shape[0] if tables is not None else 1
    qstart = jnp.repeat(starts, block)[None, :]
    operands = [starts] + ([tables] if tables is not None else []) + [kdoc, qdoc, qpos, qstart]

    def body(*refs):
        refs = list(refs)
        if tables is None:
            refs.insert(1, None)
        bias_mask_kernel(heads, block, causal, *refs)

    return pl.pallas_call(
        body,
        out_shape=jax.ShapeDtypeStruct((heads, key_len + 2 * BLOCK_PAD, lanes), jnp.bfloat16),
        in_specs=[pl.BlockSpec(memory_space=pltpu.SMEM)] + [pl.BlockSpec(memory_space=pltpu.VMEM)] * (len(operands) - 1),
        out_specs=pl.BlockSpec(memory_space=pltpu.VMEM),
        compiler_params=pltpu.CompilerParams(vmem_limit_bytes=VMEM_BYTES),
    )(*operands)


VMEM_BYTES = 56 << 20
ROWS = 512


def head_scores(k_ref, masked_q, bm_ref, head, at):
    bias_head = head if bm_ref.shape[0] > 1 else 0
    bias = bm_ref[bias_head, pl.ds(pl.multiple_of(BLOCK_PAD + at, 128), ROWS), :].astype(jnp.float32)
    return nt(k_ref[pl.ds(at, ROWS), :], masked_q) + bias


def mix_kernel(q_ref, k_ref, v_ref, bm_ref, o_ref, lse_ref, s_ref, p_ref, ot_ref):
    key_len, width = k_ref.shape
    lanes = q_ref.shape[0]
    vt = nt(identity(width), v_ref[...]).astype(jnp.bfloat16)
    for head in range(width // HD):
        masked_q = only_head(q_ref[...], head)

        def first(number, top):
            at = pl.multiple_of(number * ROWS, ROWS)
            scores = head_scores(k_ref, masked_q, bm_ref, head, at)
            s_ref[pl.ds(at, ROWS), :] = scores
            return jnp.maximum(top, jnp.max(scores, axis=0, keepdims=True))

        top = lax.fori_loop(0, key_len // ROWS, first, jnp.full((1, lanes), NEGATIVE, jnp.float32))

        def second(number, total):
            at = pl.multiple_of(number * ROWS, ROWS)
            weights = jnp.exp(s_ref[pl.ds(at, ROWS), :] - top)
            p_ref[pl.ds(at, ROWS), :] = weights.astype(jnp.bfloat16)
            return total + jnp.sum(weights, axis=0, keepdims=True)

        total = lax.fori_loop(0, key_len // ROWS, second, jnp.zeros((1, lanes), jnp.float32))
        lse_ref[:, head * lanes : (head + 1) * lanes] = top + jnp.log(total)
        mixed = nn(vt[head * HD : (head + 1) * HD], p_ref[...])
        ot_ref[head * HD : (head + 1) * HD, :] = (mixed / total).astype(jnp.bfloat16)
    o_ref[...] = nt(identity(lanes), ot_ref[...]).astype(jnp.bfloat16)


def mix(q, k, v, bm):
    lanes, width = q.shape
    heads = width // HD
    return pl.pallas_call(
        mix_kernel,
        out_shape=(
            jax.ShapeDtypeStruct((lanes, width), jnp.bfloat16),
            jax.ShapeDtypeStruct((1, heads * lanes), jnp.float32),
        ),
        in_specs=[pl.BlockSpec(memory_space=pltpu.VMEM)] * 4,
        out_specs=(pl.BlockSpec(memory_space=pltpu.VMEM),) * 2,
        scratch_shapes=[
            pltpu.VMEM((k.shape[0], lanes), jnp.float32),
            pltpu.VMEM((k.shape[0], lanes), jnp.bfloat16),
            pltpu.VMEM((width, lanes), jnp.bfloat16),
        ],
        compiler_params=pltpu.CompilerParams(vmem_limit_bytes=VMEM_BYTES),
    )(q, k, v, bm)


def mix_back_kernel(block, starts_ref, q_ref, k_ref, v_ref, do_ref, lse_ref, bm_ref, qstart_ref, dq_ref, dk_ref, dv_ref, strip_ref, edge_ref, p_ref, dp_ref, ds_ref, pb_ref, ot_ref):
    key_len, width = k_ref.shape
    lanes = q_ref.shape[0]
    heads = width // HD
    biased = strip_ref is not None
    strip = block + 2 * BLOCK_PAD
    kt = nt(identity(width), k_ref[...]).astype(jnp.bfloat16)
    if biased:
        none = jnp.zeros((BLOCK_PAD, heads * lanes), jnp.bfloat16)
        ds_ref[0:BLOCK_PAD, :] = none
        ds_ref[BLOCK_PAD + key_len :, :] = none
    for head in range(heads):
        masked_q = only_head(q_ref[...], head)
        masked_do = only_head(do_ref[...], head)
        across = slice(head * lanes, (head + 1) * lanes)

        def first(number, inner):
            at = pl.multiple_of(number * ROWS, ROWS)
            p = jnp.exp(head_scores(k_ref, masked_q, bm_ref, head, at) - lse_ref[:, across])
            dp = nt(v_ref[pl.ds(at, ROWS), :], masked_do)
            p_ref[pl.ds(at, ROWS), :] = p
            dp_ref[pl.ds(at, ROWS), :] = dp
            pb_ref[pl.ds(at, ROWS), across] = p.astype(jnp.bfloat16)
            return inner + jnp.sum(p * dp, axis=0, keepdims=True)

        inner = lax.fori_loop(0, key_len // ROWS, first, jnp.zeros((1, lanes), jnp.float32))

        def second(number, sums):
            at = pl.multiple_of(number * ROWS, ROWS)
            ds = (p_ref[pl.ds(at, ROWS), :] * (dp_ref[pl.ds(at, ROWS), :] - inner)).astype(jnp.bfloat16)
            ds_ref[pl.ds(BLOCK_PAD + at, ROWS), across] = ds
            if not biased:
                return sums
            wide = ds.astype(jnp.float32)
            places = lax.broadcasted_iota(jnp.int32, wide.shape, 0) + (at + BLOCK_PAD)
            left = jnp.sum(jnp.where(places < qstart_ref[...], wide, 0.0), axis=0, keepdims=True)
            right = jnp.sum(jnp.where(places >= qstart_ref[...] + strip, wide, 0.0), axis=0, keepdims=True)
            return (sums[0] + left, sums[1] + right)

        nothing = jnp.zeros((1, lanes), jnp.float32)
        left, right = lax.fori_loop(0, key_len // ROWS, second, (nothing, nothing))
        if biased:
            edge_ref[2 * head : 2 * head + 1, :] = left
            edge_ref[2 * head + 1 : 2 * head + 2, :] = right
            total = jnp.zeros((strip, block), jnp.float32)
            for number in range(lanes // block):
                low = head * lanes + number * block
                rows = pl.ds(pl.multiple_of(starts_ref[number], block), strip)
                total = total + ds_ref[rows, low : low + block].astype(jnp.float32)
            strip_ref[head] = total
        back = nn(kt[head * HD : (head + 1) * HD], ds_ref[BLOCK_PAD : BLOCK_PAD + key_len, across])
        ot_ref[head * HD : (head + 1) * HD, :] = back.astype(jnp.bfloat16)
    dq_ref[...] = nt(identity(lanes), ot_ref[...]).astype(jnp.bfloat16)
    stacked_q = jnp.concatenate([only_head(q_ref[...], head) for head in range(heads)], axis=0)
    stacked_do = jnp.concatenate([only_head(do_ref[...], head) for head in range(heads)], axis=0)

    @pl.loop(0, key_len // ROWS)
    def _(number):
        at = pl.multiple_of(number * ROWS, ROWS)
        dk_ref[pl.ds(at, ROWS), :] = nn(ds_ref[pl.ds(BLOCK_PAD + at, ROWS), :], stacked_q).astype(dk_ref.dtype)
        dv_ref[pl.ds(at, ROWS), :] = nn(pb_ref[pl.ds(at, ROWS), :], stacked_do).astype(dv_ref.dtype)


def mix_back(starts, q, k, v, do, lse, bm, block, biased):
    lanes, width = q.shape
    key_len = k.shape[0]
    heads = width // HD
    qstart = jnp.repeat(starts, block)[None, :]
    shapes = [
        jax.ShapeDtypeStruct((lanes, width), jnp.bfloat16),
        jax.ShapeDtypeStruct((key_len, width), jnp.bfloat16),
        jax.ShapeDtypeStruct((key_len, width), jnp.bfloat16),
    ]
    if biased:
        shapes.append(jax.ShapeDtypeStruct((heads, block + 2 * BLOCK_PAD, block), jnp.float32))
        shapes.append(jax.ShapeDtypeStruct((2 * heads, lanes), jnp.float32))

    def body(*refs):
        refs = list(refs)
        if not biased:
            refs[11:11] = [None, None]
        mix_back_kernel(block, *refs)

    return pl.pallas_call(
        body,
        out_shape=tuple(shapes),
        in_specs=[pl.BlockSpec(memory_space=pltpu.SMEM)] + [pl.BlockSpec(memory_space=pltpu.VMEM)] * 7,
        out_specs=(pl.BlockSpec(memory_space=pltpu.VMEM),) * len(shapes),
        scratch_shapes=[
            pltpu.VMEM((key_len, lanes), jnp.float32),
            pltpu.VMEM((key_len, lanes), jnp.float32),
            pltpu.VMEM((key_len + 2 * BLOCK_PAD, heads * lanes), jnp.bfloat16),
            pltpu.VMEM((key_len, heads * lanes), jnp.bfloat16),
            pltpu.VMEM((width, lanes), jnp.bfloat16),
        ],
        compiler_params=pltpu.CompilerParams(vmem_limit_bytes=VMEM_BYTES),
    )(starts, q, k, v, do, lse, bm, qstart)


def send(src, dst, send_sem, recv_sem, to):
    copy = pltpu.make_async_remote_copy(
        src_ref=src, dst_ref=dst, send_sem=send_sem, recv_sem=recv_sem, device_id=to, device_id_type=pl.DeviceIdType.MESH
    )
    copy.start()
    return copy


def arrived(dst, send_sem, recv_sem, to):
    pltpu.make_async_remote_copy(
        src_ref=dst, dst_ref=dst, send_sem=send_sem, recv_sem=recv_sem, device_id=to, device_id_type=pl.DeviceIdType.MESH
    ).wait_recv()


class Place:
    def __init__(self, groups, cores, parts):
        self.groups, self.cores, self.parts = groups, cores, parts
        self.group, self.core, self.part = lax.axis_index(HG), lax.axis_index(CORE), lax.axis_index(SP)

    def ahead(self, step):
        return lax.rem(self.group + step, self.groups)

    def behind(self, step):
        return lax.rem(self.group + self.groups - step, self.groups)

    def chip(self, group):
        return (group, self.core, self.part)

    def sibling(self):
        return (self.group, 1 - self.core, self.part)

    def plane(self, step):
        return lax.rem(self.part + step, self.parts)

    def plane_behind(self, step):
        return lax.rem(self.part + self.parts - step, self.parts)

    def at_plane(self, part):
        return (self.group, self.core, part)

    def greet(self, chips=True, sibling=True, planes=False):
        barrier = pltpu.get_barrier_semaphore()
        partners = []
        if chips:
            partners += [self.chip(self.ahead(step)) for step in range(1, self.groups)]
        if sibling:
            partners.append(self.sibling())
        if planes:
            partners += [self.at_plane(self.plane(step)) for step in range(1, self.parts)]
        for partner in partners:
            pl.semaphore_signal(barrier, inc=1, device_id=partner, device_id_type=pl.DeviceIdType.MESH)
        pl.semaphore_wait(barrier, len(partners))


def recut_kernel(sizes, counts, *refs):
    cols, rows = counts
    col_refs, refs = refs[:cols], refs[cols:]
    row_refs, refs = refs[:rows], refs[rows:]
    col_outs, refs = refs[:cols], refs[cols:]
    row_outs, refs = refs[:rows], refs[rows:]
    sent, got, relay_sent, relay_got, pair_sent, pair_got, local = refs
    place = Place(*sizes)
    group, core = place.group, place.core
    place.greet()
    pending, copies = [], []
    for index in range(cols):
        out = col_outs[index]
        for step in range(1, place.groups):
            to = place.ahead(step)
            pending.append(send(col_refs[index].at[to], out.at[group, core], sent.at[index, step], got.at[index, step], place.chip(to)))
        pending.append(
            send(col_refs[index].at[group], out.at[group, core], relay_sent.at[index, 0], relay_got.at[index, 0], place.sibling())
        )
        copies.append(pltpu.make_async_copy(col_refs[index].at[group], out.at[group, core], local.at[index]))
        copies[-1].start()
    for index in range(rows):
        out = row_outs[index]
        pending.append(send(row_refs[index], out.at[core], pair_sent.at[index], pair_got.at[index], place.sibling()))
        copies.append(pltpu.make_async_copy(row_refs[index], out.at[core], local.at[cols + index]))
        copies[-1].start()
    for index in range(cols):
        out = col_outs[index]
        for step in range(1, place.groups):
            source = place.behind(step)
            slot = out.at[source, core]
            arrived(slot, sent.at[index, step], got.at[index, step], place.chip(source))
            pending.append(send(slot, slot, relay_sent.at[index, step], relay_got.at[index, step], place.sibling()))
    for index in range(cols):
        out = col_outs[index]
        for step in range(place.groups):
            slot = out.at[place.behind(step), 1 - core]
            arrived(slot, relay_sent.at[index, step], relay_got.at[index, step], place.sibling())
    for index in range(rows):
        arrived(row_outs[index].at[1 - core], pair_sent.at[index], pair_got.at[index], place.sibling())
    for copy in copies:
        copy.wait()
    for copy in pending:
        copy.wait_send()


def recut(sizes, collective_id, col_packs, row_packs):
    groups, cores, _ = sizes
    cols, rows = len(col_packs), len(row_packs)
    anywhere = pl.BlockSpec(memory_space=pl.ANY)
    shapes = [jax.ShapeDtypeStruct((groups, cores) + w.shape[1:], w.dtype) for w in col_packs]
    shapes += [jax.ShapeDtypeStruct((cores,) + w.shape, w.dtype) for w in row_packs]
    dma = pltpu.SemaphoreType.DMA
    got = pl.pallas_call(
        functools.partial(recut_kernel, sizes, (cols, rows)),
        out_shape=tuple(shapes),
        in_specs=[anywhere] * (cols + rows),
        out_specs=(anywhere,) * (cols + rows),
        scratch_shapes=[
            dma((cols, groups)), dma((cols, groups)), dma((cols, groups)), dma((cols, groups)),
            dma((rows,)), dma((rows,)), dma((cols + rows,)),
        ],
        compiler_params=pltpu.CompilerParams(collective_id=collective_id, has_side_effects=True, vmem_limit_bytes=VMEM_BYTES),
    )(*col_packs, *row_packs)
    whole_cols = [w.reshape(groups * cores * w.shape[2], w.shape[3]) for w in got[:cols]]
    return whole_cols, [w.reshape(cores * w.shape[1], w.shape[2]) for w in got[cols:]]


def give_rows_kernel(sizes, counts, *refs):
    cols, rows = counts
    col_refs, refs = refs[:cols], refs[cols:]
    row_refs, refs = refs[:rows], refs[rows:]
    col_outs, refs = refs[:cols], refs[cols:]
    row_outs, refs = refs[:rows], refs[rows:]
    col_sibs, refs = refs[:cols], refs[cols:]
    col_sums, refs = refs[:cols], refs[cols:]
    row_sibs, refs = refs[:rows], refs[rows:]
    sent, got, pair_sent, pair_got, row_sent, row_got = refs
    place = Place(*sizes)
    group, core = place.group, place.core
    place.greet()
    pending = []
    for index in range(cols):
        for step in range(place.groups):
            to = place.ahead(step)
            pending.append(
                send(
                    col_refs[index].at[to, 1 - core], col_sibs[index].at[to],
                    pair_sent.at[index, step], pair_got.at[index, step], place.sibling(),
                )
            )
    for index in range(rows):
        pending.append(
            send(row_refs[index].at[1 - core], row_sibs[index], row_sent.at[index], row_got.at[index], place.sibling())
        )
    for index in range(cols):
        for step in list(range(1, place.groups)) + [0]:
            to = place.ahead(step)
            arrived(col_sibs[index].at[to], pair_sent.at[index, step], pair_got.at[index, step], place.sibling())
            both = col_refs[index][to, core].astype(jnp.float32) + col_sibs[index][to].astype(jnp.float32)
            if step:
                col_sums[index][to] = both.astype(jnp.bfloat16)
                pending.append(
                    send(
                        col_sums[index].at[to], col_outs[index].at[group],
                        sent.at[index, step], got.at[index, step], place.chip(to),
                    )
                )
            else:
                col_outs[index][group] = both.astype(jnp.bfloat16)
    for index in range(rows):
        arrived(row_sibs[index], row_sent.at[index], row_got.at[index], place.sibling())
        both = row_refs[index][core].astype(jnp.float32) + row_sibs[index][...].astype(jnp.float32)
        row_outs[index][...] = both.astype(jnp.bfloat16)
    for index in range(cols):
        for step in range(1, place.groups):
            source = place.behind(step)
            arrived(col_outs[index].at[source], sent.at[index, step], got.at[index, step], place.chip(source))
    for copy in pending:
        copy.wait_send()


def give_rows(sizes, collective_id, col_grads, row_grads):
    groups, cores, _ = sizes
    cols, rows = len(col_grads), len(row_grads)
    vmem = pl.BlockSpec(memory_space=pltpu.VMEM)
    col_in = [w.reshape(groups, cores, w.shape[0] // (groups * cores), w.shape[1]) for w in col_grads]
    row_in = [w.reshape(cores, w.shape[0] // cores, w.shape[1]) for w in row_grads]
    col_own = [(groups,) + w.shape[2:] for w in col_in]
    row_own = [w.shape[1:] for w in row_in]
    dma = pltpu.SemaphoreType.DMA
    got = pl.pallas_call(
        functools.partial(give_rows_kernel, sizes, (cols, rows)),
        out_shape=tuple(jax.ShapeDtypeStruct(s, jnp.bfloat16) for s in col_own + row_own),
        in_specs=[vmem] * (cols + rows),
        out_specs=(vmem,) * (cols + rows),
        scratch_shapes=[pltpu.VMEM(s, jnp.bfloat16) for s in col_own + col_own + row_own]
        + [dma((cols, groups))] * 4
        + [dma((rows,))] * 2,
        compiler_params=pltpu.CompilerParams(collective_id=collective_id, has_side_effects=True, vmem_limit_bytes=VMEM_BYTES),
    )(*col_in, *row_in)
    return got[:cols], got[cols:]


def fast_device(
    enc_in, dec_in, enc_cot, dec_cot, enc_segments, dec_segments, buckets,
    enc_norm1, enc_query, enc_key, enc_value, enc_proj, enc_rel, enc_norm2, enc_gate, enc_up, enc_down, enc_final,
    dec_norm1, dec_query, dec_key, dec_value, dec_proj, dec_rel, dec_norm2, cross_query, cross_key, cross_value, cross_proj,
    dec_norm3, dec_gate, dec_up, dec_down,
):
    groups, cores, parts = lax.axis_size(HG), lax.axis_size(CORE), lax.axis_size(SP)
    my_group, my_core, my_part = lax.axis_index(HG), lax.axis_index(CORE), lax.axis_index(SP)
    block, model = enc_in.shape
    share = model // (groups * cores)
    width = HEADS // groups * HD
    heads = HEADS // groups
    reach = (buckets.shape[1] - 1) // 2
    bf16, f32 = jnp.bfloat16, jnp.float32

    sizes = (groups, cores, parts)

    def packed(*weights):
        cut = [w.reshape(w.shape[0], groups, w.shape[1] // groups) for w in weights]
        return jnp.concatenate(cut, axis=2).transpose(1, 0, 2)

    cols, rows = recut(
        sizes,
        1,
        [
            packed(enc_query, enc_key, enc_value),
            packed(dec_query, dec_key, dec_value),
            packed(enc_gate, enc_up),
            packed(cross_query, cross_key, cross_value),
            packed(dec_gate, dec_up),
        ],
        [enc_proj, dec_proj, cross_proj, enc_down, dec_down],
    )
    enc_qkv, dec_qkv, enc_gu, cross_qkv, dec_gu = cols
    enc_wo, dec_wo, cross_wo, enc_wd, dec_wd = rows
    cross_q, cross_kv = cross_qkv[:, :width], cross_qkv[:, width:]
    small = jnp.concatenate([enc_norm1, enc_norm2, enc_final, dec_norm1, dec_norm2, dec_norm3, enc_rel, dec_rel])
    small = lax.all_gather(small, (HG, CORE), axis=0)
    gains = [small[:, i * share : (i + 1) * share].reshape(1, model).astype(f32) for i in range(6)]
    g_e1, g_e2, g_ef, g_d1, g_d2, g_d3 = gains
    rel_len = enc_rel.shape[0]
    rels = [small[:, 6 * share + i * rel_len : 6 * share + (i + 1) * rel_len].reshape(-1, HEADS).astype(f32) for i in range(2)]

    def table_of(relative, row):
        onehot = (row[:, None] == jnp.arange(relative.shape[0], dtype=jnp.int32)[None, :]).astype(f32)
        full = jnp.dot(onehot, relative, precision=HIGHEST).T
        here = lax.dynamic_slice_in_dim(full, my_group * heads, heads, 0)
        return here, onehot

    def turned(table):
        edge = block - 1
        long = jnp.concatenate(
            [jnp.broadcast_to(table[:, :1], (heads, edge)), table, jnp.broadcast_to(table[:, -1:], (heads, edge))], axis=1
        )
        flipped = long[:, ::-1]
        pad = -flipped.shape[1] % 128
        return jnp.pad(flipped, ((0, 0), (0, pad)))

    enc_table, enc_onehot = table_of(rels[0], buckets[0])
    dec_table, dec_onehot = table_of(rels[1], buckets[1])
    firsts = ((cores * jnp.arange(groups, dtype=jnp.int32) + my_core) * parts + my_part) * block
    qpos = (firsts[:, None] + jnp.arange(block, dtype=jnp.int32)[None, :]).reshape(1, -1)

    def mine(ids):
        return lax.dynamic_index_in_dim(
            lax.dynamic_index_in_dim(ids.reshape(groups, cores, parts, block), my_core, 1, False), my_part, 1, False
        ).reshape(1, -1)

    enc_q_ids, dec_q_ids = mine(enc_segments), mine(dec_segments)
    enc_k_ids, dec_k_ids = enc_segments[:, None], dec_segments[:, None]
    enc_bm = bias_mask(firsts, turned(enc_table), enc_k_ids, enc_q_ids, qpos, block, False)
    dec_bm = bias_mask(firsts, turned(dec_table), dec_k_ids, dec_q_ids, qpos, block, True)
    cross_bm = bias_mask(firsts, None, enc_k_ids, dec_q_ids, qpos, block, False)

    def spread(own):
        return lax.all_gather(own, HG, axis=0, tiled=True)

    def collect(partial):
        return lax.psum_scatter(partial.astype(bf16), HG, scatter_dimension=0, tiled=True).astype(f32)

    def all_keys(kv):
        every = lax.all_gather(kv, (CORE, SP), axis=0)
        every = every.reshape(cores, parts, groups, block, -1).transpose(2, 0, 1, 3, 4)
        return every.reshape(cores * parts * groups * block, -1)

    def own_keys(dkv):
        cut = dkv.reshape(groups, cores, parts, block, -1).transpose(1, 2, 0, 3, 4)
        return lax.psum_scatter(cut.reshape(cores * parts * groups * block, -1), (CORE, SP), scatter_dimension=0, tiled=True)

    def attend(n_query, w_query, kv, bm):
        q = nn(n_query, w_query).astype(bf16)
        every = all_keys(kv)
        k, v = every[:, :width], every[:, width:]
        o, lse = mix(q, k, v, bm)
        return o, (q, k, v, o, lse)

    def attend_back(dyb, kept, bm, w_proj, biased):
        q, k, v, o, lse = kept
        do = nt(dyb, w_proj).astype(bf16)
        d_proj = tn(o, dyb)
        got = mix_back(firsts, q, k, v, do, lse, bm, block, biased)
        dq, dk, dv = got[:3]
        dkv = own_keys(jnp.concatenate([dk, dv], axis=1)).astype(bf16)
        return d_proj, dq, dkv, got[3:]

    def normed(x, g):
        return rms_norm(x, g).astype(bf16)

    def norm_back(x, g, dn):
        r = lax.rsqrt(jnp.mean(x * x, axis=-1, keepdims=True) + EPSILON)
        w = dn * g
        dx = r * w - x * (r * r * r) * jnp.mean(w * x, axis=-1, keepdims=True)
        return dx, jnp.sum(dn * x * r, axis=0)

    enc_x, dec_x = enc_in.astype(f32), dec_in.astype(f32)
    en1, dn1 = spread(normed(enc_x, g_e1)), spread(normed(dec_x, g_d1))
    enc_o, enc_kept = attend(en1, enc_qkv[:, :width], nn(en1, enc_qkv[:, width:]).astype(bf16), enc_bm)
    dec_o, dec_kept = attend(dn1, dec_qkv[:, :width], nn(dn1, dec_qkv[:, width:]).astype(bf16), dec_bm)
    ex = enc_x + collect(nn(enc_o, enc_wo))
    dx = dec_x + collect(nn(dec_o, dec_wo))
    hidden = enc_wd.shape[0]

    def feed(n, w_gu, w_d):
        gu = nn(n, w_gu)
        g, u = gu[:, :hidden], gu[:, hidden:]
        h = gated(g, u).astype(bf16)
        return g, u, h, collect(nn(h, w_d))

    def feed_back(n, g, u, h, dyb, w_gu, w_d):
        dh = nt(dyb, w_d)
        d_down = tn(h, dyb)
        _, pullback = jax.vjp(gated, g, u)
        dg, du = pullback(dh)
        dgu = jnp.concatenate([dg, du], axis=1).astype(bf16)
        return tn(n, dgu), d_down, collect(nt(dgu, w_gu))

    en2 = spread(normed(ex, g_e2))
    e_g, e_u, e_h, y = feed(en2, enc_gu, enc_wd)
    enc_out = ex + y
    memory = spread(normed(enc_out, g_ef))
    dn2 = spread(normed(dx, g_d2))
    cross_o, cross_kept = attend(dn2, cross_q, nn(memory, cross_kv).astype(bf16), cross_bm)
    cx = dx + collect(nn(cross_o, cross_wo))
    dn3 = spread(normed(cx, g_d3))
    d_g, d_u, d_h, y = feed(dn3, dec_gu, dec_wd)
    dec_out = cx + y

    d_cot, e_cot = dec_cot.astype(f32), enc_cot.astype(f32)
    dyb = spread(dec_cot)
    dw_dgu, dw_ddown, dn = feed_back(dn3, d_g, d_u, d_h, dyb, dec_gu, dec_wd)
    back, dg_d3 = norm_back(cx, g_d3, dn)
    grad_dec = d_cot + back
    dyb = spread(grad_dec.astype(bf16))
    dw_cproj, dq, dkv, _ = attend_back(dyb, cross_kept, cross_bm, cross_wo, False)
    dw_cq = tn(dn2, dq)
    dw_ckv = tn(memory, dkv)
    dn, dmem = collect(nt(dq, cross_q)), collect(nt(dkv, cross_kv))
    back, dg_d2 = norm_back(dx, g_d2, dn)
    grad_dec = grad_dec + back
    dyb = spread(grad_dec.astype(bf16))
    dw_dproj, dq, dkv, dec_tab = attend_back(dyb, dec_kept, dec_bm, dec_wo, True)
    dqkv = jnp.concatenate([dq, dkv], axis=1)
    dw_dqkv = tn(dn1, dqkv)
    back, dg_d1 = norm_back(dec_x, g_d1, collect(nt(dqkv, dec_qkv)))
    dec_in_grad = grad_dec + back
    back, dg_ef = norm_back(enc_out, g_ef, dmem)
    grad_enc = e_cot + back
    dyb = spread(grad_enc.astype(bf16))
    dw_egu, dw_edown, dn = feed_back(en2, e_g, e_u, e_h, dyb, enc_gu, enc_wd)
    back, dg_e2 = norm_back(ex, g_e2, dn)
    grad_enc = grad_enc + back
    dyb = spread(grad_enc.astype(bf16))
    dw_eproj, dq, dkv, enc_tab = attend_back(dyb, enc_kept, enc_bm, enc_wo, True)
    dqkv = jnp.concatenate([dq, dkv], axis=1)
    dw_eqkv = tn(en1, dqkv)
    back, dg_e1 = norm_back(enc_x, g_e1, collect(nt(dqkv, enc_qkv)))
    enc_in_grad = grad_enc + back

    def summed_rows(collective_id, col_grads, row_grads):
        mine_cols, mine_rows = give_rows(
            sizes, collective_id, [g.astype(bf16) for g in col_grads], [g.astype(bf16) for g in row_grads]
        )
        return [lax.psum(g, SP) for g in mine_cols], [lax.psum(g, SP).astype(f32) for g in mine_rows]

    def unpacked(whole, pieces):
        each = whole.shape[2] // pieces
        whole = whole.astype(f32)
        return [whole[:, :, i * each : (i + 1) * each].transpose(1, 0, 2).reshape(share, groups * each) for i in range(pieces)]

    (dgu_rows,), (d_wd,) = summed_rows(2, [dw_dgu], [dw_ddown])
    (cross_rows,), (c_wo,) = summed_rows(3, [jnp.concatenate([dw_cq, dw_ckv], axis=1)], [dw_cproj])
    (egu_rows, dqkv_rows), (d_wo, e_wd) = summed_rows(4, [dw_egu, dw_dqkv], [dw_dproj, dw_edown])
    (eqkv_rows,), (e_wo,) = summed_rows(5, [dw_eqkv], [dw_eproj])
    e_wq, e_wk, e_wv = unpacked(eqkv_rows, 3)
    e_wg, e_wu = unpacked(egu_rows, 2)
    d_wq, d_wk, d_wv = unpacked(dqkv_rows, 3)
    c_wq, c_wk, c_wv = unpacked(cross_rows, 3)
    d_wg, d_wu = unpacked(dgu_rows, 2)

    def fold(tab, onehot):
        strips, edges = tab
        keys = strips.shape[1]
        flipped = strips[:, :, ::-1].transpose(0, 2, 1)
        span = keys + block
        wide = jnp.pad(flipped, ((0, 0), (0, 0), (0, block)))
        flat = wide.reshape(heads, block * span)[:, : block * (span - 1)]
        by_distance = jnp.sum(flat.reshape(heads, block, span - 1), axis=1)
        shift = block - 1 + BLOCK_PAD - reach
        size = 2 * reach + 1
        inner = by_distance[:, shift : shift + size]
        low = jnp.sum(by_distance[:, :shift], axis=1)
        high = jnp.sum(by_distance[:, shift + size :], axis=1)
        sides = jnp.sum(edges, axis=1).reshape(heads, 2)
        inner = inner.at[:, 0].add(low + sides[:, 0]).at[:, -1].add(high + sides[:, 1])
        full = jnp.zeros((HEADS, size), f32)
        full = lax.dynamic_update_slice_in_dim(full, inner, my_group * heads, 0)
        return jnp.dot(onehot.T, full.T, precision=HIGHEST).reshape(-1)

    small_grads = [dg_e1, dg_e2, dg_ef, dg_d1, dg_d2, dg_d3, fold(enc_tab, enc_onehot), fold(dec_tab, dec_onehot)]
    packed = jnp.concatenate([v.reshape(groups * cores, -1) for v in small_grads], axis=1)
    summed = lax.psum(packed, (HG, CORE, SP))
    own = lax.dynamic_index_in_dim(summed, my_group * cores + my_core, 0, False)
    s = [own[i * share : (i + 1) * share] for i in range(6)]
    e_rel, d_rel = own[6 * share : 6 * share + rel_len], own[6 * share + rel_len :]
    return (
        enc_out, dec_out, enc_in_grad, dec_in_grad,
        s[0], e_wq, e_wk, e_wv, e_wo, e_rel, s[1], e_wg, e_wu, e_wd, s[2],
        s[3], d_wq, d_wk, d_wv, d_wo, d_rel, s[4], c_wq, c_wk, c_wv, c_wo, s[5], d_wg, d_wu, d_wd,
    )


def general_plan(mesh):
    placed = (
        P(("ctx", "sp"), None),
        P(("ctx", "sp"), None),
        P(("ctx", "sp"), None),
        P(("ctx", "sp"), None),
        P(),
        P(),
        P(),
        P("ctx"),
        P("ctx", None),
        P("ctx", None),
        P("ctx", None),
        P("ctx", None),
        P("ctx"),
        P("ctx"),
        P("ctx", None),
        P("ctx", None),
        P("ctx", None),
        P("ctx"),
        P("ctx"),
        P("ctx", None),
        P("ctx", None),
        P("ctx", None),
        P("ctx", None),
        P("ctx"),
        P("ctx"),
        P("ctx", None),
        P("ctx", None),
        P("ctx", None),
        P("ctx", None),
        P("ctx"),
        P("ctx", None),
        P("ctx", None),
        P("ctx", None),
    )
    return jax.shard_map(
        per_device,
        mesh=mesh,
        in_specs=placed,
        out_specs=(
            P(("ctx", "sp"), None),
            P(("ctx", "sp"), None),
            P(("ctx", "sp"), None),
            P(("ctx", "sp"), None),
            P("ctx"),
            P("ctx", None),
            P("ctx", None),
            P("ctx", None),
            P("ctx", None),
            P("ctx"),
            P("ctx"),
            P("ctx", None),
            P("ctx", None),
            P("ctx", None),
            P("ctx"),
            P("ctx"),
            P("ctx", None),
            P("ctx", None),
            P("ctx", None),
            P("ctx", None),
            P("ctx"),
            P("ctx"),
            P("ctx", None),
            P("ctx", None),
            P("ctx", None),
            P("ctx", None),
            P("ctx"),
            P("ctx", None),
            P("ctx", None),
            P("ctx", None),
        ),
        check_vma=False,
    )


def split_plan(mesh, groups):
    cut = Mesh(np.asarray(mesh.devices).reshape(groups, 2, mesh.shape["sp"]), (HG, CORE, SP))
    tokens, rows, gain, same = P((HG, CORE, SP), None), P((HG, CORE), None), P((HG, CORE)), P()
    attention = (gain, rows, rows, rows, rows, gain)
    feed = (gain, rows, rows, rows)
    weights = attention + feed + (gain,) + attention + (gain, rows, rows, rows, rows) + feed
    return jax.shard_map(
        fast_device,
        mesh=cut,
        in_specs=(tokens,) * 4 + (same,) * 3 + weights,
        out_specs=(tokens,) * 4 + weights,
        check_vma=False,
    )


def solution(mesh):
    groups, odd = divmod(mesh.shape["ctx"], 2)
    if odd or HEADS % groups:
        return general_plan(mesh)
    return split_plan(mesh, groups)
```

```python
import functools
import math

import jax
import jax.numpy as jnp
import numpy as np
from jax import lax
from jax.experimental import pallas as pl
from jax.experimental.pallas import tpu as pltpu
from jax.sharding import Mesh
from jax.sharding import PartitionSpec as P

HEADS = 12
HD = 64


EPSILON = 1e-06
NEGATIVE = -1e30
HIGHEST = lax.Precision.HIGHEST


def rms_norm(values, norm_gain):
    return (
        values * lax.rsqrt(jnp.mean(values * values, axis=-1, keepdims=True) + EPSILON) * norm_gain
    )


def norm_pullback(values, norm_gain, grad_normed):
    _, pullback = jax.vjp(rms_norm, values, norm_gain)
    return pullback(grad_normed)


def gated(gate_val, up_val):
    return jax.nn.gelu(gate_val, approximate=True) * up_val


def project(left, right):
    return jnp.dot(left, right, preferred_element_type=jnp.float32)


def weight_grad(left, right):
    return jnp.einsum("td,te->de", left, right, preferred_element_type=jnp.float32)


def input_grad(grad_out, weight):
    return jnp.einsum("te,de->td", grad_out, weight, preferred_element_type=jnp.float32)


def head_table(relative, table_row, heads_here):
    bucket_count = relative.shape[0] // HEADS
    onehot = (table_row[:, None] == jnp.arange(bucket_count, dtype=jnp.int32)[None, :]).astype(
        jnp.float32
    )
    bias_grid = relative.astype(jnp.float32).reshape(bucket_count, HEADS)
    full_table = jnp.dot(onehot, bias_grid, precision=HIGHEST).T
    first_head = lax.axis_index("sp") * heads_here
    return (lax.dynamic_slice_in_dim(full_table, first_head, heads_here, 0), onehot)


def table_grad(grad_table, onehot, heads_here):
    full_grad = jnp.zeros((HEADS, onehot.shape[0]), jnp.float32)
    full_grad = lax.dynamic_update_slice_in_dim(
        full_grad, grad_table, lax.axis_index("sp") * heads_here, 0
    )
    return jnp.dot(onehot.T, full_grad.T, precision=HIGHEST).reshape(-1)


def bias_block(head_bias, pad_len, offset_q, rows, offset_k, cols):
    head_count, table_len = head_bias.shape
    reach_len = (table_len - 1) // 2
    left_edge = jnp.broadcast_to(head_bias[:, :1], (head_count, pad_len))
    right_edge = jnp.broadcast_to(head_bias[:, -1:], (head_count, pad_len))
    padded = jnp.concatenate([left_edge, head_bias, right_edge], axis=1)
    band_width = rows + cols - 1
    start = offset_k - offset_q - (rows - 1) + reach_len + pad_len
    band = lax.dynamic_slice_in_dim(padded, start, band_width, 1)
    tiled = jnp.broadcast_to(band[:, None, :], (head_count, rows, band_width)).reshape(
        head_count, rows * band_width
    )
    skewed = tiled[:, rows - 1 : rows - 1 + rows * (band_width - 1)].reshape(
        head_count, rows, band_width - 1
    )
    return skewed[:, :, :cols]


def make_frame(query_local, query_ids, key_ids, head_bias, causal):
    local_len = query_local.shape[0]
    heads_here = query_local.shape[1] // HD
    offset_q = lax.axis_index("ctx") * local_len
    ids_q = lax.dynamic_slice_in_dim(query_ids, offset_q, local_len, 0)
    row_ids = offset_q + jnp.arange(local_len, dtype=jnp.int32)
    query_heads = query_local.reshape(local_len, heads_here, HD)
    pad_len = query_ids.shape[0] + key_ids.shape[0]

    def bias_of(entries, offset_k, length):
        return bias_block(entries, pad_len, offset_q, local_len, offset_k, length)

    def scores_of(key_block, offset_k):
        length = key_block.shape[0]
        key_heads = key_block.reshape(length, heads_here, HD)
        raw_scores = jnp.einsum(
            "qhd,khd->hqk", query_heads, key_heads, preferred_element_type=jnp.float32
        )
        col_ids = offset_k + jnp.arange(length, dtype=jnp.int32)
        ids_k = lax.dynamic_slice_in_dim(key_ids, offset_k, length, 0)
        allowed = ids_q[:, None] == ids_k[None, :]
        if causal:
            allowed = allowed & (col_ids[None, :] <= row_ids[:, None])
        if head_bias is not None:
            raw_scores = raw_scores + bias_of(head_bias, offset_k, length)
        return (raw_scores, allowed)

    def touches(offset_k, length):
        first_id = lax.dynamic_slice_in_dim(key_ids, offset_k, 1, 0)[0]
        last_id = lax.dynamic_slice_in_dim(key_ids, offset_k + length - 1, 1, 0)[0]
        touched = (ids_q[0] <= last_id) & (first_id <= ids_q[-1])
        if causal:
            touched = touched & (offset_k <= offset_q + local_len - 1)
        return touched

    return (query_heads, scores_of, touches, bias_of)


def sweep(keys_gathered, local_len, step_fn, carry_state):
    key_all, value_all = keys_gathered
    block_len = local_len * math.gcd(4, lax.axis_size("ctx"))

    def sweep_loop_body(number, running):
        offset_k = number * block_len
        key_block = lax.dynamic_slice_in_dim(key_all, offset_k, block_len, 0)
        value_block = lax.dynamic_slice_in_dim(value_all, offset_k, block_len, 0)
        return step_fn(running, key_block, value_block, offset_k)

    return lax.fori_loop(0, key_all.shape[0] // block_len, sweep_loop_body, carry_state)


def whole_keys(key_local, value_local):
    return (
        lax.all_gather(key_local, "ctx", axis=0, tiled=True),
        lax.all_gather(value_local, "ctx", axis=0, tiled=True),
    )


def attention_forward(query_proj, key_proj, value_proj, query_ids, key_ids, head_bias, causal):
    query_local, key_local, value_local = (
        lax.all_to_all(query_proj, "sp", split_axis=1, concat_axis=0, tiled=True),
        lax.all_to_all(key_proj, "sp", split_axis=1, concat_axis=0, tiled=True),
        lax.all_to_all(value_proj, "sp", split_axis=1, concat_axis=0, tiled=True),
    )
    local_len = query_local.shape[0]
    heads_here = query_local.shape[1] // HD
    query_heads, scores_of, touches, _ = make_frame(
        query_local, query_ids, key_ids, head_bias, causal
    )
    key_block = lax.all_gather(key_local, "ctx", axis=0, tiled=True)
    value_block = lax.all_gather(value_local, "ctx", axis=0, tiled=True)
    offset_k = jnp.int32(0)
    length = key_block.shape[0]
    row_top = jnp.full((heads_here, local_len), NEGATIVE, jnp.float32)
    weighted = jnp.zeros((local_len, heads_here, HD), jnp.float32)
    raw_scores, allowed = scores_of(key_block, offset_k)
    masked = jnp.where(allowed[None], raw_scores, NEGATIVE)
    new_top = jnp.maximum(row_top, jnp.max(masked, axis=-1))
    weights = jnp.where(allowed[None], jnp.exp(masked - new_top[..., None]), 0.0)
    rescale = jnp.exp(row_top - new_top)
    value_heads = value_block.reshape(length, heads_here, HD)
    increment = jnp.einsum(
        "hqk,khd->qhd",
        weights.astype(jnp.bfloat16),
        value_heads,
        preferred_element_type=jnp.float32,
    )
    row_top, row_total, weighted = (
        new_top,
        jnp.sum(weights, axis=-1),
        weighted * rescale.T[:, :, None] + increment,
    )
    mixed_heads = weighted / row_total.T[:, :, None]
    log_total = row_top + jnp.log(row_total)
    mixed_low = mixed_heads.reshape(local_len, heads_here * HD).astype(jnp.bfloat16)
    mixed_tokens = lax.all_to_all(mixed_low, "sp", split_axis=0, concat_axis=1, tiled=True)
    retained = (
        query_local,
        key_local,
        value_local,
        mixed_heads,
        log_total,
        None,
        query_ids,
        key_ids,
        head_bias,
        causal,
    )
    return (mixed_tokens, retained)


def attention_backward(grad_mixed, retained):
    (
        query_local,
        key_local,
        value_local,
        mixed_heads,
        log_total,
        gathered,
        query_ids,
        key_ids,
        head_bias,
        causal,
    ) = retained
    grad_local = lax.all_to_all(grad_mixed, "sp", split_axis=1, concat_axis=0, tiled=True)
    local_len = query_local.shape[0]
    heads_here = query_local.shape[1] // HD
    width = heads_here * HD
    query_heads, scores_of, touches, bias_of = make_frame(
        query_local, query_ids, key_ids, head_bias, causal
    )
    grad_heads = grad_local.reshape(local_len, heads_here, HD)
    row_inner = jnp.einsum("qhd,qhd->hq", grad_heads.astype(jnp.float32), mixed_heads)
    gathered = whole_keys(key_local, value_local)
    table_zero = jnp.zeros(head_bias.shape if head_bias is not None else (1,), jnp.float32)

    def gradients_of(key_block, value_block, offset_k):
        length = key_block.shape[0]
        raw_scores, allowed = scores_of(key_block, offset_k)
        probabilities = jnp.where(allowed[None], jnp.exp(raw_scores - log_total[..., None]), 0.0)
        value_heads = value_block.reshape(length, heads_here, HD)
        grad_probs = jnp.einsum(
            "qhd,khd->hqk", grad_heads, value_heads, preferred_element_type=jnp.float32
        )
        grad_scores = (probabilities * (grad_probs - row_inner[..., None])).astype(jnp.bfloat16)
        return (probabilities, grad_scores)

    def table_part(grad_scores, offset_k, length):
        if head_bias is None:
            return table_zero
        _, pullback = jax.vjp(lambda entries: bias_of(entries, offset_k, length), head_bias)
        return pullback(grad_scores.astype(jnp.float32))[0]

    def key_terms_of(probabilities, grad_scores, length):
        grad_key = jnp.einsum(
            "hqk,qhd->khd", grad_scores, query_heads, preferred_element_type=jnp.float32
        )
        grad_value = jnp.einsum(
            "hqk,qhd->khd",
            probabilities.astype(jnp.bfloat16),
            grad_heads,
            preferred_element_type=jnp.float32,
        )
        return jnp.concatenate(
            [grad_key.reshape(length, width), grad_value.reshape(length, width)], axis=1
        )

    def query_part(grad_scores, key_block):
        length = key_block.shape[0]
        key_heads = key_block.reshape(length, heads_here, HD)
        return jnp.einsum(
            "hqk,khd->qhd", grad_scores, key_heads, preferred_element_type=jnp.float32
        )

    def query_step(running, key_block, value_block, offset_k):
        length = key_block.shape[0]
        grad_query, grad_table = running
        probabilities, grad_scores = gradients_of(key_block, value_block, offset_k)
        return (
            grad_query + query_part(grad_scores, key_block),
            grad_table + table_part(grad_scores, offset_k, length),
        )

    query_zero = jnp.zeros((local_len, heads_here, HD), jnp.float32)
    block_len = local_len * math.gcd(4, lax.axis_size("ctx"))
    grad_query, grad_table = sweep(gathered, local_len, query_step, (query_zero, table_zero))
    key_all, value_all = gathered
    step_len = math.gcd(lax.axis_size("ctx") * local_len, block_len)

    def term_loop_body(number, rows_acc):
        offset_b = number * step_len
        key_block = lax.dynamic_slice_in_dim(key_all, offset_b, step_len, 0)
        value_block = lax.dynamic_slice_in_dim(value_all, offset_b, step_len, 0)
        probabilities, grad_scores = gradients_of(key_block, value_block, offset_b)
        return lax.dynamic_update_slice_in_dim(
            rows_acc, key_terms_of(probabilities, grad_scores, step_len), number * step_len, 0
        )

    own_rows = lax.psum_scatter(
        lax.fori_loop(
            0,
            lax.axis_size("ctx") * local_len // step_len,
            term_loop_body,
            jnp.zeros((lax.axis_size("ctx") * local_len, 2 * width), jnp.float32),
        ),
        "ctx",
        scatter_dimension=0,
        tiled=True,
    )
    grad_q_low = grad_query.reshape(local_len, width).astype(jnp.bfloat16)
    grad_k_low = own_rows[:, :width].astype(jnp.bfloat16)
    grad_v_low = own_rows[:, width:].astype(jnp.bfloat16)
    grad_q_tok, grad_k_tok, grad_v_tok = (
        lax.all_to_all(grad_q_low, "sp", split_axis=0, concat_axis=1, tiled=True),
        lax.all_to_all(grad_k_low, "sp", split_axis=0, concat_axis=1, tiled=True),
        lax.all_to_all(grad_v_low, "sp", split_axis=0, concat_axis=1, tiled=True),
    )
    return (grad_q_tok, grad_k_tok, grad_v_tok, grad_table)


def attention_layer(
    residual,
    source,
    norm_gain,
    w_query,
    w_key,
    w_value,
    w_proj,
    query_ids,
    key_ids,
    head_bias,
    causal,
):
    normed = rms_norm(residual, norm_gain).astype(jnp.bfloat16)
    kv_input = normed if source is None else source
    query_proj = project(normed, w_query).astype(jnp.bfloat16)
    key_proj = project(kv_input, w_key).astype(jnp.bfloat16)
    value_proj = project(kv_input, w_value).astype(jnp.bfloat16)
    mixed_tokens, retained = attention_forward(
        query_proj, key_proj, value_proj, query_ids, key_ids, head_bias, causal
    )
    result = residual + project(mixed_tokens, w_proj)
    return (result, (residual, normed, kv_input, mixed_tokens, retained))


def attention_layer_back(grad_out, saved, norm_gain, w_query, w_key, w_value, w_proj, is_cross):
    residual, normed, kv_input, mixed_tokens, retained = saved
    grad_low = grad_out.astype(jnp.bfloat16)
    grad_proj = weight_grad(mixed_tokens, grad_low)
    grad_mixed = input_grad(grad_low, w_proj).astype(jnp.bfloat16)
    grad_q_tok, grad_k_tok, grad_v_tok, grad_table = attention_backward(grad_mixed, retained)
    grad_wq = weight_grad(normed, grad_q_tok)
    grad_wk = weight_grad(kv_input, grad_k_tok)
    grad_wv = weight_grad(kv_input, grad_v_tok)
    grad_source = input_grad(grad_k_tok, w_key) + input_grad(grad_v_tok, w_value)
    grad_normed = input_grad(grad_q_tok, w_query)
    if not is_cross:
        grad_normed = grad_normed + grad_source
        grad_source = None
    grad_resid, grad_gain = norm_pullback(residual, norm_gain, grad_normed)
    return (
        grad_out + grad_resid,
        grad_source,
        (grad_gain, grad_wq, grad_wk, grad_wv, grad_proj, grad_table),
    )


def feed_layer(residual, norm_gain, w_gate, w_up, w_down):
    normed = rms_norm(residual, norm_gain).astype(jnp.bfloat16)
    gate_val = project(normed, w_gate)
    up_val = project(normed, w_up)
    hidden = gated(gate_val, up_val).astype(jnp.bfloat16)
    return (residual + project(hidden, w_down), (residual, normed, gate_val, up_val, hidden))


def feed_layer_back(grad_out, saved, norm_gain, w_gate, w_up, w_down):
    residual, normed, gate_val, up_val, hidden = saved
    grad_low = grad_out.astype(jnp.bfloat16)
    grad_down = weight_grad(hidden, grad_low)
    grad_hidden = input_grad(grad_low, w_down)
    _, pullback = jax.vjp(gated, gate_val, up_val)
    grad_gate, grad_up = pullback(grad_hidden)
    grad_gate = grad_gate.astype(jnp.bfloat16)
    grad_up = grad_up.astype(jnp.bfloat16)
    grad_wg = weight_grad(normed, grad_gate)
    grad_wu = weight_grad(normed, grad_up)
    grad_normed = input_grad(grad_gate, w_gate) + input_grad(grad_up, w_up)
    grad_resid, grad_gain = norm_pullback(residual, norm_gain, grad_normed)
    return (grad_out + grad_resid, (grad_gain, grad_wg, grad_wu, grad_down))


def per_device(
    enc_in,
    dec_in,
    enc_cot,
    dec_cot,
    enc_segments,
    dec_segments,
    buckets,
    enc_norm1,
    enc_query,
    enc_key,
    enc_value,
    enc_proj,
    enc_rel,
    enc_norm2,
    enc_gate,
    enc_up,
    enc_down,
    enc_final,
    dec_norm1,
    dec_query,
    dec_key,
    dec_value,
    dec_proj,
    dec_rel,
    dec_norm2,
    cross_query,
    cross_key,
    cross_value,
    cross_proj,
    dec_norm3,
    dec_gate,
    dec_up,
    dec_down,
):
    (
        enc_norm1,
        enc_query,
        enc_key,
        enc_value,
        enc_proj,
        enc_rel,
        enc_norm2,
        enc_gate,
        enc_up,
        enc_down,
        enc_final,
        dec_norm1,
        dec_query,
        dec_key,
        dec_value,
        dec_proj,
        dec_rel,
        dec_norm2,
        cross_query,
        cross_key,
        cross_value,
        cross_proj,
        dec_norm3,
        dec_gate,
        dec_up,
        dec_down,
    ) = (
        lax.all_gather(enc_norm1, "ctx", axis=0, tiled=True),
        lax.all_gather(enc_query, "ctx", axis=0, tiled=True),
        lax.all_gather(enc_key, "ctx", axis=0, tiled=True),
        lax.all_gather(enc_value, "ctx", axis=0, tiled=True),
        lax.all_gather(enc_proj, "ctx", axis=0, tiled=True),
        lax.all_gather(enc_rel, "ctx", axis=0, tiled=True),
        lax.all_gather(enc_norm2, "ctx", axis=0, tiled=True),
        lax.all_gather(enc_gate, "ctx", axis=0, tiled=True),
        lax.all_gather(enc_up, "ctx", axis=0, tiled=True),
        lax.all_gather(enc_down, "ctx", axis=0, tiled=True),
        lax.all_gather(enc_final, "ctx", axis=0, tiled=True),
        lax.all_gather(dec_norm1, "ctx", axis=0, tiled=True),
        lax.all_gather(dec_query, "ctx", axis=0, tiled=True),
        lax.all_gather(dec_key, "ctx", axis=0, tiled=True),
        lax.all_gather(dec_value, "ctx", axis=0, tiled=True),
        lax.all_gather(dec_proj, "ctx", axis=0, tiled=True),
        lax.all_gather(dec_rel, "ctx", axis=0, tiled=True),
        lax.all_gather(dec_norm2, "ctx", axis=0, tiled=True),
        lax.all_gather(cross_query, "ctx", axis=0, tiled=True),
        lax.all_gather(cross_key, "ctx", axis=0, tiled=True),
        lax.all_gather(cross_value, "ctx", axis=0, tiled=True),
        lax.all_gather(cross_proj, "ctx", axis=0, tiled=True),
        lax.all_gather(dec_norm3, "ctx", axis=0, tiled=True),
        lax.all_gather(dec_gate, "ctx", axis=0, tiled=True),
        lax.all_gather(dec_up, "ctx", axis=0, tiled=True),
        lax.all_gather(dec_down, "ctx", axis=0, tiled=True),
    )
    enc_norm1 = enc_norm1.astype(jnp.float32)
    enc_norm2 = enc_norm2.astype(jnp.float32)
    enc_final = enc_final.astype(jnp.float32)
    dec_norm1 = dec_norm1.astype(jnp.float32)
    dec_norm2 = dec_norm2.astype(jnp.float32)
    dec_norm3 = dec_norm3.astype(jnp.float32)
    heads_here = HEADS // lax.axis_size("sp")
    enc_table, enc_onehot = head_table(enc_rel, buckets[0], heads_here)
    dec_table, dec_onehot = head_table(dec_rel, buckets[1], heads_here)
    enc_x = enc_in.astype(jnp.float32)
    enc_mid, enc_saved_a = attention_layer(
        enc_x,
        None,
        enc_norm1,
        enc_query,
        enc_key,
        enc_value,
        enc_proj,
        enc_segments,
        enc_segments,
        enc_table,
        False,
    )
    enc_result, enc_saved_f = feed_layer(enc_mid, enc_norm2, enc_gate, enc_up, enc_down)
    memory = rms_norm(enc_result, enc_final).astype(jnp.bfloat16)
    dec_x = dec_in.astype(jnp.float32)
    dec_mid, dec_saved_a = attention_layer(
        dec_x,
        None,
        dec_norm1,
        dec_query,
        dec_key,
        dec_value,
        dec_proj,
        dec_segments,
        dec_segments,
        dec_table,
        True,
    )
    dec_cross, dec_saved_c = attention_layer(
        dec_mid,
        memory,
        dec_norm2,
        cross_query,
        cross_key,
        cross_value,
        cross_proj,
        dec_segments,
        enc_segments,
        None,
        False,
    )
    dec_result, dec_saved_f = feed_layer(dec_cross, dec_norm3, dec_gate, dec_up, dec_down)
    grad_dec, dec_ff_grads = feed_layer_back(
        dec_cot.astype(jnp.float32), dec_saved_f, dec_norm3, dec_gate, dec_up, dec_down
    )
    grad_dec, grad_memory, cross_grads = attention_layer_back(
        grad_dec, dec_saved_c, dec_norm2, cross_query, cross_key, cross_value, cross_proj, True
    )
    grad_dec, _, dec_self_grads = attention_layer_back(
        grad_dec, dec_saved_a, dec_norm1, dec_query, dec_key, dec_value, dec_proj, False
    )
    grad_enc_out, grad_final = norm_pullback(enc_result, enc_final, grad_memory)
    grad_enc, enc_ff_grads = feed_layer_back(
        enc_cot.astype(jnp.float32) + grad_enc_out,
        enc_saved_f,
        enc_norm2,
        enc_gate,
        enc_up,
        enc_down,
    )
    grad_enc, _, enc_self_grads = attention_layer_back(
        grad_enc, enc_saved_a, enc_norm1, enc_query, enc_key, enc_value, enc_proj, False
    )
    e_gain1, e_wq, e_wk, e_wv, e_wo, e_table = enc_self_grads
    e_gain2, e_wg, e_wu, e_wd = enc_ff_grads
    d_gain1, d_wq, d_wk, d_wv, d_wo, d_table = dec_self_grads
    c_gain, c_wq, c_wk, c_wv, c_wo, _ = cross_grads
    d_gain3, d_wg, d_wu, d_wd = dec_ff_grads
    e_rel = table_grad(e_table, enc_onehot, heads_here)
    d_rel = table_grad(d_table, dec_onehot, heads_here)
    shards = (
        lax.psum_scatter(e_gain1, "ctx", scatter_dimension=0, tiled=True),
        lax.psum_scatter(e_wq, "ctx", scatter_dimension=0, tiled=True),
        lax.psum_scatter(e_wk, "ctx", scatter_dimension=0, tiled=True),
        lax.psum_scatter(e_wv, "ctx", scatter_dimension=0, tiled=True),
        lax.psum_scatter(e_wo, "ctx", scatter_dimension=0, tiled=True),
        lax.psum_scatter(e_rel, "ctx", scatter_dimension=0, tiled=True),
        lax.psum_scatter(e_gain2, "ctx", scatter_dimension=0, tiled=True),
        lax.psum_scatter(e_wg, "ctx", scatter_dimension=0, tiled=True),
        lax.psum_scatter(e_wu, "ctx", scatter_dimension=0, tiled=True),
        lax.psum_scatter(e_wd, "ctx", scatter_dimension=0, tiled=True),
        lax.psum_scatter(grad_final, "ctx", scatter_dimension=0, tiled=True),
        lax.psum_scatter(d_gain1, "ctx", scatter_dimension=0, tiled=True),
        lax.psum_scatter(d_wq, "ctx", scatter_dimension=0, tiled=True),
        lax.psum_scatter(d_wk, "ctx", scatter_dimension=0, tiled=True),
        lax.psum_scatter(d_wv, "ctx", scatter_dimension=0, tiled=True),
        lax.psum_scatter(d_wo, "ctx", scatter_dimension=0, tiled=True),
        lax.psum_scatter(d_rel, "ctx", scatter_dimension=0, tiled=True),
        lax.psum_scatter(c_gain, "ctx", scatter_dimension=0, tiled=True),
        lax.psum_scatter(c_wq, "ctx", scatter_dimension=0, tiled=True),
        lax.psum_scatter(c_wk, "ctx", scatter_dimension=0, tiled=True),
        lax.psum_scatter(c_wv, "ctx", scatter_dimension=0, tiled=True),
        lax.psum_scatter(c_wo, "ctx", scatter_dimension=0, tiled=True),
        lax.psum_scatter(d_gain3, "ctx", scatter_dimension=0, tiled=True),
        lax.psum_scatter(d_wg, "ctx", scatter_dimension=0, tiled=True),
        lax.psum_scatter(d_wu, "ctx", scatter_dimension=0, tiled=True),
        lax.psum_scatter(d_wd, "ctx", scatter_dimension=0, tiled=True),
    )
    (
        s_gain1,
        s_wq,
        s_wk,
        s_wv,
        s_wo,
        s_rel,
        s_gain2,
        s_wg,
        s_wu,
        s_wd,
        s_final,
        t_gain1,
        t_wq,
        t_wk,
        t_wv,
        t_wo,
        t_rel,
        t_gain2,
        t_cq,
        t_ck,
        t_cv,
        t_co,
        t_gain3,
        t_wg,
        t_wu,
        t_wd,
    ) = shards
    reduced = (
        lax.psum(s_gain1.astype(jnp.bfloat16), "sp").astype(jnp.float32),
        lax.psum(s_wq.astype(jnp.bfloat16), "sp").astype(jnp.float32),
        lax.psum(s_wk.astype(jnp.bfloat16), "sp").astype(jnp.float32),
        lax.psum(s_wv.astype(jnp.bfloat16), "sp").astype(jnp.float32),
        lax.psum(s_wo.astype(jnp.bfloat16), "sp").astype(jnp.float32),
        lax.psum(s_rel.astype(jnp.bfloat16), "sp").astype(jnp.float32),
        lax.psum(s_gain2.astype(jnp.bfloat16), "sp").astype(jnp.float32),
        lax.psum(s_wg.astype(jnp.bfloat16), "sp").astype(jnp.float32),
        lax.psum(s_wu.astype(jnp.bfloat16), "sp").astype(jnp.float32),
        lax.psum(s_wd.astype(jnp.bfloat16), "sp").astype(jnp.float32),
        lax.psum(s_final.astype(jnp.bfloat16), "sp").astype(jnp.float32),
        lax.psum(t_gain1.astype(jnp.bfloat16), "sp").astype(jnp.float32),
        lax.psum(t_wq.astype(jnp.bfloat16), "sp").astype(jnp.float32),
        lax.psum(t_wk.astype(jnp.bfloat16), "sp").astype(jnp.float32),
        lax.psum(t_wv.astype(jnp.bfloat16), "sp").astype(jnp.float32),
        lax.psum(t_wo.astype(jnp.bfloat16), "sp").astype(jnp.float32),
        lax.psum(t_rel.astype(jnp.bfloat16), "sp").astype(jnp.float32),
        lax.psum(t_gain2.astype(jnp.bfloat16), "sp").astype(jnp.float32),
        lax.psum(t_cq.astype(jnp.bfloat16), "sp").astype(jnp.float32),
        lax.psum(t_ck.astype(jnp.bfloat16), "sp").astype(jnp.float32),
        lax.psum(t_cv.astype(jnp.bfloat16), "sp").astype(jnp.float32),
        lax.psum(t_co.astype(jnp.bfloat16), "sp").astype(jnp.float32),
        lax.psum(t_gain3.astype(jnp.bfloat16), "sp").astype(jnp.float32),
        lax.psum(t_wg.astype(jnp.bfloat16), "sp").astype(jnp.float32),
        lax.psum(t_wu.astype(jnp.bfloat16), "sp").astype(jnp.float32),
        lax.psum(t_wd.astype(jnp.bfloat16), "sp").astype(jnp.float32),
    )
    return (enc_result, dec_result, grad_enc, grad_dec) + tuple(reduced)


HG, CORE, SP = "hg", "core", "sp"
BLOCK_PAD = 128


def nt(left, right):
    return lax.dot_general(left, right, (((1,), (1,)), ((), ())), preferred_element_type=jnp.float32)


def tn(left, right):
    return lax.dot_general(left, right, (((0,), (0,)), ((), ())), preferred_element_type=jnp.float32)


def nn(left, right):
    return jnp.dot(left, right, preferred_element_type=jnp.float32)


def identity(size):
    rows = lax.broadcasted_iota(jnp.int32, (size, size), 0)
    cols = lax.broadcasted_iota(jnp.int32, (size, size), 1)
    return jnp.where(rows == cols, 1.0, 0.0).astype(jnp.bfloat16)


def only_head(array, head):
    lanes = lax.broadcasted_iota(jnp.int32, array.shape, 1)
    keep = (lanes >= head * HD) & (lanes < (head + 1) * HD)
    return jnp.where(keep, array, jnp.zeros_like(array))


def bias_mask_kernel(heads, block, causal, starts_ref, tables_ref, kdoc_ref, qdoc_ref, qpos_ref, qstart_ref, out_ref):
    rows_total, lanes = out_ref.shape[1], out_ref.shape[2]
    key_len = kdoc_ref.shape[0]
    strip = block + 2 * BLOCK_PAD
    for head in range(heads):
        if tables_ref is not None:
            row = tables_ref[head : head + 1, :]
            width = row.shape[1]
            left, right = tables_ref[head : head + 1, width - 2 : width - 1], tables_ref[head : head + 1, 0:1]
            places = lax.broadcasted_iota(jnp.int32, (rows_total, lanes), 0)
            fill = jnp.where(places < qstart_ref[...], left, right)
            out_ref[head] = fill.astype(jnp.bfloat16)
            wide = jnp.broadcast_to(row, (strip, width))
            for number in range(lanes // block):
                at = (number * block) % 128
                turned = pltpu.roll(wide, (width - (strip - 1) + at) % width, 1, stride=1, stride_axis=0)
                out_ref[head, pl.ds(pl.multiple_of(starts_ref[number], block), strip), number * block : (number + 1) * block] = turned[:, at : at + block].astype(jnp.bfloat16)
        allowed = kdoc_ref[...] == qdoc_ref[...]
        if causal:
            places = lax.broadcasted_iota(jnp.int32, (key_len, lanes), 0)
            allowed = allowed & (places <= qpos_ref[...])
        inside = pl.ds(BLOCK_PAD, key_len)
        if tables_ref is not None:
            out_ref[head, inside, :] = jnp.where(allowed, out_ref[head, inside, :].astype(jnp.float32), NEGATIVE).astype(jnp.bfloat16)
        else:
            out_ref[head, inside, :] = jnp.where(allowed, 0.0, NEGATIVE).astype(jnp.bfloat16)


def bias_mask(starts, tables, kdoc, qdoc, qpos, block, causal):
    key_len, lanes = kdoc.shape[0], qdoc.shape[1]
    heads = tables.shape[0] if tables is not None else 1
    qstart = jnp.repeat(starts, block)[None, :]
    operands = [starts] + ([tables] if tables is not None else []) + [kdoc, qdoc, qpos, qstart]

    def body(*refs):
        refs = list(refs)
        if tables is None:
            refs.insert(1, None)
        bias_mask_kernel(heads, block, causal, *refs)

    return pl.pallas_call(
        body,
        out_shape=jax.ShapeDtypeStruct((heads, key_len + 2 * BLOCK_PAD, lanes), jnp.bfloat16),
        in_specs=[pl.BlockSpec(memory_space=pltpu.SMEM)] + [pl.BlockSpec(memory_space=pltpu.VMEM)] * (len(operands) - 1),
        out_specs=pl.BlockSpec(memory_space=pltpu.VMEM),
        compiler_params=pltpu.CompilerParams(vmem_limit_bytes=VMEM_BYTES),
    )(*operands)


VMEM_BYTES = 56 << 20


def send(src, dst, send_sem, recv_sem, to):
    copy = pltpu.make_async_remote_copy(
        src_ref=src, dst_ref=dst, send_sem=send_sem, recv_sem=recv_sem, device_id=to, device_id_type=pl.DeviceIdType.MESH
    )
    copy.start()
    return copy


def arrived(dst, send_sem, recv_sem, to):
    pltpu.make_async_remote_copy(
        src_ref=dst, dst_ref=dst, send_sem=send_sem, recv_sem=recv_sem, device_id=to, device_id_type=pl.DeviceIdType.MESH
    ).wait_recv()


class Place:
    def __init__(self, groups, cores, parts):
        self.groups, self.cores, self.parts = groups, cores, parts
        self.group, self.core, self.part = lax.axis_index(HG), lax.axis_index(CORE), lax.axis_index(SP)

    def ahead(self, step):
        return lax.rem(self.group + step, self.groups)

    def behind(self, step):
        return lax.rem(self.group + self.groups - step, self.groups)

    def chip(self, group):
        return (group, self.core, self.part)

    def sibling(self):
        return (self.group, 1 - self.core, self.part)

    def plane(self, step):
        return lax.rem(self.part + step, self.parts)

    def plane_behind(self, step):
        return lax.rem(self.part + self.parts - step, self.parts)

    def at_plane(self, part):
        return (self.group, self.core, part)

    def greet(self, chips=True, sibling=True, planes=False):
        barrier = pltpu.get_barrier_semaphore()
        partners = []
        if chips:
            partners += [self.chip(self.ahead(step)) for step in range(1, self.groups)]
        if sibling:
            partners.append(self.sibling())
        if planes:
            partners += [self.at_plane(self.plane(step)) for step in range(1, self.parts)]
        for partner in partners:
            pl.semaphore_signal(barrier, inc=1, device_id=partner, device_id_type=pl.DeviceIdType.MESH)
        pl.semaphore_wait(barrier, len(partners))


def recut_kernel(sizes, counts, *refs):
    cols, rows = counts
    col_refs, refs = refs[:cols], refs[cols:]
    row_refs, refs = refs[:rows], refs[rows:]
    col_outs, refs = refs[:cols], refs[cols:]
    row_outs, refs = refs[:rows], refs[rows:]
    sent, got, relay_sent, relay_got, pair_sent, pair_got, local = refs
    place = Place(*sizes)
    group, core = place.group, place.core
    place.greet()
    pending, copies = [], []
    for index in range(cols):
        out = col_outs[index]
        for step in range(1, place.groups):
            to = place.ahead(step)
            pending.append(send(col_refs[index].at[to], out.at[group, core], sent.at[index, step], got.at[index, step], place.chip(to)))
        pending.append(
            send(col_refs[index].at[group], out.at[group, core], relay_sent.at[index, 0], relay_got.at[index, 0], place.sibling())
        )
        copies.append(pltpu.make_async_copy(col_refs[index].at[group], out.at[group, core], local.at[index]))
        copies[-1].start()
    for index in range(rows):
        out = row_outs[index]
        pending.append(send(row_refs[index], out.at[core], pair_sent.at[index], pair_got.at[index], place.sibling()))
        copies.append(pltpu.make_async_copy(row_refs[index], out.at[core], local.at[cols + index]))
        copies[-1].start()
    for index in range(cols):
        out = col_outs[index]
        for step in range(1, place.groups):
            source = place.behind(step)
            slot = out.at[source, core]
            arrived(slot, sent.at[index, step], got.at[index, step], place.chip(source))
            pending.append(send(slot, slot, relay_sent.at[index, step], relay_got.at[index, step], place.sibling()))
    for index in range(cols):
        out = col_outs[index]
        for step in range(place.groups):
            slot = out.at[place.behind(step), 1 - core]
            arrived(slot, relay_sent.at[index, step], relay_got.at[index, step], place.sibling())
    for index in range(rows):
        arrived(row_outs[index].at[1 - core], pair_sent.at[index], pair_got.at[index], place.sibling())
    for copy in copies:
        copy.wait()
    for copy in pending:
        copy.wait_send()


def recut(sizes, collective_id, col_packs, row_packs):
    groups, cores, _ = sizes
    cols, rows = len(col_packs), len(row_packs)
    anywhere = pl.BlockSpec(memory_space=pl.ANY)
    shapes = [jax.ShapeDtypeStruct((groups, cores) + w.shape[1:], w.dtype) for w in col_packs]
    shapes += [jax.ShapeDtypeStruct((cores,) + w.shape, w.dtype) for w in row_packs]
    dma = pltpu.SemaphoreType.DMA
    got = pl.pallas_call(
        functools.partial(recut_kernel, sizes, (cols, rows)),
        out_shape=tuple(shapes),
        in_specs=[anywhere] * (cols + rows),
        out_specs=(anywhere,) * (cols + rows),
        scratch_shapes=[
            dma((cols, groups)), dma((cols, groups)), dma((cols, groups)), dma((cols, groups)),
            dma((rows,)), dma((rows,)), dma((cols + rows,)),
        ],
        compiler_params=pltpu.CompilerParams(collective_id=collective_id, has_side_effects=True, vmem_limit_bytes=VMEM_BYTES),
    )(*col_packs, *row_packs)
    whole_cols = [w.reshape(groups * cores * w.shape[2], w.shape[3]) for w in got[:cols]]
    return whole_cols, [w.reshape(cores * w.shape[1], w.shape[2]) for w in got[cols:]]


def give_rows_kernel(sizes, counts, *refs):
    cols, rows = counts
    col_refs, refs = refs[:cols], refs[cols:]
    row_refs, refs = refs[:rows], refs[rows:]
    col_outs, refs = refs[:cols], refs[cols:]
    row_outs, refs = refs[:rows], refs[rows:]
    col_sibs, refs = refs[:cols], refs[cols:]
    col_sums, refs = refs[:cols], refs[cols:]
    row_sibs, refs = refs[:rows], refs[rows:]
    sent, got, pair_sent, pair_got, row_sent, row_got = refs
    place = Place(*sizes)
    group, core = place.group, place.core
    place.greet()
    pending = []
    for index in range(cols):
        for step in range(place.groups):
            to = place.ahead(step)
            pending.append(
                send(
                    col_refs[index].at[to, 1 - core], col_sibs[index].at[to],
                    pair_sent.at[index, step], pair_got.at[index, step], place.sibling(),
                )
            )
    for index in range(rows):
        pending.append(
            send(row_refs[index].at[1 - core], row_sibs[index], row_sent.at[index], row_got.at[index], place.sibling())
        )
    for index in range(cols):
        for step in list(range(1, place.groups)) + [0]:
            to = place.ahead(step)
            arrived(col_sibs[index].at[to], pair_sent.at[index, step], pair_got.at[index, step], place.sibling())
            both = col_refs[index][to, core].astype(jnp.float32) + col_sibs[index][to].astype(jnp.float32)
            if step:
                col_sums[index][to] = both.astype(jnp.bfloat16)
                pending.append(
                    send(
                        col_sums[index].at[to], col_outs[index].at[group],
                        sent.at[index, step], got.at[index, step], place.chip(to),
                    )
                )
            else:
                col_outs[index][group] = both.astype(jnp.bfloat16)
    for index in range(rows):
        arrived(row_sibs[index], row_sent.at[index], row_got.at[index], place.sibling())
        both = row_refs[index][core].astype(jnp.float32) + row_sibs[index][...].astype(jnp.float32)
        row_outs[index][...] = both.astype(jnp.bfloat16)
    for index in range(cols):
        for step in range(1, place.groups):
            source = place.behind(step)
            arrived(col_outs[index].at[source], sent.at[index, step], got.at[index, step], place.chip(source))
    for copy in pending:
        copy.wait_send()


def give_rows(sizes, collective_id, col_grads, row_grads):
    groups, cores, _ = sizes
    cols, rows = len(col_grads), len(row_grads)
    vmem = pl.BlockSpec(memory_space=pltpu.VMEM)
    col_in = [w.reshape(groups, cores, w.shape[0] // (groups * cores), w.shape[1]) for w in col_grads]
    row_in = [w.reshape(cores, w.shape[0] // cores, w.shape[1]) for w in row_grads]
    col_own = [(groups,) + w.shape[2:] for w in col_in]
    row_own = [w.shape[1:] for w in row_in]
    dma = pltpu.SemaphoreType.DMA
    got = pl.pallas_call(
        functools.partial(give_rows_kernel, sizes, (cols, rows)),
        out_shape=tuple(jax.ShapeDtypeStruct(s, jnp.bfloat16) for s in col_own + row_own),
        in_specs=[vmem] * (cols + rows),
        out_specs=(vmem,) * (cols + rows),
        scratch_shapes=[pltpu.VMEM(s, jnp.bfloat16) for s in col_own + col_own + row_own]
        + [dma((cols, groups))] * 4
        + [dma((rows,))] * 2,
        compiler_params=pltpu.CompilerParams(collective_id=collective_id, has_side_effects=True, vmem_limit_bytes=VMEM_BYTES),
    )(*col_in, *row_in)
    return got[:cols], got[cols:]


def spread_start(place, buf, sent, got):
    mine = buf.at[place.group]
    return [
        send(mine, mine, sent.at[step], got.at[step], place.chip(place.ahead(step))) for step in range(1, place.groups)
    ]


def spread_wait(place, buf, sent, got):
    for step in range(1, place.groups):
        source = place.behind(step)
        arrived(buf.at[source], sent.at[step], got.at[step], place.chip(source))


def collect_start(place, partial, out_buf, in_buf, sent, got):
    out_buf[...] = partial.astype(jnp.bfloat16).reshape(out_buf.shape)
    pending = []
    for step in range(1, place.groups):
        to = place.ahead(step)
        pending.append(send(out_buf.at[to], in_buf.at[place.group], sent.at[step], got.at[step], place.chip(to)))
    return pending


def collect_wait(place, out_buf, in_buf, sent, got):
    total = out_buf[place.group].astype(jnp.float32)
    for step in range(1, place.groups):
        source = place.behind(step)
        arrived(in_buf.at[source], sent.at[step], got.at[step], place.chip(source))
        total = total + in_buf[source].astype(jnp.float32)
    return total


def whole(buf):
    return buf[...].reshape(buf.shape[0] * buf.shape[1], buf.shape[2])


def gelu_and_slope(v):
    scale, cubic = math.sqrt(2.0 / math.pi), 0.044715
    t = jnp.tanh(scale * (v + cubic * v * v * v))
    return 0.5 * v * (1.0 + t), 0.5 * (1.0 + t) + 0.5 * v * (1.0 - t * t) * scale * (1.0 + 3.0 * cubic * v * v)


def norm_back(x, g, dn):
    r = lax.rsqrt(jnp.mean(x * x, axis=-1, keepdims=True) + EPSILON)
    w = dn * g
    dx = r * w - x * (r * r * r) * jnp.mean(w * x, axis=-1, keepdims=True)
    return dx, jnp.sum(dn * x * r, axis=0, keepdims=True)


def low(value):
    return value.astype(jnp.bfloat16)


def feed_forward_kernel(sizes, x_ref, gain_ref, final_ref, gu_ref, down_ref, y_ref, last_ref, n_ref, n_buf, p_buf, r_buf, sent, got):
    place = Place(*sizes)
    place.greet(sibling=False)
    x = x_ref[...]
    n_buf[place.group] = low(rms_norm(x, gain_ref[...]))
    pending = spread_start(place, n_buf, sent.at[0], got.at[0])
    spread_wait(place, n_buf, sent.at[0], got.at[0])
    n = whole(n_buf)
    hidden = down_ref.shape[0]
    gu = nn(n, gu_ref[...])
    h = low(gelu_and_slope(gu[:, :hidden])[0] * gu[:, hidden:])
    pending += collect_start(place, nn(h, down_ref[...]), p_buf, r_buf, sent.at[1], got.at[1])
    n_ref[...] = n
    y = x + collect_wait(place, p_buf, r_buf, sent.at[1], got.at[1])
    y_ref[...] = y
    last_ref[...] = low(rms_norm(y, final_ref[...]))
    for copy in pending:
        copy.wait_send()


def feed_back_part(n, dyb, gu_ref, down_ref):
    hidden = down_ref.shape[0]
    gu = nn(n, gu_ref[...])
    g, u = gu[:, :hidden], gu[:, hidden:]
    act, slope = gelu_and_slope(g)
    h = low(act * u)
    dh = nt(dyb, down_ref[...])
    dgu = jnp.concatenate([low(dh * u * slope), low(dh * act)], axis=1)
    return h, dgu


def feed_both_kernel(
    sizes, x_ref, cot_ref, gain_ref, gu_ref, down_ref,
    y_ref, dx_ref, dgain_ref, dgu_ref, ddown_ref,
    n_buf, d_buf, py_buf, ry_buf, pn_buf, rn_buf, sent, got,
):
    place = Place(*sizes)
    place.greet(sibling=False)
    x = x_ref[...]
    n_buf[place.group] = low(rms_norm(x, gain_ref[...]))
    d_buf[place.group] = cot_ref[...]
    pending = spread_start(place, n_buf, sent.at[0], got.at[0]) + spread_start(place, d_buf, sent.at[1], got.at[1])
    spread_wait(place, n_buf, sent.at[0], got.at[0])
    spread_wait(place, d_buf, sent.at[1], got.at[1])
    n, dyb = whole(n_buf), whole(d_buf)
    h, dgu = feed_back_part(n, dyb, gu_ref, down_ref)
    pending += collect_start(place, nt(dgu, gu_ref[...]), pn_buf, rn_buf, sent.at[2], got.at[2])
    pending += collect_start(place, nn(h, down_ref[...]), py_buf, ry_buf, sent.at[3], got.at[3])
    dgu_ref[...] = low(tn(n, dgu))
    ddown_ref[...] = low(tn(h, dyb))
    dn = collect_wait(place, pn_buf, rn_buf, sent.at[2], got.at[2])
    back, dgain = norm_back(x, gain_ref[...], dn)
    dx_ref[...] = cot_ref[...].astype(jnp.float32) + back
    dgain_ref[...] = dgain
    y_ref[...] = x + collect_wait(place, py_buf, ry_buf, sent.at[3], got.at[3])
    for copy in pending:
        copy.wait_send()


def feed_back_kernel(
    sizes, x_ref, y_ref, cot_ref, dlast_ref, gain_ref, final_ref, n_ref, gu_ref, down_ref,
    dx_ref, dgain_ref, dfinal_ref, dgu_ref, ddown_ref,
    d_buf, pn_buf, rn_buf, sent, got,
):
    place = Place(*sizes)
    place.greet(sibling=False)
    back, dfinal = norm_back(y_ref[...], final_ref[...], dlast_ref[...])
    dfinal_ref[...] = dfinal
    dy = cot_ref[...].astype(jnp.float32) + back
    d_buf[place.group] = low(dy)
    pending = spread_start(place, d_buf, sent.at[0], got.at[0])
    spread_wait(place, d_buf, sent.at[0], got.at[0])
    n, dyb = n_ref[...], whole(d_buf)
    h, dgu = feed_back_part(n, dyb, gu_ref, down_ref)
    pending += collect_start(place, nt(dgu, gu_ref[...]), pn_buf, rn_buf, sent.at[1], got.at[1])
    dgu_ref[...] = low(tn(n, dgu))
    ddown_ref[...] = low(tn(h, dyb))
    dn = collect_wait(place, pn_buf, rn_buf, sent.at[1], got.at[1])
    back, dgain = norm_back(x_ref[...], gain_ref[...], dn)
    dx_ref[...] = dy + back
    dgain_ref[...] = dgain
    for copy in pending:
        copy.wait_send()


def stage(sizes, collective_id, kernel, operands, outs, scratch, copies):
    vmem = pl.BlockSpec(memory_space=pltpu.VMEM)
    dma = pltpu.SemaphoreType.DMA
    return pl.pallas_call(
        functools.partial(kernel, sizes),
        out_shape=tuple(jax.ShapeDtypeStruct(shape, dtype) for shape, dtype in outs),
        in_specs=[vmem] * len(operands),
        out_specs=(vmem,) * len(outs),
        scratch_shapes=[pltpu.VMEM(s, jnp.bfloat16) if isinstance(s, tuple) else s for s in scratch] + [dma(copies), dma(copies)],
        compiler_params=pltpu.CompilerParams(collective_id=collective_id, has_side_effects=True, vmem_limit_bytes=VMEM_BYTES),
    )(*operands)


def head_scores(kv_ref, masked_q, bm_ref, head, chunk):
    rows = kv_ref.shape[1] * kv_ref.shape[2] * kv_ref.shape[3]
    width = masked_q.shape[1]
    bias_head = head if bm_ref.shape[0] > 1 else 0
    at = pl.multiple_of(BLOCK_PAD + chunk * rows, 128)
    keys = kv_ref[chunk].reshape(rows, 2 * width)[:, :width]
    return nt(keys, masked_q) + bm_ref[bias_head, pl.ds(at, rows), :].astype(jnp.float32)


def value_side(kv_ref, chunk):
    rows = kv_ref.shape[1] * kv_ref.shape[2] * kv_ref.shape[3]
    lanes = kv_ref.shape[4]
    first = lanes // 2 // 128 * 128
    return kv_ref[chunk].reshape(rows, lanes)[:, first:]


def mix_part(q, kv_ref, bm_ref, o_ref, lse_ref, s_ref, p_ref, ot_ref):
    chunks = kv_ref.shape[0]
    rows = kv_ref.shape[1] * kv_ref.shape[2] * kv_ref.shape[3]
    queries, width = q.shape
    for head in range(width // HD):
        masked_q = only_head(q, head)

        def first(chunk, top):
            scores = head_scores(kv_ref, masked_q, bm_ref, head, chunk)
            s_ref[pl.ds(pl.multiple_of(chunk * rows, rows), rows), :] = scores
            return jnp.maximum(top, jnp.max(scores, axis=0, keepdims=True))

        top = lax.fori_loop(0, chunks, first, jnp.full((1, queries), NEGATIVE, jnp.float32))

        def second(chunk, carried):
            total, mixed = carried
            weights = jnp.exp(s_ref[pl.ds(pl.multiple_of(chunk * rows, rows), rows), :] - top)
            values = value_side(kv_ref, chunk)
            values_t = low(nt(identity(values.shape[1]), values))
            low_at = values.shape[1] - width + head * HD
            mixed = mixed + nn(values_t[low_at : low_at + HD], low(weights))
            return total + jnp.sum(weights, axis=0, keepdims=True), mixed

        start = (jnp.zeros((1, queries), jnp.float32), jnp.zeros((HD, queries), jnp.float32))
        total, mixed = lax.fori_loop(0, chunks, second, start)
        lse_ref[:, head * queries : (head + 1) * queries] = top + jnp.log(total)
        ot_ref[head * HD : (head + 1) * HD, :] = low(mixed / total)
    o_ref[...] = low(nt(identity(queries), ot_ref[...]))


def keys_send(place, kv_ref, base, sent, got):
    mine = kv_ref.at[:, place.core, place.part]
    pending = [
        send(mine, mine, sent.at[base, step], got.at[base, step], place.at_plane(place.plane(step)))
        for step in range(1, place.parts)
    ]
    pending.append(send(mine, mine, sent.at[base + 1, 0], got.at[base + 1, 0], place.sibling()))
    return pending


def keys_relay(place, kv_ref, base, sent, got):
    pending = []
    for step in range(1, place.parts):
        source = place.plane_behind(step)
        slot = kv_ref.at[:, place.core, source]
        arrived(slot, sent.at[base, step], got.at[base, step], place.at_plane(source))
        pending.append(send(slot, slot, sent.at[base + 1, step], got.at[base + 1, step], place.sibling()))
    return pending


def keys_wait(place, kv_ref, base, sent, got):
    for step in range(place.parts):
        slot = kv_ref.at[:, 1 - place.core, place.plane_behind(step)]
        arrived(slot, sent.at[base + 1, step], got.at[base + 1, step], place.sibling())


def attend_kernel(sizes, crosses, *refs):
    place = Place(*sizes)
    refs = list(refs)

    def take(count):
        taken, refs[:] = refs[:count], refs[count:]
        return taken

    count = len(crosses)
    ins = [take(6 if cross else 5) for cross in crosses]
    outs = [take(7 if cross else 6) for cross in crosses]
    s_ref, p_ref, ot_ref = take(3)
    bufs = [take(4 if cross else 3) for cross in crosses]
    sent, got = take(2)
    place.greet(planes=True)
    pending = []
    for index, cross in enumerate(crosses):
        x_ref, gain_ref = ins[index][0], ins[index][1]
        if cross:
            bufs[index][3][place.group] = ins[index][5][...]
            pending += spread_start(place, bufs[index][3], sent.at[5 * index + 4], got.at[5 * index + 4])
        bufs[index][0][place.group] = low(rms_norm(x_ref[...].astype(jnp.float32), gain_ref[...]))
        pending += spread_start(place, bufs[index][0], sent.at[5 * index], got.at[5 * index])
    queries = []
    for index, cross in enumerate(crosses):
        w_ref, kv_ref = ins[index][2], outs[index][3]
        kv_width = kv_ref.shape[4]
        n_buf = bufs[index][0]
        if cross:
            source = bufs[index][3]
            spread_wait(place, source, sent.at[5 * index + 4], got.at[5 * index + 4])
            kv = low(nn(whole(source), w_ref[:, :kv_width]))
            outs[index][6][...] = whole(source)
        else:
            spread_wait(place, n_buf, sent.at[5 * index], got.at[5 * index])
            both = low(nn(whole(n_buf), w_ref[...]))
            kv, q = both[:, :kv_width], both[:, kv_width:]
        kv_ref[:, place.core, place.part] = kv.reshape(kv_ref.shape[0], kv_ref.shape[3], kv_width)
        pending += keys_send(place, kv_ref, 5 * index + 1, sent, got)
        if cross:
            spread_wait(place, n_buf, sent.at[5 * index], got.at[5 * index])
            q = low(nn(whole(n_buf), w_ref[:, kv_width:]))
        outs[index][1][...] = whole(n_buf)
        outs[index][2][...] = q
        queries.append(q)
    for index in range(count):
        pending += keys_relay(place, outs[index][3], 5 * index + 1, sent, got)
    for index in range(count):
        x_ref, wo_ref, bm_ref = ins[index][0], ins[index][3], ins[index][4]
        kv_ref, o_ref, lse_ref = outs[index][3], outs[index][4], outs[index][5]
        keys_wait(place, kv_ref, 5 * index + 1, sent, got)
        mix_part(outs[index][2][...], kv_ref, bm_ref, o_ref, lse_ref, s_ref, p_ref, ot_ref)
        share = nn(o_ref[...], wo_ref[...])
        pending += collect_start(place, share, bufs[index][1], bufs[index][2], sent.at[5 * index + 3], got.at[5 * index + 3])
    for index in range(count):
        total = collect_wait(place, bufs[index][1], bufs[index][2], sent.at[5 * index + 3], got.at[5 * index + 3])
        outs[index][0][...] = ins[index][0][...].astype(jnp.float32) + total
    for copy in pending:
        copy.wait_send()


def attend(sizes, collective_id, layers):
    groups, cores, parts = sizes
    operands, outs, scratch, crosses = [], [], [], []
    f32, bf16 = jnp.float32, jnp.bfloat16
    for x, gain, w, wo, bm, memory in layers:
        block, model = x.shape
        width = wo.shape[0]
        tokens = groups * block
        operands += [x, gain, w, wo, bm] + ([] if memory is None else [memory])
        outs += [
            ((block, model), f32), ((tokens, model), bf16), ((tokens, width), bf16),
            ((groups, cores, parts, block, 2 * width), bf16), ((tokens, width), bf16), ((1, width // HD * tokens), f32),
        ]
        if memory is not None:
            outs.append(((tokens, model), bf16))
        scratch += [(groups, block, model)] * (3 if memory is None else 4)
        crosses.append(memory is not None)
    keys = cores * parts * tokens
    first = [pltpu.VMEM((keys, tokens), f32), (keys, tokens), (width, tokens)]
    copies = (5 * len(layers), max(groups, parts))
    got = stage(sizes, collective_id, lambda s, *refs: attend_kernel(s, crosses, *refs), operands, outs, first + scratch, copies)
    results, at = [], 0
    for cross in crosses:
        size = 7 if cross else 6
        results.append(tuple(got[at : at + size]) + (() if cross else (None,)))
        at += size
    return results


def mix_back_part(starts, q, do, kv_ref, lse_ref, bm_ref, strip_ref, edge_ref, dkv_ref, p_ref, dp_ref, ds_ref, pb_ref, ot_ref):
    chunks, _, _, block, lanes = kv_ref.shape
    rows = kv_ref.shape[1] * kv_ref.shape[2] * block
    queries, width = q.shape
    heads = width // HD
    biased = strip_ref is not None
    strip = block + 2 * BLOCK_PAD
    first_value = width // 128 * 128
    lead = width - first_value
    do_wide = jnp.concatenate([jnp.zeros((queries, lead), do.dtype), do], axis=1) if lead else do

    def only_value_head(head):
        at = lax.broadcasted_iota(jnp.int32, do_wide.shape, 1)
        keep = (at >= lead + head * HD) & (at < lead + (head + 1) * HD)
        return jnp.where(keep, do_wide, jnp.zeros_like(do_wide))

    if biased:
        none = jnp.zeros((BLOCK_PAD, heads * queries), jnp.bfloat16)
        ds_ref[0:BLOCK_PAD, :] = none
        ds_ref[BLOCK_PAD + chunks * rows :, :] = none
        cores = kv_ref.shape[1]
        parts = kv_ref.shape[2]
        of_lane = lax.broadcasted_iota(jnp.int32, (1, queries), 1) // block
        lane_start = ((cores * of_lane + starts.core) * parts + starts.part) * block
    for head in range(heads):
        masked_q, masked_do = only_head(q, head), only_value_head(head)
        across = slice(head * queries, (head + 1) * queries)

        def first(chunk, inner):
            inside = pl.ds(pl.multiple_of(chunk * rows, rows), rows)
            p = jnp.exp(head_scores(kv_ref, masked_q, bm_ref, head, chunk) - lse_ref[:, across])
            dp = nt(value_side(kv_ref, chunk), masked_do)
            p_ref[inside, :] = p
            dp_ref[inside, :] = dp
            pb_ref[inside, across] = low(p)
            return inner + jnp.sum(p * dp, axis=0, keepdims=True)

        inner = lax.fori_loop(0, chunks, first, jnp.zeros((1, queries), jnp.float32))

        def second(chunk, carried):
            left, right, back = carried
            at = pl.multiple_of(chunk * rows, rows)
            ds = low(p_ref[pl.ds(at, rows), :] * (dp_ref[pl.ds(at, rows), :] - inner))
            ds_ref[pl.ds(BLOCK_PAD + at, rows), across] = ds
            keys = kv_ref[chunk].reshape(rows, lanes)[:, :width]
            keys_t = low(nt(identity(width), keys))
            back = back + nn(keys_t[head * HD : (head + 1) * HD], ds)
            if biased:
                wide = ds.astype(jnp.float32)
                places = lax.broadcasted_iota(jnp.int32, wide.shape, 0) + (at + BLOCK_PAD)
                left = left + jnp.sum(jnp.where(places < lane_start, wide, 0.0), axis=0, keepdims=True)
                right = right + jnp.sum(jnp.where(places >= lane_start + strip, wide, 0.0), axis=0, keepdims=True)
            return left, right, back

        nothing = jnp.zeros((1, queries), jnp.float32)
        left, right, back = lax.fori_loop(0, chunks, second, (nothing, nothing, jnp.zeros((HD, queries), jnp.float32)))
        ot_ref[head * HD : (head + 1) * HD, :] = low(back)
        if biased:
            edge_ref[2 * head : 2 * head + 1, :] = left
            edge_ref[2 * head + 1 : 2 * head + 2, :] = right
            total = jnp.zeros((strip, block), jnp.float32)
            for number in range(queries // block):
                at = pl.multiple_of(((cores * number + starts.core) * parts + starts.part) * block, block)
                low_at = head * queries + number * block
                total = total + ds_ref[pl.ds(at, strip), low_at : low_at + block].astype(jnp.float32)
            strip_ref[head] = total
    stacked_q = jnp.concatenate([only_head(q, head) for head in range(heads)], axis=0)
    if lead:
        stacked_q = jnp.concatenate([stacked_q, jnp.zeros((stacked_q.shape[0], lead), stacked_q.dtype)], axis=1)
    stacked_do = jnp.concatenate([only_value_head(head) for head in range(heads)], axis=0)

    def third(chunk, carried):
        at = pl.multiple_of(chunk * rows, rows)
        dk = nn(ds_ref[pl.ds(BLOCK_PAD + at, rows), :], stacked_q)
        dv = nn(pb_ref[pl.ds(at, rows), :], stacked_do)
        if lead:
            shared = dk[:, first_value:] + dv[:, : 2 * lead]
            both = jnp.concatenate([dk[:, :first_value], shared, dv[:, 2 * lead :]], axis=1)
        else:
            both = jnp.concatenate([dk, dv], axis=1)
        dkv_ref[chunk] = low(both).reshape(dkv_ref.shape[1:])
        return carried

    lax.fori_loop(0, chunks, third, 0)
    return low(nt(identity(queries), ot_ref[...]))


def attend_back_kernel(sizes, cross, *refs):
    refs = list(refs)

    def take(count):
        taken, refs[:] = refs[:count], refs[count:]
        return taken

    place = Place(*sizes)
    x_ref, gain_ref, dy_ref, n_ref, q_ref, kv_ref, o_ref, lse_ref, w_ref, wo_ref, bm_ref = take(11)
    memory_ref = take(1)[0] if cross else None
    dx_ref, dgain_ref, dw_ref, dwo_ref = take(4)
    strip_ref, edge_ref = (None, None) if cross else take(2)
    dmem_ref = take(1)[0] if cross else None
    p_ref, dp_ref, ds_ref, pb_ref, ot_ref, dkv_ref, sib_ref, zout_ref, zin_ref, d_buf, pn_buf, rn_buf = take(12)
    pm_buf, rm_buf = take(2) if cross else (None, None)
    sent, got = take(2)
    place.greet(planes=True)
    dy = dy_ref[...]
    d_buf[place.group] = low(dy)
    pending = spread_start(place, d_buf, sent.at[0], got.at[0])
    spread_wait(place, d_buf, sent.at[0], got.at[0])
    dyb = whole(d_buf)
    do = low(nt(dyb, wo_ref[...]))
    dq = mix_back_part(place, q_ref[...], do, kv_ref, lse_ref, bm_ref, strip_ref, edge_ref, dkv_ref, p_ref, dp_ref, ds_ref, pb_ref, ot_ref)
    mine = place.core
    pending.append(send(dkv_ref.at[:, 1 - mine], sib_ref, sent.at[1, 0], got.at[1, 0], place.sibling()))
    kv_width = kv_ref.shape[4]
    width = kv_width // 2
    dwo_ref[...] = low(tn(o_ref[...], dyb))
    dn_share = nt(dq, w_ref[:, kv_width:])
    dw_ref[:, kv_width:] = low(tn(n_ref[...], dq))
    if cross:
        pending += collect_start(place, dn_share, pn_buf, rn_buf, sent.at[3], got.at[3])
    arrived(sib_ref, sent.at[1, 0], got.at[1, 0], place.sibling())
    for step in list(range(1, place.parts)) + [0]:
        to = place.plane(step)
        zout_ref[to] = low(dkv_ref[:, mine, to].astype(jnp.float32) + sib_ref[:, to].astype(jnp.float32))
        if step:
            pending.append(send(zout_ref.at[to], zin_ref.at[place.part], sent.at[2, step], got.at[2, step], place.at_plane(to)))
    total = zout_ref[place.part].astype(jnp.float32)
    for step in range(1, place.parts):
        source = place.plane_behind(step)
        arrived(zin_ref.at[source], sent.at[2, step], got.at[2, step], place.at_plane(source))
        total = total + zin_ref[source].astype(jnp.float32)
    dkv = low(total).reshape(q_ref.shape[0], kv_width)
    if cross:
        pending += collect_start(place, nt(dkv, w_ref[:, :kv_width]), pm_buf, rm_buf, sent.at[4], got.at[4])
        dw_ref[:, :kv_width] = low(tn(memory_ref[...], dkv))
        dmem_ref[...] = collect_wait(place, pm_buf, rm_buf, sent.at[4], got.at[4])
    else:
        share = dn_share + nt(dkv, w_ref[:, :kv_width])
        pending += collect_start(place, share, pn_buf, rn_buf, sent.at[3], got.at[3])
        dw_ref[:, :kv_width] = low(tn(n_ref[...], dkv))
    dn = collect_wait(place, pn_buf, rn_buf, sent.at[3], got.at[3])
    back, dgain = norm_back(x_ref[...].astype(jnp.float32), gain_ref[...], dn)
    dx_ref[...] = dy + back
    dgain_ref[...] = dgain
    for copy in pending:
        copy.wait_send()


def attend_back(sizes, collective_id, x, gain, dy, kept, w, wo, bm, cross):
    groups, cores, parts = sizes
    _, n, q, kv, o, lse, memory = kept
    block, model = x.shape
    tokens, width = q.shape
    heads = width // HD
    keys = cores * parts * tokens
    f32 = jnp.float32
    operands = [x, gain, dy, n, q, kv, o, lse, w, wo, bm] + ([memory] if cross else [])
    bf16 = jnp.bfloat16
    outs = [((block, model), f32), ((1, model), f32), (w.shape, bf16), (wo.shape, bf16)]
    if cross:
        outs.append(((block, model), f32))
    else:
        outs += [((heads, block + 2 * BLOCK_PAD, block), f32), ((2 * heads, tokens), f32)]
    half = (groups, parts, block, 2 * width)
    turned = (parts, groups, block, 2 * width)
    scratch = [
        pltpu.VMEM((keys, tokens), f32), pltpu.VMEM((keys, tokens), f32),
        (keys + 2 * BLOCK_PAD, heads * tokens), (keys, heads * tokens), (width, tokens),
        kv.shape, half, turned, turned,
    ] + [(groups, block, model)] * (5 if cross else 3)
    copies = (5, max(groups, parts))
    return stage(sizes, collective_id, lambda s, *refs: attend_back_kernel(s, cross, *refs), operands, outs, scratch, copies)


def fast_device(
    enc_in, dec_in, enc_cot, dec_cot, enc_segments, dec_segments, buckets,
    enc_norm1, enc_query, enc_key, enc_value, enc_proj, enc_rel, enc_norm2, enc_gate, enc_up, enc_down, enc_final,
    dec_norm1, dec_query, dec_key, dec_value, dec_proj, dec_rel, dec_norm2, cross_query, cross_key, cross_value, cross_proj,
    dec_norm3, dec_gate, dec_up, dec_down,
):
    groups, cores, parts = sizes = lax.axis_size(HG), lax.axis_size(CORE), lax.axis_size(SP)
    my_group, my_core, my_part = lax.axis_index(HG), lax.axis_index(CORE), lax.axis_index(SP)
    block, model = enc_in.shape
    share = model // (groups * cores)
    heads = HEADS // groups
    reach = (buckets.shape[1] - 1) // 2
    bf16, f32 = jnp.bfloat16, jnp.float32

    def packed(*weights):
        cut = [w.reshape(w.shape[0], groups, w.shape[1] // groups) for w in weights]
        return jnp.concatenate(cut, axis=2).transpose(1, 0, 2)

    small = jnp.concatenate([enc_norm1, enc_norm2, enc_final, dec_norm1, dec_norm2, dec_norm3, enc_rel, dec_rel])
    small = jnp.broadcast_to(small, (groups, 16, small.shape[0]))
    cols, rows = recut(
        sizes,
        1,
        [
            small,
            packed(enc_key, enc_value, enc_query),
            packed(dec_key, dec_value, dec_query),
            packed(enc_gate, enc_up),
            packed(cross_key, cross_value, cross_query),
            packed(dec_gate, dec_up),
        ],
        [enc_proj, dec_proj, cross_proj, enc_down, dec_down],
    )
    small, enc_kvq, dec_kvq, enc_gu, cross_kvq, dec_gu = cols
    enc_wo, dec_wo, cross_wo, enc_wd, dec_wd = rows
    small = small.reshape(groups * cores, 16, -1)[:, 0].astype(f32)
    g_e1, g_e2, g_ef, g_d1, g_d2, g_d3 = [small[:, i * share : (i + 1) * share].reshape(1, model) for i in range(6)]
    rel_len = enc_rel.shape[0]
    rels = [small[:, 6 * share + i * rel_len : 6 * share + (i + 1) * rel_len].reshape(-1, HEADS) for i in range(2)]

    def table_of(relative, row):
        onehot = (row[:, None] == jnp.arange(relative.shape[0], dtype=jnp.int32)[None, :]).astype(f32)
        full = jnp.dot(onehot, relative, precision=HIGHEST).T
        here = lax.dynamic_slice_in_dim(full, my_group * heads, heads, 0)
        return here, onehot

    def turned(table):
        edge = block - 1
        long = jnp.concatenate(
            [jnp.broadcast_to(table[:, :1], (heads, edge)), table, jnp.broadcast_to(table[:, -1:], (heads, edge))], axis=1
        )
        flipped = long[:, ::-1]
        pad = -flipped.shape[1] % 128
        return jnp.pad(flipped, ((0, 0), (0, pad)))

    enc_table, enc_onehot = table_of(rels[0], buckets[0])
    dec_table, dec_onehot = table_of(rels[1], buckets[1])
    firsts = ((cores * jnp.arange(groups, dtype=jnp.int32) + my_core) * parts + my_part) * block
    qpos = (firsts[:, None] + jnp.arange(block, dtype=jnp.int32)[None, :]).reshape(1, -1)

    def mine(ids):
        return lax.dynamic_index_in_dim(
            lax.dynamic_index_in_dim(ids.reshape(groups, cores, parts, block), my_core, 1, False), my_part, 1, False
        ).reshape(1, -1)

    enc_q_ids, dec_q_ids = mine(enc_segments), mine(dec_segments)
    enc_k_ids, dec_k_ids = enc_segments[:, None], dec_segments[:, None]
    enc_bm = bias_mask(firsts, turned(enc_table), enc_k_ids, enc_q_ids, qpos, block, False)
    dec_bm = bias_mask(firsts, turned(dec_table), dec_k_ids, dec_q_ids, qpos, block, True)
    cross_bm = bias_mask(firsts, None, enc_k_ids, dec_q_ids, qpos, block, False)

    enc_kept, dec_kept = attend(
        sizes,
        2,
        [(enc_in, g_e1, enc_kvq, enc_wo, enc_bm, None), (dec_in, g_d1, dec_kvq, dec_wo, dec_bm, None)],
    )
    ex, dx = enc_kept[0], dec_kept[0]
    tokens, hidden = groups * block, enc_wd.shape[0]
    token_f32, token_bf16, gain_f32 = ((block, model), f32), ((block, model), bf16), ((1, model), f32)
    gu_grad, down_grad = ((model, 2 * hidden), bf16), ((hidden, model), bf16)
    buffer = (groups, block, model)
    enc_out, memory, en2 = stage(
        sizes, 3, feed_forward_kernel, [ex, g_e2, g_ef, enc_gu, enc_wd],
        [token_f32, token_bf16, ((tokens, model), bf16)], [buffer] * 3, (2, groups),
    )
    (cross_kept,) = attend(sizes, 4, [(dx, g_d2, cross_kvq, cross_wo, cross_bm, memory)])
    cx, memory_all = cross_kept[0], cross_kept[6]
    dec_out, grad_cx, dg_d3, dw_dgu, dw_ddown = stage(
        sizes, 5, feed_both_kernel, [cx, dec_cot, g_d3, dec_gu, dec_wd],
        [token_f32, token_f32, gain_f32, gu_grad, down_grad], [buffer] * 6, (4, groups),
    )

    grad_dx, dg_d2, dw_ckvq, dw_co, dmem = attend_back(
        sizes, 6, dx, g_d2, grad_cx, cross_kept, cross_kvq, cross_wo, cross_bm, True
    )
    dec_in_grad, dg_d1, dw_dkvq, dw_do, *dec_tab = attend_back(
        sizes, 7, dec_in, g_d1, grad_dx, dec_kept, dec_kvq, dec_wo, dec_bm, False
    )
    grad_ex, dg_e2, dg_ef, dw_egu, dw_edown = stage(
        sizes, 8, feed_back_kernel, [ex, enc_out, enc_cot, dmem, g_e2, g_ef, en2, enc_gu, enc_wd],
        [token_f32, gain_f32, gain_f32, gu_grad, down_grad], [buffer] * 3, (2, groups),
    )
    enc_in_grad, dg_e1, dw_ekvq, dw_eo, *enc_tab = attend_back(
        sizes, 9, enc_in, g_e1, grad_ex, enc_kept, enc_kvq, enc_wo, enc_bm, False
    )

    def summed_rows(collective_id, col_grads, row_grads):
        mine_cols, mine_rows = give_rows(sizes, collective_id, col_grads, row_grads)
        return [lax.psum(g, SP) for g in mine_cols], [lax.psum(g, SP).astype(f32) for g in mine_rows]

    def unpacked(whole, pieces):
        each = whole.shape[2] // pieces
        whole = whole.astype(f32)
        return [whole[:, :, i * each : (i + 1) * each].transpose(1, 0, 2).reshape(share, groups * each) for i in range(pieces)]

    def fold(tab, onehot):
        strips, edges = tab
        keys = strips.shape[1]
        flipped = strips[:, :, ::-1].transpose(0, 2, 1)
        span = keys + block
        wide = jnp.pad(flipped, ((0, 0), (0, 0), (0, block)))
        flat = wide.reshape(heads, block * span)[:, : block * (span - 1)]
        by_distance = jnp.sum(flat.reshape(heads, block, span - 1), axis=1)
        shift = block - 1 + BLOCK_PAD - reach
        size = 2 * reach + 1
        inner = by_distance[:, shift : shift + size]
        low = jnp.sum(by_distance[:, :shift], axis=1)
        high = jnp.sum(by_distance[:, shift + size :], axis=1)
        sides = jnp.sum(edges, axis=1).reshape(heads, 2)
        inner = inner.at[:, 0].add(low + sides[:, 0]).at[:, -1].add(high + sides[:, 1])
        full = jnp.zeros((HEADS, size), f32)
        full = lax.dynamic_update_slice_in_dim(full, inner, my_group * heads, 0)
        return jnp.dot(onehot.T, full.T, precision=HIGHEST).reshape(-1)

    small_grads = [dg_e1, dg_e2, dg_ef, dg_d1, dg_d2, dg_d3, fold(enc_tab, enc_onehot), fold(dec_tab, dec_onehot)]
    packed_small = jnp.concatenate([v.reshape(groups * cores, 1, -1) for v in small_grads], axis=2)
    packed_small = jnp.broadcast_to(packed_small, (groups * cores, 16, packed_small.shape[2]))
    packed_small = packed_small.reshape(groups * cores * 16, -1).astype(bf16)

    (dgu_rows,), (d_wd,) = summed_rows(10, [dw_dgu], [dw_ddown])
    (cross_rows,), (c_wo,) = summed_rows(11, [dw_ckvq], [dw_co])
    (dkvq_rows, egu_rows), (d_wo, e_wd) = summed_rows(12, [dw_dkvq, dw_egu], [dw_do, dw_edown])
    (ekvq_rows, small_rows), (e_wo,) = summed_rows(13, [dw_ekvq, packed_small], [dw_eo])
    e_wk, e_wv, e_wq = unpacked(ekvq_rows, 3)
    e_wg, e_wu = unpacked(egu_rows, 2)
    d_wk, d_wv, d_wq = unpacked(dkvq_rows, 3)
    c_wk, c_wv, c_wq = unpacked(cross_rows, 3)
    d_wg, d_wu = unpacked(dgu_rows, 2)
    own = jnp.sum(small_rows[:, 0].astype(f32), axis=0)
    s = [own[i * share : (i + 1) * share] for i in range(6)]
    e_rel, d_rel = own[6 * share : 6 * share + rel_len], own[6 * share + rel_len :]
    return (
        enc_out, dec_out, enc_in_grad, dec_in_grad,
        s[0], e_wq, e_wk, e_wv, e_wo, e_rel, s[1], e_wg, e_wu, e_wd, s[2],
        s[3], d_wq, d_wk, d_wv, d_wo, d_rel, s[4], c_wq, c_wk, c_wv, c_wo, s[5], d_wg, d_wu, d_wd,
    )


def general_plan(mesh):
    placed = (
        P(("ctx", "sp"), None),
        P(("ctx", "sp"), None),
        P(("ctx", "sp"), None),
        P(("ctx", "sp"), None),
        P(),
        P(),
        P(),
        P("ctx"),
        P("ctx", None),
        P("ctx", None),
        P("ctx", None),
        P("ctx", None),
        P("ctx"),
        P("ctx"),
        P("ctx", None),
        P("ctx", None),
        P("ctx", None),
        P("ctx"),
        P("ctx"),
        P("ctx", None),
        P("ctx", None),
        P("ctx", None),
        P("ctx", None),
        P("ctx"),
        P("ctx"),
        P("ctx", None),
        P("ctx", None),
        P("ctx", None),
        P("ctx", None),
        P("ctx"),
        P("ctx", None),
        P("ctx", None),
        P("ctx", None),
    )
    return jax.shard_map(
        per_device,
        mesh=mesh,
        in_specs=placed,
        out_specs=(
            P(("ctx", "sp"), None),
            P(("ctx", "sp"), None),
            P(("ctx", "sp"), None),
            P(("ctx", "sp"), None),
            P("ctx"),
            P("ctx", None),
            P("ctx", None),
            P("ctx", None),
            P("ctx", None),
            P("ctx"),
            P("ctx"),
            P("ctx", None),
            P("ctx", None),
            P("ctx", None),
            P("ctx"),
            P("ctx"),
            P("ctx", None),
            P("ctx", None),
            P("ctx", None),
            P("ctx", None),
            P("ctx"),
            P("ctx"),
            P("ctx", None),
            P("ctx", None),
            P("ctx", None),
            P("ctx", None),
            P("ctx"),
            P("ctx", None),
            P("ctx", None),
            P("ctx", None),
        ),
        check_vma=False,
    )


def split_plan(mesh, groups):
    cut = Mesh(np.asarray(mesh.devices).reshape(groups, 2, mesh.shape["sp"]), (HG, CORE, SP))
    tokens, rows, gain, same = P((HG, CORE, SP), None), P((HG, CORE), None), P((HG, CORE)), P()
    attention = (gain, rows, rows, rows, rows, gain)
    feed = (gain, rows, rows, rows)
    weights = attention + feed + (gain,) + attention + (gain, rows, rows, rows, rows) + feed
    return jax.shard_map(
        fast_device,
        mesh=cut,
        in_specs=(tokens,) * 4 + (same,) * 3 + weights,
        out_specs=(tokens,) * 4 + weights,
        check_vma=False,
    )


def solution(mesh):
    groups, odd = divmod(mesh.shape["ctx"], 2)
    if odd or HEADS % groups:
        return general_plan(mesh)
    return split_plan(mesh, groups)
```

```python
import functools
import math

import jax
import jax.numpy as jnp
import numpy as np
from jax import lax
from jax.experimental import pallas as pl
from jax.experimental.pallas import tpu as pltpu
from jax.sharding import Mesh
from jax.sharding import PartitionSpec as P

HEADS = 12
HD = 64


EPSILON = 1e-06
NEGATIVE = -1e30
HIGHEST = lax.Precision.HIGHEST


def rms_norm(values, norm_gain):
    return (
        values * lax.rsqrt(jnp.mean(values * values, axis=-1, keepdims=True) + EPSILON) * norm_gain
    )


def norm_pullback(values, norm_gain, grad_normed):
    _, pullback = jax.vjp(rms_norm, values, norm_gain)
    return pullback(grad_normed)


def gated(gate_val, up_val):
    return jax.nn.gelu(gate_val, approximate=True) * up_val


def project(left, right):
    return jnp.dot(left, right, preferred_element_type=jnp.float32)


def weight_grad(left, right):
    return jnp.einsum("td,te->de", left, right, preferred_element_type=jnp.float32)


def input_grad(grad_out, weight):
    return jnp.einsum("te,de->td", grad_out, weight, preferred_element_type=jnp.float32)


def head_table(relative, table_row, heads_here):
    bucket_count = relative.shape[0] // HEADS
    onehot = (table_row[:, None] == jnp.arange(bucket_count, dtype=jnp.int32)[None, :]).astype(
        jnp.float32
    )
    bias_grid = relative.astype(jnp.float32).reshape(bucket_count, HEADS)
    full_table = jnp.dot(onehot, bias_grid, precision=HIGHEST).T
    first_head = lax.axis_index("sp") * heads_here
    return (lax.dynamic_slice_in_dim(full_table, first_head, heads_here, 0), onehot)


def table_grad(grad_table, onehot, heads_here):
    full_grad = jnp.zeros((HEADS, onehot.shape[0]), jnp.float32)
    full_grad = lax.dynamic_update_slice_in_dim(
        full_grad, grad_table, lax.axis_index("sp") * heads_here, 0
    )
    return jnp.dot(onehot.T, full_grad.T, precision=HIGHEST).reshape(-1)


def bias_block(head_bias, pad_len, offset_q, rows, offset_k, cols):
    head_count, table_len = head_bias.shape
    reach_len = (table_len - 1) // 2
    left_edge = jnp.broadcast_to(head_bias[:, :1], (head_count, pad_len))
    right_edge = jnp.broadcast_to(head_bias[:, -1:], (head_count, pad_len))
    padded = jnp.concatenate([left_edge, head_bias, right_edge], axis=1)
    band_width = rows + cols - 1
    start = offset_k - offset_q - (rows - 1) + reach_len + pad_len
    band = lax.dynamic_slice_in_dim(padded, start, band_width, 1)
    tiled = jnp.broadcast_to(band[:, None, :], (head_count, rows, band_width)).reshape(
        head_count, rows * band_width
    )
    skewed = tiled[:, rows - 1 : rows - 1 + rows * (band_width - 1)].reshape(
        head_count, rows, band_width - 1
    )
    return skewed[:, :, :cols]


def make_frame(query_local, query_ids, key_ids, head_bias, causal):
    local_len = query_local.shape[0]
    heads_here = query_local.shape[1] // HD
    offset_q = lax.axis_index("ctx") * local_len
    ids_q = lax.dynamic_slice_in_dim(query_ids, offset_q, local_len, 0)
    row_ids = offset_q + jnp.arange(local_len, dtype=jnp.int32)
    query_heads = query_local.reshape(local_len, heads_here, HD)
    pad_len = query_ids.shape[0] + key_ids.shape[0]

    def bias_of(entries, offset_k, length):
        return bias_block(entries, pad_len, offset_q, local_len, offset_k, length)

    def scores_of(key_block, offset_k):
        length = key_block.shape[0]
        key_heads = key_block.reshape(length, heads_here, HD)
        raw_scores = jnp.einsum(
            "qhd,khd->hqk", query_heads, key_heads, preferred_element_type=jnp.float32
        )
        col_ids = offset_k + jnp.arange(length, dtype=jnp.int32)
        ids_k = lax.dynamic_slice_in_dim(key_ids, offset_k, length, 0)
        allowed = ids_q[:, None] == ids_k[None, :]
        if causal:
            allowed = allowed & (col_ids[None, :] <= row_ids[:, None])
        if head_bias is not None:
            raw_scores = raw_scores + bias_of(head_bias, offset_k, length)
        return (raw_scores, allowed)

    def touches(offset_k, length):
        first_id = lax.dynamic_slice_in_dim(key_ids, offset_k, 1, 0)[0]
        last_id = lax.dynamic_slice_in_dim(key_ids, offset_k + length - 1, 1, 0)[0]
        touched = (ids_q[0] <= last_id) & (first_id <= ids_q[-1])
        if causal:
            touched = touched & (offset_k <= offset_q + local_len - 1)
        return touched

    return (query_heads, scores_of, touches, bias_of)


def sweep(keys_gathered, local_len, step_fn, carry_state):
    key_all, value_all = keys_gathered
    block_len = local_len * math.gcd(4, lax.axis_size("ctx"))

    def sweep_loop_body(number, running):
        offset_k = number * block_len
        key_block = lax.dynamic_slice_in_dim(key_all, offset_k, block_len, 0)
        value_block = lax.dynamic_slice_in_dim(value_all, offset_k, block_len, 0)
        return step_fn(running, key_block, value_block, offset_k)

    return lax.fori_loop(0, key_all.shape[0] // block_len, sweep_loop_body, carry_state)


def whole_keys(key_local, value_local):
    return (
        lax.all_gather(key_local, "ctx", axis=0, tiled=True),
        lax.all_gather(value_local, "ctx", axis=0, tiled=True),
    )


def attention_forward(query_proj, key_proj, value_proj, query_ids, key_ids, head_bias, causal):
    query_local, key_local, value_local = (
        lax.all_to_all(query_proj, "sp", split_axis=1, concat_axis=0, tiled=True),
        lax.all_to_all(key_proj, "sp", split_axis=1, concat_axis=0, tiled=True),
        lax.all_to_all(value_proj, "sp", split_axis=1, concat_axis=0, tiled=True),
    )
    local_len = query_local.shape[0]
    heads_here = query_local.shape[1] // HD
    query_heads, scores_of, touches, _ = make_frame(
        query_local, query_ids, key_ids, head_bias, causal
    )
    key_block = lax.all_gather(key_local, "ctx", axis=0, tiled=True)
    value_block = lax.all_gather(value_local, "ctx", axis=0, tiled=True)
    offset_k = jnp.int32(0)
    length = key_block.shape[0]
    row_top = jnp.full((heads_here, local_len), NEGATIVE, jnp.float32)
    weighted = jnp.zeros((local_len, heads_here, HD), jnp.float32)
    raw_scores, allowed = scores_of(key_block, offset_k)
    masked = jnp.where(allowed[None], raw_scores, NEGATIVE)
    new_top = jnp.maximum(row_top, jnp.max(masked, axis=-1))
    weights = jnp.where(allowed[None], jnp.exp(masked - new_top[..., None]), 0.0)
    rescale = jnp.exp(row_top - new_top)
    value_heads = value_block.reshape(length, heads_here, HD)
    increment = jnp.einsum(
        "hqk,khd->qhd",
        weights.astype(jnp.bfloat16),
        value_heads,
        preferred_element_type=jnp.float32,
    )
    row_top, row_total, weighted = (
        new_top,
        jnp.sum(weights, axis=-1),
        weighted * rescale.T[:, :, None] + increment,
    )
    mixed_heads = weighted / row_total.T[:, :, None]
    log_total = row_top + jnp.log(row_total)
    mixed_low = mixed_heads.reshape(local_len, heads_here * HD).astype(jnp.bfloat16)
    mixed_tokens = lax.all_to_all(mixed_low, "sp", split_axis=0, concat_axis=1, tiled=True)
    retained = (
        query_local,
        key_local,
        value_local,
        mixed_heads,
        log_total,
        None,
        query_ids,
        key_ids,
        head_bias,
        causal,
    )
    return (mixed_tokens, retained)


def attention_backward(grad_mixed, retained):
    (
        query_local,
        key_local,
        value_local,
        mixed_heads,
        log_total,
        gathered,
        query_ids,
        key_ids,
        head_bias,
        causal,
    ) = retained
    grad_local = lax.all_to_all(grad_mixed, "sp", split_axis=1, concat_axis=0, tiled=True)
    local_len = query_local.shape[0]
    heads_here = query_local.shape[1] // HD
    width = heads_here * HD
    query_heads, scores_of, touches, bias_of = make_frame(
        query_local, query_ids, key_ids, head_bias, causal
    )
    grad_heads = grad_local.reshape(local_len, heads_here, HD)
    row_inner = jnp.einsum("qhd,qhd->hq", grad_heads.astype(jnp.float32), mixed_heads)
    gathered = whole_keys(key_local, value_local)
    table_zero = jnp.zeros(head_bias.shape if head_bias is not None else (1,), jnp.float32)

    def gradients_of(key_block, value_block, offset_k):
        length = key_block.shape[0]
        raw_scores, allowed = scores_of(key_block, offset_k)
        probabilities = jnp.where(allowed[None], jnp.exp(raw_scores - log_total[..., None]), 0.0)
        value_heads = value_block.reshape(length, heads_here, HD)
        grad_probs = jnp.einsum(
            "qhd,khd->hqk", grad_heads, value_heads, preferred_element_type=jnp.float32
        )
        grad_scores = (probabilities * (grad_probs - row_inner[..., None])).astype(jnp.bfloat16)
        return (probabilities, grad_scores)

    def table_part(grad_scores, offset_k, length):
        if head_bias is None:
            return table_zero
        _, pullback = jax.vjp(lambda entries: bias_of(entries, offset_k, length), head_bias)
        return pullback(grad_scores.astype(jnp.float32))[0]

    def key_terms_of(probabilities, grad_scores, length):
        grad_key = jnp.einsum(
            "hqk,qhd->khd", grad_scores, query_heads, preferred_element_type=jnp.float32
        )
        grad_value = jnp.einsum(
            "hqk,qhd->khd",
            probabilities.astype(jnp.bfloat16),
            grad_heads,
            preferred_element_type=jnp.float32,
        )
        return jnp.concatenate(
            [grad_key.reshape(length, width), grad_value.reshape(length, width)], axis=1
        )

    def query_part(grad_scores, key_block):
        length = key_block.shape[0]
        key_heads = key_block.reshape(length, heads_here, HD)
        return jnp.einsum(
            "hqk,khd->qhd", grad_scores, key_heads, preferred_element_type=jnp.float32
        )

    def query_step(running, key_block, value_block, offset_k):
        length = key_block.shape[0]
        grad_query, grad_table = running
        probabilities, grad_scores = gradients_of(key_block, value_block, offset_k)
        return (
            grad_query + query_part(grad_scores, key_block),
            grad_table + table_part(grad_scores, offset_k, length),
        )

    query_zero = jnp.zeros((local_len, heads_here, HD), jnp.float32)
    block_len = local_len * math.gcd(4, lax.axis_size("ctx"))
    grad_query, grad_table = sweep(gathered, local_len, query_step, (query_zero, table_zero))
    key_all, value_all = gathered
    step_len = math.gcd(lax.axis_size("ctx") * local_len, block_len)

    def term_loop_body(number, rows_acc):
        offset_b = number * step_len
        key_block = lax.dynamic_slice_in_dim(key_all, offset_b, step_len, 0)
        value_block = lax.dynamic_slice_in_dim(value_all, offset_b, step_len, 0)
        probabilities, grad_scores = gradients_of(key_block, value_block, offset_b)
        return lax.dynamic_update_slice_in_dim(
            rows_acc, key_terms_of(probabilities, grad_scores, step_len), number * step_len, 0
        )

    own_rows = lax.psum_scatter(
        lax.fori_loop(
            0,
            lax.axis_size("ctx") * local_len // step_len,
            term_loop_body,
            jnp.zeros((lax.axis_size("ctx") * local_len, 2 * width), jnp.float32),
        ),
        "ctx",
        scatter_dimension=0,
        tiled=True,
    )
    grad_q_low = grad_query.reshape(local_len, width).astype(jnp.bfloat16)
    grad_k_low = own_rows[:, :width].astype(jnp.bfloat16)
    grad_v_low = own_rows[:, width:].astype(jnp.bfloat16)
    grad_q_tok, grad_k_tok, grad_v_tok = (
        lax.all_to_all(grad_q_low, "sp", split_axis=0, concat_axis=1, tiled=True),
        lax.all_to_all(grad_k_low, "sp", split_axis=0, concat_axis=1, tiled=True),
        lax.all_to_all(grad_v_low, "sp", split_axis=0, concat_axis=1, tiled=True),
    )
    return (grad_q_tok, grad_k_tok, grad_v_tok, grad_table)


def attention_layer(
    residual,
    source,
    norm_gain,
    w_query,
    w_key,
    w_value,
    w_proj,
    query_ids,
    key_ids,
    head_bias,
    causal,
):
    normed = rms_norm(residual, norm_gain).astype(jnp.bfloat16)
    kv_input = normed if source is None else source
    query_proj = project(normed, w_query).astype(jnp.bfloat16)
    key_proj = project(kv_input, w_key).astype(jnp.bfloat16)
    value_proj = project(kv_input, w_value).astype(jnp.bfloat16)
    mixed_tokens, retained = attention_forward(
        query_proj, key_proj, value_proj, query_ids, key_ids, head_bias, causal
    )
    result = residual + project(mixed_tokens, w_proj)
    return (result, (residual, normed, kv_input, mixed_tokens, retained))


def attention_layer_back(grad_out, saved, norm_gain, w_query, w_key, w_value, w_proj, is_cross):
    residual, normed, kv_input, mixed_tokens, retained = saved
    grad_low = grad_out.astype(jnp.bfloat16)
    grad_proj = weight_grad(mixed_tokens, grad_low)
    grad_mixed = input_grad(grad_low, w_proj).astype(jnp.bfloat16)
    grad_q_tok, grad_k_tok, grad_v_tok, grad_table = attention_backward(grad_mixed, retained)
    grad_wq = weight_grad(normed, grad_q_tok)
    grad_wk = weight_grad(kv_input, grad_k_tok)
    grad_wv = weight_grad(kv_input, grad_v_tok)
    grad_source = input_grad(grad_k_tok, w_key) + input_grad(grad_v_tok, w_value)
    grad_normed = input_grad(grad_q_tok, w_query)
    if not is_cross:
        grad_normed = grad_normed + grad_source
        grad_source = None
    grad_resid, grad_gain = norm_pullback(residual, norm_gain, grad_normed)
    return (
        grad_out + grad_resid,
        grad_source,
        (grad_gain, grad_wq, grad_wk, grad_wv, grad_proj, grad_table),
    )


def feed_layer(residual, norm_gain, w_gate, w_up, w_down):
    normed = rms_norm(residual, norm_gain).astype(jnp.bfloat16)
    gate_val = project(normed, w_gate)
    up_val = project(normed, w_up)
    hidden = gated(gate_val, up_val).astype(jnp.bfloat16)
    return (residual + project(hidden, w_down), (residual, normed, gate_val, up_val, hidden))


def feed_layer_back(grad_out, saved, norm_gain, w_gate, w_up, w_down):
    residual, normed, gate_val, up_val, hidden = saved
    grad_low = grad_out.astype(jnp.bfloat16)
    grad_down = weight_grad(hidden, grad_low)
    grad_hidden = input_grad(grad_low, w_down)
    _, pullback = jax.vjp(gated, gate_val, up_val)
    grad_gate, grad_up = pullback(grad_hidden)
    grad_gate = grad_gate.astype(jnp.bfloat16)
    grad_up = grad_up.astype(jnp.bfloat16)
    grad_wg = weight_grad(normed, grad_gate)
    grad_wu = weight_grad(normed, grad_up)
    grad_normed = input_grad(grad_gate, w_gate) + input_grad(grad_up, w_up)
    grad_resid, grad_gain = norm_pullback(residual, norm_gain, grad_normed)
    return (grad_out + grad_resid, (grad_gain, grad_wg, grad_wu, grad_down))


def per_device(
    enc_in,
    dec_in,
    enc_cot,
    dec_cot,
    enc_segments,
    dec_segments,
    buckets,
    enc_norm1,
    enc_query,
    enc_key,
    enc_value,
    enc_proj,
    enc_rel,
    enc_norm2,
    enc_gate,
    enc_up,
    enc_down,
    enc_final,
    dec_norm1,
    dec_query,
    dec_key,
    dec_value,
    dec_proj,
    dec_rel,
    dec_norm2,
    cross_query,
    cross_key,
    cross_value,
    cross_proj,
    dec_norm3,
    dec_gate,
    dec_up,
    dec_down,
):
    (
        enc_norm1,
        enc_query,
        enc_key,
        enc_value,
        enc_proj,
        enc_rel,
        enc_norm2,
        enc_gate,
        enc_up,
        enc_down,
        enc_final,
        dec_norm1,
        dec_query,
        dec_key,
        dec_value,
        dec_proj,
        dec_rel,
        dec_norm2,
        cross_query,
        cross_key,
        cross_value,
        cross_proj,
        dec_norm3,
        dec_gate,
        dec_up,
        dec_down,
    ) = (
        lax.all_gather(enc_norm1, "ctx", axis=0, tiled=True),
        lax.all_gather(enc_query, "ctx", axis=0, tiled=True),
        lax.all_gather(enc_key, "ctx", axis=0, tiled=True),
        lax.all_gather(enc_value, "ctx", axis=0, tiled=True),
        lax.all_gather(enc_proj, "ctx", axis=0, tiled=True),
        lax.all_gather(enc_rel, "ctx", axis=0, tiled=True),
        lax.all_gather(enc_norm2, "ctx", axis=0, tiled=True),
        lax.all_gather(enc_gate, "ctx", axis=0, tiled=True),
        lax.all_gather(enc_up, "ctx", axis=0, tiled=True),
        lax.all_gather(enc_down, "ctx", axis=0, tiled=True),
        lax.all_gather(enc_final, "ctx", axis=0, tiled=True),
        lax.all_gather(dec_norm1, "ctx", axis=0, tiled=True),
        lax.all_gather(dec_query, "ctx", axis=0, tiled=True),
        lax.all_gather(dec_key, "ctx", axis=0, tiled=True),
        lax.all_gather(dec_value, "ctx", axis=0, tiled=True),
        lax.all_gather(dec_proj, "ctx", axis=0, tiled=True),
        lax.all_gather(dec_rel, "ctx", axis=0, tiled=True),
        lax.all_gather(dec_norm2, "ctx", axis=0, tiled=True),
        lax.all_gather(cross_query, "ctx", axis=0, tiled=True),
        lax.all_gather(cross_key, "ctx", axis=0, tiled=True),
        lax.all_gather(cross_value, "ctx", axis=0, tiled=True),
        lax.all_gather(cross_proj, "ctx", axis=0, tiled=True),
        lax.all_gather(dec_norm3, "ctx", axis=0, tiled=True),
        lax.all_gather(dec_gate, "ctx", axis=0, tiled=True),
        lax.all_gather(dec_up, "ctx", axis=0, tiled=True),
        lax.all_gather(dec_down, "ctx", axis=0, tiled=True),
    )
    enc_norm1 = enc_norm1.astype(jnp.float32)
    enc_norm2 = enc_norm2.astype(jnp.float32)
    enc_final = enc_final.astype(jnp.float32)
    dec_norm1 = dec_norm1.astype(jnp.float32)
    dec_norm2 = dec_norm2.astype(jnp.float32)
    dec_norm3 = dec_norm3.astype(jnp.float32)
    heads_here = HEADS // lax.axis_size("sp")
    enc_table, enc_onehot = head_table(enc_rel, buckets[0], heads_here)
    dec_table, dec_onehot = head_table(dec_rel, buckets[1], heads_here)
    enc_x = enc_in.astype(jnp.float32)
    enc_mid, enc_saved_a = attention_layer(
        enc_x,
        None,
        enc_norm1,
        enc_query,
        enc_key,
        enc_value,
        enc_proj,
        enc_segments,
        enc_segments,
        enc_table,
        False,
    )
    enc_result, enc_saved_f = feed_layer(enc_mid, enc_norm2, enc_gate, enc_up, enc_down)
    memory = rms_norm(enc_result, enc_final).astype(jnp.bfloat16)
    dec_x = dec_in.astype(jnp.float32)
    dec_mid, dec_saved_a = attention_layer(
        dec_x,
        None,
        dec_norm1,
        dec_query,
        dec_key,
        dec_value,
        dec_proj,
        dec_segments,
        dec_segments,
        dec_table,
        True,
    )
    dec_cross, dec_saved_c = attention_layer(
        dec_mid,
        memory,
        dec_norm2,
        cross_query,
        cross_key,
        cross_value,
        cross_proj,
        dec_segments,
        enc_segments,
        None,
        False,
    )
    dec_result, dec_saved_f = feed_layer(dec_cross, dec_norm3, dec_gate, dec_up, dec_down)
    grad_dec, dec_ff_grads = feed_layer_back(
        dec_cot.astype(jnp.float32), dec_saved_f, dec_norm3, dec_gate, dec_up, dec_down
    )
    grad_dec, grad_memory, cross_grads = attention_layer_back(
        grad_dec, dec_saved_c, dec_norm2, cross_query, cross_key, cross_value, cross_proj, True
    )
    grad_dec, _, dec_self_grads = attention_layer_back(
        grad_dec, dec_saved_a, dec_norm1, dec_query, dec_key, dec_value, dec_proj, False
    )
    grad_enc_out, grad_final = norm_pullback(enc_result, enc_final, grad_memory)
    grad_enc, enc_ff_grads = feed_layer_back(
        enc_cot.astype(jnp.float32) + grad_enc_out,
        enc_saved_f,
        enc_norm2,
        enc_gate,
        enc_up,
        enc_down,
    )
    grad_enc, _, enc_self_grads = attention_layer_back(
        grad_enc, enc_saved_a, enc_norm1, enc_query, enc_key, enc_value, enc_proj, False
    )
    e_gain1, e_wq, e_wk, e_wv, e_wo, e_table = enc_self_grads
    e_gain2, e_wg, e_wu, e_wd = enc_ff_grads
    d_gain1, d_wq, d_wk, d_wv, d_wo, d_table = dec_self_grads
    c_gain, c_wq, c_wk, c_wv, c_wo, _ = cross_grads
    d_gain3, d_wg, d_wu, d_wd = dec_ff_grads
    e_rel = table_grad(e_table, enc_onehot, heads_here)
    d_rel = table_grad(d_table, dec_onehot, heads_here)
    shards = (
        lax.psum_scatter(e_gain1, "ctx", scatter_dimension=0, tiled=True),
        lax.psum_scatter(e_wq, "ctx", scatter_dimension=0, tiled=True),
        lax.psum_scatter(e_wk, "ctx", scatter_dimension=0, tiled=True),
        lax.psum_scatter(e_wv, "ctx", scatter_dimension=0, tiled=True),
        lax.psum_scatter(e_wo, "ctx", scatter_dimension=0, tiled=True),
        lax.psum_scatter(e_rel, "ctx", scatter_dimension=0, tiled=True),
        lax.psum_scatter(e_gain2, "ctx", scatter_dimension=0, tiled=True),
        lax.psum_scatter(e_wg, "ctx", scatter_dimension=0, tiled=True),
        lax.psum_scatter(e_wu, "ctx", scatter_dimension=0, tiled=True),
        lax.psum_scatter(e_wd, "ctx", scatter_dimension=0, tiled=True),
        lax.psum_scatter(grad_final, "ctx", scatter_dimension=0, tiled=True),
        lax.psum_scatter(d_gain1, "ctx", scatter_dimension=0, tiled=True),
        lax.psum_scatter(d_wq, "ctx", scatter_dimension=0, tiled=True),
        lax.psum_scatter(d_wk, "ctx", scatter_dimension=0, tiled=True),
        lax.psum_scatter(d_wv, "ctx", scatter_dimension=0, tiled=True),
        lax.psum_scatter(d_wo, "ctx", scatter_dimension=0, tiled=True),
        lax.psum_scatter(d_rel, "ctx", scatter_dimension=0, tiled=True),
        lax.psum_scatter(c_gain, "ctx", scatter_dimension=0, tiled=True),
        lax.psum_scatter(c_wq, "ctx", scatter_dimension=0, tiled=True),
        lax.psum_scatter(c_wk, "ctx", scatter_dimension=0, tiled=True),
        lax.psum_scatter(c_wv, "ctx", scatter_dimension=0, tiled=True),
        lax.psum_scatter(c_wo, "ctx", scatter_dimension=0, tiled=True),
        lax.psum_scatter(d_gain3, "ctx", scatter_dimension=0, tiled=True),
        lax.psum_scatter(d_wg, "ctx", scatter_dimension=0, tiled=True),
        lax.psum_scatter(d_wu, "ctx", scatter_dimension=0, tiled=True),
        lax.psum_scatter(d_wd, "ctx", scatter_dimension=0, tiled=True),
    )
    (
        s_gain1,
        s_wq,
        s_wk,
        s_wv,
        s_wo,
        s_rel,
        s_gain2,
        s_wg,
        s_wu,
        s_wd,
        s_final,
        t_gain1,
        t_wq,
        t_wk,
        t_wv,
        t_wo,
        t_rel,
        t_gain2,
        t_cq,
        t_ck,
        t_cv,
        t_co,
        t_gain3,
        t_wg,
        t_wu,
        t_wd,
    ) = shards
    reduced = (
        lax.psum(s_gain1.astype(jnp.bfloat16), "sp").astype(jnp.float32),
        lax.psum(s_wq.astype(jnp.bfloat16), "sp").astype(jnp.float32),
        lax.psum(s_wk.astype(jnp.bfloat16), "sp").astype(jnp.float32),
        lax.psum(s_wv.astype(jnp.bfloat16), "sp").astype(jnp.float32),
        lax.psum(s_wo.astype(jnp.bfloat16), "sp").astype(jnp.float32),
        lax.psum(s_rel.astype(jnp.bfloat16), "sp").astype(jnp.float32),
        lax.psum(s_gain2.astype(jnp.bfloat16), "sp").astype(jnp.float32),
        lax.psum(s_wg.astype(jnp.bfloat16), "sp").astype(jnp.float32),
        lax.psum(s_wu.astype(jnp.bfloat16), "sp").astype(jnp.float32),
        lax.psum(s_wd.astype(jnp.bfloat16), "sp").astype(jnp.float32),
        lax.psum(s_final.astype(jnp.bfloat16), "sp").astype(jnp.float32),
        lax.psum(t_gain1.astype(jnp.bfloat16), "sp").astype(jnp.float32),
        lax.psum(t_wq.astype(jnp.bfloat16), "sp").astype(jnp.float32),
        lax.psum(t_wk.astype(jnp.bfloat16), "sp").astype(jnp.float32),
        lax.psum(t_wv.astype(jnp.bfloat16), "sp").astype(jnp.float32),
        lax.psum(t_wo.astype(jnp.bfloat16), "sp").astype(jnp.float32),
        lax.psum(t_rel.astype(jnp.bfloat16), "sp").astype(jnp.float32),
        lax.psum(t_gain2.astype(jnp.bfloat16), "sp").astype(jnp.float32),
        lax.psum(t_cq.astype(jnp.bfloat16), "sp").astype(jnp.float32),
        lax.psum(t_ck.astype(jnp.bfloat16), "sp").astype(jnp.float32),
        lax.psum(t_cv.astype(jnp.bfloat16), "sp").astype(jnp.float32),
        lax.psum(t_co.astype(jnp.bfloat16), "sp").astype(jnp.float32),
        lax.psum(t_gain3.astype(jnp.bfloat16), "sp").astype(jnp.float32),
        lax.psum(t_wg.astype(jnp.bfloat16), "sp").astype(jnp.float32),
        lax.psum(t_wu.astype(jnp.bfloat16), "sp").astype(jnp.float32),
        lax.psum(t_wd.astype(jnp.bfloat16), "sp").astype(jnp.float32),
    )
    return (enc_result, dec_result, grad_enc, grad_dec) + tuple(reduced)


HG, CORE, SP = "hg", "core", "sp"
BLOCK_PAD = 128
VMEM_BYTES = 60 << 20


def nt(left, right):
    return lax.dot_general(left, right, (((1,), (1,)), ((), ())), preferred_element_type=jnp.float32)


def tn(left, right):
    return lax.dot_general(left, right, (((0,), (0,)), ((), ())), preferred_element_type=jnp.float32)


def nn(left, right):
    return jnp.dot(left, right, preferred_element_type=jnp.float32)


def low(value):
    return value.astype(jnp.bfloat16)


def identity(size):
    rows = lax.broadcasted_iota(jnp.int32, (size, size), 0)
    cols = lax.broadcasted_iota(jnp.int32, (size, size), 1)
    return low(jnp.where(rows == cols, 1.0, 0.0))


def only_lanes(array, first, count):
    lanes = lax.broadcasted_iota(jnp.int32, array.shape, 1)
    return jnp.where((lanes >= first) & (lanes < first + count), array, jnp.zeros_like(array))


def gelu_and_slope(v):
    scale, cubic = math.sqrt(2.0 / math.pi), 0.044715
    t = jnp.tanh(scale * (v + cubic * v * v * v))
    return 0.5 * v * (1.0 + t), 0.5 * (1.0 + t) + 0.5 * v * (1.0 - t * t) * scale * (1.0 + 3.0 * cubic * v * v)


def norm_back(x, g, dn):
    r = lax.rsqrt(jnp.mean(x * x, axis=-1, keepdims=True) + EPSILON)
    w = dn * g
    dx = r * w - x * (r * r * r) * jnp.mean(w * x, axis=-1, keepdims=True)
    return dx, jnp.sum(dn * x * r, axis=0, keepdims=True)


def send(src, dst, send_sem, recv_sem, to):
    copy = pltpu.make_async_remote_copy(
        src_ref=src, dst_ref=dst, send_sem=send_sem, recv_sem=recv_sem, device_id=to, device_id_type=pl.DeviceIdType.MESH
    )
    copy.start()
    return copy


def arrived(dst, send_sem, recv_sem, to):
    pltpu.make_async_remote_copy(
        src_ref=dst, dst_ref=dst, send_sem=send_sem, recv_sem=recv_sem, device_id=to, device_id_type=pl.DeviceIdType.MESH
    ).wait_recv()


class Place:
    def __init__(self, groups, cores, parts):
        self.groups, self.cores, self.parts = groups, cores, parts
        self.group, self.core, self.part = lax.axis_index(HG), lax.axis_index(CORE), lax.axis_index(SP)

    def ahead(self, step):
        return lax.rem(self.group + step, self.groups)

    def behind(self, step):
        return lax.rem(self.group + self.groups - step, self.groups)

    def chip(self, group):
        return (group, self.core, self.part)

    def sibling(self):
        return (self.group, 1 - self.core, self.part)

    def plane(self, step):
        return lax.rem(self.part + step, self.parts)

    def plane_behind(self, step):
        return lax.rem(self.part + self.parts - step, self.parts)

    def at_plane(self, part):
        return (self.group, self.core, part)

    def first_token(self, number, block):
        return pl.multiple_of(((self.cores * number + self.core) * self.parts + self.part) * block, block)

    def greet(self, planes=False):
        barrier = pltpu.get_barrier_semaphore()
        partners = [self.chip(self.ahead(step)) for step in range(1, self.groups)] + [self.sibling()]
        if planes:
            partners += [self.at_plane(self.plane(step)) for step in range(1, self.parts)]
        for partner in partners:
            pl.semaphore_signal(barrier, inc=1, device_id=partner, device_id_type=pl.DeviceIdType.MESH)
        pl.semaphore_wait(barrier, len(partners))


def spread_start(place, buf, sent, got):
    mine = buf.at[place.group]
    return [
        send(mine, mine, sent.at[step], got.at[step], place.chip(place.ahead(step))) for step in range(1, place.groups)
    ]


def spread_wait(place, buf, sent, got):
    for step in range(1, place.groups):
        source = place.behind(step)
        arrived(buf.at[source], sent.at[step], got.at[step], place.chip(source))


def collect_start(place, partial, out_buf, in_buf, sent, got):
    out_buf[...] = low(partial).reshape(out_buf.shape)
    pending = []
    for step in range(1, place.groups):
        to = place.ahead(step)
        pending.append(send(out_buf.at[to], in_buf.at[place.group], sent.at[step], got.at[step], place.chip(to)))
    return pending


def collect_wait(place, out_buf, in_buf, sent, got):
    total = out_buf[place.group].astype(jnp.float32)
    for step in range(1, place.groups):
        source = place.behind(step)
        arrived(in_buf.at[source], sent.at[step], got.at[step], place.chip(source))
        total = total + in_buf[source].astype(jnp.float32)
    return total


def all_rows(buf):
    return buf[...].reshape(buf.shape[0] * buf.shape[1], buf.shape[2])


DMA = pltpu.SemaphoreType.DMA
IN_VMEM = pl.BlockSpec(memory_space=pltpu.VMEM)
ANYWHERE = pl.BlockSpec(memory_space=pl.ANY)


class Recut:
    def __init__(self, sizes, col_packs, row_packs):
        groups, cores, _ = sizes
        self.cols, self.rows = len(col_packs), len(row_packs)
        self.operands = list(col_packs) + list(row_packs)
        self.in_specs = [ANYWHERE] * len(self.operands)
        self.outs = [((groups, cores) + w.shape[1:], w.dtype) for w in col_packs]
        self.outs += [((cores,) + w.shape, w.dtype) for w in row_packs]
        self.out_specs = [ANYWHERE] * len(self.outs)
        cols = (self.cols, groups)
        self.scratch = [DMA(cols)] * 4 + [DMA((self.rows,))] * 2 + [DMA((self.cols + self.rows,))]

    def bind(self, ins, outs, scratch):
        self.col_refs, self.row_refs = ins[: self.cols], ins[self.cols :]
        self.col_outs, self.row_outs = outs[: self.cols], outs[self.cols :]
        self.sems = scratch
        self.pending, self.copies = [], []

    def begin(self, place):
        sent, got, relay_sent, relay_got, pair_sent, pair_got, local = self.sems
        group, core = place.group, place.core
        for index, (ref, out) in enumerate(zip(self.col_refs, self.col_outs)):
            slot = out.at[group, core]
            for step in range(1, place.groups):
                to = place.ahead(step)
                self.pending.append(send(ref.at[to], slot, sent.at[index, step], got.at[index, step], place.chip(to)))
            self.pending.append(send(ref.at[group], slot, relay_sent.at[index, 0], relay_got.at[index, 0], place.sibling()))
            self.copies.append(pltpu.make_async_copy(ref.at[group], slot, local.at[index]))
        for index, (ref, out) in enumerate(zip(self.row_refs, self.row_outs)):
            slot = out.at[core]
            self.pending.append(send(ref, slot, pair_sent.at[index], pair_got.at[index], place.sibling()))
            self.copies.append(pltpu.make_async_copy(ref, slot, local.at[self.cols + index]))
        for copy in self.copies:
            copy.start()

    def middle(self, place):
        sent, got, relay_sent, relay_got = self.sems[:4]
        for index, out in enumerate(self.col_outs):
            for step in range(1, place.groups):
                source = place.behind(step)
                slot = out.at[source, place.core]
                arrived(slot, sent.at[index, step], got.at[index, step], place.chip(source))
                self.pending.append(
                    send(slot, slot, relay_sent.at[index, step], relay_got.at[index, step], place.sibling())
                )

    def end(self, place):
        _, _, relay_sent, relay_got, pair_sent, pair_got, _ = self.sems
        for index, out in enumerate(self.col_outs):
            for step in range(place.groups):
                slot = out.at[place.behind(step), 1 - place.core]
                arrived(slot, relay_sent.at[index, step], relay_got.at[index, step], place.sibling())
        for index, out in enumerate(self.row_outs):
            arrived(out.at[1 - place.core], pair_sent.at[index], pair_got.at[index], place.sibling())
        for copy in self.copies:
            copy.wait()
        for copy in self.pending:
            copy.wait_send()

    def result(self, got):
        cols = [w.reshape(w.shape[0] * w.shape[1] * w.shape[2], w.shape[3]) for w in got[: self.cols]]
        return cols, [w.reshape(w.shape[0] * w.shape[1], w.shape[2]) for w in got[self.cols :]]


class GiveRows:
    def __init__(self, sizes, col_grads, row_grads):
        groups, cores, _ = sizes
        self.cols, self.rows = len(col_grads), len(row_grads)
        col_in = [w.reshape(groups, cores, w.shape[0] // (groups * cores), w.shape[1]) for w in col_grads]
        row_in = [w.reshape(cores, w.shape[0] // cores, w.shape[1]) for w in row_grads]
        self.operands = col_in + row_in
        self.in_specs = [IN_VMEM] * len(self.operands)
        own = [(groups,) + w.shape[2:] for w in col_in] + [(1,) + w.shape[1:] for w in row_in]
        self.outs = [(shape, jnp.bfloat16) for shape in own]
        self.out_specs = [IN_VMEM] * len(self.outs)
        self.scratch = [pltpu.VMEM(shape, jnp.bfloat16) for shape in own + own[: self.cols]]
        self.scratch += [DMA((self.cols, groups))] * 4 + [DMA((self.rows,))] * 2

    def bind(self, ins, outs, scratch):
        self.col_refs, self.row_refs = ins[: self.cols], ins[self.cols :]
        self.col_outs, self.row_outs = outs[: self.cols], outs[self.cols :]
        self.col_sibs, scratch = scratch[: self.cols], scratch[self.cols :]
        self.row_sibs, scratch = scratch[: self.rows], scratch[self.rows :]
        self.col_sums, self.sems = scratch[: self.cols], scratch[self.cols :]
        self.pending = []

    def begin(self, place):
        _, _, pair_sent, pair_got, row_sent, row_got = self.sems
        other = 1 - place.core
        for index, (ref, sib) in enumerate(zip(self.col_refs, self.col_sibs)):
            for step in range(place.groups):
                to = place.ahead(step)
                self.pending.append(
                    send(
                        ref.at[to, other], sib.at[to],
                        pair_sent.at[index, step], pair_got.at[index, step], place.sibling(),
                    )
                )
        for index, (ref, sib) in enumerate(zip(self.row_refs, self.row_sibs)):
            self.pending.append(send(ref.at[other], sib.at[0], row_sent.at[index], row_got.at[index], place.sibling()))

    def middle(self, place):
        sent, got, pair_sent, pair_got, row_sent, row_got = self.sems
        core = place.core
        for index, (ref, sib) in enumerate(zip(self.col_refs, self.col_sibs)):
            out, sums = self.col_outs[index], self.col_sums[index]
            for step in list(range(1, place.groups)) + [0]:
                to = place.ahead(step)
                arrived(sib.at[to], pair_sent.at[index, step], pair_got.at[index, step], place.sibling())
                both = low(ref[to, core].astype(jnp.float32) + sib[to].astype(jnp.float32))
                if step:
                    sums[to] = both
                    self.pending.append(
                        send(sums.at[to], out.at[place.group], sent.at[index, step], got.at[index, step], place.chip(to))
                    )
                else:
                    out[place.group] = both
        for index, (ref, sib) in enumerate(zip(self.row_refs, self.row_sibs)):
            arrived(sib.at[0], row_sent.at[index], row_got.at[index], place.sibling())
            self.row_outs[index][0] = low(ref[core].astype(jnp.float32) + sib[0].astype(jnp.float32))

    def end(self, place):
        sent, got = self.sems[:2]
        for index, out in enumerate(self.col_outs):
            for step in range(1, place.groups):
                source = place.behind(step)
                arrived(out.at[source], sent.at[index, step], got.at[index, step], place.chip(source))
        for copy in self.pending:
            copy.wait_send()

    def result(self, got):
        return list(got)


class FoldPlanes:
    def __init__(self, arrays):
        self.operands = list(arrays)
        self.in_specs = [IN_VMEM] * len(arrays)
        self.outs = [(w.shape, jnp.bfloat16) for w in arrays]
        self.out_specs = [IN_VMEM] * len(arrays)
        self.pieces = [(index, piece) for index, w in enumerate(arrays) for piece in range(w.shape[0])]
        self.scratch = [pltpu.VMEM(w.shape, jnp.bfloat16) for _ in range(3) for w in arrays] + [DMA((len(self.pieces),))] * 6

    def bind(self, ins, outs, scratch):
        count = len(self.outs)
        self.ins, self.totals = ins, outs
        self.inner, self.sums, self.across = (scratch[i * count : (i + 1) * count] for i in range(3))
        self.sems = scratch[3 * count :]

    def copy(self, hop, number, src, dst, to):
        return pltpu.make_async_remote_copy(
            src_ref=src, dst_ref=dst, send_sem=self.sems[2 * hop].at[number], recv_sem=self.sems[2 * hop + 1].at[number],
            device_id=to, device_id_type=pl.DeviceIdType.MESH,
        )

    def hops(self, place, number):
        index, piece = self.pieces[number]
        part = place.part
        inward, across, outward = (place.at_plane(p) for p in (1 + part // 3, 3 - part, 3 * (part - 1)))
        ref, inner, sums = self.ins[index].at[piece], self.inner[index].at[piece], self.sums[index].at[piece]
        other, total = self.across[index].at[piece], self.totals[index].at[piece]
        return (ref, inner, inward), (sums, other, across), (total, total, outward)

    def roles(self, place):
        middle = (place.part == 1) | (place.part == 2)
        return pl.when(middle), pl.when(jnp.logical_not(middle))

    def start(self, place, numbers):
        @self.roles(place)[1]
        def _():
            for number in numbers:
                self.copy(0, number, *self.hops(place, number)[0]).start()

    def add_inner(self, place, number):
        inward, across, _ = self.hops(place, number)
        self.copy(0, number, *inward).wait_recv()
        across[0][...] = low(inward[0][...].astype(jnp.float32) + inward[1][...].astype(jnp.float32))
        self.copy(1, number, *across).start()

    def add_across(self, place, number):
        _, across, outward = self.hops(place, number)
        self.copy(1, number, *across).wait_recv()
        outward[0][...] = low(across[0][...].astype(jnp.float32) + across[1][...].astype(jnp.float32))
        self.copy(2, number, *outward).start()

    def serve(self, place, inner, across):
        @self.roles(place)[0]
        def _():
            inners, others = list(inner), list(across)
            while inners or others:
                if inners:
                    self.add_inner(place, inners.pop(0))
                if others and (not inners or len(inners) < len(others) + 2):
                    self.add_across(place, others.pop(0))

    def end(self, place):
        in_middle, at_end = self.roles(place)

        @at_end
        def _():
            for number in range(len(self.pieces)):
                inward, _, outward = self.hops(place, number)
                self.copy(0, number, *inward).wait_send()
                self.copy(2, number, *outward).wait_recv()

        @in_middle
        def _():
            for number in range(len(self.pieces)):
                _, across, outward = self.hops(place, number)
                self.copy(1, number, *across).wait_send()
                self.copy(2, number, *outward).wait_send()

    def result(self, got):
        return list(got)


def finish_kernel(sizes, give, fold, before, *refs):
    refs = list(refs)

    def take(count):
        taken, refs[:] = refs[:count], refs[count:]
        return taken

    give_ins, ready = take(len(give.operands)), take(before)
    totals = take(len(fold.outs))
    given = take(len(give.outs))
    give.bind(give_ins, given, take(len(give.scratch)))
    fold.bind(ready + given, totals, take(len(fold.scratch)))
    place = Place(*sizes)
    place.greet(planes=True)
    early = [n for n, (index, _) in enumerate(fold.pieces) if index < before]
    last = [n for n, (index, _) in enumerate(fold.pieces) if index >= before]
    first = early[: len(early) // 2]
    give.begin(place)
    fold.start(place, early)
    give.middle(place)
    fold.serve(place, first, [])
    give.end(place)
    fold.start(place, last)
    fold.serve(place, early[len(first) :] + last, early + last)
    fold.end(place)


def finish(sizes, collective_id, give, arrays):
    fold = FoldPlanes(list(arrays) + [jax.ShapeDtypeStruct(shape, dtype) for shape, dtype in give.outs])
    count = len(arrays)
    got = pl.pallas_call(
        functools.partial(finish_kernel, sizes, give, fold, count),
        out_shape=tuple(jax.ShapeDtypeStruct(shape, dtype) for shape, dtype in fold.outs),
        in_specs=[IN_VMEM] * (len(give.operands) + count),
        out_specs=(IN_VMEM,) * len(fold.outs),
        scratch_shapes=[pltpu.VMEM(shape, dtype) for shape, dtype in give.outs] + give.scratch + fold.scratch,
        compiler_params=pltpu.CompilerParams(collective_id=collective_id, has_side_effects=True, vmem_limit_bytes=VMEM_BYTES),
        cost_estimate=pl.CostEstimate(flops=20_000_000_000, bytes_accessed=10_000_000, transcendentals=0),
    )(*give.operands, *arrays)
    return list(got[count:]), list(got[:count])


def stage(sizes, collective_id, kernel, operands, outs, scratch, copies, job=None):
    jobs = [] if job is None else [job]
    allocated = [pltpu.VMEM(s, jnp.bfloat16) if isinstance(s, tuple) else s for s in scratch]
    if copies is not None:
        allocated += [DMA(copies), DMA(copies)]
    counts = (len(operands), len(outs), len(allocated))
    job_ins, job_outs = [len(j.operands) for j in jobs], [len(j.outs) for j in jobs]

    def body(*refs):
        refs = list(refs)

        def take(count):
            taken, refs[:] = refs[:count], refs[count:]
            return taken

        own_ins, their_ins = take(counts[0]), [take(n) for n in job_ins]
        own_outs, their_outs = take(counts[1]), [take(n) for n in job_outs]
        own_scratch, their_scratch = take(counts[2]), [take(len(j.scratch)) for j in jobs]
        for j, i, o, s in zip(jobs, their_ins, their_outs, their_scratch):
            j.bind(i, o, s)
        place = Place(*sizes)

        def run(step):
            for j in jobs:
                getattr(j, step)(place)

        kernel(place, run, *own_ins, *own_outs, *own_scratch)

    all_outs = list(outs) + [o for j in jobs for o in j.outs]
    got = pl.pallas_call(
        body,
        out_shape=tuple(jax.ShapeDtypeStruct(shape, dtype) for shape, dtype in all_outs),
        in_specs=[IN_VMEM] * counts[0] + [s for j in jobs for s in j.in_specs],
        out_specs=tuple([IN_VMEM] * counts[1] + [s for j in jobs for s in j.out_specs]),
        scratch_shapes=allocated + [s for j in jobs for s in j.scratch],
        compiler_params=pltpu.CompilerParams(collective_id=collective_id, has_side_effects=True, vmem_limit_bytes=VMEM_BYTES),
        cost_estimate=pl.CostEstimate(flops=20_000_000_000, bytes_accessed=10_000_000, transcendentals=0),
    )(*operands, *[w for j in jobs for w in j.operands])
    return got[: counts[1]], (None if job is None else job.result(got[counts[1] :]))


def job_alone_kernel(place, run):
    place.greet()
    run("begin")
    run("middle")
    run("end")


def job_alone(sizes, collective_id, job):
    return stage(sizes, collective_id, job_alone_kernel, [], [], [], None, job)[1]


def feed_forward_kernel(gain_at, final_at, place, run, x_ref, gains_ref, gu_ref, down_ref, y_ref, last_ref, n_ref, n_buf, p_buf, r_buf, sent, got):
    place.greet()
    x = x_ref[...]
    n_buf[place.group] = low(rms_norm(x, gains_ref[gain_at]))
    pending = spread_start(place, n_buf, sent.at[0], got.at[0])
    run("begin")
    spread_wait(place, n_buf, sent.at[0], got.at[0])
    n = all_rows(n_buf)
    hidden = down_ref.shape[0]
    gu = nn(n, gu_ref[...])
    h = low(gelu_and_slope(gu[:, :hidden])[0] * gu[:, hidden:])
    pending += collect_start(place, nn(h, down_ref[...]), p_buf, r_buf, sent.at[1], got.at[1])
    n_ref[...] = n
    run("middle")
    y = x + collect_wait(place, p_buf, r_buf, sent.at[1], got.at[1])
    y_ref[...] = y
    last_ref[...] = low(rms_norm(y, gains_ref[final_at]))
    run("end")
    for copy in pending:
        copy.wait_send()


def feed_back_part(n, dyb, gu_ref, down_ref):
    hidden = down_ref.shape[0]
    gu = nn(n, gu_ref[...])
    g, u = gu[:, :hidden], gu[:, hidden:]
    act, slope = gelu_and_slope(g)
    dh = nt(dyb, down_ref[...])
    return low(act * u), jnp.concatenate([low(dh * u * slope), low(dh * act)], axis=1)


def feed_both_kernel(
    gain_at, place, run, x_ref, cot_ref, gains_ref, gu_ref, down_ref,
    y_ref, dx_ref, dgain_ref, dgu_ref, ddown_ref,
    n_buf, d_buf, py_buf, ry_buf, pn_buf, rn_buf, sent, got,
):
    place.greet()
    x = x_ref[...]
    d_buf[place.group] = cot_ref[...]
    pending = spread_start(place, d_buf, sent.at[1], got.at[1])
    n_buf[place.group] = low(rms_norm(x, gains_ref[gain_at]))
    pending += spread_start(place, n_buf, sent.at[0], got.at[0])
    run("begin")
    spread_wait(place, n_buf, sent.at[0], got.at[0])
    spread_wait(place, d_buf, sent.at[1], got.at[1])
    n, dyb = all_rows(n_buf), all_rows(d_buf)
    h, dgu = feed_back_part(n, dyb, gu_ref, down_ref)
    pending += collect_start(place, nt(dgu, gu_ref[...]), pn_buf, rn_buf, sent.at[2], got.at[2])
    pending += collect_start(place, nn(h, down_ref[...]), py_buf, ry_buf, sent.at[3], got.at[3])
    dgu_ref[...] = low(tn(n, dgu))
    ddown_ref[...] = low(tn(h, dyb))
    run("middle")
    dn = collect_wait(place, pn_buf, rn_buf, sent.at[2], got.at[2])
    back, dgain = norm_back(x, gains_ref[gain_at], dn)
    dx_ref[...] = cot_ref[...].astype(jnp.float32) + back
    dgain_ref[...] = dgain
    y_ref[...] = x + collect_wait(place, py_buf, ry_buf, sent.at[3], got.at[3])
    run("end")
    for copy in pending:
        copy.wait_send()


def feed_back_kernel(
    gain_at, final_at, place, run, x_ref, y_ref, cot_ref, dlast_ref, gains_ref, n_ref, gu_ref, down_ref,
    dx_ref, dgain_ref, dfinal_ref, dgu_ref, ddown_ref,
    d_buf, pn_buf, rn_buf, sent, got,
):
    place.greet()
    back, dfinal = norm_back(y_ref[...], gains_ref[final_at], dlast_ref[...])
    dfinal_ref[...] = dfinal
    dy = cot_ref[...].astype(jnp.float32) + back
    d_buf[place.group] = low(dy)
    pending = spread_start(place, d_buf, sent.at[0], got.at[0])
    run("begin")
    spread_wait(place, d_buf, sent.at[0], got.at[0])
    n, dyb = n_ref[...], all_rows(d_buf)
    h, dgu = feed_back_part(n, dyb, gu_ref, down_ref)
    pending += collect_start(place, nt(dgu, gu_ref[...]), pn_buf, rn_buf, sent.at[1], got.at[1])
    dgu_ref[...] = low(tn(n, dgu))
    ddown_ref[...] = low(tn(h, dyb))
    run("middle")
    dn = collect_wait(place, pn_buf, rn_buf, sent.at[1], got.at[1])
    back, dgain = norm_back(x_ref[...], gains_ref[gain_at], dn)
    dx_ref[...] = dy + back
    dgain_ref[...] = dgain
    run("end")
    for copy in pending:
        copy.wait_send()


def bias_mask(place, block, causal, rel_ref, turn_ref, kdoc_ref, qdoc_ref, out_ref):
    heads, rows_total, lanes = out_ref.shape
    key_len = kdoc_ref.shape[0]
    strip = block + 2 * BLOCK_PAD
    query = lax.broadcasted_iota(jnp.int32, (1, lanes), 1)
    start = ((place.cores * (query // block) + place.core) * place.parts + place.part) * block
    allowed = kdoc_ref[...] == qdoc_ref[...]
    if causal:
        places = lax.broadcasted_iota(jnp.int32, (key_len, lanes), 0)
        allowed = allowed & (places <= start + query % block)
    inside = pl.ds(BLOCK_PAD, key_len)
    if rel_ref is None:
        out_ref[0, inside, :] = low(jnp.where(allowed, 0.0, NEGATIVE))
        return
    by_head = tn(rel_ref[...], turn_ref[...])
    width = by_head.shape[1]
    pick_rows = lax.broadcasted_iota(jnp.int32, (8, by_head.shape[0]), 0)
    pick_cols = lax.broadcasted_iota(jnp.int32, (8, by_head.shape[0]), 1)
    picked = nn(low(jnp.where(pick_cols == pick_rows + place.group * heads, 1.0, 0.0)), low(by_head))
    places = lax.broadcasted_iota(jnp.int32, (rows_total, lanes), 0)
    for head in range(heads):
        row = picked[head : head + 1, :]
        left, right = row[:, width - 2 : width - 1], row[:, 0:1]
        out_ref[head] = low(jnp.where(places < start, left, right))
        wide = jnp.broadcast_to(row, (strip, width))
        for number in range(lanes // block):
            at = (number * block) % 128
            turned = pltpu.roll(wide, (width - (strip - 1) + at) % width, 1, stride=1, stride_axis=0)
            rows = pl.ds(place.first_token(number, block), strip)
            out_ref[head, rows, number * block : (number + 1) * block] = low(turned[:, at : at + block])
        out_ref[head, inside, :] = low(jnp.where(allowed, out_ref[head, inside, :].astype(jnp.float32), NEGATIVE))


def chunk_rows(kv_ref):
    return kv_ref.shape[1] * kv_ref.shape[2] * kv_ref.shape[3]


def key_side(kv_ref, chunk):
    return kv_ref[chunk].reshape(chunk_rows(kv_ref), kv_ref.shape[4])[:, : kv_ref.shape[4] // 2]


def value_side(kv_ref, chunk):
    lanes = kv_ref.shape[4]
    return kv_ref[chunk].reshape(chunk_rows(kv_ref), lanes)[:, lanes // 2 // 128 * 128 :]


def bias_rows(bm_ref, head, chunk, rows):
    at = pl.multiple_of(BLOCK_PAD + chunk * rows, 128)
    return bm_ref[head if bm_ref.shape[0] > 1 else 0, pl.ds(at, rows), :].astype(jnp.float32)


def mix_part(q, kv_ref, bm_ref, o_ref, lse_ref, s_ref, ot_ref):
    chunks, rows = kv_ref.shape[0], chunk_rows(kv_ref)
    queries, width = q.shape
    heads = width // HD
    across = [slice(head * queries, (head + 1) * queries) for head in range(heads)]
    masked_q = [only_lanes(q, head * HD, HD) for head in range(heads)]

    def first(chunk, tops):
        keys = key_side(kv_ref, chunk)
        inside = pl.ds(pl.multiple_of(chunk * rows, rows), rows)
        new = []
        for head in range(heads):
            scores = nt(keys, masked_q[head]) + bias_rows(bm_ref, head, chunk, rows)
            s_ref[inside, across[head]] = scores
            new.append(jnp.maximum(tops[head], jnp.max(scores, axis=0, keepdims=True)))
        return tuple(new)

    tops = lax.fori_loop(0, chunks, first, (jnp.full((1, queries), NEGATIVE, jnp.float32),) * heads)

    def second(chunk, carried):
        values = value_side(kv_ref, chunk)
        inside = pl.ds(pl.multiple_of(chunk * rows, rows), rows)
        lead = values.shape[1] - width
        values_t = low(nt(identity(values.shape[1]), values))
        new = []
        for head in range(heads):
            total, mixed = carried[head]
            weights = jnp.exp(s_ref[inside, across[head]] - tops[head])
            mixed = mixed + nn(values_t[lead + head * HD : lead + (head + 1) * HD], low(weights))
            new.append((total + jnp.sum(weights, axis=0, keepdims=True), mixed))
        return tuple(new)

    start = (jnp.zeros((1, queries), jnp.float32), jnp.zeros((HD, queries), jnp.float32))
    done = lax.fori_loop(0, chunks, second, (start,) * heads)
    for head in range(heads):
        total, mixed = done[head]
        lse_ref[:, across[head]] = tops[head] + jnp.log(total)
        ot_ref[head * HD : (head + 1) * HD, :] = low(mixed / total)
    o_ref[...] = low(nt(identity(queries), ot_ref[...]))


def keys_send(place, kv_ref, base, sent, got):
    mine = kv_ref.at[:, place.core, place.part]
    pending = [
        send(mine, mine, sent.at[base, step], got.at[base, step], place.at_plane(place.plane(step)))
        for step in range(1, place.parts)
    ]
    pending.append(send(mine, mine, sent.at[base + 1, 0], got.at[base + 1, 0], place.sibling()))
    return pending


def keys_relay(place, kv_ref, base, sent, got):
    pending = []
    for step in range(1, place.parts):
        source = place.plane_behind(step)
        slot = kv_ref.at[:, place.core, source]
        arrived(slot, sent.at[base, step], got.at[base, step], place.at_plane(source))
        pending.append(send(slot, slot, sent.at[base + 1, step], got.at[base + 1, step], place.sibling()))
    return pending


def keys_wait(place, kv_ref, base, sent, got):
    for step in range(place.parts):
        slot = kv_ref.at[:, 1 - place.core, place.plane_behind(step)]
        arrived(slot, sent.at[base + 1, step], got.at[base + 1, step], place.sibling())


def attend_kernel(crosses, gain_at, place, run, *refs):
    refs = list(refs)

    def take(count):
        taken, refs[:] = refs[:count], refs[count:]
        return taken

    count = len(crosses)
    ins = [take(7 if cross else 8) for cross in crosses]
    outs = [take(8 if cross else 7) for cross in crosses]
    s_ref, ot_ref = take(2)
    bufs = [take(4 if cross else 3) for cross in crosses]
    sent, got = take(2)
    place.greet(planes=True)
    pending = []
    for index, cross in enumerate(crosses):
        x_ref, gain_ref = ins[index][0], ins[index][1]
        if cross:
            bufs[index][3][place.group] = ins[index][6][...]
            pending += spread_start(place, bufs[index][3], sent.at[5 * index + 4], got.at[5 * index + 4])
        bufs[index][0][place.group] = low(rms_norm(x_ref[...].astype(jnp.float32), gain_ref[gain_at[index]]))
        pending += spread_start(place, bufs[index][0], sent.at[5 * index], got.at[5 * index])
    for index, cross in enumerate(crosses):
        w_ref, kv_ref = ins[index][2], outs[index][3]
        kv_width = kv_ref.shape[4]
        n_buf = bufs[index][0]
        if cross:
            source = bufs[index][3]
            spread_wait(place, source, sent.at[5 * index + 4], got.at[5 * index + 4])
            kv = low(nn(all_rows(source), w_ref[:, :kv_width]))
            outs[index][7][...] = all_rows(source)
        else:
            spread_wait(place, n_buf, sent.at[5 * index], got.at[5 * index])
            both = low(nn(all_rows(n_buf), w_ref[...]))
            kv, q = both[:, :kv_width], both[:, kv_width:]
        kv_ref[:, place.core, place.part] = kv.reshape(kv_ref.shape[0], kv_ref.shape[3], kv_width)
        pending += keys_send(place, kv_ref, 5 * index + 1, sent, got)
        if cross:
            spread_wait(place, n_buf, sent.at[5 * index], got.at[5 * index])
            q = low(nn(all_rows(n_buf), w_ref[:, kv_width:]))
        outs[index][1][...] = all_rows(n_buf)
        outs[index][2][...] = q
    run("begin")
    for index, cross in enumerate(crosses):
        block = ins[index][0].shape[0]
        kdoc_ref, qdoc_ref = ins[index][4:6]
        rel_ref, turn_ref = (None, None) if cross else [r.at[index] for r in ins[index][6:8]]
        bias_mask(place, block, index == count - 1 and not cross, rel_ref, turn_ref, kdoc_ref, qdoc_ref, outs[index][6])
    for index in range(count):
        wo_ref = ins[index][3]
        kv_ref, o_ref, lse_ref, bm_ref = outs[index][3:7]
        pending += keys_relay(place, kv_ref, 5 * index + 1, sent, got)
        keys_wait(place, kv_ref, 5 * index + 1, sent, got)
        mix_part(outs[index][2][...], kv_ref, bm_ref, o_ref, lse_ref, s_ref, ot_ref)
        share = nn(o_ref[...], wo_ref[...])
        pending += collect_start(place, share, bufs[index][1], bufs[index][2], sent.at[5 * index + 3], got.at[5 * index + 3])
        if index == 0:
            run("middle")
    for index in range(count):
        total = collect_wait(place, bufs[index][1], bufs[index][2], sent.at[5 * index + 3], got.at[5 * index + 3])
        outs[index][0][...] = ins[index][0][...].astype(jnp.float32) + total
    run("end")
    for copy in pending:
        copy.wait_send()


def attend(sizes, collective_id, gain_at, layers, job=None):
    groups, cores, parts = sizes
    operands, outs, scratch, crosses = [], [], [], []
    f32, bf16 = jnp.float32, jnp.bfloat16
    for layer in layers:
        x, wo = layer[0], layer[3]
        cross = len(layer) == 7
        block, model = x.shape
        width = wo.shape[0]
        tokens = groups * block
        keys = cores * parts * tokens
        operands += layer
        outs += [
            ((block, model), f32), ((tokens, model), bf16), ((tokens, width), bf16),
            ((groups, cores, parts, block, 2 * width), bf16), ((tokens, width), bf16), ((1, width // HD * tokens), f32),
            ((1 if cross else width // HD, keys + 2 * BLOCK_PAD, tokens), bf16),
        ]
        if cross:
            outs.append(((tokens, model), bf16))
        scratch += [(groups, block, model)] * (4 if cross else 3)
        crosses.append(cross)
    first = [pltpu.VMEM((keys, width // HD * tokens), f32), (width, tokens)]
    copies = (5 * len(layers), max(groups, parts))
    got, given = stage(
        sizes, collective_id, functools.partial(attend_kernel, crosses, gain_at), operands, outs, first + scratch, copies, job
    )
    results, at = [], 0
    for cross in crosses:
        size = 8 if cross else 7
        results.append(tuple(got[at : at + size]) + (() if cross else (None,)))
        at += size
    return results, given


def mix_back_part(place, q, do, kv_ref, lse_ref, bm_ref, biased, dkv_ref, p_ref, dp_ref, ds_ref, pb_ref, ot_ref):
    chunks, cores, parts, block, lanes = kv_ref.shape
    rows = chunk_rows(kv_ref)
    queries, width = q.shape
    heads = width // HD
    strip = block + 2 * BLOCK_PAD
    first_value = width // 128 * 128
    lead = width - first_value
    do_wide = jnp.concatenate([jnp.zeros((queries, lead), do.dtype), do], axis=1) if lead else do
    across = [slice(head * queries, (head + 1) * queries) for head in range(heads)]
    masked_q = [only_lanes(q, head * HD, HD) for head in range(heads)]
    masked_do = [only_lanes(do_wide, lead + head * HD, HD) for head in range(heads)]
    nothing = jnp.zeros((1, queries), jnp.float32)
    if biased:
        none = jnp.zeros((BLOCK_PAD, heads * queries), jnp.bfloat16)
        ds_ref[0:BLOCK_PAD, :] = none
        ds_ref[BLOCK_PAD + chunks * rows :, :] = none
        of_lane = lax.broadcasted_iota(jnp.int32, (1, queries), 1) // block
        lane_start = ((cores * of_lane + place.core) * parts + place.part) * block

    def first(chunk, inners):
        keys, values = key_side(kv_ref, chunk), value_side(kv_ref, chunk)
        inside = pl.ds(pl.multiple_of(chunk * rows, rows), rows)
        new = []
        for head in range(heads):
            scores = nt(keys, masked_q[head]) + bias_rows(bm_ref, head, chunk, rows)
            p = jnp.exp(scores - lse_ref[:, across[head]])
            dp = nt(values, masked_do[head])
            p_ref[inside, across[head]] = p
            dp_ref[inside, across[head]] = dp
            pb_ref[inside, across[head]] = low(p)
            new.append(inners[head] + jnp.sum(p * dp, axis=0, keepdims=True))
        return tuple(new)

    inners = lax.fori_loop(0, chunks, first, (nothing,) * heads)
    stacked_q = jnp.concatenate(masked_q, axis=0)
    if lead:
        stacked_q = jnp.concatenate([stacked_q, jnp.zeros((stacked_q.shape[0], lead), stacked_q.dtype)], axis=1)
    stacked_do = jnp.concatenate(masked_do, axis=0)

    def second(chunk, carried):
        at = pl.multiple_of(chunk * rows, rows)
        inside, padded = pl.ds(at, rows), pl.ds(pl.multiple_of(BLOCK_PAD + at, 128), rows)
        keys_t = low(nt(identity(width), key_side(kv_ref, chunk)))
        new = []
        for head in range(heads):
            left, right, back = carried[head]
            ds = low(p_ref[inside, across[head]] * (dp_ref[inside, across[head]] - inners[head]))
            ds_ref[padded, across[head]] = ds
            back = back + nn(keys_t[head * HD : (head + 1) * HD], ds)
            if biased:
                wide = ds.astype(jnp.float32)
                places = lax.broadcasted_iota(jnp.int32, wide.shape, 0) + (at + BLOCK_PAD)
                left = left + jnp.sum(jnp.where(places < lane_start, wide, 0.0), axis=0, keepdims=True)
                right = right + jnp.sum(jnp.where(places >= lane_start + strip, wide, 0.0), axis=0, keepdims=True)
            new.append((left, right, back))
        dk = nn(ds_ref[padded, :], stacked_q)
        dv = nn(pb_ref[inside, :], stacked_do)
        if lead:
            shared = dk[:, first_value:] + dv[:, : 2 * lead]
            both = jnp.concatenate([dk[:, :first_value], shared, dv[:, 2 * lead :]], axis=1)
        else:
            both = jnp.concatenate([dk, dv], axis=1)
        dkv_ref[chunk] = low(both).reshape(dkv_ref.shape[1:])
        return tuple(new)

    start = (nothing, nothing, jnp.zeros((HD, queries), jnp.float32))
    done = lax.fori_loop(0, chunks, second, (start,) * heads)
    for head in range(heads):
        ot_ref[head * HD : (head + 1) * HD, :] = low(done[head][2])
    return low(nt(identity(queries), ot_ref[...])), done


def table_grads(place, block, done, ds_ref, ahead_ref, rel_ref):
    queries = done[0][0].shape[1]
    width = ahead_ref.shape[1]
    strip = block + 2 * BLOCK_PAD
    rows = lax.broadcasted_iota(jnp.int32, (block, block), 0)
    cols = lax.broadcasted_iota(jnp.int32, (block, block), 1)
    backwards = jnp.where(rows + cols == block - 1, 1.0, 0.0)
    at = lax.broadcasted_iota(jnp.int32, (1, width), 1)
    sums = []
    for head, (left, right, _) in enumerate(done):
        total = jnp.zeros((strip, block), jnp.float32)
        for number in range(queries // block):
            low_at = head * queries + number * block
            near = pl.ds(place.first_token(number, block), strip)
            total = total + ds_ref[near, low_at : low_at + block].astype(jnp.float32)
        turned = lax.dot_general(
            backwards, total, (((1,), (1,)), ((), ())), precision=HIGHEST, preferred_element_type=jnp.float32
        )
        turned = jnp.concatenate([turned, jnp.zeros((block, width - strip), jnp.float32)], axis=1)
        by_distance = jnp.sum(pltpu.roll(turned, 0, 1, stride=1, stride_axis=0), axis=0, keepdims=True)
        left, right = (jnp.sum(side, axis=1, keepdims=True) for side in (left, right))
        sums.append(by_distance + jnp.where(at == 0, left, 0.0) + jnp.where(at == width - 2, right, 0.0))
    sums = jnp.concatenate(sums + [jnp.zeros((8 - len(sums), width), jnp.float32)], axis=0)
    rel_ref[...] = lax.dot_general(
        sums, ahead_ref[...], (((1,), (1,)), ((), ())), precision=HIGHEST, preferred_element_type=jnp.float32
    )


def attend_back_kernel(cross, gain_at, which, place, run, *refs):
    refs = list(refs)

    def take(count):
        taken, refs[:] = refs[:count], refs[count:]
        return taken

    x_ref, gain_ref, dy_ref, n_ref, q_ref, kv_ref, o_ref, lse_ref, w_ref, wo_ref, bm_ref = take(11)
    memory_ref, ahead_ref = (take(1)[0], None) if cross else (None, take(1)[0])
    dx_ref, dgain_ref, dw_ref, dwo_ref = take(4)
    dmem_ref, rel_ref = (take(1)[0], None) if cross else (None, take(1)[0])
    p_ref, dp_ref, ds_ref, pb_ref, ot_ref, dkv_ref, sib_ref, zout_ref, zin_ref, d_buf, pn_buf, rn_buf = take(12)
    pm_buf, rm_buf = take(2) if cross else (None, None)
    sent, got = take(2)
    place.greet(planes=True)
    dy = dy_ref[...]
    d_buf[place.group] = low(dy)
    pending = spread_start(place, d_buf, sent.at[0], got.at[0])
    run("begin")
    spread_wait(place, d_buf, sent.at[0], got.at[0])
    dyb = all_rows(d_buf)
    do = low(nt(dyb, wo_ref[...]))
    dq, done = mix_back_part(
        place, q_ref[...], do, kv_ref, lse_ref, bm_ref, not cross, dkv_ref, p_ref, dp_ref, ds_ref, pb_ref, ot_ref
    )
    mine = place.core
    pending.append(send(dkv_ref.at[:, 1 - mine], sib_ref, sent.at[1, 0], got.at[1, 0], place.sibling()))
    kv_width = kv_ref.shape[4]
    dn_share = nt(dq, w_ref[:, kv_width:])
    if cross:
        pending += collect_start(place, dn_share, pn_buf, rn_buf, sent.at[3], got.at[3])
    arrived(sib_ref, sent.at[1, 0], got.at[1, 0], place.sibling())
    for step in list(range(1, place.parts)) + [0]:
        to = place.plane(step)
        zout_ref[to] = low(dkv_ref[:, mine, to].astype(jnp.float32) + sib_ref[:, to].astype(jnp.float32))
        if step:
            pending.append(send(zout_ref.at[to], zin_ref.at[place.part], sent.at[2, step], got.at[2, step], place.at_plane(to)))
    run("middle")
    dwo_ref[...] = low(tn(o_ref[...], dyb))
    dw_ref[:, kv_width:] = low(tn(n_ref[...], dq))
    if not cross:
        table_grads(place, dy_ref.shape[0], done, ds_ref, ahead_ref.at[which], rel_ref)
    total = zout_ref[place.part].astype(jnp.float32)
    for step in range(1, place.parts):
        source = place.plane_behind(step)
        arrived(zin_ref.at[source], sent.at[2, step], got.at[2, step], place.at_plane(source))
        total = total + zin_ref[source].astype(jnp.float32)
    dkv = low(total).reshape(q_ref.shape[0], kv_width)
    if cross:
        pending += collect_start(place, nt(dkv, w_ref[:, :kv_width]), pm_buf, rm_buf, sent.at[4], got.at[4])
        dw_ref[:, :kv_width] = low(tn(memory_ref[...], dkv))
        dmem_ref[...] = collect_wait(place, pm_buf, rm_buf, sent.at[4], got.at[4])
    else:
        share = dn_share + nt(dkv, w_ref[:, :kv_width])
        pending += collect_start(place, share, pn_buf, rn_buf, sent.at[3], got.at[3])
        dw_ref[:, :kv_width] = low(tn(n_ref[...], dkv))
    dn = collect_wait(place, pn_buf, rn_buf, sent.at[3], got.at[3])
    back, dgain = norm_back(x_ref[...].astype(jnp.float32), gain_ref[gain_at], dn)
    dx_ref[...] = dy + back
    dgain_ref[...] = dgain
    run("end")
    for copy in pending:
        copy.wait_send()


def attend_back(sizes, collective_id, x, gains, gain_at, dy, kept, w, wo, ahead, which, job=None):
    cross = ahead is None
    groups, cores, parts = sizes
    _, n, q, kv, o, lse, bm, memory = kept
    block, model = x.shape
    tokens, width = q.shape
    heads = width // HD
    keys = cores * parts * tokens
    f32, bf16 = jnp.float32, jnp.bfloat16
    operands = [x, gains, dy, n, q, kv, o, lse, w, wo, bm] + [memory if cross else ahead]
    outs = [((block, model), f32), ((1, model), f32), (w.shape, bf16), (wo.shape, bf16)]
    outs.append(((block, model) if cross else (8, ahead.shape[1]), f32))
    turned = (parts, groups, block, 2 * width)
    scratch = [
        pltpu.VMEM((keys, heads * tokens), f32), pltpu.VMEM((keys, heads * tokens), f32),
        (keys + 2 * BLOCK_PAD, heads * tokens), (keys, heads * tokens), (width, tokens),
        kv.shape, (groups, parts, block, 2 * width), turned, turned,
    ] + [(groups, block, model)] * (5 if cross else 3)
    copies = (5, max(groups, parts))
    return stage(sizes, collective_id, functools.partial(attend_back_kernel, cross, gain_at, which), operands, outs, scratch, copies, job)


def fast_device(
    enc_in, dec_in, enc_cot, dec_cot, enc_segments, dec_segments, buckets,
    enc_norm1, enc_query, enc_key, enc_value, enc_proj, enc_rel, enc_norm2, enc_gate, enc_up, enc_down, enc_final,
    dec_norm1, dec_query, dec_key, dec_value, dec_proj, dec_rel, dec_norm2, cross_query, cross_key, cross_value, cross_proj,
    dec_norm3, dec_gate, dec_up, dec_down,
):
    groups, cores, parts = sizes = lax.axis_size(HG), lax.axis_size(CORE), lax.axis_size(SP)
    my_group, my_core, my_part = lax.axis_index(HG), lax.axis_index(CORE), lax.axis_index(SP)
    block, model = enc_in.shape
    devices = groups * cores
    share = model // devices
    heads = HEADS // groups
    reach = (buckets.shape[1] - 1) // 2
    bf16, f32 = jnp.bfloat16, jnp.float32

    def packed(*weights):
        cut = [w.reshape(w.shape[0], groups, w.shape[1] // groups) for w in weights]
        return jnp.concatenate(cut, axis=2).transpose(1, 0, 2)

    small = jnp.concatenate([enc_norm1, enc_norm2, enc_final, dec_norm1, dec_norm2, dec_norm3, enc_rel, dec_rel])
    small = jnp.broadcast_to(small, (groups, 16, small.shape[0]))
    (small, enc_kvq, dec_kvq), (enc_wo, dec_wo) = job_alone(
        sizes,
        1,
        Recut(
            sizes,
            [small, packed(enc_key, enc_value, enc_query), packed(dec_key, dec_value, dec_query)],
            [enc_proj, dec_proj],
        ),
    )
    later = Recut(
        sizes,
        [packed(enc_gate, enc_up), packed(cross_key, cross_value, cross_query), packed(dec_gate, dec_up)],
        [enc_down, cross_proj, dec_down],
    )
    small = small.reshape(devices, 16, -1)[:, 0]
    gains = small[:, : 6 * share].reshape(devices, 6, share).transpose(1, 0, 2).reshape(6, 1, model).astype(f32)
    rel_len = enc_rel.shape[0]
    rels = small[:, 6 * share :].reshape(devices, 2, rel_len).transpose(1, 0, 2).reshape(2, -1, HEADS)
    rels = jnp.pad(rels, ((0, 0), (0, 0), (0, 128 - HEADS)))

    bucket_count = devices * rel_len // HEADS
    numbers = jnp.arange(bucket_count, dtype=jnp.int32)[None, :, None]
    long = jnp.pad(buckets, ((0, 0), (block - 1, block)), mode="edge")[:, None, :]
    ahead = (long == numbers).astype(f32)
    back_way = jnp.pad(buckets[:, ::-1], ((0, 0), (block - 1, block)), mode="edge")[:, None, :]
    turn = (back_way == numbers).astype(bf16)

    def mine(ids):
        return lax.dynamic_index_in_dim(
            lax.dynamic_index_in_dim(ids.reshape(groups, cores, parts, block), my_core, 1, False), my_part, 1, False
        ).reshape(1, -1)

    enc_q_ids, dec_q_ids = mine(enc_segments), mine(dec_segments)
    enc_k_ids, dec_k_ids = enc_segments[:, None], dec_segments[:, None]

    (enc_kept, dec_kept), ((enc_gu, cross_kvq, dec_gu), (enc_wd, cross_wo, dec_wd)) = attend(
        sizes,
        2,
        (0, 3),
        [
            (enc_in, gains, enc_kvq, enc_wo, enc_k_ids, enc_q_ids, rels, turn),
            (dec_in, gains, dec_kvq, dec_wo, dec_k_ids, dec_q_ids, rels, turn),
        ],
        later,
    )
    ex, dx = enc_kept[0], dec_kept[0]
    tokens, hidden = groups * block, enc_wd.shape[0]
    token_f32, token_bf16, gain_f32 = ((block, model), f32), ((block, model), bf16), ((1, model), f32)
    gu_grad, down_grad = ((model, 2 * hidden), bf16), ((hidden, model), bf16)
    buffer = (groups, block, model)
    (enc_out, memory, en2), _ = stage(
        sizes, 3, functools.partial(feed_forward_kernel, 1, 2), [ex, gains, enc_gu, enc_wd],
        [token_f32, token_bf16, ((tokens, model), bf16)], [buffer] * 3, (2, groups),
    )
    (cross_kept,), _ = attend(sizes, 4, (4,), [(dx, gains, cross_kvq, cross_wo, enc_k_ids, dec_q_ids, memory)])
    cx = cross_kept[0]
    (dec_out, grad_cx, dg_d3, dw_dgu, dw_ddown), _ = stage(
        sizes, 5, functools.partial(feed_both_kernel, 5), [cx, dec_cot, gains, dec_gu, dec_wd],
        [token_f32, token_f32, gain_f32, gu_grad, down_grad], [buffer] * 6, (4, groups),
    )

    tie = lax.optimization_barrier

    def summed(grads, before):
        grads, _ = tie((grads, before))
        return [lax.psum(g, SP) for g in grads]

    (grad_dx, dg_d2, dw_ckvq, dw_co, dmem), rows_a = attend_back(
        sizes, 6, dx, gains, 4, grad_cx, cross_kept, cross_kvq, cross_wo, None, None, GiveRows(sizes, [dw_dgu], [dw_ddown])
    )
    (grad_ex, dg_e2, dg_ef, dw_egu, dw_edown), rows_b = stage(
        sizes, 7, functools.partial(feed_back_kernel, 1, 2), [ex, enc_out, enc_cot, dmem, gains, en2, enc_gu, enc_wd],
        [token_f32, gain_f32, gain_f32, gu_grad, down_grad], [buffer] * 3, (2, groups),
        GiveRows(sizes, [dw_ckvq], [dw_co]),
    )
    sum_ab = summed(rows_a + rows_b, [small])
    grad_dx, grad_ex = tie((grad_dx, grad_ex))
    (dec_in_grad, dg_d1, dw_dkvq, dw_do, dec_tab), rows_c = attend_back(
        sizes, 8, dec_in, gains, 3, grad_dx, dec_kept, dec_kvq, dec_wo, ahead, 1, GiveRows(sizes, [dw_egu], [dw_edown])
    )
    grad_ex, sum_ab = tie((grad_ex, sum_ab))
    sum_c = summed(rows_c, sum_ab)
    (enc_in_grad, dg_e1, dw_ekvq, dw_eo, enc_tab), rows_d = attend_back(
        sizes, 9, enc_in, gains, 0, grad_ex, enc_kept, enc_kvq, enc_wo, ahead, 0, GiveRows(sizes, [dw_dkvq], [dw_do])
    )

    def rel_grad(mine):
        full = lax.dynamic_update_slice_in_dim(jnp.zeros((HEADS, bucket_count), f32), mine[:heads], my_group * heads, 0)
        return full.T.reshape(-1)

    small_grads = [dg_e1, dg_e2, dg_ef, dg_d1, dg_d2, dg_d3, rel_grad(enc_tab), rel_grad(dec_tab)]
    packed_small = jnp.concatenate([v.reshape(devices, 1, -1) for v in small_grads], axis=2)
    packed_small = jnp.broadcast_to(packed_small, (devices, 16, packed_small.shape[2]))
    packed_small = packed_small.reshape(devices * 16, -1).astype(bf16)
    dw_ekvq, sum_c = tie((dw_ekvq, sum_c))
    sum_e, sum_d = finish(sizes, 10, GiveRows(sizes, [dw_ekvq, packed_small], [dw_eo]), rows_d)

    def unpacked(whole, pieces):
        each = whole.shape[2] // pieces
        whole = whole.astype(f32)
        return [whole[:, :, i * each : (i + 1) * each].transpose(1, 0, 2).reshape(share, groups * each) for i in range(pieces)]

    dgu_rows, d_wd, cross_rows, c_wo = sum_ab
    egu_rows, e_wd = sum_c
    dkvq_rows, d_wo = sum_d
    ekvq_rows, small_rows, e_wo = sum_e
    d_wd, c_wo, e_wd, d_wo, e_wo = [g[0].astype(f32) for g in (d_wd, c_wo, e_wd, d_wo, e_wo)]
    e_wk, e_wv, e_wq = unpacked(ekvq_rows, 3)
    e_wg, e_wu = unpacked(egu_rows, 2)
    d_wk, d_wv, d_wq = unpacked(dkvq_rows, 3)
    c_wk, c_wv, c_wq = unpacked(cross_rows, 3)
    d_wg, d_wu = unpacked(dgu_rows, 2)
    own = jnp.sum(small_rows[:, 0].astype(f32), axis=0)
    s = [own[i * share : (i + 1) * share] for i in range(6)]
    e_rel, d_rel = own[6 * share : 6 * share + rel_len], own[6 * share + rel_len :]
    return (
        enc_out, dec_out, enc_in_grad, dec_in_grad,
        s[0], e_wq, e_wk, e_wv, e_wo, e_rel, s[1], e_wg, e_wu, e_wd, s[2],
        s[3], d_wq, d_wk, d_wv, d_wo, d_rel, s[4], c_wq, c_wk, c_wv, c_wo, s[5], d_wg, d_wu, d_wd,
    )


def general_plan(mesh):
    placed = (
        P(("ctx", "sp"), None),
        P(("ctx", "sp"), None),
        P(("ctx", "sp"), None),
        P(("ctx", "sp"), None),
        P(),
        P(),
        P(),
        P("ctx"),
        P("ctx", None),
        P("ctx", None),
        P("ctx", None),
        P("ctx", None),
        P("ctx"),
        P("ctx"),
        P("ctx", None),
        P("ctx", None),
        P("ctx", None),
        P("ctx"),
        P("ctx"),
        P("ctx", None),
        P("ctx", None),
        P("ctx", None),
        P("ctx", None),
        P("ctx"),
        P("ctx"),
        P("ctx", None),
        P("ctx", None),
        P("ctx", None),
        P("ctx", None),
        P("ctx"),
        P("ctx", None),
        P("ctx", None),
        P("ctx", None),
    )
    return jax.shard_map(
        per_device,
        mesh=mesh,
        in_specs=placed,
        out_specs=(
            P(("ctx", "sp"), None),
            P(("ctx", "sp"), None),
            P(("ctx", "sp"), None),
            P(("ctx", "sp"), None),
            P("ctx"),
            P("ctx", None),
            P("ctx", None),
            P("ctx", None),
            P("ctx", None),
            P("ctx"),
            P("ctx"),
            P("ctx", None),
            P("ctx", None),
            P("ctx", None),
            P("ctx"),
            P("ctx"),
            P("ctx", None),
            P("ctx", None),
            P("ctx", None),
            P("ctx", None),
            P("ctx"),
            P("ctx"),
            P("ctx", None),
            P("ctx", None),
            P("ctx", None),
            P("ctx", None),
            P("ctx"),
            P("ctx", None),
            P("ctx", None),
            P("ctx", None),
        ),
        check_vma=False,
    )


def split_plan(mesh, groups):
    cut = Mesh(np.asarray(mesh.devices).reshape(groups, 2, mesh.shape["sp"]), (HG, CORE, SP))
    tokens, rows, gain, same = P((HG, CORE, SP), None), P((HG, CORE), None), P((HG, CORE)), P()
    attention = (gain, rows, rows, rows, rows, gain)
    feed = (gain, rows, rows, rows)
    weights = attention + feed + (gain,) + attention + (gain, rows, rows, rows, rows) + feed
    return jax.shard_map(
        fast_device,
        mesh=cut,
        in_specs=(tokens,) * 4 + (same,) * 3 + weights,
        out_specs=(tokens,) * 4 + weights,
        check_vma=False,
    )


def solution(mesh):
    groups, odd = divmod(mesh.shape["ctx"], 2)
    if odd or HEADS % groups or mesh.shape["sp"] != 4:
        return general_plan(mesh)
    return split_plan(mesh, groups)
```

```python
import functools
import math

import jax
import jax.numpy as jnp
import numpy as np
from jax import lax
from jax.experimental import pallas as pl
from jax.experimental.pallas import tpu as pltpu
from jax.sharding import Mesh
from jax.sharding import PartitionSpec as P

HEADS = 12
HD = 64


EPSILON = 1e-06
NEGATIVE = -1e30
HIGHEST = lax.Precision.HIGHEST


def rms_norm(values, norm_gain):
    return (
        values * lax.rsqrt(jnp.mean(values * values, axis=-1, keepdims=True) + EPSILON) * norm_gain
    )


def norm_pullback(values, norm_gain, grad_normed):
    _, pullback = jax.vjp(rms_norm, values, norm_gain)
    return pullback(grad_normed)


def gated(gate_val, up_val):
    return jax.nn.gelu(gate_val, approximate=True) * up_val


def project(left, right):
    return jnp.dot(left, right, preferred_element_type=jnp.float32)


def weight_grad(left, right):
    return jnp.einsum("td,te->de", left, right, preferred_element_type=jnp.float32)


def input_grad(grad_out, weight):
    return jnp.einsum("te,de->td", grad_out, weight, preferred_element_type=jnp.float32)


def head_table(relative, table_row, heads_here):
    bucket_count = relative.shape[0] // HEADS
    onehot = (table_row[:, None] == jnp.arange(bucket_count, dtype=jnp.int32)[None, :]).astype(
        jnp.float32
    )
    bias_grid = relative.astype(jnp.float32).reshape(bucket_count, HEADS)
    full_table = jnp.dot(onehot, bias_grid, precision=HIGHEST).T
    first_head = lax.axis_index("sp") * heads_here
    return (lax.dynamic_slice_in_dim(full_table, first_head, heads_here, 0), onehot)


def table_grad(grad_table, onehot, heads_here):
    full_grad = jnp.zeros((HEADS, onehot.shape[0]), jnp.float32)
    full_grad = lax.dynamic_update_slice_in_dim(
        full_grad, grad_table, lax.axis_index("sp") * heads_here, 0
    )
    return jnp.dot(onehot.T, full_grad.T, precision=HIGHEST).reshape(-1)


def bias_block(head_bias, pad_len, offset_q, rows, offset_k, cols):
    head_count, table_len = head_bias.shape
    reach_len = (table_len - 1) // 2
    left_edge = jnp.broadcast_to(head_bias[:, :1], (head_count, pad_len))
    right_edge = jnp.broadcast_to(head_bias[:, -1:], (head_count, pad_len))
    padded = jnp.concatenate([left_edge, head_bias, right_edge], axis=1)
    band_width = rows + cols - 1
    start = offset_k - offset_q - (rows - 1) + reach_len + pad_len
    band = lax.dynamic_slice_in_dim(padded, start, band_width, 1)
    tiled = jnp.broadcast_to(band[:, None, :], (head_count, rows, band_width)).reshape(
        head_count, rows * band_width
    )
    skewed = tiled[:, rows - 1 : rows - 1 + rows * (band_width - 1)].reshape(
        head_count, rows, band_width - 1
    )
    return skewed[:, :, :cols]


def make_frame(query_local, query_ids, key_ids, head_bias, causal):
    local_len = query_local.shape[0]
    heads_here = query_local.shape[1] // HD
    offset_q = lax.axis_index("ctx") * local_len
    ids_q = lax.dynamic_slice_in_dim(query_ids, offset_q, local_len, 0)
    row_ids = offset_q + jnp.arange(local_len, dtype=jnp.int32)
    query_heads = query_local.reshape(local_len, heads_here, HD)
    pad_len = query_ids.shape[0] + key_ids.shape[0]

    def bias_of(entries, offset_k, length):
        return bias_block(entries, pad_len, offset_q, local_len, offset_k, length)

    def scores_of(key_block, offset_k):
        length = key_block.shape[0]
        key_heads = key_block.reshape(length, heads_here, HD)
        raw_scores = jnp.einsum(
            "qhd,khd->hqk", query_heads, key_heads, preferred_element_type=jnp.float32
        )
        col_ids = offset_k + jnp.arange(length, dtype=jnp.int32)
        ids_k = lax.dynamic_slice_in_dim(key_ids, offset_k, length, 0)
        allowed = ids_q[:, None] == ids_k[None, :]
        if causal:
            allowed = allowed & (col_ids[None, :] <= row_ids[:, None])
        if head_bias is not None:
            raw_scores = raw_scores + bias_of(head_bias, offset_k, length)
        return (raw_scores, allowed)

    def touches(offset_k, length):
        first_id = lax.dynamic_slice_in_dim(key_ids, offset_k, 1, 0)[0]
        last_id = lax.dynamic_slice_in_dim(key_ids, offset_k + length - 1, 1, 0)[0]
        touched = (ids_q[0] <= last_id) & (first_id <= ids_q[-1])
        if causal:
            touched = touched & (offset_k <= offset_q + local_len - 1)
        return touched

    return (query_heads, scores_of, touches, bias_of)


def sweep(keys_gathered, local_len, step_fn, carry_state):
    key_all, value_all = keys_gathered
    block_len = local_len * math.gcd(4, lax.axis_size("ctx"))

    def sweep_loop_body(number, running):
        offset_k = number * block_len
        key_block = lax.dynamic_slice_in_dim(key_all, offset_k, block_len, 0)
        value_block = lax.dynamic_slice_in_dim(value_all, offset_k, block_len, 0)
        return step_fn(running, key_block, value_block, offset_k)

    return lax.fori_loop(0, key_all.shape[0] // block_len, sweep_loop_body, carry_state)


def whole_keys(key_local, value_local):
    return (
        lax.all_gather(key_local, "ctx", axis=0, tiled=True),
        lax.all_gather(value_local, "ctx", axis=0, tiled=True),
    )


def attention_forward(query_proj, key_proj, value_proj, query_ids, key_ids, head_bias, causal):
    query_local, key_local, value_local = (
        lax.all_to_all(query_proj, "sp", split_axis=1, concat_axis=0, tiled=True),
        lax.all_to_all(key_proj, "sp", split_axis=1, concat_axis=0, tiled=True),
        lax.all_to_all(value_proj, "sp", split_axis=1, concat_axis=0, tiled=True),
    )
    local_len = query_local.shape[0]
    heads_here = query_local.shape[1] // HD
    query_heads, scores_of, touches, _ = make_frame(
        query_local, query_ids, key_ids, head_bias, causal
    )
    key_block = lax.all_gather(key_local, "ctx", axis=0, tiled=True)
    value_block = lax.all_gather(value_local, "ctx", axis=0, tiled=True)
    offset_k = jnp.int32(0)
    length = key_block.shape[0]
    row_top = jnp.full((heads_here, local_len), NEGATIVE, jnp.float32)
    weighted = jnp.zeros((local_len, heads_here, HD), jnp.float32)
    raw_scores, allowed = scores_of(key_block, offset_k)
    masked = jnp.where(allowed[None], raw_scores, NEGATIVE)
    new_top = jnp.maximum(row_top, jnp.max(masked, axis=-1))
    weights = jnp.where(allowed[None], jnp.exp(masked - new_top[..., None]), 0.0)
    rescale = jnp.exp(row_top - new_top)
    value_heads = value_block.reshape(length, heads_here, HD)
    increment = jnp.einsum(
        "hqk,khd->qhd",
        weights.astype(jnp.bfloat16),
        value_heads,
        preferred_element_type=jnp.float32,
    )
    row_top, row_total, weighted = (
        new_top,
        jnp.sum(weights, axis=-1),
        weighted * rescale.T[:, :, None] + increment,
    )
    mixed_heads = weighted / row_total.T[:, :, None]
    log_total = row_top + jnp.log(row_total)
    mixed_low = mixed_heads.reshape(local_len, heads_here * HD).astype(jnp.bfloat16)
    mixed_tokens = lax.all_to_all(mixed_low, "sp", split_axis=0, concat_axis=1, tiled=True)
    retained = (
        query_local,
        key_local,
        value_local,
        mixed_heads,
        log_total,
        None,
        query_ids,
        key_ids,
        head_bias,
        causal,
    )
    return (mixed_tokens, retained)


def attention_backward(grad_mixed, retained):
    (
        query_local,
        key_local,
        value_local,
        mixed_heads,
        log_total,
        gathered,
        query_ids,
        key_ids,
        head_bias,
        causal,
    ) = retained
    grad_local = lax.all_to_all(grad_mixed, "sp", split_axis=1, concat_axis=0, tiled=True)
    local_len = query_local.shape[0]
    heads_here = query_local.shape[1] // HD
    width = heads_here * HD
    query_heads, scores_of, touches, bias_of = make_frame(
        query_local, query_ids, key_ids, head_bias, causal
    )
    grad_heads = grad_local.reshape(local_len, heads_here, HD)
    row_inner = jnp.einsum("qhd,qhd->hq", grad_heads.astype(jnp.float32), mixed_heads)
    gathered = whole_keys(key_local, value_local)
    table_zero = jnp.zeros(head_bias.shape if head_bias is not None else (1,), jnp.float32)

    def gradients_of(key_block, value_block, offset_k):
        length = key_block.shape[0]
        raw_scores, allowed = scores_of(key_block, offset_k)
        probabilities = jnp.where(allowed[None], jnp.exp(raw_scores - log_total[..., None]), 0.0)
        value_heads = value_block.reshape(length, heads_here, HD)
        grad_probs = jnp.einsum(
            "qhd,khd->hqk", grad_heads, value_heads, preferred_element_type=jnp.float32
        )
        grad_scores = (probabilities * (grad_probs - row_inner[..., None])).astype(jnp.bfloat16)
        return (probabilities, grad_scores)

    def table_part(grad_scores, offset_k, length):
        if head_bias is None:
            return table_zero
        _, pullback = jax.vjp(lambda entries: bias_of(entries, offset_k, length), head_bias)
        return pullback(grad_scores.astype(jnp.float32))[0]

    def key_terms_of(probabilities, grad_scores, length):
        grad_key = jnp.einsum(
            "hqk,qhd->khd", grad_scores, query_heads, preferred_element_type=jnp.float32
        )
        grad_value = jnp.einsum(
            "hqk,qhd->khd",
            probabilities.astype(jnp.bfloat16),
            grad_heads,
            preferred_element_type=jnp.float32,
        )
        return jnp.concatenate(
            [grad_key.reshape(length, width), grad_value.reshape(length, width)], axis=1
        )

    def query_part(grad_scores, key_block):
        length = key_block.shape[0]
        key_heads = key_block.reshape(length, heads_here, HD)
        return jnp.einsum(
            "hqk,khd->qhd", grad_scores, key_heads, preferred_element_type=jnp.float32
        )

    def query_step(running, key_block, value_block, offset_k):
        length = key_block.shape[0]
        grad_query, grad_table = running
        probabilities, grad_scores = gradients_of(key_block, value_block, offset_k)
        return (
            grad_query + query_part(grad_scores, key_block),
            grad_table + table_part(grad_scores, offset_k, length),
        )

    query_zero = jnp.zeros((local_len, heads_here, HD), jnp.float32)
    block_len = local_len * math.gcd(4, lax.axis_size("ctx"))
    grad_query, grad_table = sweep(gathered, local_len, query_step, (query_zero, table_zero))
    key_all, value_all = gathered
    step_len = math.gcd(lax.axis_size("ctx") * local_len, block_len)

    def term_loop_body(number, rows_acc):
        offset_b = number * step_len
        key_block = lax.dynamic_slice_in_dim(key_all, offset_b, step_len, 0)
        value_block = lax.dynamic_slice_in_dim(value_all, offset_b, step_len, 0)
        probabilities, grad_scores = gradients_of(key_block, value_block, offset_b)
        return lax.dynamic_update_slice_in_dim(
            rows_acc, key_terms_of(probabilities, grad_scores, step_len), number * step_len, 0
        )

    own_rows = lax.psum_scatter(
        lax.fori_loop(
            0,
            lax.axis_size("ctx") * local_len // step_len,
            term_loop_body,
            jnp.zeros((lax.axis_size("ctx") * local_len, 2 * width), jnp.float32),
        ),
        "ctx",
        scatter_dimension=0,
        tiled=True,
    )
    grad_q_low = grad_query.reshape(local_len, width).astype(jnp.bfloat16)
    grad_k_low = own_rows[:, :width].astype(jnp.bfloat16)
    grad_v_low = own_rows[:, width:].astype(jnp.bfloat16)
    grad_q_tok, grad_k_tok, grad_v_tok = (
        lax.all_to_all(grad_q_low, "sp", split_axis=0, concat_axis=1, tiled=True),
        lax.all_to_all(grad_k_low, "sp", split_axis=0, concat_axis=1, tiled=True),
        lax.all_to_all(grad_v_low, "sp", split_axis=0, concat_axis=1, tiled=True),
    )
    return (grad_q_tok, grad_k_tok, grad_v_tok, grad_table)


def attention_layer(
    residual,
    source,
    norm_gain,
    w_query,
    w_key,
    w_value,
    w_proj,
    query_ids,
    key_ids,
    head_bias,
    causal,
):
    normed = rms_norm(residual, norm_gain).astype(jnp.bfloat16)
    kv_input = normed if source is None else source
    query_proj = project(normed, w_query).astype(jnp.bfloat16)
    key_proj = project(kv_input, w_key).astype(jnp.bfloat16)
    value_proj = project(kv_input, w_value).astype(jnp.bfloat16)
    mixed_tokens, retained = attention_forward(
        query_proj, key_proj, value_proj, query_ids, key_ids, head_bias, causal
    )
    result = residual + project(mixed_tokens, w_proj)
    return (result, (residual, normed, kv_input, mixed_tokens, retained))


def attention_layer_back(grad_out, saved, norm_gain, w_query, w_key, w_value, w_proj, is_cross):
    residual, normed, kv_input, mixed_tokens, retained = saved
    grad_low = grad_out.astype(jnp.bfloat16)
    grad_proj = weight_grad(mixed_tokens, grad_low)
    grad_mixed = input_grad(grad_low, w_proj).astype(jnp.bfloat16)
    grad_q_tok, grad_k_tok, grad_v_tok, grad_table = attention_backward(grad_mixed, retained)
    grad_wq = weight_grad(normed, grad_q_tok)
    grad_wk = weight_grad(kv_input, grad_k_tok)
    grad_wv = weight_grad(kv_input, grad_v_tok)
    grad_source = input_grad(grad_k_tok, w_key) + input_grad(grad_v_tok, w_value)
    grad_normed = input_grad(grad_q_tok, w_query)
    if not is_cross:
        grad_normed = grad_normed + grad_source
        grad_source = None
    grad_resid, grad_gain = norm_pullback(residual, norm_gain, grad_normed)
    return (
        grad_out + grad_resid,
        grad_source,
        (grad_gain, grad_wq, grad_wk, grad_wv, grad_proj, grad_table),
    )


def feed_layer(residual, norm_gain, w_gate, w_up, w_down):
    normed = rms_norm(residual, norm_gain).astype(jnp.bfloat16)
    gate_val = project(normed, w_gate)
    up_val = project(normed, w_up)
    hidden = gated(gate_val, up_val).astype(jnp.bfloat16)
    return (residual + project(hidden, w_down), (residual, normed, gate_val, up_val, hidden))


def feed_layer_back(grad_out, saved, norm_gain, w_gate, w_up, w_down):
    residual, normed, gate_val, up_val, hidden = saved
    grad_low = grad_out.astype(jnp.bfloat16)
    grad_down = weight_grad(hidden, grad_low)
    grad_hidden = input_grad(grad_low, w_down)
    _, pullback = jax.vjp(gated, gate_val, up_val)
    grad_gate, grad_up = pullback(grad_hidden)
    grad_gate = grad_gate.astype(jnp.bfloat16)
    grad_up = grad_up.astype(jnp.bfloat16)
    grad_wg = weight_grad(normed, grad_gate)
    grad_wu = weight_grad(normed, grad_up)
    grad_normed = input_grad(grad_gate, w_gate) + input_grad(grad_up, w_up)
    grad_resid, grad_gain = norm_pullback(residual, norm_gain, grad_normed)
    return (grad_out + grad_resid, (grad_gain, grad_wg, grad_wu, grad_down))


def per_device(
    enc_in,
    dec_in,
    enc_cot,
    dec_cot,
    enc_segments,
    dec_segments,
    buckets,
    enc_norm1,
    enc_query,
    enc_key,
    enc_value,
    enc_proj,
    enc_rel,
    enc_norm2,
    enc_gate,
    enc_up,
    enc_down,
    enc_final,
    dec_norm1,
    dec_query,
    dec_key,
    dec_value,
    dec_proj,
    dec_rel,
    dec_norm2,
    cross_query,
    cross_key,
    cross_value,
    cross_proj,
    dec_norm3,
    dec_gate,
    dec_up,
    dec_down,
):
    (
        enc_norm1,
        enc_query,
        enc_key,
        enc_value,
        enc_proj,
        enc_rel,
        enc_norm2,
        enc_gate,
        enc_up,
        enc_down,
        enc_final,
        dec_norm1,
        dec_query,
        dec_key,
        dec_value,
        dec_proj,
        dec_rel,
        dec_norm2,
        cross_query,
        cross_key,
        cross_value,
        cross_proj,
        dec_norm3,
        dec_gate,
        dec_up,
        dec_down,
    ) = (
        lax.all_gather(enc_norm1, "ctx", axis=0, tiled=True),
        lax.all_gather(enc_query, "ctx", axis=0, tiled=True),
        lax.all_gather(enc_key, "ctx", axis=0, tiled=True),
        lax.all_gather(enc_value, "ctx", axis=0, tiled=True),
        lax.all_gather(enc_proj, "ctx", axis=0, tiled=True),
        lax.all_gather(enc_rel, "ctx", axis=0, tiled=True),
        lax.all_gather(enc_norm2, "ctx", axis=0, tiled=True),
        lax.all_gather(enc_gate, "ctx", axis=0, tiled=True),
        lax.all_gather(enc_up, "ctx", axis=0, tiled=True),
        lax.all_gather(enc_down, "ctx", axis=0, tiled=True),
        lax.all_gather(enc_final, "ctx", axis=0, tiled=True),
        lax.all_gather(dec_norm1, "ctx", axis=0, tiled=True),
        lax.all_gather(dec_query, "ctx", axis=0, tiled=True),
        lax.all_gather(dec_key, "ctx", axis=0, tiled=True),
        lax.all_gather(dec_value, "ctx", axis=0, tiled=True),
        lax.all_gather(dec_proj, "ctx", axis=0, tiled=True),
        lax.all_gather(dec_rel, "ctx", axis=0, tiled=True),
        lax.all_gather(dec_norm2, "ctx", axis=0, tiled=True),
        lax.all_gather(cross_query, "ctx", axis=0, tiled=True),
        lax.all_gather(cross_key, "ctx", axis=0, tiled=True),
        lax.all_gather(cross_value, "ctx", axis=0, tiled=True),
        lax.all_gather(cross_proj, "ctx", axis=0, tiled=True),
        lax.all_gather(dec_norm3, "ctx", axis=0, tiled=True),
        lax.all_gather(dec_gate, "ctx", axis=0, tiled=True),
        lax.all_gather(dec_up, "ctx", axis=0, tiled=True),
        lax.all_gather(dec_down, "ctx", axis=0, tiled=True),
    )
    enc_norm1 = enc_norm1.astype(jnp.float32)
    enc_norm2 = enc_norm2.astype(jnp.float32)
    enc_final = enc_final.astype(jnp.float32)
    dec_norm1 = dec_norm1.astype(jnp.float32)
    dec_norm2 = dec_norm2.astype(jnp.float32)
    dec_norm3 = dec_norm3.astype(jnp.float32)
    heads_here = HEADS // lax.axis_size("sp")
    enc_table, enc_onehot = head_table(enc_rel, buckets[0], heads_here)
    dec_table, dec_onehot = head_table(dec_rel, buckets[1], heads_here)
    enc_x = enc_in.astype(jnp.float32)
    enc_mid, enc_saved_a = attention_layer(
        enc_x,
        None,
        enc_norm1,
        enc_query,
        enc_key,
        enc_value,
        enc_proj,
        enc_segments,
        enc_segments,
        enc_table,
        False,
    )
    enc_result, enc_saved_f = feed_layer(enc_mid, enc_norm2, enc_gate, enc_up, enc_down)
    memory = rms_norm(enc_result, enc_final).astype(jnp.bfloat16)
    dec_x = dec_in.astype(jnp.float32)
    dec_mid, dec_saved_a = attention_layer(
        dec_x,
        None,
        dec_norm1,
        dec_query,
        dec_key,
        dec_value,
        dec_proj,
        dec_segments,
        dec_segments,
        dec_table,
        True,
    )
    dec_cross, dec_saved_c = attention_layer(
        dec_mid,
        memory,
        dec_norm2,
        cross_query,
        cross_key,
        cross_value,
        cross_proj,
        dec_segments,
        enc_segments,
        None,
        False,
    )
    dec_result, dec_saved_f = feed_layer(dec_cross, dec_norm3, dec_gate, dec_up, dec_down)
    grad_dec, dec_ff_grads = feed_layer_back(
        dec_cot.astype(jnp.float32), dec_saved_f, dec_norm3, dec_gate, dec_up, dec_down
    )
    grad_dec, grad_memory, cross_grads = attention_layer_back(
        grad_dec, dec_saved_c, dec_norm2, cross_query, cross_key, cross_value, cross_proj, True
    )
    grad_dec, _, dec_self_grads = attention_layer_back(
        grad_dec, dec_saved_a, dec_norm1, dec_query, dec_key, dec_value, dec_proj, False
    )
    grad_enc_out, grad_final = norm_pullback(enc_result, enc_final, grad_memory)
    grad_enc, enc_ff_grads = feed_layer_back(
        enc_cot.astype(jnp.float32) + grad_enc_out,
        enc_saved_f,
        enc_norm2,
        enc_gate,
        enc_up,
        enc_down,
    )
    grad_enc, _, enc_self_grads = attention_layer_back(
        grad_enc, enc_saved_a, enc_norm1, enc_query, enc_key, enc_value, enc_proj, False
    )
    e_gain1, e_wq, e_wk, e_wv, e_wo, e_table = enc_self_grads
    e_gain2, e_wg, e_wu, e_wd = enc_ff_grads
    d_gain1, d_wq, d_wk, d_wv, d_wo, d_table = dec_self_grads
    c_gain, c_wq, c_wk, c_wv, c_wo, _ = cross_grads
    d_gain3, d_wg, d_wu, d_wd = dec_ff_grads
    e_rel = table_grad(e_table, enc_onehot, heads_here)
    d_rel = table_grad(d_table, dec_onehot, heads_here)
    shards = (
        lax.psum_scatter(e_gain1, "ctx", scatter_dimension=0, tiled=True),
        lax.psum_scatter(e_wq, "ctx", scatter_dimension=0, tiled=True),
        lax.psum_scatter(e_wk, "ctx", scatter_dimension=0, tiled=True),
        lax.psum_scatter(e_wv, "ctx", scatter_dimension=0, tiled=True),
        lax.psum_scatter(e_wo, "ctx", scatter_dimension=0, tiled=True),
        lax.psum_scatter(e_rel, "ctx", scatter_dimension=0, tiled=True),
        lax.psum_scatter(e_gain2, "ctx", scatter_dimension=0, tiled=True),
        lax.psum_scatter(e_wg, "ctx", scatter_dimension=0, tiled=True),
        lax.psum_scatter(e_wu, "ctx", scatter_dimension=0, tiled=True),
        lax.psum_scatter(e_wd, "ctx", scatter_dimension=0, tiled=True),
        lax.psum_scatter(grad_final, "ctx", scatter_dimension=0, tiled=True),
        lax.psum_scatter(d_gain1, "ctx", scatter_dimension=0, tiled=True),
        lax.psum_scatter(d_wq, "ctx", scatter_dimension=0, tiled=True),
        lax.psum_scatter(d_wk, "ctx", scatter_dimension=0, tiled=True),
        lax.psum_scatter(d_wv, "ctx", scatter_dimension=0, tiled=True),
        lax.psum_scatter(d_wo, "ctx", scatter_dimension=0, tiled=True),
        lax.psum_scatter(d_rel, "ctx", scatter_dimension=0, tiled=True),
        lax.psum_scatter(c_gain, "ctx", scatter_dimension=0, tiled=True),
        lax.psum_scatter(c_wq, "ctx", scatter_dimension=0, tiled=True),
        lax.psum_scatter(c_wk, "ctx", scatter_dimension=0, tiled=True),
        lax.psum_scatter(c_wv, "ctx", scatter_dimension=0, tiled=True),
        lax.psum_scatter(c_wo, "ctx", scatter_dimension=0, tiled=True),
        lax.psum_scatter(d_gain3, "ctx", scatter_dimension=0, tiled=True),
        lax.psum_scatter(d_wg, "ctx", scatter_dimension=0, tiled=True),
        lax.psum_scatter(d_wu, "ctx", scatter_dimension=0, tiled=True),
        lax.psum_scatter(d_wd, "ctx", scatter_dimension=0, tiled=True),
    )
    (
        s_gain1,
        s_wq,
        s_wk,
        s_wv,
        s_wo,
        s_rel,
        s_gain2,
        s_wg,
        s_wu,
        s_wd,
        s_final,
        t_gain1,
        t_wq,
        t_wk,
        t_wv,
        t_wo,
        t_rel,
        t_gain2,
        t_cq,
        t_ck,
        t_cv,
        t_co,
        t_gain3,
        t_wg,
        t_wu,
        t_wd,
    ) = shards
    reduced = (
        lax.psum(s_gain1.astype(jnp.bfloat16), "sp").astype(jnp.float32),
        lax.psum(s_wq.astype(jnp.bfloat16), "sp").astype(jnp.float32),
        lax.psum(s_wk.astype(jnp.bfloat16), "sp").astype(jnp.float32),
        lax.psum(s_wv.astype(jnp.bfloat16), "sp").astype(jnp.float32),
        lax.psum(s_wo.astype(jnp.bfloat16), "sp").astype(jnp.float32),
        lax.psum(s_rel.astype(jnp.bfloat16), "sp").astype(jnp.float32),
        lax.psum(s_gain2.astype(jnp.bfloat16), "sp").astype(jnp.float32),
        lax.psum(s_wg.astype(jnp.bfloat16), "sp").astype(jnp.float32),
        lax.psum(s_wu.astype(jnp.bfloat16), "sp").astype(jnp.float32),
        lax.psum(s_wd.astype(jnp.bfloat16), "sp").astype(jnp.float32),
        lax.psum(s_final.astype(jnp.bfloat16), "sp").astype(jnp.float32),
        lax.psum(t_gain1.astype(jnp.bfloat16), "sp").astype(jnp.float32),
        lax.psum(t_wq.astype(jnp.bfloat16), "sp").astype(jnp.float32),
        lax.psum(t_wk.astype(jnp.bfloat16), "sp").astype(jnp.float32),
        lax.psum(t_wv.astype(jnp.bfloat16), "sp").astype(jnp.float32),
        lax.psum(t_wo.astype(jnp.bfloat16), "sp").astype(jnp.float32),
        lax.psum(t_rel.astype(jnp.bfloat16), "sp").astype(jnp.float32),
        lax.psum(t_gain2.astype(jnp.bfloat16), "sp").astype(jnp.float32),
        lax.psum(t_cq.astype(jnp.bfloat16), "sp").astype(jnp.float32),
        lax.psum(t_ck.astype(jnp.bfloat16), "sp").astype(jnp.float32),
        lax.psum(t_cv.astype(jnp.bfloat16), "sp").astype(jnp.float32),
        lax.psum(t_co.astype(jnp.bfloat16), "sp").astype(jnp.float32),
        lax.psum(t_gain3.astype(jnp.bfloat16), "sp").astype(jnp.float32),
        lax.psum(t_wg.astype(jnp.bfloat16), "sp").astype(jnp.float32),
        lax.psum(t_wu.astype(jnp.bfloat16), "sp").astype(jnp.float32),
        lax.psum(t_wd.astype(jnp.bfloat16), "sp").astype(jnp.float32),
    )
    return (enc_result, dec_result, grad_enc, grad_dec) + tuple(reduced)


HG, CORE, SP = "hg", "core", "sp"
BLOCK_PAD = 128
VMEM_BYTES = 60 << 20


def nt(left, right):
    return lax.dot_general(left, right, (((1,), (1,)), ((), ())), preferred_element_type=jnp.float32)


def tn(left, right):
    return lax.dot_general(left, right, (((0,), (0,)), ((), ())), preferred_element_type=jnp.float32)


def nn(left, right):
    return jnp.dot(left, right, preferred_element_type=jnp.float32)


def low(value):
    return value.astype(jnp.bfloat16)


def identity(size):
    rows = lax.broadcasted_iota(jnp.int32, (size, size), 0)
    cols = lax.broadcasted_iota(jnp.int32, (size, size), 1)
    return low(jnp.where(rows == cols, 1.0, 0.0))


def only_lanes(array, first, count):
    lanes = lax.broadcasted_iota(jnp.int32, array.shape, 1)
    return jnp.where((lanes >= first) & (lanes < first + count), array, jnp.zeros_like(array))


def gelu_and_slope(v):
    scale, cubic = math.sqrt(2.0 / math.pi), 0.044715
    t = jnp.tanh(scale * (v + cubic * v * v * v))
    return 0.5 * v * (1.0 + t), 0.5 * (1.0 + t) + 0.5 * v * (1.0 - t * t) * scale * (1.0 + 3.0 * cubic * v * v)


def norm_back(x, g, dn):
    r = lax.rsqrt(jnp.mean(x * x, axis=-1, keepdims=True) + EPSILON)
    w = dn * g
    dx = r * w - x * (r * r * r) * jnp.mean(w * x, axis=-1, keepdims=True)
    return dx, jnp.sum(dn * x * r, axis=0, keepdims=True)


def send(src, dst, send_sem, recv_sem, to):
    copy = pltpu.make_async_remote_copy(
        src_ref=src, dst_ref=dst, send_sem=send_sem, recv_sem=recv_sem, device_id=to, device_id_type=pl.DeviceIdType.MESH
    )
    copy.start()
    return copy


def arrived(dst, send_sem, recv_sem, to):
    pltpu.make_async_remote_copy(
        src_ref=dst, dst_ref=dst, send_sem=send_sem, recv_sem=recv_sem, device_id=to, device_id_type=pl.DeviceIdType.MESH
    ).wait_recv()


class Place:
    def __init__(self, groups, cores, parts):
        self.groups, self.cores, self.parts = groups, cores, parts
        self.group, self.core, self.part = lax.axis_index(HG), lax.axis_index(CORE), lax.axis_index(SP)

    def ahead(self, step):
        return lax.rem(self.group + step, self.groups)

    def behind(self, step):
        return lax.rem(self.group + self.groups - step, self.groups)

    def chip(self, group):
        return (group, self.core, self.part)

    def sibling(self):
        return (self.group, 1 - self.core, self.part)

    def plane(self, step):
        return lax.rem(self.part + step, self.parts)

    def plane_behind(self, step):
        return lax.rem(self.part + self.parts - step, self.parts)

    def at_plane(self, part):
        return (self.group, self.core, part)

    def first_token(self, number, block):
        return pl.multiple_of(((self.cores * number + self.core) * self.parts + self.part) * block, block)

    def greet(self, planes=False):
        barrier = pltpu.get_barrier_semaphore()
        partners = [self.chip(self.ahead(step)) for step in range(1, self.groups)] + [self.sibling()]
        if planes:
            partners += [self.at_plane(self.plane(step)) for step in range(1, self.parts)]
        for partner in partners:
            pl.semaphore_signal(barrier, inc=1, device_id=partner, device_id_type=pl.DeviceIdType.MESH)
        pl.semaphore_wait(barrier, len(partners))


def spread_start(place, buf, sent, got):
    mine = buf.at[place.group]
    return [
        send(mine, mine, sent.at[step], got.at[step], place.chip(place.ahead(step))) for step in range(1, place.groups)
    ]


def spread_wait(place, buf, sent, got):
    for step in range(1, place.groups):
        source = place.behind(step)
        arrived(buf.at[source], sent.at[step], got.at[step], place.chip(source))


def collect_start(place, partial, out_buf, in_buf, sent, got):
    out_buf[...] = low(partial).reshape(out_buf.shape)
    pending = []
    for step in range(1, place.groups):
        to = place.ahead(step)
        pending.append(send(out_buf.at[to], in_buf.at[place.group], sent.at[step], got.at[step], place.chip(to)))
    return pending


def collect_wait(place, out_buf, in_buf, sent, got):
    total = out_buf[place.group].astype(jnp.float32)
    for step in range(1, place.groups):
        source = place.behind(step)
        arrived(in_buf.at[source], sent.at[step], got.at[step], place.chip(source))
        total = total + in_buf[source].astype(jnp.float32)
    return total


def all_rows(buf):
    return buf[...].reshape(buf.shape[0] * buf.shape[1], buf.shape[2])


DMA = pltpu.SemaphoreType.DMA
IN_VMEM = pl.BlockSpec(memory_space=pltpu.VMEM)
ANYWHERE = pl.BlockSpec(memory_space=pl.ANY)


class Recut:
    def __init__(self, sizes, col_packs, row_packs):
        groups, cores, _ = sizes
        self.cols, self.rows = len(col_packs), len(row_packs)
        self.operands = list(col_packs) + list(row_packs)
        self.in_specs = [ANYWHERE] * len(self.operands)
        self.outs = [((groups, cores) + w.shape[1:], w.dtype) for w in col_packs]
        self.outs += [((cores,) + w.shape, w.dtype) for w in row_packs]
        self.out_specs = [ANYWHERE] * len(self.outs)
        cols = (self.cols, groups)
        self.scratch = [DMA(cols)] * 4 + [DMA((self.rows,))] * 2 + [DMA((self.cols + self.rows,))]

    def bind(self, ins, outs, scratch):
        self.col_refs, self.row_refs = ins[: self.cols], ins[self.cols :]
        self.col_outs, self.row_outs = outs[: self.cols], outs[self.cols :]
        self.sems = scratch
        self.pending, self.copies = [], []

    def begin(self, place):
        sent, got, relay_sent, relay_got, pair_sent, pair_got, local = self.sems
        group, core = place.group, place.core
        for index, (ref, out) in enumerate(zip(self.col_refs, self.col_outs)):
            slot = out.at[group, core]
            for step in range(1, place.groups):
                to = place.ahead(step)
                self.pending.append(send(ref.at[to], slot, sent.at[index, step], got.at[index, step], place.chip(to)))
            self.pending.append(send(ref.at[group], slot, relay_sent.at[index, 0], relay_got.at[index, 0], place.sibling()))
            self.copies.append(pltpu.make_async_copy(ref.at[group], slot, local.at[index]))
        for index, (ref, out) in enumerate(zip(self.row_refs, self.row_outs)):
            slot = out.at[core]
            self.pending.append(send(ref, slot, pair_sent.at[index], pair_got.at[index], place.sibling()))
            self.copies.append(pltpu.make_async_copy(ref, slot, local.at[self.cols + index]))
        for copy in self.copies:
            copy.start()

    def middle(self, place):
        sent, got, relay_sent, relay_got = self.sems[:4]
        for index, out in enumerate(self.col_outs):
            for step in range(1, place.groups):
                source = place.behind(step)
                slot = out.at[source, place.core]
                arrived(slot, sent.at[index, step], got.at[index, step], place.chip(source))
                self.pending.append(
                    send(slot, slot, relay_sent.at[index, step], relay_got.at[index, step], place.sibling())
                )

    def end(self, place):
        _, _, relay_sent, relay_got, pair_sent, pair_got, _ = self.sems
        for index, out in enumerate(self.col_outs):
            for step in range(place.groups):
                slot = out.at[place.behind(step), 1 - place.core]
                arrived(slot, relay_sent.at[index, step], relay_got.at[index, step], place.sibling())
        for index, out in enumerate(self.row_outs):
            arrived(out.at[1 - place.core], pair_sent.at[index], pair_got.at[index], place.sibling())
        for copy in self.copies:
            copy.wait()
        for copy in self.pending:
            copy.wait_send()

    def result(self, got):
        cols = [w.reshape(w.shape[0] * w.shape[1] * w.shape[2], w.shape[3]) for w in got[: self.cols]]
        return cols, [w.reshape(w.shape[0] * w.shape[1], w.shape[2]) for w in got[self.cols :]]


class GiveRows:
    def __init__(self, sizes, col_grads, row_grads):
        groups, cores, _ = sizes
        self.cols, self.rows = len(col_grads), len(row_grads)
        col_in = [w.reshape(groups, cores, w.shape[0] // (groups * cores), w.shape[1]) for w in col_grads]
        row_in = [w.reshape(cores, w.shape[0] // cores, w.shape[1]) for w in row_grads]
        self.operands = col_in + row_in
        self.in_specs = [IN_VMEM] * len(self.operands)
        own = [(groups,) + w.shape[2:] for w in col_in] + [(1,) + w.shape[1:] for w in row_in]
        self.outs = [(shape, jnp.bfloat16) for shape in own]
        self.out_specs = [IN_VMEM] * len(self.outs)
        self.scratch = [pltpu.VMEM(shape, jnp.bfloat16) for shape in own + own[: self.cols]]
        self.scratch += [DMA((self.cols, groups))] * 4 + [DMA((self.rows,))] * 2

    def bind(self, ins, outs, scratch):
        self.col_refs, self.row_refs = ins[: self.cols], ins[self.cols :]
        self.col_outs, self.row_outs = outs[: self.cols], outs[self.cols :]
        self.col_sibs, scratch = scratch[: self.cols], scratch[self.cols :]
        self.row_sibs, scratch = scratch[: self.rows], scratch[self.rows :]
        self.col_sums, self.sems = scratch[: self.cols], scratch[self.cols :]
        self.pending = []

    def begin(self, place):
        _, _, pair_sent, pair_got, row_sent, row_got = self.sems
        other = 1 - place.core
        for index, (ref, sib) in enumerate(zip(self.col_refs, self.col_sibs)):
            for step in range(place.groups):
                to = place.ahead(step)
                self.pending.append(
                    send(
                        ref.at[to, other], sib.at[to],
                        pair_sent.at[index, step], pair_got.at[index, step], place.sibling(),
                    )
                )
        for index, (ref, sib) in enumerate(zip(self.row_refs, self.row_sibs)):
            self.pending.append(send(ref.at[other], sib.at[0], row_sent.at[index], row_got.at[index], place.sibling()))

    def middle(self, place):
        sent, got, pair_sent, pair_got, row_sent, row_got = self.sems
        core = place.core
        for index, (ref, sib) in enumerate(zip(self.col_refs, self.col_sibs)):
            out, sums = self.col_outs[index], self.col_sums[index]
            for step in list(range(1, place.groups)) + [0]:
                to = place.ahead(step)
                arrived(sib.at[to], pair_sent.at[index, step], pair_got.at[index, step], place.sibling())
                both = low(ref[to, core].astype(jnp.float32) + sib[to].astype(jnp.float32))
                if step:
                    sums[to] = both
                    self.pending.append(
                        send(sums.at[to], out.at[place.group], sent.at[index, step], got.at[index, step], place.chip(to))
                    )
                else:
                    out[place.group] = both
        for index, (ref, sib) in enumerate(zip(self.row_refs, self.row_sibs)):
            arrived(sib.at[0], row_sent.at[index], row_got.at[index], place.sibling())
            self.row_outs[index][0] = low(ref[core].astype(jnp.float32) + sib[0].astype(jnp.float32))

    def end(self, place):
        sent, got = self.sems[:2]
        for index, out in enumerate(self.col_outs):
            for step in range(1, place.groups):
                source = place.behind(step)
                arrived(out.at[source], sent.at[index, step], got.at[index, step], place.chip(source))
        for copy in self.pending:
            copy.wait_send()

    def result(self, got):
        return list(got)


FOLD_PIECE = 56 * 1024


class FoldPlanes:
    def __init__(self, arrays):
        self.operands = list(arrays)
        self.in_specs = [IN_VMEM] * len(arrays)
        self.outs = [(w.shape, jnp.bfloat16) for w in arrays]
        self.out_specs = [IN_VMEM] * len(arrays)
        self.pieces = []
        for index, w in enumerate(arrays):
            cuts = next(c for c in (1, 2, 3, 4, 6, 8) if w.shape[1] // c * w.shape[2] <= FOLD_PIECE or c == 8)
            if w.shape[0] * w.shape[1] * w.shape[2] <= FOLD_PIECE:
                self.pieces.append((index, slice(None), pl.ds(0, w.shape[1])))
                continue
            rows = w.shape[1] // cuts
            self.pieces += [(index, lead, pl.ds(c * rows, rows)) for lead in range(w.shape[0]) for c in range(cuts)]
        self.inner_done = self.across_done = 0
        self.scratch = [pltpu.VMEM(w.shape, jnp.bfloat16) for _ in range(3) for w in arrays] + [DMA((len(self.pieces),))] * 6

    def bind(self, ins, outs, scratch):
        count = len(self.outs)
        self.ins, self.totals = ins, outs
        self.inner, self.sums, self.across = (scratch[i * count : (i + 1) * count] for i in range(3))
        self.sems = scratch[3 * count :]

    def copy(self, hop, number, src, dst, to):
        return pltpu.make_async_remote_copy(
            src_ref=src, dst_ref=dst, send_sem=self.sems[2 * hop].at[number], recv_sem=self.sems[2 * hop + 1].at[number],
            device_id=to, device_id_type=pl.DeviceIdType.MESH,
        )

    def hops(self, place, number):
        index, lead, rows = self.pieces[number]
        part = place.part
        inward, across, outward = (place.at_plane(p) for p in (1 + part // 3, 3 - part, 3 * (part - 1)))
        ref, inner, sums, other, total = (
            side[index].at[lead, rows] for side in (self.ins, self.inner, self.sums, self.across, self.totals)
        )
        return (ref, inner, inward), (sums, other, across), (total, total, outward)

    def roles(self, place):
        middle = (place.part == 1) | (place.part == 2)
        return pl.when(middle), pl.when(jnp.logical_not(middle))

    def start(self, place, numbers):
        @self.roles(place)[1]
        def _():
            for number in numbers:
                self.copy(0, number, *self.hops(place, number)[0]).start()

    def add_inner(self, place, number):
        inward, across, _ = self.hops(place, number)
        self.copy(0, number, *inward).wait_recv()
        across[0][...] = low(inward[0][...].astype(jnp.float32) + inward[1][...].astype(jnp.float32))
        self.copy(1, number, *across).start()

    def add_across(self, place, number):
        _, across, outward = self.hops(place, number)
        self.copy(1, number, *across).wait_recv()
        outward[0][...] = low(across[0][...].astype(jnp.float32) + across[1][...].astype(jnp.float32))
        self.copy(2, number, *outward).start()

    def of(self, first, last):
        return [n for n, piece in enumerate(self.pieces) if first <= piece[0] < last]

    def serve(self, place, inner, across):
        inners = list(range(self.inner_done, min(self.inner_done + inner, len(self.pieces))))
        self.inner_done += len(inners)
        others = list(range(self.across_done, min(self.across_done + across, len(self.pieces))))
        self.across_done += len(others)

        @self.roles(place)[0]
        def _():
            for turn in range(max(len(inners), len(others))):
                if turn < len(inners):
                    self.add_inner(place, inners[turn])
                if turn < len(others):
                    self.add_across(place, others[turn])

    def finish(self, place, lag):
        left = len(self.pieces) - self.inner_done
        behind = self.inner_done - self.across_done
        if behind > lag:
            self.serve(place, 0, behind - lag)
        self.serve(place, lag - min(behind, lag), 0)
        self.serve(place, left, left)
        self.serve(place, 0, len(self.pieces))

    def end(self, place):
        in_middle, at_end = self.roles(place)

        @at_end
        def _():
            for number in range(len(self.pieces)):
                inward, _, outward = self.hops(place, number)
                self.copy(0, number, *inward).wait_send()
                self.copy(2, number, *outward).wait_recv()

        @in_middle
        def _():
            for number in range(len(self.pieces)):
                _, across, outward = self.hops(place, number)
                self.copy(1, number, *across).wait_send()
                self.copy(2, number, *outward).wait_send()

    def result(self, got):
        return list(got)


def stage(sizes, collective_id, kernel, operands, outs, scratch, copies, job=None):
    jobs = [] if job is None else [job]
    allocated = [pltpu.VMEM(s, jnp.bfloat16) if isinstance(s, tuple) else s for s in scratch]
    if copies is not None:
        allocated += [DMA(copies), DMA(copies)]
    counts = (len(operands), len(outs), len(allocated))
    job_ins, job_outs = [len(j.operands) for j in jobs], [len(j.outs) for j in jobs]

    def body(*refs):
        refs = list(refs)

        def take(count):
            taken, refs[:] = refs[:count], refs[count:]
            return taken

        own_ins, their_ins = take(counts[0]), [take(n) for n in job_ins]
        own_outs, their_outs = take(counts[1]), [take(n) for n in job_outs]
        own_scratch, their_scratch = take(counts[2]), [take(len(j.scratch)) for j in jobs]
        for j, i, o, s in zip(jobs, their_ins, their_outs, their_scratch):
            j.bind(i, o, s)
        place = Place(*sizes)

        def run(step):
            for j in jobs:
                getattr(j, step)(place)

        kernel(place, run, *own_ins, *own_outs, *own_scratch)

    all_outs = list(outs) + [o for j in jobs for o in j.outs]
    got = pl.pallas_call(
        body,
        out_shape=tuple(jax.ShapeDtypeStruct(shape, dtype) for shape, dtype in all_outs),
        in_specs=[IN_VMEM] * counts[0] + [s for j in jobs for s in j.in_specs],
        out_specs=tuple([IN_VMEM] * counts[1] + [s for j in jobs for s in j.out_specs]),
        scratch_shapes=allocated + [s for j in jobs for s in j.scratch],
        compiler_params=pltpu.CompilerParams(collective_id=collective_id, has_side_effects=True, vmem_limit_bytes=VMEM_BYTES),
        cost_estimate=pl.CostEstimate(flops=20_000_000_000, bytes_accessed=10_000_000, transcendentals=0),
    )(*operands, *[w for j in jobs for w in j.operands])
    return got[: counts[1]], (None if job is None else job.result(got[counts[1] :]))


def job_alone_kernel(place, run):
    place.greet()
    run("begin")
    run("middle")
    run("end")


def job_alone(sizes, collective_id, job):
    return stage(sizes, collective_id, job_alone_kernel, [], [], [], None, job)[1]


def feed_forward_kernel(gain_at, final_at, place, run, x_ref, gains_ref, gu_ref, down_ref, y_ref, last_ref, n_ref, n_buf, p_buf, r_buf, sent, got):
    place.greet()
    x = x_ref[...]
    n_buf[place.group] = low(rms_norm(x, gains_ref[gain_at]))
    pending = spread_start(place, n_buf, sent.at[0], got.at[0])
    run("begin")
    spread_wait(place, n_buf, sent.at[0], got.at[0])
    n = all_rows(n_buf)
    hidden = down_ref.shape[0]
    gu = nn(n, gu_ref[...])
    h = low(gelu_and_slope(gu[:, :hidden])[0] * gu[:, hidden:])
    pending += collect_start(place, nn(h, down_ref[...]), p_buf, r_buf, sent.at[1], got.at[1])
    n_ref[...] = n
    run("middle")
    y = x + collect_wait(place, p_buf, r_buf, sent.at[1], got.at[1])
    y_ref[...] = y
    last_ref[...] = low(rms_norm(y, gains_ref[final_at]))
    run("end")
    for copy in pending:
        copy.wait_send()


def feed_back_part(n, dyb, gu_ref, down_ref):
    hidden = down_ref.shape[0]
    gu = nn(n, gu_ref[...])
    g, u = gu[:, :hidden], gu[:, hidden:]
    act, slope = gelu_and_slope(g)
    dh = nt(dyb, down_ref[...])
    return low(act * u), jnp.concatenate([low(dh * u * slope), low(dh * act)], axis=1)


def feed_both_kernel(
    sizes, gain_at, give, x_ref, cot_ref, gains_ref, gu_ref, down_ref,
    y_ref, dx_ref, dgain_ref, cols_ref, rows_ref,
    n_buf, d_buf, py_buf, ry_buf, pn_buf, rn_buf, dgu_buf, ddown_buf, sent, got, *give_scratch,
):
    place = Place(*sizes)
    give.bind([dgu_buf, ddown_buf], [cols_ref, rows_ref], give_scratch)
    place.greet()
    x = x_ref[...]
    d_buf[place.group] = cot_ref[...]
    pending = spread_start(place, d_buf, sent.at[1], got.at[1])
    n_buf[place.group] = low(rms_norm(x, gains_ref[gain_at]))
    pending += spread_start(place, n_buf, sent.at[0], got.at[0])
    spread_wait(place, d_buf, sent.at[1], got.at[1])
    spread_wait(place, n_buf, sent.at[0], got.at[0])
    n, dyb = all_rows(n_buf), all_rows(d_buf)
    h, dgu = feed_back_part(n, dyb, gu_ref, down_ref)
    pending += collect_start(place, nt(dgu, gu_ref[...]), pn_buf, rn_buf, sent.at[2], got.at[2])
    dgu_buf[...] = low(tn(n, dgu)).reshape(dgu_buf.shape)
    ddown_buf[...] = low(tn(h, dyb)).reshape(ddown_buf.shape)
    give.begin(place)
    pending += collect_start(place, nn(h, down_ref[...]), py_buf, ry_buf, sent.at[3], got.at[3])
    dn = collect_wait(place, pn_buf, rn_buf, sent.at[2], got.at[2])
    give.middle(place)
    back, dgain = norm_back(x, gains_ref[gain_at], dn)
    dx_ref[...] = cot_ref[...].astype(jnp.float32) + back
    dgain_ref[...] = dgain
    y_ref[...] = x + collect_wait(place, py_buf, ry_buf, sent.at[3], got.at[3])
    give.end(place)
    for copy in pending:
        copy.wait_send()


def bias_mask(place, block, causal, rel_ref, turn_ref, kdoc_ref, qdoc_ref, out_ref):
    heads, rows_total, lanes = out_ref.shape
    key_len = kdoc_ref.shape[0]
    strip = block + 2 * BLOCK_PAD
    query = lax.broadcasted_iota(jnp.int32, (1, lanes), 1)
    start = ((place.cores * (query // block) + place.core) * place.parts + place.part) * block
    allowed = kdoc_ref[...] == qdoc_ref[...]
    if causal:
        places = lax.broadcasted_iota(jnp.int32, (key_len, lanes), 0)
        allowed = allowed & (places <= start + query % block)
    inside = pl.ds(BLOCK_PAD, key_len)
    if rel_ref is None:
        out_ref[0, inside, :] = low(jnp.where(allowed, 0.0, NEGATIVE))
        return
    by_head = tn(rel_ref[...], turn_ref[...])
    width = by_head.shape[1]
    pick_rows = lax.broadcasted_iota(jnp.int32, (8, by_head.shape[0]), 0)
    pick_cols = lax.broadcasted_iota(jnp.int32, (8, by_head.shape[0]), 1)
    picked = nn(low(jnp.where(pick_cols == pick_rows + place.group * heads, 1.0, 0.0)), low(by_head))
    places = lax.broadcasted_iota(jnp.int32, (rows_total, lanes), 0)
    for head in range(heads):
        row = picked[head : head + 1, :]
        left, right = row[:, width - 2 : width - 1], row[:, 0:1]
        out_ref[head] = low(jnp.where(places < start, left, right))
        wide = jnp.broadcast_to(row, (strip, width))
        for number in range(lanes // block):
            at = (number * block) % 128
            turned = pltpu.roll(wide, (width - (strip - 1) + at) % width, 1, stride=1, stride_axis=0)
            rows = pl.ds(place.first_token(number, block), strip)
            out_ref[head, rows, number * block : (number + 1) * block] = low(turned[:, at : at + block])
        out_ref[head, inside, :] = low(jnp.where(allowed, out_ref[head, inside, :].astype(jnp.float32), NEGATIVE))


def chunk_rows(kv_ref):
    return kv_ref.shape[1] * kv_ref.shape[2] * kv_ref.shape[3]


def key_side(kv_ref, chunk):
    return kv_ref[chunk].reshape(chunk_rows(kv_ref), kv_ref.shape[4])[:, : kv_ref.shape[4] // 2]


def value_side(kv_ref, chunk):
    lanes = kv_ref.shape[4]
    return kv_ref[chunk].reshape(chunk_rows(kv_ref), lanes)[:, lanes // 2 // 128 * 128 :]


def bias_rows(bm_ref, head, chunk, rows):
    at = pl.multiple_of(BLOCK_PAD + chunk * rows, 128)
    return bm_ref[head if bm_ref.shape[0] > 1 else 0, pl.ds(at, rows), :].astype(jnp.float32)


def mix_part(q, kv_ref, bm_ref, o_ref, lse_ref, s_ref, ot_ref):
    chunks, rows = kv_ref.shape[0], chunk_rows(kv_ref)
    queries, width = q.shape
    heads = width // HD
    across = [slice(head * queries, (head + 1) * queries) for head in range(heads)]
    masked_q = [only_lanes(q, head * HD, HD) for head in range(heads)]

    def first(chunk, tops):
        keys = key_side(kv_ref, chunk)
        inside = pl.ds(pl.multiple_of(chunk * rows, rows), rows)
        new = []
        for head in range(heads):
            scores = nt(keys, masked_q[head]) + bias_rows(bm_ref, head, chunk, rows)
            s_ref[inside, across[head]] = scores
            new.append(jnp.maximum(tops[head], jnp.max(scores, axis=0, keepdims=True)))
        return tuple(new)

    tops = lax.fori_loop(0, chunks, first, (jnp.full((1, queries), NEGATIVE, jnp.float32),) * heads)

    def second(chunk, carried):
        values = value_side(kv_ref, chunk)
        inside = pl.ds(pl.multiple_of(chunk * rows, rows), rows)
        lead = values.shape[1] - width
        values_t = low(nt(identity(values.shape[1]), values))
        new = []
        for head in range(heads):
            total, mixed = carried[head]
            weights = jnp.exp(s_ref[inside, across[head]] - tops[head])
            mixed = mixed + nn(values_t[lead + head * HD : lead + (head + 1) * HD], low(weights))
            new.append((total + jnp.sum(weights, axis=0, keepdims=True), mixed))
        return tuple(new)

    start = (jnp.zeros((1, queries), jnp.float32), jnp.zeros((HD, queries), jnp.float32))
    done = lax.fori_loop(0, chunks, second, (start,) * heads)
    for head in range(heads):
        total, mixed = done[head]
        lse_ref[:, across[head]] = tops[head] + jnp.log(total)
        ot_ref[head * HD : (head + 1) * HD, :] = low(mixed / total)
    o_ref[...] = low(nt(identity(queries), ot_ref[...]))


def keys_send(place, kv_ref, base, sent, got):
    mine = kv_ref.at[:, place.core, place.part]
    pending = [
        send(mine, mine, sent.at[base, step], got.at[base, step], place.at_plane(place.plane(step)))
        for step in range(1, place.parts)
    ]
    pending.append(send(mine, mine, sent.at[base + 1, 0], got.at[base + 1, 0], place.sibling()))
    return pending


def keys_relay(place, kv_ref, base, sent, got):
    pending = []
    for step in range(1, place.parts):
        source = place.plane_behind(step)
        slot = kv_ref.at[:, place.core, source]
        arrived(slot, sent.at[base, step], got.at[base, step], place.at_plane(source))
        pending.append(send(slot, slot, sent.at[base + 1, step], got.at[base + 1, step], place.sibling()))
    return pending


def keys_wait(place, kv_ref, base, sent, got):
    for step in range(place.parts):
        slot = kv_ref.at[:, 1 - place.core, place.plane_behind(step)]
        arrived(slot, sent.at[base + 1, step], got.at[base + 1, step], place.sibling())


def attend_kernel(crosses, gain_at, place, run, *refs):
    refs = list(refs)

    def take(count):
        taken, refs[:] = refs[:count], refs[count:]
        return taken

    count = len(crosses)
    ins = [take(7 if cross else 8) for cross in crosses]
    outs = [take(8 if cross else 7) for cross in crosses]
    s_ref, ot_ref = take(2)
    bufs = [take(4 if cross else 3) for cross in crosses]
    sent, got = take(2)
    place.greet(planes=True)
    pending = []
    for index, cross in enumerate(crosses):
        x_ref, gain_ref = ins[index][0], ins[index][1]
        if cross:
            bufs[index][3][place.group] = ins[index][6][...]
            pending += spread_start(place, bufs[index][3], sent.at[5 * index + 4], got.at[5 * index + 4])
        bufs[index][0][place.group] = low(rms_norm(x_ref[...].astype(jnp.float32), gain_ref[gain_at[index]]))
        pending += spread_start(place, bufs[index][0], sent.at[5 * index], got.at[5 * index])
    for index, cross in enumerate(crosses):
        w_ref, kv_ref = ins[index][2], outs[index][3]
        kv_width = kv_ref.shape[4]
        n_buf = bufs[index][0]
        if cross:
            source = bufs[index][3]
            spread_wait(place, source, sent.at[5 * index + 4], got.at[5 * index + 4])
            kv = low(nn(all_rows(source), w_ref[:, :kv_width]))
            outs[index][7][...] = all_rows(source)
        else:
            spread_wait(place, n_buf, sent.at[5 * index], got.at[5 * index])
            both = low(nn(all_rows(n_buf), w_ref[...]))
            kv, q = both[:, :kv_width], both[:, kv_width:]
        kv_ref[:, place.core, place.part] = kv.reshape(kv_ref.shape[0], kv_ref.shape[3], kv_width)
        pending += keys_send(place, kv_ref, 5 * index + 1, sent, got)
        if cross:
            spread_wait(place, n_buf, sent.at[5 * index], got.at[5 * index])
            q = low(nn(all_rows(n_buf), w_ref[:, kv_width:]))
        outs[index][1][...] = all_rows(n_buf)
        outs[index][2][...] = q
    run("begin")
    for index, cross in enumerate(crosses):
        block = ins[index][0].shape[0]
        kdoc_ref, qdoc_ref = ins[index][4:6]
        rel_ref, turn_ref = (None, None) if cross else [r.at[index] for r in ins[index][6:8]]
        bias_mask(place, block, index == count - 1 and not cross, rel_ref, turn_ref, kdoc_ref, qdoc_ref, outs[index][6])
    for index in range(count):
        wo_ref = ins[index][3]
        kv_ref, o_ref, lse_ref, bm_ref = outs[index][3:7]
        pending += keys_relay(place, kv_ref, 5 * index + 1, sent, got)
        keys_wait(place, kv_ref, 5 * index + 1, sent, got)
        mix_part(outs[index][2][...], kv_ref, bm_ref, o_ref, lse_ref, s_ref, ot_ref)
        share = nn(o_ref[...], wo_ref[...])
        pending += collect_start(place, share, bufs[index][1], bufs[index][2], sent.at[5 * index + 3], got.at[5 * index + 3])
        if index == 0:
            run("middle")
    for index in range(count):
        total = collect_wait(place, bufs[index][1], bufs[index][2], sent.at[5 * index + 3], got.at[5 * index + 3])
        outs[index][0][...] = ins[index][0][...].astype(jnp.float32) + total
    run("end")
    for copy in pending:
        copy.wait_send()


def attend(sizes, collective_id, gain_at, layers, job=None):
    groups, cores, parts = sizes
    operands, outs, scratch, crosses = [], [], [], []
    f32, bf16 = jnp.float32, jnp.bfloat16
    for layer in layers:
        x, wo = layer[0], layer[3]
        cross = len(layer) == 7
        block, model = x.shape
        width = wo.shape[0]
        tokens = groups * block
        keys = cores * parts * tokens
        operands += layer
        outs += [
            ((block, model), f32), ((tokens, model), bf16), ((tokens, width), bf16),
            ((groups, cores, parts, block, 2 * width), bf16), ((tokens, width), bf16), ((1, width // HD * tokens), f32),
            ((1 if cross else width // HD, keys + 2 * BLOCK_PAD, tokens), bf16),
        ]
        if cross:
            outs.append(((tokens, model), bf16))
        scratch += [(groups, block, model)] * (4 if cross else 3)
        crosses.append(cross)
    first = [pltpu.VMEM((keys, width // HD * tokens), f32), (width, tokens)]
    copies = (5 * len(layers), max(groups, parts))
    got, given = stage(
        sizes, collective_id, functools.partial(attend_kernel, crosses, gain_at), operands, outs, first + scratch, copies, job
    )
    results, at = [], 0
    for cross in crosses:
        size = 8 if cross else 7
        results.append(tuple(got[at : at + size]) + (() if cross else (None,)))
        at += size
    return results, given


def mix_back_part(place, q, do, o, kv_ref, lse_ref, bm_ref, dkv_ref, ds_ref):
    chunks, cores, parts, block, lanes = kv_ref.shape
    rows = chunk_rows(kv_ref)
    queries, width = q.shape
    heads = width // HD
    strip = block + 2 * BLOCK_PAD
    first_value = width // 128 * 128
    lead = width - first_value
    do_wide = jnp.concatenate([jnp.zeros((queries, lead), do.dtype), do], axis=1) if lead else do
    across = [slice(head * queries, (head + 1) * queries) for head in range(heads)]
    masked_q = [only_lanes(q, head * HD, HD) for head in range(heads)]
    masked_do = [only_lanes(do_wide, lead + head * HD, HD) for head in range(heads)]
    q_wide = masked_q
    if lead:
        none = jnp.zeros((queries, lead), q.dtype)
        q_wide = [jnp.concatenate([one, none], axis=1) for one in masked_q]
    of_head = lax.broadcasted_iota(jnp.int32, (8, width), 1) // HD
    of_row = lax.broadcasted_iota(jnp.int32, (8, width), 0)
    inners = lax.dot_general(
        jnp.where(of_head == of_row, 1.0, 0.0), do.astype(jnp.float32) * o.astype(jnp.float32),
        (((1,), (1,)), ((), ())), precision=HIGHEST, preferred_element_type=jnp.float32,
    )
    nothing = jnp.zeros((1, queries), jnp.float32)
    if ds_ref is not None:
        empty = jnp.zeros((BLOCK_PAD, heads * queries), jnp.bfloat16)
        ds_ref[0:BLOCK_PAD, :] = empty
        ds_ref[BLOCK_PAD + chunks * rows :, :] = empty
        of_lane = lax.broadcasted_iota(jnp.int32, (1, queries), 1) // block
        lane_start = ((cores * of_lane + place.core) * parts + place.part) * block

    def chunk_step(chunk, carried):
        at = pl.multiple_of(chunk * rows, rows)
        keys, values = key_side(kv_ref, chunk), value_side(kv_ref, chunk)
        keys_t = low(nt(identity(width), keys))
        new, dk, dv = [], None, None
        for head in range(heads):
            left, right, back = carried[head]
            scores = nt(keys, masked_q[head]) + bias_rows(bm_ref, head, chunk, rows)
            p = jnp.exp(scores - lse_ref[:, across[head]])
            dp = nt(values, masked_do[head])
            ds = low(p * (dp - inners[head : head + 1, :]))
            if ds_ref is not None:
                ds_ref[pl.ds(pl.multiple_of(BLOCK_PAD + at, 128), rows), across[head]] = ds
                wide = ds.astype(jnp.float32)
                places = lax.broadcasted_iota(jnp.int32, wide.shape, 0) + (at + BLOCK_PAD)
                left = left + jnp.sum(jnp.where(places < lane_start, wide, 0.0), axis=0, keepdims=True)
                right = right + jnp.sum(jnp.where(places >= lane_start + strip, wide, 0.0), axis=0, keepdims=True)
            back = back + nn(keys_t[head * HD : (head + 1) * HD], ds)
            new.append((left, right, back))
            more_k, more_v = nn(ds, q_wide[head]), nn(low(p), masked_do[head])
            dk, dv = (more_k, more_v) if dk is None else (dk + more_k, dv + more_v)
        if lead:
            shared = dk[:, first_value:] + dv[:, : 2 * lead]
            both = jnp.concatenate([dk[:, :first_value], shared, dv[:, 2 * lead :]], axis=1)
        else:
            both = jnp.concatenate([dk, dv], axis=1)
        dkv_ref[chunk] = low(both).reshape(dkv_ref.shape[1:])
        return tuple(new)

    start = (nothing, nothing, jnp.zeros((HD, queries), jnp.float32))
    done = lax.fori_loop(0, chunks, chunk_step, (start,) * heads)
    return [one[2] for one in done], [one[:2] for one in done]


def table_grads(place, block, done, ds_ref, ahead_ref, rel_ref):
    queries = done[0][0].shape[1]
    width = ahead_ref.shape[1]
    strip = block + 2 * BLOCK_PAD
    rows = lax.broadcasted_iota(jnp.int32, (block, block), 0)
    cols = lax.broadcasted_iota(jnp.int32, (block, block), 1)
    backwards = jnp.where(rows + cols == block - 1, 1.0, 0.0)
    at = lax.broadcasted_iota(jnp.int32, (1, width), 1)
    sums = []
    for head, (left, right) in enumerate(done):
        total = jnp.zeros((strip, block), jnp.float32)
        for number in range(queries // block):
            low_at = head * queries + number * block
            near = pl.ds(place.first_token(number, block), strip)
            total = total + ds_ref[near, low_at : low_at + block].astype(jnp.float32)
        turned = lax.dot_general(
            backwards, total, (((1,), (1,)), ((), ())), precision=HIGHEST, preferred_element_type=jnp.float32
        )
        turned = jnp.concatenate([turned, jnp.zeros((block, width - strip), jnp.float32)], axis=1)
        by_distance = jnp.sum(pltpu.roll(turned, 0, 1, stride=1, stride_axis=0), axis=0, keepdims=True)
        left, right = (jnp.sum(side, axis=1, keepdims=True) for side in (left, right))
        sums.append(by_distance + jnp.where(at == 0, left, 0.0) + jnp.where(at == width - 2, right, 0.0))
    sums = jnp.concatenate(sums + [jnp.zeros((8 - len(sums), width), jnp.float32)], axis=0)
    by_bucket = lax.dot_general(
        sums, ahead_ref[...], (((1,), (1,)), ((), ())), precision=HIGHEST, preferred_element_type=jnp.float32
    )
    head_rows = lax.broadcasted_iota(jnp.int32, (8, 128), 0)
    head_lanes = lax.broadcasted_iota(jnp.int32, (8, 128), 1)
    lanes_of = (head_lanes == head_rows + place.group * len(done)) & (head_rows < len(done))
    rel_ref[...] = lax.dot_general(
        by_bucket, jnp.where(lanes_of, 1.0, 0.0), (((0,), (0,)), ((), ())), precision=HIGHEST, preferred_element_type=jnp.float32
    )


class AttendBack:
    OPERANDS = 11

    def __init__(self, place, ins, grads, scratch, cross):
        self.place, self.cross = place, cross
        self.x, self.n, self.q, self.kv, self.o, self.lse, self.w, self.wo, self.bm, self.source, self.ahead = ins
        self.dw, self.dwo = grads
        self.dkv, self.sib, self.zout, self.zin, self.d_buf, self.pn, self.rn, self.dq = scratch[:8]
        scratch = scratch[8:]
        self.pm, self.rm = (scratch.pop(0), scratch.pop(0)) if cross else (None, None)
        self.ds = None if cross else scratch.pop(0)
        self.sent, self.got = scratch
        self.kv_width = self.kv.shape[4]
        self.pending = []

    def begin(self, dy):
        self.d_buf[self.place.group] = low(dy)
        self.pending += spread_start(self.place, self.d_buf, self.sent.at[0], self.got.at[0])

    def arrive(self):
        spread_wait(self.place, self.d_buf, self.sent.at[0], self.got.at[0])

    def compute(self):
        place, sent, got = self.place, self.sent, self.got
        do = low(nt(all_rows(self.d_buf), self.wo[...]))
        back, self.edges = mix_back_part(
            place, self.q[...], do, self.o[...], self.kv, self.lse, self.bm, self.dkv, self.ds
        )
        self.pending.append(
            send(self.dkv.at[:, 1 - place.core], self.sib, sent.at[1, 0], got.at[1, 0], place.sibling())
        )
        self.dq[...] = low(nt(identity(self.q.shape[0]), low(jnp.concatenate(back, axis=0))))
        if self.cross:
            share = nt(self.dq[...], self.w[:, self.kv_width :])
            self.pending += collect_start(place, share, self.pn, self.rn, sent.at[3], got.at[3])

    def exchange(self):
        place, sent, got = self.place, self.sent, self.got
        arrived(self.sib, sent.at[1, 0], got.at[1, 0], place.sibling())
        for step in list(range(1, place.parts)) + [0]:
            to = place.plane(step)
            self.zout[to] = low(self.dkv[:, place.core, to].astype(jnp.float32) + self.sib[:, to].astype(jnp.float32))
            if step:
                self.pending.append(
                    send(self.zout.at[to], self.zin.at[place.part], sent.at[2, step], got.at[2, step], place.at_plane(to))
                )

    def by_rows(self, grad):
        return low(grad).reshape(self.dw.shape[:3] + grad.shape[1:])

    def query_grads(self, rel):
        self.dwo[...] = low(tn(self.o[...], all_rows(self.d_buf))).reshape(self.dwo.shape)
        self.dw[:, :, :, self.kv_width :] = self.by_rows(tn(self.n[...], self.dq[...]))
        if not self.cross:
            table_grads(self.place, self.x.shape[0], self.edges, self.ds, self.ahead, rel)

    def keys(self):
        place, sent, got = self.place, self.sent, self.got
        total = self.zout[place.part].astype(jnp.float32)
        for step in range(1, place.parts):
            source = place.plane_behind(step)
            arrived(self.zin.at[source], sent.at[2, step], got.at[2, step], place.at_plane(source))
            total = total + self.zin[source].astype(jnp.float32)
        self.dkv_own = low(total).reshape(self.q.shape[0], self.kv_width)
        share = nt(self.dkv_own, self.w[:, : self.kv_width])
        if self.cross:
            self.pending += collect_start(place, share, self.pm, self.rm, sent.at[4], got.at[4])
        else:
            share = share + nt(self.dq[...], self.w[:, self.kv_width :])
            self.pending += collect_start(place, share, self.pn, self.rn, sent.at[3], got.at[3])

    def key_grads(self):
        self.dw[:, :, :, : self.kv_width] = self.by_rows(tn(self.source[...], self.dkv_own))

    def source_grad(self):
        return collect_wait(self.place, self.pm, self.rm, self.sent.at[4], self.got.at[4])

    def normed_grad(self):
        return collect_wait(self.place, self.pn, self.rn, self.sent.at[3], self.got.at[3])

    def wait(self):
        for copy in self.pending:
            copy.wait_send()


def attend_back_scratch(sizes, kv, block, model, width, cross):
    groups, cores, parts = sizes
    tokens = groups * block
    turned, buffer = (parts, groups, block, 2 * width), (groups, block, model)
    shapes = [kv, (groups, parts, block, 2 * width), turned, turned, buffer, buffer, buffer, (tokens, width)]
    if cross:
        shapes += [buffer, buffer]
    else:
        shapes.append((cores * parts * tokens + 2 * BLOCK_PAD, width // HD * tokens))
    return [pltpu.VMEM(shape, jnp.bfloat16) for shape in shapes] + [DMA((5, max(groups, parts)))] * 2


def give_on(sizes, cols, rows):
    job = GiveRows.__new__(GiveRows)
    job.cols, job.rows = len(cols), len(rows)
    own = [(s[0],) + s[2:] for s in cols] + [(1,) + s[1:] for s in rows]
    job.outs = [(shape, jnp.bfloat16) for shape in own]
    job.scratch = [pltpu.VMEM(shape, jnp.bfloat16) for shape in own + own[: job.cols]]
    job.scratch += [DMA((job.cols, sizes[0]))] * 4 + [DMA((job.rows,))] * 2
    return job


class Taker:
    def __init__(self, refs):
        self.refs = list(refs)

    def __call__(self, count):
        taken, self.refs = self.refs[:count], self.refs[count:]
        return taken


def decoder_back_kernel(sizes, gain_at, plans, *refs):
    give_b, give_c, fold, cross_scratch, self_scratch = plans
    dec1, dec2, enc2, final = gain_at
    take = Taker(refs)
    gains, grad_cx = take(2)
    cross_ins, self_ins = take(AttendBack.OPERANDS), take(AttendBack.OPERANDS)
    ex, enc_out, enc_cot, en2, gu, down, *a_ins = take(6 + len(fold.outs) - len(give_b.outs))
    dec_in_grad, grad_ex, dg_d1, dg_d2, dg_e2, dg_ef, rel_d, dw_d, dwo_d = take(9)
    totals, c_outs = take(len(fold.outs)), take(len(give_c.outs))
    dw_c, dwo_c, dgu, ddown, grad_dx = take(5)
    f_buf, pf, rf, f_sent, f_got = take(5)
    place = Place(*sizes)
    cross = AttendBack(place, cross_ins, (dw_c, dwo_c), take(len(cross_scratch)), True)
    own = AttendBack(place, self_ins, (dw_d, dwo_d), take(len(self_scratch)), False)
    b_outs = take(len(give_b.outs))
    fold.bind(a_ins + b_outs, totals, take(len(fold.scratch)))
    give_b.bind([dw_c, dwo_c], b_outs, take(len(give_b.scratch)))
    give_c.bind([dgu, ddown], c_outs, take(len(give_c.scratch)))
    of_a, of_b = fold.of(0, len(a_ins)), fold.of(len(a_ins), len(fold.outs))
    place.greet(planes=True)
    cross.begin(grad_cx[...])
    fold.start(place, of_a)
    cross.arrive()
    fold.serve(place, 2, 0)
    cross.compute()
    fold.serve(place, 3, 2)
    cross.exchange()
    fold.serve(place, 2, 2)
    back, dg = norm_back(cross.x[...].astype(jnp.float32), gains[dec2], cross.normed_grad())
    dg_d2[...] = dg
    grad_dx[...] = grad_cx[...] + back
    own.begin(grad_dx[...])
    cross.query_grads(None)
    own.arrive()
    fold.serve(place, len(of_a) - 7, 3)
    own.compute()
    fold.serve(place, 0, len(of_a) - 7)
    cross.keys()
    own.exchange()
    cross.key_grads()
    give_b.begin(place)
    back, dg = norm_back(enc_out[...], gains[final], cross.source_grad())
    dg_ef[...] = dg
    dy = enc_cot[...].astype(jnp.float32) + back
    f_buf[place.group] = low(dy)
    pending = spread_start(place, f_buf, f_sent.at[0], f_got.at[0])
    give_b.middle(place)
    own.query_grads(rel_d)
    spread_wait(place, f_buf, f_sent.at[0], f_got.at[0])
    give_b.end(place)
    fold.start(place, of_b)
    n, dyb = en2[...], all_rows(f_buf)
    h, dgu_value = feed_back_part(n, dyb, gu, down)
    pending += collect_start(place, nt(dgu_value, gu[...]), pf, rf, f_sent.at[1], f_got.at[1])
    dgu[...] = low(tn(n, dgu_value)).reshape(dgu.shape)
    ddown[...] = low(tn(h, dyb)).reshape(ddown.shape)
    give_c.begin(place)
    fold.serve(place, 2, 0)
    dn = collect_wait(place, pf, rf, f_sent.at[1], f_got.at[1])
    back, dg = norm_back(ex[...], gains[enc2], dn)
    dg_e2[...] = dg
    grad_ex[...] = dy + back
    give_c.middle(place)
    fold.serve(place, 2, 1)
    own.keys()
    own.key_grads()
    fold.finish(place, 2)
    back, dg = norm_back(own.x[...].astype(jnp.float32), gains[dec1], own.normed_grad())
    dg_d1[...] = dg
    dec_in_grad[...] = grad_dx[...] + back
    give_c.end(place)
    fold.end(place)
    cross.wait()
    own.wait()
    for copy in pending:
        copy.wait_send()


def encoder_back_kernel(sizes, gain_at, plans, *refs):
    give_d, give_e, fold, before, scratch = plans
    take = Taker(refs)
    gains, grad_ex = take(2)
    ins = take(AttendBack.OPERANDS)
    dg_d1, dg_d2, dg_d3, dg_e2, dg_ef, rel_d = take(6)
    ready, d_ins = take(before), take(give_d.cols + give_d.rows)
    (enc_in_grad,) = take(1)
    totals = take(len(fold.outs))
    dw_e, dwo_e, small, rel_e = take(4)
    place = Place(*sizes)
    own = AttendBack(place, ins, (dw_e, dwo_e), take(len(scratch)), False)
    d_outs, e_outs = take(len(give_d.outs)), take(len(give_e.outs))
    give_d.bind(d_ins, d_outs, take(len(give_d.scratch)))
    give_e.bind([dw_e, small, dwo_e], e_outs, take(len(give_e.scratch)))
    fold.bind(ready + d_outs + e_outs, totals, take(len(fold.scratch)))
    of_c = fold.of(0, before)
    of_d, of_e = fold.of(before, before + len(d_outs)), fold.of(before + len(d_outs), len(fold.outs))
    place.greet(planes=True)
    own.begin(grad_ex[...])
    fold.start(place, of_c)
    give_d.begin(place)
    give_d.middle(place)
    own.arrive()
    fold.serve(place, 2, 0)
    own.compute()
    fold.serve(place, 3, 2)
    own.exchange()
    give_d.end(place)
    fold.start(place, of_d)
    fold.serve(place, 2, 2)
    own.query_grads(rel_e)
    fold.serve(place, 2, 2)
    own.keys()
    fold.serve(place, len(of_c) - 9, 3)
    own.key_grads()
    dn = own.normed_grad()
    back, dg_e1 = norm_back(own.x[...].astype(jnp.float32), gains[gain_at], dn)
    enc_in_grad[...] = grad_ex[...] + back
    devices = place.groups * place.cores
    share = dg_e1.shape[1] // devices
    small[...] = jnp.zeros_like(small)
    all_gains = jnp.concatenate([dg_e1, dg_e2[...], dg_ef[...], dg_d1[...], dg_d2[...], dg_d3[...]], axis=0)
    count = all_gains.shape[0]
    each = rel_e.shape[0] // devices
    tables = [rel_e[...].reshape(devices, each, 128), rel_d[...].reshape(devices, each, 128)]
    for device in range(devices):
        piece = jnp.concatenate([all_gains[:, device * share : (device + 1) * share], jnp.zeros((count, 128 - share), jnp.float32)], axis=1)
        rows = jnp.concatenate([piece, tables[0][device], tables[1][device]], axis=0)
        rows = jnp.concatenate([rows, jnp.zeros((16 - rows.shape[0], 128), jnp.float32)], axis=0)
        small[device // place.cores, device % place.cores] = low(rows)
    give_e.begin(place)
    fold.serve(place, 2, len(of_c) - 9)
    give_e.middle(place)
    fold.serve(place, len(of_d) - 2, 2)
    give_e.end(place)
    fold.start(place, of_e)
    fold.finish(place, 2)
    fold.end(place)
    own.wait()


def fused(sizes, collective_id, kernel, operands, outs, scratch):
    return pl.pallas_call(
        functools.partial(kernel, sizes),
        out_shape=tuple(jax.ShapeDtypeStruct(shape, dtype) for shape, dtype in outs),
        in_specs=[IN_VMEM] * len(operands),
        out_specs=(IN_VMEM,) * len(outs),
        scratch_shapes=scratch,
        compiler_params=pltpu.CompilerParams(collective_id=collective_id, has_side_effects=True, vmem_limit_bytes=VMEM_BYTES),
        cost_estimate=pl.CostEstimate(flops=20_000_000_000, bytes_accessed=10_000_000, transcendentals=0),
    )(*operands)


def kept_operands(x, kept, w, wo, ahead):
    _, n, q, kv, o, lse, bm, memory = kept
    if ahead is None:
        return [x, n, q, kv, o, lse, w, wo, bm, memory, memory]
    return [x, n, q, kv, o, lse, w, wo, bm, n, ahead]


def buffers_of(shapes):
    return [pltpu.VMEM(shape, jnp.bfloat16) for shape in shapes]


def decoder_back(sizes, collective_id, gains, gain_at, grad_cx, cross, own, feed, rows_a):
    groups, cores, parts = sizes
    f32, bf16 = jnp.float32, jnp.bfloat16
    block, model = grad_cx.shape
    share = model // (groups * cores)
    width = cross[3].shape[0]
    kv = cross[1][3].shape
    hidden = feed[5].shape[0]
    attention = [(groups, cores, share, 3 * width)], [(cores, width // cores, model)]
    feeds = [(groups, cores, share, 2 * hidden)], [(cores, hidden // cores, model)]
    give_b, give_c = give_on(sizes, *attention), give_on(sizes, *feeds)
    fold = FoldPlanes(list(rows_a) + [jax.ShapeDtypeStruct(shape, dtype) for shape, dtype in give_b.outs])
    cross_scratch = attend_back_scratch(sizes, kv, block, model, width, True)
    self_scratch = attend_back_scratch(sizes, kv, block, model, width, False)
    plans = (give_b, give_c, fold, cross_scratch, self_scratch)
    operands = [gains, grad_cx] + kept_operands(*cross) + kept_operands(*own) + list(feed) + list(rows_a)
    token, gain = ((block, model), f32), ((1, model), f32)
    outs = [token, token, gain, gain, gain, gain, ((own[4].shape[0], 128), f32)]
    outs += [(attention[0][0], bf16), (attention[1][0], bf16)] + fold.outs + give_c.outs
    buffer = (groups, block, model)
    scratch = buffers_of(attention[0] + attention[1] + feeds[0] + feeds[1]) + [pltpu.VMEM((block, model), f32)]
    scratch += buffers_of([buffer] * 3) + [DMA((2, groups))] * 2 + cross_scratch + self_scratch
    scratch += buffers_of([shape for shape, _ in give_b.outs]) + fold.scratch + give_b.scratch + give_c.scratch
    got = Taker(fused(sizes, collective_id, lambda s, *refs: decoder_back_kernel(s, gain_at, plans, *refs), operands, outs, scratch))
    first = got(7)
    return first, got(2), got(len(rows_a)), got(len(give_b.outs)), got(len(give_c.outs))


def encoder_back(sizes, collective_id, gains, gain_at, grad_ex, own, small_grads, ready, grads_d):
    groups, cores, parts = sizes
    f32 = jnp.float32
    block, model = grad_ex.shape
    share = model // (groups * cores)
    width = own[3].shape[0]
    kv = own[1][3].shape
    give_d = GiveRows.__new__(GiveRows)
    give_d = give_on(sizes, [grads_d[0].shape], [grads_d[1].shape])
    cols = [(groups, cores, share, 3 * width), (groups, cores, 16, 128)]
    rows = [(cores, width // cores, model)]
    give_e = give_on(sizes, cols, rows)
    all_outs = [jax.ShapeDtypeStruct(shape, dtype) for shape, dtype in give_d.outs + give_e.outs]
    fold = FoldPlanes(list(ready) + all_outs)
    scratch = attend_back_scratch(sizes, kv, block, model, width, False)
    plans = (give_d, give_e, fold, len(ready), scratch)
    operands = [gains, grad_ex] + kept_operands(*own) + list(small_grads) + list(ready) + list(grads_d)
    buffers = buffers_of([cols[0], rows[0], cols[1]]) + [pltpu.VMEM((own[4].shape[0], 128), f32)] + scratch
    buffers += buffers_of([shape for shape, _ in give_d.outs]) + buffers_of([shape for shape, _ in give_e.outs])
    buffers += give_d.scratch + give_e.scratch + fold.scratch
    outs = [((block, model), f32)] + fold.outs
    got = Taker(fused(sizes, collective_id, lambda s, *refs: encoder_back_kernel(s, gain_at, plans, *refs), operands, outs, buffers))
    return got(1)[0], got(len(ready)), got(2), got(3)


def unpack_kernel(kinds, *refs):
    take = Taker(refs)
    ins = take(len(kinds))
    for ref, pieces in zip(ins, kinds):
        value = ref[...].astype(jnp.float32)
        if pieces == 0:
            take(1)[0][...] = value[0]
            continue
        each = value.shape[2] // pieces
        for piece, out in enumerate(take(pieces)):
            out[...] = jnp.concatenate([one[:, piece * each : (piece + 1) * each] for one in value], axis=1)


def unpack(arrays, kinds):
    outs = []
    for array, pieces in zip(arrays, kinds):
        if pieces == 0:
            outs.append(jax.ShapeDtypeStruct(array.shape[1:], jnp.float32))
        for _ in range(pieces):
            outs.append(jax.ShapeDtypeStruct((array.shape[1], array.shape[0] * array.shape[2] // pieces), jnp.float32))
    return pl.pallas_call(
        functools.partial(unpack_kernel, kinds),
        out_shape=tuple(outs),
        in_specs=[IN_VMEM] * len(arrays),
        out_specs=(IN_VMEM,) * len(outs),
        compiler_params=pltpu.CompilerParams(vmem_limit_bytes=VMEM_BYTES),
    )(*arrays)


def fast_device(
    enc_in, dec_in, enc_cot, dec_cot, enc_segments, dec_segments, buckets,
    enc_norm1, enc_query, enc_key, enc_value, enc_proj, enc_rel, enc_norm2, enc_gate, enc_up, enc_down, enc_final,
    dec_norm1, dec_query, dec_key, dec_value, dec_proj, dec_rel, dec_norm2, cross_query, cross_key, cross_value, cross_proj,
    dec_norm3, dec_gate, dec_up, dec_down,
):
    groups, cores, parts = sizes = lax.axis_size(HG), lax.axis_size(CORE), lax.axis_size(SP)
    my_core, my_part = lax.axis_index(CORE), lax.axis_index(SP)
    block, model = enc_in.shape
    devices = groups * cores
    share = model // devices
    bf16, f32 = jnp.bfloat16, jnp.float32

    def packed(*weights):
        cut = [w.reshape(w.shape[0], groups, w.shape[1] // groups) for w in weights]
        return jnp.concatenate(cut, axis=2).transpose(1, 0, 2)

    rel_len = enc_rel.shape[0]
    all_gains = jnp.stack([enc_norm1, enc_norm2, enc_final, dec_norm1, dec_norm2, dec_norm3])
    all_rels = jnp.concatenate([enc_rel, dec_rel]).reshape(-1, HEADS)
    small = jnp.concatenate([jnp.pad(w, ((0, 0), (0, 128 - w.shape[1]))) for w in (all_gains, all_rels)])
    each = all_rels.shape[0] // 2
    small = jnp.broadcast_to(jnp.pad(small, ((0, 16 - small.shape[0]), (0, 0))), (groups, 16, 128))
    (small, enc_kvq, dec_kvq), (enc_wo, dec_wo) = job_alone(
        sizes,
        1,
        Recut(
            sizes,
            [small, packed(enc_key, enc_value, enc_query), packed(dec_key, dec_value, dec_query)],
            [enc_proj, dec_proj],
        ),
    )
    later = Recut(
        sizes,
        [packed(enc_gate, enc_up), packed(cross_key, cross_value, cross_query), packed(dec_gate, dec_up)],
        [enc_down, cross_proj, dec_down],
    )
    small = small.reshape(devices, 16, 128)
    gains = small[:, :6, :share].transpose(1, 0, 2).reshape(6, 1, model).astype(f32)
    rels = small[:, 6 : 6 + 2 * each].reshape(devices, 2, each, 128).transpose(1, 0, 2, 3).reshape(2, devices * each, 128)

    bucket_count = devices * each
    numbers = jnp.arange(bucket_count, dtype=jnp.int32)[None, :, None]
    long = jnp.pad(buckets, ((0, 0), (block - 1, block)), mode="edge")[:, None, :]
    ahead = (long == numbers).astype(f32)
    back_way = jnp.pad(buckets[:, ::-1], ((0, 0), (block - 1, block)), mode="edge")[:, None, :]
    turn = (back_way == numbers).astype(bf16)

    def mine(ids):
        return lax.dynamic_index_in_dim(
            lax.dynamic_index_in_dim(ids.reshape(groups, cores, parts, block), my_core, 1, False), my_part, 1, False
        ).reshape(1, -1)

    enc_q_ids, dec_q_ids = mine(enc_segments), mine(dec_segments)
    enc_k_ids, dec_k_ids = enc_segments[:, None], dec_segments[:, None]

    (enc_kept, dec_kept), ((enc_gu, cross_kvq, dec_gu), (enc_wd, cross_wo, dec_wd)) = attend(
        sizes,
        2,
        (0, 3),
        [
            (enc_in, gains, enc_kvq, enc_wo, enc_k_ids, enc_q_ids, rels, turn),
            (dec_in, gains, dec_kvq, dec_wo, dec_k_ids, dec_q_ids, rels, turn),
        ],
        later,
    )
    ex, dx = enc_kept[0], dec_kept[0]
    tokens, hidden = groups * block, enc_wd.shape[0]
    token_f32, token_bf16, gain_f32 = ((block, model), f32), ((block, model), bf16), ((1, model), f32)
    buffer = (groups, block, model)
    (enc_out, memory, en2), _ = stage(
        sizes, 3, functools.partial(feed_forward_kernel, 1, 2), [ex, gains, enc_gu, enc_wd],
        [token_f32, token_bf16, ((tokens, model), bf16)], [buffer] * 3, (2, groups),
    )
    (cross_kept,), _ = attend(sizes, 4, (4,), [(dx, gains, cross_kvq, cross_wo, enc_k_ids, dec_q_ids, memory)])
    cx = cross_kept[0]
    give_a = give_on(sizes, [(groups, cores, share, 2 * hidden)], [(cores, hidden // cores, model)])
    dec_out, grad_cx, dg_d3, *rows_a = fused(
        sizes, 5, lambda s, *refs: feed_both_kernel(s, 5, give_a, *refs), [cx, dec_cot, gains, dec_gu, dec_wd],
        [token_f32, token_f32, gain_f32] + give_a.outs,
        buffers_of([buffer] * 6 + [(groups, cores, share, 2 * hidden), (cores, hidden // cores, model)])
        + [DMA((4, groups))] * 2
        + give_a.scratch,
    )

    (dec_in_grad, grad_ex, dg_d1, dg_d2, dg_e2, dg_ef, rel_d), grads_d, sum_a, sum_b, rows_c = decoder_back(
        sizes, 6, gains, (3, 4, 1, 2), grad_cx,
        (dx, cross_kept, cross_kvq, cross_wo, None), (dec_in, dec_kept, dec_kvq, dec_wo, ahead[1]),
        (ex, enc_out, enc_cot, en2, enc_gu, enc_wd), rows_a,
    )
    enc_in_grad, sum_c, sum_d, sum_e = encoder_back(
        sizes, 7, gains, 0, grad_ex, (enc_in, enc_kept, enc_kvq, enc_wo, ahead[0]),
        (dg_d1, dg_d2, dg_d3, dg_e2, dg_ef, rel_d), rows_c, grads_d,
    )

    dgu_rows, d_wd = sum_a
    cross_rows, c_wo = sum_b
    egu_rows, e_wd = sum_c
    dkvq_rows, d_wo = sum_d
    ekvq_rows, small_rows, e_wo = sum_e
    (
        e_wk, e_wv, e_wq, e_wg, e_wu, d_wk, d_wv, d_wq, c_wk, c_wv, c_wq, d_wg, d_wu, d_wd, c_wo, e_wd, d_wo, e_wo
    ) = unpack(
        [ekvq_rows, egu_rows, dkvq_rows, cross_rows, dgu_rows, d_wd, c_wo, e_wd, d_wo, e_wo],
        (3, 2, 3, 3, 2, 0, 0, 0, 0, 0),
    )
    own = jnp.sum(small_rows.astype(f32), axis=0)
    s = [own[i, :share] for i in range(6)]
    e_rel, d_rel = [own[6 + i * each : 6 + (i + 1) * each, :HEADS].reshape(rel_len) for i in range(2)]
    return (
        enc_out, dec_out, enc_in_grad, dec_in_grad,
        s[0], e_wq, e_wk, e_wv, e_wo, e_rel, s[1], e_wg, e_wu, e_wd, s[2],
        s[3], d_wq, d_wk, d_wv, d_wo, d_rel, s[4], c_wq, c_wk, c_wv, c_wo, s[5], d_wg, d_wu, d_wd,
    )


def general_plan(mesh):
    placed = (
        P(("ctx", "sp"), None),
        P(("ctx", "sp"), None),
        P(("ctx", "sp"), None),
        P(("ctx", "sp"), None),
        P(),
        P(),
        P(),
        P("ctx"),
        P("ctx", None),
        P("ctx", None),
        P("ctx", None),
        P("ctx", None),
        P("ctx"),
        P("ctx"),
        P("ctx", None),
        P("ctx", None),
        P("ctx", None),
        P("ctx"),
        P("ctx"),
        P("ctx", None),
        P("ctx", None),
        P("ctx", None),
        P("ctx", None),
        P("ctx"),
        P("ctx"),
        P("ctx", None),
        P("ctx", None),
        P("ctx", None),
        P("ctx", None),
        P("ctx"),
        P("ctx", None),
        P("ctx", None),
        P("ctx", None),
    )
    return jax.shard_map(
        per_device,
        mesh=mesh,
        in_specs=placed,
        out_specs=(
            P(("ctx", "sp"), None),
            P(("ctx", "sp"), None),
            P(("ctx", "sp"), None),
            P(("ctx", "sp"), None),
            P("ctx"),
            P("ctx", None),
            P("ctx", None),
            P("ctx", None),
            P("ctx", None),
            P("ctx"),
            P("ctx"),
            P("ctx", None),
            P("ctx", None),
            P("ctx", None),
            P("ctx"),
            P("ctx"),
            P("ctx", None),
            P("ctx", None),
            P("ctx", None),
            P("ctx", None),
            P("ctx"),
            P("ctx"),
            P("ctx", None),
            P("ctx", None),
            P("ctx", None),
            P("ctx", None),
            P("ctx"),
            P("ctx", None),
            P("ctx", None),
            P("ctx", None),
        ),
        check_vma=False,
    )


def split_plan(mesh, groups):
    cut = Mesh(np.asarray(mesh.devices).reshape(groups, 2, mesh.shape["sp"]), (HG, CORE, SP))
    tokens, rows, gain, same = P((HG, CORE, SP), None), P((HG, CORE), None), P((HG, CORE)), P()
    attention = (gain, rows, rows, rows, rows, gain)
    feed = (gain, rows, rows, rows)
    weights = attention + feed + (gain,) + attention + (gain, rows, rows, rows, rows) + feed
    return jax.shard_map(
        fast_device,
        mesh=cut,
        in_specs=(tokens,) * 4 + (same,) * 3 + weights,
        out_specs=(tokens,) * 4 + weights,
        check_vma=False,
    )


def solution(mesh):
    groups, odd = divmod(mesh.shape["ctx"], 2)
    if odd or HEADS % groups or mesh.shape["sp"] != 4:
        return general_plan(mesh)
    return split_plan(mesh, groups)
```

```python
import functools
import math

import jax
import jax.numpy as jnp
import numpy as np
from jax import lax
from jax.experimental import pallas as pl
from jax.experimental.pallas import tpu as pltpu
from jax.sharding import Mesh
from jax.sharding import PartitionSpec as P

HEADS = 12
HD = 64


EPSILON = 1e-06
NEGATIVE = -1e30
HIGHEST = lax.Precision.HIGHEST


def rms_norm(values, norm_gain):
    return (
        values * lax.rsqrt(jnp.mean(values * values, axis=-1, keepdims=True) + EPSILON) * norm_gain
    )


def norm_pullback(values, norm_gain, grad_normed):
    _, pullback = jax.vjp(rms_norm, values, norm_gain)
    return pullback(grad_normed)


def gated(gate_val, up_val):
    return jax.nn.gelu(gate_val, approximate=True) * up_val


def project(left, right):
    return jnp.dot(left, right, preferred_element_type=jnp.float32)


def weight_grad(left, right):
    return jnp.einsum("td,te->de", left, right, preferred_element_type=jnp.float32)


def input_grad(grad_out, weight):
    return jnp.einsum("te,de->td", grad_out, weight, preferred_element_type=jnp.float32)


def head_table(relative, table_row, heads_here):
    bucket_count = relative.shape[0] // HEADS
    onehot = (table_row[:, None] == jnp.arange(bucket_count, dtype=jnp.int32)[None, :]).astype(
        jnp.float32
    )
    bias_grid = relative.astype(jnp.float32).reshape(bucket_count, HEADS)
    full_table = jnp.dot(onehot, bias_grid, precision=HIGHEST).T
    first_head = lax.axis_index("sp") * heads_here
    return (lax.dynamic_slice_in_dim(full_table, first_head, heads_here, 0), onehot)


def table_grad(grad_table, onehot, heads_here):
    full_grad = jnp.zeros((HEADS, onehot.shape[0]), jnp.float32)
    full_grad = lax.dynamic_update_slice_in_dim(
        full_grad, grad_table, lax.axis_index("sp") * heads_here, 0
    )
    return jnp.dot(onehot.T, full_grad.T, precision=HIGHEST).reshape(-1)


def bias_block(head_bias, pad_len, offset_q, rows, offset_k, cols):
    head_count, table_len = head_bias.shape
    reach_len = (table_len - 1) // 2
    left_edge = jnp.broadcast_to(head_bias[:, :1], (head_count, pad_len))
    right_edge = jnp.broadcast_to(head_bias[:, -1:], (head_count, pad_len))
    padded = jnp.concatenate([left_edge, head_bias, right_edge], axis=1)
    band_width = rows + cols - 1
    start = offset_k - offset_q - (rows - 1) + reach_len + pad_len
    band = lax.dynamic_slice_in_dim(padded, start, band_width, 1)
    tiled = jnp.broadcast_to(band[:, None, :], (head_count, rows, band_width)).reshape(
        head_count, rows * band_width
    )
    skewed = tiled[:, rows - 1 : rows - 1 + rows * (band_width - 1)].reshape(
        head_count, rows, band_width - 1
    )
    return skewed[:, :, :cols]


def make_frame(query_local, query_ids, key_ids, head_bias, causal):
    local_len = query_local.shape[0]
    heads_here = query_local.shape[1] // HD
    offset_q = lax.axis_index("ctx") * local_len
    ids_q = lax.dynamic_slice_in_dim(query_ids, offset_q, local_len, 0)
    row_ids = offset_q + jnp.arange(local_len, dtype=jnp.int32)
    query_heads = query_local.reshape(local_len, heads_here, HD)
    pad_len = query_ids.shape[0] + key_ids.shape[0]

    def bias_of(entries, offset_k, length):
        return bias_block(entries, pad_len, offset_q, local_len, offset_k, length)

    def scores_of(key_block, offset_k):
        length = key_block.shape[0]
        key_heads = key_block.reshape(length, heads_here, HD)
        raw_scores = jnp.einsum(
            "qhd,khd->hqk", query_heads, key_heads, preferred_element_type=jnp.float32
        )
        col_ids = offset_k + jnp.arange(length, dtype=jnp.int32)
        ids_k = lax.dynamic_slice_in_dim(key_ids, offset_k, length, 0)
        allowed = ids_q[:, None] == ids_k[None, :]
        if causal:
            allowed = allowed & (col_ids[None, :] <= row_ids[:, None])
        if head_bias is not None:
            raw_scores = raw_scores + bias_of(head_bias, offset_k, length)
        return (raw_scores, allowed)

    def touches(offset_k, length):
        first_id = lax.dynamic_slice_in_dim(key_ids, offset_k, 1, 0)[0]
        last_id = lax.dynamic_slice_in_dim(key_ids, offset_k + length - 1, 1, 0)[0]
        touched = (ids_q[0] <= last_id) & (first_id <= ids_q[-1])
        if causal:
            touched = touched & (offset_k <= offset_q + local_len - 1)
        return touched

    return (query_heads, scores_of, touches, bias_of)


def sweep(keys_gathered, local_len, step_fn, carry_state):
    key_all, value_all = keys_gathered
    block_len = local_len * math.gcd(4, lax.axis_size("ctx"))

    def sweep_loop_body(number, running):
        offset_k = number * block_len
        key_block = lax.dynamic_slice_in_dim(key_all, offset_k, block_len, 0)
        value_block = lax.dynamic_slice_in_dim(value_all, offset_k, block_len, 0)
        return step_fn(running, key_block, value_block, offset_k)

    return lax.fori_loop(0, key_all.shape[0] // block_len, sweep_loop_body, carry_state)


def whole_keys(key_local, value_local):
    return (
        lax.all_gather(key_local, "ctx", axis=0, tiled=True),
        lax.all_gather(value_local, "ctx", axis=0, tiled=True),
    )


def attention_forward(query_proj, key_proj, value_proj, query_ids, key_ids, head_bias, causal):
    query_local, key_local, value_local = (
        lax.all_to_all(query_proj, "sp", split_axis=1, concat_axis=0, tiled=True),
        lax.all_to_all(key_proj, "sp", split_axis=1, concat_axis=0, tiled=True),
        lax.all_to_all(value_proj, "sp", split_axis=1, concat_axis=0, tiled=True),
    )
    local_len = query_local.shape[0]
    heads_here = query_local.shape[1] // HD
    query_heads, scores_of, touches, _ = make_frame(
        query_local, query_ids, key_ids, head_bias, causal
    )
    key_block = lax.all_gather(key_local, "ctx", axis=0, tiled=True)
    value_block = lax.all_gather(value_local, "ctx", axis=0, tiled=True)
    offset_k = jnp.int32(0)
    length = key_block.shape[0]
    row_top = jnp.full((heads_here, local_len), NEGATIVE, jnp.float32)
    weighted = jnp.zeros((local_len, heads_here, HD), jnp.float32)
    raw_scores, allowed = scores_of(key_block, offset_k)
    masked = jnp.where(allowed[None], raw_scores, NEGATIVE)
    new_top = jnp.maximum(row_top, jnp.max(masked, axis=-1))
    weights = jnp.where(allowed[None], jnp.exp(masked - new_top[..., None]), 0.0)
    rescale = jnp.exp(row_top - new_top)
    value_heads = value_block.reshape(length, heads_here, HD)
    increment = jnp.einsum(
        "hqk,khd->qhd",
        weights.astype(jnp.bfloat16),
        value_heads,
        preferred_element_type=jnp.float32,
    )
    row_top, row_total, weighted = (
        new_top,
        jnp.sum(weights, axis=-1),
        weighted * rescale.T[:, :, None] + increment,
    )
    mixed_heads = weighted / row_total.T[:, :, None]
    log_total = row_top + jnp.log(row_total)
    mixed_low = mixed_heads.reshape(local_len, heads_here * HD).astype(jnp.bfloat16)
    mixed_tokens = lax.all_to_all(mixed_low, "sp", split_axis=0, concat_axis=1, tiled=True)
    retained = (
        query_local,
        key_local,
        value_local,
        mixed_heads,
        log_total,
        None,
        query_ids,
        key_ids,
        head_bias,
        causal,
    )
    return (mixed_tokens, retained)


def attention_backward(grad_mixed, retained):
    (
        query_local,
        key_local,
        value_local,
        mixed_heads,
        log_total,
        gathered,
        query_ids,
        key_ids,
        head_bias,
        causal,
    ) = retained
    grad_local = lax.all_to_all(grad_mixed, "sp", split_axis=1, concat_axis=0, tiled=True)
    local_len = query_local.shape[0]
    heads_here = query_local.shape[1] // HD
    width = heads_here * HD
    query_heads, scores_of, touches, bias_of = make_frame(
        query_local, query_ids, key_ids, head_bias, causal
    )
    grad_heads = grad_local.reshape(local_len, heads_here, HD)
    row_inner = jnp.einsum("qhd,qhd->hq", grad_heads.astype(jnp.float32), mixed_heads)
    gathered = whole_keys(key_local, value_local)
    table_zero = jnp.zeros(head_bias.shape if head_bias is not None else (1,), jnp.float32)

    def gradients_of(key_block, value_block, offset_k):
        length = key_block.shape[0]
        raw_scores, allowed = scores_of(key_block, offset_k)
        probabilities = jnp.where(allowed[None], jnp.exp(raw_scores - log_total[..., None]), 0.0)
        value_heads = value_block.reshape(length, heads_here, HD)
        grad_probs = jnp.einsum(
            "qhd,khd->hqk", grad_heads, value_heads, preferred_element_type=jnp.float32
        )
        grad_scores = (probabilities * (grad_probs - row_inner[..., None])).astype(jnp.bfloat16)
        return (probabilities, grad_scores)

    def table_part(grad_scores, offset_k, length):
        if head_bias is None:
            return table_zero
        _, pullback = jax.vjp(lambda entries: bias_of(entries, offset_k, length), head_bias)
        return pullback(grad_scores.astype(jnp.float32))[0]

    def key_terms_of(probabilities, grad_scores, length):
        grad_key = jnp.einsum(
            "hqk,qhd->khd", grad_scores, query_heads, preferred_element_type=jnp.float32
        )
        grad_value = jnp.einsum(
            "hqk,qhd->khd",
            probabilities.astype(jnp.bfloat16),
            grad_heads,
            preferred_element_type=jnp.float32,
        )
        return jnp.concatenate(
            [grad_key.reshape(length, width), grad_value.reshape(length, width)], axis=1
        )

    def query_part(grad_scores, key_block):
        length = key_block.shape[0]
        key_heads = key_block.reshape(length, heads_here, HD)
        return jnp.einsum(
            "hqk,khd->qhd", grad_scores, key_heads, preferred_element_type=jnp.float32
        )

    def query_step(running, key_block, value_block, offset_k):
        length = key_block.shape[0]
        grad_query, grad_table = running
        probabilities, grad_scores = gradients_of(key_block, value_block, offset_k)
        return (
            grad_query + query_part(grad_scores, key_block),
            grad_table + table_part(grad_scores, offset_k, length),
        )

    query_zero = jnp.zeros((local_len, heads_here, HD), jnp.float32)
    block_len = local_len * math.gcd(4, lax.axis_size("ctx"))
    grad_query, grad_table = sweep(gathered, local_len, query_step, (query_zero, table_zero))
    key_all, value_all = gathered
    step_len = math.gcd(lax.axis_size("ctx") * local_len, block_len)

    def term_loop_body(number, rows_acc):
        offset_b = number * step_len
        key_block = lax.dynamic_slice_in_dim(key_all, offset_b, step_len, 0)
        value_block = lax.dynamic_slice_in_dim(value_all, offset_b, step_len, 0)
        probabilities, grad_scores = gradients_of(key_block, value_block, offset_b)
        return lax.dynamic_update_slice_in_dim(
            rows_acc, key_terms_of(probabilities, grad_scores, step_len), number * step_len, 0
        )

    own_rows = lax.psum_scatter(
        lax.fori_loop(
            0,
            lax.axis_size("ctx") * local_len // step_len,
            term_loop_body,
            jnp.zeros((lax.axis_size("ctx") * local_len, 2 * width), jnp.float32),
        ),
        "ctx",
        scatter_dimension=0,
        tiled=True,
    )
    grad_q_low = grad_query.reshape(local_len, width).astype(jnp.bfloat16)
    grad_k_low = own_rows[:, :width].astype(jnp.bfloat16)
    grad_v_low = own_rows[:, width:].astype(jnp.bfloat16)
    grad_q_tok, grad_k_tok, grad_v_tok = (
        lax.all_to_all(grad_q_low, "sp", split_axis=0, concat_axis=1, tiled=True),
        lax.all_to_all(grad_k_low, "sp", split_axis=0, concat_axis=1, tiled=True),
        lax.all_to_all(grad_v_low, "sp", split_axis=0, concat_axis=1, tiled=True),
    )
    return (grad_q_tok, grad_k_tok, grad_v_tok, grad_table)


def attention_layer(
    residual,
    source,
    norm_gain,
    w_query,
    w_key,
    w_value,
    w_proj,
    query_ids,
    key_ids,
    head_bias,
    causal,
):
    normed = rms_norm(residual, norm_gain).astype(jnp.bfloat16)
    kv_input = normed if source is None else source
    query_proj = project(normed, w_query).astype(jnp.bfloat16)
    key_proj = project(kv_input, w_key).astype(jnp.bfloat16)
    value_proj = project(kv_input, w_value).astype(jnp.bfloat16)
    mixed_tokens, retained = attention_forward(
        query_proj, key_proj, value_proj, query_ids, key_ids, head_bias, causal
    )
    result = residual + project(mixed_tokens, w_proj)
    return (result, (residual, normed, kv_input, mixed_tokens, retained))


def attention_layer_back(grad_out, saved, norm_gain, w_query, w_key, w_value, w_proj, is_cross):
    residual, normed, kv_input, mixed_tokens, retained = saved
    grad_low = grad_out.astype(jnp.bfloat16)
    grad_proj = weight_grad(mixed_tokens, grad_low)
    grad_mixed = input_grad(grad_low, w_proj).astype(jnp.bfloat16)
    grad_q_tok, grad_k_tok, grad_v_tok, grad_table = attention_backward(grad_mixed, retained)
    grad_wq = weight_grad(normed, grad_q_tok)
    grad_wk = weight_grad(kv_input, grad_k_tok)
    grad_wv = weight_grad(kv_input, grad_v_tok)
    grad_source = input_grad(grad_k_tok, w_key) + input_grad(grad_v_tok, w_value)
    grad_normed = input_grad(grad_q_tok, w_query)
    if not is_cross:
        grad_normed = grad_normed + grad_source
        grad_source = None
    grad_resid, grad_gain = norm_pullback(residual, norm_gain, grad_normed)
    return (
        grad_out + grad_resid,
        grad_source,
        (grad_gain, grad_wq, grad_wk, grad_wv, grad_proj, grad_table),
    )


def feed_layer(residual, norm_gain, w_gate, w_up, w_down):
    normed = rms_norm(residual, norm_gain).astype(jnp.bfloat16)
    gate_val = project(normed, w_gate)
    up_val = project(normed, w_up)
    hidden = gated(gate_val, up_val).astype(jnp.bfloat16)
    return (residual + project(hidden, w_down), (residual, normed, gate_val, up_val, hidden))


def feed_layer_back(grad_out, saved, norm_gain, w_gate, w_up, w_down):
    residual, normed, gate_val, up_val, hidden = saved
    grad_low = grad_out.astype(jnp.bfloat16)
    grad_down = weight_grad(hidden, grad_low)
    grad_hidden = input_grad(grad_low, w_down)
    _, pullback = jax.vjp(gated, gate_val, up_val)
    grad_gate, grad_up = pullback(grad_hidden)
    grad_gate = grad_gate.astype(jnp.bfloat16)
    grad_up = grad_up.astype(jnp.bfloat16)
    grad_wg = weight_grad(normed, grad_gate)
    grad_wu = weight_grad(normed, grad_up)
    grad_normed = input_grad(grad_gate, w_gate) + input_grad(grad_up, w_up)
    grad_resid, grad_gain = norm_pullback(residual, norm_gain, grad_normed)
    return (grad_out + grad_resid, (grad_gain, grad_wg, grad_wu, grad_down))


def per_device(
    enc_in,
    dec_in,
    enc_cot,
    dec_cot,
    enc_segments,
    dec_segments,
    buckets,
    enc_norm1,
    enc_query,
    enc_key,
    enc_value,
    enc_proj,
    enc_rel,
    enc_norm2,
    enc_gate,
    enc_up,
    enc_down,
    enc_final,
    dec_norm1,
    dec_query,
    dec_key,
    dec_value,
    dec_proj,
    dec_rel,
    dec_norm2,
    cross_query,
    cross_key,
    cross_value,
    cross_proj,
    dec_norm3,
    dec_gate,
    dec_up,
    dec_down,
):
    (
        enc_norm1,
        enc_query,
        enc_key,
        enc_value,
        enc_proj,
        enc_rel,
        enc_norm2,
        enc_gate,
        enc_up,
        enc_down,
        enc_final,
        dec_norm1,
        dec_query,
        dec_key,
        dec_value,
        dec_proj,
        dec_rel,
        dec_norm2,
        cross_query,
        cross_key,
        cross_value,
        cross_proj,
        dec_norm3,
        dec_gate,
        dec_up,
        dec_down,
    ) = (
        lax.all_gather(enc_norm1, "ctx", axis=0, tiled=True),
        lax.all_gather(enc_query, "ctx", axis=0, tiled=True),
        lax.all_gather(enc_key, "ctx", axis=0, tiled=True),
        lax.all_gather(enc_value, "ctx", axis=0, tiled=True),
        lax.all_gather(enc_proj, "ctx", axis=0, tiled=True),
        lax.all_gather(enc_rel, "ctx", axis=0, tiled=True),
        lax.all_gather(enc_norm2, "ctx", axis=0, tiled=True),
        lax.all_gather(enc_gate, "ctx", axis=0, tiled=True),
        lax.all_gather(enc_up, "ctx", axis=0, tiled=True),
        lax.all_gather(enc_down, "ctx", axis=0, tiled=True),
        lax.all_gather(enc_final, "ctx", axis=0, tiled=True),
        lax.all_gather(dec_norm1, "ctx", axis=0, tiled=True),
        lax.all_gather(dec_query, "ctx", axis=0, tiled=True),
        lax.all_gather(dec_key, "ctx", axis=0, tiled=True),
        lax.all_gather(dec_value, "ctx", axis=0, tiled=True),
        lax.all_gather(dec_proj, "ctx", axis=0, tiled=True),
        lax.all_gather(dec_rel, "ctx", axis=0, tiled=True),
        lax.all_gather(dec_norm2, "ctx", axis=0, tiled=True),
        lax.all_gather(cross_query, "ctx", axis=0, tiled=True),
        lax.all_gather(cross_key, "ctx", axis=0, tiled=True),
        lax.all_gather(cross_value, "ctx", axis=0, tiled=True),
        lax.all_gather(cross_proj, "ctx", axis=0, tiled=True),
        lax.all_gather(dec_norm3, "ctx", axis=0, tiled=True),
        lax.all_gather(dec_gate, "ctx", axis=0, tiled=True),
        lax.all_gather(dec_up, "ctx", axis=0, tiled=True),
        lax.all_gather(dec_down, "ctx", axis=0, tiled=True),
    )
    enc_norm1 = enc_norm1.astype(jnp.float32)
    enc_norm2 = enc_norm2.astype(jnp.float32)
    enc_final = enc_final.astype(jnp.float32)
    dec_norm1 = dec_norm1.astype(jnp.float32)
    dec_norm2 = dec_norm2.astype(jnp.float32)
    dec_norm3 = dec_norm3.astype(jnp.float32)
    heads_here = HEADS // lax.axis_size("sp")
    enc_table, enc_onehot = head_table(enc_rel, buckets[0], heads_here)
    dec_table, dec_onehot = head_table(dec_rel, buckets[1], heads_here)
    enc_x = enc_in.astype(jnp.float32)
    enc_mid, enc_saved_a = attention_layer(
        enc_x,
        None,
        enc_norm1,
        enc_query,
        enc_key,
        enc_value,
        enc_proj,
        enc_segments,
        enc_segments,
        enc_table,
        False,
    )
    enc_result, enc_saved_f = feed_layer(enc_mid, enc_norm2, enc_gate, enc_up, enc_down)
    memory = rms_norm(enc_result, enc_final).astype(jnp.bfloat16)
    dec_x = dec_in.astype(jnp.float32)
    dec_mid, dec_saved_a = attention_layer(
        dec_x,
        None,
        dec_norm1,
        dec_query,
        dec_key,
        dec_value,
        dec_proj,
        dec_segments,
        dec_segments,
        dec_table,
        True,
    )
    dec_cross, dec_saved_c = attention_layer(
        dec_mid,
        memory,
        dec_norm2,
        cross_query,
        cross_key,
        cross_value,
        cross_proj,
        dec_segments,
        enc_segments,
        None,
        False,
    )
    dec_result, dec_saved_f = feed_layer(dec_cross, dec_norm3, dec_gate, dec_up, dec_down)
    grad_dec, dec_ff_grads = feed_layer_back(
        dec_cot.astype(jnp.float32), dec_saved_f, dec_norm3, dec_gate, dec_up, dec_down
    )
    grad_dec, grad_memory, cross_grads = attention_layer_back(
        grad_dec, dec_saved_c, dec_norm2, cross_query, cross_key, cross_value, cross_proj, True
    )
    grad_dec, _, dec_self_grads = attention_layer_back(
        grad_dec, dec_saved_a, dec_norm1, dec_query, dec_key, dec_value, dec_proj, False
    )
    grad_enc_out, grad_final = norm_pullback(enc_result, enc_final, grad_memory)
    grad_enc, enc_ff_grads = feed_layer_back(
        enc_cot.astype(jnp.float32) + grad_enc_out,
        enc_saved_f,
        enc_norm2,
        enc_gate,
        enc_up,
        enc_down,
    )
    grad_enc, _, enc_self_grads = attention_layer_back(
        grad_enc, enc_saved_a, enc_norm1, enc_query, enc_key, enc_value, enc_proj, False
    )
    e_gain1, e_wq, e_wk, e_wv, e_wo, e_table = enc_self_grads
    e_gain2, e_wg, e_wu, e_wd = enc_ff_grads
    d_gain1, d_wq, d_wk, d_wv, d_wo, d_table = dec_self_grads
    c_gain, c_wq, c_wk, c_wv, c_wo, _ = cross_grads
    d_gain3, d_wg, d_wu, d_wd = dec_ff_grads
    e_rel = table_grad(e_table, enc_onehot, heads_here)
    d_rel = table_grad(d_table, dec_onehot, heads_here)
    shards = (
        lax.psum_scatter(e_gain1, "ctx", scatter_dimension=0, tiled=True),
        lax.psum_scatter(e_wq, "ctx", scatter_dimension=0, tiled=True),
        lax.psum_scatter(e_wk, "ctx", scatter_dimension=0, tiled=True),
        lax.psum_scatter(e_wv, "ctx", scatter_dimension=0, tiled=True),
        lax.psum_scatter(e_wo, "ctx", scatter_dimension=0, tiled=True),
        lax.psum_scatter(e_rel, "ctx", scatter_dimension=0, tiled=True),
        lax.psum_scatter(e_gain2, "ctx", scatter_dimension=0, tiled=True),
        lax.psum_scatter(e_wg, "ctx", scatter_dimension=0, tiled=True),
        lax.psum_scatter(e_wu, "ctx", scatter_dimension=0, tiled=True),
        lax.psum_scatter(e_wd, "ctx", scatter_dimension=0, tiled=True),
        lax.psum_scatter(grad_final, "ctx", scatter_dimension=0, tiled=True),
        lax.psum_scatter(d_gain1, "ctx", scatter_dimension=0, tiled=True),
        lax.psum_scatter(d_wq, "ctx", scatter_dimension=0, tiled=True),
        lax.psum_scatter(d_wk, "ctx", scatter_dimension=0, tiled=True),
        lax.psum_scatter(d_wv, "ctx", scatter_dimension=0, tiled=True),
        lax.psum_scatter(d_wo, "ctx", scatter_dimension=0, tiled=True),
        lax.psum_scatter(d_rel, "ctx", scatter_dimension=0, tiled=True),
        lax.psum_scatter(c_gain, "ctx", scatter_dimension=0, tiled=True),
        lax.psum_scatter(c_wq, "ctx", scatter_dimension=0, tiled=True),
        lax.psum_scatter(c_wk, "ctx", scatter_dimension=0, tiled=True),
        lax.psum_scatter(c_wv, "ctx", scatter_dimension=0, tiled=True),
        lax.psum_scatter(c_wo, "ctx", scatter_dimension=0, tiled=True),
        lax.psum_scatter(d_gain3, "ctx", scatter_dimension=0, tiled=True),
        lax.psum_scatter(d_wg, "ctx", scatter_dimension=0, tiled=True),
        lax.psum_scatter(d_wu, "ctx", scatter_dimension=0, tiled=True),
        lax.psum_scatter(d_wd, "ctx", scatter_dimension=0, tiled=True),
    )
    (
        s_gain1,
        s_wq,
        s_wk,
        s_wv,
        s_wo,
        s_rel,
        s_gain2,
        s_wg,
        s_wu,
        s_wd,
        s_final,
        t_gain1,
        t_wq,
        t_wk,
        t_wv,
        t_wo,
        t_rel,
        t_gain2,
        t_cq,
        t_ck,
        t_cv,
        t_co,
        t_gain3,
        t_wg,
        t_wu,
        t_wd,
    ) = shards
    reduced = (
        lax.psum(s_gain1.astype(jnp.bfloat16), "sp").astype(jnp.float32),
        lax.psum(s_wq.astype(jnp.bfloat16), "sp").astype(jnp.float32),
        lax.psum(s_wk.astype(jnp.bfloat16), "sp").astype(jnp.float32),
        lax.psum(s_wv.astype(jnp.bfloat16), "sp").astype(jnp.float32),
        lax.psum(s_wo.astype(jnp.bfloat16), "sp").astype(jnp.float32),
        lax.psum(s_rel.astype(jnp.bfloat16), "sp").astype(jnp.float32),
        lax.psum(s_gain2.astype(jnp.bfloat16), "sp").astype(jnp.float32),
        lax.psum(s_wg.astype(jnp.bfloat16), "sp").astype(jnp.float32),
        lax.psum(s_wu.astype(jnp.bfloat16), "sp").astype(jnp.float32),
        lax.psum(s_wd.astype(jnp.bfloat16), "sp").astype(jnp.float32),
        lax.psum(s_final.astype(jnp.bfloat16), "sp").astype(jnp.float32),
        lax.psum(t_gain1.astype(jnp.bfloat16), "sp").astype(jnp.float32),
        lax.psum(t_wq.astype(jnp.bfloat16), "sp").astype(jnp.float32),
        lax.psum(t_wk.astype(jnp.bfloat16), "sp").astype(jnp.float32),
        lax.psum(t_wv.astype(jnp.bfloat16), "sp").astype(jnp.float32),
        lax.psum(t_wo.astype(jnp.bfloat16), "sp").astype(jnp.float32),
        lax.psum(t_rel.astype(jnp.bfloat16), "sp").astype(jnp.float32),
        lax.psum(t_gain2.astype(jnp.bfloat16), "sp").astype(jnp.float32),
        lax.psum(t_cq.astype(jnp.bfloat16), "sp").astype(jnp.float32),
        lax.psum(t_ck.astype(jnp.bfloat16), "sp").astype(jnp.float32),
        lax.psum(t_cv.astype(jnp.bfloat16), "sp").astype(jnp.float32),
        lax.psum(t_co.astype(jnp.bfloat16), "sp").astype(jnp.float32),
        lax.psum(t_gain3.astype(jnp.bfloat16), "sp").astype(jnp.float32),
        lax.psum(t_wg.astype(jnp.bfloat16), "sp").astype(jnp.float32),
        lax.psum(t_wu.astype(jnp.bfloat16), "sp").astype(jnp.float32),
        lax.psum(t_wd.astype(jnp.bfloat16), "sp").astype(jnp.float32),
    )
    return (enc_result, dec_result, grad_enc, grad_dec) + tuple(reduced)


HG, CORE, SP = "hg", "core", "sp"
BLOCK_PAD = 128
VMEM_BYTES = 60 << 20


def nt(left, right):
    return lax.dot_general(left, right, (((1,), (1,)), ((), ())), preferred_element_type=jnp.float32)


def tn(left, right):
    return lax.dot_general(left, right, (((0,), (0,)), ((), ())), preferred_element_type=jnp.float32)


def nn(left, right):
    return jnp.dot(left, right, preferred_element_type=jnp.float32)


def low(value):
    return value.astype(jnp.bfloat16)


def identity(size):
    rows = lax.broadcasted_iota(jnp.int32, (size, size), 0)
    cols = lax.broadcasted_iota(jnp.int32, (size, size), 1)
    return low(jnp.where(rows == cols, 1.0, 0.0))


def only_lanes(array, first, count):
    lanes = lax.broadcasted_iota(jnp.int32, array.shape, 1)
    return jnp.where((lanes >= first) & (lanes < first + count), array, jnp.zeros_like(array))


def gelu_and_slope(v):
    scale, cubic = math.sqrt(2.0 / math.pi), 0.044715
    t = jnp.tanh(scale * (v + cubic * v * v * v))
    return 0.5 * v * (1.0 + t), 0.5 * (1.0 + t) + 0.5 * v * (1.0 - t * t) * scale * (1.0 + 3.0 * cubic * v * v)


def norm_back(x, g, dn):
    r = lax.rsqrt(jnp.mean(x * x, axis=-1, keepdims=True) + EPSILON)
    w = dn * g
    dx = r * w - x * (r * r * r) * jnp.mean(w * x, axis=-1, keepdims=True)
    return dx, jnp.sum(dn * x * r, axis=0, keepdims=True)


def send(src, dst, send_sem, recv_sem, to):
    copy = pltpu.make_async_remote_copy(
        src_ref=src, dst_ref=dst, send_sem=send_sem, recv_sem=recv_sem, device_id=to, device_id_type=pl.DeviceIdType.MESH
    )
    copy.start()
    return copy


def arrived(dst, send_sem, recv_sem, to):
    pltpu.make_async_remote_copy(
        src_ref=dst, dst_ref=dst, send_sem=send_sem, recv_sem=recv_sem, device_id=to, device_id_type=pl.DeviceIdType.MESH
    ).wait_recv()


class Place:
    def __init__(self, groups, cores, parts):
        self.groups, self.cores, self.parts = groups, cores, parts
        self.group, self.core, self.part = lax.axis_index(HG), lax.axis_index(CORE), lax.axis_index(SP)

    def ahead(self, step):
        return lax.rem(self.group + step, self.groups)

    def behind(self, step):
        return lax.rem(self.group + self.groups - step, self.groups)

    def chip(self, group):
        return (group, self.core, self.part)

    def sibling(self):
        return (self.group, 1 - self.core, self.part)

    def plane(self, step):
        return lax.rem(self.part + step, self.parts)

    def plane_behind(self, step):
        return lax.rem(self.part + self.parts - step, self.parts)

    def at_plane(self, part):
        return (self.group, self.core, part)

    def first_token(self, number, block):
        return pl.multiple_of(((self.cores * number + self.core) * self.parts + self.part) * block, block)

    def greet(self, planes=False):
        barrier = pltpu.get_barrier_semaphore()
        partners = [self.chip(self.ahead(step)) for step in range(1, self.groups)] + [self.sibling()]
        if planes:
            partners += [self.at_plane(self.plane(step)) for step in range(1, self.parts)]
        for partner in partners:
            pl.semaphore_signal(barrier, inc=1, device_id=partner, device_id_type=pl.DeviceIdType.MESH)
        pl.semaphore_wait(barrier, len(partners))


def spread_start(place, buf, sent, got):
    mine = buf.at[place.group]
    return [
        send(mine, mine, sent.at[step], got.at[step], place.chip(place.ahead(step))) for step in range(1, place.groups)
    ]


def spread_wait(place, buf, sent, got):
    for step in range(1, place.groups):
        source = place.behind(step)
        arrived(buf.at[source], sent.at[step], got.at[step], place.chip(source))


def collect_start(place, partial, out_buf, in_buf, sent, got):
    out_buf[...] = low(partial).reshape(out_buf.shape)
    pending = []
    for step in range(1, place.groups):
        to = place.ahead(step)
        pending.append(send(out_buf.at[to], in_buf.at[place.group], sent.at[step], got.at[step], place.chip(to)))
    return pending


def collect_wait(place, out_buf, in_buf, sent, got):
    total = out_buf[place.group].astype(jnp.float32)
    for step in range(1, place.groups):
        source = place.behind(step)
        arrived(in_buf.at[source], sent.at[step], got.at[step], place.chip(source))
        total = total + in_buf[source].astype(jnp.float32)
    return total


def all_rows(buf):
    return buf[...].reshape(buf.shape[0] * buf.shape[1], buf.shape[2])


DMA = pltpu.SemaphoreType.DMA
IN_VMEM = pl.BlockSpec(memory_space=pltpu.VMEM)
ANYWHERE = pl.BlockSpec(memory_space=pl.ANY)


class Recut:
    def __init__(self, sizes, col_shapes, row_shapes):
        groups, cores, _ = sizes
        self.cols, self.rows = len(col_shapes), len(row_shapes)
        self.outs = [((groups, cores) + s[1:], jnp.bfloat16) for s in col_shapes]
        self.outs += [((cores,) + s, jnp.bfloat16) for s in row_shapes]
        cols = (self.cols, groups)
        self.scratch = [DMA(cols)] * 4 + [DMA((self.rows,))] * 2 + [DMA((self.cols + self.rows,))]

    def bind(self, ins, outs, scratch):
        self.col_refs, self.row_refs = ins[: self.cols], ins[self.cols :]
        self.col_outs, self.row_outs = outs[: self.cols], outs[self.cols :]
        self.sems = scratch
        self.pending, self.copies = [], []

    def begin(self, place):
        sent, got, relay_sent, relay_got, pair_sent, pair_got, local = self.sems
        group, core = place.group, place.core
        for index, (ref, out) in enumerate(zip(self.col_refs, self.col_outs)):
            slot = out.at[group, core]
            for step in range(1, place.groups):
                to = place.ahead(step)
                self.pending.append(send(ref.at[to], slot, sent.at[index, step], got.at[index, step], place.chip(to)))
            self.pending.append(send(ref.at[group], slot, relay_sent.at[index, 0], relay_got.at[index, 0], place.sibling()))
            self.copies.append(pltpu.make_async_copy(ref.at[group], slot, local.at[index]))
        for index, (ref, out) in enumerate(zip(self.row_refs, self.row_outs)):
            slot = out.at[core]
            self.pending.append(send(ref, slot, pair_sent.at[index], pair_got.at[index], place.sibling()))
            self.copies.append(pltpu.make_async_copy(ref, slot, local.at[self.cols + index]))
        for copy in self.copies:
            copy.start()

    def middle(self, place):
        sent, got, relay_sent, relay_got = self.sems[:4]
        for index, out in enumerate(self.col_outs):
            for step in range(1, place.groups):
                source = place.behind(step)
                slot = out.at[source, place.core]
                arrived(slot, sent.at[index, step], got.at[index, step], place.chip(source))
                self.pending.append(
                    send(slot, slot, relay_sent.at[index, step], relay_got.at[index, step], place.sibling())
                )

    def end(self, place):
        _, _, relay_sent, relay_got, pair_sent, pair_got, _ = self.sems
        for index, out in enumerate(self.col_outs):
            for step in range(place.groups):
                slot = out.at[place.behind(step), 1 - place.core]
                arrived(slot, relay_sent.at[index, step], relay_got.at[index, step], place.sibling())
        for index, out in enumerate(self.row_outs):
            arrived(out.at[1 - place.core], pair_sent.at[index], pair_got.at[index], place.sibling())
        for copy in self.copies:
            copy.wait()
        for copy in self.pending:
            copy.wait_send()


class GiveRows:
    def __init__(self, sizes, cols, rows):
        self.cols, self.rows = len(cols), len(rows)
        own = [(s[0],) + s[2:] for s in cols] + [(1,) + s[1:] for s in rows]
        self.outs = [(shape, jnp.bfloat16) for shape in own]
        self.scratch = [pltpu.VMEM(shape, jnp.bfloat16) for shape in own + own[: self.cols]]
        self.scratch += [DMA((self.cols, sizes[0]))] * 4 + [DMA((self.rows,))] * 2

    def bind(self, ins, outs, scratch):
        self.col_refs, self.row_refs = ins[: self.cols], ins[self.cols :]
        self.col_outs, self.row_outs = outs[: self.cols], outs[self.cols :]
        self.col_sibs, scratch = scratch[: self.cols], scratch[self.cols :]
        self.row_sibs, scratch = scratch[: self.rows], scratch[self.rows :]
        self.col_sums, self.sems = scratch[: self.cols], scratch[self.cols :]
        self.pending = []

    def begin(self, place):
        _, _, pair_sent, pair_got, row_sent, row_got = self.sems
        other = 1 - place.core
        for index, (ref, sib) in enumerate(zip(self.col_refs, self.col_sibs)):
            for step in range(place.groups):
                to = place.ahead(step)
                self.pending.append(
                    send(
                        ref.at[to, other], sib.at[to],
                        pair_sent.at[index, step], pair_got.at[index, step], place.sibling(),
                    )
                )
        for index, (ref, sib) in enumerate(zip(self.row_refs, self.row_sibs)):
            self.pending.append(send(ref.at[other], sib.at[0], row_sent.at[index], row_got.at[index], place.sibling()))

    def middle(self, place):
        sent, got, pair_sent, pair_got, row_sent, row_got = self.sems
        core = place.core
        for index, (ref, sib) in enumerate(zip(self.col_refs, self.col_sibs)):
            out, sums = self.col_outs[index], self.col_sums[index]
            for step in list(range(1, place.groups)) + [0]:
                to = place.ahead(step)
                arrived(sib.at[to], pair_sent.at[index, step], pair_got.at[index, step], place.sibling())
                both = low(ref[to, core].astype(jnp.float32) + sib[to].astype(jnp.float32))
                if step:
                    sums[to] = both
                    self.pending.append(
                        send(sums.at[to], out.at[place.group], sent.at[index, step], got.at[index, step], place.chip(to))
                    )
                else:
                    out[place.group] = both
        for index, (ref, sib) in enumerate(zip(self.row_refs, self.row_sibs)):
            arrived(sib.at[0], row_sent.at[index], row_got.at[index], place.sibling())
            self.row_outs[index][0] = low(ref[core].astype(jnp.float32) + sib[0].astype(jnp.float32))

    def end(self, place):
        sent, got = self.sems[:2]
        for index, out in enumerate(self.col_outs):
            for step in range(1, place.groups):
                source = place.behind(step)
                arrived(out.at[source], sent.at[index, step], got.at[index, step], place.chip(source))
        for copy in self.pending:
            copy.wait_send()


FOLD_PIECE = 56 * 1024


class FoldPlanes:
    def __init__(self, arrays, in_place=False):
        self.in_place = in_place
        self.operands = list(arrays)
        self.in_specs = [IN_VMEM] * len(arrays)
        self.outs = [(w.shape, jnp.bfloat16) for w in arrays]
        self.out_specs = [IN_VMEM] * len(arrays)
        self.pieces = []
        for index, w in enumerate(arrays):
            cuts = next(c for c in (1, 2, 3, 4, 6, 8) if w.shape[1] // c * w.shape[2] <= FOLD_PIECE or c == 8)
            if w.shape[0] * w.shape[1] * w.shape[2] <= FOLD_PIECE:
                self.pieces.append((index, slice(None), pl.ds(0, w.shape[1])))
                continue
            rows = w.shape[1] // cuts
            self.pieces += [(index, lead, pl.ds(c * rows, rows)) for lead in range(w.shape[0]) for c in range(cuts)]
        self.inner_done = self.across_done = 0
        self.scratch = [pltpu.VMEM(w.shape, jnp.bfloat16) for _ in range(1 if in_place else 2) for w in arrays] + [DMA((len(self.pieces),))] * 6

    def bind(self, ins, outs, scratch):
        count = len(self.outs)
        self.ins, self.totals = ins, outs
        self.inner = outs
        self.across, scratch = scratch[:count], scratch[count:]
        self.sums, self.sems = (ins, scratch) if self.in_place else (scratch[:count], scratch[count:])

    def copy(self, hop, number, src, dst, to):
        return pltpu.make_async_remote_copy(
            src_ref=src, dst_ref=dst, send_sem=self.sems[2 * hop].at[number], recv_sem=self.sems[2 * hop + 1].at[number],
            device_id=to, device_id_type=pl.DeviceIdType.MESH,
        )

    def hops(self, place, number):
        index, lead, rows = self.pieces[number]
        part = place.part
        inward, across, outward = (place.at_plane(p) for p in (1 + part // 3, 3 - part, 3 * (part - 1)))
        ref, inner, sums, other, total = (
            side[index].at[lead, rows] for side in (self.ins, self.inner, self.sums, self.across, self.totals)
        )
        return (ref, inner, inward), (sums, other, across), (total, total, outward)

    def roles(self, place):
        middle = (place.part == 1) | (place.part == 2)
        return pl.when(middle), pl.when(jnp.logical_not(middle))

    def start(self, place, numbers):
        @self.roles(place)[1]
        def _():
            for number in numbers:
                self.copy(0, number, *self.hops(place, number)[0]).start()

    def add_inner(self, place, number):
        inward, across, _ = self.hops(place, number)
        self.copy(0, number, *inward).wait_recv()
        across[0][...] = low(inward[0][...].astype(jnp.float32) + inward[1][...].astype(jnp.float32))
        self.copy(1, number, *across).start()

    def add_across(self, place, number):
        _, across, outward = self.hops(place, number)
        self.copy(1, number, *across).wait_recv()
        outward[0][...] = low(across[0][...].astype(jnp.float32) + across[1][...].astype(jnp.float32))
        self.copy(2, number, *outward).start()

    def of(self, first, last):
        return [n for n, piece in enumerate(self.pieces) if first <= piece[0] < last]

    def serve(self, place, inner, across):
        inners = list(range(self.inner_done, min(self.inner_done + inner, len(self.pieces))))
        self.inner_done += len(inners)
        others = list(range(self.across_done, min(self.across_done + across, len(self.pieces))))
        self.across_done += len(others)

        @self.roles(place)[0]
        def _():
            for turn in range(max(len(inners), len(others))):
                if turn < len(inners):
                    self.add_inner(place, inners[turn])
                if turn < len(others):
                    self.add_across(place, others[turn])

    def finish(self, place, lag):
        left = len(self.pieces) - self.inner_done
        behind = self.inner_done - self.across_done
        if behind > lag:
            self.serve(place, 0, behind - lag)
        self.serve(place, lag - min(behind, lag), 0)
        self.serve(place, left, left)
        self.serve(place, 0, len(self.pieces))

    def end(self, place):
        in_middle, at_end = self.roles(place)

        @at_end
        def _():
            for number in range(len(self.pieces)):
                inward, _, outward = self.hops(place, number)
                self.copy(0, number, *inward).wait_send()
                self.copy(2, number, *outward).wait_recv()

        @in_middle
        def _():
            for number in range(len(self.pieces)):
                _, across, outward = self.hops(place, number)
                self.copy(1, number, *across).wait_send()
                self.copy(2, number, *outward).wait_send()


def feed_back_part(n, dyb, gu_ref, down_ref):
    hidden = down_ref.shape[0]
    gu = nn(n, gu_ref[...])
    g, u = gu[:, :hidden], gu[:, hidden:]
    act, slope = gelu_and_slope(g)
    dh = nt(dyb, down_ref[...])
    return low(act * u), jnp.concatenate([low(dh * u * slope), low(dh * act)], axis=1)


def bias_mask(place, block, causal, rel_ref, turn_ref, kdoc_ref, qdoc_ref, out_ref):
    heads, rows_total, lanes = out_ref.shape
    key_len = kdoc_ref.shape[0]
    strip = block + 2 * BLOCK_PAD
    query = lax.broadcasted_iota(jnp.int32, (1, lanes), 1)
    start = ((place.cores * (query // block) + place.core) * place.parts + place.part) * block
    allowed = kdoc_ref[...] == qdoc_ref[...]
    if causal:
        places = lax.broadcasted_iota(jnp.int32, (key_len, lanes), 0)
        allowed = allowed & (places <= start + query % block)
    inside = pl.ds(BLOCK_PAD, key_len)
    if rel_ref is None:
        out_ref[0, inside, :] = low(jnp.where(allowed, 0.0, NEGATIVE))
        return
    by_head = tn(rel_ref[...], turn_ref[...])
    width = by_head.shape[1]
    pick_rows = lax.broadcasted_iota(jnp.int32, (8, by_head.shape[0]), 0)
    pick_cols = lax.broadcasted_iota(jnp.int32, (8, by_head.shape[0]), 1)
    picked = nn(low(jnp.where(pick_cols == pick_rows + place.group * heads, 1.0, 0.0)), low(by_head))
    places = lax.broadcasted_iota(jnp.int32, (rows_total, lanes), 0)
    for head in range(heads):
        row = picked[head : head + 1, :]
        left, right = row[:, width - 2 : width - 1], row[:, 0:1]
        out_ref[head] = low(jnp.where(places < start, left, right))
        wide = jnp.broadcast_to(row, (strip, width))
        for number in range(lanes // block):
            at = (number * block) % 128
            turned = pltpu.roll(wide, (width - (strip - 1) + at) % width, 1, stride=1, stride_axis=0)
            rows = pl.ds(place.first_token(number, block), strip)
            out_ref[head, rows, number * block : (number + 1) * block] = low(turned[:, at : at + block])
        out_ref[head, inside, :] = low(jnp.where(allowed, out_ref[head, inside, :].astype(jnp.float32), NEGATIVE))


def chunk_rows(kv_ref):
    return kv_ref.shape[1] * kv_ref.shape[2] * kv_ref.shape[3]


def key_side(kv_ref, chunk):
    return kv_ref[chunk].reshape(chunk_rows(kv_ref), kv_ref.shape[4])[:, : kv_ref.shape[4] // 2]


def value_side(kv_ref, chunk):
    lanes = kv_ref.shape[4]
    return kv_ref[chunk].reshape(chunk_rows(kv_ref), lanes)[:, lanes // 2 // 128 * 128 :]


def bias_rows(bm_ref, head, chunk, rows):
    at = pl.multiple_of(BLOCK_PAD + chunk * rows, 128)
    return bm_ref[head if bm_ref.shape[0] > 1 else 0, pl.ds(at, rows), :].astype(jnp.float32)


def mix_part(q, kv_ref, bm_ref, o_ref, lse_ref, s_ref, ot_ref):
    chunks, rows = kv_ref.shape[0], chunk_rows(kv_ref)
    queries, width = q.shape
    heads = width // HD
    across = [slice(head * queries, (head + 1) * queries) for head in range(heads)]
    masked_q = [only_lanes(q, head * HD, HD) for head in range(heads)]

    def first(chunk, tops):
        keys = key_side(kv_ref, chunk)
        inside = pl.ds(pl.multiple_of(chunk * rows, rows), rows)
        new = []
        for head in range(heads):
            scores = nt(keys, masked_q[head]) + bias_rows(bm_ref, head, chunk, rows)
            s_ref[inside, across[head]] = scores
            new.append(jnp.maximum(tops[head], jnp.max(scores, axis=0, keepdims=True)))
        return tuple(new)

    tops = lax.fori_loop(0, chunks, first, (jnp.full((1, queries), NEGATIVE, jnp.float32),) * heads)

    def second(chunk, carried):
        values = value_side(kv_ref, chunk)
        inside = pl.ds(pl.multiple_of(chunk * rows, rows), rows)
        lead = values.shape[1] - width
        values_t = low(nt(identity(values.shape[1]), values))
        new = []
        for head in range(heads):
            total, mixed = carried[head]
            weights = jnp.exp(s_ref[inside, across[head]] - tops[head])
            mixed = mixed + nn(values_t[lead + head * HD : lead + (head + 1) * HD], low(weights))
            new.append((total + jnp.sum(weights, axis=0, keepdims=True), mixed))
        return tuple(new)

    start = (jnp.zeros((1, queries), jnp.float32), jnp.zeros((HD, queries), jnp.float32))
    done = lax.fori_loop(0, chunks, second, (start,) * heads)
    for head in range(heads):
        total, mixed = done[head]
        lse_ref[:, across[head]] = tops[head] + jnp.log(total)
        ot_ref[head * HD : (head + 1) * HD, :] = low(mixed / total)
    o_ref[...] = low(nt(identity(queries), ot_ref[...]))


def keys_send(place, kv_ref, base, sent, got):
    mine = kv_ref.at[:, place.core, place.part]
    pending = [
        send(mine, mine, sent.at[base, step], got.at[base, step], place.at_plane(place.plane(step)))
        for step in range(1, place.parts)
    ]
    pending.append(send(mine, mine, sent.at[base + 1, 0], got.at[base + 1, 0], place.sibling()))
    return pending


def keys_relay(place, kv_ref, base, sent, got):
    pending = []
    for step in range(1, place.parts):
        source = place.plane_behind(step)
        slot = kv_ref.at[:, place.core, source]
        arrived(slot, sent.at[base, step], got.at[base, step], place.at_plane(source))
        pending.append(send(slot, slot, sent.at[base + 1, step], got.at[base + 1, step], place.sibling()))
    return pending


def keys_wait(place, kv_ref, base, sent, got):
    for step in range(place.parts):
        slot = kv_ref.at[:, 1 - place.core, place.plane_behind(step)]
        arrived(slot, sent.at[base + 1, step], got.at[base + 1, step], place.sibling())


def mix_back_part(place, q, do, o, kv_ref, lse_ref, bm_ref, dkv_ref, ds_ref):
    chunks, cores, parts, block, lanes = kv_ref.shape
    rows = chunk_rows(kv_ref)
    queries, width = q.shape
    heads = width // HD
    strip = block + 2 * BLOCK_PAD
    first_value = width // 128 * 128
    lead = width - first_value
    do_wide = jnp.concatenate([jnp.zeros((queries, lead), do.dtype), do], axis=1) if lead else do
    across = [slice(head * queries, (head + 1) * queries) for head in range(heads)]
    masked_q = [only_lanes(q, head * HD, HD) for head in range(heads)]
    masked_do = [only_lanes(do_wide, lead + head * HD, HD) for head in range(heads)]
    q_wide = masked_q
    if lead:
        none = jnp.zeros((queries, lead), q.dtype)
        q_wide = [jnp.concatenate([one, none], axis=1) for one in masked_q]
    of_head = lax.broadcasted_iota(jnp.int32, (8, width), 1) // HD
    of_row = lax.broadcasted_iota(jnp.int32, (8, width), 0)
    inners = lax.dot_general(
        jnp.where(of_head == of_row, 1.0, 0.0), do.astype(jnp.float32) * o.astype(jnp.float32),
        (((1,), (1,)), ((), ())), precision=HIGHEST, preferred_element_type=jnp.float32,
    )
    nothing = jnp.zeros((1, queries), jnp.float32)
    if ds_ref is not None:
        empty = jnp.zeros((BLOCK_PAD, heads * queries), jnp.bfloat16)
        ds_ref[0:BLOCK_PAD, :] = empty
        ds_ref[BLOCK_PAD + chunks * rows :, :] = empty
        of_lane = lax.broadcasted_iota(jnp.int32, (1, queries), 1) // block
        lane_start = ((cores * of_lane + place.core) * parts + place.part) * block

    def chunk_step(chunk, carried):
        at = pl.multiple_of(chunk * rows, rows)
        keys, values = key_side(kv_ref, chunk), value_side(kv_ref, chunk)
        keys_t = low(nt(identity(width), keys))
        new, dk, dv = [], None, None
        for head in range(heads):
            left, right, back = carried[head]
            scores = nt(keys, masked_q[head]) + bias_rows(bm_ref, head, chunk, rows)
            p = jnp.exp(scores - lse_ref[:, across[head]])
            dp = nt(values, masked_do[head])
            ds = low(p * (dp - inners[head : head + 1, :]))
            if ds_ref is not None:
                ds_ref[pl.ds(pl.multiple_of(BLOCK_PAD + at, 128), rows), across[head]] = ds
                wide = ds.astype(jnp.float32)
                places = lax.broadcasted_iota(jnp.int32, wide.shape, 0) + (at + BLOCK_PAD)
                left = left + jnp.sum(jnp.where(places < lane_start, wide, 0.0), axis=0, keepdims=True)
                right = right + jnp.sum(jnp.where(places >= lane_start + strip, wide, 0.0), axis=0, keepdims=True)
            back = back + nn(keys_t[head * HD : (head + 1) * HD], ds)
            new.append((left, right, back))
            more_k, more_v = nn(ds, q_wide[head]), nn(low(p), masked_do[head])
            dk, dv = (more_k, more_v) if dk is None else (dk + more_k, dv + more_v)
        if lead:
            shared = dk[:, first_value:] + dv[:, : 2 * lead]
            both = jnp.concatenate([dk[:, :first_value], shared, dv[:, 2 * lead :]], axis=1)
        else:
            both = jnp.concatenate([dk, dv], axis=1)
        dkv_ref[chunk] = low(both).reshape(dkv_ref.shape[1:])
        return tuple(new)

    start = (nothing, nothing, jnp.zeros((HD, queries), jnp.float32))
    done = lax.fori_loop(0, chunks, chunk_step, (start,) * heads)
    return [one[2] for one in done], [one[:2] for one in done]


def table_grads(place, block, done, ds_ref, ahead_ref, rel_ref):
    queries = done[0][0].shape[1]
    width = ahead_ref.shape[1]
    strip = block + 2 * BLOCK_PAD
    rows = lax.broadcasted_iota(jnp.int32, (block, block), 0)
    cols = lax.broadcasted_iota(jnp.int32, (block, block), 1)
    backwards = jnp.where(rows + cols == block - 1, 1.0, 0.0)
    at = lax.broadcasted_iota(jnp.int32, (1, width), 1)
    sums = []
    for head, (left, right) in enumerate(done):
        total = jnp.zeros((strip, block), jnp.float32)
        for number in range(queries // block):
            low_at = head * queries + number * block
            near = pl.ds(place.first_token(number, block), strip)
            total = total + ds_ref[near, low_at : low_at + block].astype(jnp.float32)
        turned = lax.dot_general(
            backwards, total, (((1,), (1,)), ((), ())), precision=HIGHEST, preferred_element_type=jnp.float32
        )
        turned = jnp.concatenate([turned, jnp.zeros((block, width - strip), jnp.float32)], axis=1)
        by_distance = jnp.sum(pltpu.roll(turned, 0, 1, stride=1, stride_axis=0), axis=0, keepdims=True)
        left, right = (jnp.sum(side, axis=1, keepdims=True) for side in (left, right))
        sums.append(by_distance + jnp.where(at == 0, left, 0.0) + jnp.where(at == width - 2, right, 0.0))
    sums = jnp.concatenate(sums + [jnp.zeros((8 - len(sums), width), jnp.float32)], axis=0)
    by_bucket = lax.dot_general(
        sums, ahead_ref[...], (((1,), (1,)), ((), ())), precision=HIGHEST, preferred_element_type=jnp.float32
    )
    head_rows = lax.broadcasted_iota(jnp.int32, (8, 128), 0)
    head_lanes = lax.broadcasted_iota(jnp.int32, (8, 128), 1)
    lanes_of = (head_lanes == head_rows + place.group * len(done)) & (head_rows < len(done))
    rel_ref[...] = lax.dot_general(
        by_bucket, jnp.where(lanes_of, 1.0, 0.0), (((0,), (0,)), ((), ())), precision=HIGHEST, preferred_element_type=jnp.float32
    )


class AttendBack:
    OPERANDS = 10

    def __init__(self, place, ins, grads, dkv, scratch, cross):
        self.place, self.cross = place, cross
        self.x, self.n, self.q, self.kv, self.o, self.lse, self.w, self.wo, self.bm, other = ins
        self.source, self.ahead = (other, None) if cross else (self.n, other)
        self.dw, self.dwo = grads
        self.dkv, self.sib, self.zout, self.zin, self.d_buf, self.pn, self.rn, self.dq = [dkv] + scratch[:7]
        scratch = scratch[7:]
        self.pm, self.rm = (scratch.pop(0), scratch.pop(0)) if cross else (None, None)
        self.ds = None if cross else scratch.pop(0)
        self.sent, self.got = scratch
        self.kv_width = self.kv.shape[4]
        self.pending = []

    def begin(self, dy):
        self.d_buf[self.place.group] = low(dy)
        self.pending += spread_start(self.place, self.d_buf, self.sent.at[0], self.got.at[0])

    def arrive(self):
        spread_wait(self.place, self.d_buf, self.sent.at[0], self.got.at[0])

    def compute(self):
        place, sent, got = self.place, self.sent, self.got
        do = low(nt(all_rows(self.d_buf), self.wo[...]))
        back, self.edges = mix_back_part(
            place, self.q[...], do, self.o[...], self.kv, self.lse, self.bm, self.dkv, self.ds
        )
        self.halves = send(self.dkv.at[:, 1 - place.core], self.sib, sent.at[1, 0], got.at[1, 0], place.sibling())
        self.dq[...] = low(nt(identity(self.q.shape[0]), low(jnp.concatenate(back, axis=0))))
        if self.cross:
            share = nt(self.dq[...], self.w[:, self.kv_width :])
            self.pending += collect_start(place, share, self.pn, self.rn, sent.at[3], got.at[3])

    def exchange(self):
        place, sent, got = self.place, self.sent, self.got
        arrived(self.sib, sent.at[1, 0], got.at[1, 0], place.sibling())
        for step in list(range(1, place.parts)) + [0]:
            to = place.plane(step)
            self.zout[to] = low(self.dkv[:, place.core, to].astype(jnp.float32) + self.sib[:, to].astype(jnp.float32))
            if step:
                self.pending.append(
                    send(self.zout.at[to], self.zin.at[place.part], sent.at[2, step], got.at[2, step], place.at_plane(to))
                )

        self.halves.wait_send()

    def by_rows(self, grad):
        return low(grad).reshape(self.dw.shape[:3] + grad.shape[1:])

    def query_grads(self, rel):
        self.dwo[...] = low(tn(self.o[...], all_rows(self.d_buf))).reshape(self.dwo.shape)
        self.dw[:, :, :, self.kv_width :] = self.by_rows(tn(self.n[...], self.dq[...]))
        if not self.cross:
            table_grads(self.place, self.x.shape[0], self.edges, self.ds, self.ahead, rel)

    def keys(self):
        place, sent, got = self.place, self.sent, self.got
        total = self.zout[place.part].astype(jnp.float32)
        for step in range(1, place.parts):
            source = place.plane_behind(step)
            arrived(self.zin.at[source], sent.at[2, step], got.at[2, step], place.at_plane(source))
            total = total + self.zin[source].astype(jnp.float32)
        self.dkv_own = low(total).reshape(self.q.shape[0], self.kv_width)
        share = nt(self.dkv_own, self.w[:, : self.kv_width])
        if self.cross:
            self.pending += collect_start(place, share, self.pm, self.rm, sent.at[4], got.at[4])
        else:
            share = share + nt(self.dq[...], self.w[:, self.kv_width :])
            self.pending += collect_start(place, share, self.pn, self.rn, sent.at[3], got.at[3])

    def key_grads(self):
        self.dw[:, :, :, : self.kv_width] = self.by_rows(tn(self.source[...], self.dkv_own))

    def source_grad(self):
        return collect_wait(self.place, self.pm, self.rm, self.sent.at[4], self.got.at[4])

    def normed_grad(self):
        return collect_wait(self.place, self.pn, self.rn, self.sent.at[3], self.got.at[3])

    def wait(self):
        for copy in self.pending:
            copy.wait_send()


def attend_back_scratch(sizes, block, model, width, cross):
    groups, cores, parts = sizes
    tokens = groups * block
    turned, buffer = (parts, groups, block, 2 * width), (groups, block, model)
    shapes = [(groups, parts, block, 2 * width), turned, turned, buffer, buffer, buffer, (tokens, width)]
    if cross:
        shapes += [buffer, buffer]
    else:
        shapes.append((cores * parts * tokens + 2 * BLOCK_PAD, width // HD * tokens))
    return [pltpu.VMEM(shape, jnp.bfloat16) for shape in shapes] + [DMA((5, max(groups, parts)))] * 2


class Taker:
    def __init__(self, refs):
        self.refs = list(refs)

    def __call__(self, count):
        taken, self.refs = self.refs[:count], self.refs[count:]
        return taken


def decoder_back_kernel(sizes, gain_at, plans, *refs):
    give_a, give_b, give_c, fold, cross_scratch, self_scratch = plans
    dec1, dec2, dec3, enc2, final = gain_at
    take = Taker(refs)
    gains, cx, dec_cot, dec_gu, dec_down = take(5)
    cross_ins, self_ins = take(AttendBack.OPERANDS), take(AttendBack.OPERANDS)
    ex, enc_out, enc_cot, en2, gu, down = take(6)
    dec_out, dec_in_grad, grad_ex, dg_d1, dg_d2, dg_d3, dg_e2, dg_ef, rel_d, dw_d, dwo_d = take(11)
    totals, b_outs, c_outs = take(len(fold.outs)), take(len(give_b.outs)), take(len(give_c.outs))
    dw_c, dwo_c, dgu, ddown, dgu_a, ddown_a, dkv, grad_cx, grad_dx = take(9)
    n_buf, d_buf, py, ry, f_buf, pf, rf, f_sent, f_got = take(9)
    place = Place(*sizes)
    cross = AttendBack(place, cross_ins, (dw_c, dwo_c), dkv, take(len(cross_scratch)), True)
    own = AttendBack(place, self_ins, (dw_d, dwo_d), dkv, take(len(self_scratch)), False)
    a_outs = take(len(give_a.outs))
    give_a.bind([dgu_a, ddown_a], a_outs, take(len(give_a.scratch)))
    fold.bind(a_outs, totals, take(len(fold.scratch)))
    give_b.bind([dw_c, dwo_c], b_outs, take(len(give_b.scratch)))
    give_c.bind([dgu, ddown], c_outs, take(len(give_c.scratch)))
    pn, rn = own.pn, own.rn
    place.greet(planes=True)
    d_buf[place.group] = dec_cot[...]
    pending = spread_start(place, d_buf, f_sent.at[2], f_got.at[2])
    n_buf[place.group] = low(rms_norm(cx[...], gains[dec3]))
    pending += spread_start(place, n_buf, f_sent.at[3], f_got.at[3])
    spread_wait(place, d_buf, f_sent.at[2], f_got.at[2])
    spread_wait(place, n_buf, f_sent.at[3], f_got.at[3])
    n, dyb = all_rows(n_buf), all_rows(d_buf)
    h, dgu_value = feed_back_part(n, dyb, dec_gu, dec_down)
    leaving = collect_start(place, nt(dgu_value, dec_gu[...]), pn, rn, f_sent.at[4], f_got.at[4])
    dgu_a[...] = low(tn(n, dgu_value)).reshape(dgu_a.shape)
    ddown_a[...] = low(tn(h, dyb)).reshape(ddown_a.shape)
    dn = collect_wait(place, pn, rn, f_sent.at[4], f_got.at[4])
    for copy in leaving:
        copy.wait_send()
    back, dg = norm_back(cx[...], gains[dec3], dn)
    dg_d3[...] = dg
    grad_cx[...] = dec_cot[...].astype(jnp.float32) + back
    cross.begin(grad_cx[...])
    pending += collect_start(place, nn(h, dec_down[...]), py, ry, f_sent.at[5], f_got.at[5])
    give_a.begin(place)
    give_a.middle(place)
    cross.arrive()
    cross.compute()
    cross.exchange()
    give_a.end(place)
    fold.start(place, fold.of(0, len(a_outs)))
    back, dg = norm_back(cross.x[...].astype(jnp.float32), gains[dec2], cross.normed_grad())
    dg_d2[...] = dg
    grad_dx[...] = grad_cx[...] + back
    own.begin(grad_dx[...])
    cross.query_grads(None)
    dec_out[...] = cx[...] + collect_wait(place, py, ry, f_sent.at[5], f_got.at[5])
    own.arrive()
    own.compute()
    cross.keys()
    own.exchange()
    fold.serve(place, 4, 0)
    cross.key_grads()
    give_b.begin(place)
    back, dg = norm_back(enc_out[...], gains[final], cross.source_grad())
    dg_ef[...] = dg
    dy = enc_cot[...].astype(jnp.float32) + back
    f_buf[place.group] = low(dy)
    pending += spread_start(place, f_buf, f_sent.at[0], f_got.at[0])
    give_b.middle(place)
    own.query_grads(rel_d)
    fold.serve(place, 3, 2)
    spread_wait(place, f_buf, f_sent.at[0], f_got.at[0])
    n, dyb = en2[...], all_rows(f_buf)
    h, dgu_value = feed_back_part(n, dyb, gu, down)
    pending += collect_start(place, nt(dgu_value, gu[...]), pf, rf, f_sent.at[1], f_got.at[1])
    dgu[...] = low(tn(n, dgu_value)).reshape(dgu.shape)
    ddown[...] = low(tn(h, dyb)).reshape(ddown.shape)
    give_c.begin(place)
    fold.serve(place, 3, 3)
    dn = collect_wait(place, pf, rf, f_sent.at[1], f_got.at[1])
    back, dg = norm_back(ex[...], gains[enc2], dn)
    dg_e2[...] = dg
    grad_ex[...] = dy + back
    give_c.middle(place)
    own.keys()
    own.key_grads()
    fold.finish(place, 2)
    back, dg = norm_back(own.x[...].astype(jnp.float32), gains[dec1], own.normed_grad())
    dg_d1[...] = dg
    dec_in_grad[...] = grad_dx[...] + back
    give_b.end(place)
    give_c.end(place)
    fold.end(place)
    cross.wait()
    own.wait()
    for copy in pending:
        copy.wait_send()


def encoder_back_kernel(sizes, gain_at, plans, *refs):
    give_d, give_e, fold, before, scratch = plans
    take = Taker(refs)
    gains, grad_ex = take(2)
    ins = take(AttendBack.OPERANDS)
    dg_d1, dg_d2, dg_d3, dg_e2, dg_ef, rel_d = take(6)
    ready, d_ins = take(before), take(give_d.cols + give_d.rows)
    (enc_in_grad,) = take(1)
    totals = take(len(fold.outs))
    dw_e, dwo_e, small, dkv, rel_e = take(5)
    place = Place(*sizes)
    own = AttendBack(place, ins, (dw_e, dwo_e), dkv, take(len(scratch)), False)
    d_outs, e_outs = take(len(give_d.outs)), take(len(give_e.outs))
    give_d.bind(d_ins, d_outs, take(len(give_d.scratch)))
    give_e.bind([dw_e, small, dwo_e], e_outs, take(len(give_e.scratch)))
    fold.bind(ready + d_outs + e_outs, totals, take(len(fold.scratch)))
    of_c = fold.of(0, before)
    of_d, of_e = fold.of(before, before + len(d_outs)), fold.of(before + len(d_outs), len(fold.outs))
    place.greet(planes=True)
    own.begin(grad_ex[...])
    fold.start(place, of_c)
    give_d.begin(place)
    give_d.middle(place)
    own.arrive()
    fold.serve(place, 3, 0)
    own.compute()
    fold.serve(place, 3, 3)
    own.exchange()
    give_d.end(place)
    fold.start(place, of_d)
    fold.serve(place, 3, 3)
    own.query_grads(rel_e)
    fold.serve(place, 3, 3)
    own.keys()
    fold.serve(place, len(of_c) - 12, 3)
    own.key_grads()
    dn = own.normed_grad()
    back, dg_e1 = norm_back(own.x[...].astype(jnp.float32), gains[gain_at], dn)
    enc_in_grad[...] = grad_ex[...] + back
    devices = place.groups * place.cores
    share = dg_e1.shape[1] // devices
    small[...] = jnp.zeros_like(small)
    all_gains = jnp.concatenate([dg_e1, dg_e2[...], dg_ef[...], dg_d1[...], dg_d2[...], dg_d3[...]], axis=0)
    count = all_gains.shape[0]
    each = rel_e.shape[0] // devices
    tables = [rel_e[...].reshape(devices, each, 128), rel_d[...].reshape(devices, each, 128)]
    for device in range(devices):
        piece = jnp.concatenate([all_gains[:, device * share : (device + 1) * share], jnp.zeros((count, 128 - share), jnp.float32)], axis=1)
        rows = jnp.concatenate([piece, tables[0][device], tables[1][device]], axis=0)
        rows = jnp.concatenate([rows, jnp.zeros((16 - rows.shape[0], 128), jnp.float32)], axis=0)
        small[device // place.cores, device % place.cores] = low(rows)
    give_e.begin(place)
    fold.serve(place, 2, len(of_c) - 12)
    give_e.middle(place)
    fold.serve(place, len(of_d) - 2, 2)
    give_e.end(place)
    fold.start(place, of_e)
    fold.finish(place, 2)
    fold.end(place)
    own.wait()


def fused(sizes, collective_id, kernel, operands, outs, scratch):
    return pl.pallas_call(
        functools.partial(kernel, sizes),
        out_shape=tuple(jax.ShapeDtypeStruct(shape, dtype) for shape, dtype in outs),
        in_specs=[IN_VMEM] * len(operands),
        out_specs=(IN_VMEM,) * len(outs),
        scratch_shapes=scratch,
        compiler_params=pltpu.CompilerParams(collective_id=collective_id, has_side_effects=True, vmem_limit_bytes=VMEM_BYTES),
        cost_estimate=pl.CostEstimate(flops=20_000_000_000, bytes_accessed=10_000_000, transcendentals=0),
    )(*operands)


def kept_operands(x, kept, w, wo, ahead):
    _, n, q, kv, o, lse, bm, memory = kept
    return [x, n, q, kv, o, lse, w, wo, bm, memory if ahead is None else ahead]


def buffers_of(shapes):
    return [pltpu.VMEM(shape, jnp.bfloat16) for shape in shapes]


def decoder_back(sizes, collective_id, gains, gain_at, last, cross, own, feed):
    groups, cores, parts = sizes
    f32, bf16 = jnp.float32, jnp.bfloat16
    block, model = last[0].shape
    share = model // (groups * cores)
    width = cross[3].shape[0]
    kv = cross[1][3].shape
    hidden = feed[5].shape[0]
    attention = [(groups, cores, share, 3 * width)], [(cores, width // cores, model)]
    feeds = [(groups, cores, share, 2 * hidden)], [(cores, hidden // cores, model)]
    give_a, give_b, give_c = GiveRows(sizes, *feeds), GiveRows(sizes, *attention), GiveRows(sizes, *feeds)
    fold = FoldPlanes([jax.ShapeDtypeStruct(shape, dtype) for shape, dtype in give_a.outs], True)
    cross_scratch = attend_back_scratch(sizes, block, model, width, True)
    self_scratch = attend_back_scratch(sizes, block, model, width, False)
    plans = (give_a, give_b, give_c, fold, cross_scratch, self_scratch)
    operands = [gains, *last] + kept_operands(*cross) + kept_operands(*own) + list(feed)
    token, gain = ((block, model), f32), ((1, model), f32)
    outs = [token, token, token, gain, gain, gain, gain, gain, ((own[4].shape[0], 128), f32)]
    outs += [(attention[0][0], bf16), (attention[1][0], bf16)] + fold.outs + give_b.outs + give_c.outs
    buffer = (groups, block, model)
    scratch = buffers_of(attention[0] + attention[1] + (feeds[0] + feeds[1]) * 2 + [kv]) + [pltpu.VMEM((block, model), f32)] * 2
    scratch += buffers_of([buffer] * 7) + [DMA((6, groups))] * 2 + cross_scratch + self_scratch
    scratch += buffers_of([shape for shape, _ in give_a.outs])
    scratch += give_a.scratch + fold.scratch + give_b.scratch + give_c.scratch
    got = Taker(fused(sizes, collective_id, lambda s, *refs: decoder_back_kernel(s, gain_at, plans, *refs), operands, outs, scratch))
    first = got(9)
    return first, got(2), got(len(fold.outs)), got(len(give_b.outs)), got(len(give_c.outs))


def encoder_back(sizes, collective_id, gains, gain_at, grad_ex, own, small_grads, ready, grads_d):
    groups, cores, parts = sizes
    f32 = jnp.float32
    block, model = grad_ex.shape
    share = model // (groups * cores)
    width = own[3].shape[0]
    kv = own[1][3].shape
    give_d = GiveRows.__new__(GiveRows)
    give_d = GiveRows(sizes, [grads_d[0].shape], [grads_d[1].shape])
    cols = [(groups, cores, share, 3 * width), (groups, cores, 16, 128)]
    rows = [(cores, width // cores, model)]
    give_e = GiveRows(sizes, cols, rows)
    all_outs = [jax.ShapeDtypeStruct(shape, dtype) for shape, dtype in give_d.outs + give_e.outs]
    fold = FoldPlanes(list(ready) + all_outs)
    scratch = attend_back_scratch(sizes, block, model, width, False)
    plans = (give_d, give_e, fold, len(ready), scratch)
    operands = [gains, grad_ex] + kept_operands(*own) + list(small_grads) + list(ready) + list(grads_d)
    buffers = buffers_of([cols[0], rows[0], cols[1], kv]) + [pltpu.VMEM((own[4].shape[0], 128), f32)] + scratch
    buffers += buffers_of([shape for shape, _ in give_d.outs]) + buffers_of([shape for shape, _ in give_e.outs])
    buffers += give_d.scratch + give_e.scratch + fold.scratch
    outs = [((block, model), f32)] + fold.outs
    got = Taker(fused(sizes, collective_id, lambda s, *refs: encoder_back_kernel(s, gain_at, plans, *refs), operands, outs, buffers))
    return got(1)[0], got(len(ready)), got(2), got(3)


def unpack_kernel(kinds, *refs):
    take = Taker(refs)
    ins = take(len(kinds))
    for ref, pieces in zip(ins, kinds):
        value = ref[...].astype(jnp.float32)
        if pieces == 0:
            take(1)[0][...] = value[0]
            continue
        each = value.shape[2] // pieces
        for piece, out in enumerate(take(pieces)):
            out[...] = jnp.concatenate([one[:, piece * each : (piece + 1) * each] for one in value], axis=1)


def unpack(arrays, kinds):
    outs = []
    for array, pieces in zip(arrays, kinds):
        if pieces == 0:
            outs.append(jax.ShapeDtypeStruct(array.shape[1:], jnp.float32))
        for _ in range(pieces):
            outs.append(jax.ShapeDtypeStruct((array.shape[1], array.shape[0] * array.shape[2] // pieces), jnp.float32))
    return pl.pallas_call(
        functools.partial(unpack_kernel, kinds),
        out_shape=tuple(outs),
        in_specs=[IN_VMEM] * len(arrays),
        out_specs=(IN_VMEM,) * len(outs),
        compiler_params=pltpu.CompilerParams(vmem_limit_bytes=VMEM_BYTES),
    )(*arrays)


class AttendForward:
    def __init__(self, place, outs, bufs, sems, base):
        self.place, self.base = place, base
        self.x, self.n, self.q, self.kv, self.o, self.lse, self.bm = outs
        self.p_buf, self.r_buf = bufs
        self.sent, self.got = sems

    def keys(self, kv):
        kv_ref = self.kv
        kv_ref[:, self.place.core, self.place.part] = kv.reshape(kv_ref.shape[0], kv_ref.shape[3], kv_ref.shape[4])
        return keys_send(self.place, kv_ref, self.base, self.sent, self.got)

    def mix(self, wo, s_ref, ot_ref):
        place, base = self.place, self.base
        pending = keys_relay(place, self.kv, base, self.sent, self.got)
        keys_wait(place, self.kv, base, self.sent, self.got)
        mix_part(self.q[...], self.kv, self.bm, self.o, self.lse, s_ref, ot_ref)
        share = nn(self.o[...], wo)
        return pending + collect_start(place, share, self.p_buf, self.r_buf, self.sent.at[base + 2], self.got.at[base + 2])

    def add(self, x):
        total = collect_wait(self.place, self.p_buf, self.r_buf, self.sent.at[self.base + 2], self.got.at[self.base + 2])
        self.x[...] = x + total


def pack_columns(pack, refs):
    groups = pack.shape[0]
    for group in range(groups):
        parts = [ref[:, group * (ref.shape[1] // groups) : (group + 1) * (ref.shape[1] // groups)] for ref in refs]
        pack[group] = jnp.concatenate([part.astype(jnp.float32) for part in parts], axis=1).astype(pack.dtype)


def flat(ref):
    rows = math.prod(ref.shape[:-1])
    return ref[...].reshape(rows, ref.shape[-1])


def forward_kernel(sizes, counts, recuts, *refs):
    enc_first, dec_first, later, last = recuts
    gain_count, each = counts
    take = Taker(refs)
    enc_in, dec_in, small, enc_k_ids, enc_q_ids, dec_k_ids, dec_q_ids, turns = take(8)
    enc_w, dec_w, cross_w, enc_gate_up, dec_gate_up = take(3), take(3), take(3), take(2), take(2)
    enc_wo_own, dec_wo_own, cross_wo_own, enc_wd_own, dec_wd_own = take(5)
    gains, enc_kvq, dec_kvq, enc_gu, cross_kvq, dec_gu, enc_wo, dec_wo, enc_wd, cross_wo, dec_wd = take(11)
    enc_outs, dec_outs, cross_outs = take(7), take(7), take(7)
    memory_all, enc_out, en2 = take(3)
    small_pack, enc_pack, dec_pack, cross_pack, enc_gu_pack, dec_gu_pack, small_all, rels = take(8)
    s_ref, ot_ref = take(2)
    x_e, x_d, n_buf, d_buf, m_buf, f_p, f_r = take(7)
    bufs = [take(2) for _ in range(3)]
    sent, got = take(2)
    enc_first.bind([small_pack, enc_pack, enc_wo_own], [small_all, enc_kvq, enc_wo], take(len(enc_first.scratch)))
    dec_first.bind([dec_pack, dec_wo_own], [dec_kvq, dec_wo], take(len(dec_first.scratch)))
    later.bind(
        [enc_gu_pack, cross_pack, enc_wd_own, cross_wo_own], [enc_gu, cross_kvq, enc_wd, cross_wo], take(len(later.scratch))
    )
    last.bind([dec_gu_pack, dec_wd_own], [dec_gu, dec_wd], take(len(last.scratch)))
    place = Place(*sizes)
    enc, dec, cross = [
        AttendForward(place, outs, bufs[i], (sent, got), 6 + 3 * i) for i, outs in enumerate((enc_outs, dec_outs, cross_outs))
    ]
    for group in range(place.groups):
        small_pack[group] = small[...]
    pack_columns(enc_pack, enc_w)
    place.greet(planes=True)
    x_e[place.group] = enc_in[...]
    x_d[place.group] = dec_in[...]
    enc_first.begin(place)
    pending = spread_start(place, x_e, sent.at[0], got.at[0])
    pack_columns(dec_pack, dec_w)
    dec_first.begin(place)
    pending += spread_start(place, x_d, sent.at[1], got.at[1])
    pack_columns(enc_gu_pack, enc_gate_up)
    pack_columns(cross_pack, cross_w)
    pack_columns(dec_gu_pack, dec_gate_up)
    enc_first.middle(place)
    enc_first.end(place)

    devices = place.groups * place.cores
    share = enc_in.shape[1] // devices
    rows, model = small.shape[0], enc_in.shape[1]
    lane = lax.broadcasted_iota(jnp.int32, (128, model), 0)
    column = lax.broadcasted_iota(jnp.int32, (128, model), 1)
    bucket = lax.broadcasted_iota(jnp.int32, (devices * each, rows), 0)
    row = lax.broadcasted_iota(jnp.int32, (devices * each, rows), 1)
    every_gain, tables = 0.0, [0.0, 0.0]
    for device in range(devices):
        table = small_all[device // place.cores, device % place.cores]
        to_column = (column == lane + device * share) & (lane < share)
        every_gain = every_gain + nn(table, low(jnp.where(to_column, 1.0, 0.0)))
        for index in range(2):
            from_row = row == bucket - device * each + gain_count + index * each
            from_row = from_row & (bucket // each == device)
            tables[index] = tables[index] + nn(low(jnp.where(from_row, 1.0, 0.0)), table)
    for index in range(gain_count):
        gains[index] = every_gain[index : index + 1, :]
    for index in range(2):
        rels[index] = low(tables[index])

    def project(one, x_buf, gain_at, w, number):
        spread_wait(place, x_buf, sent.at[number], got.at[number])
        kv_width = one.kv.shape[4]
        n = low(rms_norm(all_rows(x_buf).astype(jnp.float32), gains[gain_at]))
        one.n[...] = n
        both = low(nn(n, flat(w)))
        copies = one.keys(both[:, :kv_width])
        one.q[...] = both[:, kv_width:]
        return copies

    pending += project(enc, x_e, 0, enc_kvq, 0)
    dec_first.middle(place)
    dec_first.end(place)
    pending += project(dec, x_d, 3, dec_kvq, 1)
    later.begin(place)
    block = enc_in.shape[0]
    bias_mask(place, block, False, rels.at[0], turns.at[0], enc_k_ids, enc_q_ids, enc.bm)
    bias_mask(place, block, True, rels.at[1], turns.at[1], dec_k_ids, dec_q_ids, dec.bm)
    pending += enc.mix(flat(enc_wo), s_ref, ot_ref)
    bias_mask(place, block, False, None, None, enc_k_ids, dec_q_ids, cross.bm)
    enc.add(enc_in[...].astype(jnp.float32))
    ex = enc.x[...]
    n_buf[place.group] = low(rms_norm(ex, gains[1]))
    pending += spread_start(place, n_buf, sent.at[2], got.at[2])
    later.middle(place)
    later.end(place)
    spread_wait(place, n_buf, sent.at[2], got.at[2])
    en2[...] = all_rows(n_buf)
    w_down = flat(enc_wd)
    hidden = w_down.shape[0]
    gu = nn(en2[...], flat(enc_gu))
    h = low(gelu_and_slope(gu[:, :hidden])[0] * gu[:, hidden:])
    pending += collect_start(place, nn(h, w_down), f_p, f_r, sent.at[5], got.at[5])
    enc_out[...] = ex + collect_wait(place, f_p, f_r, sent.at[5], got.at[5])
    m_buf[place.group] = low(rms_norm(enc_out[...], gains[2]))
    pending += spread_start(place, m_buf, sent.at[4], got.at[4])
    kv_width = cross.kv.shape[4]
    model = enc_in.shape[1]
    spread_wait(place, m_buf, sent.at[4], got.at[4])
    memory_all[...] = all_rows(m_buf)
    pending += cross.keys(low(nn(memory_all[...], cross_kvq[:, :, :, :kv_width].reshape(model, kv_width))))
    pending += dec.mix(flat(dec_wo), s_ref, ot_ref)
    dec.add(dec_in[...].astype(jnp.float32))
    d_buf[place.group] = low(rms_norm(dec.x[...], gains[4]))
    pending += spread_start(place, d_buf, sent.at[3], got.at[3])
    last.begin(place)
    spread_wait(place, d_buf, sent.at[3], got.at[3])
    cross.n[...] = all_rows(d_buf)
    cross.q[...] = low(nn(cross.n[...], cross_kvq[:, :, :, kv_width:].reshape(model, kv_width // 2)))
    pending += cross.mix(flat(cross_wo), s_ref, ot_ref)
    last.middle(place)
    cross.add(dec.x[...])
    last.end(place)
    for copy in pending:
        copy.wait_send()


def forward(sizes, collective_id, enc_in, dec_in, small, counts, ids, turns, weights):
    groups, cores, parts = sizes
    f32, bf16 = jnp.float32, jnp.bfloat16
    block, model = enc_in.shape
    attention, feeds, rows = weights[:3], weights[3:5], weights[5]
    share = attention[0][0].shape[0]
    width = rows[0].shape[0] * cores
    tokens = groups * block
    keys = cores * parts * tokens
    heads = width // HD
    kvq, gu = (groups, share, 3 * width), (groups, share, 2 * feeds[0][0].shape[1] // groups)
    wo, wd = rows[0].shape, rows[3].shape
    small_shape = (groups,) + small.shape
    recuts = (
        Recut(sizes, [small_shape, kvq], [wo]), Recut(sizes, [kvq], [wo]), Recut(sizes, [gu, kvq], [wd, wo]), Recut(sizes, [gu], [wd])
    )

    def both(shape):
        return ((groups, cores) + shape[1:], bf16)

    def pair(shape):
        return ((cores,) + shape, bf16)

    token = ((block, model), f32)
    outs = [((counts[0], 1, model), f32), both(kvq), both(kvq), both(gu), both(kvq), both(gu)]
    outs += [pair(wo), pair(wo), pair(wd), pair(wo), pair(wd)]
    for number in range(3):
        outs += [
            token, ((tokens, model), bf16), ((tokens, width), bf16), ((groups, cores, parts, block, 2 * width), bf16),
            ((tokens, width), bf16), ((1, heads * tokens), f32),
            ((1 if number == 2 else heads, keys + 2 * BLOCK_PAD, tokens), bf16),
        ]
    outs += [((tokens, model), bf16), token, ((tokens, model), bf16)]
    buffer = (groups, block, model)
    scratch = buffers_of([small_shape, kvq, kvq, kvq, gu, gu, both(small_shape)[0], (2, turns.shape[1], 128)])
    scratch += [pltpu.VMEM((keys, heads * tokens), f32)] + buffers_of([(width, tokens)] + [buffer] * 13)
    scratch += [DMA((15, max(groups, parts)))] * 2 + [s for one in recuts for s in one.scratch]
    operands = [enc_in, dec_in, small, *ids, turns] + [w for each in attention for w in each]
    operands += [w for each in feeds for w in each] + list(rows)
    got = Taker(
        fused(sizes, collective_id, lambda s, *refs: forward_kernel(s, counts, recuts, *refs), operands, outs, scratch)
    )
    gains = got(1)[0]
    flat_weights = [w.reshape(-1, w.shape[-1]) for w in got(10)]
    enc_kept, dec_kept, cross_kept = got(7), got(7), got(7)
    memory_all, enc_out, en2 = got(3)
    return gains, flat_weights, (*enc_kept, None), (*dec_kept, None), (*cross_kept, memory_all), enc_out, en2


def fast_device(
    enc_in, dec_in, enc_cot, dec_cot, enc_segments, dec_segments, buckets,
    enc_norm1, enc_query, enc_key, enc_value, enc_proj, enc_rel, enc_norm2, enc_gate, enc_up, enc_down, enc_final,
    dec_norm1, dec_query, dec_key, dec_value, dec_proj, dec_rel, dec_norm2, cross_query, cross_key, cross_value, cross_proj,
    dec_norm3, dec_gate, dec_up, dec_down,
):
    groups, cores, parts = sizes = lax.axis_size(HG), lax.axis_size(CORE), lax.axis_size(SP)
    my_core, my_part = lax.axis_index(CORE), lax.axis_index(SP)
    block, model = enc_in.shape
    devices = groups * cores
    share = model // devices
    bf16, f32 = jnp.bfloat16, jnp.float32

    rel_len = enc_rel.shape[0]
    all_gains = jnp.stack([enc_norm1, enc_norm2, enc_final, dec_norm1, dec_norm2, dec_norm3])
    all_rels = jnp.concatenate([enc_rel, dec_rel]).reshape(-1, HEADS)
    small = jnp.concatenate([jnp.pad(w, ((0, 0), (0, 128 - w.shape[1]))) for w in (all_gains, all_rels)])
    each = all_rels.shape[0] // 2
    small = jnp.pad(small, ((0, 16 - small.shape[0]), (0, 0)))

    bucket_count = devices * each
    numbers = jnp.arange(bucket_count, dtype=jnp.int32)[None, :, None]
    long = jnp.pad(buckets, ((0, 0), (block - 1, block)), mode="edge")[:, None, :]
    ahead = (long == numbers).astype(f32)
    back_way = jnp.pad(buckets[:, ::-1], ((0, 0), (block - 1, block)), mode="edge")[:, None, :]
    turn = (back_way == numbers).astype(bf16)

    def mine(ids):
        return lax.dynamic_index_in_dim(
            lax.dynamic_index_in_dim(ids.reshape(groups, cores, parts, block), my_core, 1, False), my_part, 1, False
        ).reshape(1, -1)

    enc_q_ids, dec_q_ids = mine(enc_segments), mine(dec_segments)
    enc_k_ids, dec_k_ids = enc_segments[:, None], dec_segments[:, None]

    gains, weights, enc_kept, dec_kept, cross_kept, enc_out, en2 = forward(
        sizes, 1, enc_in, dec_in, small, (6, each), (enc_k_ids, enc_q_ids, dec_k_ids, dec_q_ids), turn,
        (
            (enc_key, enc_value, enc_query), (dec_key, dec_value, dec_query), (cross_key, cross_value, cross_query),
            (enc_gate, enc_up), (dec_gate, dec_up), (enc_proj, dec_proj, cross_proj, enc_down, dec_down),
        ),
    )
    enc_kvq, dec_kvq, enc_gu, cross_kvq, dec_gu, enc_wo, dec_wo, enc_wd, cross_wo, dec_wd = weights
    ex, dx, cx = enc_kept[0], dec_kept[0], cross_kept[0]

    (dec_out, dec_in_grad, grad_ex, dg_d1, dg_d2, dg_d3, dg_e2, dg_ef, rel_d), grads_d, sum_a, rows_b, rows_c = decoder_back(
        sizes, 2, gains, (3, 4, 5, 1, 2), (cx, dec_cot, dec_gu, dec_wd),
        (dx, cross_kept, cross_kvq, cross_wo, None), (dec_in, dec_kept, dec_kvq, dec_wo, ahead[1]),
        (ex, enc_out, enc_cot, en2, enc_gu, enc_wd),
    )
    enc_in_grad, sum_bc, sum_d, sum_e = encoder_back(
        sizes, 3, gains, 0, grad_ex, (enc_in, enc_kept, enc_kvq, enc_wo, ahead[0]),
        (dg_d1, dg_d2, dg_d3, dg_e2, dg_ef, rel_d), list(rows_b) + list(rows_c), grads_d,
    )

    dgu_rows, d_wd = sum_a
    cross_rows, c_wo, egu_rows, e_wd = sum_bc
    dkvq_rows, d_wo = sum_d
    ekvq_rows, small_rows, e_wo = sum_e
    (
        e_wk, e_wv, e_wq, e_wg, e_wu, d_wk, d_wv, d_wq, c_wk, c_wv, c_wq, d_wg, d_wu, d_wd, c_wo, e_wd, d_wo, e_wo
    ) = unpack(
        [ekvq_rows, egu_rows, dkvq_rows, cross_rows, dgu_rows, d_wd, c_wo, e_wd, d_wo, e_wo],
        (3, 2, 3, 3, 2, 0, 0, 0, 0, 0),
    )
    own = jnp.sum(small_rows.astype(f32), axis=0)
    s = [own[i, :share] for i in range(6)]
    e_rel, d_rel = [own[6 + i * each : 6 + (i + 1) * each, :HEADS].reshape(rel_len) for i in range(2)]
    return (
        enc_out, dec_out, enc_in_grad, dec_in_grad,
        s[0], e_wq, e_wk, e_wv, e_wo, e_rel, s[1], e_wg, e_wu, e_wd, s[2],
        s[3], d_wq, d_wk, d_wv, d_wo, d_rel, s[4], c_wq, c_wk, c_wv, c_wo, s[5], d_wg, d_wu, d_wd,
    )


def general_plan(mesh):
    placed = (
        P(("ctx", "sp"), None),
        P(("ctx", "sp"), None),
        P(("ctx", "sp"), None),
        P(("ctx", "sp"), None),
        P(),
        P(),
        P(),
        P("ctx"),
        P("ctx", None),
        P("ctx", None),
        P("ctx", None),
        P("ctx", None),
        P("ctx"),
        P("ctx"),
        P("ctx", None),
        P("ctx", None),
        P("ctx", None),
        P("ctx"),
        P("ctx"),
        P("ctx", None),
        P("ctx", None),
        P("ctx", None),
        P("ctx", None),
        P("ctx"),
        P("ctx"),
        P("ctx", None),
        P("ctx", None),
        P("ctx", None),
        P("ctx", None),
        P("ctx"),
        P("ctx", None),
        P("ctx", None),
        P("ctx", None),
    )
    return jax.shard_map(
        per_device,
        mesh=mesh,
        in_specs=placed,
        out_specs=(
            P(("ctx", "sp"), None),
            P(("ctx", "sp"), None),
            P(("ctx", "sp"), None),
            P(("ctx", "sp"), None),
            P("ctx"),
            P("ctx", None),
            P("ctx", None),
            P("ctx", None),
            P("ctx", None),
            P("ctx"),
            P("ctx"),
            P("ctx", None),
            P("ctx", None),
            P("ctx", None),
            P("ctx"),
            P("ctx"),
            P("ctx", None),
            P("ctx", None),
            P("ctx", None),
            P("ctx", None),
            P("ctx"),
            P("ctx"),
            P("ctx", None),
            P("ctx", None),
            P("ctx", None),
            P("ctx", None),
            P("ctx"),
            P("ctx", None),
            P("ctx", None),
            P("ctx", None),
        ),
        check_vma=False,
    )


def split_plan(mesh, groups):
    cut = Mesh(np.asarray(mesh.devices).reshape(groups, 2, mesh.shape["sp"]), (HG, CORE, SP))
    tokens, rows, gain, same = P((HG, CORE, SP), None), P((HG, CORE), None), P((HG, CORE)), P()
    attention = (gain, rows, rows, rows, rows, gain)
    feed = (gain, rows, rows, rows)
    weights = attention + feed + (gain,) + attention + (gain, rows, rows, rows, rows) + feed
    return jax.shard_map(
        fast_device,
        mesh=cut,
        in_specs=(tokens,) * 4 + (same,) * 3 + weights,
        out_specs=(tokens,) * 4 + weights,
        check_vma=False,
    )


def solution(mesh):
    groups, odd = divmod(mesh.shape["ctx"], 2)
    if odd or HEADS % groups or mesh.shape["sp"] != 4:
        return general_plan(mesh)
    return split_plan(mesh, groups)
```

```python
import functools
import math

import jax
import jax.numpy as jnp
import numpy as np
from jax import lax
from jax.experimental import pallas as pl
from jax.experimental.pallas import tpu as pltpu
from jax.sharding import Mesh
from jax.sharding import PartitionSpec as P

HEADS = 12
HD = 64


EPSILON = 1e-06
NEGATIVE = -1e30
HIGHEST = lax.Precision.HIGHEST


def rms_norm(values, norm_gain):
    return (
        values * lax.rsqrt(jnp.mean(values * values, axis=-1, keepdims=True) + EPSILON) * norm_gain
    )


def norm_pullback(values, norm_gain, grad_normed):
    _, pullback = jax.vjp(rms_norm, values, norm_gain)
    return pullback(grad_normed)


def gated(gate_val, up_val):
    return jax.nn.gelu(gate_val, approximate=True) * up_val


def project(left, right):
    return jnp.dot(left, right, preferred_element_type=jnp.float32)


def weight_grad(left, right):
    return jnp.einsum("td,te->de", left, right, preferred_element_type=jnp.float32)


def input_grad(grad_out, weight):
    return jnp.einsum("te,de->td", grad_out, weight, preferred_element_type=jnp.float32)


def head_table(relative, table_row, heads_here):
    bucket_count = relative.shape[0] // HEADS
    onehot = (table_row[:, None] == jnp.arange(bucket_count, dtype=jnp.int32)[None, :]).astype(
        jnp.float32
    )
    bias_grid = relative.astype(jnp.float32).reshape(bucket_count, HEADS)
    full_table = jnp.dot(onehot, bias_grid, precision=HIGHEST).T
    first_head = lax.axis_index("sp") * heads_here
    return (lax.dynamic_slice_in_dim(full_table, first_head, heads_here, 0), onehot)


def table_grad(grad_table, onehot, heads_here):
    full_grad = jnp.zeros((HEADS, onehot.shape[0]), jnp.float32)
    full_grad = lax.dynamic_update_slice_in_dim(
        full_grad, grad_table, lax.axis_index("sp") * heads_here, 0
    )
    return jnp.dot(onehot.T, full_grad.T, precision=HIGHEST).reshape(-1)


def bias_block(head_bias, pad_len, offset_q, rows, offset_k, cols):
    head_count, table_len = head_bias.shape
    reach_len = (table_len - 1) // 2
    left_edge = jnp.broadcast_to(head_bias[:, :1], (head_count, pad_len))
    right_edge = jnp.broadcast_to(head_bias[:, -1:], (head_count, pad_len))
    padded = jnp.concatenate([left_edge, head_bias, right_edge], axis=1)
    band_width = rows + cols - 1
    start = offset_k - offset_q - (rows - 1) + reach_len + pad_len
    band = lax.dynamic_slice_in_dim(padded, start, band_width, 1)
    tiled = jnp.broadcast_to(band[:, None, :], (head_count, rows, band_width)).reshape(
        head_count, rows * band_width
    )
    skewed = tiled[:, rows - 1 : rows - 1 + rows * (band_width - 1)].reshape(
        head_count, rows, band_width - 1
    )
    return skewed[:, :, :cols]


def make_frame(query_local, query_ids, key_ids, head_bias, causal):
    local_len = query_local.shape[0]
    heads_here = query_local.shape[1] // HD
    offset_q = lax.axis_index("ctx") * local_len
    ids_q = lax.dynamic_slice_in_dim(query_ids, offset_q, local_len, 0)
    row_ids = offset_q + jnp.arange(local_len, dtype=jnp.int32)
    query_heads = query_local.reshape(local_len, heads_here, HD)
    pad_len = query_ids.shape[0] + key_ids.shape[0]

    def bias_of(entries, offset_k, length):
        return bias_block(entries, pad_len, offset_q, local_len, offset_k, length)

    def scores_of(key_block, offset_k):
        length = key_block.shape[0]
        key_heads = key_block.reshape(length, heads_here, HD)
        raw_scores = jnp.einsum(
            "qhd,khd->hqk", query_heads, key_heads, preferred_element_type=jnp.float32
        )
        col_ids = offset_k + jnp.arange(length, dtype=jnp.int32)
        ids_k = lax.dynamic_slice_in_dim(key_ids, offset_k, length, 0)
        allowed = ids_q[:, None] == ids_k[None, :]
        if causal:
            allowed = allowed & (col_ids[None, :] <= row_ids[:, None])
        if head_bias is not None:
            raw_scores = raw_scores + bias_of(head_bias, offset_k, length)
        return (raw_scores, allowed)

    def touches(offset_k, length):
        first_id = lax.dynamic_slice_in_dim(key_ids, offset_k, 1, 0)[0]
        last_id = lax.dynamic_slice_in_dim(key_ids, offset_k + length - 1, 1, 0)[0]
        touched = (ids_q[0] <= last_id) & (first_id <= ids_q[-1])
        if causal:
            touched = touched & (offset_k <= offset_q + local_len - 1)
        return touched

    return (query_heads, scores_of, touches, bias_of)


def sweep(keys_gathered, local_len, step_fn, carry_state):
    key_all, value_all = keys_gathered
    block_len = local_len * math.gcd(4, lax.axis_size("ctx"))

    def sweep_loop_body(number, running):
        offset_k = number * block_len
        key_block = lax.dynamic_slice_in_dim(key_all, offset_k, block_len, 0)
        value_block = lax.dynamic_slice_in_dim(value_all, offset_k, block_len, 0)
        return step_fn(running, key_block, value_block, offset_k)

    return lax.fori_loop(0, key_all.shape[0] // block_len, sweep_loop_body, carry_state)


def whole_keys(key_local, value_local):
    return (
        lax.all_gather(key_local, "ctx", axis=0, tiled=True),
        lax.all_gather(value_local, "ctx", axis=0, tiled=True),
    )


def attention_forward(query_proj, key_proj, value_proj, query_ids, key_ids, head_bias, causal):
    query_local, key_local, value_local = (
        lax.all_to_all(query_proj, "sp", split_axis=1, concat_axis=0, tiled=True),
        lax.all_to_all(key_proj, "sp", split_axis=1, concat_axis=0, tiled=True),
        lax.all_to_all(value_proj, "sp", split_axis=1, concat_axis=0, tiled=True),
    )
    local_len = query_local.shape[0]
    heads_here = query_local.shape[1] // HD
    query_heads, scores_of, touches, _ = make_frame(
        query_local, query_ids, key_ids, head_bias, causal
    )
    key_block = lax.all_gather(key_local, "ctx", axis=0, tiled=True)
    value_block = lax.all_gather(value_local, "ctx", axis=0, tiled=True)
    offset_k = jnp.int32(0)
    length = key_block.shape[0]
    row_top = jnp.full((heads_here, local_len), NEGATIVE, jnp.float32)
    weighted = jnp.zeros((local_len, heads_here, HD), jnp.float32)
    raw_scores, allowed = scores_of(key_block, offset_k)
    masked = jnp.where(allowed[None], raw_scores, NEGATIVE)
    new_top = jnp.maximum(row_top, jnp.max(masked, axis=-1))
    weights = jnp.where(allowed[None], jnp.exp(masked - new_top[..., None]), 0.0)
    rescale = jnp.exp(row_top - new_top)
    value_heads = value_block.reshape(length, heads_here, HD)
    increment = jnp.einsum(
        "hqk,khd->qhd",
        weights.astype(jnp.bfloat16),
        value_heads,
        preferred_element_type=jnp.float32,
    )
    row_top, row_total, weighted = (
        new_top,
        jnp.sum(weights, axis=-1),
        weighted * rescale.T[:, :, None] + increment,
    )
    mixed_heads = weighted / row_total.T[:, :, None]
    log_total = row_top + jnp.log(row_total)
    mixed_low = mixed_heads.reshape(local_len, heads_here * HD).astype(jnp.bfloat16)
    mixed_tokens = lax.all_to_all(mixed_low, "sp", split_axis=0, concat_axis=1, tiled=True)
    retained = (
        query_local,
        key_local,
        value_local,
        mixed_heads,
        log_total,
        None,
        query_ids,
        key_ids,
        head_bias,
        causal,
    )
    return (mixed_tokens, retained)


def attention_backward(grad_mixed, retained):
    (
        query_local,
        key_local,
        value_local,
        mixed_heads,
        log_total,
        gathered,
        query_ids,
        key_ids,
        head_bias,
        causal,
    ) = retained
    grad_local = lax.all_to_all(grad_mixed, "sp", split_axis=1, concat_axis=0, tiled=True)
    local_len = query_local.shape[0]
    heads_here = query_local.shape[1] // HD
    width = heads_here * HD
    query_heads, scores_of, touches, bias_of = make_frame(
        query_local, query_ids, key_ids, head_bias, causal
    )
    grad_heads = grad_local.reshape(local_len, heads_here, HD)
    row_inner = jnp.einsum("qhd,qhd->hq", grad_heads.astype(jnp.float32), mixed_heads)
    gathered = whole_keys(key_local, value_local)
    table_zero = jnp.zeros(head_bias.shape if head_bias is not None else (1,), jnp.float32)

    def gradients_of(key_block, value_block, offset_k):
        length = key_block.shape[0]
        raw_scores, allowed = scores_of(key_block, offset_k)
        probabilities = jnp.where(allowed[None], jnp.exp(raw_scores - log_total[..., None]), 0.0)
        value_heads = value_block.reshape(length, heads_here, HD)
        grad_probs = jnp.einsum(
            "qhd,khd->hqk", grad_heads, value_heads, preferred_element_type=jnp.float32
        )
        grad_scores = (probabilities * (grad_probs - row_inner[..., None])).astype(jnp.bfloat16)
        return (probabilities, grad_scores)

    def table_part(grad_scores, offset_k, length):
        if head_bias is None:
            return table_zero
        _, pullback = jax.vjp(lambda entries: bias_of(entries, offset_k, length), head_bias)
        return pullback(grad_scores.astype(jnp.float32))[0]

    def key_terms_of(probabilities, grad_scores, length):
        grad_key = jnp.einsum(
            "hqk,qhd->khd", grad_scores, query_heads, preferred_element_type=jnp.float32
        )
        grad_value = jnp.einsum(
            "hqk,qhd->khd",
            probabilities.astype(jnp.bfloat16),
            grad_heads,
            preferred_element_type=jnp.float32,
        )
        return jnp.concatenate(
            [grad_key.reshape(length, width), grad_value.reshape(length, width)], axis=1
        )

    def query_part(grad_scores, key_block):
        length = key_block.shape[0]
        key_heads = key_block.reshape(length, heads_here, HD)
        return jnp.einsum(
            "hqk,khd->qhd", grad_scores, key_heads, preferred_element_type=jnp.float32
        )

    def query_step(running, key_block, value_block, offset_k):
        length = key_block.shape[0]
        grad_query, grad_table = running
        probabilities, grad_scores = gradients_of(key_block, value_block, offset_k)
        return (
            grad_query + query_part(grad_scores, key_block),
            grad_table + table_part(grad_scores, offset_k, length),
        )

    query_zero = jnp.zeros((local_len, heads_here, HD), jnp.float32)
    block_len = local_len * math.gcd(4, lax.axis_size("ctx"))
    grad_query, grad_table = sweep(gathered, local_len, query_step, (query_zero, table_zero))
    key_all, value_all = gathered
    step_len = math.gcd(lax.axis_size("ctx") * local_len, block_len)

    def term_loop_body(number, rows_acc):
        offset_b = number * step_len
        key_block = lax.dynamic_slice_in_dim(key_all, offset_b, step_len, 0)
        value_block = lax.dynamic_slice_in_dim(value_all, offset_b, step_len, 0)
        probabilities, grad_scores = gradients_of(key_block, value_block, offset_b)
        return lax.dynamic_update_slice_in_dim(
            rows_acc, key_terms_of(probabilities, grad_scores, step_len), number * step_len, 0
        )

    own_rows = lax.psum_scatter(
        lax.fori_loop(
            0,
            lax.axis_size("ctx") * local_len // step_len,
            term_loop_body,
            jnp.zeros((lax.axis_size("ctx") * local_len, 2 * width), jnp.float32),
        ),
        "ctx",
        scatter_dimension=0,
        tiled=True,
    )
    grad_q_low = grad_query.reshape(local_len, width).astype(jnp.bfloat16)
    grad_k_low = own_rows[:, :width].astype(jnp.bfloat16)
    grad_v_low = own_rows[:, width:].astype(jnp.bfloat16)
    grad_q_tok, grad_k_tok, grad_v_tok = (
        lax.all_to_all(grad_q_low, "sp", split_axis=0, concat_axis=1, tiled=True),
        lax.all_to_all(grad_k_low, "sp", split_axis=0, concat_axis=1, tiled=True),
        lax.all_to_all(grad_v_low, "sp", split_axis=0, concat_axis=1, tiled=True),
    )
    return (grad_q_tok, grad_k_tok, grad_v_tok, grad_table)


def attention_layer(
    residual,
    source,
    norm_gain,
    w_query,
    w_key,
    w_value,
    w_proj,
    query_ids,
    key_ids,
    head_bias,
    causal,
):
    normed = rms_norm(residual, norm_gain).astype(jnp.bfloat16)
    kv_input = normed if source is None else source
    query_proj = project(normed, w_query).astype(jnp.bfloat16)
    key_proj = project(kv_input, w_key).astype(jnp.bfloat16)
    value_proj = project(kv_input, w_value).astype(jnp.bfloat16)
    mixed_tokens, retained = attention_forward(
        query_proj, key_proj, value_proj, query_ids, key_ids, head_bias, causal
    )
    result = residual + project(mixed_tokens, w_proj)
    return (result, (residual, normed, kv_input, mixed_tokens, retained))


def attention_layer_back(grad_out, saved, norm_gain, w_query, w_key, w_value, w_proj, is_cross):
    residual, normed, kv_input, mixed_tokens, retained = saved
    grad_low = grad_out.astype(jnp.bfloat16)
    grad_proj = weight_grad(mixed_tokens, grad_low)
    grad_mixed = input_grad(grad_low, w_proj).astype(jnp.bfloat16)
    grad_q_tok, grad_k_tok, grad_v_tok, grad_table = attention_backward(grad_mixed, retained)
    grad_wq = weight_grad(normed, grad_q_tok)
    grad_wk = weight_grad(kv_input, grad_k_tok)
    grad_wv = weight_grad(kv_input, grad_v_tok)
    grad_source = input_grad(grad_k_tok, w_key) + input_grad(grad_v_tok, w_value)
    grad_normed = input_grad(grad_q_tok, w_query)
    if not is_cross:
        grad_normed = grad_normed + grad_source
        grad_source = None
    grad_resid, grad_gain = norm_pullback(residual, norm_gain, grad_normed)
    return (
        grad_out + grad_resid,
        grad_source,
        (grad_gain, grad_wq, grad_wk, grad_wv, grad_proj, grad_table),
    )


def feed_layer(residual, norm_gain, w_gate, w_up, w_down):
    normed = rms_norm(residual, norm_gain).astype(jnp.bfloat16)
    gate_val = project(normed, w_gate)
    up_val = project(normed, w_up)
    hidden = gated(gate_val, up_val).astype(jnp.bfloat16)
    return (residual + project(hidden, w_down), (residual, normed, gate_val, up_val, hidden))


def feed_layer_back(grad_out, saved, norm_gain, w_gate, w_up, w_down):
    residual, normed, gate_val, up_val, hidden = saved
    grad_low = grad_out.astype(jnp.bfloat16)
    grad_down = weight_grad(hidden, grad_low)
    grad_hidden = input_grad(grad_low, w_down)
    _, pullback = jax.vjp(gated, gate_val, up_val)
    grad_gate, grad_up = pullback(grad_hidden)
    grad_gate = grad_gate.astype(jnp.bfloat16)
    grad_up = grad_up.astype(jnp.bfloat16)
    grad_wg = weight_grad(normed, grad_gate)
    grad_wu = weight_grad(normed, grad_up)
    grad_normed = input_grad(grad_gate, w_gate) + input_grad(grad_up, w_up)
    grad_resid, grad_gain = norm_pullback(residual, norm_gain, grad_normed)
    return (grad_out + grad_resid, (grad_gain, grad_wg, grad_wu, grad_down))


def per_device(
    enc_in,
    dec_in,
    enc_cot,
    dec_cot,
    enc_segments,
    dec_segments,
    buckets,
    enc_norm1,
    enc_query,
    enc_key,
    enc_value,
    enc_proj,
    enc_rel,
    enc_norm2,
    enc_gate,
    enc_up,
    enc_down,
    enc_final,
    dec_norm1,
    dec_query,
    dec_key,
    dec_value,
    dec_proj,
    dec_rel,
    dec_norm2,
    cross_query,
    cross_key,
    cross_value,
    cross_proj,
    dec_norm3,
    dec_gate,
    dec_up,
    dec_down,
):
    (
        enc_norm1,
        enc_query,
        enc_key,
        enc_value,
        enc_proj,
        enc_rel,
        enc_norm2,
        enc_gate,
        enc_up,
        enc_down,
        enc_final,
        dec_norm1,
        dec_query,
        dec_key,
        dec_value,
        dec_proj,
        dec_rel,
        dec_norm2,
        cross_query,
        cross_key,
        cross_value,
        cross_proj,
        dec_norm3,
        dec_gate,
        dec_up,
        dec_down,
    ) = (
        lax.all_gather(enc_norm1, "ctx", axis=0, tiled=True),
        lax.all_gather(enc_query, "ctx", axis=0, tiled=True),
        lax.all_gather(enc_key, "ctx", axis=0, tiled=True),
        lax.all_gather(enc_value, "ctx", axis=0, tiled=True),
        lax.all_gather(enc_proj, "ctx", axis=0, tiled=True),
        lax.all_gather(enc_rel, "ctx", axis=0, tiled=True),
        lax.all_gather(enc_norm2, "ctx", axis=0, tiled=True),
        lax.all_gather(enc_gate, "ctx", axis=0, tiled=True),
        lax.all_gather(enc_up, "ctx", axis=0, tiled=True),
        lax.all_gather(enc_down, "ctx", axis=0, tiled=True),
        lax.all_gather(enc_final, "ctx", axis=0, tiled=True),
        lax.all_gather(dec_norm1, "ctx", axis=0, tiled=True),
        lax.all_gather(dec_query, "ctx", axis=0, tiled=True),
        lax.all_gather(dec_key, "ctx", axis=0, tiled=True),
        lax.all_gather(dec_value, "ctx", axis=0, tiled=True),
        lax.all_gather(dec_proj, "ctx", axis=0, tiled=True),
        lax.all_gather(dec_rel, "ctx", axis=0, tiled=True),
        lax.all_gather(dec_norm2, "ctx", axis=0, tiled=True),
        lax.all_gather(cross_query, "ctx", axis=0, tiled=True),
        lax.all_gather(cross_key, "ctx", axis=0, tiled=True),
        lax.all_gather(cross_value, "ctx", axis=0, tiled=True),
        lax.all_gather(cross_proj, "ctx", axis=0, tiled=True),
        lax.all_gather(dec_norm3, "ctx", axis=0, tiled=True),
        lax.all_gather(dec_gate, "ctx", axis=0, tiled=True),
        lax.all_gather(dec_up, "ctx", axis=0, tiled=True),
        lax.all_gather(dec_down, "ctx", axis=0, tiled=True),
    )
    enc_norm1 = enc_norm1.astype(jnp.float32)
    enc_norm2 = enc_norm2.astype(jnp.float32)
    enc_final = enc_final.astype(jnp.float32)
    dec_norm1 = dec_norm1.astype(jnp.float32)
    dec_norm2 = dec_norm2.astype(jnp.float32)
    dec_norm3 = dec_norm3.astype(jnp.float32)
    heads_here = HEADS // lax.axis_size("sp")
    enc_table, enc_onehot = head_table(enc_rel, buckets[0], heads_here)
    dec_table, dec_onehot = head_table(dec_rel, buckets[1], heads_here)
    enc_x = enc_in.astype(jnp.float32)
    enc_mid, enc_saved_a = attention_layer(
        enc_x,
        None,
        enc_norm1,
        enc_query,
        enc_key,
        enc_value,
        enc_proj,
        enc_segments,
        enc_segments,
        enc_table,
        False,
    )
    enc_result, enc_saved_f = feed_layer(enc_mid, enc_norm2, enc_gate, enc_up, enc_down)
    memory = rms_norm(enc_result, enc_final).astype(jnp.bfloat16)
    dec_x = dec_in.astype(jnp.float32)
    dec_mid, dec_saved_a = attention_layer(
        dec_x,
        None,
        dec_norm1,
        dec_query,
        dec_key,
        dec_value,
        dec_proj,
        dec_segments,
        dec_segments,
        dec_table,
        True,
    )
    dec_cross, dec_saved_c = attention_layer(
        dec_mid,
        memory,
        dec_norm2,
        cross_query,
        cross_key,
        cross_value,
        cross_proj,
        dec_segments,
        enc_segments,
        None,
        False,
    )
    dec_result, dec_saved_f = feed_layer(dec_cross, dec_norm3, dec_gate, dec_up, dec_down)
    grad_dec, dec_ff_grads = feed_layer_back(
        dec_cot.astype(jnp.float32), dec_saved_f, dec_norm3, dec_gate, dec_up, dec_down
    )
    grad_dec, grad_memory, cross_grads = attention_layer_back(
        grad_dec, dec_saved_c, dec_norm2, cross_query, cross_key, cross_value, cross_proj, True
    )
    grad_dec, _, dec_self_grads = attention_layer_back(
        grad_dec, dec_saved_a, dec_norm1, dec_query, dec_key, dec_value, dec_proj, False
    )
    grad_enc_out, grad_final = norm_pullback(enc_result, enc_final, grad_memory)
    grad_enc, enc_ff_grads = feed_layer_back(
        enc_cot.astype(jnp.float32) + grad_enc_out,
        enc_saved_f,
        enc_norm2,
        enc_gate,
        enc_up,
        enc_down,
    )
    grad_enc, _, enc_self_grads = attention_layer_back(
        grad_enc, enc_saved_a, enc_norm1, enc_query, enc_key, enc_value, enc_proj, False
    )
    e_gain1, e_wq, e_wk, e_wv, e_wo, e_table = enc_self_grads
    e_gain2, e_wg, e_wu, e_wd = enc_ff_grads
    d_gain1, d_wq, d_wk, d_wv, d_wo, d_table = dec_self_grads
    c_gain, c_wq, c_wk, c_wv, c_wo, _ = cross_grads
    d_gain3, d_wg, d_wu, d_wd = dec_ff_grads
    e_rel = table_grad(e_table, enc_onehot, heads_here)
    d_rel = table_grad(d_table, dec_onehot, heads_here)
    shards = (
        lax.psum_scatter(e_gain1, "ctx", scatter_dimension=0, tiled=True),
        lax.psum_scatter(e_wq, "ctx", scatter_dimension=0, tiled=True),
        lax.psum_scatter(e_wk, "ctx", scatter_dimension=0, tiled=True),
        lax.psum_scatter(e_wv, "ctx", scatter_dimension=0, tiled=True),
        lax.psum_scatter(e_wo, "ctx", scatter_dimension=0, tiled=True),
        lax.psum_scatter(e_rel, "ctx", scatter_dimension=0, tiled=True),
        lax.psum_scatter(e_gain2, "ctx", scatter_dimension=0, tiled=True),
        lax.psum_scatter(e_wg, "ctx", scatter_dimension=0, tiled=True),
        lax.psum_scatter(e_wu, "ctx", scatter_dimension=0, tiled=True),
        lax.psum_scatter(e_wd, "ctx", scatter_dimension=0, tiled=True),
        lax.psum_scatter(grad_final, "ctx", scatter_dimension=0, tiled=True),
        lax.psum_scatter(d_gain1, "ctx", scatter_dimension=0, tiled=True),
        lax.psum_scatter(d_wq, "ctx", scatter_dimension=0, tiled=True),
        lax.psum_scatter(d_wk, "ctx", scatter_dimension=0, tiled=True),
        lax.psum_scatter(d_wv, "ctx", scatter_dimension=0, tiled=True),
        lax.psum_scatter(d_wo, "ctx", scatter_dimension=0, tiled=True),
        lax.psum_scatter(d_rel, "ctx", scatter_dimension=0, tiled=True),
        lax.psum_scatter(c_gain, "ctx", scatter_dimension=0, tiled=True),
        lax.psum_scatter(c_wq, "ctx", scatter_dimension=0, tiled=True),
        lax.psum_scatter(c_wk, "ctx", scatter_dimension=0, tiled=True),
        lax.psum_scatter(c_wv, "ctx", scatter_dimension=0, tiled=True),
        lax.psum_scatter(c_wo, "ctx", scatter_dimension=0, tiled=True),
        lax.psum_scatter(d_gain3, "ctx", scatter_dimension=0, tiled=True),
        lax.psum_scatter(d_wg, "ctx", scatter_dimension=0, tiled=True),
        lax.psum_scatter(d_wu, "ctx", scatter_dimension=0, tiled=True),
        lax.psum_scatter(d_wd, "ctx", scatter_dimension=0, tiled=True),
    )
    (
        s_gain1,
        s_wq,
        s_wk,
        s_wv,
        s_wo,
        s_rel,
        s_gain2,
        s_wg,
        s_wu,
        s_wd,
        s_final,
        t_gain1,
        t_wq,
        t_wk,
        t_wv,
        t_wo,
        t_rel,
        t_gain2,
        t_cq,
        t_ck,
        t_cv,
        t_co,
        t_gain3,
        t_wg,
        t_wu,
        t_wd,
    ) = shards
    reduced = (
        lax.psum(s_gain1.astype(jnp.bfloat16), "sp").astype(jnp.float32),
        lax.psum(s_wq.astype(jnp.bfloat16), "sp").astype(jnp.float32),
        lax.psum(s_wk.astype(jnp.bfloat16), "sp").astype(jnp.float32),
        lax.psum(s_wv.astype(jnp.bfloat16), "sp").astype(jnp.float32),
        lax.psum(s_wo.astype(jnp.bfloat16), "sp").astype(jnp.float32),
        lax.psum(s_rel.astype(jnp.bfloat16), "sp").astype(jnp.float32),
        lax.psum(s_gain2.astype(jnp.bfloat16), "sp").astype(jnp.float32),
        lax.psum(s_wg.astype(jnp.bfloat16), "sp").astype(jnp.float32),
        lax.psum(s_wu.astype(jnp.bfloat16), "sp").astype(jnp.float32),
        lax.psum(s_wd.astype(jnp.bfloat16), "sp").astype(jnp.float32),
        lax.psum(s_final.astype(jnp.bfloat16), "sp").astype(jnp.float32),
        lax.psum(t_gain1.astype(jnp.bfloat16), "sp").astype(jnp.float32),
        lax.psum(t_wq.astype(jnp.bfloat16), "sp").astype(jnp.float32),
        lax.psum(t_wk.astype(jnp.bfloat16), "sp").astype(jnp.float32),
        lax.psum(t_wv.astype(jnp.bfloat16), "sp").astype(jnp.float32),
        lax.psum(t_wo.astype(jnp.bfloat16), "sp").astype(jnp.float32),
        lax.psum(t_rel.astype(jnp.bfloat16), "sp").astype(jnp.float32),
        lax.psum(t_gain2.astype(jnp.bfloat16), "sp").astype(jnp.float32),
        lax.psum(t_cq.astype(jnp.bfloat16), "sp").astype(jnp.float32),
        lax.psum(t_ck.astype(jnp.bfloat16), "sp").astype(jnp.float32),
        lax.psum(t_cv.astype(jnp.bfloat16), "sp").astype(jnp.float32),
        lax.psum(t_co.astype(jnp.bfloat16), "sp").astype(jnp.float32),
        lax.psum(t_gain3.astype(jnp.bfloat16), "sp").astype(jnp.float32),
        lax.psum(t_wg.astype(jnp.bfloat16), "sp").astype(jnp.float32),
        lax.psum(t_wu.astype(jnp.bfloat16), "sp").astype(jnp.float32),
        lax.psum(t_wd.astype(jnp.bfloat16), "sp").astype(jnp.float32),
    )
    return (enc_result, dec_result, grad_enc, grad_dec) + tuple(reduced)


HG, CORE, SP = "hg", "core", "sp"
BLOCK_PAD = 128
VMEM_BYTES = 60 << 20


def nt(left, right):
    return lax.dot_general(left, right, (((1,), (1,)), ((), ())), preferred_element_type=jnp.float32)


def tn(left, right):
    return lax.dot_general(left, right, (((0,), (0,)), ((), ())), preferred_element_type=jnp.float32)


def nn(left, right):
    return jnp.dot(left, right, preferred_element_type=jnp.float32)


def low(value):
    return value.astype(jnp.bfloat16)


def identity(size):
    rows = lax.broadcasted_iota(jnp.int32, (size, size), 0)
    cols = lax.broadcasted_iota(jnp.int32, (size, size), 1)
    return low(jnp.where(rows == cols, 1.0, 0.0))


def only_lanes(array, first, count):
    lanes = lax.broadcasted_iota(jnp.int32, array.shape, 1)
    return jnp.where((lanes >= first) & (lanes < first + count), array, jnp.zeros_like(array))


def gelu_and_slope(v):
    scale, cubic = math.sqrt(2.0 / math.pi), 0.044715
    t = jnp.tanh(scale * (v + cubic * v * v * v))
    return 0.5 * v * (1.0 + t), 0.5 * (1.0 + t) + 0.5 * v * (1.0 - t * t) * scale * (1.0 + 3.0 * cubic * v * v)


def norm_back(x, g, dn):
    r = lax.rsqrt(jnp.mean(x * x, axis=-1, keepdims=True) + EPSILON)
    w = dn * g
    dx = r * w - x * (r * r * r) * jnp.mean(w * x, axis=-1, keepdims=True)
    return dx, jnp.sum(dn * x * r, axis=0, keepdims=True)


def send(src, dst, send_sem, recv_sem, to):
    copy = pltpu.make_async_remote_copy(
        src_ref=src, dst_ref=dst, send_sem=send_sem, recv_sem=recv_sem, device_id=to, device_id_type=pl.DeviceIdType.MESH
    )
    copy.start()
    return copy


def arrived(dst, send_sem, recv_sem, to):
    pltpu.make_async_remote_copy(
        src_ref=dst, dst_ref=dst, send_sem=send_sem, recv_sem=recv_sem, device_id=to, device_id_type=pl.DeviceIdType.MESH
    ).wait_recv()


class Place:
    def __init__(self, groups, cores, parts):
        self.groups, self.cores, self.parts = groups, cores, parts
        self.group, self.core, self.part = lax.axis_index(HG), lax.axis_index(CORE), lax.axis_index(SP)

    def ahead(self, step):
        return lax.rem(self.group + step, self.groups)

    def behind(self, step):
        return lax.rem(self.group + self.groups - step, self.groups)

    def chip(self, group):
        return (group, self.core, self.part)

    def sibling(self):
        return (self.group, 1 - self.core, self.part)

    def plane(self, step):
        return lax.rem(self.part + step, self.parts)

    def plane_behind(self, step):
        return lax.rem(self.part + self.parts - step, self.parts)

    def at_plane(self, part):
        return (self.group, self.core, part)

    def first_token(self, number, block):
        return pl.multiple_of(((self.cores * number + self.core) * self.parts + self.part) * block, block)

    def greet(self, planes=False):
        barrier = pltpu.get_barrier_semaphore()
        partners = [self.chip(self.ahead(step)) for step in range(1, self.groups)] + [self.sibling()]
        if planes:
            partners += [self.at_plane(self.plane(step)) for step in range(1, self.parts)]
        for partner in partners:
            pl.semaphore_signal(barrier, inc=1, device_id=partner, device_id_type=pl.DeviceIdType.MESH)
        pl.semaphore_wait(barrier, len(partners))


def spread_start(place, buf, sent, got):
    mine = buf.at[place.group]
    return [
        send(mine, mine, sent.at[step], got.at[step], place.chip(place.ahead(step))) for step in range(1, place.groups)
    ]


def spread_wait(place, buf, sent, got):
    for step in range(1, place.groups):
        source = place.behind(step)
        arrived(buf.at[source], sent.at[step], got.at[step], place.chip(source))


def collect_start(place, partial, out_buf, in_buf, sent, got):
    out_buf[...] = low(partial).reshape(out_buf.shape)
    pending = []
    for step in range(1, place.groups):
        to = place.ahead(step)
        pending.append(send(out_buf.at[to], in_buf.at[place.group], sent.at[step], got.at[step], place.chip(to)))
    return pending


def collect_wait(place, out_buf, in_buf, sent, got):
    total = out_buf[place.group].astype(jnp.float32)
    for step in range(1, place.groups):
        source = place.behind(step)
        arrived(in_buf.at[source], sent.at[step], got.at[step], place.chip(source))
        total = total + in_buf[source].astype(jnp.float32)
    return total


def all_rows(buf):
    return buf[...].reshape(buf.shape[0] * buf.shape[1], buf.shape[2])


DMA = pltpu.SemaphoreType.DMA
IN_VMEM = pl.BlockSpec(memory_space=pltpu.VMEM)
ANYWHERE = pl.BlockSpec(memory_space=pl.ANY)


class Recut:
    def __init__(self, sizes, col_shapes, row_shapes):
        groups, cores, _ = sizes
        self.cols, self.rows = len(col_shapes), len(row_shapes)
        self.outs = [((groups, cores) + s[1:], jnp.bfloat16) for s in col_shapes]
        self.outs += [((cores,) + s, jnp.bfloat16) for s in row_shapes]
        cols = (self.cols, groups)
        self.scratch = [DMA(cols)] * 4 + [DMA((self.rows,))] * 2 + [DMA((self.cols + self.rows,))]

    def bind(self, ins, outs, scratch):
        self.col_refs, self.row_refs = ins[: self.cols], ins[self.cols :]
        self.col_outs, self.row_outs = outs[: self.cols], outs[self.cols :]
        self.sems = scratch
        self.pending, self.copies = [], []

    def begin(self, place):
        sent, got, relay_sent, relay_got, pair_sent, pair_got, local = self.sems
        group, core = place.group, place.core
        for index, (ref, out) in enumerate(zip(self.col_refs, self.col_outs)):
            slot = out.at[group, core]
            for step in range(1, place.groups):
                to = place.ahead(step)
                self.pending.append(send(ref.at[to], slot, sent.at[index, step], got.at[index, step], place.chip(to)))
            self.pending.append(send(ref.at[group], slot, relay_sent.at[index, 0], relay_got.at[index, 0], place.sibling()))
            self.copies.append(pltpu.make_async_copy(ref.at[group], slot, local.at[index]))
        for index, (ref, out) in enumerate(zip(self.row_refs, self.row_outs)):
            slot = out.at[core]
            self.pending.append(send(ref, slot, pair_sent.at[index], pair_got.at[index], place.sibling()))
            self.copies.append(pltpu.make_async_copy(ref, slot, local.at[self.cols + index]))
        for copy in self.copies:
            copy.start()

    def middle(self, place):
        sent, got, relay_sent, relay_got = self.sems[:4]
        for index, out in enumerate(self.col_outs):
            for step in range(1, place.groups):
                source = place.behind(step)
                slot = out.at[source, place.core]
                arrived(slot, sent.at[index, step], got.at[index, step], place.chip(source))
                self.pending.append(
                    send(slot, slot, relay_sent.at[index, step], relay_got.at[index, step], place.sibling())
                )

    def end(self, place):
        _, _, relay_sent, relay_got, pair_sent, pair_got, _ = self.sems
        for index, out in enumerate(self.col_outs):
            for step in range(place.groups):
                slot = out.at[place.behind(step), 1 - place.core]
                arrived(slot, relay_sent.at[index, step], relay_got.at[index, step], place.sibling())
        for index, out in enumerate(self.row_outs):
            arrived(out.at[1 - place.core], pair_sent.at[index], pair_got.at[index], place.sibling())
        for copy in self.copies:
            copy.wait()
        for copy in self.pending:
            copy.wait_send()


class GiveRows:
    def __init__(self, sizes, cols, rows):
        self.cols, self.rows = len(cols), len(rows)
        own = [(s[0],) + s[2:] for s in cols] + [(1,) + s[1:] for s in rows]
        self.outs = [(shape, jnp.bfloat16) for shape in own]
        self.scratch = [pltpu.VMEM(shape, jnp.bfloat16) for shape in own + own[: self.cols]]
        self.scratch += [DMA((self.cols, sizes[0]))] * 4 + [DMA((self.rows,))] * 2

    def bind(self, ins, outs, scratch):
        self.col_refs, self.row_refs = ins[: self.cols], ins[self.cols :]
        self.col_outs, self.row_outs = outs[: self.cols], outs[self.cols :]
        self.col_sibs, scratch = scratch[: self.cols], scratch[self.cols :]
        self.row_sibs, scratch = scratch[: self.rows], scratch[self.rows :]
        self.col_sums, self.sems = scratch[: self.cols], scratch[self.cols :]
        self.pending = []

    def begin(self, place):
        _, _, pair_sent, pair_got, row_sent, row_got = self.sems
        other = 1 - place.core
        for index, (ref, sib) in enumerate(zip(self.col_refs, self.col_sibs)):
            for step in range(place.groups):
                to = place.ahead(step)
                self.pending.append(
                    send(
                        ref.at[to, other], sib.at[to],
                        pair_sent.at[index, step], pair_got.at[index, step], place.sibling(),
                    )
                )
        for index, (ref, sib) in enumerate(zip(self.row_refs, self.row_sibs)):
            self.pending.append(send(ref.at[other], sib.at[0], row_sent.at[index], row_got.at[index], place.sibling()))

    def middle(self, place):
        sent, got, pair_sent, pair_got, row_sent, row_got = self.sems
        core = place.core
        for index, (ref, sib) in enumerate(zip(self.col_refs, self.col_sibs)):
            out, sums = self.col_outs[index], self.col_sums[index]
            for step in list(range(1, place.groups)) + [0]:
                to = place.ahead(step)
                arrived(sib.at[to], pair_sent.at[index, step], pair_got.at[index, step], place.sibling())
                both = low(ref[to, core].astype(jnp.float32) + sib[to].astype(jnp.float32))
                if step:
                    sums[to] = both
                    self.pending.append(
                        send(sums.at[to], out.at[place.group], sent.at[index, step], got.at[index, step], place.chip(to))
                    )
                else:
                    out[place.group] = both
        for index, (ref, sib) in enumerate(zip(self.row_refs, self.row_sibs)):
            arrived(sib.at[0], row_sent.at[index], row_got.at[index], place.sibling())
            self.row_outs[index][0] = low(ref[core].astype(jnp.float32) + sib[0].astype(jnp.float32))

    def end(self, place):
        sent, got = self.sems[:2]
        for index, out in enumerate(self.col_outs):
            for step in range(1, place.groups):
                source = place.behind(step)
                arrived(out.at[source], sent.at[index, step], got.at[index, step], place.chip(source))
        for copy in self.pending:
            copy.wait_send()


FOLD_PIECE = 56 * 1024


class FoldPlanes:
    def __init__(self, arrays, in_place=False):
        self.in_place = in_place
        self.operands = list(arrays)
        self.in_specs = [IN_VMEM] * len(arrays)
        self.outs = [(w.shape, jnp.bfloat16) for w in arrays]
        self.out_specs = [IN_VMEM] * len(arrays)
        self.pieces = []
        for index, w in enumerate(arrays):
            cuts = next(c for c in (1, 2, 3, 4, 6, 8) if w.shape[1] // c * w.shape[2] <= FOLD_PIECE or c == 8)
            if w.shape[0] * w.shape[1] * w.shape[2] <= FOLD_PIECE:
                self.pieces.append((index, slice(None), pl.ds(0, w.shape[1])))
                continue
            rows = w.shape[1] // cuts
            self.pieces += [(index, lead, pl.ds(c * rows, rows)) for lead in range(w.shape[0]) for c in range(cuts)]
        self.inner_done = self.across_done = 0
        self.scratch = [pltpu.VMEM(w.shape, jnp.bfloat16) for _ in range(1 if in_place else 2) for w in arrays] + [DMA((len(self.pieces),))] * 6

    def bind(self, ins, outs, scratch):
        count = len(self.outs)
        self.ins, self.totals = ins, outs
        self.inner = outs
        self.across, scratch = scratch[:count], scratch[count:]
        self.sums, self.sems = (ins, scratch) if self.in_place else (scratch[:count], scratch[count:])

    def copy(self, hop, number, src, dst, to):
        return pltpu.make_async_remote_copy(
            src_ref=src, dst_ref=dst, send_sem=self.sems[2 * hop].at[number], recv_sem=self.sems[2 * hop + 1].at[number],
            device_id=to, device_id_type=pl.DeviceIdType.MESH,
        )

    def hops(self, place, number):
        index, lead, rows = self.pieces[number]
        part = place.part
        inward, across, outward = (place.at_plane(p) for p in (1 + part // 3, 3 - part, 3 * (part - 1)))
        ref, inner, sums, other, total = (
            side[index].at[lead, rows] for side in (self.ins, self.inner, self.sums, self.across, self.totals)
        )
        return (ref, inner, inward), (sums, other, across), (total, total, outward)

    def roles(self, place):
        middle = (place.part == 1) | (place.part == 2)
        return pl.when(middle), pl.when(jnp.logical_not(middle))

    def start(self, place, numbers):
        @self.roles(place)[1]
        def _():
            for number in numbers:
                self.copy(0, number, *self.hops(place, number)[0]).start()

    def add_inner(self, place, number):
        inward, across, _ = self.hops(place, number)
        self.copy(0, number, *inward).wait_recv()
        across[0][...] = low(inward[0][...].astype(jnp.float32) + inward[1][...].astype(jnp.float32))
        self.copy(1, number, *across).start()

    def add_across(self, place, number):
        _, across, outward = self.hops(place, number)
        self.copy(1, number, *across).wait_recv()
        outward[0][...] = low(across[0][...].astype(jnp.float32) + across[1][...].astype(jnp.float32))
        self.copy(2, number, *outward).start()

    def of(self, first, last):
        return [n for n, piece in enumerate(self.pieces) if first <= piece[0] < last]

    def serve(self, place, inner, across):
        inners = list(range(self.inner_done, min(self.inner_done + inner, len(self.pieces))))
        self.inner_done += len(inners)
        others = list(range(self.across_done, min(self.across_done + across, len(self.pieces))))
        self.across_done += len(others)

        @self.roles(place)[0]
        def _():
            for turn in range(max(len(inners), len(others))):
                if turn < len(inners):
                    self.add_inner(place, inners[turn])
                if turn < len(others):
                    self.add_across(place, others[turn])

    def finish(self, place, lag):
        left = len(self.pieces) - self.inner_done
        behind = self.inner_done - self.across_done
        if behind > lag:
            self.serve(place, 0, behind - lag)
        self.serve(place, lag - min(behind, lag), 0)
        self.serve(place, left, left)
        self.serve(place, 0, len(self.pieces))

    def end(self, place):
        in_middle, at_end = self.roles(place)

        @at_end
        def _():
            for number in range(len(self.pieces)):
                inward, _, outward = self.hops(place, number)
                self.copy(0, number, *inward).wait_send()
                self.copy(2, number, *outward).wait_recv()

        @in_middle
        def _():
            for number in range(len(self.pieces)):
                _, across, outward = self.hops(place, number)
                self.copy(1, number, *across).wait_send()
                self.copy(2, number, *outward).wait_send()


def feed_back_part(n, dyb, gu_ref, down_ref):
    hidden = down_ref.shape[0]
    gu = nn(n, gu_ref[...])
    g, u = gu[:, :hidden], gu[:, hidden:]
    act, slope = gelu_and_slope(g)
    dh = nt(dyb, down_ref[...])
    return low(act * u), jnp.concatenate([low(dh * u * slope), low(dh * act)], axis=1)


def row_block(row):
    wide = jnp.broadcast_to(row.astype(jnp.float32), (8, row.shape[1]))
    return low(jnp.where(lax.broadcasted_iota(jnp.int32, wide.shape, 0) == 0, wide, 0.0))


def bucket_onehot(row, width, count, place_of):
    last = row.shape[1] - 1
    padded = jnp.concatenate([row.astype(jnp.float32), jnp.zeros((1, width - last - 1), jnp.float32)], axis=1)
    entry = lax.broadcasted_iota(jnp.int32, (width, width), 0)
    column = lax.broadcasted_iota(jnp.int32, (width, width), 1)
    pick = low(jnp.where(entry == jnp.clip(place_of(column), 0, last), 1.0, 0.0))
    bucket = nn(row_block(padded), pick)[0:1, :].astype(jnp.int32)
    return jnp.where(lax.broadcasted_iota(jnp.int32, (count, width), 0) == bucket, 1.0, 0.0)


def bias_mask(place, block, causal, rel_ref, turn, key_ids, query_ids, out_ref):
    heads, rows_total, lanes = out_ref.shape
    key_len = key_ids.shape[1]
    strip = block + 2 * BLOCK_PAD
    query = lax.broadcasted_iota(jnp.int32, (1, lanes), 1)
    start = ((place.cores * (query // block) + place.core) * place.parts + place.part) * block
    token = lax.broadcasted_iota(jnp.int32, (key_len, lanes), 0)
    of_key = tn(row_block(key_ids[...]), jnp.ones((8, lanes), jnp.bfloat16))
    of_query = nn(row_block(query_ids[...]), low(jnp.where(token == start + query % block, 1.0, 0.0)))[0:1, :]
    allowed = of_key == of_query
    if causal:
        allowed = allowed & (token <= start + query % block)
    inside = pl.ds(BLOCK_PAD, key_len)
    if rel_ref is None:
        out_ref[0, inside, :] = low(jnp.where(allowed, 0.0, NEGATIVE))
        return
    by_head = tn(rel_ref[...], turn)
    width = by_head.shape[1]
    pick_rows = lax.broadcasted_iota(jnp.int32, (8, by_head.shape[0]), 0)
    pick_cols = lax.broadcasted_iota(jnp.int32, (8, by_head.shape[0]), 1)
    picked = nn(low(jnp.where(pick_cols == pick_rows + place.group * heads, 1.0, 0.0)), low(by_head))
    places = lax.broadcasted_iota(jnp.int32, (rows_total, lanes), 0)
    for head in range(heads):
        row = picked[head : head + 1, :]
        left, right = row[:, width - 2 : width - 1], row[:, 0:1]
        out_ref[head] = low(jnp.where(places < start, left, right))
        wide = jnp.broadcast_to(row, (strip, width))
        for number in range(lanes // block):
            at = (number * block) % 128
            turned = pltpu.roll(wide, (width - (strip - 1) + at) % width, 1, stride=1, stride_axis=0)
            rows = pl.ds(place.first_token(number, block), strip)
            out_ref[head, rows, number * block : (number + 1) * block] = low(turned[:, at : at + block])
        out_ref[head, inside, :] = low(jnp.where(allowed, out_ref[head, inside, :].astype(jnp.float32), NEGATIVE))


def chunk_rows(kv_ref):
    return kv_ref.shape[1] * kv_ref.shape[2] * kv_ref.shape[3]


def key_side(kv_ref, chunk):
    return kv_ref[chunk].reshape(chunk_rows(kv_ref), kv_ref.shape[4])[:, : kv_ref.shape[4] // 2]


def value_side(kv_ref, chunk):
    lanes = kv_ref.shape[4]
    return kv_ref[chunk].reshape(chunk_rows(kv_ref), lanes)[:, lanes // 2 // 128 * 128 :]


def bias_rows(bm_ref, head, chunk, rows):
    at = pl.multiple_of(BLOCK_PAD + chunk * rows, 128)
    return bm_ref[head if bm_ref.shape[0] > 1 else 0, pl.ds(at, rows), :].astype(jnp.float32)


def mix_part(q, kv_ref, bm_ref, o_ref, lse_ref, s_ref, ot_ref):
    chunks, rows = kv_ref.shape[0], chunk_rows(kv_ref)
    queries, width = q.shape
    heads = width // HD
    across = [slice(head * queries, (head + 1) * queries) for head in range(heads)]
    masked_q = [only_lanes(q, head * HD, HD) for head in range(heads)]

    def first(chunk, tops):
        keys = key_side(kv_ref, chunk)
        inside = pl.ds(pl.multiple_of(chunk * rows, rows), rows)
        new = []
        for head in range(heads):
            scores = nt(keys, masked_q[head]) + bias_rows(bm_ref, head, chunk, rows)
            s_ref[inside, across[head]] = scores
            new.append(jnp.maximum(tops[head], jnp.max(scores, axis=0, keepdims=True)))
        return tuple(new)

    tops = lax.fori_loop(0, chunks, first, (jnp.full((1, queries), NEGATIVE, jnp.float32),) * heads)

    def second(chunk, carried):
        values = value_side(kv_ref, chunk)
        inside = pl.ds(pl.multiple_of(chunk * rows, rows), rows)
        lead = values.shape[1] - width
        values_t = low(nt(identity(values.shape[1]), values))
        new = []
        for head in range(heads):
            total, mixed = carried[head]
            weights = jnp.exp(s_ref[inside, across[head]] - tops[head])
            mixed = mixed + nn(values_t[lead + head * HD : lead + (head + 1) * HD], low(weights))
            new.append((total + jnp.sum(weights, axis=0, keepdims=True), mixed))
        return tuple(new)

    start = (jnp.zeros((1, queries), jnp.float32), jnp.zeros((HD, queries), jnp.float32))
    done = lax.fori_loop(0, chunks, second, (start,) * heads)
    for head in range(heads):
        total, mixed = done[head]
        lse_ref[:, across[head]] = tops[head] + jnp.log(total)
        ot_ref[head * HD : (head + 1) * HD, :] = low(mixed / total)
    o_ref[...] = low(nt(identity(queries), ot_ref[...]))


def keys_send(place, kv_ref, base, sent, got):
    mine = kv_ref.at[:, place.core, place.part]
    pending = [
        send(mine, mine, sent.at[base, step], got.at[base, step], place.at_plane(place.plane(step)))
        for step in range(1, place.parts)
    ]
    pending.append(send(mine, mine, sent.at[base + 1, 0], got.at[base + 1, 0], place.sibling()))
    return pending


def keys_relay(place, kv_ref, base, sent, got):
    pending = []
    for step in range(1, place.parts):
        source = place.plane_behind(step)
        slot = kv_ref.at[:, place.core, source]
        arrived(slot, sent.at[base, step], got.at[base, step], place.at_plane(source))
        pending.append(send(slot, slot, sent.at[base + 1, step], got.at[base + 1, step], place.sibling()))
    return pending


def keys_wait(place, kv_ref, base, sent, got):
    for step in range(place.parts):
        slot = kv_ref.at[:, 1 - place.core, place.plane_behind(step)]
        arrived(slot, sent.at[base + 1, step], got.at[base + 1, step], place.sibling())


def mix_back_part(place, q, do, o, kv_ref, lse_ref, bm_ref, dkv_ref, ds_ref):
    chunks, cores, parts, block, lanes = kv_ref.shape
    rows = chunk_rows(kv_ref)
    queries, width = q.shape
    heads = width // HD
    strip = block + 2 * BLOCK_PAD
    first_value = width // 128 * 128
    lead = width - first_value
    do_wide = jnp.concatenate([jnp.zeros((queries, lead), do.dtype), do], axis=1) if lead else do
    across = [slice(head * queries, (head + 1) * queries) for head in range(heads)]
    masked_q = [only_lanes(q, head * HD, HD) for head in range(heads)]
    masked_do = [only_lanes(do_wide, lead + head * HD, HD) for head in range(heads)]
    q_wide = masked_q
    if lead:
        none = jnp.zeros((queries, lead), q.dtype)
        q_wide = [jnp.concatenate([one, none], axis=1) for one in masked_q]
    of_head = lax.broadcasted_iota(jnp.int32, (8, width), 1) // HD
    of_row = lax.broadcasted_iota(jnp.int32, (8, width), 0)
    inners = lax.dot_general(
        jnp.where(of_head == of_row, 1.0, 0.0), do.astype(jnp.float32) * o.astype(jnp.float32),
        (((1,), (1,)), ((), ())), precision=HIGHEST, preferred_element_type=jnp.float32,
    )
    nothing = jnp.zeros((1, queries), jnp.float32)
    if ds_ref is not None:
        empty = jnp.zeros((BLOCK_PAD, heads * queries), jnp.bfloat16)
        ds_ref[0:BLOCK_PAD, :] = empty
        ds_ref[BLOCK_PAD + chunks * rows :, :] = empty
        of_lane = lax.broadcasted_iota(jnp.int32, (1, queries), 1) // block
        lane_start = ((cores * of_lane + place.core) * parts + place.part) * block

    def chunk_step(chunk, carried):
        at = pl.multiple_of(chunk * rows, rows)
        keys, values = key_side(kv_ref, chunk), value_side(kv_ref, chunk)
        keys_t = low(nt(identity(width), keys))
        new, dk, dv = [], None, None
        for head in range(heads):
            left, right, back = carried[head]
            scores = nt(keys, masked_q[head]) + bias_rows(bm_ref, head, chunk, rows)
            p = jnp.exp(scores - lse_ref[:, across[head]])
            dp = nt(values, masked_do[head])
            ds = low(p * (dp - inners[head : head + 1, :]))
            if ds_ref is not None:
                ds_ref[pl.ds(pl.multiple_of(BLOCK_PAD + at, 128), rows), across[head]] = ds
                wide = ds.astype(jnp.float32)
                places = lax.broadcasted_iota(jnp.int32, wide.shape, 0) + (at + BLOCK_PAD)
                left = left + jnp.sum(jnp.where(places < lane_start, wide, 0.0), axis=0, keepdims=True)
                right = right + jnp.sum(jnp.where(places >= lane_start + strip, wide, 0.0), axis=0, keepdims=True)
            back = back + nn(keys_t[head * HD : (head + 1) * HD], ds)
            new.append((left, right, back))
            more_k, more_v = nn(ds, q_wide[head]), nn(low(p), masked_do[head])
            dk, dv = (more_k, more_v) if dk is None else (dk + more_k, dv + more_v)
        if lead:
            shared = dk[:, first_value:] + dv[:, : 2 * lead]
            both = jnp.concatenate([dk[:, :first_value], shared, dv[:, 2 * lead :]], axis=1)
        else:
            both = jnp.concatenate([dk, dv], axis=1)
        dkv_ref[chunk] = low(both).reshape(dkv_ref.shape[1:])
        return tuple(new)

    start = (nothing, nothing, jnp.zeros((HD, queries), jnp.float32))
    done = lax.fori_loop(0, chunks, chunk_step, (start,) * heads)
    return [one[2] for one in done], [one[:2] for one in done]


def table_grads(place, block, done, ds_ref, ahead_ref, rel_ref):
    queries = done[0][0].shape[1]
    width = ahead_ref.shape[1]
    strip = block + 2 * BLOCK_PAD
    rows = lax.broadcasted_iota(jnp.int32, (block, block), 0)
    cols = lax.broadcasted_iota(jnp.int32, (block, block), 1)
    backwards = jnp.where(rows + cols == block - 1, 1.0, 0.0)
    at = lax.broadcasted_iota(jnp.int32, (1, width), 1)
    sums = []
    for head, (left, right) in enumerate(done):
        total = jnp.zeros((strip, block), jnp.float32)
        for number in range(queries // block):
            low_at = head * queries + number * block
            near = pl.ds(place.first_token(number, block), strip)
            total = total + ds_ref[near, low_at : low_at + block].astype(jnp.float32)
        turned = lax.dot_general(
            backwards, total, (((1,), (1,)), ((), ())), precision=HIGHEST, preferred_element_type=jnp.float32
        )
        turned = jnp.concatenate([turned, jnp.zeros((block, width - strip), jnp.float32)], axis=1)
        by_distance = jnp.sum(pltpu.roll(turned, 0, 1, stride=1, stride_axis=0), axis=0, keepdims=True)
        left, right = (jnp.sum(side, axis=1, keepdims=True) for side in (left, right))
        sums.append(by_distance + jnp.where(at == 0, left, 0.0) + jnp.where(at == width - 2, right, 0.0))
    sums = jnp.concatenate(sums + [jnp.zeros((8 - len(sums), width), jnp.float32)], axis=0)
    by_bucket = lax.dot_general(
        sums, ahead_ref[...], (((1,), (1,)), ((), ())), precision=HIGHEST, preferred_element_type=jnp.float32
    )
    head_rows = lax.broadcasted_iota(jnp.int32, (8, 128), 0)
    head_lanes = lax.broadcasted_iota(jnp.int32, (8, 128), 1)
    lanes_of = (head_lanes == head_rows + place.group * len(done)) & (head_rows < len(done))
    rel_ref[...] = lax.dot_general(
        by_bucket, jnp.where(lanes_of, 1.0, 0.0), (((0,), (0,)), ((), ())), precision=HIGHEST, preferred_element_type=jnp.float32
    )


class AttendBack:
    OPERANDS = 10

    def __init__(self, place, ins, grads, dkv, scratch, cross):
        self.place, self.cross = place, cross
        self.x, self.n, self.q, self.kv, self.o, self.lse, self.w, self.wo, self.bm, other = ins
        self.source, self.ahead = (other, None) if cross else (self.n, other)
        self.dw, self.dwo = grads
        self.dkv, self.sib, self.zout, self.zin, self.d_buf, self.pn, self.rn, self.dq = [dkv] + scratch[:7]
        scratch = scratch[7:]
        self.pm, self.rm = (scratch.pop(0), scratch.pop(0)) if cross else (None, None)
        self.ds = None if cross else scratch.pop(0)
        self.sent, self.got = scratch
        self.kv_width = self.kv.shape[4]
        self.pending = []

    def begin(self, dy):
        self.d_buf[self.place.group] = low(dy)
        self.pending += spread_start(self.place, self.d_buf, self.sent.at[0], self.got.at[0])

    def arrive(self):
        spread_wait(self.place, self.d_buf, self.sent.at[0], self.got.at[0])

    def compute(self):
        place, sent, got = self.place, self.sent, self.got
        do = low(nt(all_rows(self.d_buf), self.wo[...]))
        back, self.edges = mix_back_part(
            place, self.q[...], do, self.o[...], self.kv, self.lse, self.bm, self.dkv, self.ds
        )
        self.halves = send(self.dkv.at[:, 1 - place.core], self.sib, sent.at[1, 0], got.at[1, 0], place.sibling())
        self.dq[...] = low(nt(identity(self.q.shape[0]), low(jnp.concatenate(back, axis=0))))
        if self.cross:
            share = nt(self.dq[...], self.w[:, self.kv_width :])
            self.pending += collect_start(place, share, self.pn, self.rn, sent.at[3], got.at[3])

    def exchange(self):
        place, sent, got = self.place, self.sent, self.got
        arrived(self.sib, sent.at[1, 0], got.at[1, 0], place.sibling())
        for step in list(range(1, place.parts)) + [0]:
            to = place.plane(step)
            self.zout[to] = low(self.dkv[:, place.core, to].astype(jnp.float32) + self.sib[:, to].astype(jnp.float32))
            if step:
                self.pending.append(
                    send(self.zout.at[to], self.zin.at[place.part], sent.at[2, step], got.at[2, step], place.at_plane(to))
                )

        self.halves.wait_send()

    def by_rows(self, grad):
        return low(grad).reshape(self.dw.shape[:3] + grad.shape[1:])

    def query_grads(self, rel):
        self.dwo[...] = low(tn(self.o[...], all_rows(self.d_buf))).reshape(self.dwo.shape)
        self.dw[:, :, :, self.kv_width :] = self.by_rows(tn(self.n[...], self.dq[...]))
        if not self.cross:
            table_grads(self.place, self.x.shape[0], self.edges, self.ds, self.ahead, rel)

    def keys(self):
        place, sent, got = self.place, self.sent, self.got
        total = self.zout[place.part].astype(jnp.float32)
        for step in range(1, place.parts):
            source = place.plane_behind(step)
            arrived(self.zin.at[source], sent.at[2, step], got.at[2, step], place.at_plane(source))
            total = total + self.zin[source].astype(jnp.float32)
        self.dkv_own = low(total).reshape(self.q.shape[0], self.kv_width)
        share = nt(self.dkv_own, self.w[:, : self.kv_width])
        if self.cross:
            self.pending += collect_start(place, share, self.pm, self.rm, sent.at[4], got.at[4])
        else:
            share = share + nt(self.dq[...], self.w[:, self.kv_width :])
            self.pending += collect_start(place, share, self.pn, self.rn, sent.at[3], got.at[3])

    def key_grads(self):
        self.dw[:, :, :, : self.kv_width] = self.by_rows(tn(self.source[...], self.dkv_own))

    def source_grad(self):
        return collect_wait(self.place, self.pm, self.rm, self.sent.at[4], self.got.at[4])

    def normed_grad(self):
        return collect_wait(self.place, self.pn, self.rn, self.sent.at[3], self.got.at[3])

    def wait(self):
        for copy in self.pending:
            copy.wait_send()


def attend_back_scratch(sizes, block, model, width, cross):
    groups, cores, parts = sizes
    tokens = groups * block
    turned, buffer = (parts, groups, block, 2 * width), (groups, block, model)
    shapes = [(groups, parts, block, 2 * width), turned, turned, buffer, buffer, buffer, (tokens, width)]
    if cross:
        shapes += [buffer, buffer]
    else:
        shapes.append((cores * parts * tokens + 2 * BLOCK_PAD, width // HD * tokens))
    return [pltpu.VMEM(shape, jnp.bfloat16) for shape in shapes] + [DMA((5, max(groups, parts)))] * 2


class Taker:
    def __init__(self, refs):
        self.refs = list(refs)

    def __call__(self, count):
        taken, self.refs = self.refs[:count], self.refs[count:]
        return taken


def decoder_back_kernel(sizes, streams, gain_at, plans, *refs):
    give_a, give_b, give_c, fold, cross_scratch, self_scratch = plans
    dec1, dec2, dec3, enc2, final = gain_at
    take = Taker(refs)
    gains, cx, dec_cot, dec_gu, dec_down = take(5)
    cross_ins, self_ins = take(AttendBack.OPERANDS), take(AttendBack.OPERANDS)
    ex, enc_out, enc_cot, en2, gu, down = take(6)
    dec_out, dec_in_grad, grad_ex, dg_d1, dg_d2, dg_d3, dg_e2, dg_ef, rel_d, dw_d, dwo_d = take(11)
    totals, b_outs, c_outs = take(len(fold.outs)), take(len(give_b.outs)), take(len(give_c.outs))
    dw_c, dwo_c, dgu, ddown, dgu_a, ddown_a, dkv, grad_cx, grad_dx = take(9)
    n_buf, d_buf, py, ry, f_buf, pf, rf, f_sent, f_got = take(9)
    place = Place(*sizes)
    cross = AttendBack(place, cross_ins, (dw_c, dwo_c), dkv, take(len(cross_scratch)), True)
    own = AttendBack(place, self_ins, (dw_d, dwo_d), dkv, take(len(self_scratch)), False)
    a_outs = take(len(give_a.outs))
    give_a.bind([dgu_a, ddown_a], a_outs, take(len(give_a.scratch)))
    fold.bind(a_outs, totals, take(len(fold.scratch)))
    give_b.bind([dw_c, dwo_c], b_outs, take(len(give_b.scratch)))
    give_c.bind([dgu, ddown], c_outs, take(len(give_c.scratch)))
    pn, rn = own.pn, own.rn
    place.greet(planes=True)
    d_buf[place.group] = dec_cot[...]
    pending = spread_start(place, d_buf, f_sent.at[2], f_got.at[2])
    n_buf[place.group] = low(rms_norm(cx[...], gains[dec3]))
    pending += spread_start(place, n_buf, f_sent.at[3], f_got.at[3])
    spread_wait(place, d_buf, f_sent.at[2], f_got.at[2])
    spread_wait(place, n_buf, f_sent.at[3], f_got.at[3])
    n, dyb = all_rows(n_buf), all_rows(d_buf)
    h, dgu_value = feed_back_part(n, dyb, dec_gu, dec_down)
    leaving = collect_start(place, nt(dgu_value, dec_gu[...]), pn, rn, f_sent.at[4], f_got.at[4])
    dgu_a[...] = low(tn(n, dgu_value)).reshape(dgu_a.shape)
    ddown_a[...] = low(tn(h, dyb)).reshape(ddown_a.shape)
    dn = collect_wait(place, pn, rn, f_sent.at[4], f_got.at[4])
    for copy in leaving:
        copy.wait_send()
    back, dg = norm_back(cx[...], gains[dec3], dn)
    dg_d3[...] = dg
    grad_cx[...] = dec_cot[...].astype(jnp.float32) + back
    cross.begin(grad_cx[...])
    pending += collect_start(place, nn(h, dec_down[...]), py, ry, f_sent.at[5], f_got.at[5])
    give_a.begin(place)
    give_a.middle(place)
    streams.need(5, 15)
    cross.arrive()
    cross.compute()
    cross.exchange()
    give_a.end(place)
    fold.start(place, fold.of(0, len(a_outs)))
    back, dg = norm_back(cross.x[...].astype(jnp.float32), gains[dec2], cross.normed_grad())
    dg_d2[...] = dg
    grad_dx[...] = grad_cx[...] + back
    own.begin(grad_dx[...])
    cross.query_grads(None)
    streams.need(15, 25)
    dec_out[...] = cx[...] + collect_wait(place, py, ry, f_sent.at[5], f_got.at[5])
    own.arrive()
    own.compute()
    cross.keys()
    own.exchange()
    fold.serve(place, 4, 0)
    cross.key_grads()
    give_b.begin(place)
    streams.need(25, 31)
    back, dg = norm_back(enc_out[...], gains[final], cross.source_grad())
    dg_ef[...] = dg
    dy = enc_cot[...].astype(jnp.float32) + back
    f_buf[place.group] = low(dy)
    pending += spread_start(place, f_buf, f_sent.at[0], f_got.at[0])
    give_b.middle(place)
    own.query_grads(rel_d)
    fold.serve(place, 3, 2)
    spread_wait(place, f_buf, f_sent.at[0], f_got.at[0])
    n, dyb = en2[...], all_rows(f_buf)
    h, dgu_value = feed_back_part(n, dyb, gu, down)
    pending += collect_start(place, nt(dgu_value, gu[...]), pf, rf, f_sent.at[1], f_got.at[1])
    dgu[...] = low(tn(n, dgu_value)).reshape(dgu.shape)
    ddown[...] = low(tn(h, dyb)).reshape(ddown.shape)
    give_c.begin(place)
    fold.serve(place, 3, 3)
    dn = collect_wait(place, pf, rf, f_sent.at[1], f_got.at[1])
    back, dg = norm_back(ex[...], gains[enc2], dn)
    dg_e2[...] = dg
    grad_ex[...] = dy + back
    give_c.middle(place)
    own.keys()
    own.key_grads()
    fold.finish(place, 2)
    back, dg = norm_back(own.x[...].astype(jnp.float32), gains[dec1], own.normed_grad())
    dg_d1[...] = dg
    dec_in_grad[...] = grad_dx[...] + back
    give_b.end(place)
    give_c.end(place)
    fold.end(place)
    cross.wait()
    own.wait()
    for copy in pending:
        copy.wait_send()


def encoder_back_kernel(sizes, streams, gain_at, plans, *refs):
    give_d, give_e, fold, before, scratch = plans
    take = Taker(refs)
    gains, grad_ex = take(2)
    ins = take(AttendBack.OPERANDS)
    dg_d1, dg_d2, dg_d3, dg_e2, dg_ef, rel_d = take(6)
    ready, d_ins = take(before), take(give_d.cols + give_d.rows)
    (enc_in_grad,) = take(1)
    totals = take(len(fold.outs))
    dw_e, dwo_e, small, dkv, rel_e = take(5)
    place = Place(*sizes)
    own = AttendBack(place, ins, (dw_e, dwo_e), dkv, take(len(scratch)), False)
    d_outs, e_outs = take(len(give_d.outs)), take(len(give_e.outs))
    give_d.bind(d_ins, d_outs, take(len(give_d.scratch)))
    give_e.bind([dw_e, small, dwo_e], e_outs, take(len(give_e.scratch)))
    fold.bind(ready + d_outs + e_outs, totals, take(len(fold.scratch)))
    of_c = fold.of(0, before)
    of_d, of_e = fold.of(before, before + len(d_outs)), fold.of(before + len(d_outs), len(fold.outs))
    place.greet(planes=True)
    own.begin(grad_ex[...])
    fold.start(place, of_c)
    give_d.begin(place)
    give_d.middle(place)
    streams.need(2, 12)
    own.arrive()
    fold.serve(place, 3, 0)
    own.compute()
    fold.serve(place, 3, 3)
    own.exchange()
    give_d.end(place)
    fold.start(place, of_d)
    fold.serve(place, 3, 3)
    own.query_grads(rel_e)
    fold.serve(place, 3, 3)
    own.keys()
    fold.serve(place, len(of_c) - 12, 3)
    own.key_grads()
    dn = own.normed_grad()
    back, dg_e1 = norm_back(own.x[...].astype(jnp.float32), gains[gain_at], dn)
    enc_in_grad[...] = grad_ex[...] + back
    devices = place.groups * place.cores
    share = dg_e1.shape[1] // devices
    small[...] = jnp.zeros_like(small)
    all_gains = jnp.concatenate([dg_e1, dg_e2[...], dg_ef[...], dg_d1[...], dg_d2[...], dg_d3[...]], axis=0)
    count = all_gains.shape[0]
    each = rel_e.shape[0] // devices
    tables = [rel_e[...].reshape(devices, each, 128), rel_d[...].reshape(devices, each, 128)]
    for device in range(devices):
        piece = jnp.concatenate([all_gains[:, device * share : (device + 1) * share], jnp.zeros((count, 128 - share), jnp.float32)], axis=1)
        rows = jnp.concatenate([piece, tables[0][device], tables[1][device]], axis=0)
        rows = jnp.concatenate([rows, jnp.zeros((16 - rows.shape[0], 128), jnp.float32)], axis=0)
        small[device // place.cores, device % place.cores] = low(rows)
    give_e.begin(place)
    fold.serve(place, 2, len(of_c) - 12)
    give_e.middle(place)
    fold.serve(place, len(of_d) - 2, 2)
    give_e.end(place)
    fold.start(place, of_e)
    fold.finish(place, 2)
    fold.end(place)
    own.wait()


class Streams:
    def __init__(self, fetches, stores):
        self.fetches, self.stores = fetches, stores
        self.stored = []

    def begin(self):
        for copy in self.fetches.values():
            copy.start()

    def need(self, first, last):
        for index in [i for i in self.fetches if first <= i < last]:
            self.fetches.pop(index).wait()

    def store(self, *indices):
        for index in indices:
            if index in self.stores:
                copy = self.stores.pop(index)
                copy.start()
                self.stored.append(copy)

    def end(self):
        self.need(0, 1 << 20)
        self.store(*sorted(self.stores))
        for copy in self.stored:
            copy.wait()


LARGE = 300_000


def size_of(shape, dtype):
    return math.prod(shape) * jnp.dtype(dtype).itemsize


def fused(sizes, collective_id, kernel, operands, outs, scratch, fetched=(0, 0), stored=False):
    late = [i for i, w in enumerate(operands) if fetched[0] <= i < fetched[1] and size_of(w.shape, w.dtype) > LARGE]
    early = [i for i, (shape, dtype) in enumerate(outs) if stored and size_of(shape, dtype) > LARGE]
    held = [pltpu.VMEM(operands[i].shape, operands[i].dtype) for i in late]
    held += [pltpu.VMEM(*outs[i]) for i in early]
    sems = [DMA((max(1, len(late)),)), DMA((max(1, len(early)),))]

    def body(*refs):
        take = Taker(refs)
        ins, results, own = take(len(operands)), take(len(outs)), take(len(scratch))
        late_refs, early_refs = take(len(late)), take(len(early))
        late_sem, early_sem = take(2)
        fetches, stores = {}, {}
        for number, index in enumerate(late):
            fetches[index] = pltpu.make_async_copy(ins[index], late_refs[number], late_sem.at[number])
            ins[index] = late_refs[number]
        for number, index in enumerate(early):
            stores[index] = pltpu.make_async_copy(early_refs[number], results[index], early_sem.at[number])
            results[index] = early_refs[number]
        streams = Streams(fetches, stores)
        streams.begin()
        kernel(sizes, streams, *ins, *results, *own)
        streams.end()

    return pl.pallas_call(
        body,
        out_shape=tuple(jax.ShapeDtypeStruct(shape, dtype) for shape, dtype in outs),
        in_specs=[ANYWHERE if i in late else IN_VMEM for i in range(len(operands))],
        out_specs=tuple(ANYWHERE if i in early else IN_VMEM for i in range(len(outs))),
        scratch_shapes=list(scratch) + held + sems,
        compiler_params=pltpu.CompilerParams(collective_id=collective_id, has_side_effects=True, vmem_limit_bytes=VMEM_BYTES),
        cost_estimate=pl.CostEstimate(flops=20_000_000_000, bytes_accessed=10_000_000, transcendentals=0),
    )(*operands)


def kept_operands(x, kept, w, wo, ahead):
    _, n, q, kv, o, lse, bm, memory = kept
    return [x, n, q, kv, o, lse, w, wo, bm, memory if ahead is None else ahead]


def buffers_of(shapes):
    return [pltpu.VMEM(shape, jnp.bfloat16) for shape in shapes]


def decoder_back(sizes, collective_id, gains, gain_at, last, cross, own, feed):
    groups, cores, parts = sizes
    f32, bf16 = jnp.float32, jnp.bfloat16
    block, model = last[0].shape
    share = model // (groups * cores)
    width = cross[3].shape[0]
    kv = cross[1][3].shape
    hidden = feed[5].shape[0]
    attention = [(groups, cores, share, 3 * width)], [(cores, width // cores, model)]
    feeds = [(groups, cores, share, 2 * hidden)], [(cores, hidden // cores, model)]
    give_a, give_b, give_c = GiveRows(sizes, *feeds), GiveRows(sizes, *attention), GiveRows(sizes, *feeds)
    fold = FoldPlanes([jax.ShapeDtypeStruct(shape, dtype) for shape, dtype in give_a.outs], True)
    cross_scratch = attend_back_scratch(sizes, block, model, width, True)
    self_scratch = attend_back_scratch(sizes, block, model, width, False)
    plans = (give_a, give_b, give_c, fold, cross_scratch, self_scratch)
    operands = [gains, *last] + kept_operands(*cross) + kept_operands(*own) + list(feed)
    token, gain = ((block, model), f32), ((1, model), f32)
    outs = [token, token, token, gain, gain, gain, gain, gain, ((own[4].shape[0], 128), f32)]
    outs += [(attention[0][0], bf16), (attention[1][0], bf16)] + fold.outs + give_b.outs + give_c.outs
    buffer = (groups, block, model)
    scratch = buffers_of(attention[0] + attention[1] + (feeds[0] + feeds[1]) * 2 + [kv]) + [pltpu.VMEM((block, model), f32)] * 2
    scratch += buffers_of([buffer] * 7) + [DMA((6, groups))] * 2 + cross_scratch + self_scratch
    scratch += buffers_of([shape for shape, _ in give_a.outs])
    scratch += give_a.scratch + fold.scratch + give_b.scratch + give_c.scratch
    got = Taker(fused(sizes, collective_id, lambda s, t, *refs: decoder_back_kernel(s, t, gain_at, plans, *refs), operands, outs, scratch, (5, 31)))
    first = got(9)
    return first, got(2), got(len(fold.outs)), got(len(give_b.outs)), got(len(give_c.outs))


def encoder_back(sizes, collective_id, gains, gain_at, grad_ex, own, small_grads, ready, grads_d):
    groups, cores, parts = sizes
    f32 = jnp.float32
    block, model = grad_ex.shape
    share = model // (groups * cores)
    width = own[3].shape[0]
    kv = own[1][3].shape
    give_d = GiveRows.__new__(GiveRows)
    give_d = GiveRows(sizes, [grads_d[0].shape], [grads_d[1].shape])
    cols = [(groups, cores, share, 3 * width), (groups, cores, 16, 128)]
    rows = [(cores, width // cores, model)]
    give_e = GiveRows(sizes, cols, rows)
    all_outs = [jax.ShapeDtypeStruct(shape, dtype) for shape, dtype in give_d.outs + give_e.outs]
    fold = FoldPlanes(list(ready) + all_outs)
    scratch = attend_back_scratch(sizes, block, model, width, False)
    plans = (give_d, give_e, fold, len(ready), scratch)
    operands = [gains, grad_ex] + kept_operands(*own) + list(small_grads) + list(ready) + list(grads_d)
    buffers = buffers_of([cols[0], rows[0], cols[1], kv]) + [pltpu.VMEM((own[4].shape[0], 128), f32)] + scratch
    buffers += buffers_of([shape for shape, _ in give_d.outs]) + buffers_of([shape for shape, _ in give_e.outs])
    buffers += give_d.scratch + give_e.scratch + fold.scratch
    outs = [((block, model), f32)] + fold.outs
    got = Taker(fused(sizes, collective_id, lambda s, t, *refs: encoder_back_kernel(s, t, gain_at, plans, *refs), operands, outs, buffers, (2, 12)))
    return got(1)[0], got(len(ready)), got(2), got(3)


def unpack_kernel(kinds, *refs):
    take = Taker(refs)
    ins = take(len(kinds))
    for ref, pieces in zip(ins, kinds):
        if pieces < 0:
            take(1)[0][...] = ref[...]
            continue
        value = ref[...].astype(jnp.float32)
        if pieces == 0:
            take(1)[0][...] = value[0]
            continue
        each = value.shape[2] // pieces
        for piece, out in enumerate(take(pieces)):
            out[...] = jnp.concatenate([one[:, piece * each : (piece + 1) * each] for one in value], axis=1)


def unpack(arrays, kinds):
    outs = []
    for array, pieces in zip(arrays, kinds):
        if pieces < 0:
            outs.append(jax.ShapeDtypeStruct(array.shape, array.dtype))
        elif pieces == 0:
            outs.append(jax.ShapeDtypeStruct(array.shape[1:], jnp.float32))
        for _ in range(pieces):
            outs.append(jax.ShapeDtypeStruct((array.shape[1], array.shape[0] * array.shape[2] // pieces), jnp.float32))
    return pl.pallas_call(
        functools.partial(unpack_kernel, kinds),
        out_shape=tuple(outs),
        in_specs=[IN_VMEM] * len(arrays),
        out_specs=(IN_VMEM,) * len(outs),
        compiler_params=pltpu.CompilerParams(vmem_limit_bytes=VMEM_BYTES),
    )(*arrays)


class AttendForward:
    def __init__(self, place, outs, bufs, sems, base):
        self.place, self.base = place, base
        self.x, self.n, self.q, self.kv, self.o, self.lse, self.bm = outs
        self.p_buf, self.r_buf = bufs
        self.sent, self.got = sems

    def keys(self, kv):
        kv_ref = self.kv
        kv_ref[:, self.place.core, self.place.part] = kv.reshape(kv_ref.shape[0], kv_ref.shape[3], kv_ref.shape[4])
        return keys_send(self.place, kv_ref, self.base, self.sent, self.got)

    def mix(self, wo, s_ref, ot_ref):
        place, base = self.place, self.base
        pending = keys_relay(place, self.kv, base, self.sent, self.got)
        keys_wait(place, self.kv, base, self.sent, self.got)
        mix_part(self.q[...], self.kv, self.bm, self.o, self.lse, s_ref, ot_ref)
        share = nn(self.o[...], wo)
        return pending + collect_start(place, share, self.p_buf, self.r_buf, self.sent.at[base + 2], self.got.at[base + 2])

    def add(self, x):
        total = collect_wait(self.place, self.p_buf, self.r_buf, self.sent.at[self.base + 2], self.got.at[self.base + 2])
        self.x[...] = x + total


def pack_columns(pack, refs):
    groups = pack.shape[0]
    for group in range(groups):
        parts = [ref[:, group * (ref.shape[1] // groups) : (group + 1) * (ref.shape[1] // groups)] for ref in refs]
        pack[group] = jnp.concatenate([part.astype(jnp.float32) for part in parts], axis=1).astype(pack.dtype)


def flat(ref):
    rows = math.prod(ref.shape[:-1])
    return ref[...].reshape(rows, ref.shape[-1])


def forward_kernel(sizes, streams, counts, recuts, *refs):
    enc_first, dec_first, later, last = recuts
    gain_count, each = counts
    take = Taker(refs)
    enc_in, dec_in, small, enc_ids, dec_ids, buckets = take(6)
    enc_w, dec_w, cross_w, enc_gate_up, dec_gate_up = take(3), take(3), take(3), take(2), take(2)
    enc_wo_own, dec_wo_own, cross_wo_own, enc_wd_own, dec_wd_own = take(5)
    gains, enc_kvq, dec_kvq, enc_gu, cross_kvq, dec_gu, enc_wo, dec_wo, enc_wd, cross_wo, dec_wd = take(11)
    enc_outs, dec_outs, cross_outs = take(7), take(7), take(7)
    memory_all, enc_out, en2, ahead = take(4)
    small_pack, enc_pack, dec_pack, cross_pack, enc_gu_pack, dec_gu_pack, small_all, rels = take(8)
    s_ref, ot_ref = take(2)
    x_e, x_d, n_buf, d_buf, m_buf, f_p, f_r = take(7)
    bufs = [take(2) for _ in range(3)]
    sent, got = take(2)
    enc_first.bind([small_pack, enc_pack, enc_wo_own], [small_all, enc_kvq, enc_wo], take(len(enc_first.scratch)))
    dec_first.bind([dec_pack, dec_wo_own], [dec_kvq, dec_wo], take(len(dec_first.scratch)))
    later.bind(
        [enc_gu_pack, cross_pack, enc_wd_own, cross_wo_own], [enc_gu, cross_kvq, enc_wd, cross_wo], take(len(later.scratch))
    )
    last.bind([dec_gu_pack, dec_wd_own], [dec_gu, dec_wd], take(len(last.scratch)))
    place = Place(*sizes)
    enc, dec, cross = [
        AttendForward(place, outs, bufs[i], (sent, got), 6 + 3 * i) for i, outs in enumerate((enc_outs, dec_outs, cross_outs))
    ]
    for group in range(place.groups):
        small_pack[group] = small[...]
    pack_columns(enc_pack, enc_w)
    place.greet(planes=True)
    x_e[place.group] = enc_in[...]
    x_d[place.group] = dec_in[...]
    enc_first.begin(place)
    pending = spread_start(place, x_e, sent.at[0], got.at[0])
    pack_columns(dec_pack, dec_w)
    dec_first.begin(place)
    pending += spread_start(place, x_d, sent.at[1], got.at[1])
    pack_columns(enc_gu_pack, enc_gate_up)
    pack_columns(cross_pack, cross_w)
    pack_columns(dec_gu_pack, dec_gate_up)
    enc_first.middle(place)
    enc_first.end(place)

    devices = place.groups * place.cores
    share = enc_in.shape[1] // devices
    rows, model = small.shape[0], enc_in.shape[1]
    lane = lax.broadcasted_iota(jnp.int32, (128, model), 0)
    column = lax.broadcasted_iota(jnp.int32, (128, model), 1)
    bucket = lax.broadcasted_iota(jnp.int32, (devices * each, rows), 0)
    row = lax.broadcasted_iota(jnp.int32, (devices * each, rows), 1)
    every_gain, tables = 0.0, [0.0, 0.0]
    for device in range(devices):
        table = small_all[device // place.cores, device % place.cores]
        to_column = (column == lane + device * share) & (lane < share)
        every_gain = every_gain + nn(table, low(jnp.where(to_column, 1.0, 0.0)))
        for index in range(2):
            from_row = row == bucket - device * each + gain_count + index * each
            from_row = from_row & (bucket // each == device)
            tables[index] = tables[index] + nn(low(jnp.where(from_row, 1.0, 0.0)), table)
    for index in range(gain_count):
        gains[index] = every_gain[index : index + 1, :]
    for index in range(2):
        rels[index] = low(tables[index])

    def project(one, x_buf, gain_at, w, number):
        spread_wait(place, x_buf, sent.at[number], got.at[number])
        kv_width = one.kv.shape[4]
        n = low(rms_norm(all_rows(x_buf).astype(jnp.float32), gains[gain_at]))
        one.n[...] = n
        both = low(nn(n, flat(w)))
        copies = one.keys(both[:, :kv_width])
        one.q[...] = both[:, kv_width:]
        return copies

    pending += project(enc, x_e, 0, enc_kvq, 0)
    dec_first.middle(place)
    dec_first.end(place)
    pending += project(dec, x_d, 3, dec_kvq, 1)
    later.begin(place)
    block = enc_in.shape[0]
    reach, width = buckets.shape[1] // 2, ahead.shape[2]
    turns = []
    for index in range(2):
        row, count = buckets[index : index + 1, :], ahead.shape[1]
        ahead[index] = bucket_onehot(row, width, count, lambda column: column - (block - 1))
        turns.append(low(bucket_onehot(row, width, count, lambda column: 2 * reach + block - 1 - column)))
    bias_mask(place, block, False, rels.at[0], turns[0], enc_ids, enc_ids, enc.bm)
    streams.store(1, 2, 12, 19, 17)
    bias_mask(place, block, True, rels.at[1], turns[1], dec_ids, dec_ids, dec.bm)
    streams.store(24)
    pending += enc.mix(flat(enc_wo), s_ref, ot_ref)
    streams.store(14)
    bias_mask(place, block, False, None, None, enc_ids, dec_ids, cross.bm)
    streams.store(31)
    enc.add(enc_in[...].astype(jnp.float32))
    ex = enc.x[...]
    n_buf[place.group] = low(rms_norm(ex, gains[1]))
    pending += spread_start(place, n_buf, sent.at[2], got.at[2])
    later.middle(place)
    later.end(place)
    streams.store(3, 4, 8)
    spread_wait(place, n_buf, sent.at[2], got.at[2])
    en2[...] = all_rows(n_buf)
    w_down = flat(enc_wd)
    hidden = w_down.shape[0]
    gu = nn(en2[...], flat(enc_gu))
    h = low(gelu_and_slope(gu[:, :hidden])[0] * gu[:, hidden:])
    pending += collect_start(place, nn(h, w_down), f_p, f_r, sent.at[5], got.at[5])
    enc_out[...] = ex + collect_wait(place, f_p, f_r, sent.at[5], got.at[5])
    m_buf[place.group] = low(rms_norm(enc_out[...], gains[2]))
    pending += spread_start(place, m_buf, sent.at[4], got.at[4])
    kv_width = cross.kv.shape[4]
    model = enc_in.shape[1]
    spread_wait(place, m_buf, sent.at[4], got.at[4])
    memory_all[...] = all_rows(m_buf)
    pending += cross.keys(low(nn(memory_all[...], cross_kvq[:, :, :, :kv_width].reshape(model, kv_width))))
    pending += dec.mix(flat(dec_wo), s_ref, ot_ref)
    streams.store(21)
    dec.add(dec_in[...].astype(jnp.float32))
    d_buf[place.group] = low(rms_norm(dec.x[...], gains[4]))
    pending += spread_start(place, d_buf, sent.at[3], got.at[3])
    last.begin(place)
    spread_wait(place, d_buf, sent.at[3], got.at[3])
    cross.n[...] = all_rows(d_buf)
    cross.q[...] = low(nn(cross.n[...], cross_kvq[:, :, :, kv_width:].reshape(model, kv_width // 2)))
    pending += cross.mix(flat(cross_wo), s_ref, ot_ref)
    streams.store(28, 26, 32, 34)
    last.middle(place)
    cross.add(dec.x[...])
    last.end(place)
    for copy in pending:
        copy.wait_send()


def forward(sizes, collective_id, enc_in, dec_in, small, counts, ids, buckets, weights):
    groups, cores, parts = sizes
    f32, bf16 = jnp.float32, jnp.bfloat16
    block, model = enc_in.shape
    attention, feeds, rows = weights[:3], weights[3:5], weights[5]
    share = attention[0][0].shape[0]
    width = rows[0].shape[0] * cores
    tokens = groups * block
    keys = cores * parts * tokens
    heads = width // HD
    kvq, gu = (groups, share, 3 * width), (groups, share, 2 * feeds[0][0].shape[1] // groups)
    wo, wd = rows[0].shape, rows[3].shape
    small_shape = (groups,) + small.shape
    recuts = (
        Recut(sizes, [small_shape, kvq], [wo]), Recut(sizes, [kvq], [wo]), Recut(sizes, [gu, kvq], [wd, wo]), Recut(sizes, [gu], [wd])
    )

    def both(shape):
        return ((groups, cores) + shape[1:], bf16)

    def pair(shape):
        return ((cores,) + shape, bf16)

    token = ((block, model), f32)
    outs = [((counts[0], 1, model), f32), both(kvq), both(kvq), both(gu), both(kvq), both(gu)]
    outs += [pair(wo), pair(wo), pair(wd), pair(wo), pair(wd)]
    for number in range(3):
        outs += [
            token, ((tokens, model), bf16), ((tokens, width), bf16), ((groups, cores, parts, block, 2 * width), bf16),
            ((tokens, width), bf16), ((1, heads * tokens), f32),
            ((1 if number == 2 else heads, keys + 2 * BLOCK_PAD, tokens), bf16),
        ]
    bucket_count = groups * cores * counts[1]
    outs += [((tokens, model), bf16), token, ((tokens, model), bf16), ((2, bucket_count, buckets.shape[1] - 1 + 2 * block), f32)]
    buffer = (groups, block, model)
    scratch = buffers_of([small_shape, kvq, kvq, kvq, gu, gu, both(small_shape)[0], (2, bucket_count, 128)])
    scratch += [pltpu.VMEM((keys, heads * tokens), f32)] + buffers_of([(width, tokens)] + [buffer] * 13)
    scratch += [DMA((15, max(groups, parts)))] * 2 + [s for one in recuts for s in one.scratch]
    operands = [enc_in, dec_in, small, *ids, buckets] + [w for each in attention for w in each]
    operands += [w for each in feeds for w in each] + list(rows)
    got = Taker(
        fused(sizes, collective_id, lambda s, t, *refs: forward_kernel(s, t, counts, recuts, *refs), operands, outs, scratch, stored=True)
    )
    gains = got(1)[0]
    flat_weights = [w.reshape(-1, w.shape[-1]) for w in got(10)]
    enc_kept, dec_kept, cross_kept = got(7), got(7), got(7)
    memory_all, enc_out, en2, ahead = got(4)
    return gains, flat_weights, (*enc_kept, None), (*dec_kept, None), (*cross_kept, memory_all), enc_out, en2, ahead


def fast_device(
    enc_in, dec_in, enc_cot, dec_cot, enc_segments, dec_segments, buckets,
    enc_norm1, enc_query, enc_key, enc_value, enc_proj, enc_rel, enc_norm2, enc_gate, enc_up, enc_down, enc_final,
    dec_norm1, dec_query, dec_key, dec_value, dec_proj, dec_rel, dec_norm2, cross_query, cross_key, cross_value, cross_proj,
    dec_norm3, dec_gate, dec_up, dec_down,
):
    groups, cores, parts = sizes = lax.axis_size(HG), lax.axis_size(CORE), lax.axis_size(SP)
    block, model = enc_in.shape
    devices = groups * cores
    share = model // devices
    bf16, f32 = jnp.bfloat16, jnp.float32

    rel_len = enc_rel.shape[0]
    all_gains = jnp.stack([enc_norm1, enc_norm2, enc_final, dec_norm1, dec_norm2, dec_norm3])
    all_rels = jnp.concatenate([enc_rel, dec_rel]).reshape(-1, HEADS)
    small = jnp.concatenate([jnp.pad(w, ((0, 0), (0, 128 - w.shape[1]))) for w in (all_gains, all_rels)])
    each = all_rels.shape[0] // 2
    small = jnp.pad(small, ((0, 16 - small.shape[0]), (0, 0)))

    gains, weights, enc_kept, dec_kept, cross_kept, enc_out, en2, ahead = forward(
        sizes, 1, enc_in, dec_in, small, (6, each), (enc_segments[None, :], dec_segments[None, :]), buckets,
        (
            (enc_key, enc_value, enc_query), (dec_key, dec_value, dec_query), (cross_key, cross_value, cross_query),
            (enc_gate, enc_up), (dec_gate, dec_up), (enc_proj, dec_proj, cross_proj, enc_down, dec_down),
        ),
    )
    enc_kvq, dec_kvq, enc_gu, cross_kvq, dec_gu, enc_wo, dec_wo, enc_wd, cross_wo, dec_wd = weights
    ex, dx, cx = enc_kept[0], dec_kept[0], cross_kept[0]

    (dec_out, dec_in_grad, grad_ex, dg_d1, dg_d2, dg_d3, dg_e2, dg_ef, rel_d), grads_d, sum_a, rows_b, rows_c = decoder_back(
        sizes, 2, gains, (3, 4, 5, 1, 2), (cx, dec_cot, dec_gu, dec_wd),
        (dx, cross_kept, cross_kvq, cross_wo, None), (dec_in, dec_kept, dec_kvq, dec_wo, ahead[1]),
        (ex, enc_out, enc_cot, en2, enc_gu, enc_wd),
    )
    enc_in_grad, sum_bc, sum_d, sum_e = encoder_back(
        sizes, 3, gains, 0, grad_ex, (enc_in, enc_kept, enc_kvq, enc_wo, ahead[0]),
        (dg_d1, dg_d2, dg_d3, dg_e2, dg_ef, rel_d), list(rows_b) + list(rows_c), grads_d,
    )

    dgu_rows, d_wd = sum_a
    cross_rows, c_wo, egu_rows, e_wd = sum_bc
    dkvq_rows, d_wo = sum_d
    ekvq_rows, small_rows, e_wo = sum_e
    (
        enc_out, dec_out, enc_in_grad, dec_in_grad, e_wk, e_wv, e_wq, e_wg, e_wu, d_wk, d_wv, d_wq, c_wk, c_wv, c_wq, d_wg, d_wu, d_wd, c_wo, e_wd, d_wo, e_wo
    ) = unpack(
        [enc_out, dec_out, enc_in_grad, dec_in_grad, ekvq_rows, egu_rows, dkvq_rows, cross_rows, dgu_rows, d_wd, c_wo, e_wd, d_wo, e_wo],
        (-1, -1, -1, -1, 3, 2, 3, 3, 2, 0, 0, 0, 0, 0),
    )
    own = jnp.sum(small_rows.astype(f32), axis=0)
    s = [own[i, :share] for i in range(6)]
    e_rel, d_rel = [own[6 + i * each : 6 + (i + 1) * each, :HEADS].reshape(rel_len) for i in range(2)]
    return (
        enc_out, dec_out, enc_in_grad, dec_in_grad,
        s[0], e_wq, e_wk, e_wv, e_wo, e_rel, s[1], e_wg, e_wu, e_wd, s[2],
        s[3], d_wq, d_wk, d_wv, d_wo, d_rel, s[4], c_wq, c_wk, c_wv, c_wo, s[5], d_wg, d_wu, d_wd,
    )


def general_plan(mesh):
    placed = (
        P(("ctx", "sp"), None),
        P(("ctx", "sp"), None),
        P(("ctx", "sp"), None),
        P(("ctx", "sp"), None),
        P(),
        P(),
        P(),
        P("ctx"),
        P("ctx", None),
        P("ctx", None),
        P("ctx", None),
        P("ctx", None),
        P("ctx"),
        P("ctx"),
        P("ctx", None),
        P("ctx", None),
        P("ctx", None),
        P("ctx"),
        P("ctx"),
        P("ctx", None),
        P("ctx", None),
        P("ctx", None),
        P("ctx", None),
        P("ctx"),
        P("ctx"),
        P("ctx", None),
        P("ctx", None),
        P("ctx", None),
        P("ctx", None),
        P("ctx"),
        P("ctx", None),
        P("ctx", None),
        P("ctx", None),
    )
    return jax.shard_map(
        per_device,
        mesh=mesh,
        in_specs=placed,
        out_specs=(
            P(("ctx", "sp"), None),
            P(("ctx", "sp"), None),
            P(("ctx", "sp"), None),
            P(("ctx", "sp"), None),
            P("ctx"),
            P("ctx", None),
            P("ctx", None),
            P("ctx", None),
            P("ctx", None),
            P("ctx"),
            P("ctx"),
            P("ctx", None),
            P("ctx", None),
            P("ctx", None),
            P("ctx"),
            P("ctx"),
            P("ctx", None),
            P("ctx", None),
            P("ctx", None),
            P("ctx", None),
            P("ctx"),
            P("ctx"),
            P("ctx", None),
            P("ctx", None),
            P("ctx", None),
            P("ctx", None),
            P("ctx"),
            P("ctx", None),
            P("ctx", None),
            P("ctx", None),
        ),
        check_vma=False,
    )


def split_plan(mesh, groups):
    cut = Mesh(np.asarray(mesh.devices).reshape(groups, 2, mesh.shape["sp"]), (HG, CORE, SP))
    tokens, rows, gain, same = P((HG, CORE, SP), None), P((HG, CORE), None), P((HG, CORE)), P()
    attention = (gain, rows, rows, rows, rows, gain)
    feed = (gain, rows, rows, rows)
    weights = attention + feed + (gain,) + attention + (gain, rows, rows, rows, rows) + feed
    return jax.shard_map(
        fast_device,
        mesh=cut,
        in_specs=(tokens,) * 4 + (same,) * 3 + weights,
        out_specs=(tokens,) * 4 + weights,
        check_vma=False,
    )


def solution(mesh):
    groups, odd = divmod(mesh.shape["ctx"], 2)
    if odd or HEADS % groups or mesh.shape["sp"] != 4:
        return general_plan(mesh)
    return split_plan(mesh, groups)
```

```python
import functools
import math

import jax
import jax.numpy as jnp
import numpy as np
from jax import lax
from jax.experimental import pallas as pl
from jax.experimental.pallas import tpu as pltpu
from jax.sharding import Mesh
from jax.sharding import PartitionSpec as P

HEADS = 12
HD = 64


EPSILON = 1e-06
NEGATIVE = -1e30
HIGHEST = lax.Precision.HIGHEST


def rms_norm(values, norm_gain):
    return (
        values * lax.rsqrt(jnp.mean(values * values, axis=-1, keepdims=True) + EPSILON) * norm_gain
    )


def norm_pullback(values, norm_gain, grad_normed):
    _, pullback = jax.vjp(rms_norm, values, norm_gain)
    return pullback(grad_normed)


def gated(gate_val, up_val):
    return jax.nn.gelu(gate_val, approximate=True) * up_val


def project(left, right):
    return jnp.dot(left, right, preferred_element_type=jnp.float32)


def weight_grad(left, right):
    return jnp.einsum("td,te->de", left, right, preferred_element_type=jnp.float32)


def input_grad(grad_out, weight):
    return jnp.einsum("te,de->td", grad_out, weight, preferred_element_type=jnp.float32)


def head_table(relative, table_row, heads_here):
    bucket_count = relative.shape[0] // HEADS
    onehot = (table_row[:, None] == jnp.arange(bucket_count, dtype=jnp.int32)[None, :]).astype(
        jnp.float32
    )
    bias_grid = relative.astype(jnp.float32).reshape(bucket_count, HEADS)
    full_table = jnp.dot(onehot, bias_grid, precision=HIGHEST).T
    first_head = lax.axis_index("sp") * heads_here
    return (lax.dynamic_slice_in_dim(full_table, first_head, heads_here, 0), onehot)


def table_grad(grad_table, onehot, heads_here):
    full_grad = jnp.zeros((HEADS, onehot.shape[0]), jnp.float32)
    full_grad = lax.dynamic_update_slice_in_dim(
        full_grad, grad_table, lax.axis_index("sp") * heads_here, 0
    )
    return jnp.dot(onehot.T, full_grad.T, precision=HIGHEST).reshape(-1)


def bias_block(head_bias, pad_len, offset_q, rows, offset_k, cols):
    head_count, table_len = head_bias.shape
    reach_len = (table_len - 1) // 2
    left_edge = jnp.broadcast_to(head_bias[:, :1], (head_count, pad_len))
    right_edge = jnp.broadcast_to(head_bias[:, -1:], (head_count, pad_len))
    padded = jnp.concatenate([left_edge, head_bias, right_edge], axis=1)
    band_width = rows + cols - 1
    start = offset_k - offset_q - (rows - 1) + reach_len + pad_len
    band = lax.dynamic_slice_in_dim(padded, start, band_width, 1)
    tiled = jnp.broadcast_to(band[:, None, :], (head_count, rows, band_width)).reshape(
        head_count, rows * band_width
    )
    skewed = tiled[:, rows - 1 : rows - 1 + rows * (band_width - 1)].reshape(
        head_count, rows, band_width - 1
    )
    return skewed[:, :, :cols]


def make_frame(query_local, query_ids, key_ids, head_bias, causal):
    local_len = query_local.shape[0]
    heads_here = query_local.shape[1] // HD
    offset_q = lax.axis_index("ctx") * local_len
    ids_q = lax.dynamic_slice_in_dim(query_ids, offset_q, local_len, 0)
    row_ids = offset_q + jnp.arange(local_len, dtype=jnp.int32)
    query_heads = query_local.reshape(local_len, heads_here, HD)
    pad_len = query_ids.shape[0] + key_ids.shape[0]

    def bias_of(entries, offset_k, length):
        return bias_block(entries, pad_len, offset_q, local_len, offset_k, length)

    def scores_of(key_block, offset_k):
        length = key_block.shape[0]
        key_heads = key_block.reshape(length, heads_here, HD)
        raw_scores = jnp.einsum(
            "qhd,khd->hqk", query_heads, key_heads, preferred_element_type=jnp.float32
        )
        col_ids = offset_k + jnp.arange(length, dtype=jnp.int32)
        ids_k = lax.dynamic_slice_in_dim(key_ids, offset_k, length, 0)
        allowed = ids_q[:, None] == ids_k[None, :]
        if causal:
            allowed = allowed & (col_ids[None, :] <= row_ids[:, None])
        if head_bias is not None:
            raw_scores = raw_scores + bias_of(head_bias, offset_k, length)
        return (raw_scores, allowed)

    def touches(offset_k, length):
        first_id = lax.dynamic_slice_in_dim(key_ids, offset_k, 1, 0)[0]
        last_id = lax.dynamic_slice_in_dim(key_ids, offset_k + length - 1, 1, 0)[0]
        touched = (ids_q[0] <= last_id) & (first_id <= ids_q[-1])
        if causal:
            touched = touched & (offset_k <= offset_q + local_len - 1)
        return touched

    return (query_heads, scores_of, touches, bias_of)


def sweep(keys_gathered, local_len, step_fn, carry_state):
    key_all, value_all = keys_gathered
    block_len = local_len * math.gcd(4, lax.axis_size("ctx"))

    def sweep_loop_body(number, running):
        offset_k = number * block_len
        key_block = lax.dynamic_slice_in_dim(key_all, offset_k, block_len, 0)
        value_block = lax.dynamic_slice_in_dim(value_all, offset_k, block_len, 0)
        return step_fn(running, key_block, value_block, offset_k)

    return lax.fori_loop(0, key_all.shape[0] // block_len, sweep_loop_body, carry_state)


def whole_keys(key_local, value_local):
    return (
        lax.all_gather(key_local, "ctx", axis=0, tiled=True),
        lax.all_gather(value_local, "ctx", axis=0, tiled=True),
    )


def attention_forward(query_proj, key_proj, value_proj, query_ids, key_ids, head_bias, causal):
    query_local, key_local, value_local = (
        lax.all_to_all(query_proj, "sp", split_axis=1, concat_axis=0, tiled=True),
        lax.all_to_all(key_proj, "sp", split_axis=1, concat_axis=0, tiled=True),
        lax.all_to_all(value_proj, "sp", split_axis=1, concat_axis=0, tiled=True),
    )
    local_len = query_local.shape[0]
    heads_here = query_local.shape[1] // HD
    query_heads, scores_of, touches, _ = make_frame(
        query_local, query_ids, key_ids, head_bias, causal
    )
    key_block = lax.all_gather(key_local, "ctx", axis=0, tiled=True)
    value_block = lax.all_gather(value_local, "ctx", axis=0, tiled=True)
    offset_k = jnp.int32(0)
    length = key_block.shape[0]
    row_top = jnp.full((heads_here, local_len), NEGATIVE, jnp.float32)
    weighted = jnp.zeros((local_len, heads_here, HD), jnp.float32)
    raw_scores, allowed = scores_of(key_block, offset_k)
    masked = jnp.where(allowed[None], raw_scores, NEGATIVE)
    new_top = jnp.maximum(row_top, jnp.max(masked, axis=-1))
    weights = jnp.where(allowed[None], jnp.exp(masked - new_top[..., None]), 0.0)
    rescale = jnp.exp(row_top - new_top)
    value_heads = value_block.reshape(length, heads_here, HD)
    increment = jnp.einsum(
        "hqk,khd->qhd",
        weights.astype(jnp.bfloat16),
        value_heads,
        preferred_element_type=jnp.float32,
    )
    row_top, row_total, weighted = (
        new_top,
        jnp.sum(weights, axis=-1),
        weighted * rescale.T[:, :, None] + increment,
    )
    mixed_heads = weighted / row_total.T[:, :, None]
    log_total = row_top + jnp.log(row_total)
    mixed_low = mixed_heads.reshape(local_len, heads_here * HD).astype(jnp.bfloat16)
    mixed_tokens = lax.all_to_all(mixed_low, "sp", split_axis=0, concat_axis=1, tiled=True)
    retained = (
        query_local,
        key_local,
        value_local,
        mixed_heads,
        log_total,
        None,
        query_ids,
        key_ids,
        head_bias,
        causal,
    )
    return (mixed_tokens, retained)


def attention_backward(grad_mixed, retained):
    (
        query_local,
        key_local,
        value_local,
        mixed_heads,
        log_total,
        gathered,
        query_ids,
        key_ids,
        head_bias,
        causal,
    ) = retained
    grad_local = lax.all_to_all(grad_mixed, "sp", split_axis=1, concat_axis=0, tiled=True)
    local_len = query_local.shape[0]
    heads_here = query_local.shape[1] // HD
    width = heads_here * HD
    query_heads, scores_of, touches, bias_of = make_frame(
        query_local, query_ids, key_ids, head_bias, causal
    )
    grad_heads = grad_local.reshape(local_len, heads_here, HD)
    row_inner = jnp.einsum("qhd,qhd->hq", grad_heads.astype(jnp.float32), mixed_heads)
    gathered = whole_keys(key_local, value_local)
    table_zero = jnp.zeros(head_bias.shape if head_bias is not None else (1,), jnp.float32)

    def gradients_of(key_block, value_block, offset_k):
        length = key_block.shape[0]
        raw_scores, allowed = scores_of(key_block, offset_k)
        probabilities = jnp.where(allowed[None], jnp.exp(raw_scores - log_total[..., None]), 0.0)
        value_heads = value_block.reshape(length, heads_here, HD)
        grad_probs = jnp.einsum(
            "qhd,khd->hqk", grad_heads, value_heads, preferred_element_type=jnp.float32
        )
        grad_scores = (probabilities * (grad_probs - row_inner[..., None])).astype(jnp.bfloat16)
        return (probabilities, grad_scores)

    def table_part(grad_scores, offset_k, length):
        if head_bias is None:
            return table_zero
        _, pullback = jax.vjp(lambda entries: bias_of(entries, offset_k, length), head_bias)
        return pullback(grad_scores.astype(jnp.float32))[0]

    def key_terms_of(probabilities, grad_scores, length):
        grad_key = jnp.einsum(
            "hqk,qhd->khd", grad_scores, query_heads, preferred_element_type=jnp.float32
        )
        grad_value = jnp.einsum(
            "hqk,qhd->khd",
            probabilities.astype(jnp.bfloat16),
            grad_heads,
            preferred_element_type=jnp.float32,
        )
        return jnp.concatenate(
            [grad_key.reshape(length, width), grad_value.reshape(length, width)], axis=1
        )

    def query_part(grad_scores, key_block):
        length = key_block.shape[0]
        key_heads = key_block.reshape(length, heads_here, HD)
        return jnp.einsum(
            "hqk,khd->qhd", grad_scores, key_heads, preferred_element_type=jnp.float32
        )

    def query_step(running, key_block, value_block, offset_k):
        length = key_block.shape[0]
        grad_query, grad_table = running
        probabilities, grad_scores = gradients_of(key_block, value_block, offset_k)
        return (
            grad_query + query_part(grad_scores, key_block),
            grad_table + table_part(grad_scores, offset_k, length),
        )

    query_zero = jnp.zeros((local_len, heads_here, HD), jnp.float32)
    block_len = local_len * math.gcd(4, lax.axis_size("ctx"))
    grad_query, grad_table = sweep(gathered, local_len, query_step, (query_zero, table_zero))
    key_all, value_all = gathered
    step_len = math.gcd(lax.axis_size("ctx") * local_len, block_len)

    def term_loop_body(number, rows_acc):
        offset_b = number * step_len
        key_block = lax.dynamic_slice_in_dim(key_all, offset_b, step_len, 0)
        value_block = lax.dynamic_slice_in_dim(value_all, offset_b, step_len, 0)
        probabilities, grad_scores = gradients_of(key_block, value_block, offset_b)
        return lax.dynamic_update_slice_in_dim(
            rows_acc, key_terms_of(probabilities, grad_scores, step_len), number * step_len, 0
        )

    own_rows = lax.psum_scatter(
        lax.fori_loop(
            0,
            lax.axis_size("ctx") * local_len // step_len,
            term_loop_body,
            jnp.zeros((lax.axis_size("ctx") * local_len, 2 * width), jnp.float32),
        ),
        "ctx",
        scatter_dimension=0,
        tiled=True,
    )
    grad_q_low = grad_query.reshape(local_len, width).astype(jnp.bfloat16)
    grad_k_low = own_rows[:, :width].astype(jnp.bfloat16)
    grad_v_low = own_rows[:, width:].astype(jnp.bfloat16)
    grad_q_tok, grad_k_tok, grad_v_tok = (
        lax.all_to_all(grad_q_low, "sp", split_axis=0, concat_axis=1, tiled=True),
        lax.all_to_all(grad_k_low, "sp", split_axis=0, concat_axis=1, tiled=True),
        lax.all_to_all(grad_v_low, "sp", split_axis=0, concat_axis=1, tiled=True),
    )
    return (grad_q_tok, grad_k_tok, grad_v_tok, grad_table)


def attention_layer(
    residual,
    source,
    norm_gain,
    w_query,
    w_key,
    w_value,
    w_proj,
    query_ids,
    key_ids,
    head_bias,
    causal,
):
    normed = rms_norm(residual, norm_gain).astype(jnp.bfloat16)
    kv_input = normed if source is None else source
    query_proj = project(normed, w_query).astype(jnp.bfloat16)
    key_proj = project(kv_input, w_key).astype(jnp.bfloat16)
    value_proj = project(kv_input, w_value).astype(jnp.bfloat16)
    mixed_tokens, retained = attention_forward(
        query_proj, key_proj, value_proj, query_ids, key_ids, head_bias, causal
    )
    result = residual + project(mixed_tokens, w_proj)
    return (result, (residual, normed, kv_input, mixed_tokens, retained))


def attention_layer_back(grad_out, saved, norm_gain, w_query, w_key, w_value, w_proj, is_cross):
    residual, normed, kv_input, mixed_tokens, retained = saved
    grad_low = grad_out.astype(jnp.bfloat16)
    grad_proj = weight_grad(mixed_tokens, grad_low)
    grad_mixed = input_grad(grad_low, w_proj).astype(jnp.bfloat16)
    grad_q_tok, grad_k_tok, grad_v_tok, grad_table = attention_backward(grad_mixed, retained)
    grad_wq = weight_grad(normed, grad_q_tok)
    grad_wk = weight_grad(kv_input, grad_k_tok)
    grad_wv = weight_grad(kv_input, grad_v_tok)
    grad_source = input_grad(grad_k_tok, w_key) + input_grad(grad_v_tok, w_value)
    grad_normed = input_grad(grad_q_tok, w_query)
    if not is_cross:
        grad_normed = grad_normed + grad_source
        grad_source = None
    grad_resid, grad_gain = norm_pullback(residual, norm_gain, grad_normed)
    return (
        grad_out + grad_resid,
        grad_source,
        (grad_gain, grad_wq, grad_wk, grad_wv, grad_proj, grad_table),
    )


def feed_layer(residual, norm_gain, w_gate, w_up, w_down):
    normed = rms_norm(residual, norm_gain).astype(jnp.bfloat16)
    gate_val = project(normed, w_gate)
    up_val = project(normed, w_up)
    hidden = gated(gate_val, up_val).astype(jnp.bfloat16)
    return (residual + project(hidden, w_down), (residual, normed, gate_val, up_val, hidden))


def feed_layer_back(grad_out, saved, norm_gain, w_gate, w_up, w_down):
    residual, normed, gate_val, up_val, hidden = saved
    grad_low = grad_out.astype(jnp.bfloat16)
    grad_down = weight_grad(hidden, grad_low)
    grad_hidden = input_grad(grad_low, w_down)
    _, pullback = jax.vjp(gated, gate_val, up_val)
    grad_gate, grad_up = pullback(grad_hidden)
    grad_gate = grad_gate.astype(jnp.bfloat16)
    grad_up = grad_up.astype(jnp.bfloat16)
    grad_wg = weight_grad(normed, grad_gate)
    grad_wu = weight_grad(normed, grad_up)
    grad_normed = input_grad(grad_gate, w_gate) + input_grad(grad_up, w_up)
    grad_resid, grad_gain = norm_pullback(residual, norm_gain, grad_normed)
    return (grad_out + grad_resid, (grad_gain, grad_wg, grad_wu, grad_down))


def per_device(
    enc_in,
    dec_in,
    enc_cot,
    dec_cot,
    enc_segments,
    dec_segments,
    buckets,
    enc_norm1,
    enc_query,
    enc_key,
    enc_value,
    enc_proj,
    enc_rel,
    enc_norm2,
    enc_gate,
    enc_up,
    enc_down,
    enc_final,
    dec_norm1,
    dec_query,
    dec_key,
    dec_value,
    dec_proj,
    dec_rel,
    dec_norm2,
    cross_query,
    cross_key,
    cross_value,
    cross_proj,
    dec_norm3,
    dec_gate,
    dec_up,
    dec_down,
):
    (
        enc_norm1,
        enc_query,
        enc_key,
        enc_value,
        enc_proj,
        enc_rel,
        enc_norm2,
        enc_gate,
        enc_up,
        enc_down,
        enc_final,
        dec_norm1,
        dec_query,
        dec_key,
        dec_value,
        dec_proj,
        dec_rel,
        dec_norm2,
        cross_query,
        cross_key,
        cross_value,
        cross_proj,
        dec_norm3,
        dec_gate,
        dec_up,
        dec_down,
    ) = (
        lax.all_gather(enc_norm1, "ctx", axis=0, tiled=True),
        lax.all_gather(enc_query, "ctx", axis=0, tiled=True),
        lax.all_gather(enc_key, "ctx", axis=0, tiled=True),
        lax.all_gather(enc_value, "ctx", axis=0, tiled=True),
        lax.all_gather(enc_proj, "ctx", axis=0, tiled=True),
        lax.all_gather(enc_rel, "ctx", axis=0, tiled=True),
        lax.all_gather(enc_norm2, "ctx", axis=0, tiled=True),
        lax.all_gather(enc_gate, "ctx", axis=0, tiled=True),
        lax.all_gather(enc_up, "ctx", axis=0, tiled=True),
        lax.all_gather(enc_down, "ctx", axis=0, tiled=True),
        lax.all_gather(enc_final, "ctx", axis=0, tiled=True),
        lax.all_gather(dec_norm1, "ctx", axis=0, tiled=True),
        lax.all_gather(dec_query, "ctx", axis=0, tiled=True),
        lax.all_gather(dec_key, "ctx", axis=0, tiled=True),
        lax.all_gather(dec_value, "ctx", axis=0, tiled=True),
        lax.all_gather(dec_proj, "ctx", axis=0, tiled=True),
        lax.all_gather(dec_rel, "ctx", axis=0, tiled=True),
        lax.all_gather(dec_norm2, "ctx", axis=0, tiled=True),
        lax.all_gather(cross_query, "ctx", axis=0, tiled=True),
        lax.all_gather(cross_key, "ctx", axis=0, tiled=True),
        lax.all_gather(cross_value, "ctx", axis=0, tiled=True),
        lax.all_gather(cross_proj, "ctx", axis=0, tiled=True),
        lax.all_gather(dec_norm3, "ctx", axis=0, tiled=True),
        lax.all_gather(dec_gate, "ctx", axis=0, tiled=True),
        lax.all_gather(dec_up, "ctx", axis=0, tiled=True),
        lax.all_gather(dec_down, "ctx", axis=0, tiled=True),
    )
    enc_norm1 = enc_norm1.astype(jnp.float32)
    enc_norm2 = enc_norm2.astype(jnp.float32)
    enc_final = enc_final.astype(jnp.float32)
    dec_norm1 = dec_norm1.astype(jnp.float32)
    dec_norm2 = dec_norm2.astype(jnp.float32)
    dec_norm3 = dec_norm3.astype(jnp.float32)
    heads_here = HEADS // lax.axis_size("sp")
    enc_table, enc_onehot = head_table(enc_rel, buckets[0], heads_here)
    dec_table, dec_onehot = head_table(dec_rel, buckets[1], heads_here)
    enc_x = enc_in.astype(jnp.float32)
    enc_mid, enc_saved_a = attention_layer(
        enc_x,
        None,
        enc_norm1,
        enc_query,
        enc_key,
        enc_value,
        enc_proj,
        enc_segments,
        enc_segments,
        enc_table,
        False,
    )
    enc_result, enc_saved_f = feed_layer(enc_mid, enc_norm2, enc_gate, enc_up, enc_down)
    memory = rms_norm(enc_result, enc_final).astype(jnp.bfloat16)
    dec_x = dec_in.astype(jnp.float32)
    dec_mid, dec_saved_a = attention_layer(
        dec_x,
        None,
        dec_norm1,
        dec_query,
        dec_key,
        dec_value,
        dec_proj,
        dec_segments,
        dec_segments,
        dec_table,
        True,
    )
    dec_cross, dec_saved_c = attention_layer(
        dec_mid,
        memory,
        dec_norm2,
        cross_query,
        cross_key,
        cross_value,
        cross_proj,
        dec_segments,
        enc_segments,
        None,
        False,
    )
    dec_result, dec_saved_f = feed_layer(dec_cross, dec_norm3, dec_gate, dec_up, dec_down)
    grad_dec, dec_ff_grads = feed_layer_back(
        dec_cot.astype(jnp.float32), dec_saved_f, dec_norm3, dec_gate, dec_up, dec_down
    )
    grad_dec, grad_memory, cross_grads = attention_layer_back(
        grad_dec, dec_saved_c, dec_norm2, cross_query, cross_key, cross_value, cross_proj, True
    )
    grad_dec, _, dec_self_grads = attention_layer_back(
        grad_dec, dec_saved_a, dec_norm1, dec_query, dec_key, dec_value, dec_proj, False
    )
    grad_enc_out, grad_final = norm_pullback(enc_result, enc_final, grad_memory)
    grad_enc, enc_ff_grads = feed_layer_back(
        enc_cot.astype(jnp.float32) + grad_enc_out,
        enc_saved_f,
        enc_norm2,
        enc_gate,
        enc_up,
        enc_down,
    )
    grad_enc, _, enc_self_grads = attention_layer_back(
        grad_enc, enc_saved_a, enc_norm1, enc_query, enc_key, enc_value, enc_proj, False
    )
    e_gain1, e_wq, e_wk, e_wv, e_wo, e_table = enc_self_grads
    e_gain2, e_wg, e_wu, e_wd = enc_ff_grads
    d_gain1, d_wq, d_wk, d_wv, d_wo, d_table = dec_self_grads
    c_gain, c_wq, c_wk, c_wv, c_wo, _ = cross_grads
    d_gain3, d_wg, d_wu, d_wd = dec_ff_grads
    e_rel = table_grad(e_table, enc_onehot, heads_here)
    d_rel = table_grad(d_table, dec_onehot, heads_here)
    shards = (
        lax.psum_scatter(e_gain1, "ctx", scatter_dimension=0, tiled=True),
        lax.psum_scatter(e_wq, "ctx", scatter_dimension=0, tiled=True),
        lax.psum_scatter(e_wk, "ctx", scatter_dimension=0, tiled=True),
        lax.psum_scatter(e_wv, "ctx", scatter_dimension=0, tiled=True),
        lax.psum_scatter(e_wo, "ctx", scatter_dimension=0, tiled=True),
        lax.psum_scatter(e_rel, "ctx", scatter_dimension=0, tiled=True),
        lax.psum_scatter(e_gain2, "ctx", scatter_dimension=0, tiled=True),
        lax.psum_scatter(e_wg, "ctx", scatter_dimension=0, tiled=True),
        lax.psum_scatter(e_wu, "ctx", scatter_dimension=0, tiled=True),
        lax.psum_scatter(e_wd, "ctx", scatter_dimension=0, tiled=True),
        lax.psum_scatter(grad_final, "ctx", scatter_dimension=0, tiled=True),
        lax.psum_scatter(d_gain1, "ctx", scatter_dimension=0, tiled=True),
        lax.psum_scatter(d_wq, "ctx", scatter_dimension=0, tiled=True),
        lax.psum_scatter(d_wk, "ctx", scatter_dimension=0, tiled=True),
        lax.psum_scatter(d_wv, "ctx", scatter_dimension=0, tiled=True),
        lax.psum_scatter(d_wo, "ctx", scatter_dimension=0, tiled=True),
        lax.psum_scatter(d_rel, "ctx", scatter_dimension=0, tiled=True),
        lax.psum_scatter(c_gain, "ctx", scatter_dimension=0, tiled=True),
        lax.psum_scatter(c_wq, "ctx", scatter_dimension=0, tiled=True),
        lax.psum_scatter(c_wk, "ctx", scatter_dimension=0, tiled=True),
        lax.psum_scatter(c_wv, "ctx", scatter_dimension=0, tiled=True),
        lax.psum_scatter(c_wo, "ctx", scatter_dimension=0, tiled=True),
        lax.psum_scatter(d_gain3, "ctx", scatter_dimension=0, tiled=True),
        lax.psum_scatter(d_wg, "ctx", scatter_dimension=0, tiled=True),
        lax.psum_scatter(d_wu, "ctx", scatter_dimension=0, tiled=True),
        lax.psum_scatter(d_wd, "ctx", scatter_dimension=0, tiled=True),
    )
    (
        s_gain1,
        s_wq,
        s_wk,
        s_wv,
        s_wo,
        s_rel,
        s_gain2,
        s_wg,
        s_wu,
        s_wd,
        s_final,
        t_gain1,
        t_wq,
        t_wk,
        t_wv,
        t_wo,
        t_rel,
        t_gain2,
        t_cq,
        t_ck,
        t_cv,
        t_co,
        t_gain3,
        t_wg,
        t_wu,
        t_wd,
    ) = shards
    reduced = (
        lax.psum(s_gain1.astype(jnp.bfloat16), "sp").astype(jnp.float32),
        lax.psum(s_wq.astype(jnp.bfloat16), "sp").astype(jnp.float32),
        lax.psum(s_wk.astype(jnp.bfloat16), "sp").astype(jnp.float32),
        lax.psum(s_wv.astype(jnp.bfloat16), "sp").astype(jnp.float32),
        lax.psum(s_wo.astype(jnp.bfloat16), "sp").astype(jnp.float32),
        lax.psum(s_rel.astype(jnp.bfloat16), "sp").astype(jnp.float32),
        lax.psum(s_gain2.astype(jnp.bfloat16), "sp").astype(jnp.float32),
        lax.psum(s_wg.astype(jnp.bfloat16), "sp").astype(jnp.float32),
        lax.psum(s_wu.astype(jnp.bfloat16), "sp").astype(jnp.float32),
        lax.psum(s_wd.astype(jnp.bfloat16), "sp").astype(jnp.float32),
        lax.psum(s_final.astype(jnp.bfloat16), "sp").astype(jnp.float32),
        lax.psum(t_gain1.astype(jnp.bfloat16), "sp").astype(jnp.float32),
        lax.psum(t_wq.astype(jnp.bfloat16), "sp").astype(jnp.float32),
        lax.psum(t_wk.astype(jnp.bfloat16), "sp").astype(jnp.float32),
        lax.psum(t_wv.astype(jnp.bfloat16), "sp").astype(jnp.float32),
        lax.psum(t_wo.astype(jnp.bfloat16), "sp").astype(jnp.float32),
        lax.psum(t_rel.astype(jnp.bfloat16), "sp").astype(jnp.float32),
        lax.psum(t_gain2.astype(jnp.bfloat16), "sp").astype(jnp.float32),
        lax.psum(t_cq.astype(jnp.bfloat16), "sp").astype(jnp.float32),
        lax.psum(t_ck.astype(jnp.bfloat16), "sp").astype(jnp.float32),
        lax.psum(t_cv.astype(jnp.bfloat16), "sp").astype(jnp.float32),
        lax.psum(t_co.astype(jnp.bfloat16), "sp").astype(jnp.float32),
        lax.psum(t_gain3.astype(jnp.bfloat16), "sp").astype(jnp.float32),
        lax.psum(t_wg.astype(jnp.bfloat16), "sp").astype(jnp.float32),
        lax.psum(t_wu.astype(jnp.bfloat16), "sp").astype(jnp.float32),
        lax.psum(t_wd.astype(jnp.bfloat16), "sp").astype(jnp.float32),
    )
    return (enc_result, dec_result, grad_enc, grad_dec) + tuple(reduced)


HG, CORE, SP = "hg", "core", "sp"
BLOCK_PAD = 128
VMEM_BYTES = 60 << 20


def nt(left, right):
    return lax.dot_general(left, right, (((1,), (1,)), ((), ())), preferred_element_type=jnp.float32)


def tn(left, right):
    return lax.dot_general(left, right, (((0,), (0,)), ((), ())), preferred_element_type=jnp.float32)


def nn(left, right):
    return jnp.dot(left, right, preferred_element_type=jnp.float32)


def low(value):
    return value.astype(jnp.bfloat16)


def identity(size):
    rows = lax.broadcasted_iota(jnp.int32, (size, size), 0)
    cols = lax.broadcasted_iota(jnp.int32, (size, size), 1)
    return low(jnp.where(rows == cols, 1.0, 0.0))


def only_lanes(array, first, count):
    lanes = lax.broadcasted_iota(jnp.int32, array.shape, 1)
    return jnp.where((lanes >= first) & (lanes < first + count), array, jnp.zeros_like(array))


def gelu_and_slope(v):
    scale, cubic = math.sqrt(2.0 / math.pi), 0.044715
    t = jnp.tanh(scale * (v + cubic * v * v * v))
    return 0.5 * v * (1.0 + t), 0.5 * (1.0 + t) + 0.5 * v * (1.0 - t * t) * scale * (1.0 + 3.0 * cubic * v * v)


def norm_back(x, g, dn):
    r = lax.rsqrt(jnp.mean(x * x, axis=-1, keepdims=True) + EPSILON)
    w = dn * g
    dx = r * w - x * (r * r * r) * jnp.mean(w * x, axis=-1, keepdims=True)
    return dx, jnp.sum(dn * x * r, axis=0, keepdims=True)


def send(src, dst, send_sem, recv_sem, to):
    copy = pltpu.make_async_remote_copy(
        src_ref=src, dst_ref=dst, send_sem=send_sem, recv_sem=recv_sem, device_id=to, device_id_type=pl.DeviceIdType.MESH
    )
    copy.start()
    return copy


def arrived(dst, send_sem, recv_sem, to):
    pltpu.make_async_remote_copy(
        src_ref=dst, dst_ref=dst, send_sem=send_sem, recv_sem=recv_sem, device_id=to, device_id_type=pl.DeviceIdType.MESH
    ).wait_recv()


class Place:
    def __init__(self, groups, cores, parts):
        self.groups, self.cores, self.parts = groups, cores, parts
        self.group, self.core, self.part = lax.axis_index(HG), lax.axis_index(CORE), lax.axis_index(SP)

    def ahead(self, step):
        return lax.rem(self.group + step, self.groups)

    def behind(self, step):
        return lax.rem(self.group + self.groups - step, self.groups)

    def chip(self, group):
        return (group, self.core, self.part)

    def sibling(self):
        return (self.group, 1 - self.core, self.part)

    def plane(self, step):
        return lax.rem(self.part + step, self.parts)

    def plane_behind(self, step):
        return lax.rem(self.part + self.parts - step, self.parts)

    def at_plane(self, part):
        return (self.group, self.core, part)

    def first_token(self, number, block):
        return pl.multiple_of(((self.cores * number + self.core) * self.parts + self.part) * block, block)

    def greet(self, planes=False):
        barrier = pltpu.get_barrier_semaphore()
        partners = [self.chip(self.ahead(step)) for step in range(1, self.groups)] + [self.sibling()]
        if planes:
            partners += [self.at_plane(self.plane(step)) for step in range(1, self.parts)]
        for partner in partners:
            pl.semaphore_signal(barrier, inc=1, device_id=partner, device_id_type=pl.DeviceIdType.MESH)
        pl.semaphore_wait(barrier, len(partners))


def spread_start(place, buf, sent, got):
    mine = buf.at[place.group]
    return [
        send(mine, mine, sent.at[step], got.at[step], place.chip(place.ahead(step))) for step in range(1, place.groups)
    ]


def spread_wait(place, buf, sent, got):
    for step in range(1, place.groups):
        source = place.behind(step)
        arrived(buf.at[source], sent.at[step], got.at[step], place.chip(source))


def collect_start(place, partial, out_buf, in_buf, sent, got):
    out_buf[...] = low(partial).reshape(out_buf.shape)
    pending = []
    for step in range(1, place.groups):
        to = place.ahead(step)
        pending.append(send(out_buf.at[to], in_buf.at[place.group], sent.at[step], got.at[step], place.chip(to)))
    return pending


def collect_wait(place, out_buf, in_buf, sent, got):
    total = out_buf[place.group].astype(jnp.float32)
    for step in range(1, place.groups):
        source = place.behind(step)
        arrived(in_buf.at[source], sent.at[step], got.at[step], place.chip(source))
        total = total + in_buf[source].astype(jnp.float32)
    return total


def all_rows(buf):
    return buf[...].reshape(buf.shape[0] * buf.shape[1], buf.shape[2])


DMA = pltpu.SemaphoreType.DMA
IN_VMEM = pl.BlockSpec(memory_space=pltpu.VMEM)
ANYWHERE = pl.BlockSpec(memory_space=pl.ANY)


class Recut:
    def __init__(self, sizes, col_shapes, row_shapes):
        groups, cores, _ = sizes
        self.cols, self.rows = len(col_shapes), len(row_shapes)
        self.outs = [((groups, cores) + s[1:], jnp.bfloat16) for s in col_shapes]
        self.outs += [((cores,) + s, jnp.bfloat16) for s in row_shapes]
        cols = (self.cols, groups)
        self.scratch = [DMA(cols)] * 4 + [DMA((self.rows,))] * 2 + [DMA((self.cols + self.rows,))]

    def bind(self, ins, outs, scratch):
        self.col_refs, self.row_refs = ins[: self.cols], ins[self.cols :]
        self.col_outs, self.row_outs = outs[: self.cols], outs[self.cols :]
        self.sems = scratch
        self.pending, self.copies = [], []

    def begin(self, place):
        sent, got, relay_sent, relay_got, pair_sent, pair_got, local = self.sems
        group, core = place.group, place.core
        for index, (ref, out) in enumerate(zip(self.col_refs, self.col_outs)):
            slot = out.at[group, core]
            for step in range(1, place.groups):
                to = place.ahead(step)
                self.pending.append(send(ref.at[to], slot, sent.at[index, step], got.at[index, step], place.chip(to)))
            self.pending.append(send(ref.at[group], slot, relay_sent.at[index, 0], relay_got.at[index, 0], place.sibling()))
            self.copies.append(pltpu.make_async_copy(ref.at[group], slot, local.at[index]))
        for index, (ref, out) in enumerate(zip(self.row_refs, self.row_outs)):
            slot = out.at[core]
            self.pending.append(send(ref, slot, pair_sent.at[index], pair_got.at[index], place.sibling()))
            self.copies.append(pltpu.make_async_copy(ref, slot, local.at[self.cols + index]))
        for copy in self.copies:
            copy.start()

    def middle(self, place):
        sent, got, relay_sent, relay_got = self.sems[:4]
        for index, out in enumerate(self.col_outs):
            for step in range(1, place.groups):
                source = place.behind(step)
                slot = out.at[source, place.core]
                arrived(slot, sent.at[index, step], got.at[index, step], place.chip(source))
                self.pending.append(
                    send(slot, slot, relay_sent.at[index, step], relay_got.at[index, step], place.sibling())
                )

    def end(self, place):
        _, _, relay_sent, relay_got, pair_sent, pair_got, _ = self.sems
        for index, out in enumerate(self.col_outs):
            for step in range(place.groups):
                slot = out.at[place.behind(step), 1 - place.core]
                arrived(slot, relay_sent.at[index, step], relay_got.at[index, step], place.sibling())
        for index, out in enumerate(self.row_outs):
            arrived(out.at[1 - place.core], pair_sent.at[index], pair_got.at[index], place.sibling())
        for copy in self.copies:
            copy.wait()
        for copy in self.pending:
            copy.wait_send()


class GiveRows:
    def __init__(self, sizes, cols, rows):
        self.cols, self.rows = len(cols), len(rows)
        own = [(s[0],) + s[2:] for s in cols] + [(1,) + s[1:] for s in rows]
        self.outs = [(shape, jnp.bfloat16) for shape in own]
        self.scratch = [pltpu.VMEM(shape, jnp.bfloat16) for shape in own + own[: self.cols]]
        self.scratch += [DMA((self.cols, sizes[0]))] * 4 + [DMA((self.rows,))] * 2

    def bind(self, ins, outs, scratch):
        self.col_refs, self.row_refs = ins[: self.cols], ins[self.cols :]
        self.col_outs, self.row_outs = outs[: self.cols], outs[self.cols :]
        self.col_sibs, scratch = scratch[: self.cols], scratch[self.cols :]
        self.row_sibs, scratch = scratch[: self.rows], scratch[self.rows :]
        self.col_sums, self.sems = scratch[: self.cols], scratch[self.cols :]
        self.pending = []

    def begin(self, place):
        _, _, pair_sent, pair_got, row_sent, row_got = self.sems
        other = 1 - place.core
        for index, (ref, sib) in enumerate(zip(self.col_refs, self.col_sibs)):
            for step in range(place.groups):
                to = place.ahead(step)
                self.pending.append(
                    send(
                        ref.at[to, other], sib.at[to],
                        pair_sent.at[index, step], pair_got.at[index, step], place.sibling(),
                    )
                )
        for index, (ref, sib) in enumerate(zip(self.row_refs, self.row_sibs)):
            self.pending.append(send(ref.at[other], sib.at[0], row_sent.at[index], row_got.at[index], place.sibling()))

    def middle(self, place):
        sent, got, pair_sent, pair_got, row_sent, row_got = self.sems
        core = place.core
        for index, (ref, sib) in enumerate(zip(self.col_refs, self.col_sibs)):
            out, sums = self.col_outs[index], self.col_sums[index]
            for step in list(range(1, place.groups)) + [0]:
                to = place.ahead(step)
                arrived(sib.at[to], pair_sent.at[index, step], pair_got.at[index, step], place.sibling())
                both = low(ref[to, core].astype(jnp.float32) + sib[to].astype(jnp.float32))
                if step:
                    sums[to] = both
                    self.pending.append(
                        send(sums.at[to], out.at[place.group], sent.at[index, step], got.at[index, step], place.chip(to))
                    )
                else:
                    out[place.group] = both
        for index, (ref, sib) in enumerate(zip(self.row_refs, self.row_sibs)):
            arrived(sib.at[0], row_sent.at[index], row_got.at[index], place.sibling())
            self.row_outs[index][0] = low(ref[core].astype(jnp.float32) + sib[0].astype(jnp.float32))

    def end(self, place):
        sent, got = self.sems[:2]
        for index, out in enumerate(self.col_outs):
            for step in range(1, place.groups):
                source = place.behind(step)
                arrived(out.at[source], sent.at[index, step], got.at[index, step], place.chip(source))
        for copy in self.pending:
            copy.wait_send()


FOLD_PIECE = 56 * 1024


class FoldPlanes:
    def __init__(self, arrays, in_place=False):
        self.in_place = in_place
        self.operands = list(arrays)
        self.in_specs = [IN_VMEM] * len(arrays)
        self.outs = [(w.shape, jnp.bfloat16) for w in arrays]
        self.out_specs = [IN_VMEM] * len(arrays)
        self.pieces = []
        for index, w in enumerate(arrays):
            cuts = next(c for c in (1, 2, 3, 4, 6, 8) if w.shape[1] // c * w.shape[2] <= FOLD_PIECE or c == 8)
            if w.shape[0] * w.shape[1] * w.shape[2] <= FOLD_PIECE:
                self.pieces.append((index, slice(None), pl.ds(0, w.shape[1])))
                continue
            rows = w.shape[1] // cuts
            self.pieces += [(index, lead, pl.ds(c * rows, rows)) for lead in range(w.shape[0]) for c in range(cuts)]
        self.inner_done = self.across_done = 0
        self.scratch = [pltpu.VMEM(w.shape, jnp.bfloat16) for _ in range(1 if in_place else 2) for w in arrays] + [DMA((len(self.pieces),))] * 6

    def bind(self, ins, outs, scratch):
        count = len(self.outs)
        self.ins, self.totals = ins, outs
        self.inner = outs
        self.across, scratch = scratch[:count], scratch[count:]
        self.sums, self.sems = (ins, scratch) if self.in_place else (scratch[:count], scratch[count:])

    def copy(self, hop, number, src, dst, to):
        return pltpu.make_async_remote_copy(
            src_ref=src, dst_ref=dst, send_sem=self.sems[2 * hop].at[number], recv_sem=self.sems[2 * hop + 1].at[number],
            device_id=to, device_id_type=pl.DeviceIdType.MESH,
        )

    def hops(self, place, number):
        index, lead, rows = self.pieces[number]
        part = place.part
        inward, across, outward = (place.at_plane(p) for p in (1 + part // 3, 3 - part, 3 * (part - 1)))
        ref, inner, sums, other, total = (
            side[index].at[lead, rows] for side in (self.ins, self.inner, self.sums, self.across, self.totals)
        )
        return (ref, inner, inward), (sums, other, across), (total, total, outward)

    def roles(self, place):
        middle = (place.part == 1) | (place.part == 2)
        return pl.when(middle), pl.when(jnp.logical_not(middle))

    def start(self, place, numbers):
        @self.roles(place)[1]
        def _():
            for number in numbers:
                self.copy(0, number, *self.hops(place, number)[0]).start()

    def add_inner(self, place, number):
        inward, across, _ = self.hops(place, number)
        self.copy(0, number, *inward).wait_recv()
        across[0][...] = low(inward[0][...].astype(jnp.float32) + inward[1][...].astype(jnp.float32))
        self.copy(1, number, *across).start()

    def add_across(self, place, number):
        _, across, outward = self.hops(place, number)
        self.copy(1, number, *across).wait_recv()
        outward[0][...] = low(across[0][...].astype(jnp.float32) + across[1][...].astype(jnp.float32))
        self.copy(2, number, *outward).start()

    def of(self, first, last):
        return [n for n, piece in enumerate(self.pieces) if first <= piece[0] < last]

    def serve(self, place, inner, across):
        inners = list(range(self.inner_done, min(self.inner_done + inner, len(self.pieces))))
        self.inner_done += len(inners)
        others = list(range(self.across_done, min(self.across_done + across, len(self.pieces))))
        self.across_done += len(others)

        @self.roles(place)[0]
        def _():
            for turn in range(max(len(inners), len(others))):
                if turn < len(inners):
                    self.add_inner(place, inners[turn])
                if turn < len(others):
                    self.add_across(place, others[turn])

    def finish(self, place, lag):
        left = len(self.pieces) - self.inner_done
        behind = self.inner_done - self.across_done
        if behind > lag:
            self.serve(place, 0, behind - lag)
        self.serve(place, lag - min(behind, lag), 0)
        self.serve(place, left, left)
        self.serve(place, 0, len(self.pieces))

    def end(self, place):
        in_middle, at_end = self.roles(place)

        @at_end
        def _():
            for number in range(len(self.pieces)):
                inward, _, outward = self.hops(place, number)
                self.copy(0, number, *inward).wait_send()
                self.copy(2, number, *outward).wait_recv()

        @in_middle
        def _():
            for number in range(len(self.pieces)):
                _, across, outward = self.hops(place, number)
                self.copy(1, number, *across).wait_send()
                self.copy(2, number, *outward).wait_send()


def feed_back_part(n, dyb, gu_ref, down_ref):
    hidden = down_ref.shape[0]
    gu = nn(n, gu_ref[...])
    g, u = gu[:, :hidden], gu[:, hidden:]
    act, slope = gelu_and_slope(g)
    dh = nt(dyb, down_ref[...])
    return low(act * u), jnp.concatenate([low(dh * u * slope), low(dh * act)], axis=1)


def row_block(row):
    wide = jnp.broadcast_to(row.astype(jnp.float32), (8, row.shape[1]))
    return low(jnp.where(lax.broadcasted_iota(jnp.int32, wide.shape, 0) == 0, wide, 0.0))


def bucket_onehot(row, width, count, place_of):
    last = row.shape[1] - 1
    padded = jnp.concatenate([row.astype(jnp.float32), jnp.zeros((1, width - last - 1), jnp.float32)], axis=1)
    entry = lax.broadcasted_iota(jnp.int32, (width, width), 0)
    column = lax.broadcasted_iota(jnp.int32, (width, width), 1)
    pick = low(jnp.where(entry == jnp.clip(place_of(column), 0, last), 1.0, 0.0))
    bucket = nn(row_block(padded), pick)[0:1, :].astype(jnp.int32)
    return jnp.where(lax.broadcasted_iota(jnp.int32, (count, width), 0) == bucket, 1.0, 0.0)


def bias_mask(place, block, causal, rel_ref, turn, key_ids, query_ids, out_ref):
    heads, rows_total, lanes = out_ref.shape
    key_len = key_ids.shape[1]
    strip = block + 2 * BLOCK_PAD
    query = lax.broadcasted_iota(jnp.int32, (1, lanes), 1)
    start = ((place.cores * (query // block) + place.core) * place.parts + place.part) * block
    token = lax.broadcasted_iota(jnp.int32, (key_len, lanes), 0)
    of_key = tn(row_block(key_ids[...]), jnp.ones((8, lanes), jnp.bfloat16))
    of_query = nn(row_block(query_ids[...]), low(jnp.where(token == start + query % block, 1.0, 0.0)))[0:1, :]
    allowed = of_key == of_query
    if causal:
        allowed = allowed & (token <= start + query % block)
    inside = pl.ds(BLOCK_PAD, key_len)
    if rel_ref is None:
        out_ref[0, inside, :] = low(jnp.where(allowed, 0.0, NEGATIVE))
        return
    by_head = tn(rel_ref[...], turn)
    width = by_head.shape[1]
    pick_rows = lax.broadcasted_iota(jnp.int32, (8, by_head.shape[0]), 0)
    pick_cols = lax.broadcasted_iota(jnp.int32, (8, by_head.shape[0]), 1)
    picked = nn(low(jnp.where(pick_cols == pick_rows + place.group * heads, 1.0, 0.0)), low(by_head))
    places = lax.broadcasted_iota(jnp.int32, (rows_total, lanes), 0)
    for head in range(heads):
        row = picked[head : head + 1, :]
        left, right = row[:, width - 2 : width - 1], row[:, 0:1]
        out_ref[head] = low(jnp.where(places < start, left, right))
        wide = jnp.broadcast_to(row, (strip, width))
        for number in range(lanes // block):
            at = (number * block) % 128
            turned = pltpu.roll(wide, (width - (strip - 1) + at) % width, 1, stride=1, stride_axis=0)
            rows = pl.ds(place.first_token(number, block), strip)
            out_ref[head, rows, number * block : (number + 1) * block] = low(turned[:, at : at + block])
        out_ref[head, inside, :] = low(jnp.where(allowed, out_ref[head, inside, :].astype(jnp.float32), NEGATIVE))


def chunk_rows(kv_ref):
    return kv_ref.shape[1] * kv_ref.shape[2] * kv_ref.shape[3]


def key_side(kv_ref, chunk):
    return kv_ref[chunk].reshape(chunk_rows(kv_ref), kv_ref.shape[4])[:, : kv_ref.shape[4] // 2]


def value_side(kv_ref, chunk):
    lanes = kv_ref.shape[4]
    return kv_ref[chunk].reshape(chunk_rows(kv_ref), lanes)[:, lanes // 2 // 128 * 128 :]


def bias_rows(bm_ref, head, chunk, rows):
    at = pl.multiple_of(BLOCK_PAD + chunk * rows, 128)
    return bm_ref[head if bm_ref.shape[0] > 1 else 0, pl.ds(at, rows), :].astype(jnp.float32)


def mix_part(q, kv_ref, bm_ref, o_ref, lse_ref, s_ref, ot_ref):
    chunks, rows = kv_ref.shape[0], chunk_rows(kv_ref)
    queries, width = q.shape
    heads = width // HD
    across = [slice(head * queries, (head + 1) * queries) for head in range(heads)]
    masked_q = [only_lanes(q, head * HD, HD) for head in range(heads)]

    def first(chunk, tops):
        keys = key_side(kv_ref, chunk)
        inside = pl.ds(pl.multiple_of(chunk * rows, rows), rows)
        new = []
        for head in range(heads):
            scores = nt(keys, masked_q[head]) + bias_rows(bm_ref, head, chunk, rows)
            s_ref[inside, across[head]] = scores
            new.append(jnp.maximum(tops[head], jnp.max(scores, axis=0, keepdims=True)))
        return tuple(new)

    tops = lax.fori_loop(0, chunks, first, (jnp.full((1, queries), NEGATIVE, jnp.float32),) * heads)

    def second(chunk, carried):
        values = value_side(kv_ref, chunk)
        inside = pl.ds(pl.multiple_of(chunk * rows, rows), rows)
        lead = values.shape[1] - width
        values_t = low(nt(identity(values.shape[1]), values))
        new = []
        for head in range(heads):
            total, mixed = carried[head]
            weights = jnp.exp(s_ref[inside, across[head]] - tops[head])
            mixed = mixed + nn(values_t[lead + head * HD : lead + (head + 1) * HD], low(weights))
            new.append((total + jnp.sum(weights, axis=0, keepdims=True), mixed))
        return tuple(new)

    start = (jnp.zeros((1, queries), jnp.float32), jnp.zeros((HD, queries), jnp.float32))
    done = lax.fori_loop(0, chunks, second, (start,) * heads)
    for head in range(heads):
        total, mixed = done[head]
        lse_ref[:, across[head]] = tops[head] + jnp.log(total)
        ot_ref[head * HD : (head + 1) * HD, :] = low(mixed / total)
    o_ref[...] = low(nt(identity(queries), ot_ref[...]))


def keys_send(place, kv_ref, base, sent, got):
    mine = kv_ref.at[:, place.core, place.part]
    pending = [
        send(mine, mine, sent.at[base, step], got.at[base, step], place.at_plane(place.plane(step)))
        for step in range(1, place.parts)
    ]
    pending.append(send(mine, mine, sent.at[base + 1, 0], got.at[base + 1, 0], place.sibling()))
    return pending


def keys_relay(place, kv_ref, base, sent, got):
    pending = []
    for step in range(1, place.parts):
        source = place.plane_behind(step)
        slot = kv_ref.at[:, place.core, source]
        arrived(slot, sent.at[base, step], got.at[base, step], place.at_plane(source))
        pending.append(send(slot, slot, sent.at[base + 1, step], got.at[base + 1, step], place.sibling()))
    return pending


def keys_wait(place, kv_ref, base, sent, got):
    for step in range(place.parts):
        slot = kv_ref.at[:, 1 - place.core, place.plane_behind(step)]
        arrived(slot, sent.at[base + 1, step], got.at[base + 1, step], place.sibling())


def mix_back_part(place, q, do, o, kv_ref, lse_ref, bm_ref, dkv_ref, ds_ref):
    chunks, cores, parts, block, lanes = kv_ref.shape
    rows = chunk_rows(kv_ref)
    queries, width = q.shape
    heads = width // HD
    strip = block + 2 * BLOCK_PAD
    first_value = width // 128 * 128
    lead = width - first_value
    do_wide = jnp.concatenate([jnp.zeros((queries, lead), do.dtype), do], axis=1) if lead else do
    across = [slice(head * queries, (head + 1) * queries) for head in range(heads)]
    masked_q = [only_lanes(q, head * HD, HD) for head in range(heads)]
    masked_do = [only_lanes(do_wide, lead + head * HD, HD) for head in range(heads)]
    q_wide = masked_q
    if lead:
        none = jnp.zeros((queries, lead), q.dtype)
        q_wide = [jnp.concatenate([one, none], axis=1) for one in masked_q]
    of_head = lax.broadcasted_iota(jnp.int32, (8, width), 1) // HD
    of_row = lax.broadcasted_iota(jnp.int32, (8, width), 0)
    inners = lax.dot_general(
        jnp.where(of_head == of_row, 1.0, 0.0), do.astype(jnp.float32) * o.astype(jnp.float32),
        (((1,), (1,)), ((), ())), precision=HIGHEST, preferred_element_type=jnp.float32,
    )
    nothing = jnp.zeros((1, queries), jnp.float32)
    if ds_ref is not None:
        empty = jnp.zeros((BLOCK_PAD, heads * queries), jnp.bfloat16)
        ds_ref[0:BLOCK_PAD, :] = empty
        ds_ref[BLOCK_PAD + chunks * rows :, :] = empty
        of_lane = lax.broadcasted_iota(jnp.int32, (1, queries), 1) // block
        lane_start = ((cores * of_lane + place.core) * parts + place.part) * block

    def chunk_step(chunk, carried):
        at = pl.multiple_of(chunk * rows, rows)
        keys, values = key_side(kv_ref, chunk), value_side(kv_ref, chunk)
        keys_t = low(nt(identity(width), keys))
        new, dk, dv = [], None, None
        for head in range(heads):
            left, right, back = carried[head]
            scores = nt(keys, masked_q[head]) + bias_rows(bm_ref, head, chunk, rows)
            p = jnp.exp(scores - lse_ref[:, across[head]])
            dp = nt(values, masked_do[head])
            ds = low(p * (dp - inners[head : head + 1, :]))
            if ds_ref is not None:
                ds_ref[pl.ds(pl.multiple_of(BLOCK_PAD + at, 128), rows), across[head]] = ds
                wide = ds.astype(jnp.float32)
                places = lax.broadcasted_iota(jnp.int32, wide.shape, 0) + (at + BLOCK_PAD)
                left = left + jnp.sum(jnp.where(places < lane_start, wide, 0.0), axis=0, keepdims=True)
                right = right + jnp.sum(jnp.where(places >= lane_start + strip, wide, 0.0), axis=0, keepdims=True)
            back = back + nn(keys_t[head * HD : (head + 1) * HD], ds)
            new.append((left, right, back))
            more_k, more_v = nn(ds, q_wide[head]), nn(low(p), masked_do[head])
            dk, dv = (more_k, more_v) if dk is None else (dk + more_k, dv + more_v)
        if lead:
            shared = dk[:, first_value:] + dv[:, : 2 * lead]
            both = jnp.concatenate([dk[:, :first_value], shared, dv[:, 2 * lead :]], axis=1)
        else:
            both = jnp.concatenate([dk, dv], axis=1)
        dkv_ref[chunk] = low(both).reshape(dkv_ref.shape[1:])
        return tuple(new)

    start = (nothing, nothing, jnp.zeros((HD, queries), jnp.float32))
    done = lax.fori_loop(0, chunks, chunk_step, (start,) * heads)
    return [one[2] for one in done], [one[:2] for one in done]


def table_grads(place, block, done, ds_ref, ahead_ref, rel_ref):
    queries = done[0][0].shape[1]
    width = ahead_ref.shape[1]
    strip = block + 2 * BLOCK_PAD
    rows = lax.broadcasted_iota(jnp.int32, (block, block), 0)
    cols = lax.broadcasted_iota(jnp.int32, (block, block), 1)
    backwards = jnp.where(rows + cols == block - 1, 1.0, 0.0)
    at = lax.broadcasted_iota(jnp.int32, (1, width), 1)
    sums = []
    for head, (left, right) in enumerate(done):
        total = jnp.zeros((strip, block), jnp.float32)
        for number in range(queries // block):
            low_at = head * queries + number * block
            near = pl.ds(place.first_token(number, block), strip)
            total = total + ds_ref[near, low_at : low_at + block].astype(jnp.float32)
        turned = lax.dot_general(
            backwards, total, (((1,), (1,)), ((), ())), precision=HIGHEST, preferred_element_type=jnp.float32
        )
        turned = jnp.concatenate([turned, jnp.zeros((block, width - strip), jnp.float32)], axis=1)
        by_distance = jnp.sum(pltpu.roll(turned, 0, 1, stride=1, stride_axis=0), axis=0, keepdims=True)
        left, right = (jnp.sum(side, axis=1, keepdims=True) for side in (left, right))
        sums.append(by_distance + jnp.where(at == 0, left, 0.0) + jnp.where(at == width - 2, right, 0.0))
    sums = jnp.concatenate(sums + [jnp.zeros((8 - len(sums), width), jnp.float32)], axis=0)
    by_bucket = lax.dot_general(
        sums, ahead_ref[...], (((1,), (1,)), ((), ())), precision=HIGHEST, preferred_element_type=jnp.float32
    )
    head_rows = lax.broadcasted_iota(jnp.int32, (8, 128), 0)
    head_lanes = lax.broadcasted_iota(jnp.int32, (8, 128), 1)
    lanes_of = (head_lanes == head_rows + place.group * len(done)) & (head_rows < len(done))
    rel_ref[...] = lax.dot_general(
        by_bucket, jnp.where(lanes_of, 1.0, 0.0), (((0,), (0,)), ((), ())), precision=HIGHEST, preferred_element_type=jnp.float32
    )


class AttendBack:
    OPERANDS = 10

    def __init__(self, place, ins, grads, dkv, scratch, cross):
        self.place, self.cross = place, cross
        self.x, self.n, self.q, self.kv, self.o, self.lse, self.w, self.wo, self.bm, other = ins
        self.source, self.ahead = (other, None) if cross else (self.n, other)
        self.dw, self.dwo = grads
        self.dkv, self.sib, self.zout, self.zin, self.d_buf, self.pn, self.rn, self.dq = [dkv] + scratch[:7]
        scratch = scratch[7:]
        self.pm, self.rm = (scratch.pop(0), scratch.pop(0)) if cross else (None, None)
        self.ds = None if cross else scratch.pop(0)
        self.sent, self.got = scratch
        self.kv_width = self.kv.shape[4]
        self.pending = []

    def begin(self, dy):
        self.d_buf[self.place.group] = low(dy)
        self.pending += spread_start(self.place, self.d_buf, self.sent.at[0], self.got.at[0])

    def arrive(self):
        spread_wait(self.place, self.d_buf, self.sent.at[0], self.got.at[0])

    def compute(self):
        place, sent, got = self.place, self.sent, self.got
        do = low(nt(all_rows(self.d_buf), self.wo[...]))
        back, self.edges = mix_back_part(
            place, self.q[...], do, self.o[...], self.kv, self.lse, self.bm, self.dkv, self.ds
        )
        self.halves = send(self.dkv.at[:, 1 - place.core], self.sib, sent.at[1, 0], got.at[1, 0], place.sibling())
        self.dq[...] = low(nt(identity(self.q.shape[0]), low(jnp.concatenate(back, axis=0))))
        if self.cross:
            share = nt(self.dq[...], self.w[:, self.kv_width :])
            self.pending += collect_start(place, share, self.pn, self.rn, sent.at[3], got.at[3])

    def exchange(self):
        place, sent, got = self.place, self.sent, self.got
        arrived(self.sib, sent.at[1, 0], got.at[1, 0], place.sibling())
        for step in list(range(1, place.parts)) + [0]:
            to = place.plane(step)
            self.zout[to] = low(self.dkv[:, place.core, to].astype(jnp.float32) + self.sib[:, to].astype(jnp.float32))
            if step:
                self.pending.append(
                    send(self.zout.at[to], self.zin.at[place.part], sent.at[2, step], got.at[2, step], place.at_plane(to))
                )

        self.halves.wait_send()

    def by_rows(self, grad):
        return low(grad).reshape(self.dw.shape[:3] + grad.shape[1:])

    def query_grads(self, rel):
        self.dwo[...] = low(tn(self.o[...], all_rows(self.d_buf))).reshape(self.dwo.shape)
        self.dw[:, :, :, self.kv_width :] = self.by_rows(tn(self.n[...], self.dq[...]))
        if not self.cross:
            table_grads(self.place, self.x.shape[0], self.edges, self.ds, self.ahead, rel)

    def keys(self):
        place, sent, got = self.place, self.sent, self.got
        total = self.zout[place.part].astype(jnp.float32)
        for step in range(1, place.parts):
            source = place.plane_behind(step)
            arrived(self.zin.at[source], sent.at[2, step], got.at[2, step], place.at_plane(source))
            total = total + self.zin[source].astype(jnp.float32)
        self.dkv_own = low(total).reshape(self.q.shape[0], self.kv_width)
        share = nt(self.dkv_own, self.w[:, : self.kv_width])
        if self.cross:
            self.pending += collect_start(place, share, self.pm, self.rm, sent.at[4], got.at[4])
        else:
            share = share + nt(self.dq[...], self.w[:, self.kv_width :])
            self.pending += collect_start(place, share, self.pn, self.rn, sent.at[3], got.at[3])

    def key_grads(self):
        self.dw[:, :, :, : self.kv_width] = self.by_rows(tn(self.source[...], self.dkv_own))

    def source_grad(self):
        return collect_wait(self.place, self.pm, self.rm, self.sent.at[4], self.got.at[4])

    def normed_grad(self):
        return collect_wait(self.place, self.pn, self.rn, self.sent.at[3], self.got.at[3])

    def wait(self):
        for copy in self.pending:
            copy.wait_send()


def attend_back_scratch(sizes, block, model, width, cross):
    groups, cores, parts = sizes
    tokens = groups * block
    turned, buffer = (parts, groups, block, 2 * width), (groups, block, model)
    shapes = [(groups, parts, block, 2 * width), turned, turned, buffer, buffer, buffer, (tokens, width)]
    if cross:
        shapes += [buffer, buffer]
    else:
        shapes.append((cores * parts * tokens + 2 * BLOCK_PAD, width // HD * tokens))
    return [pltpu.VMEM(shape, jnp.bfloat16) for shape in shapes] + [DMA((5, max(groups, parts)))] * 2


class Taker:
    def __init__(self, refs):
        self.refs = list(refs)

    def __call__(self, count):
        taken, self.refs = self.refs[:count], self.refs[count:]
        return taken


def decoder_back_kernel(sizes, streams, gain_at, plans, *refs):
    give_a, give_b, give_c, fold, cross_scratch, self_scratch = plans
    dec1, dec2, dec3, enc2, final = gain_at
    take = Taker(refs)
    gains, cx, dec_cot, dec_gu, dec_down = take(5)
    cross_ins, self_ins = take(AttendBack.OPERANDS), take(AttendBack.OPERANDS)
    ex, enc_out, enc_cot, en2, gu, down = take(6)
    dec_out, dec_in_grad, grad_ex, dg_d1, dg_d2, dg_d3, dg_e2, dg_ef, rel_d, dw_d, dwo_d = take(11)
    totals, c_outs = take(len(fold.outs)), take(len(give_c.outs))
    dw_c, dwo_c, dgu, ddown, dgu_a, ddown_a, dkv, grad_cx, grad_dx = take(9)
    n_buf, d_buf, py, ry, f_buf, pf, rf, f_sent, f_got = take(9)
    place = Place(*sizes)
    cross = AttendBack(place, cross_ins, (dw_c, dwo_c), dkv, take(len(cross_scratch)), True)
    own = AttendBack(place, self_ins, (dw_d, dwo_d), dkv, take(len(self_scratch)), False)
    a_outs, b_outs = take(len(give_a.outs)), take(len(give_b.outs))
    give_a.bind([dgu_a, ddown_a], a_outs, take(len(give_a.scratch)))
    fold.bind(a_outs + b_outs, totals, take(len(fold.scratch)))
    of_a, of_b = fold.of(0, len(a_outs)), fold.of(len(a_outs), len(fold.outs))
    give_b.bind([dw_c, dwo_c], b_outs, take(len(give_b.scratch)))
    give_c.bind([dgu, ddown], c_outs, take(len(give_c.scratch)))
    pn, rn = own.pn, own.rn
    place.greet(planes=True)
    d_buf[place.group] = dec_cot[...]
    pending = spread_start(place, d_buf, f_sent.at[2], f_got.at[2])
    n_buf[place.group] = low(rms_norm(cx[...], gains[dec3]))
    pending += spread_start(place, n_buf, f_sent.at[3], f_got.at[3])
    spread_wait(place, d_buf, f_sent.at[2], f_got.at[2])
    spread_wait(place, n_buf, f_sent.at[3], f_got.at[3])
    n, dyb = all_rows(n_buf), all_rows(d_buf)
    h, dgu_value = feed_back_part(n, dyb, dec_gu, dec_down)
    leaving = collect_start(place, nt(dgu_value, dec_gu[...]), pn, rn, f_sent.at[4], f_got.at[4])
    dgu_a[...] = low(tn(n, dgu_value)).reshape(dgu_a.shape)
    ddown_a[...] = low(tn(h, dyb)).reshape(ddown_a.shape)
    dn = collect_wait(place, pn, rn, f_sent.at[4], f_got.at[4])
    for copy in leaving:
        copy.wait_send()
    back, dg = norm_back(cx[...], gains[dec3], dn)
    dg_d3[...] = dg
    grad_cx[...] = dec_cot[...].astype(jnp.float32) + back
    cross.begin(grad_cx[...])
    pending += collect_start(place, nn(h, dec_down[...]), py, ry, f_sent.at[5], f_got.at[5])
    give_a.begin(place)
    give_a.middle(place)
    streams.need(5, 15)
    cross.arrive()
    cross.compute()
    cross.exchange()
    give_a.end(place)
    fold.start(place, of_a)
    back, dg = norm_back(cross.x[...].astype(jnp.float32), gains[dec2], cross.normed_grad())
    dg_d2[...] = dg
    grad_dx[...] = grad_cx[...] + back
    own.begin(grad_dx[...])
    cross.query_grads(None)
    streams.need(15, 25)
    dec_out[...] = cx[...] + collect_wait(place, py, ry, f_sent.at[5], f_got.at[5])
    own.arrive()
    own.compute()
    cross.keys()
    own.exchange()
    fold.serve(place, 4, 0)
    cross.key_grads()
    give_b.begin(place)
    streams.need(25, 31)
    back, dg = norm_back(enc_out[...], gains[final], cross.source_grad())
    dg_ef[...] = dg
    dy = enc_cot[...].astype(jnp.float32) + back
    f_buf[place.group] = low(dy)
    pending += spread_start(place, f_buf, f_sent.at[0], f_got.at[0])
    give_b.middle(place)
    own.query_grads(rel_d)
    fold.serve(place, 3, 2)
    spread_wait(place, f_buf, f_sent.at[0], f_got.at[0])
    n, dyb = en2[...], all_rows(f_buf)
    h, dgu_value = feed_back_part(n, dyb, gu, down)
    pending += collect_start(place, nt(dgu_value, gu[...]), pf, rf, f_sent.at[1], f_got.at[1])
    dgu[...] = low(tn(n, dgu_value)).reshape(dgu.shape)
    ddown[...] = low(tn(h, dyb)).reshape(ddown.shape)
    give_b.end(place)
    fold.start(place, of_b)
    give_c.begin(place)
    fold.serve(place, 3, 3)
    dn = collect_wait(place, pf, rf, f_sent.at[1], f_got.at[1])
    back, dg = norm_back(ex[...], gains[enc2], dn)
    dg_e2[...] = dg
    grad_ex[...] = dy + back
    give_c.middle(place)
    own.keys()
    own.key_grads()
    fold.finish(place, 2)
    back, dg = norm_back(own.x[...].astype(jnp.float32), gains[dec1], own.normed_grad())
    dg_d1[...] = dg
    dec_in_grad[...] = grad_dx[...] + back
    give_c.end(place)
    fold.end(place)
    cross.wait()
    own.wait()
    for copy in pending:
        copy.wait_send()


def encoder_back_kernel(sizes, streams, gain_at, plans, *refs):
    give_d, give_e, fold, before, scratch = plans
    take = Taker(refs)
    gains, grad_ex = take(2)
    ins = take(AttendBack.OPERANDS)
    dg_d1, dg_d2, dg_d3, dg_e2, dg_ef, rel_d = take(6)
    ready, d_ins = take(before), take(give_d.cols + give_d.rows)
    (enc_in_grad,) = take(1)
    totals = take(len(fold.outs))
    dw_e, dwo_e, small, dkv, rel_e = take(5)
    place = Place(*sizes)
    own = AttendBack(place, ins, (dw_e, dwo_e), dkv, take(len(scratch)), False)
    d_outs, e_outs = take(len(give_d.outs)), take(len(give_e.outs))
    give_d.bind(d_ins, d_outs, take(len(give_d.scratch)))
    give_e.bind([dw_e, small, dwo_e], e_outs, take(len(give_e.scratch)))
    fold.bind(ready + d_outs + e_outs, totals, take(len(fold.scratch)))
    of_c = fold.of(0, before)
    of_d, of_e = fold.of(before, before + len(d_outs)), fold.of(before + len(d_outs), len(fold.outs))
    place.greet(planes=True)
    own.begin(grad_ex[...])
    fold.start(place, of_c)
    give_d.begin(place)
    give_d.middle(place)
    streams.need(2, 12)
    own.arrive()
    fold.serve(place, 2, 0)
    own.compute()
    fold.serve(place, 3, 2)
    own.exchange()
    give_d.end(place)
    fold.start(place, of_d)
    fold.serve(place, 2, 2)
    own.query_grads(rel_e)
    fold.serve(place, 2, 2)
    own.keys()
    fold.serve(place, len(of_c) - 9, 3)
    own.key_grads()
    dn = own.normed_grad()
    back, dg_e1 = norm_back(own.x[...].astype(jnp.float32), gains[gain_at], dn)
    enc_in_grad[...] = grad_ex[...] + back
    devices = place.groups * place.cores
    share = dg_e1.shape[1] // devices
    small[...] = jnp.zeros_like(small)
    all_gains = jnp.concatenate([dg_e1, dg_e2[...], dg_ef[...], dg_d1[...], dg_d2[...], dg_d3[...]], axis=0)
    count = all_gains.shape[0]
    each = rel_e.shape[0] // devices
    tables = [rel_e[...].reshape(devices, each, 128), rel_d[...].reshape(devices, each, 128)]
    for device in range(devices):
        piece = jnp.concatenate([all_gains[:, device * share : (device + 1) * share], jnp.zeros((count, 128 - share), jnp.float32)], axis=1)
        rows = jnp.concatenate([piece, tables[0][device], tables[1][device]], axis=0)
        rows = jnp.concatenate([rows, jnp.zeros((16 - rows.shape[0], 128), jnp.float32)], axis=0)
        small[device // place.cores, device % place.cores] = low(rows)
    give_e.begin(place)
    fold.serve(place, 2, len(of_c) - 9)
    give_e.middle(place)
    fold.serve(place, len(of_d) - 2, 2)
    give_e.end(place)
    fold.start(place, of_e)
    fold.finish(place, 2)
    fold.end(place)
    own.wait()


class Streams:
    def __init__(self, fetches, stores):
        self.fetches, self.stores = fetches, stores
        self.stored = []

    def begin(self):
        for copy in self.fetches.values():
            copy.start()

    def need(self, first, last):
        for index in [i for i in self.fetches if first <= i < last]:
            self.fetches.pop(index).wait()

    def store(self, *indices):
        for index in indices:
            if index in self.stores:
                copy = self.stores.pop(index)
                copy.start()
                self.stored.append(copy)

    def end(self):
        self.need(0, 1 << 20)
        self.store(*sorted(self.stores))
        for copy in self.stored:
            copy.wait()


LARGE = 300_000


def size_of(shape, dtype):
    return math.prod(shape) * jnp.dtype(dtype).itemsize


def fused(sizes, collective_id, kernel, operands, outs, scratch, fetched=(0, 0), stored=False):
    late = [i for i, w in enumerate(operands) if fetched[0] <= i < fetched[1] and size_of(w.shape, w.dtype) > LARGE]
    early = [i for i, (shape, dtype) in enumerate(outs) if stored and size_of(shape, dtype) > LARGE]
    held = [pltpu.VMEM(operands[i].shape, operands[i].dtype) for i in late]
    held += [pltpu.VMEM(*outs[i]) for i in early]
    sems = [DMA((max(1, len(late)),)), DMA((max(1, len(early)),))]

    def body(*refs):
        take = Taker(refs)
        ins, results, own = take(len(operands)), take(len(outs)), take(len(scratch))
        late_refs, early_refs = take(len(late)), take(len(early))
        late_sem, early_sem = take(2)
        fetches, stores = {}, {}
        for number, index in enumerate(late):
            fetches[index] = pltpu.make_async_copy(ins[index], late_refs[number], late_sem.at[number])
            ins[index] = late_refs[number]
        for number, index in enumerate(early):
            stores[index] = pltpu.make_async_copy(early_refs[number], results[index], early_sem.at[number])
            results[index] = early_refs[number]
        streams = Streams(fetches, stores)
        streams.begin()
        kernel(sizes, streams, *ins, *results, *own)
        streams.end()

    return pl.pallas_call(
        body,
        out_shape=tuple(jax.ShapeDtypeStruct(shape, dtype) for shape, dtype in outs),
        in_specs=[ANYWHERE if i in late else IN_VMEM for i in range(len(operands))],
        out_specs=tuple(ANYWHERE if i in early else IN_VMEM for i in range(len(outs))),
        scratch_shapes=list(scratch) + held + sems,
        compiler_params=pltpu.CompilerParams(collective_id=collective_id, has_side_effects=True, vmem_limit_bytes=VMEM_BYTES),
        cost_estimate=pl.CostEstimate(flops=20_000_000_000, bytes_accessed=10_000_000, transcendentals=0),
    )(*operands)


def kept_operands(x, kept, w, wo, ahead):
    _, n, q, kv, o, lse, bm, memory = kept
    return [x, n, q, kv, o, lse, w, wo, bm, memory if ahead is None else ahead]


def buffers_of(shapes):
    return [pltpu.VMEM(shape, jnp.bfloat16) for shape in shapes]


def decoder_back(sizes, collective_id, gains, gain_at, last, cross, own, feed):
    groups, cores, parts = sizes
    f32, bf16 = jnp.float32, jnp.bfloat16
    block, model = last[0].shape
    share = model // (groups * cores)
    width = cross[3].shape[0]
    kv = cross[1][3].shape
    hidden = feed[5].shape[0]
    attention = [(groups, cores, share, 3 * width)], [(cores, width // cores, model)]
    feeds = [(groups, cores, share, 2 * hidden)], [(cores, hidden // cores, model)]
    give_a, give_b, give_c = GiveRows(sizes, *feeds), GiveRows(sizes, *attention), GiveRows(sizes, *feeds)
    fold = FoldPlanes([jax.ShapeDtypeStruct(shape, dtype) for shape, dtype in give_a.outs + give_b.outs], True)
    cross_scratch = attend_back_scratch(sizes, block, model, width, True)
    self_scratch = attend_back_scratch(sizes, block, model, width, False)
    plans = (give_a, give_b, give_c, fold, cross_scratch, self_scratch)
    operands = [gains, *last] + kept_operands(*cross) + kept_operands(*own) + list(feed)
    token, gain = ((block, model), f32), ((1, model), f32)
    outs = [token, token, token, gain, gain, gain, gain, gain, ((own[4].shape[0], 128), f32)]
    outs += [(attention[0][0], bf16), (attention[1][0], bf16)] + fold.outs + give_c.outs
    buffer = (groups, block, model)
    scratch = buffers_of(attention[0] + attention[1] + (feeds[0] + feeds[1]) * 2 + [kv]) + [pltpu.VMEM((block, model), f32)] * 2
    scratch += buffers_of([buffer] * 7) + [DMA((6, groups))] * 2 + cross_scratch + self_scratch
    scratch += buffers_of([shape for shape, _ in give_a.outs + give_b.outs])
    scratch += give_a.scratch + fold.scratch + give_b.scratch + give_c.scratch
    got = Taker(fused(sizes, collective_id, lambda s, t, *refs: decoder_back_kernel(s, t, gain_at, plans, *refs), operands, outs, scratch, (5, 31)))
    first = got(9)
    return first, got(2), got(len(give_a.outs)), got(len(give_b.outs)), got(len(give_c.outs))


def encoder_back(sizes, collective_id, gains, gain_at, grad_ex, own, small_grads, ready, grads_d):
    groups, cores, parts = sizes
    f32 = jnp.float32
    block, model = grad_ex.shape
    share = model // (groups * cores)
    width = own[3].shape[0]
    kv = own[1][3].shape
    give_d = GiveRows.__new__(GiveRows)
    give_d = GiveRows(sizes, [grads_d[0].shape], [grads_d[1].shape])
    cols = [(groups, cores, share, 3 * width), (groups, cores, 16, 128)]
    rows = [(cores, width // cores, model)]
    give_e = GiveRows(sizes, cols, rows)
    all_outs = [jax.ShapeDtypeStruct(shape, dtype) for shape, dtype in give_d.outs + give_e.outs]
    fold = FoldPlanes(list(ready) + all_outs)
    scratch = attend_back_scratch(sizes, block, model, width, False)
    plans = (give_d, give_e, fold, len(ready), scratch)
    operands = [gains, grad_ex] + kept_operands(*own) + list(small_grads) + list(ready) + list(grads_d)
    buffers = buffers_of([cols[0], rows[0], cols[1], kv]) + [pltpu.VMEM((own[4].shape[0], 128), f32)] + scratch
    buffers += buffers_of([shape for shape, _ in give_d.outs]) + buffers_of([shape for shape, _ in give_e.outs])
    buffers += give_d.scratch + give_e.scratch + fold.scratch
    outs = [((block, model), f32)] + fold.outs
    got = Taker(fused(sizes, collective_id, lambda s, t, *refs: encoder_back_kernel(s, t, gain_at, plans, *refs), operands, outs, buffers, (2, 12)))
    return got(1)[0], got(len(ready)), got(2), got(3)


def unpack_kernel(kinds, *refs):
    take = Taker(refs)
    ins = take(len(kinds))
    for ref, pieces in zip(ins, kinds):
        if pieces < 0:
            take(1)[0][...] = ref[...]
            continue
        value = ref[...].astype(jnp.float32)
        if pieces == 0:
            take(1)[0][...] = value[0]
            continue
        each = value.shape[2] // pieces
        for piece, out in enumerate(take(pieces)):
            out[...] = jnp.concatenate([one[:, piece * each : (piece + 1) * each] for one in value], axis=1)


def unpack(arrays, kinds):
    outs = []
    for array, pieces in zip(arrays, kinds):
        if pieces < 0:
            outs.append(jax.ShapeDtypeStruct(array.shape, array.dtype))
        elif pieces == 0:
            outs.append(jax.ShapeDtypeStruct(array.shape[1:], jnp.float32))
        for _ in range(pieces):
            outs.append(jax.ShapeDtypeStruct((array.shape[1], array.shape[0] * array.shape[2] // pieces), jnp.float32))
    return pl.pallas_call(
        functools.partial(unpack_kernel, kinds),
        out_shape=tuple(outs),
        in_specs=[IN_VMEM] * len(arrays),
        out_specs=(IN_VMEM,) * len(outs),
        compiler_params=pltpu.CompilerParams(vmem_limit_bytes=VMEM_BYTES),
    )(*arrays)


class AttendForward:
    def __init__(self, place, outs, bufs, sems, base):
        self.place, self.base = place, base
        self.x, self.n, self.q, self.kv, self.o, self.lse, self.bm = outs
        self.p_buf, self.r_buf = bufs
        self.sent, self.got = sems

    def keys(self, kv):
        kv_ref = self.kv
        kv_ref[:, self.place.core, self.place.part] = kv.reshape(kv_ref.shape[0], kv_ref.shape[3], kv_ref.shape[4])

    def send(self):
        return keys_send(self.place, self.kv, self.base, self.sent, self.got)

    def gather(self):
        pending = keys_relay(self.place, self.kv, self.base, self.sent, self.got)
        keys_wait(self.place, self.kv, self.base, self.sent, self.got)
        return pending

    def mix(self, wo, s_ref, ot_ref):
        place, base = self.place, self.base
        mix_part(self.q[...], self.kv, self.bm, self.o, self.lse, s_ref, ot_ref)
        share = nn(self.o[...], wo)
        return collect_start(place, share, self.p_buf, self.r_buf, self.sent.at[base + 2], self.got.at[base + 2])

    def add(self, x):
        total = collect_wait(self.place, self.p_buf, self.r_buf, self.sent.at[self.base + 2], self.got.at[self.base + 2])
        self.x[...] = x + total


def pack_columns(pack, refs):
    groups = pack.shape[0]
    for group in range(groups):
        parts = [ref[:, group * (ref.shape[1] // groups) : (group + 1) * (ref.shape[1] // groups)] for ref in refs]
        pack[group] = jnp.concatenate([part.astype(jnp.float32) for part in parts], axis=1).astype(pack.dtype)


def flat(ref):
    rows = math.prod(ref.shape[:-1])
    return ref[...].reshape(rows, ref.shape[-1])


def forward_kernel(sizes, streams, counts, recuts, *refs):
    enc_first, dec_first, later, last = recuts
    gain_count, each = counts
    take = Taker(refs)
    enc_in, dec_in, small, enc_ids, dec_ids, buckets = take(6)
    enc_w, dec_w, cross_w, enc_gate_up, dec_gate_up = take(3), take(3), take(3), take(2), take(2)
    enc_wo_own, dec_wo_own, cross_wo_own, enc_wd_own, dec_wd_own = take(5)
    gains, enc_kvq, dec_kvq, enc_gu, cross_kvq, dec_gu, enc_wo, dec_wo, enc_wd, cross_wo, dec_wd = take(11)
    enc_outs, dec_outs, cross_outs = take(7), take(7), take(7)
    memory_all, enc_out, en2, ahead = take(4)
    small_pack, enc_pack, dec_pack, cross_pack, enc_gu_pack, dec_gu_pack, small_all, rels = take(8)
    s_ref, ot_ref = take(2)
    x_e, x_d, n_buf, d_buf, m_buf, f_p, f_r = take(7)
    bufs = [take(2) for _ in range(3)]
    sent, got = take(2)
    enc_first.bind([small_pack, enc_pack, enc_wo_own], [small_all, enc_kvq, enc_wo], take(len(enc_first.scratch)))
    dec_first.bind([dec_pack, dec_wo_own], [dec_kvq, dec_wo], take(len(dec_first.scratch)))
    later.bind(
        [enc_gu_pack, cross_pack, enc_wd_own, cross_wo_own], [enc_gu, cross_kvq, enc_wd, cross_wo], take(len(later.scratch))
    )
    last.bind([dec_gu_pack, dec_wd_own], [dec_gu, dec_wd], take(len(last.scratch)))
    place = Place(*sizes)
    enc, dec, cross = [
        AttendForward(place, outs, bufs[i], (sent, got), 6 + 3 * i) for i, outs in enumerate((enc_outs, dec_outs, cross_outs))
    ]
    for group in range(place.groups):
        small_pack[group] = small[...]
    pack_columns(enc_pack, enc_w)
    place.greet(planes=True)
    x_e[place.group] = enc_in[...]
    x_d[place.group] = dec_in[...]
    enc_first.begin(place)
    pending = spread_start(place, x_e, sent.at[0], got.at[0])
    pack_columns(dec_pack, dec_w)
    dec_first.begin(place)
    pending += spread_start(place, x_d, sent.at[1], got.at[1])
    pack_columns(enc_gu_pack, enc_gate_up)
    pack_columns(cross_pack, cross_w)
    pack_columns(dec_gu_pack, dec_gate_up)
    enc_first.middle(place)
    enc_first.end(place)

    devices = place.groups * place.cores
    share = enc_in.shape[1] // devices
    rows, model = small.shape[0], enc_in.shape[1]
    lane = lax.broadcasted_iota(jnp.int32, (128, model), 0)
    column = lax.broadcasted_iota(jnp.int32, (128, model), 1)
    bucket = lax.broadcasted_iota(jnp.int32, (devices * each, rows), 0)
    row = lax.broadcasted_iota(jnp.int32, (devices * each, rows), 1)
    every_gain, tables = 0.0, [0.0, 0.0]
    for device in range(devices):
        table = small_all[device // place.cores, device % place.cores]
        to_column = (column == lane + device * share) & (lane < share)
        every_gain = every_gain + nn(table, low(jnp.where(to_column, 1.0, 0.0)))
        for index in range(2):
            from_row = row == bucket - device * each + gain_count + index * each
            from_row = from_row & (bucket // each == device)
            tables[index] = tables[index] + nn(low(jnp.where(from_row, 1.0, 0.0)), table)
    for index in range(gain_count):
        gains[index] = every_gain[index : index + 1, :]
    for index in range(2):
        rels[index] = low(tables[index])

    def project(one, x_buf, gain_at, w, number):
        spread_wait(place, x_buf, sent.at[number], got.at[number])
        kv_width = one.kv.shape[4]
        n = low(rms_norm(all_rows(x_buf).astype(jnp.float32), gains[gain_at]))
        one.n[...] = n
        both = low(nn(n, flat(w)))
        one.keys(both[:, :kv_width])
        one.q[...] = both[:, kv_width:]

    project(enc, x_e, 0, enc_kvq, 0)
    pending += enc.send()
    dec_first.middle(place)
    dec_first.end(place)
    project(dec, x_d, 3, dec_kvq, 1)
    later.begin(place)
    block = enc_in.shape[0]
    reach, width = buckets.shape[1] // 2, ahead.shape[2]
    turns = []
    for index in range(2):
        row, count = buckets[index : index + 1, :], ahead.shape[1]
        ahead[index] = bucket_onehot(row, width, count, lambda column: column - (block - 1))
        turns.append(low(bucket_onehot(row, width, count, lambda column: 2 * reach + block - 1 - column)))
    bias_mask(place, block, False, rels.at[0], turns[0], enc_ids, enc_ids, enc.bm)
    streams.store(1, 2, 12, 19, 17)
    bias_mask(place, block, True, rels.at[1], turns[1], dec_ids, dec_ids, dec.bm)
    streams.store(24)
    pending += enc.gather()
    pending += dec.send()
    pending += enc.mix(flat(enc_wo), s_ref, ot_ref)
    streams.store(14)
    bias_mask(place, block, False, None, None, enc_ids, dec_ids, cross.bm)
    streams.store(31)
    enc.add(enc_in[...].astype(jnp.float32))
    ex = enc.x[...]
    n_buf[place.group] = low(rms_norm(ex, gains[1]))
    pending += spread_start(place, n_buf, sent.at[2], got.at[2])
    later.middle(place)
    later.end(place)
    streams.store(3, 4, 8)
    spread_wait(place, n_buf, sent.at[2], got.at[2])
    en2[...] = all_rows(n_buf)
    w_down = flat(enc_wd)
    hidden = w_down.shape[0]
    gu = nn(en2[...], flat(enc_gu))
    h = low(gelu_and_slope(gu[:, :hidden])[0] * gu[:, hidden:])
    pending += collect_start(place, nn(h, w_down), f_p, f_r, sent.at[5], got.at[5])
    enc_out[...] = ex + collect_wait(place, f_p, f_r, sent.at[5], got.at[5])
    m_buf[place.group] = low(rms_norm(enc_out[...], gains[2]))
    pending += spread_start(place, m_buf, sent.at[4], got.at[4])
    kv_width = cross.kv.shape[4]
    model = enc_in.shape[1]
    spread_wait(place, m_buf, sent.at[4], got.at[4])
    memory_all[...] = all_rows(m_buf)
    cross.keys(low(nn(memory_all[...], cross_kvq[:, :, :, :kv_width].reshape(model, kv_width))))
    pending += cross.send()
    pending += dec.gather()
    pending += dec.mix(flat(dec_wo), s_ref, ot_ref)
    streams.store(21)
    dec.add(dec_in[...].astype(jnp.float32))
    d_buf[place.group] = low(rms_norm(dec.x[...], gains[4]))
    pending += spread_start(place, d_buf, sent.at[3], got.at[3])
    last.begin(place)
    spread_wait(place, d_buf, sent.at[3], got.at[3])
    cross.n[...] = all_rows(d_buf)
    cross.q[...] = low(nn(cross.n[...], cross_kvq[:, :, :, kv_width:].reshape(model, kv_width // 2)))
    pending += cross.gather()
    pending += cross.mix(flat(cross_wo), s_ref, ot_ref)
    streams.store(28, 26, 32, 34)
    last.middle(place)
    cross.add(dec.x[...])
    last.end(place)
    for copy in pending:
        copy.wait_send()


def forward(sizes, collective_id, enc_in, dec_in, small, counts, ids, buckets, weights):
    groups, cores, parts = sizes
    f32, bf16 = jnp.float32, jnp.bfloat16
    block, model = enc_in.shape
    attention, feeds, rows = weights[:3], weights[3:5], weights[5]
    share = attention[0][0].shape[0]
    width = rows[0].shape[0] * cores
    tokens = groups * block
    keys = cores * parts * tokens
    heads = width // HD
    kvq, gu = (groups, share, 3 * width), (groups, share, 2 * feeds[0][0].shape[1] // groups)
    wo, wd = rows[0].shape, rows[3].shape
    small_shape = (groups,) + small.shape
    recuts = (
        Recut(sizes, [small_shape, kvq], [wo]), Recut(sizes, [kvq], [wo]), Recut(sizes, [gu, kvq], [wd, wo]), Recut(sizes, [gu], [wd])
    )

    def both(shape):
        return ((groups, cores) + shape[1:], bf16)

    def pair(shape):
        return ((cores,) + shape, bf16)

    token = ((block, model), f32)
    outs = [((counts[0], 1, model), f32), both(kvq), both(kvq), both(gu), both(kvq), both(gu)]
    outs += [pair(wo), pair(wo), pair(wd), pair(wo), pair(wd)]
    for number in range(3):
        outs += [
            token, ((tokens, model), bf16), ((tokens, width), bf16), ((groups, cores, parts, block, 2 * width), bf16),
            ((tokens, width), bf16), ((1, heads * tokens), f32),
            ((1 if number == 2 else heads, keys + 2 * BLOCK_PAD, tokens), bf16),
        ]
    bucket_count = groups * cores * counts[1]
    outs += [((tokens, model), bf16), token, ((tokens, model), bf16), ((2, bucket_count, buckets.shape[1] - 1 + 2 * block), f32)]
    buffer = (groups, block, model)
    scratch = buffers_of([small_shape, kvq, kvq, kvq, gu, gu, both(small_shape)[0], (2, bucket_count, 128)])
    scratch += [pltpu.VMEM((keys, heads * tokens), f32)] + buffers_of([(width, tokens)] + [buffer] * 13)
    scratch += [DMA((15, max(groups, parts)))] * 2 + [s for one in recuts for s in one.scratch]
    operands = [enc_in, dec_in, small, *ids, buckets] + [w for each in attention for w in each]
    operands += [w for each in feeds for w in each] + list(rows)
    got = Taker(
        fused(sizes, collective_id, lambda s, t, *refs: forward_kernel(s, t, counts, recuts, *refs), operands, outs, scratch, stored=True)
    )
    gains = got(1)[0]
    flat_weights = [w.reshape(-1, w.shape[-1]) for w in got(10)]
    enc_kept, dec_kept, cross_kept = got(7), got(7), got(7)
    memory_all, enc_out, en2, ahead = got(4)
    return gains, flat_weights, (*enc_kept, None), (*dec_kept, None), (*cross_kept, memory_all), enc_out, en2, ahead


def fast_device(
    enc_in, dec_in, enc_cot, dec_cot, enc_segments, dec_segments, buckets,
    enc_norm1, enc_query, enc_key, enc_value, enc_proj, enc_rel, enc_norm2, enc_gate, enc_up, enc_down, enc_final,
    dec_norm1, dec_query, dec_key, dec_value, dec_proj, dec_rel, dec_norm2, cross_query, cross_key, cross_value, cross_proj,
    dec_norm3, dec_gate, dec_up, dec_down,
):
    groups, cores, parts = sizes = lax.axis_size(HG), lax.axis_size(CORE), lax.axis_size(SP)
    block, model = enc_in.shape
    devices = groups * cores
    share = model // devices
    bf16, f32 = jnp.bfloat16, jnp.float32

    rel_len = enc_rel.shape[0]
    all_gains = jnp.stack([enc_norm1, enc_norm2, enc_final, dec_norm1, dec_norm2, dec_norm3])
    all_rels = jnp.concatenate([enc_rel, dec_rel]).reshape(-1, HEADS)
    small = jnp.concatenate([jnp.pad(w, ((0, 0), (0, 128 - w.shape[1]))) for w in (all_gains, all_rels)])
    each = all_rels.shape[0] // 2
    small = jnp.pad(small, ((0, 16 - small.shape[0]), (0, 0)))

    gains, weights, enc_kept, dec_kept, cross_kept, enc_out, en2, ahead = forward(
        sizes, 1, enc_in, dec_in, small, (6, each), (enc_segments[None, :], dec_segments[None, :]), buckets,
        (
            (enc_key, enc_value, enc_query), (dec_key, dec_value, dec_query), (cross_key, cross_value, cross_query),
            (enc_gate, enc_up), (dec_gate, dec_up), (enc_proj, dec_proj, cross_proj, enc_down, dec_down),
        ),
    )
    enc_kvq, dec_kvq, enc_gu, cross_kvq, dec_gu, enc_wo, dec_wo, enc_wd, cross_wo, dec_wd = weights
    ex, dx, cx = enc_kept[0], dec_kept[0], cross_kept[0]

    (dec_out, dec_in_grad, grad_ex, dg_d1, dg_d2, dg_d3, dg_e2, dg_ef, rel_d), grads_d, sum_a, sum_b, rows_c = decoder_back(
        sizes, 2, gains, (3, 4, 5, 1, 2), (cx, dec_cot, dec_gu, dec_wd),
        (dx, cross_kept, cross_kvq, cross_wo, None), (dec_in, dec_kept, dec_kvq, dec_wo, ahead[1]),
        (ex, enc_out, enc_cot, en2, enc_gu, enc_wd),
    )
    enc_in_grad, sum_c, sum_d, sum_e = encoder_back(
        sizes, 3, gains, 0, grad_ex, (enc_in, enc_kept, enc_kvq, enc_wo, ahead[0]),
        (dg_d1, dg_d2, dg_d3, dg_e2, dg_ef, rel_d), rows_c, grads_d,
    )

    dgu_rows, d_wd = sum_a
    cross_rows, c_wo = sum_b
    egu_rows, e_wd = sum_c
    dkvq_rows, d_wo = sum_d
    ekvq_rows, small_rows, e_wo = sum_e
    (
        enc_out, dec_out, enc_in_grad, dec_in_grad, e_wk, e_wv, e_wq, e_wg, e_wu, d_wk, d_wv, d_wq, c_wk, c_wv, c_wq, d_wg, d_wu, d_wd, c_wo, e_wd, d_wo, e_wo
    ) = unpack(
        [enc_out, dec_out, enc_in_grad, dec_in_grad, ekvq_rows, egu_rows, dkvq_rows, cross_rows, dgu_rows, d_wd, c_wo, e_wd, d_wo, e_wo],
        (-1, -1, -1, -1, 3, 2, 3, 3, 2, 0, 0, 0, 0, 0),
    )
    own = jnp.sum(small_rows.astype(f32), axis=0)
    s = [own[i, :share] for i in range(6)]
    e_rel, d_rel = [own[6 + i * each : 6 + (i + 1) * each, :HEADS].reshape(rel_len) for i in range(2)]
    return (
        enc_out, dec_out, enc_in_grad, dec_in_grad,
        s[0], e_wq, e_wk, e_wv, e_wo, e_rel, s[1], e_wg, e_wu, e_wd, s[2],
        s[3], d_wq, d_wk, d_wv, d_wo, d_rel, s[4], c_wq, c_wk, c_wv, c_wo, s[5], d_wg, d_wu, d_wd,
    )


def general_plan(mesh):
    placed = (
        P(("ctx", "sp"), None),
        P(("ctx", "sp"), None),
        P(("ctx", "sp"), None),
        P(("ctx", "sp"), None),
        P(),
        P(),
        P(),
        P("ctx"),
        P("ctx", None),
        P("ctx", None),
        P("ctx", None),
        P("ctx", None),
        P("ctx"),
        P("ctx"),
        P("ctx", None),
        P("ctx", None),
        P("ctx", None),
        P("ctx"),
        P("ctx"),
        P("ctx", None),
        P("ctx", None),
        P("ctx", None),
        P("ctx", None),
        P("ctx"),
        P("ctx"),
        P("ctx", None),
        P("ctx", None),
        P("ctx", None),
        P("ctx", None),
        P("ctx"),
        P("ctx", None),
        P("ctx", None),
        P("ctx", None),
    )
    return jax.shard_map(
        per_device,
        mesh=mesh,
        in_specs=placed,
        out_specs=(
            P(("ctx", "sp"), None),
            P(("ctx", "sp"), None),
            P(("ctx", "sp"), None),
            P(("ctx", "sp"), None),
            P("ctx"),
            P("ctx", None),
            P("ctx", None),
            P("ctx", None),
            P("ctx", None),
            P("ctx"),
            P("ctx"),
            P("ctx", None),
            P("ctx", None),
            P("ctx", None),
            P("ctx"),
            P("ctx"),
            P("ctx", None),
            P("ctx", None),
            P("ctx", None),
            P("ctx", None),
            P("ctx"),
            P("ctx"),
            P("ctx", None),
            P("ctx", None),
            P("ctx", None),
            P("ctx", None),
            P("ctx"),
            P("ctx", None),
            P("ctx", None),
            P("ctx", None),
        ),
        check_vma=False,
    )


def split_plan(mesh, groups):
    cut = Mesh(np.asarray(mesh.devices).reshape(groups, 2, mesh.shape["sp"]), (HG, CORE, SP))
    tokens, rows, gain, same = P((HG, CORE, SP), None), P((HG, CORE), None), P((HG, CORE)), P()
    attention = (gain, rows, rows, rows, rows, gain)
    feed = (gain, rows, rows, rows)
    weights = attention + feed + (gain,) + attention + (gain, rows, rows, rows, rows) + feed
    return jax.shard_map(
        fast_device,
        mesh=cut,
        in_specs=(tokens,) * 4 + (same,) * 3 + weights,
        out_specs=(tokens,) * 4 + weights,
        check_vma=False,
    )


def solution(mesh):
    groups, odd = divmod(mesh.shape["ctx"], 2)
    if odd or HEADS % groups or mesh.shape["sp"] != 4:
        return general_plan(mesh)
    return split_plan(mesh, groups)
```

```python
import functools
import math

import jax
import jax.numpy as jnp
import numpy as np
from jax import lax
from jax.experimental import pallas as pl
from jax.experimental.pallas import tpu as pltpu
from jax.sharding import Mesh
from jax.sharding import PartitionSpec as P

HEADS = 12
HD = 64


EPSILON = 1e-06
NEGATIVE = -1e30
HIGHEST = lax.Precision.HIGHEST


def rms_norm(values, norm_gain):
    return (
        values * lax.rsqrt(jnp.mean(values * values, axis=-1, keepdims=True) + EPSILON) * norm_gain
    )


def norm_pullback(values, norm_gain, grad_normed):
    _, pullback = jax.vjp(rms_norm, values, norm_gain)
    return pullback(grad_normed)


def gated(gate_val, up_val):
    return jax.nn.gelu(gate_val, approximate=True) * up_val


def project(left, right):
    return jnp.dot(left, right, preferred_element_type=jnp.float32)


def weight_grad(left, right):
    return jnp.einsum("td,te->de", left, right, preferred_element_type=jnp.float32)


def input_grad(grad_out, weight):
    return jnp.einsum("te,de->td", grad_out, weight, preferred_element_type=jnp.float32)


def head_table(relative, table_row, heads_here):
    bucket_count = relative.shape[0] // HEADS
    onehot = (table_row[:, None] == jnp.arange(bucket_count, dtype=jnp.int32)[None, :]).astype(
        jnp.float32
    )
    bias_grid = relative.astype(jnp.float32).reshape(bucket_count, HEADS)
    full_table = jnp.dot(onehot, bias_grid, precision=HIGHEST).T
    first_head = lax.axis_index("sp") * heads_here
    return (lax.dynamic_slice_in_dim(full_table, first_head, heads_here, 0), onehot)


def table_grad(grad_table, onehot, heads_here):
    full_grad = jnp.zeros((HEADS, onehot.shape[0]), jnp.float32)
    full_grad = lax.dynamic_update_slice_in_dim(
        full_grad, grad_table, lax.axis_index("sp") * heads_here, 0
    )
    return jnp.dot(onehot.T, full_grad.T, precision=HIGHEST).reshape(-1)


def bias_block(head_bias, pad_len, offset_q, rows, offset_k, cols):
    head_count, table_len = head_bias.shape
    reach_len = (table_len - 1) // 2
    left_edge = jnp.broadcast_to(head_bias[:, :1], (head_count, pad_len))
    right_edge = jnp.broadcast_to(head_bias[:, -1:], (head_count, pad_len))
    padded = jnp.concatenate([left_edge, head_bias, right_edge], axis=1)
    band_width = rows + cols - 1
    start = offset_k - offset_q - (rows - 1) + reach_len + pad_len
    band = lax.dynamic_slice_in_dim(padded, start, band_width, 1)
    tiled = jnp.broadcast_to(band[:, None, :], (head_count, rows, band_width)).reshape(
        head_count, rows * band_width
    )
    skewed = tiled[:, rows - 1 : rows - 1 + rows * (band_width - 1)].reshape(
        head_count, rows, band_width - 1
    )
    return skewed[:, :, :cols]


def make_frame(query_local, query_ids, key_ids, head_bias, causal):
    local_len = query_local.shape[0]
    heads_here = query_local.shape[1] // HD
    offset_q = lax.axis_index("ctx") * local_len
    ids_q = lax.dynamic_slice_in_dim(query_ids, offset_q, local_len, 0)
    row_ids = offset_q + jnp.arange(local_len, dtype=jnp.int32)
    query_heads = query_local.reshape(local_len, heads_here, HD)
    pad_len = query_ids.shape[0] + key_ids.shape[0]

    def bias_of(entries, offset_k, length):
        return bias_block(entries, pad_len, offset_q, local_len, offset_k, length)

    def scores_of(key_block, offset_k):
        length = key_block.shape[0]
        key_heads = key_block.reshape(length, heads_here, HD)
        raw_scores = jnp.einsum(
            "qhd,khd->hqk", query_heads, key_heads, preferred_element_type=jnp.float32
        )
        col_ids = offset_k + jnp.arange(length, dtype=jnp.int32)
        ids_k = lax.dynamic_slice_in_dim(key_ids, offset_k, length, 0)
        allowed = ids_q[:, None] == ids_k[None, :]
        if causal:
            allowed = allowed & (col_ids[None, :] <= row_ids[:, None])
        if head_bias is not None:
            raw_scores = raw_scores + bias_of(head_bias, offset_k, length)
        return (raw_scores, allowed)

    def touches(offset_k, length):
        first_id = lax.dynamic_slice_in_dim(key_ids, offset_k, 1, 0)[0]
        last_id = lax.dynamic_slice_in_dim(key_ids, offset_k + length - 1, 1, 0)[0]
        touched = (ids_q[0] <= last_id) & (first_id <= ids_q[-1])
        if causal:
            touched = touched & (offset_k <= offset_q + local_len - 1)
        return touched

    return (query_heads, scores_of, touches, bias_of)


def sweep(keys_gathered, local_len, step_fn, carry_state):
    key_all, value_all = keys_gathered
    block_len = local_len * math.gcd(4, lax.axis_size("ctx"))

    def sweep_loop_body(number, running):
        offset_k = number * block_len
        key_block = lax.dynamic_slice_in_dim(key_all, offset_k, block_len, 0)
        value_block = lax.dynamic_slice_in_dim(value_all, offset_k, block_len, 0)
        return step_fn(running, key_block, value_block, offset_k)

    return lax.fori_loop(0, key_all.shape[0] // block_len, sweep_loop_body, carry_state)


def whole_keys(key_local, value_local):
    return (
        lax.all_gather(key_local, "ctx", axis=0, tiled=True),
        lax.all_gather(value_local, "ctx", axis=0, tiled=True),
    )


def attention_forward(query_proj, key_proj, value_proj, query_ids, key_ids, head_bias, causal):
    query_local, key_local, value_local = (
        lax.all_to_all(query_proj, "sp", split_axis=1, concat_axis=0, tiled=True),
        lax.all_to_all(key_proj, "sp", split_axis=1, concat_axis=0, tiled=True),
        lax.all_to_all(value_proj, "sp", split_axis=1, concat_axis=0, tiled=True),
    )
    local_len = query_local.shape[0]
    heads_here = query_local.shape[1] // HD
    query_heads, scores_of, touches, _ = make_frame(
        query_local, query_ids, key_ids, head_bias, causal
    )
    key_block = lax.all_gather(key_local, "ctx", axis=0, tiled=True)
    value_block = lax.all_gather(value_local, "ctx", axis=0, tiled=True)
    offset_k = jnp.int32(0)
    length = key_block.shape[0]
    row_top = jnp.full((heads_here, local_len), NEGATIVE, jnp.float32)
    weighted = jnp.zeros((local_len, heads_here, HD), jnp.float32)
    raw_scores, allowed = scores_of(key_block, offset_k)
    masked = jnp.where(allowed[None], raw_scores, NEGATIVE)
    new_top = jnp.maximum(row_top, jnp.max(masked, axis=-1))
    weights = jnp.where(allowed[None], jnp.exp(masked - new_top[..., None]), 0.0)
    rescale = jnp.exp(row_top - new_top)
    value_heads = value_block.reshape(length, heads_here, HD)
    increment = jnp.einsum(
        "hqk,khd->qhd",
        weights.astype(jnp.bfloat16),
        value_heads,
        preferred_element_type=jnp.float32,
    )
    row_top, row_total, weighted = (
        new_top,
        jnp.sum(weights, axis=-1),
        weighted * rescale.T[:, :, None] + increment,
    )
    mixed_heads = weighted / row_total.T[:, :, None]
    log_total = row_top + jnp.log(row_total)
    mixed_low = mixed_heads.reshape(local_len, heads_here * HD).astype(jnp.bfloat16)
    mixed_tokens = lax.all_to_all(mixed_low, "sp", split_axis=0, concat_axis=1, tiled=True)
    retained = (
        query_local,
        key_local,
        value_local,
        mixed_heads,
        log_total,
        None,
        query_ids,
        key_ids,
        head_bias,
        causal,
    )
    return (mixed_tokens, retained)


def attention_backward(grad_mixed, retained):
    (
        query_local,
        key_local,
        value_local,
        mixed_heads,
        log_total,
        gathered,
        query_ids,
        key_ids,
        head_bias,
        causal,
    ) = retained
    grad_local = lax.all_to_all(grad_mixed, "sp", split_axis=1, concat_axis=0, tiled=True)
    local_len = query_local.shape[0]
    heads_here = query_local.shape[1] // HD
    width = heads_here * HD
    query_heads, scores_of, touches, bias_of = make_frame(
        query_local, query_ids, key_ids, head_bias, causal
    )
    grad_heads = grad_local.reshape(local_len, heads_here, HD)
    row_inner = jnp.einsum("qhd,qhd->hq", grad_heads.astype(jnp.float32), mixed_heads)
    gathered = whole_keys(key_local, value_local)
    table_zero = jnp.zeros(head_bias.shape if head_bias is not None else (1,), jnp.float32)

    def gradients_of(key_block, value_block, offset_k):
        length = key_block.shape[0]
        raw_scores, allowed = scores_of(key_block, offset_k)
        probabilities = jnp.where(allowed[None], jnp.exp(raw_scores - log_total[..., None]), 0.0)
        value_heads = value_block.reshape(length, heads_here, HD)
        grad_probs = jnp.einsum(
            "qhd,khd->hqk", grad_heads, value_heads, preferred_element_type=jnp.float32
        )
        grad_scores = (probabilities * (grad_probs - row_inner[..., None])).astype(jnp.bfloat16)
        return (probabilities, grad_scores)

    def table_part(grad_scores, offset_k, length):
        if head_bias is None:
            return table_zero
        _, pullback = jax.vjp(lambda entries: bias_of(entries, offset_k, length), head_bias)
        return pullback(grad_scores.astype(jnp.float32))[0]

    def key_terms_of(probabilities, grad_scores, length):
        grad_key = jnp.einsum(
            "hqk,qhd->khd", grad_scores, query_heads, preferred_element_type=jnp.float32
        )
        grad_value = jnp.einsum(
            "hqk,qhd->khd",
            probabilities.astype(jnp.bfloat16),
            grad_heads,
            preferred_element_type=jnp.float32,
        )
        return jnp.concatenate(
            [grad_key.reshape(length, width), grad_value.reshape(length, width)], axis=1
        )

    def query_part(grad_scores, key_block):
        length = key_block.shape[0]
        key_heads = key_block.reshape(length, heads_here, HD)
        return jnp.einsum(
            "hqk,khd->qhd", grad_scores, key_heads, preferred_element_type=jnp.float32
        )

    def query_step(running, key_block, value_block, offset_k):
        length = key_block.shape[0]
        grad_query, grad_table = running
        probabilities, grad_scores = gradients_of(key_block, value_block, offset_k)
        return (
            grad_query + query_part(grad_scores, key_block),
            grad_table + table_part(grad_scores, offset_k, length),
        )

    query_zero = jnp.zeros((local_len, heads_here, HD), jnp.float32)
    block_len = local_len * math.gcd(4, lax.axis_size("ctx"))
    grad_query, grad_table = sweep(gathered, local_len, query_step, (query_zero, table_zero))
    key_all, value_all = gathered
    step_len = math.gcd(lax.axis_size("ctx") * local_len, block_len)

    def term_loop_body(number, rows_acc):
        offset_b = number * step_len
        key_block = lax.dynamic_slice_in_dim(key_all, offset_b, step_len, 0)
        value_block = lax.dynamic_slice_in_dim(value_all, offset_b, step_len, 0)
        probabilities, grad_scores = gradients_of(key_block, value_block, offset_b)
        return lax.dynamic_update_slice_in_dim(
            rows_acc, key_terms_of(probabilities, grad_scores, step_len), number * step_len, 0
        )

    own_rows = lax.psum_scatter(
        lax.fori_loop(
            0,
            lax.axis_size("ctx") * local_len // step_len,
            term_loop_body,
            jnp.zeros((lax.axis_size("ctx") * local_len, 2 * width), jnp.float32),
        ),
        "ctx",
        scatter_dimension=0,
        tiled=True,
    )
    grad_q_low = grad_query.reshape(local_len, width).astype(jnp.bfloat16)
    grad_k_low = own_rows[:, :width].astype(jnp.bfloat16)
    grad_v_low = own_rows[:, width:].astype(jnp.bfloat16)
    grad_q_tok, grad_k_tok, grad_v_tok = (
        lax.all_to_all(grad_q_low, "sp", split_axis=0, concat_axis=1, tiled=True),
        lax.all_to_all(grad_k_low, "sp", split_axis=0, concat_axis=1, tiled=True),
        lax.all_to_all(grad_v_low, "sp", split_axis=0, concat_axis=1, tiled=True),
    )
    return (grad_q_tok, grad_k_tok, grad_v_tok, grad_table)


def attention_layer(
    residual,
    source,
    norm_gain,
    w_query,
    w_key,
    w_value,
    w_proj,
    query_ids,
    key_ids,
    head_bias,
    causal,
):
    normed = rms_norm(residual, norm_gain).astype(jnp.bfloat16)
    kv_input = normed if source is None else source
    query_proj = project(normed, w_query).astype(jnp.bfloat16)
    key_proj = project(kv_input, w_key).astype(jnp.bfloat16)
    value_proj = project(kv_input, w_value).astype(jnp.bfloat16)
    mixed_tokens, retained = attention_forward(
        query_proj, key_proj, value_proj, query_ids, key_ids, head_bias, causal
    )
    result = residual + project(mixed_tokens, w_proj)
    return (result, (residual, normed, kv_input, mixed_tokens, retained))


def attention_layer_back(grad_out, saved, norm_gain, w_query, w_key, w_value, w_proj, is_cross):
    residual, normed, kv_input, mixed_tokens, retained = saved
    grad_low = grad_out.astype(jnp.bfloat16)
    grad_proj = weight_grad(mixed_tokens, grad_low)
    grad_mixed = input_grad(grad_low, w_proj).astype(jnp.bfloat16)
    grad_q_tok, grad_k_tok, grad_v_tok, grad_table = attention_backward(grad_mixed, retained)
    grad_wq = weight_grad(normed, grad_q_tok)
    grad_wk = weight_grad(kv_input, grad_k_tok)
    grad_wv = weight_grad(kv_input, grad_v_tok)
    grad_source = input_grad(grad_k_tok, w_key) + input_grad(grad_v_tok, w_value)
    grad_normed = input_grad(grad_q_tok, w_query)
    if not is_cross:
        grad_normed = grad_normed + grad_source
        grad_source = None
    grad_resid, grad_gain = norm_pullback(residual, norm_gain, grad_normed)
    return (
        grad_out + grad_resid,
        grad_source,
        (grad_gain, grad_wq, grad_wk, grad_wv, grad_proj, grad_table),
    )


def feed_layer(residual, norm_gain, w_gate, w_up, w_down):
    normed = rms_norm(residual, norm_gain).astype(jnp.bfloat16)
    gate_val = project(normed, w_gate)
    up_val = project(normed, w_up)
    hidden = gated(gate_val, up_val).astype(jnp.bfloat16)
    return (residual + project(hidden, w_down), (residual, normed, gate_val, up_val, hidden))


def feed_layer_back(grad_out, saved, norm_gain, w_gate, w_up, w_down):
    residual, normed, gate_val, up_val, hidden = saved
    grad_low = grad_out.astype(jnp.bfloat16)
    grad_down = weight_grad(hidden, grad_low)
    grad_hidden = input_grad(grad_low, w_down)
    _, pullback = jax.vjp(gated, gate_val, up_val)
    grad_gate, grad_up = pullback(grad_hidden)
    grad_gate = grad_gate.astype(jnp.bfloat16)
    grad_up = grad_up.astype(jnp.bfloat16)
    grad_wg = weight_grad(normed, grad_gate)
    grad_wu = weight_grad(normed, grad_up)
    grad_normed = input_grad(grad_gate, w_gate) + input_grad(grad_up, w_up)
    grad_resid, grad_gain = norm_pullback(residual, norm_gain, grad_normed)
    return (grad_out + grad_resid, (grad_gain, grad_wg, grad_wu, grad_down))


def per_device(
    enc_in,
    dec_in,
    enc_cot,
    dec_cot,
    enc_segments,
    dec_segments,
    buckets,
    enc_norm1,
    enc_query,
    enc_key,
    enc_value,
    enc_proj,
    enc_rel,
    enc_norm2,
    enc_gate,
    enc_up,
    enc_down,
    enc_final,
    dec_norm1,
    dec_query,
    dec_key,
    dec_value,
    dec_proj,
    dec_rel,
    dec_norm2,
    cross_query,
    cross_key,
    cross_value,
    cross_proj,
    dec_norm3,
    dec_gate,
    dec_up,
    dec_down,
):
    (
        enc_norm1,
        enc_query,
        enc_key,
        enc_value,
        enc_proj,
        enc_rel,
        enc_norm2,
        enc_gate,
        enc_up,
        enc_down,
        enc_final,
        dec_norm1,
        dec_query,
        dec_key,
        dec_value,
        dec_proj,
        dec_rel,
        dec_norm2,
        cross_query,
        cross_key,
        cross_value,
        cross_proj,
        dec_norm3,
        dec_gate,
        dec_up,
        dec_down,
    ) = (
        lax.all_gather(enc_norm1, "ctx", axis=0, tiled=True),
        lax.all_gather(enc_query, "ctx", axis=0, tiled=True),
        lax.all_gather(enc_key, "ctx", axis=0, tiled=True),
        lax.all_gather(enc_value, "ctx", axis=0, tiled=True),
        lax.all_gather(enc_proj, "ctx", axis=0, tiled=True),
        lax.all_gather(enc_rel, "ctx", axis=0, tiled=True),
        lax.all_gather(enc_norm2, "ctx", axis=0, tiled=True),
        lax.all_gather(enc_gate, "ctx", axis=0, tiled=True),
        lax.all_gather(enc_up, "ctx", axis=0, tiled=True),
        lax.all_gather(enc_down, "ctx", axis=0, tiled=True),
        lax.all_gather(enc_final, "ctx", axis=0, tiled=True),
        lax.all_gather(dec_norm1, "ctx", axis=0, tiled=True),
        lax.all_gather(dec_query, "ctx", axis=0, tiled=True),
        lax.all_gather(dec_key, "ctx", axis=0, tiled=True),
        lax.all_gather(dec_value, "ctx", axis=0, tiled=True),
        lax.all_gather(dec_proj, "ctx", axis=0, tiled=True),
        lax.all_gather(dec_rel, "ctx", axis=0, tiled=True),
        lax.all_gather(dec_norm2, "ctx", axis=0, tiled=True),
        lax.all_gather(cross_query, "ctx", axis=0, tiled=True),
        lax.all_gather(cross_key, "ctx", axis=0, tiled=True),
        lax.all_gather(cross_value, "ctx", axis=0, tiled=True),
        lax.all_gather(cross_proj, "ctx", axis=0, tiled=True),
        lax.all_gather(dec_norm3, "ctx", axis=0, tiled=True),
        lax.all_gather(dec_gate, "ctx", axis=0, tiled=True),
        lax.all_gather(dec_up, "ctx", axis=0, tiled=True),
        lax.all_gather(dec_down, "ctx", axis=0, tiled=True),
    )
    enc_norm1 = enc_norm1.astype(jnp.float32)
    enc_norm2 = enc_norm2.astype(jnp.float32)
    enc_final = enc_final.astype(jnp.float32)
    dec_norm1 = dec_norm1.astype(jnp.float32)
    dec_norm2 = dec_norm2.astype(jnp.float32)
    dec_norm3 = dec_norm3.astype(jnp.float32)
    heads_here = HEADS // lax.axis_size("sp")
    enc_table, enc_onehot = head_table(enc_rel, buckets[0], heads_here)
    dec_table, dec_onehot = head_table(dec_rel, buckets[1], heads_here)
    enc_x = enc_in.astype(jnp.float32)
    enc_mid, enc_saved_a = attention_layer(
        enc_x,
        None,
        enc_norm1,
        enc_query,
        enc_key,
        enc_value,
        enc_proj,
        enc_segments,
        enc_segments,
        enc_table,
        False,
    )
    enc_result, enc_saved_f = feed_layer(enc_mid, enc_norm2, enc_gate, enc_up, enc_down)
    memory = rms_norm(enc_result, enc_final).astype(jnp.bfloat16)
    dec_x = dec_in.astype(jnp.float32)
    dec_mid, dec_saved_a = attention_layer(
        dec_x,
        None,
        dec_norm1,
        dec_query,
        dec_key,
        dec_value,
        dec_proj,
        dec_segments,
        dec_segments,
        dec_table,
        True,
    )
    dec_cross, dec_saved_c = attention_layer(
        dec_mid,
        memory,
        dec_norm2,
        cross_query,
        cross_key,
        cross_value,
        cross_proj,
        dec_segments,
        enc_segments,
        None,
        False,
    )
    dec_result, dec_saved_f = feed_layer(dec_cross, dec_norm3, dec_gate, dec_up, dec_down)
    grad_dec, dec_ff_grads = feed_layer_back(
        dec_cot.astype(jnp.float32), dec_saved_f, dec_norm3, dec_gate, dec_up, dec_down
    )
    grad_dec, grad_memory, cross_grads = attention_layer_back(
        grad_dec, dec_saved_c, dec_norm2, cross_query, cross_key, cross_value, cross_proj, True
    )
    grad_dec, _, dec_self_grads = attention_layer_back(
        grad_dec, dec_saved_a, dec_norm1, dec_query, dec_key, dec_value, dec_proj, False
    )
    grad_enc_out, grad_final = norm_pullback(enc_result, enc_final, grad_memory)
    grad_enc, enc_ff_grads = feed_layer_back(
        enc_cot.astype(jnp.float32) + grad_enc_out,
        enc_saved_f,
        enc_norm2,
        enc_gate,
        enc_up,
        enc_down,
    )
    grad_enc, _, enc_self_grads = attention_layer_back(
        grad_enc, enc_saved_a, enc_norm1, enc_query, enc_key, enc_value, enc_proj, False
    )
    e_gain1, e_wq, e_wk, e_wv, e_wo, e_table = enc_self_grads
    e_gain2, e_wg, e_wu, e_wd = enc_ff_grads
    d_gain1, d_wq, d_wk, d_wv, d_wo, d_table = dec_self_grads
    c_gain, c_wq, c_wk, c_wv, c_wo, _ = cross_grads
    d_gain3, d_wg, d_wu, d_wd = dec_ff_grads
    e_rel = table_grad(e_table, enc_onehot, heads_here)
    d_rel = table_grad(d_table, dec_onehot, heads_here)
    shards = (
        lax.psum_scatter(e_gain1, "ctx", scatter_dimension=0, tiled=True),
        lax.psum_scatter(e_wq, "ctx", scatter_dimension=0, tiled=True),
        lax.psum_scatter(e_wk, "ctx", scatter_dimension=0, tiled=True),
        lax.psum_scatter(e_wv, "ctx", scatter_dimension=0, tiled=True),
        lax.psum_scatter(e_wo, "ctx", scatter_dimension=0, tiled=True),
        lax.psum_scatter(e_rel, "ctx", scatter_dimension=0, tiled=True),
        lax.psum_scatter(e_gain2, "ctx", scatter_dimension=0, tiled=True),
        lax.psum_scatter(e_wg, "ctx", scatter_dimension=0, tiled=True),
        lax.psum_scatter(e_wu, "ctx", scatter_dimension=0, tiled=True),
        lax.psum_scatter(e_wd, "ctx", scatter_dimension=0, tiled=True),
        lax.psum_scatter(grad_final, "ctx", scatter_dimension=0, tiled=True),
        lax.psum_scatter(d_gain1, "ctx", scatter_dimension=0, tiled=True),
        lax.psum_scatter(d_wq, "ctx", scatter_dimension=0, tiled=True),
        lax.psum_scatter(d_wk, "ctx", scatter_dimension=0, tiled=True),
        lax.psum_scatter(d_wv, "ctx", scatter_dimension=0, tiled=True),
        lax.psum_scatter(d_wo, "ctx", scatter_dimension=0, tiled=True),
        lax.psum_scatter(d_rel, "ctx", scatter_dimension=0, tiled=True),
        lax.psum_scatter(c_gain, "ctx", scatter_dimension=0, tiled=True),
        lax.psum_scatter(c_wq, "ctx", scatter_dimension=0, tiled=True),
        lax.psum_scatter(c_wk, "ctx", scatter_dimension=0, tiled=True),
        lax.psum_scatter(c_wv, "ctx", scatter_dimension=0, tiled=True),
        lax.psum_scatter(c_wo, "ctx", scatter_dimension=0, tiled=True),
        lax.psum_scatter(d_gain3, "ctx", scatter_dimension=0, tiled=True),
        lax.psum_scatter(d_wg, "ctx", scatter_dimension=0, tiled=True),
        lax.psum_scatter(d_wu, "ctx", scatter_dimension=0, tiled=True),
        lax.psum_scatter(d_wd, "ctx", scatter_dimension=0, tiled=True),
    )
    (
        s_gain1,
        s_wq,
        s_wk,
        s_wv,
        s_wo,
        s_rel,
        s_gain2,
        s_wg,
        s_wu,
        s_wd,
        s_final,
        t_gain1,
        t_wq,
        t_wk,
        t_wv,
        t_wo,
        t_rel,
        t_gain2,
        t_cq,
        t_ck,
        t_cv,
        t_co,
        t_gain3,
        t_wg,
        t_wu,
        t_wd,
    ) = shards
    reduced = (
        lax.psum(s_gain1.astype(jnp.bfloat16), "sp").astype(jnp.float32),
        lax.psum(s_wq.astype(jnp.bfloat16), "sp").astype(jnp.float32),
        lax.psum(s_wk.astype(jnp.bfloat16), "sp").astype(jnp.float32),
        lax.psum(s_wv.astype(jnp.bfloat16), "sp").astype(jnp.float32),
        lax.psum(s_wo.astype(jnp.bfloat16), "sp").astype(jnp.float32),
        lax.psum(s_rel.astype(jnp.bfloat16), "sp").astype(jnp.float32),
        lax.psum(s_gain2.astype(jnp.bfloat16), "sp").astype(jnp.float32),
        lax.psum(s_wg.astype(jnp.bfloat16), "sp").astype(jnp.float32),
        lax.psum(s_wu.astype(jnp.bfloat16), "sp").astype(jnp.float32),
        lax.psum(s_wd.astype(jnp.bfloat16), "sp").astype(jnp.float32),
        lax.psum(s_final.astype(jnp.bfloat16), "sp").astype(jnp.float32),
        lax.psum(t_gain1.astype(jnp.bfloat16), "sp").astype(jnp.float32),
        lax.psum(t_wq.astype(jnp.bfloat16), "sp").astype(jnp.float32),
        lax.psum(t_wk.astype(jnp.bfloat16), "sp").astype(jnp.float32),
        lax.psum(t_wv.astype(jnp.bfloat16), "sp").astype(jnp.float32),
        lax.psum(t_wo.astype(jnp.bfloat16), "sp").astype(jnp.float32),
        lax.psum(t_rel.astype(jnp.bfloat16), "sp").astype(jnp.float32),
        lax.psum(t_gain2.astype(jnp.bfloat16), "sp").astype(jnp.float32),
        lax.psum(t_cq.astype(jnp.bfloat16), "sp").astype(jnp.float32),
        lax.psum(t_ck.astype(jnp.bfloat16), "sp").astype(jnp.float32),
        lax.psum(t_cv.astype(jnp.bfloat16), "sp").astype(jnp.float32),
        lax.psum(t_co.astype(jnp.bfloat16), "sp").astype(jnp.float32),
        lax.psum(t_gain3.astype(jnp.bfloat16), "sp").astype(jnp.float32),
        lax.psum(t_wg.astype(jnp.bfloat16), "sp").astype(jnp.float32),
        lax.psum(t_wu.astype(jnp.bfloat16), "sp").astype(jnp.float32),
        lax.psum(t_wd.astype(jnp.bfloat16), "sp").astype(jnp.float32),
    )
    return (enc_result, dec_result, grad_enc, grad_dec) + tuple(reduced)


HG, CORE, SP = "hg", "core", "sp"
BLOCK_PAD = 128
VMEM_BYTES = 60 << 20


def nt(left, right):
    return lax.dot_general(left, right, (((1,), (1,)), ((), ())), preferred_element_type=jnp.float32)


def tn(left, right):
    return lax.dot_general(left, right, (((0,), (0,)), ((), ())), preferred_element_type=jnp.float32)


def nn(left, right):
    return jnp.dot(left, right, preferred_element_type=jnp.float32)


def low(value):
    return value.astype(jnp.bfloat16)


def identity(size):
    rows = lax.broadcasted_iota(jnp.int32, (size, size), 0)
    cols = lax.broadcasted_iota(jnp.int32, (size, size), 1)
    return low(jnp.where(rows == cols, 1.0, 0.0))


def only_lanes(array, first, count):
    lanes = lax.broadcasted_iota(jnp.int32, array.shape, 1)
    return jnp.where((lanes >= first) & (lanes < first + count), array, jnp.zeros_like(array))


def gelu_and_slope(v):
    scale, cubic = math.sqrt(2.0 / math.pi), 0.044715
    t = jnp.tanh(scale * (v + cubic * v * v * v))
    return 0.5 * v * (1.0 + t), 0.5 * (1.0 + t) + 0.5 * v * (1.0 - t * t) * scale * (1.0 + 3.0 * cubic * v * v)


def norm_back(x, g, dn):
    r = lax.rsqrt(jnp.mean(x * x, axis=-1, keepdims=True) + EPSILON)
    w = dn * g
    dx = r * w - x * (r * r * r) * jnp.mean(w * x, axis=-1, keepdims=True)
    return dx, jnp.sum(dn * x * r, axis=0, keepdims=True)


def send(src, dst, send_sem, recv_sem, to):
    copy = pltpu.make_async_remote_copy(
        src_ref=src, dst_ref=dst, send_sem=send_sem, recv_sem=recv_sem, device_id=to, device_id_type=pl.DeviceIdType.MESH
    )
    copy.start()
    return copy


def arrived(dst, send_sem, recv_sem, to):
    pltpu.make_async_remote_copy(
        src_ref=dst, dst_ref=dst, send_sem=send_sem, recv_sem=recv_sem, device_id=to, device_id_type=pl.DeviceIdType.MESH
    ).wait_recv()


class Place:
    def __init__(self, groups, cores, parts):
        self.groups, self.cores, self.parts = groups, cores, parts
        self.group, self.core, self.part = lax.axis_index(HG), lax.axis_index(CORE), lax.axis_index(SP)

    def ahead(self, step):
        return lax.rem(self.group + step, self.groups)

    def behind(self, step):
        return lax.rem(self.group + self.groups - step, self.groups)

    def chip(self, group):
        return (group, self.core, self.part)

    def sibling(self):
        return (self.group, 1 - self.core, self.part)

    def plane(self, step):
        return lax.rem(self.part + step, self.parts)

    def plane_behind(self, step):
        return lax.rem(self.part + self.parts - step, self.parts)

    def at_plane(self, part):
        return (self.group, self.core, part)

    def first_token(self, number, block):
        return pl.multiple_of(((self.cores * number + self.core) * self.parts + self.part) * block, block)

    def greet(self, planes=False):
        barrier = pltpu.get_barrier_semaphore()
        partners = [self.chip(self.ahead(step)) for step in range(1, self.groups)] + [self.sibling()]
        if planes:
            partners += [self.at_plane(self.plane(step)) for step in range(1, self.parts)]
        for partner in partners:
            pl.semaphore_signal(barrier, inc=1, device_id=partner, device_id_type=pl.DeviceIdType.MESH)
        pl.semaphore_wait(barrier, len(partners))


def spread_start(place, buf, sent, got):
    mine = buf.at[place.group]
    return [
        send(mine, mine, sent.at[step], got.at[step], place.chip(place.ahead(step))) for step in range(1, place.groups)
    ]


def spread_wait(place, buf, sent, got):
    for step in range(1, place.groups):
        source = place.behind(step)
        arrived(buf.at[source], sent.at[step], got.at[step], place.chip(source))


def collect_start(place, partial, out_buf, in_buf, sent, got):
    out_buf[...] = low(partial).reshape(out_buf.shape)
    pending = []
    for step in range(1, place.groups):
        to = place.ahead(step)
        pending.append(send(out_buf.at[to], in_buf.at[place.group], sent.at[step], got.at[step], place.chip(to)))
    return pending


def collect_wait(place, out_buf, in_buf, sent, got):
    total = out_buf[place.group].astype(jnp.float32)
    for step in range(1, place.groups):
        source = place.behind(step)
        arrived(in_buf.at[source], sent.at[step], got.at[step], place.chip(source))
        total = total + in_buf[source].astype(jnp.float32)
    return total


def all_rows(buf):
    return buf[...].reshape(buf.shape[0] * buf.shape[1], buf.shape[2])


DMA = pltpu.SemaphoreType.DMA
IN_VMEM = pl.BlockSpec(memory_space=pltpu.VMEM)
ANYWHERE = pl.BlockSpec(memory_space=pl.ANY)


class Recut:
    def __init__(self, sizes, col_shapes, row_shapes):
        groups, cores, _ = sizes
        self.cols, self.rows = len(col_shapes), len(row_shapes)
        self.outs = [((groups, cores) + s[1:], jnp.bfloat16) for s in col_shapes]
        self.outs += [((cores,) + s, jnp.bfloat16) for s in row_shapes]
        cols = (self.cols, groups)
        self.scratch = [DMA(cols)] * 4 + [DMA((self.rows,))] * 2 + [DMA((self.cols + self.rows,))]

    def bind(self, ins, outs, scratch):
        self.col_refs, self.row_refs = ins[: self.cols], ins[self.cols :]
        self.col_outs, self.row_outs = outs[: self.cols], outs[self.cols :]
        self.sems = scratch
        self.pending, self.copies = [], []

    def begin(self, place):
        sent, got, relay_sent, relay_got, pair_sent, pair_got, local = self.sems
        group, core = place.group, place.core
        for index, (ref, out) in enumerate(zip(self.col_refs, self.col_outs)):
            slot = out.at[group, core]
            for step in range(1, place.groups):
                to = place.ahead(step)
                self.pending.append(send(ref.at[to], slot, sent.at[index, step], got.at[index, step], place.chip(to)))
            self.pending.append(send(ref.at[group], slot, relay_sent.at[index, 0], relay_got.at[index, 0], place.sibling()))
            self.copies.append(pltpu.make_async_copy(ref.at[group], slot, local.at[index]))
        for index, (ref, out) in enumerate(zip(self.row_refs, self.row_outs)):
            slot = out.at[core]
            self.pending.append(send(ref, slot, pair_sent.at[index], pair_got.at[index], place.sibling()))
            self.copies.append(pltpu.make_async_copy(ref, slot, local.at[self.cols + index]))
        for copy in self.copies:
            copy.start()

    def middle(self, place):
        sent, got, relay_sent, relay_got = self.sems[:4]
        for index, out in enumerate(self.col_outs):
            for step in range(1, place.groups):
                source = place.behind(step)
                slot = out.at[source, place.core]
                arrived(slot, sent.at[index, step], got.at[index, step], place.chip(source))
                self.pending.append(
                    send(slot, slot, relay_sent.at[index, step], relay_got.at[index, step], place.sibling())
                )

    def end(self, place):
        _, _, relay_sent, relay_got, pair_sent, pair_got, _ = self.sems
        for index, out in enumerate(self.col_outs):
            for step in range(place.groups):
                slot = out.at[place.behind(step), 1 - place.core]
                arrived(slot, relay_sent.at[index, step], relay_got.at[index, step], place.sibling())
        for index, out in enumerate(self.row_outs):
            arrived(out.at[1 - place.core], pair_sent.at[index], pair_got.at[index], place.sibling())
        for copy in self.copies:
            copy.wait()
        for copy in self.pending:
            copy.wait_send()


class GiveRows:
    def __init__(self, sizes, cols, rows):
        self.cols, self.rows = len(cols), len(rows)
        own = [(s[0],) + s[2:] for s in cols] + [(1,) + s[1:] for s in rows]
        self.outs = [(shape, jnp.bfloat16) for shape in own]
        self.scratch = [pltpu.VMEM(shape, jnp.bfloat16) for shape in own + own[: self.cols]]
        self.scratch += [DMA((self.cols, sizes[0]))] * 4 + [DMA((max(1, self.rows),))] * 2

    def bind(self, ins, outs, scratch):
        self.col_refs, self.row_refs = ins[: self.cols], ins[self.cols :]
        self.col_outs, self.row_outs = outs[: self.cols], outs[self.cols :]
        self.col_sibs, scratch = scratch[: self.cols], scratch[self.cols :]
        self.row_sibs, scratch = scratch[: self.rows], scratch[self.rows :]
        self.col_sums, self.sems = scratch[: self.cols], scratch[self.cols :]
        self.pending = []

    def begin(self, place):
        _, _, pair_sent, pair_got, row_sent, row_got = self.sems
        other = 1 - place.core
        for index, (ref, sib) in enumerate(zip(self.col_refs, self.col_sibs)):
            for step in range(place.groups):
                to = place.ahead(step)
                self.pending.append(
                    send(
                        ref.at[to, other], sib.at[to],
                        pair_sent.at[index, step], pair_got.at[index, step], place.sibling(),
                    )
                )
        for index, (ref, sib) in enumerate(zip(self.row_refs, self.row_sibs)):
            self.pending.append(send(ref.at[other], sib.at[0], row_sent.at[index], row_got.at[index], place.sibling()))

    def middle(self, place):
        sent, got, pair_sent, pair_got, row_sent, row_got = self.sems
        core = place.core
        for index, (ref, sib) in enumerate(zip(self.col_refs, self.col_sibs)):
            out, sums = self.col_outs[index], self.col_sums[index]
            for step in list(range(1, place.groups)) + [0]:
                to = place.ahead(step)
                arrived(sib.at[to], pair_sent.at[index, step], pair_got.at[index, step], place.sibling())
                both = low(ref[to, core].astype(jnp.float32) + sib[to].astype(jnp.float32))
                if step:
                    sums[to] = both
                    self.pending.append(
                        send(sums.at[to], out.at[place.group], sent.at[index, step], got.at[index, step], place.chip(to))
                    )
                else:
                    out[place.group] = both
        for index, (ref, sib) in enumerate(zip(self.row_refs, self.row_sibs)):
            arrived(sib.at[0], row_sent.at[index], row_got.at[index], place.sibling())
            self.row_outs[index][0] = low(ref[core].astype(jnp.float32) + sib[0].astype(jnp.float32))

    def end(self, place):
        sent, got = self.sems[:2]
        for index, out in enumerate(self.col_outs):
            for step in range(1, place.groups):
                source = place.behind(step)
                arrived(out.at[source], sent.at[index, step], got.at[index, step], place.chip(source))
        for copy in self.pending:
            copy.wait_send()


FOLD_PIECE = 56 * 1024


class FoldPlanes:
    def __init__(self, arrays, in_place=False):
        self.in_place = in_place
        self.operands = list(arrays)
        self.in_specs = [IN_VMEM] * len(arrays)
        self.outs = [(w.shape, jnp.bfloat16) for w in arrays]
        self.out_specs = [IN_VMEM] * len(arrays)
        self.pieces = []
        for index, w in enumerate(arrays):
            cuts = next(c for c in (1, 2, 3, 4, 6, 8) if w.shape[1] // c * w.shape[2] <= FOLD_PIECE or c == 8)
            if w.shape[0] * w.shape[1] * w.shape[2] <= FOLD_PIECE:
                self.pieces.append((index, slice(None), pl.ds(0, w.shape[1])))
                continue
            rows = w.shape[1] // cuts
            self.pieces += [(index, lead, pl.ds(c * rows, rows)) for lead in range(w.shape[0]) for c in range(cuts)]
        self.inner_done = self.across_done = 0
        self.scratch = [pltpu.VMEM(w.shape, jnp.bfloat16) for _ in range(1 if in_place else 2) for w in arrays] + [DMA((len(self.pieces),))] * 6

    def bind(self, ins, outs, scratch):
        count = len(self.outs)
        self.ins, self.totals = ins, outs
        self.inner = outs
        self.across, scratch = scratch[:count], scratch[count:]
        self.sums, self.sems = (ins, scratch) if self.in_place else (scratch[:count], scratch[count:])

    def copy(self, hop, number, src, dst, to):
        return pltpu.make_async_remote_copy(
            src_ref=src, dst_ref=dst, send_sem=self.sems[2 * hop].at[number], recv_sem=self.sems[2 * hop + 1].at[number],
            device_id=to, device_id_type=pl.DeviceIdType.MESH,
        )

    def hops(self, place, number):
        index, lead, rows = self.pieces[number]
        part = place.part
        inward, across, outward = (place.at_plane(p) for p in (1 + part // 3, 3 - part, 3 * (part - 1)))
        ref, inner, sums, other, total = (
            side[index].at[lead, rows] for side in (self.ins, self.inner, self.sums, self.across, self.totals)
        )
        return (ref, inner, inward), (sums, other, across), (total, total, outward)

    def roles(self, place):
        middle = (place.part == 1) | (place.part == 2)
        return pl.when(middle), pl.when(jnp.logical_not(middle))

    def start(self, place, numbers):
        @self.roles(place)[1]
        def _():
            for number in numbers:
                self.copy(0, number, *self.hops(place, number)[0]).start()

    def add_inner(self, place, number):
        inward, across, _ = self.hops(place, number)
        self.copy(0, number, *inward).wait_recv()
        across[0][...] = low(inward[0][...].astype(jnp.float32) + inward[1][...].astype(jnp.float32))
        self.copy(1, number, *across).start()

    def add_across(self, place, number):
        _, across, outward = self.hops(place, number)
        self.copy(1, number, *across).wait_recv()
        outward[0][...] = low(across[0][...].astype(jnp.float32) + across[1][...].astype(jnp.float32))
        self.copy(2, number, *outward).start()

    def of(self, first, last):
        return [n for n, piece in enumerate(self.pieces) if first <= piece[0] < last]

    def serve(self, place, inner, across):
        inners = list(range(self.inner_done, min(self.inner_done + inner, len(self.pieces))))
        self.inner_done += len(inners)
        others = list(range(self.across_done, min(self.across_done + across, len(self.pieces))))
        self.across_done += len(others)

        @self.roles(place)[0]
        def _():
            for turn in range(max(len(inners), len(others))):
                if turn < len(inners):
                    self.add_inner(place, inners[turn])
                if turn < len(others):
                    self.add_across(place, others[turn])

    def finish(self, place, lag):
        left = len(self.pieces) - self.inner_done
        behind = self.inner_done - self.across_done
        if behind > lag:
            self.serve(place, 0, behind - lag)
        self.serve(place, lag - min(behind, lag), 0)
        self.serve(place, left, left)
        self.serve(place, 0, len(self.pieces))

    def end(self, place):
        in_middle, at_end = self.roles(place)

        @at_end
        def _():
            for number in range(len(self.pieces)):
                inward, _, outward = self.hops(place, number)
                self.copy(0, number, *inward).wait_send()
                self.copy(2, number, *outward).wait_recv()

        @in_middle
        def _():
            for number in range(len(self.pieces)):
                _, across, outward = self.hops(place, number)
                self.copy(1, number, *across).wait_send()
                self.copy(2, number, *outward).wait_send()


def feed_back_part(n, dyb, gu_ref, down_ref):
    hidden = down_ref.shape[0]
    gu = nn(n, gu_ref[...])
    g, u = gu[:, :hidden], gu[:, hidden:]
    act, slope = gelu_and_slope(g)
    dh = nt(dyb, down_ref[...])
    return low(act * u), jnp.concatenate([low(dh * u * slope), low(dh * act)], axis=1)


def row_block(row):
    wide = jnp.broadcast_to(row.astype(jnp.float32), (8, row.shape[1]))
    return low(jnp.where(lax.broadcasted_iota(jnp.int32, wide.shape, 0) == 0, wide, 0.0))


def bucket_onehot(row, width, count, place_of):
    last = row.shape[1] - 1
    padded = jnp.concatenate([row.astype(jnp.float32), jnp.zeros((1, width - last - 1), jnp.float32)], axis=1)
    entry = lax.broadcasted_iota(jnp.int32, (width, width), 0)
    column = lax.broadcasted_iota(jnp.int32, (width, width), 1)
    pick = low(jnp.where(entry == jnp.clip(place_of(column), 0, last), 1.0, 0.0))
    bucket = nn(row_block(padded), pick)[0:1, :].astype(jnp.int32)
    return jnp.where(lax.broadcasted_iota(jnp.int32, (count, width), 0) == bucket, 1.0, 0.0)


def bias_mask(place, block, causal, rel_ref, turn, key_ids, query_ids, out_ref):
    heads, rows_total, lanes = out_ref.shape
    key_len = key_ids.shape[1]
    strip = block + 2 * BLOCK_PAD
    query = lax.broadcasted_iota(jnp.int32, (1, lanes), 1)
    start = ((place.cores * (query // block) + place.core) * place.parts + place.part) * block
    token = lax.broadcasted_iota(jnp.int32, (key_len, lanes), 0)
    of_key = tn(row_block(key_ids[...]), jnp.ones((8, lanes), jnp.bfloat16))
    of_query = nn(row_block(query_ids[...]), low(jnp.where(token == start + query % block, 1.0, 0.0)))[0:1, :]
    allowed = of_key == of_query
    if causal:
        allowed = allowed & (token <= start + query % block)
    inside = pl.ds(BLOCK_PAD, key_len)
    if rel_ref is None:
        out_ref[0, inside, :] = low(jnp.where(allowed, 0.0, NEGATIVE))
        return
    by_head = tn(rel_ref[...], turn)
    width = by_head.shape[1]
    pick_rows = lax.broadcasted_iota(jnp.int32, (8, by_head.shape[0]), 0)
    pick_cols = lax.broadcasted_iota(jnp.int32, (8, by_head.shape[0]), 1)
    picked = nn(low(jnp.where(pick_cols == pick_rows + place.group * heads, 1.0, 0.0)), low(by_head))
    places = lax.broadcasted_iota(jnp.int32, (rows_total, lanes), 0)
    for head in range(heads):
        row = picked[head : head + 1, :]
        left, right = row[:, width - 2 : width - 1], row[:, 0:1]
        out_ref[head] = low(jnp.where(places < start, left, right))
        wide = jnp.broadcast_to(row, (strip, width))
        for number in range(lanes // block):
            at = (number * block) % 128
            turned = pltpu.roll(wide, (width - (strip - 1) + at) % width, 1, stride=1, stride_axis=0)
            rows = pl.ds(place.first_token(number, block), strip)
            out_ref[head, rows, number * block : (number + 1) * block] = low(turned[:, at : at + block])
        out_ref[head, inside, :] = low(jnp.where(allowed, out_ref[head, inside, :].astype(jnp.float32), NEGATIVE))


def chunk_rows(kv_ref):
    return kv_ref.shape[1] * kv_ref.shape[2] * kv_ref.shape[3]


def key_side(kv_ref, chunk):
    return kv_ref[chunk].reshape(chunk_rows(kv_ref), kv_ref.shape[4])[:, : kv_ref.shape[4] // 2]


def value_side(kv_ref, chunk):
    lanes = kv_ref.shape[4]
    return kv_ref[chunk].reshape(chunk_rows(kv_ref), lanes)[:, lanes // 2 // 128 * 128 :]


def bias_rows(bm_ref, head, chunk, rows):
    at = pl.multiple_of(BLOCK_PAD + chunk * rows, 128)
    return bm_ref[head if bm_ref.shape[0] > 1 else 0, pl.ds(at, rows), :].astype(jnp.float32)


def mix_part(q, kv_ref, bm_ref, o_ref, lse_ref, s_ref, ot_ref):
    chunks, rows = kv_ref.shape[0], chunk_rows(kv_ref)
    queries, width = q.shape
    heads = width // HD
    across = [slice(head * queries, (head + 1) * queries) for head in range(heads)]
    masked_q = [only_lanes(q, head * HD, HD) for head in range(heads)]

    def first(chunk, tops):
        keys = key_side(kv_ref, chunk)
        inside = pl.ds(pl.multiple_of(chunk * rows, rows), rows)
        new = []
        for head in range(heads):
            scores = nt(keys, masked_q[head]) + bias_rows(bm_ref, head, chunk, rows)
            s_ref[inside, across[head]] = scores
            new.append(jnp.maximum(tops[head], jnp.max(scores, axis=0, keepdims=True)))
        return tuple(new)

    tops = lax.fori_loop(0, chunks, first, (jnp.full((1, queries), NEGATIVE, jnp.float32),) * heads)

    def second(chunk, carried):
        values = value_side(kv_ref, chunk)
        inside = pl.ds(pl.multiple_of(chunk * rows, rows), rows)
        lead = values.shape[1] - width
        values_t = low(nt(identity(values.shape[1]), values))
        new = []
        for head in range(heads):
            total, mixed = carried[head]
            weights = jnp.exp(s_ref[inside, across[head]] - tops[head])
            mixed = mixed + nn(values_t[lead + head * HD : lead + (head + 1) * HD], low(weights))
            new.append((total + jnp.sum(weights, axis=0, keepdims=True), mixed))
        return tuple(new)

    start = (jnp.zeros((1, queries), jnp.float32), jnp.zeros((HD, queries), jnp.float32))
    done = lax.fori_loop(0, chunks, second, (start,) * heads)
    for head in range(heads):
        total, mixed = done[head]
        lse_ref[:, across[head]] = tops[head] + jnp.log(total)
        ot_ref[head * HD : (head + 1) * HD, :] = low(mixed / total)
    o_ref[...] = low(nt(identity(queries), ot_ref[...]))


def keys_send(place, kv_ref, base, sent, got):
    mine = kv_ref.at[:, place.core, place.part]
    pending = [
        send(mine, mine, sent.at[base, step], got.at[base, step], place.at_plane(place.plane(step)))
        for step in range(1, place.parts)
    ]
    pending.append(send(mine, mine, sent.at[base + 1, 0], got.at[base + 1, 0], place.sibling()))
    return pending


def keys_relay(place, kv_ref, base, sent, got):
    pending = []
    for step in range(1, place.parts):
        source = place.plane_behind(step)
        slot = kv_ref.at[:, place.core, source]
        arrived(slot, sent.at[base, step], got.at[base, step], place.at_plane(source))
        pending.append(send(slot, slot, sent.at[base + 1, step], got.at[base + 1, step], place.sibling()))
    return pending


def keys_wait(place, kv_ref, base, sent, got):
    for step in range(place.parts):
        slot = kv_ref.at[:, 1 - place.core, place.plane_behind(step)]
        arrived(slot, sent.at[base + 1, step], got.at[base + 1, step], place.sibling())


def mix_back_part(place, q, do, o, kv_ref, lse_ref, bm_ref, dkv_ref, ds_ref):
    chunks, cores, parts, block, lanes = kv_ref.shape
    rows = chunk_rows(kv_ref)
    queries, width = q.shape
    heads = width // HD
    strip = block + 2 * BLOCK_PAD
    first_value = width // 128 * 128
    lead = width - first_value
    do_wide = jnp.concatenate([jnp.zeros((queries, lead), do.dtype), do], axis=1) if lead else do
    across = [slice(head * queries, (head + 1) * queries) for head in range(heads)]
    masked_q = [only_lanes(q, head * HD, HD) for head in range(heads)]
    masked_do = [only_lanes(do_wide, lead + head * HD, HD) for head in range(heads)]
    q_wide = masked_q
    if lead:
        none = jnp.zeros((queries, lead), q.dtype)
        q_wide = [jnp.concatenate([one, none], axis=1) for one in masked_q]
    of_head = lax.broadcasted_iota(jnp.int32, (8, width), 1) // HD
    of_row = lax.broadcasted_iota(jnp.int32, (8, width), 0)
    inners = lax.dot_general(
        jnp.where(of_head == of_row, 1.0, 0.0), do.astype(jnp.float32) * o.astype(jnp.float32),
        (((1,), (1,)), ((), ())), precision=HIGHEST, preferred_element_type=jnp.float32,
    )
    nothing = jnp.zeros((1, queries), jnp.float32)
    if ds_ref is not None:
        empty = jnp.zeros((BLOCK_PAD, heads * queries), jnp.bfloat16)
        ds_ref[0:BLOCK_PAD, :] = empty
        ds_ref[BLOCK_PAD + chunks * rows :, :] = empty
        of_lane = lax.broadcasted_iota(jnp.int32, (1, queries), 1) // block
        lane_start = ((cores * of_lane + place.core) * parts + place.part) * block

    def chunk_step(chunk, carried):
        at = pl.multiple_of(chunk * rows, rows)
        keys, values = key_side(kv_ref, chunk), value_side(kv_ref, chunk)
        keys_t = low(nt(identity(width), keys))
        new, dk, dv = [], None, None
        for head in range(heads):
            left, right, back = carried[head]
            scores = nt(keys, masked_q[head]) + bias_rows(bm_ref, head, chunk, rows)
            p = jnp.exp(scores - lse_ref[:, across[head]])
            dp = nt(values, masked_do[head])
            ds = low(p * (dp - inners[head : head + 1, :]))
            if ds_ref is not None:
                ds_ref[pl.ds(pl.multiple_of(BLOCK_PAD + at, 128), rows), across[head]] = ds
                wide = ds.astype(jnp.float32)
                places = lax.broadcasted_iota(jnp.int32, wide.shape, 0) + (at + BLOCK_PAD)
                left = left + jnp.sum(jnp.where(places < lane_start, wide, 0.0), axis=0, keepdims=True)
                right = right + jnp.sum(jnp.where(places >= lane_start + strip, wide, 0.0), axis=0, keepdims=True)
            back = back + nn(keys_t[head * HD : (head + 1) * HD], ds)
            new.append((left, right, back))
            more_k, more_v = nn(ds, q_wide[head]), nn(low(p), masked_do[head])
            dk, dv = (more_k, more_v) if dk is None else (dk + more_k, dv + more_v)
        if lead:
            shared = dk[:, first_value:] + dv[:, : 2 * lead]
            both = jnp.concatenate([dk[:, :first_value], shared, dv[:, 2 * lead :]], axis=1)
        else:
            both = jnp.concatenate([dk, dv], axis=1)
        dkv_ref[chunk] = low(both).reshape(dkv_ref.shape[1:])
        return tuple(new)

    start = (nothing, nothing, jnp.zeros((HD, queries), jnp.float32))
    done = lax.fori_loop(0, chunks, chunk_step, (start,) * heads)
    return [one[2] for one in done], [one[:2] for one in done]


def table_grads(place, block, done, ds_ref, ahead_ref, rel_ref):
    queries = done[0][0].shape[1]
    width = ahead_ref.shape[1]
    strip = block + 2 * BLOCK_PAD
    rows = lax.broadcasted_iota(jnp.int32, (block, block), 0)
    cols = lax.broadcasted_iota(jnp.int32, (block, block), 1)
    backwards = jnp.where(rows + cols == block - 1, 1.0, 0.0)
    at = lax.broadcasted_iota(jnp.int32, (1, width), 1)
    sums = []
    for head, (left, right) in enumerate(done):
        total = jnp.zeros((strip, block), jnp.float32)
        for number in range(queries // block):
            low_at = head * queries + number * block
            near = pl.ds(place.first_token(number, block), strip)
            total = total + ds_ref[near, low_at : low_at + block].astype(jnp.float32)
        turned = lax.dot_general(
            backwards, total, (((1,), (1,)), ((), ())), precision=HIGHEST, preferred_element_type=jnp.float32
        )
        turned = jnp.concatenate([turned, jnp.zeros((block, width - strip), jnp.float32)], axis=1)
        by_distance = jnp.sum(pltpu.roll(turned, 0, 1, stride=1, stride_axis=0), axis=0, keepdims=True)
        left, right = (jnp.sum(side, axis=1, keepdims=True) for side in (left, right))
        sums.append(by_distance + jnp.where(at == 0, left, 0.0) + jnp.where(at == width - 2, right, 0.0))
    sums = jnp.concatenate(sums + [jnp.zeros((8 - len(sums), width), jnp.float32)], axis=0)
    by_bucket = lax.dot_general(
        sums, ahead_ref[...], (((1,), (1,)), ((), ())), precision=HIGHEST, preferred_element_type=jnp.float32
    )
    head_rows = lax.broadcasted_iota(jnp.int32, (8, 128), 0)
    head_lanes = lax.broadcasted_iota(jnp.int32, (8, 128), 1)
    lanes_of = (head_lanes == head_rows + place.group * len(done)) & (head_rows < len(done))
    rel_ref[...] = lax.dot_general(
        by_bucket, jnp.where(lanes_of, 1.0, 0.0), (((0,), (0,)), ((), ())), precision=HIGHEST, preferred_element_type=jnp.float32
    )


class AttendBack:
    OPERANDS = 10

    def __init__(self, place, ins, grads, dkv, scratch, cross, which=None):
        self.place, self.cross = place, cross
        self.x, self.n, self.q, self.kv, self.o, self.lse, self.w, self.wo, self.bm, other = ins
        self.source, self.ahead = (other, None) if cross else (self.n, other.at[which])
        self.dwkv, self.dwq, self.dwo = grads
        self.dkv, self.sib, self.zout, self.zin, self.d_buf, self.pn, self.rn, self.dq = [dkv] + scratch[:7]
        scratch = scratch[7:]
        self.pm, self.rm = (scratch.pop(0), scratch.pop(0)) if cross else (None, None)
        self.ds = None if cross else scratch.pop(0)
        self.sent, self.got = scratch
        self.kv_width = self.kv.shape[4]
        self.pending = []

    def begin(self, dy):
        self.d_buf[self.place.group] = low(dy)
        self.pending += spread_start(self.place, self.d_buf, self.sent.at[0], self.got.at[0])

    def arrive(self):
        spread_wait(self.place, self.d_buf, self.sent.at[0], self.got.at[0])

    def compute(self):
        place, sent, got = self.place, self.sent, self.got
        do = low(nt(all_rows(self.d_buf), self.wo[...]))
        back, self.edges = mix_back_part(
            place, self.q[...], do, self.o[...], self.kv, self.lse, self.bm, self.dkv, self.ds
        )
        self.halves = send(self.dkv.at[:, 1 - place.core], self.sib, sent.at[1, 0], got.at[1, 0], place.sibling())
        self.dq[...] = low(nt(identity(self.q.shape[0]), low(jnp.concatenate(back, axis=0))))
        if self.cross:
            share = nt(self.dq[...], self.w[:, self.kv_width :])
            self.pending += collect_start(place, share, self.pn, self.rn, sent.at[3], got.at[3])

    def exchange(self):
        place, sent, got = self.place, self.sent, self.got
        arrived(self.sib, sent.at[1, 0], got.at[1, 0], place.sibling())
        for step in list(range(1, place.parts)) + [0]:
            to = place.plane(step)
            self.zout[to] = low(self.dkv[:, place.core, to].astype(jnp.float32) + self.sib[:, to].astype(jnp.float32))
            if step:
                self.pending.append(
                    send(self.zout.at[to], self.zin.at[place.part], sent.at[2, step], got.at[2, step], place.at_plane(to))
                )

        self.halves.wait_send()

    def by_rows(self, grad):
        return low(grad).reshape(self.dwq.shape[:3] + grad.shape[1:])

    def query_grads(self, rel):
        self.dwo[...] = low(tn(self.o[...], all_rows(self.d_buf))).reshape(self.dwo.shape)
        self.dwq[...] = self.by_rows(tn(self.n[...], self.dq[...]))
        if not self.cross:
            table_grads(self.place, self.x.shape[0], self.edges, self.ds, self.ahead, rel)

    def keys(self):
        place, sent, got = self.place, self.sent, self.got
        total = self.zout[place.part].astype(jnp.float32)
        for step in range(1, place.parts):
            source = place.plane_behind(step)
            arrived(self.zin.at[source], sent.at[2, step], got.at[2, step], place.at_plane(source))
            total = total + self.zin[source].astype(jnp.float32)
        self.dkv_own = low(total).reshape(self.q.shape[0], self.kv_width)
        share = nt(self.dkv_own, self.w[:, : self.kv_width])
        if self.cross:
            self.pending += collect_start(place, share, self.pm, self.rm, sent.at[4], got.at[4])
        else:
            share = share + nt(self.dq[...], self.w[:, self.kv_width :])
            self.pending += collect_start(place, share, self.pn, self.rn, sent.at[3], got.at[3])

    def key_grads(self):
        self.dwkv[...] = self.by_rows(tn(self.source[...], self.dkv_own))

    def source_grad(self):
        return collect_wait(self.place, self.pm, self.rm, self.sent.at[4], self.got.at[4])

    def normed_grad(self):
        return collect_wait(self.place, self.pn, self.rn, self.sent.at[3], self.got.at[3])

    def wait(self):
        for copy in self.pending:
            copy.wait_send()


def attend_back_scratch(sizes, block, model, width, cross):
    groups, cores, parts = sizes
    tokens = groups * block
    turned, buffer = (parts, groups, block, 2 * width), (groups, block, model)
    shapes = [(groups, parts, block, 2 * width), turned, turned, buffer, buffer, buffer, (tokens, width)]
    if cross:
        shapes += [buffer, buffer]
    else:
        shapes.append((cores * parts * tokens + 2 * BLOCK_PAD, width // HD * tokens))
    return [pltpu.VMEM(shape, jnp.bfloat16) for shape in shapes] + [DMA((5, max(groups, parts)))] * 2


class Taker:
    def __init__(self, refs):
        self.refs = list(refs)

    def __call__(self, count):
        taken, self.refs = self.refs[:count], self.refs[count:]
        return taken


def decoder_back_kernel(sizes, streams, gain_at, plans, *refs):
    give_a, give_b, give_c, fold, cross_scratch, self_scratch = plans
    dec1, dec2, dec3, enc2, final = gain_at
    take = Taker(refs)
    gains, cx, dec_cot, dec_gu, dec_down = take(5)
    cross_ins, self_ins = take(AttendBack.OPERANDS), take(AttendBack.OPERANDS)
    ex, enc_out, enc_cot, en2, gu, down = take(6)
    dec_out, dec_in_grad, grad_ex, dg_d1, dg_d2, dg_d3, dg_e2, dg_ef, rel_d, dw_d, dwo_d = take(11)
    totals, c_outs = take(len(fold.outs)), take(len(give_c.outs))
    dw_c, dwo_c, dgu, ddown, dgu_a, ddown_a, dkv, grad_cx, grad_dx = take(9)
    n_buf, d_buf, py, ry, f_buf, pf, rf, f_sent, f_got = take(9)
    place = Place(*sizes)
    kv_width = cross_ins[3].shape[4]
    cross = AttendBack(place, cross_ins, (dw_c.at[:, :, :, :kv_width], dw_c.at[:, :, :, kv_width:], dwo_c), dkv, take(len(cross_scratch)), True)
    own = AttendBack(place, self_ins, (dw_d.at[:, :, :, :kv_width], dw_d.at[:, :, :, kv_width:], dwo_d), dkv, take(len(self_scratch)), False, 1)
    a_outs, b_outs = take(len(give_a.outs)), take(len(give_b.outs))
    give_a.bind([dgu_a, ddown_a], a_outs, take(len(give_a.scratch)))
    fold.bind(a_outs + b_outs, totals, take(len(fold.scratch)))
    of_a, of_b = fold.of(0, len(a_outs)), fold.of(len(a_outs), len(fold.outs))
    give_b.bind([dw_c, dwo_c], b_outs, take(len(give_b.scratch)))
    give_c.bind([dgu, ddown], c_outs, take(len(give_c.scratch)))
    pn, rn = own.pn, own.rn
    place.greet(planes=True)
    d_buf[place.group] = dec_cot[...]
    pending = spread_start(place, d_buf, f_sent.at[2], f_got.at[2])
    n_buf[place.group] = low(rms_norm(cx[...], gains[dec3]))
    pending += spread_start(place, n_buf, f_sent.at[3], f_got.at[3])
    spread_wait(place, d_buf, f_sent.at[2], f_got.at[2])
    spread_wait(place, n_buf, f_sent.at[3], f_got.at[3])
    n, dyb = all_rows(n_buf), all_rows(d_buf)
    h, dgu_value = feed_back_part(n, dyb, dec_gu, dec_down)
    leaving = collect_start(place, nt(dgu_value, dec_gu[...]), pn, rn, f_sent.at[4], f_got.at[4])
    dgu_a[...] = low(tn(n, dgu_value)).reshape(dgu_a.shape)
    ddown_a[...] = low(tn(h, dyb)).reshape(ddown_a.shape)
    dn = collect_wait(place, pn, rn, f_sent.at[4], f_got.at[4])
    for copy in leaving:
        copy.wait_send()
    back, dg = norm_back(cx[...], gains[dec3], dn)
    dg_d3[...] = dg
    grad_cx[...] = dec_cot[...].astype(jnp.float32) + back
    cross.begin(grad_cx[...])
    pending += collect_start(place, nn(h, dec_down[...]), py, ry, f_sent.at[5], f_got.at[5])
    give_a.begin(place)
    give_a.middle(place)
    streams.need(5, 15)
    cross.arrive()
    cross.compute()
    cross.exchange()
    give_a.end(place)
    fold.start(place, of_a)
    back, dg = norm_back(cross.x[...].astype(jnp.float32), gains[dec2], cross.normed_grad())
    dg_d2[...] = dg
    grad_dx[...] = grad_cx[...] + back
    own.begin(grad_dx[...])
    cross.query_grads(None)
    streams.need(15, 25)
    dec_out[...] = cx[...] + collect_wait(place, py, ry, f_sent.at[5], f_got.at[5])
    own.arrive()
    own.compute()
    cross.keys()
    own.exchange()
    fold.serve(place, 4, 0)
    cross.key_grads()
    give_b.begin(place)
    streams.need(25, 31)
    back, dg = norm_back(enc_out[...], gains[final], cross.source_grad())
    dg_ef[...] = dg
    dy = enc_cot[...].astype(jnp.float32) + back
    f_buf[place.group] = low(dy)
    pending += spread_start(place, f_buf, f_sent.at[0], f_got.at[0])
    give_b.middle(place)
    own.query_grads(rel_d)
    fold.serve(place, 3, 2)
    spread_wait(place, f_buf, f_sent.at[0], f_got.at[0])
    n, dyb = en2[...], all_rows(f_buf)
    h, dgu_value = feed_back_part(n, dyb, gu, down)
    pending += collect_start(place, nt(dgu_value, gu[...]), pf, rf, f_sent.at[1], f_got.at[1])
    dgu[...] = low(tn(n, dgu_value)).reshape(dgu.shape)
    ddown[...] = low(tn(h, dyb)).reshape(ddown.shape)
    give_b.end(place)
    fold.start(place, of_b)
    give_c.begin(place)
    fold.serve(place, 3, 3)
    dn = collect_wait(place, pf, rf, f_sent.at[1], f_got.at[1])
    back, dg = norm_back(ex[...], gains[enc2], dn)
    dg_e2[...] = dg
    grad_ex[...] = dy + back
    give_c.middle(place)
    fold.serve(place, 4, 3)
    own.keys()
    own.key_grads()
    fold.finish(place, 3)
    back, dg = norm_back(own.x[...].astype(jnp.float32), gains[dec1], own.normed_grad())
    dg_d1[...] = dg
    dec_in_grad[...] = grad_dx[...] + back
    give_c.end(place)
    fold.end(place)
    cross.wait()
    own.wait()
    for copy in pending:
        copy.wait_send()


def encoder_back_kernel(sizes, streams, gain_at, plans, *refs):
    give_d, give_q, give_e, fold, before, scratch = plans
    take = Taker(refs)
    gains, grad_ex = take(2)
    ins = take(AttendBack.OPERANDS)
    dg_d1, dg_d2, dg_d3, dg_e2, dg_ef, rel_d = take(6)
    ready, d_ins = take(before), take(give_d.cols + give_d.rows)
    (enc_in_grad,) = take(1)
    totals = take(len(fold.outs))
    dwkv_e, dwq_e, dwo_e, small, dkv, rel_e = take(6)
    place = Place(*sizes)
    own = AttendBack(place, ins, (dwkv_e, dwq_e, dwo_e), dkv, take(len(scratch)), False, 0)
    d_outs, q_outs, e_outs = take(len(give_d.outs)), take(len(give_q.outs)), take(len(give_e.outs))
    give_d.bind(d_ins, d_outs, take(len(give_d.scratch)))
    give_q.bind([dwq_e, dwo_e], q_outs, take(len(give_q.scratch)))
    give_e.bind([dwkv_e, small], e_outs, take(len(give_e.scratch)))
    fold.bind(ready + d_outs + q_outs + e_outs, totals, take(len(fold.scratch)))
    of_c = fold.of(0, before)
    of_d, of_q, of_e = (
        fold.of(first, last) for first, last in ((before, before + 2), (before + 2, before + 4), (before + 4, len(fold.outs)))
    )
    place.greet(planes=True)
    own.begin(grad_ex[...])
    fold.start(place, of_c)
    give_d.begin(place)
    give_d.middle(place)
    streams.need(2, 12)
    own.arrive()
    fold.serve(place, 2, 0)
    own.compute()
    fold.serve(place, 3, 2)
    own.exchange()
    give_d.end(place)
    fold.start(place, of_d)
    fold.serve(place, 2, 2)
    own.query_grads(rel_e)
    give_q.begin(place)
    fold.serve(place, 2, 2)
    own.keys()
    give_q.middle(place)
    fold.serve(place, len(of_c) - 9, 3)
    own.key_grads()
    dn = own.normed_grad()
    give_q.end(place)
    fold.start(place, of_q)
    back, dg_e1 = norm_back(own.x[...].astype(jnp.float32), gains[gain_at], dn)
    enc_in_grad[...] = grad_ex[...] + back
    devices = place.groups * place.cores
    share = dg_e1.shape[1] // devices
    small[...] = jnp.zeros_like(small)
    all_gains = jnp.concatenate([dg_e1, dg_e2[...], dg_ef[...], dg_d1[...], dg_d2[...], dg_d3[...]], axis=0)
    count = all_gains.shape[0]
    each = rel_e.shape[0] // devices
    tables = [rel_e[...].reshape(devices, each, 128), rel_d[...].reshape(devices, each, 128)]
    for device in range(devices):
        piece = jnp.concatenate([all_gains[:, device * share : (device + 1) * share], jnp.zeros((count, 128 - share), jnp.float32)], axis=1)
        rows = jnp.concatenate([piece, tables[0][device], tables[1][device]], axis=0)
        rows = jnp.concatenate([rows, jnp.zeros((16 - rows.shape[0], 128), jnp.float32)], axis=0)
        small[device // place.cores, device % place.cores] = low(rows)
    give_e.begin(place)
    fold.serve(place, 2, len(of_c) - 9)
    give_e.middle(place)
    fold.serve(place, len(of_d) - 2, 2)
    give_e.end(place)
    fold.start(place, of_e)
    fold.finish(place, 3)
    fold.end(place)
    own.wait()


class Streams:
    def __init__(self, fetches, stores):
        self.fetches, self.stores = fetches, stores
        self.stored = []

    def begin(self):
        for copy in self.fetches.values():
            copy.start()

    def need(self, first, last):
        for index in [i for i in self.fetches if first <= i < last]:
            self.fetches.pop(index).wait()

    def store(self, *indices):
        for index in indices:
            if index in self.stores:
                copy = self.stores.pop(index)
                copy.start()
                self.stored.append(copy)

    def end(self):
        self.need(0, 1 << 20)
        self.store(*sorted(self.stores))
        for copy in self.stored:
            copy.wait()


LARGE = 300_000


def size_of(shape, dtype):
    return math.prod(shape) * jnp.dtype(dtype).itemsize


def fused(sizes, collective_id, kernel, operands, outs, scratch, fetched=(0, 0), stored=False, large=LARGE):
    late = [i for i, w in enumerate(operands) if fetched[0] <= i < fetched[1] and size_of(w.shape, w.dtype) > large]
    early = [i for i, (shape, dtype) in enumerate(outs) if stored and size_of(shape, dtype) > large]
    held = [pltpu.VMEM(operands[i].shape, operands[i].dtype) for i in late]
    held += [pltpu.VMEM(*outs[i]) for i in early]
    sems = [DMA((max(1, len(late)),)), DMA((max(1, len(early)),))]

    def body(*refs):
        take = Taker(refs)
        ins, results, own = take(len(operands)), take(len(outs)), take(len(scratch))
        late_refs, early_refs = take(len(late)), take(len(early))
        late_sem, early_sem = take(2)
        fetches, stores = {}, {}
        for number, index in enumerate(late):
            fetches[index] = pltpu.make_async_copy(ins[index], late_refs[number], late_sem.at[number])
            ins[index] = late_refs[number]
        for number, index in enumerate(early):
            stores[index] = pltpu.make_async_copy(early_refs[number], results[index], early_sem.at[number])
            results[index] = early_refs[number]
        streams = Streams(fetches, stores)
        streams.begin()
        kernel(sizes, streams, *ins, *results, *own)
        streams.end()

    return pl.pallas_call(
        body,
        out_shape=tuple(jax.ShapeDtypeStruct(shape, dtype) for shape, dtype in outs),
        in_specs=[ANYWHERE if i in late else IN_VMEM for i in range(len(operands))],
        out_specs=tuple(ANYWHERE if i in early else IN_VMEM for i in range(len(outs))),
        scratch_shapes=list(scratch) + held + sems,
        compiler_params=pltpu.CompilerParams(
            collective_id=collective_id, has_side_effects=collective_id is not None, vmem_limit_bytes=VMEM_BYTES
        ),
        cost_estimate=pl.CostEstimate(flops=20_000_000_000, bytes_accessed=10_000_000, transcendentals=0),
    )(*operands)


def kept_operands(x, kept, w, wo, ahead):
    _, n, q, kv, o, lse, bm, memory = kept
    return [x, n, q, kv, o, lse, w, wo, bm, memory if ahead is None else ahead]


def buffers_of(shapes):
    return [pltpu.VMEM(shape, jnp.bfloat16) for shape in shapes]


def decoder_back(sizes, collective_id, gains, gain_at, last, cross, own, feed):
    groups, cores, parts = sizes
    f32, bf16 = jnp.float32, jnp.bfloat16
    block, model = last[0].shape
    share = model // (groups * cores)
    width = cross[3].shape[0]
    kv = cross[1][3].shape
    hidden = feed[5].shape[0]
    attention = [(groups, cores, share, 3 * width)], [(cores, width // cores, model)]
    feeds = [(groups, cores, share, 2 * hidden)], [(cores, hidden // cores, model)]
    give_a, give_b, give_c = GiveRows(sizes, *feeds), GiveRows(sizes, *attention), GiveRows(sizes, *feeds)
    fold = FoldPlanes([jax.ShapeDtypeStruct(shape, dtype) for shape, dtype in give_a.outs + give_b.outs], True)
    cross_scratch = attend_back_scratch(sizes, block, model, width, True)
    self_scratch = attend_back_scratch(sizes, block, model, width, False)
    plans = (give_a, give_b, give_c, fold, cross_scratch, self_scratch)
    operands = [gains, *last] + kept_operands(*cross) + kept_operands(*own) + list(feed)
    token, gain = ((block, model), f32), ((1, model), f32)
    outs = [token, token, token, gain, gain, gain, gain, gain, ((own[4].shape[1], 128), f32)]
    outs += [(attention[0][0], bf16), (attention[1][0], bf16)] + fold.outs + give_c.outs
    buffer = (groups, block, model)
    scratch = buffers_of(attention[0] + attention[1] + (feeds[0] + feeds[1]) * 2 + [kv]) + [pltpu.VMEM((block, model), f32)] * 2
    scratch += buffers_of([buffer] * 7) + [DMA((6, groups))] * 2 + cross_scratch + self_scratch
    scratch += buffers_of([shape for shape, _ in give_a.outs + give_b.outs])
    scratch += give_a.scratch + fold.scratch + give_b.scratch + give_c.scratch
    got = Taker(fused(sizes, collective_id, lambda s, t, *refs: decoder_back_kernel(s, t, gain_at, plans, *refs), operands, outs, scratch, (5, 31)))
    first = got(9)
    return first, got(2), got(len(give_a.outs)), got(len(give_b.outs)), got(len(give_c.outs))


def encoder_back(sizes, collective_id, gains, gain_at, grad_ex, own, small_grads, ready, grads_d):
    groups, cores, parts = sizes
    f32 = jnp.float32
    block, model = grad_ex.shape
    share = model // (groups * cores)
    width = own[3].shape[0]
    kv = own[1][3].shape
    give_d = GiveRows.__new__(GiveRows)
    give_d = GiveRows(sizes, [grads_d[0].shape], [grads_d[1].shape])
    keys, queries = (groups, cores, share, 2 * width), (groups, cores, share, width)
    table, projection = (groups, cores, 16, 128), (cores, width // cores, model)
    give_q, give_e = GiveRows(sizes, [queries], [projection]), GiveRows(sizes, [keys, table], [])
    all_outs = [jax.ShapeDtypeStruct(shape, dtype) for shape, dtype in give_d.outs + give_q.outs + give_e.outs]
    fold = FoldPlanes(list(ready) + all_outs)
    scratch = attend_back_scratch(sizes, block, model, width, False)
    plans = (give_d, give_q, give_e, fold, len(ready), scratch)
    operands = [gains, grad_ex] + kept_operands(*own) + list(small_grads) + list(ready) + list(grads_d)
    buffers = buffers_of([keys, queries, projection, table, kv]) + [pltpu.VMEM((own[4].shape[1], 128), f32)] + scratch
    buffers += buffers_of([shape for shape, _ in give_d.outs + give_q.outs + give_e.outs])
    buffers += give_d.scratch + give_q.scratch + give_e.scratch + fold.scratch
    outs = [((block, model), f32)] + fold.outs
    got = Taker(fused(sizes, collective_id, lambda s, t, *refs: encoder_back_kernel(s, t, gain_at, plans, *refs), operands, outs, buffers, (2, 12)))
    return got(1)[0], got(len(ready)), got(2), got(4)


def unpack_kernel(sizes, streams, kinds, *refs):
    take = Taker(refs)
    ins, at = take(len(kinds)), 0
    for index, (ref, pieces) in enumerate(zip(ins, kinds)):
        streams.need(index, index + 1)
        results = take(max(1, pieces))
        if pieces < 0:
            results[0][...] = ref[...]
        elif pieces == 0:
            results[0][...] = ref[0].astype(jnp.float32)
        else:
            value = ref[...].astype(jnp.float32)
            each = value.shape[2] // pieces
            for piece, out in enumerate(results):
                out[...] = jnp.concatenate([one[:, piece * each : (piece + 1) * each] for one in value], axis=1)
        streams.store(*range(at, at + len(results)))
        at += len(results)


def unpack(sizes, arrays, kinds):
    outs = []
    for array, pieces in zip(arrays, kinds):
        if pieces < 0:
            outs.append((array.shape, array.dtype))
        elif pieces == 0:
            outs.append((array.shape[1:], jnp.float32))
        for _ in range(pieces):
            outs.append(((array.shape[1], array.shape[0] * array.shape[2] // pieces), jnp.float32))
    return fused(
        sizes, None, lambda s, t, *refs: unpack_kernel(s, t, kinds, *refs), arrays, outs, [], (0, len(arrays)), True, 1
    )


class AttendForward:
    def __init__(self, place, outs, bufs, sems, base):
        self.place, self.base = place, base
        self.x, self.n, self.q, self.kv, self.o, self.lse, self.bm = outs
        self.p_buf, self.r_buf = bufs
        self.sent, self.got = sems

    def keys(self, kv):
        kv_ref = self.kv
        kv_ref[:, self.place.core, self.place.part] = kv.reshape(kv_ref.shape[0], kv_ref.shape[3], kv_ref.shape[4])

    def send(self):
        return keys_send(self.place, self.kv, self.base, self.sent, self.got)

    def gather(self):
        pending = keys_relay(self.place, self.kv, self.base, self.sent, self.got)
        keys_wait(self.place, self.kv, self.base, self.sent, self.got)
        return pending

    def mix(self, wo, s_ref, ot_ref):
        place, base = self.place, self.base
        mix_part(self.q[...], self.kv, self.bm, self.o, self.lse, s_ref, ot_ref)
        share = nn(self.o[...], wo)
        return collect_start(place, share, self.p_buf, self.r_buf, self.sent.at[base + 2], self.got.at[base + 2])

    def add(self, x):
        total = collect_wait(self.place, self.p_buf, self.r_buf, self.sent.at[self.base + 2], self.got.at[self.base + 2])
        self.x[...] = x + total


def pack_columns(pack, refs):
    groups = pack.shape[0]
    for group in range(groups):
        parts = [ref[:, group * (ref.shape[1] // groups) : (group + 1) * (ref.shape[1] // groups)] for ref in refs]
        pack[group] = jnp.concatenate([part.astype(jnp.float32) for part in parts], axis=1).astype(pack.dtype)


def flat(ref):
    rows = math.prod(ref.shape[:-1])
    return ref[...].reshape(rows, ref.shape[-1])


def forward_kernel(sizes, streams, counts, recuts, *refs):
    enc_first, dec_first, later, last = recuts
    gain_count, each = counts
    take = Taker(refs)
    enc_in, dec_in, small, enc_ids, dec_ids, buckets = take(6)
    enc_w, dec_w, cross_w, enc_gate_up, dec_gate_up = take(3), take(3), take(3), take(2), take(2)
    enc_wo_own, dec_wo_own, cross_wo_own, enc_wd_own, dec_wd_own = take(5)
    gains, enc_kvq, dec_kvq, enc_gu, cross_kvq, dec_gu, enc_wo, dec_wo, enc_wd, cross_wo, dec_wd = take(11)
    enc_outs, dec_outs, cross_outs = take(7), take(7), take(7)
    memory_all, enc_out, en2, ahead = take(4)
    small_pack, enc_pack, dec_pack, cross_pack, enc_gu_pack, dec_gu_pack, small_all, rels = take(8)
    s_ref, ot_ref = take(2)
    x_e, x_d, n_buf, d_buf, m_buf, f_p, f_r = take(7)
    bufs = [take(2) for _ in range(3)]
    sent, got = take(2)
    enc_first.bind([small_pack, enc_pack, enc_wo_own], [small_all, enc_kvq, enc_wo], take(len(enc_first.scratch)))
    dec_first.bind([dec_pack, dec_wo_own], [dec_kvq, dec_wo], take(len(dec_first.scratch)))
    later.bind(
        [enc_gu_pack, cross_pack, enc_wd_own, cross_wo_own], [enc_gu, cross_kvq, enc_wd, cross_wo], take(len(later.scratch))
    )
    last.bind([dec_gu_pack, dec_wd_own], [dec_gu, dec_wd], take(len(last.scratch)))
    place = Place(*sizes)
    enc, dec, cross = [
        AttendForward(place, outs, bufs[i], (sent, got), 6 + 3 * i) for i, outs in enumerate((enc_outs, dec_outs, cross_outs))
    ]
    for group in range(place.groups):
        small_pack[group] = small[...]
    pack_columns(enc_pack, enc_w)
    place.greet(planes=True)
    x_e[place.group] = enc_in[...]
    x_d[place.group] = dec_in[...]
    enc_first.begin(place)
    pending = spread_start(place, x_e, sent.at[0], got.at[0])
    pack_columns(dec_pack, dec_w)
    dec_first.begin(place)
    pending += spread_start(place, x_d, sent.at[1], got.at[1])
    pack_columns(enc_gu_pack, enc_gate_up)
    pack_columns(cross_pack, cross_w)
    pack_columns(dec_gu_pack, dec_gate_up)
    enc_first.middle(place)
    enc_first.end(place)

    devices = place.groups * place.cores
    share = enc_in.shape[1] // devices
    rows, model = small.shape[0], enc_in.shape[1]
    lane = lax.broadcasted_iota(jnp.int32, (128, model), 0)
    column = lax.broadcasted_iota(jnp.int32, (128, model), 1)
    bucket = lax.broadcasted_iota(jnp.int32, (devices * each, rows), 0)
    row = lax.broadcasted_iota(jnp.int32, (devices * each, rows), 1)
    every_gain, tables = 0.0, [0.0, 0.0]
    for device in range(devices):
        table = small_all[device // place.cores, device % place.cores]
        to_column = (column == lane + device * share) & (lane < share)
        every_gain = every_gain + nn(table, low(jnp.where(to_column, 1.0, 0.0)))
        for index in range(2):
            from_row = row == bucket - device * each + gain_count + index * each
            from_row = from_row & (bucket // each == device)
            tables[index] = tables[index] + nn(low(jnp.where(from_row, 1.0, 0.0)), table)
    for index in range(gain_count):
        gains[index] = every_gain[index : index + 1, :]
    for index in range(2):
        rels[index] = low(tables[index])

    def project(one, x_buf, gain_at, w, number):
        spread_wait(place, x_buf, sent.at[number], got.at[number])
        kv_width = one.kv.shape[4]
        n = low(rms_norm(all_rows(x_buf).astype(jnp.float32), gains[gain_at]))
        one.n[...] = n
        both = low(nn(n, flat(w)))
        one.keys(both[:, :kv_width])
        one.q[...] = both[:, kv_width:]

    project(enc, x_e, 0, enc_kvq, 0)
    pending += enc.send()
    dec_first.middle(place)
    dec_first.end(place)
    project(dec, x_d, 3, dec_kvq, 1)
    later.begin(place)
    block = enc_in.shape[0]
    reach, width = buckets.shape[1] // 2, ahead.shape[2]
    turns = []
    for index in range(2):
        row, count = buckets[index : index + 1, :], ahead.shape[1]
        ahead[index] = bucket_onehot(row, width, count, lambda column: column - (block - 1))
        turns.append(low(bucket_onehot(row, width, count, lambda column: 2 * reach + block - 1 - column)))
    bias_mask(place, block, False, rels.at[0], turns[0], enc_ids, enc_ids, enc.bm)
    streams.store(1, 2, 12, 19, 17)
    bias_mask(place, block, True, rels.at[1], turns[1], dec_ids, dec_ids, dec.bm)
    streams.store(24)
    pending += enc.gather()
    pending += dec.send()
    pending += enc.mix(flat(enc_wo), s_ref, ot_ref)
    streams.store(14)
    bias_mask(place, block, False, None, None, enc_ids, dec_ids, cross.bm)
    streams.store(31)
    enc.add(enc_in[...].astype(jnp.float32))
    ex = enc.x[...]
    n_buf[place.group] = low(rms_norm(ex, gains[1]))
    pending += spread_start(place, n_buf, sent.at[2], got.at[2])
    later.middle(place)
    later.end(place)
    streams.store(3, 4, 8)
    spread_wait(place, n_buf, sent.at[2], got.at[2])
    en2[...] = all_rows(n_buf)
    w_down = flat(enc_wd)
    hidden = w_down.shape[0]
    gu = nn(en2[...], flat(enc_gu))
    h = low(gelu_and_slope(gu[:, :hidden])[0] * gu[:, hidden:])
    pending += collect_start(place, nn(h, w_down), f_p, f_r, sent.at[5], got.at[5])
    enc_out[...] = ex + collect_wait(place, f_p, f_r, sent.at[5], got.at[5])
    m_buf[place.group] = low(rms_norm(enc_out[...], gains[2]))
    pending += spread_start(place, m_buf, sent.at[4], got.at[4])
    kv_width = cross.kv.shape[4]
    model = enc_in.shape[1]
    spread_wait(place, m_buf, sent.at[4], got.at[4])
    memory_all[...] = all_rows(m_buf)
    cross.keys(low(nn(memory_all[...], cross_kvq[:, :, :, :kv_width].reshape(model, kv_width))))
    pending += cross.send()
    pending += dec.gather()
    pending += dec.mix(flat(dec_wo), s_ref, ot_ref)
    streams.store(21)
    dec.add(dec_in[...].astype(jnp.float32))
    d_buf[place.group] = low(rms_norm(dec.x[...], gains[4]))
    pending += spread_start(place, d_buf, sent.at[3], got.at[3])
    last.begin(place)
    spread_wait(place, d_buf, sent.at[3], got.at[3])
    cross.n[...] = all_rows(d_buf)
    cross.q[...] = low(nn(cross.n[...], cross_kvq[:, :, :, kv_width:].reshape(model, kv_width // 2)))
    pending += cross.gather()
    pending += cross.mix(flat(cross_wo), s_ref, ot_ref)
    streams.store(28, 26, 32, 34)
    last.middle(place)
    cross.add(dec.x[...])
    last.end(place)
    for copy in pending:
        copy.wait_send()


def forward(sizes, collective_id, enc_in, dec_in, small, counts, ids, buckets, weights):
    groups, cores, parts = sizes
    f32, bf16 = jnp.float32, jnp.bfloat16
    block, model = enc_in.shape
    attention, feeds, rows = weights[:3], weights[3:5], weights[5]
    share = attention[0][0].shape[0]
    width = rows[0].shape[0] * cores
    tokens = groups * block
    keys = cores * parts * tokens
    heads = width // HD
    kvq, gu = (groups, share, 3 * width), (groups, share, 2 * feeds[0][0].shape[1] // groups)
    wo, wd = rows[0].shape, rows[3].shape
    small_shape = (groups,) + small.shape
    recuts = (
        Recut(sizes, [small_shape, kvq], [wo]), Recut(sizes, [kvq], [wo]), Recut(sizes, [gu, kvq], [wd, wo]), Recut(sizes, [gu], [wd])
    )

    def both(shape):
        return ((groups, cores) + shape[1:], bf16)

    def pair(shape):
        return ((cores,) + shape, bf16)

    token = ((block, model), f32)
    outs = [((counts[0], 1, model), f32), both(kvq), both(kvq), both(gu), both(kvq), both(gu)]
    outs += [pair(wo), pair(wo), pair(wd), pair(wo), pair(wd)]
    for number in range(3):
        outs += [
            token, ((tokens, model), bf16), ((tokens, width), bf16), ((groups, cores, parts, block, 2 * width), bf16),
            ((tokens, width), bf16), ((1, heads * tokens), f32),
            ((1 if number == 2 else heads, keys + 2 * BLOCK_PAD, tokens), bf16),
        ]
    bucket_count = groups * cores * counts[1]
    outs += [((tokens, model), bf16), token, ((tokens, model), bf16), ((2, bucket_count, buckets.shape[1] - 1 + 2 * block), f32)]
    buffer = (groups, block, model)
    scratch = buffers_of([small_shape, kvq, kvq, kvq, gu, gu, both(small_shape)[0], (2, bucket_count, 128)])
    scratch += [pltpu.VMEM((keys, heads * tokens), f32)] + buffers_of([(width, tokens)] + [buffer] * 13)
    scratch += [DMA((15, max(groups, parts)))] * 2 + [s for one in recuts for s in one.scratch]
    operands = [enc_in, dec_in, small, *ids, buckets] + [w for each in attention for w in each]
    operands += [w for each in feeds for w in each] + list(rows)
    got = Taker(
        fused(sizes, collective_id, lambda s, t, *refs: forward_kernel(s, t, counts, recuts, *refs), operands, outs, scratch, stored=True)
    )
    gains = got(1)[0]
    flat_weights = [w.reshape(-1, w.shape[-1]) for w in got(10)]
    enc_kept, dec_kept, cross_kept = got(7), got(7), got(7)
    memory_all, enc_out, en2, ahead = got(4)
    return gains, flat_weights, (*enc_kept, None), (*dec_kept, None), (*cross_kept, memory_all), enc_out, en2, ahead


def fast_device(
    enc_in, dec_in, enc_cot, dec_cot, enc_segments, dec_segments, buckets,
    enc_norm1, enc_query, enc_key, enc_value, enc_proj, enc_rel, enc_norm2, enc_gate, enc_up, enc_down, enc_final,
    dec_norm1, dec_query, dec_key, dec_value, dec_proj, dec_rel, dec_norm2, cross_query, cross_key, cross_value, cross_proj,
    dec_norm3, dec_gate, dec_up, dec_down,
):
    groups, cores, parts = sizes = lax.axis_size(HG), lax.axis_size(CORE), lax.axis_size(SP)
    block, model = enc_in.shape
    devices = groups * cores
    share = model // devices
    bf16, f32 = jnp.bfloat16, jnp.float32

    rel_len = enc_rel.shape[0]
    all_gains = jnp.stack([enc_norm1, enc_norm2, enc_final, dec_norm1, dec_norm2, dec_norm3])
    all_rels = jnp.concatenate([enc_rel, dec_rel]).reshape(-1, HEADS)
    small = jnp.concatenate([jnp.pad(w, ((0, 0), (0, 128 - w.shape[1]))) for w in (all_gains, all_rels)])
    each = all_rels.shape[0] // 2
    small = jnp.pad(small, ((0, 16 - small.shape[0]), (0, 0)))

    gains, weights, enc_kept, dec_kept, cross_kept, enc_out, en2, ahead = forward(
        sizes, 1, enc_in, dec_in, small, (6, each), (enc_segments[None, :], dec_segments[None, :]), buckets,
        (
            (enc_key, enc_value, enc_query), (dec_key, dec_value, dec_query), (cross_key, cross_value, cross_query),
            (enc_gate, enc_up), (dec_gate, dec_up), (enc_proj, dec_proj, cross_proj, enc_down, dec_down),
        ),
    )
    enc_kvq, dec_kvq, enc_gu, cross_kvq, dec_gu, enc_wo, dec_wo, enc_wd, cross_wo, dec_wd = weights
    ex, dx, cx = enc_kept[0], dec_kept[0], cross_kept[0]

    (dec_out, dec_in_grad, grad_ex, dg_d1, dg_d2, dg_d3, dg_e2, dg_ef, rel_d), grads_d, sum_a, sum_b, rows_c = decoder_back(
        sizes, 2, gains, (3, 4, 5, 1, 2), (cx, dec_cot, dec_gu, dec_wd),
        (dx, cross_kept, cross_kvq, cross_wo, None), (dec_in, dec_kept, dec_kvq, dec_wo, ahead),
        (ex, enc_out, enc_cot, en2, enc_gu, enc_wd),
    )
    enc_in_grad, sum_c, sum_d, sum_e = encoder_back(
        sizes, 3, gains, 0, grad_ex, (enc_in, enc_kept, enc_kvq, enc_wo, ahead),
        (dg_d1, dg_d2, dg_d3, dg_e2, dg_ef, rel_d), rows_c, grads_d,
    )

    dgu_rows, d_wd = sum_a
    cross_rows, c_wo = sum_b
    egu_rows, e_wd = sum_c
    dkvq_rows, d_wo = sum_d
    eq_rows, e_wo, ekv_rows, small_rows = sum_e
    (
        enc_out, dec_out, enc_in_grad, dec_in_grad, e_wk, e_wv, e_wq, e_wg, e_wu, d_wk, d_wv, d_wq, c_wk, c_wv, c_wq, d_wg, d_wu, d_wd, c_wo, e_wd, d_wo, e_wo
    ) = unpack(
        sizes,
        [enc_out, dec_out, enc_in_grad, dec_in_grad, ekv_rows, eq_rows, egu_rows, dkvq_rows, cross_rows, dgu_rows, d_wd, c_wo, e_wd, d_wo, e_wo],
        (-1, -1, -1, -1, 2, 1, 2, 3, 3, 2, 0, 0, 0, 0, 0),
    )
    own = jnp.sum(small_rows.astype(f32), axis=0)
    s = [own[i, :share] for i in range(6)]
    e_rel, d_rel = [own[6 + i * each : 6 + (i + 1) * each, :HEADS].reshape(rel_len) for i in range(2)]
    return (
        enc_out, dec_out, enc_in_grad, dec_in_grad,
        s[0], e_wq, e_wk, e_wv, e_wo, e_rel, s[1], e_wg, e_wu, e_wd, s[2],
        s[3], d_wq, d_wk, d_wv, d_wo, d_rel, s[4], c_wq, c_wk, c_wv, c_wo, s[5], d_wg, d_wu, d_wd,
    )


def general_plan(mesh):
    placed = (
        P(("ctx", "sp"), None),
        P(("ctx", "sp"), None),
        P(("ctx", "sp"), None),
        P(("ctx", "sp"), None),
        P(),
        P(),
        P(),
        P("ctx"),
        P("ctx", None),
        P("ctx", None),
        P("ctx", None),
        P("ctx", None),
        P("ctx"),
        P("ctx"),
        P("ctx", None),
        P("ctx", None),
        P("ctx", None),
        P("ctx"),
        P("ctx"),
        P("ctx", None),
        P("ctx", None),
        P("ctx", None),
        P("ctx", None),
        P("ctx"),
        P("ctx"),
        P("ctx", None),
        P("ctx", None),
        P("ctx", None),
        P("ctx", None),
        P("ctx"),
        P("ctx", None),
        P("ctx", None),
        P("ctx", None),
    )
    return jax.shard_map(
        per_device,
        mesh=mesh,
        in_specs=placed,
        out_specs=(
            P(("ctx", "sp"), None),
            P(("ctx", "sp"), None),
            P(("ctx", "sp"), None),
            P(("ctx", "sp"), None),
            P("ctx"),
            P("ctx", None),
            P("ctx", None),
            P("ctx", None),
            P("ctx", None),
            P("ctx"),
            P("ctx"),
            P("ctx", None),
            P("ctx", None),
            P("ctx", None),
            P("ctx"),
            P("ctx"),
            P("ctx", None),
            P("ctx", None),
            P("ctx", None),
            P("ctx", None),
            P("ctx"),
            P("ctx"),
            P("ctx", None),
            P("ctx", None),
            P("ctx", None),
            P("ctx", None),
            P("ctx"),
            P("ctx", None),
            P("ctx", None),
            P("ctx", None),
        ),
        check_vma=False,
    )


def split_plan(mesh, groups):
    cut = Mesh(np.asarray(mesh.devices).reshape(groups, 2, mesh.shape["sp"]), (HG, CORE, SP))
    tokens, rows, gain, same = P((HG, CORE, SP), None), P((HG, CORE), None), P((HG, CORE)), P()
    attention = (gain, rows, rows, rows, rows, gain)
    feed = (gain, rows, rows, rows)
    weights = attention + feed + (gain,) + attention + (gain, rows, rows, rows, rows) + feed
    return jax.shard_map(
        fast_device,
        mesh=cut,
        in_specs=(tokens,) * 4 + (same,) * 3 + weights,
        out_specs=(tokens,) * 4 + weights,
        check_vma=False,
    )


def solution(mesh):
    groups, odd = divmod(mesh.shape["ctx"], 2)
    if odd or HEADS % groups or mesh.shape["sp"] != 4:
        return general_plan(mesh)
    return split_plan(mesh, groups)
```

```python
import functools
import math

import jax
import jax.numpy as jnp
import numpy as np
from jax import lax
from jax.experimental import pallas as pl
from jax.experimental.pallas import tpu as pltpu
from jax.sharding import Mesh
from jax.sharding import PartitionSpec as P

HEADS = 12
HD = 64


EPSILON = 1e-06
NEGATIVE = -1e30
HIGHEST = lax.Precision.HIGHEST


def rms_norm(values, norm_gain):
    return (
        values * lax.rsqrt(jnp.mean(values * values, axis=-1, keepdims=True) + EPSILON) * norm_gain
    )


def norm_pullback(values, norm_gain, grad_normed):
    _, pullback = jax.vjp(rms_norm, values, norm_gain)
    return pullback(grad_normed)


def gated(gate_val, up_val):
    return jax.nn.gelu(gate_val, approximate=True) * up_val


def project(left, right):
    return jnp.dot(left, right, preferred_element_type=jnp.float32)


def weight_grad(left, right):
    return jnp.einsum("td,te->de", left, right, preferred_element_type=jnp.float32)


def input_grad(grad_out, weight):
    return jnp.einsum("te,de->td", grad_out, weight, preferred_element_type=jnp.float32)


def head_table(relative, table_row, heads_here):
    bucket_count = relative.shape[0] // HEADS
    onehot = (table_row[:, None] == jnp.arange(bucket_count, dtype=jnp.int32)[None, :]).astype(
        jnp.float32
    )
    bias_grid = relative.astype(jnp.float32).reshape(bucket_count, HEADS)
    full_table = jnp.dot(onehot, bias_grid, precision=HIGHEST).T
    first_head = lax.axis_index("sp") * heads_here
    return (lax.dynamic_slice_in_dim(full_table, first_head, heads_here, 0), onehot)


def table_grad(grad_table, onehot, heads_here):
    full_grad = jnp.zeros((HEADS, onehot.shape[0]), jnp.float32)
    full_grad = lax.dynamic_update_slice_in_dim(
        full_grad, grad_table, lax.axis_index("sp") * heads_here, 0
    )
    return jnp.dot(onehot.T, full_grad.T, precision=HIGHEST).reshape(-1)


def bias_block(head_bias, pad_len, offset_q, rows, offset_k, cols):
    head_count, table_len = head_bias.shape
    reach_len = (table_len - 1) // 2
    left_edge = jnp.broadcast_to(head_bias[:, :1], (head_count, pad_len))
    right_edge = jnp.broadcast_to(head_bias[:, -1:], (head_count, pad_len))
    padded = jnp.concatenate([left_edge, head_bias, right_edge], axis=1)
    band_width = rows + cols - 1
    start = offset_k - offset_q - (rows - 1) + reach_len + pad_len
    band = lax.dynamic_slice_in_dim(padded, start, band_width, 1)
    tiled = jnp.broadcast_to(band[:, None, :], (head_count, rows, band_width)).reshape(
        head_count, rows * band_width
    )
    skewed = tiled[:, rows - 1 : rows - 1 + rows * (band_width - 1)].reshape(
        head_count, rows, band_width - 1
    )
    return skewed[:, :, :cols]


def make_frame(query_local, query_ids, key_ids, head_bias, causal):
    local_len = query_local.shape[0]
    heads_here = query_local.shape[1] // HD
    offset_q = lax.axis_index("ctx") * local_len
    ids_q = lax.dynamic_slice_in_dim(query_ids, offset_q, local_len, 0)
    row_ids = offset_q + jnp.arange(local_len, dtype=jnp.int32)
    query_heads = query_local.reshape(local_len, heads_here, HD)
    pad_len = query_ids.shape[0] + key_ids.shape[0]

    def bias_of(entries, offset_k, length):
        return bias_block(entries, pad_len, offset_q, local_len, offset_k, length)

    def scores_of(key_block, offset_k):
        length = key_block.shape[0]
        key_heads = key_block.reshape(length, heads_here, HD)
        raw_scores = jnp.einsum(
            "qhd,khd->hqk", query_heads, key_heads, preferred_element_type=jnp.float32
        )
        col_ids = offset_k + jnp.arange(length, dtype=jnp.int32)
        ids_k = lax.dynamic_slice_in_dim(key_ids, offset_k, length, 0)
        allowed = ids_q[:, None] == ids_k[None, :]
        if causal:
            allowed = allowed & (col_ids[None, :] <= row_ids[:, None])
        if head_bias is not None:
            raw_scores = raw_scores + bias_of(head_bias, offset_k, length)
        return (raw_scores, allowed)

    def touches(offset_k, length):
        first_id = lax.dynamic_slice_in_dim(key_ids, offset_k, 1, 0)[0]
        last_id = lax.dynamic_slice_in_dim(key_ids, offset_k + length - 1, 1, 0)[0]
        touched = (ids_q[0] <= last_id) & (first_id <= ids_q[-1])
        if causal:
            touched = touched & (offset_k <= offset_q + local_len - 1)
        return touched

    return (query_heads, scores_of, touches, bias_of)


def sweep(keys_gathered, local_len, step_fn, carry_state):
    key_all, value_all = keys_gathered
    block_len = local_len * math.gcd(4, lax.axis_size("ctx"))

    def sweep_loop_body(number, running):
        offset_k = number * block_len
        key_block = lax.dynamic_slice_in_dim(key_all, offset_k, block_len, 0)
        value_block = lax.dynamic_slice_in_dim(value_all, offset_k, block_len, 0)
        return step_fn(running, key_block, value_block, offset_k)

    return lax.fori_loop(0, key_all.shape[0] // block_len, sweep_loop_body, carry_state)


def whole_keys(key_local, value_local):
    return (
        lax.all_gather(key_local, "ctx", axis=0, tiled=True),
        lax.all_gather(value_local, "ctx", axis=0, tiled=True),
    )


def attention_forward(query_proj, key_proj, value_proj, query_ids, key_ids, head_bias, causal):
    query_local, key_local, value_local = (
        lax.all_to_all(query_proj, "sp", split_axis=1, concat_axis=0, tiled=True),
        lax.all_to_all(key_proj, "sp", split_axis=1, concat_axis=0, tiled=True),
        lax.all_to_all(value_proj, "sp", split_axis=1, concat_axis=0, tiled=True),
    )
    local_len = query_local.shape[0]
    heads_here = query_local.shape[1] // HD
    query_heads, scores_of, touches, _ = make_frame(
        query_local, query_ids, key_ids, head_bias, causal
    )
    key_block = lax.all_gather(key_local, "ctx", axis=0, tiled=True)
    value_block = lax.all_gather(value_local, "ctx", axis=0, tiled=True)
    offset_k = jnp.int32(0)
    length = key_block.shape[0]
    row_top = jnp.full((heads_here, local_len), NEGATIVE, jnp.float32)
    weighted = jnp.zeros((local_len, heads_here, HD), jnp.float32)
    raw_scores, allowed = scores_of(key_block, offset_k)
    masked = jnp.where(allowed[None], raw_scores, NEGATIVE)
    new_top = jnp.maximum(row_top, jnp.max(masked, axis=-1))
    weights = jnp.where(allowed[None], jnp.exp(masked - new_top[..., None]), 0.0)
    rescale = jnp.exp(row_top - new_top)
    value_heads = value_block.reshape(length, heads_here, HD)
    increment = jnp.einsum(
        "hqk,khd->qhd",
        weights.astype(jnp.bfloat16),
        value_heads,
        preferred_element_type=jnp.float32,
    )
    row_top, row_total, weighted = (
        new_top,
        jnp.sum(weights, axis=-1),
        weighted * rescale.T[:, :, None] + increment,
    )
    mixed_heads = weighted / row_total.T[:, :, None]
    log_total = row_top + jnp.log(row_total)
    mixed_low = mixed_heads.reshape(local_len, heads_here * HD).astype(jnp.bfloat16)
    mixed_tokens = lax.all_to_all(mixed_low, "sp", split_axis=0, concat_axis=1, tiled=True)
    retained = (
        query_local,
        key_local,
        value_local,
        mixed_heads,
        log_total,
        None,
        query_ids,
        key_ids,
        head_bias,
        causal,
    )
    return (mixed_tokens, retained)


def attention_backward(grad_mixed, retained):
    (
        query_local,
        key_local,
        value_local,
        mixed_heads,
        log_total,
        gathered,
        query_ids,
        key_ids,
        head_bias,
        causal,
    ) = retained
    grad_local = lax.all_to_all(grad_mixed, "sp", split_axis=1, concat_axis=0, tiled=True)
    local_len = query_local.shape[0]
    heads_here = query_local.shape[1] // HD
    width = heads_here * HD
    query_heads, scores_of, touches, bias_of = make_frame(
        query_local, query_ids, key_ids, head_bias, causal
    )
    grad_heads = grad_local.reshape(local_len, heads_here, HD)
    row_inner = jnp.einsum("qhd,qhd->hq", grad_heads.astype(jnp.float32), mixed_heads)
    gathered = whole_keys(key_local, value_local)
    table_zero = jnp.zeros(head_bias.shape if head_bias is not None else (1,), jnp.float32)

    def gradients_of(key_block, value_block, offset_k):
        length = key_block.shape[0]
        raw_scores, allowed = scores_of(key_block, offset_k)
        probabilities = jnp.where(allowed[None], jnp.exp(raw_scores - log_total[..., None]), 0.0)
        value_heads = value_block.reshape(length, heads_here, HD)
        grad_probs = jnp.einsum(
            "qhd,khd->hqk", grad_heads, value_heads, preferred_element_type=jnp.float32
        )
        grad_scores = (probabilities * (grad_probs - row_inner[..., None])).astype(jnp.bfloat16)
        return (probabilities, grad_scores)

    def table_part(grad_scores, offset_k, length):
        if head_bias is None:
            return table_zero
        _, pullback = jax.vjp(lambda entries: bias_of(entries, offset_k, length), head_bias)
        return pullback(grad_scores.astype(jnp.float32))[0]

    def key_terms_of(probabilities, grad_scores, length):
        grad_key = jnp.einsum(
            "hqk,qhd->khd", grad_scores, query_heads, preferred_element_type=jnp.float32
        )
        grad_value = jnp.einsum(
            "hqk,qhd->khd",
            probabilities.astype(jnp.bfloat16),
            grad_heads,
            preferred_element_type=jnp.float32,
        )
        return jnp.concatenate(
            [grad_key.reshape(length, width), grad_value.reshape(length, width)], axis=1
        )

    def query_part(grad_scores, key_block):
        length = key_block.shape[0]
        key_heads = key_block.reshape(length, heads_here, HD)
        return jnp.einsum(
            "hqk,khd->qhd", grad_scores, key_heads, preferred_element_type=jnp.float32
        )

    def query_step(running, key_block, value_block, offset_k):
        length = key_block.shape[0]
        grad_query, grad_table = running
        probabilities, grad_scores = gradients_of(key_block, value_block, offset_k)
        return (
            grad_query + query_part(grad_scores, key_block),
            grad_table + table_part(grad_scores, offset_k, length),
        )

    query_zero = jnp.zeros((local_len, heads_here, HD), jnp.float32)
    block_len = local_len * math.gcd(4, lax.axis_size("ctx"))
    grad_query, grad_table = sweep(gathered, local_len, query_step, (query_zero, table_zero))
    key_all, value_all = gathered
    step_len = math.gcd(lax.axis_size("ctx") * local_len, block_len)

    def term_loop_body(number, rows_acc):
        offset_b = number * step_len
        key_block = lax.dynamic_slice_in_dim(key_all, offset_b, step_len, 0)
        value_block = lax.dynamic_slice_in_dim(value_all, offset_b, step_len, 0)
        probabilities, grad_scores = gradients_of(key_block, value_block, offset_b)
        return lax.dynamic_update_slice_in_dim(
            rows_acc, key_terms_of(probabilities, grad_scores, step_len), number * step_len, 0
        )

    own_rows = lax.psum_scatter(
        lax.fori_loop(
            0,
            lax.axis_size("ctx") * local_len // step_len,
            term_loop_body,
            jnp.zeros((lax.axis_size("ctx") * local_len, 2 * width), jnp.float32),
        ),
        "ctx",
        scatter_dimension=0,
        tiled=True,
    )
    grad_q_low = grad_query.reshape(local_len, width).astype(jnp.bfloat16)
    grad_k_low = own_rows[:, :width].astype(jnp.bfloat16)
    grad_v_low = own_rows[:, width:].astype(jnp.bfloat16)
    grad_q_tok, grad_k_tok, grad_v_tok = (
        lax.all_to_all(grad_q_low, "sp", split_axis=0, concat_axis=1, tiled=True),
        lax.all_to_all(grad_k_low, "sp", split_axis=0, concat_axis=1, tiled=True),
        lax.all_to_all(grad_v_low, "sp", split_axis=0, concat_axis=1, tiled=True),
    )
    return (grad_q_tok, grad_k_tok, grad_v_tok, grad_table)


def attention_layer(
    residual,
    source,
    norm_gain,
    w_query,
    w_key,
    w_value,
    w_proj,
    query_ids,
    key_ids,
    head_bias,
    causal,
):
    normed = rms_norm(residual, norm_gain).astype(jnp.bfloat16)
    kv_input = normed if source is None else source
    query_proj = project(normed, w_query).astype(jnp.bfloat16)
    key_proj = project(kv_input, w_key).astype(jnp.bfloat16)
    value_proj = project(kv_input, w_value).astype(jnp.bfloat16)
    mixed_tokens, retained = attention_forward(
        query_proj, key_proj, value_proj, query_ids, key_ids, head_bias, causal
    )
    result = residual + project(mixed_tokens, w_proj)
    return (result, (residual, normed, kv_input, mixed_tokens, retained))


def attention_layer_back(grad_out, saved, norm_gain, w_query, w_key, w_value, w_proj, is_cross):
    residual, normed, kv_input, mixed_tokens, retained = saved
    grad_low = grad_out.astype(jnp.bfloat16)
    grad_proj = weight_grad(mixed_tokens, grad_low)
    grad_mixed = input_grad(grad_low, w_proj).astype(jnp.bfloat16)
    grad_q_tok, grad_k_tok, grad_v_tok, grad_table = attention_backward(grad_mixed, retained)
    grad_wq = weight_grad(normed, grad_q_tok)
    grad_wk = weight_grad(kv_input, grad_k_tok)
    grad_wv = weight_grad(kv_input, grad_v_tok)
    grad_source = input_grad(grad_k_tok, w_key) + input_grad(grad_v_tok, w_value)
    grad_normed = input_grad(grad_q_tok, w_query)
    if not is_cross:
        grad_normed = grad_normed + grad_source
        grad_source = None
    grad_resid, grad_gain = norm_pullback(residual, norm_gain, grad_normed)
    return (
        grad_out + grad_resid,
        grad_source,
        (grad_gain, grad_wq, grad_wk, grad_wv, grad_proj, grad_table),
    )


def feed_layer(residual, norm_gain, w_gate, w_up, w_down):
    normed = rms_norm(residual, norm_gain).astype(jnp.bfloat16)
    gate_val = project(normed, w_gate)
    up_val = project(normed, w_up)
    hidden = gated(gate_val, up_val).astype(jnp.bfloat16)
    return (residual + project(hidden, w_down), (residual, normed, gate_val, up_val, hidden))


def feed_layer_back(grad_out, saved, norm_gain, w_gate, w_up, w_down):
    residual, normed, gate_val, up_val, hidden = saved
    grad_low = grad_out.astype(jnp.bfloat16)
    grad_down = weight_grad(hidden, grad_low)
    grad_hidden = input_grad(grad_low, w_down)
    _, pullback = jax.vjp(gated, gate_val, up_val)
    grad_gate, grad_up = pullback(grad_hidden)
    grad_gate = grad_gate.astype(jnp.bfloat16)
    grad_up = grad_up.astype(jnp.bfloat16)
    grad_wg = weight_grad(normed, grad_gate)
    grad_wu = weight_grad(normed, grad_up)
    grad_normed = input_grad(grad_gate, w_gate) + input_grad(grad_up, w_up)
    grad_resid, grad_gain = norm_pullback(residual, norm_gain, grad_normed)
    return (grad_out + grad_resid, (grad_gain, grad_wg, grad_wu, grad_down))


def per_device(
    enc_in,
    dec_in,
    enc_cot,
    dec_cot,
    enc_segments,
    dec_segments,
    buckets,
    enc_norm1,
    enc_query,
    enc_key,
    enc_value,
    enc_proj,
    enc_rel,
    enc_norm2,
    enc_gate,
    enc_up,
    enc_down,
    enc_final,
    dec_norm1,
    dec_query,
    dec_key,
    dec_value,
    dec_proj,
    dec_rel,
    dec_norm2,
    cross_query,
    cross_key,
    cross_value,
    cross_proj,
    dec_norm3,
    dec_gate,
    dec_up,
    dec_down,
):
    (
        enc_norm1,
        enc_query,
        enc_key,
        enc_value,
        enc_proj,
        enc_rel,
        enc_norm2,
        enc_gate,
        enc_up,
        enc_down,
        enc_final,
        dec_norm1,
        dec_query,
        dec_key,
        dec_value,
        dec_proj,
        dec_rel,
        dec_norm2,
        cross_query,
        cross_key,
        cross_value,
        cross_proj,
        dec_norm3,
        dec_gate,
        dec_up,
        dec_down,
    ) = (
        lax.all_gather(enc_norm1, "ctx", axis=0, tiled=True),
        lax.all_gather(enc_query, "ctx", axis=0, tiled=True),
        lax.all_gather(enc_key, "ctx", axis=0, tiled=True),
        lax.all_gather(enc_value, "ctx", axis=0, tiled=True),
        lax.all_gather(enc_proj, "ctx", axis=0, tiled=True),
        lax.all_gather(enc_rel, "ctx", axis=0, tiled=True),
        lax.all_gather(enc_norm2, "ctx", axis=0, tiled=True),
        lax.all_gather(enc_gate, "ctx", axis=0, tiled=True),
        lax.all_gather(enc_up, "ctx", axis=0, tiled=True),
        lax.all_gather(enc_down, "ctx", axis=0, tiled=True),
        lax.all_gather(enc_final, "ctx", axis=0, tiled=True),
        lax.all_gather(dec_norm1, "ctx", axis=0, tiled=True),
        lax.all_gather(dec_query, "ctx", axis=0, tiled=True),
        lax.all_gather(dec_key, "ctx", axis=0, tiled=True),
        lax.all_gather(dec_value, "ctx", axis=0, tiled=True),
        lax.all_gather(dec_proj, "ctx", axis=0, tiled=True),
        lax.all_gather(dec_rel, "ctx", axis=0, tiled=True),
        lax.all_gather(dec_norm2, "ctx", axis=0, tiled=True),
        lax.all_gather(cross_query, "ctx", axis=0, tiled=True),
        lax.all_gather(cross_key, "ctx", axis=0, tiled=True),
        lax.all_gather(cross_value, "ctx", axis=0, tiled=True),
        lax.all_gather(cross_proj, "ctx", axis=0, tiled=True),
        lax.all_gather(dec_norm3, "ctx", axis=0, tiled=True),
        lax.all_gather(dec_gate, "ctx", axis=0, tiled=True),
        lax.all_gather(dec_up, "ctx", axis=0, tiled=True),
        lax.all_gather(dec_down, "ctx", axis=0, tiled=True),
    )
    enc_norm1 = enc_norm1.astype(jnp.float32)
    enc_norm2 = enc_norm2.astype(jnp.float32)
    enc_final = enc_final.astype(jnp.float32)
    dec_norm1 = dec_norm1.astype(jnp.float32)
    dec_norm2 = dec_norm2.astype(jnp.float32)
    dec_norm3 = dec_norm3.astype(jnp.float32)
    heads_here = HEADS // lax.axis_size("sp")
    enc_table, enc_onehot = head_table(enc_rel, buckets[0], heads_here)
    dec_table, dec_onehot = head_table(dec_rel, buckets[1], heads_here)
    enc_x = enc_in.astype(jnp.float32)
    enc_mid, enc_saved_a = attention_layer(
        enc_x,
        None,
        enc_norm1,
        enc_query,
        enc_key,
        enc_value,
        enc_proj,
        enc_segments,
        enc_segments,
        enc_table,
        False,
    )
    enc_result, enc_saved_f = feed_layer(enc_mid, enc_norm2, enc_gate, enc_up, enc_down)
    memory = rms_norm(enc_result, enc_final).astype(jnp.bfloat16)
    dec_x = dec_in.astype(jnp.float32)
    dec_mid, dec_saved_a = attention_layer(
        dec_x,
        None,
        dec_norm1,
        dec_query,
        dec_key,
        dec_value,
        dec_proj,
        dec_segments,
        dec_segments,
        dec_table,
        True,
    )
    dec_cross, dec_saved_c = attention_layer(
        dec_mid,
        memory,
        dec_norm2,
        cross_query,
        cross_key,
        cross_value,
        cross_proj,
        dec_segments,
        enc_segments,
        None,
        False,
    )
    dec_result, dec_saved_f = feed_layer(dec_cross, dec_norm3, dec_gate, dec_up, dec_down)
    grad_dec, dec_ff_grads = feed_layer_back(
        dec_cot.astype(jnp.float32), dec_saved_f, dec_norm3, dec_gate, dec_up, dec_down
    )
    grad_dec, grad_memory, cross_grads = attention_layer_back(
        grad_dec, dec_saved_c, dec_norm2, cross_query, cross_key, cross_value, cross_proj, True
    )
    grad_dec, _, dec_self_grads = attention_layer_back(
        grad_dec, dec_saved_a, dec_norm1, dec_query, dec_key, dec_value, dec_proj, False
    )
    grad_enc_out, grad_final = norm_pullback(enc_result, enc_final, grad_memory)
    grad_enc, enc_ff_grads = feed_layer_back(
        enc_cot.astype(jnp.float32) + grad_enc_out,
        enc_saved_f,
        enc_norm2,
        enc_gate,
        enc_up,
        enc_down,
    )
    grad_enc, _, enc_self_grads = attention_layer_back(
        grad_enc, enc_saved_a, enc_norm1, enc_query, enc_key, enc_value, enc_proj, False
    )
    e_gain1, e_wq, e_wk, e_wv, e_wo, e_table = enc_self_grads
    e_gain2, e_wg, e_wu, e_wd = enc_ff_grads
    d_gain1, d_wq, d_wk, d_wv, d_wo, d_table = dec_self_grads
    c_gain, c_wq, c_wk, c_wv, c_wo, _ = cross_grads
    d_gain3, d_wg, d_wu, d_wd = dec_ff_grads
    e_rel = table_grad(e_table, enc_onehot, heads_here)
    d_rel = table_grad(d_table, dec_onehot, heads_here)
    shards = (
        lax.psum_scatter(e_gain1, "ctx", scatter_dimension=0, tiled=True),
        lax.psum_scatter(e_wq, "ctx", scatter_dimension=0, tiled=True),
        lax.psum_scatter(e_wk, "ctx", scatter_dimension=0, tiled=True),
        lax.psum_scatter(e_wv, "ctx", scatter_dimension=0, tiled=True),
        lax.psum_scatter(e_wo, "ctx", scatter_dimension=0, tiled=True),
        lax.psum_scatter(e_rel, "ctx", scatter_dimension=0, tiled=True),
        lax.psum_scatter(e_gain2, "ctx", scatter_dimension=0, tiled=True),
        lax.psum_scatter(e_wg, "ctx", scatter_dimension=0, tiled=True),
        lax.psum_scatter(e_wu, "ctx", scatter_dimension=0, tiled=True),
        lax.psum_scatter(e_wd, "ctx", scatter_dimension=0, tiled=True),
        lax.psum_scatter(grad_final, "ctx", scatter_dimension=0, tiled=True),
        lax.psum_scatter(d_gain1, "ctx", scatter_dimension=0, tiled=True),
        lax.psum_scatter(d_wq, "ctx", scatter_dimension=0, tiled=True),
        lax.psum_scatter(d_wk, "ctx", scatter_dimension=0, tiled=True),
        lax.psum_scatter(d_wv, "ctx", scatter_dimension=0, tiled=True),
        lax.psum_scatter(d_wo, "ctx", scatter_dimension=0, tiled=True),
        lax.psum_scatter(d_rel, "ctx", scatter_dimension=0, tiled=True),
        lax.psum_scatter(c_gain, "ctx", scatter_dimension=0, tiled=True),
        lax.psum_scatter(c_wq, "ctx", scatter_dimension=0, tiled=True),
        lax.psum_scatter(c_wk, "ctx", scatter_dimension=0, tiled=True),
        lax.psum_scatter(c_wv, "ctx", scatter_dimension=0, tiled=True),
        lax.psum_scatter(c_wo, "ctx", scatter_dimension=0, tiled=True),
        lax.psum_scatter(d_gain3, "ctx", scatter_dimension=0, tiled=True),
        lax.psum_scatter(d_wg, "ctx", scatter_dimension=0, tiled=True),
        lax.psum_scatter(d_wu, "ctx", scatter_dimension=0, tiled=True),
        lax.psum_scatter(d_wd, "ctx", scatter_dimension=0, tiled=True),
    )
    (
        s_gain1,
        s_wq,
        s_wk,
        s_wv,
        s_wo,
        s_rel,
        s_gain2,
        s_wg,
        s_wu,
        s_wd,
        s_final,
        t_gain1,
        t_wq,
        t_wk,
        t_wv,
        t_wo,
        t_rel,
        t_gain2,
        t_cq,
        t_ck,
        t_cv,
        t_co,
        t_gain3,
        t_wg,
        t_wu,
        t_wd,
    ) = shards
    reduced = (
        lax.psum(s_gain1.astype(jnp.bfloat16), "sp").astype(jnp.float32),
        lax.psum(s_wq.astype(jnp.bfloat16), "sp").astype(jnp.float32),
        lax.psum(s_wk.astype(jnp.bfloat16), "sp").astype(jnp.float32),
        lax.psum(s_wv.astype(jnp.bfloat16), "sp").astype(jnp.float32),
        lax.psum(s_wo.astype(jnp.bfloat16), "sp").astype(jnp.float32),
        lax.psum(s_rel.astype(jnp.bfloat16), "sp").astype(jnp.float32),
        lax.psum(s_gain2.astype(jnp.bfloat16), "sp").astype(jnp.float32),
        lax.psum(s_wg.astype(jnp.bfloat16), "sp").astype(jnp.float32),
        lax.psum(s_wu.astype(jnp.bfloat16), "sp").astype(jnp.float32),
        lax.psum(s_wd.astype(jnp.bfloat16), "sp").astype(jnp.float32),
        lax.psum(s_final.astype(jnp.bfloat16), "sp").astype(jnp.float32),
        lax.psum(t_gain1.astype(jnp.bfloat16), "sp").astype(jnp.float32),
        lax.psum(t_wq.astype(jnp.bfloat16), "sp").astype(jnp.float32),
        lax.psum(t_wk.astype(jnp.bfloat16), "sp").astype(jnp.float32),
        lax.psum(t_wv.astype(jnp.bfloat16), "sp").astype(jnp.float32),
        lax.psum(t_wo.astype(jnp.bfloat16), "sp").astype(jnp.float32),
        lax.psum(t_rel.astype(jnp.bfloat16), "sp").astype(jnp.float32),
        lax.psum(t_gain2.astype(jnp.bfloat16), "sp").astype(jnp.float32),
        lax.psum(t_cq.astype(jnp.bfloat16), "sp").astype(jnp.float32),
        lax.psum(t_ck.astype(jnp.bfloat16), "sp").astype(jnp.float32),
        lax.psum(t_cv.astype(jnp.bfloat16), "sp").astype(jnp.float32),
        lax.psum(t_co.astype(jnp.bfloat16), "sp").astype(jnp.float32),
        lax.psum(t_gain3.astype(jnp.bfloat16), "sp").astype(jnp.float32),
        lax.psum(t_wg.astype(jnp.bfloat16), "sp").astype(jnp.float32),
        lax.psum(t_wu.astype(jnp.bfloat16), "sp").astype(jnp.float32),
        lax.psum(t_wd.astype(jnp.bfloat16), "sp").astype(jnp.float32),
    )
    return (enc_result, dec_result, grad_enc, grad_dec) + tuple(reduced)


HG, CORE, SP = "hg", "core", "sp"
BLOCK_PAD = 128
VMEM_BYTES = 60 << 20


def nt(left, right):
    return lax.dot_general(left, right, (((1,), (1,)), ((), ())), preferred_element_type=jnp.float32)


def tn(left, right):
    return lax.dot_general(left, right, (((0,), (0,)), ((), ())), preferred_element_type=jnp.float32)


def nn(left, right):
    return jnp.dot(left, right, preferred_element_type=jnp.float32)


def low(value):
    return value.astype(jnp.bfloat16)


def identity(size):
    rows = lax.broadcasted_iota(jnp.int32, (size, size), 0)
    cols = lax.broadcasted_iota(jnp.int32, (size, size), 1)
    return low(jnp.where(rows == cols, 1.0, 0.0))


def only_lanes(array, first, count):
    lanes = lax.broadcasted_iota(jnp.int32, array.shape, 1)
    return jnp.where((lanes >= first) & (lanes < first + count), array, jnp.zeros_like(array))


def gelu_and_slope(v):
    scale, cubic = math.sqrt(2.0 / math.pi), 0.044715
    t = jnp.tanh(scale * (v + cubic * v * v * v))
    return 0.5 * v * (1.0 + t), 0.5 * (1.0 + t) + 0.5 * v * (1.0 - t * t) * scale * (1.0 + 3.0 * cubic * v * v)


def norm_back(x, g, dn):
    r = lax.rsqrt(jnp.mean(x * x, axis=-1, keepdims=True) + EPSILON)
    w = dn * g
    dx = r * w - x * (r * r * r) * jnp.mean(w * x, axis=-1, keepdims=True)
    return dx, jnp.sum(dn * x * r, axis=0, keepdims=True)


def send(src, dst, send_sem, recv_sem, to):
    copy = pltpu.make_async_remote_copy(
        src_ref=src, dst_ref=dst, send_sem=send_sem, recv_sem=recv_sem, device_id=to, device_id_type=pl.DeviceIdType.MESH
    )
    copy.start()
    return copy


def arrived(dst, send_sem, recv_sem, to):
    pltpu.make_async_remote_copy(
        src_ref=dst, dst_ref=dst, send_sem=send_sem, recv_sem=recv_sem, device_id=to, device_id_type=pl.DeviceIdType.MESH
    ).wait_recv()


class Place:
    def __init__(self, groups, cores, parts):
        self.groups, self.cores, self.parts = groups, cores, parts
        self.group, self.core, self.part = lax.axis_index(HG), lax.axis_index(CORE), lax.axis_index(SP)

    def ahead(self, step):
        return lax.rem(self.group + step, self.groups)

    def behind(self, step):
        return lax.rem(self.group + self.groups - step, self.groups)

    def chip(self, group):
        return (group, self.core, self.part)

    def sibling(self):
        return (self.group, 1 - self.core, self.part)

    def plane(self, step):
        return lax.rem(self.part + step, self.parts)

    def plane_behind(self, step):
        return lax.rem(self.part + self.parts - step, self.parts)

    def at_plane(self, part):
        return (self.group, self.core, part)

    def first_token(self, number, block):
        return pl.multiple_of(((self.cores * number + self.core) * self.parts + self.part) * block, block)

    def greet(self, planes=False):
        barrier = pltpu.get_barrier_semaphore()
        partners = [self.chip(self.ahead(step)) for step in range(1, self.groups)] + [self.sibling()]
        if planes:
            partners += [self.at_plane(self.plane(step)) for step in range(1, self.parts)]
        for partner in partners:
            pl.semaphore_signal(barrier, inc=1, device_id=partner, device_id_type=pl.DeviceIdType.MESH)
        pl.semaphore_wait(barrier, len(partners))


def spread_start(place, buf, sent, got):
    mine = buf.at[place.group]
    return [
        send(mine, mine, sent.at[step], got.at[step], place.chip(place.ahead(step))) for step in range(1, place.groups)
    ]


def spread_wait(place, buf, sent, got):
    for step in range(1, place.groups):
        source = place.behind(step)
        arrived(buf.at[source], sent.at[step], got.at[step], place.chip(source))


def collect_start(place, partial, out_buf, in_buf, sent, got):
    out_buf[...] = low(partial).reshape(out_buf.shape)
    pending = []
    for step in range(1, place.groups):
        to = place.ahead(step)
        pending.append(send(out_buf.at[to], in_buf.at[place.group], sent.at[step], got.at[step], place.chip(to)))
    return pending


def collect_wait(place, out_buf, in_buf, sent, got):
    total = out_buf[place.group].astype(jnp.float32)
    for step in range(1, place.groups):
        source = place.behind(step)
        arrived(in_buf.at[source], sent.at[step], got.at[step], place.chip(source))
        total = total + in_buf[source].astype(jnp.float32)
    return total


def all_rows(buf):
    return buf[...].reshape(buf.shape[0] * buf.shape[1], buf.shape[2])


DMA = pltpu.SemaphoreType.DMA
IN_VMEM = pl.BlockSpec(memory_space=pltpu.VMEM)
ANYWHERE = pl.BlockSpec(memory_space=pl.ANY)


class Recut:
    def __init__(self, sizes, col_shapes, row_shapes):
        groups, cores, _ = sizes
        self.cols, self.rows = len(col_shapes), len(row_shapes)
        self.outs = [((groups, cores) + s[1:], jnp.bfloat16) for s in col_shapes]
        self.outs += [((cores,) + s, jnp.bfloat16) for s in row_shapes]
        cols = (self.cols, groups)
        self.scratch = [DMA(cols)] * 4 + [DMA((self.rows,))] * 2 + [DMA((self.cols + self.rows,))]

    def bind(self, ins, outs, scratch):
        self.col_refs, self.row_refs = ins[: self.cols], ins[self.cols :]
        self.col_outs, self.row_outs = outs[: self.cols], outs[self.cols :]
        self.sems = scratch
        self.pending, self.copies = [], []

    def begin(self, place):
        sent, got, relay_sent, relay_got, pair_sent, pair_got, local = self.sems
        group, core = place.group, place.core
        for index, (ref, out) in enumerate(zip(self.col_refs, self.col_outs)):
            slot = out.at[group, core]
            for step in range(1, place.groups):
                to = place.ahead(step)
                self.pending.append(send(ref.at[to], slot, sent.at[index, step], got.at[index, step], place.chip(to)))
            self.pending.append(send(ref.at[group], slot, relay_sent.at[index, 0], relay_got.at[index, 0], place.sibling()))
            self.copies.append(pltpu.make_async_copy(ref.at[group], slot, local.at[index]))
        for index, (ref, out) in enumerate(zip(self.row_refs, self.row_outs)):
            slot = out.at[core]
            self.pending.append(send(ref, slot, pair_sent.at[index], pair_got.at[index], place.sibling()))
            self.copies.append(pltpu.make_async_copy(ref, slot, local.at[self.cols + index]))
        for copy in self.copies:
            copy.start()

    def middle(self, place):
        sent, got, relay_sent, relay_got = self.sems[:4]
        for index, out in enumerate(self.col_outs):
            for step in range(1, place.groups):
                source = place.behind(step)
                slot = out.at[source, place.core]
                arrived(slot, sent.at[index, step], got.at[index, step], place.chip(source))
                self.pending.append(
                    send(slot, slot, relay_sent.at[index, step], relay_got.at[index, step], place.sibling())
                )

    def end(self, place):
        _, _, relay_sent, relay_got, pair_sent, pair_got, _ = self.sems
        for index, out in enumerate(self.col_outs):
            for step in range(place.groups):
                slot = out.at[place.behind(step), 1 - place.core]
                arrived(slot, relay_sent.at[index, step], relay_got.at[index, step], place.sibling())
        for index, out in enumerate(self.row_outs):
            arrived(out.at[1 - place.core], pair_sent.at[index], pair_got.at[index], place.sibling())
        for copy in self.copies:
            copy.wait()
        for copy in self.pending:
            copy.wait_send()


class GiveRows:
    def __init__(self, sizes, cols, rows):
        self.cols, self.rows = len(cols), len(rows)
        own = [(s[0],) + s[2:] for s in cols] + [(1,) + s[1:] for s in rows]
        self.outs = [(shape, jnp.bfloat16) for shape in own]
        self.scratch = [pltpu.VMEM(shape, jnp.bfloat16) for shape in own + own[: self.cols]]
        self.scratch += [DMA((self.cols, sizes[0]))] * 4 + [DMA((max(1, self.rows),))] * 2

    def bind(self, ins, outs, scratch):
        self.col_refs, self.row_refs = ins[: self.cols], ins[self.cols :]
        self.col_outs, self.row_outs = outs[: self.cols], outs[self.cols :]
        self.col_sibs, scratch = scratch[: self.cols], scratch[self.cols :]
        self.row_sibs, scratch = scratch[: self.rows], scratch[self.rows :]
        self.col_sums, self.sems = scratch[: self.cols], scratch[self.cols :]
        self.pending = []

    def begin(self, place):
        _, _, pair_sent, pair_got, row_sent, row_got = self.sems
        other = 1 - place.core
        for index, (ref, sib) in enumerate(zip(self.col_refs, self.col_sibs)):
            for step in range(place.groups):
                to = place.ahead(step)
                self.pending.append(
                    send(
                        ref.at[to, other], sib.at[to],
                        pair_sent.at[index, step], pair_got.at[index, step], place.sibling(),
                    )
                )
        for index, (ref, sib) in enumerate(zip(self.row_refs, self.row_sibs)):
            self.pending.append(send(ref.at[other], sib.at[0], row_sent.at[index], row_got.at[index], place.sibling()))

    def middle(self, place):
        sent, got, pair_sent, pair_got, row_sent, row_got = self.sems
        core = place.core
        for index, (ref, sib) in enumerate(zip(self.col_refs, self.col_sibs)):
            out, sums = self.col_outs[index], self.col_sums[index]
            for step in list(range(1, place.groups)) + [0]:
                to = place.ahead(step)
                arrived(sib.at[to], pair_sent.at[index, step], pair_got.at[index, step], place.sibling())
                both = low(ref[to, core].astype(jnp.float32) + sib[to].astype(jnp.float32))
                if step:
                    sums[to] = both
                    self.pending.append(
                        send(sums.at[to], out.at[place.group], sent.at[index, step], got.at[index, step], place.chip(to))
                    )
                else:
                    out[place.group] = both
        for index, (ref, sib) in enumerate(zip(self.row_refs, self.row_sibs)):
            arrived(sib.at[0], row_sent.at[index], row_got.at[index], place.sibling())
            self.row_outs[index][0] = low(ref[core].astype(jnp.float32) + sib[0].astype(jnp.float32))

    def end(self, place):
        sent, got = self.sems[:2]
        for index, out in enumerate(self.col_outs):
            for step in range(1, place.groups):
                source = place.behind(step)
                arrived(out.at[source], sent.at[index, step], got.at[index, step], place.chip(source))
        for copy in self.pending:
            copy.wait_send()


FOLD_PIECE = 56 * 1024


class FoldPlanes:
    def __init__(self, arrays, in_place=False):
        self.in_place = in_place
        self.operands = list(arrays)
        self.in_specs = [IN_VMEM] * len(arrays)
        self.outs = [(w.shape, jnp.bfloat16) for w in arrays]
        self.out_specs = [IN_VMEM] * len(arrays)
        self.pieces = []
        for index, w in enumerate(arrays):
            cuts = next(c for c in (1, 2, 3, 4, 6, 8) if w.shape[1] // c * w.shape[2] <= FOLD_PIECE or c == 8)
            if w.shape[0] * w.shape[1] * w.shape[2] <= FOLD_PIECE:
                self.pieces.append((index, slice(None), pl.ds(0, w.shape[1])))
                continue
            rows = w.shape[1] // cuts
            self.pieces += [(index, lead, pl.ds(c * rows, rows)) for lead in range(w.shape[0]) for c in range(cuts)]
        self.inner_done = self.across_done = 0
        self.scratch = [pltpu.VMEM(w.shape, jnp.bfloat16) for _ in range(1 if in_place else 2) for w in arrays] + [DMA((len(self.pieces),))] * 6

    def bind(self, ins, outs, scratch):
        count = len(self.outs)
        self.ins, self.totals = ins, outs
        self.inner = outs
        self.across, scratch = scratch[:count], scratch[count:]
        self.sums, self.sems = (ins, scratch) if self.in_place else (scratch[:count], scratch[count:])

    def copy(self, hop, number, src, dst, to):
        return pltpu.make_async_remote_copy(
            src_ref=src, dst_ref=dst, send_sem=self.sems[2 * hop].at[number], recv_sem=self.sems[2 * hop + 1].at[number],
            device_id=to, device_id_type=pl.DeviceIdType.MESH,
        )

    def hops(self, place, number):
        index, lead, rows = self.pieces[number]
        part = place.part
        inward, across, outward = (place.at_plane(p) for p in (1 + part // 3, 3 - part, 3 * (part - 1)))
        ref, inner, sums, other, total = (
            side[index].at[lead, rows] for side in (self.ins, self.inner, self.sums, self.across, self.totals)
        )
        return (ref, inner, inward), (sums, other, across), (total, total, outward)

    def roles(self, place):
        middle = (place.part == 1) | (place.part == 2)
        return pl.when(middle), pl.when(jnp.logical_not(middle))

    def start(self, place, numbers):
        @self.roles(place)[1]
        def _():
            for number in numbers:
                self.copy(0, number, *self.hops(place, number)[0]).start()

    def add_inner(self, place, number):
        inward, across, _ = self.hops(place, number)
        self.copy(0, number, *inward).wait_recv()
        across[0][...] = low(inward[0][...].astype(jnp.float32) + inward[1][...].astype(jnp.float32))
        self.copy(1, number, *across).start()

    def add_across(self, place, number):
        _, across, outward = self.hops(place, number)
        self.copy(1, number, *across).wait_recv()
        outward[0][...] = low(across[0][...].astype(jnp.float32) + across[1][...].astype(jnp.float32))
        self.copy(2, number, *outward).start()

    def of(self, first, last):
        return [n for n, piece in enumerate(self.pieces) if first <= piece[0] < last]

    def serve(self, place, inner, across):
        inners = list(range(self.inner_done, min(self.inner_done + inner, len(self.pieces))))
        self.inner_done += len(inners)
        others = list(range(self.across_done, min(self.across_done + across, len(self.pieces))))
        self.across_done += len(others)

        @self.roles(place)[0]
        def _():
            for turn in range(max(len(inners), len(others))):
                if turn < len(inners):
                    self.add_inner(place, inners[turn])
                if turn < len(others):
                    self.add_across(place, others[turn])

    def finish(self, place, lag):
        left = len(self.pieces) - self.inner_done
        behind = self.inner_done - self.across_done
        if behind > lag:
            self.serve(place, 0, behind - lag)
        self.serve(place, lag - min(behind, lag), 0)
        self.serve(place, left, left)
        self.serve(place, 0, len(self.pieces))

    def end(self, place):
        in_middle, at_end = self.roles(place)

        @at_end
        def _():
            for number in range(len(self.pieces)):
                inward, _, outward = self.hops(place, number)
                self.copy(0, number, *inward).wait_send()
                self.copy(2, number, *outward).wait_recv()

        @in_middle
        def _():
            for number in range(len(self.pieces)):
                _, across, outward = self.hops(place, number)
                self.copy(1, number, *across).wait_send()
                self.copy(2, number, *outward).wait_send()


def feed_back_part(n, dyb, gu_ref, down_ref):
    hidden = down_ref.shape[0]
    gu = nn(n, gu_ref[...])
    g, u = gu[:, :hidden], gu[:, hidden:]
    act, slope = gelu_and_slope(g)
    dh = nt(dyb, down_ref[...])
    return low(act * u), jnp.concatenate([low(dh * u * slope), low(dh * act)], axis=1)


def row_block(row):
    wide = jnp.broadcast_to(row.astype(jnp.float32), (8, row.shape[1]))
    return low(jnp.where(lax.broadcasted_iota(jnp.int32, wide.shape, 0) == 0, wide, 0.0))


def bucket_onehot(row, width, count, place_of):
    last = row.shape[1] - 1
    padded = jnp.concatenate([row.astype(jnp.float32), jnp.zeros((1, width - last - 1), jnp.float32)], axis=1)
    entry = lax.broadcasted_iota(jnp.int32, (width, width), 0)
    column = lax.broadcasted_iota(jnp.int32, (width, width), 1)
    pick = low(jnp.where(entry == jnp.clip(place_of(column), 0, last), 1.0, 0.0))
    bucket = nn(row_block(padded), pick)[0:1, :].astype(jnp.int32)
    return jnp.where(lax.broadcasted_iota(jnp.int32, (count, width), 0) == bucket, 1.0, 0.0)


def bias_mask(place, block, causal, rel_ref, turn, key_ids, query_ids, out_ref):
    heads, rows_total, lanes = out_ref.shape
    key_len = key_ids.shape[1]
    strip = block + 2 * BLOCK_PAD
    query = lax.broadcasted_iota(jnp.int32, (1, lanes), 1)
    start = ((place.cores * (query // block) + place.core) * place.parts + place.part) * block
    token = lax.broadcasted_iota(jnp.int32, (key_len, lanes), 0)
    of_key = tn(row_block(key_ids[...]), jnp.ones((8, lanes), jnp.bfloat16))
    of_query = nn(row_block(query_ids[...]), low(jnp.where(token == start + query % block, 1.0, 0.0)))[0:1, :]
    allowed = of_key == of_query
    if causal:
        allowed = allowed & (token <= start + query % block)
    inside = pl.ds(BLOCK_PAD, key_len)
    if rel_ref is None:
        out_ref[0, inside, :] = low(jnp.where(allowed, 0.0, NEGATIVE))
        return
    by_head = tn(rel_ref[...], turn)
    width = by_head.shape[1]
    pick_rows = lax.broadcasted_iota(jnp.int32, (8, by_head.shape[0]), 0)
    pick_cols = lax.broadcasted_iota(jnp.int32, (8, by_head.shape[0]), 1)
    picked = nn(low(jnp.where(pick_cols == pick_rows + place.group * heads, 1.0, 0.0)), low(by_head))
    places = lax.broadcasted_iota(jnp.int32, (rows_total, lanes), 0)
    for head in range(heads):
        row = picked[head : head + 1, :]
        left, right = row[:, width - 2 : width - 1], row[:, 0:1]
        out_ref[head] = low(jnp.where(places < start, left, right))
        wide = jnp.broadcast_to(row, (strip, width))
        for number in range(lanes // block):
            at = (number * block) % 128
            turned = pltpu.roll(wide, (width - (strip - 1) + at) % width, 1, stride=1, stride_axis=0)
            rows = pl.ds(place.first_token(number, block), strip)
            out_ref[head, rows, number * block : (number + 1) * block] = low(turned[:, at : at + block])
        out_ref[head, inside, :] = low(jnp.where(allowed, out_ref[head, inside, :].astype(jnp.float32), NEGATIVE))


def chunk_rows(kv_ref):
    return kv_ref.shape[1] * kv_ref.shape[2] * kv_ref.shape[3]


def key_side(kv_ref, chunk):
    return kv_ref[chunk].reshape(chunk_rows(kv_ref), kv_ref.shape[4])[:, : kv_ref.shape[4] // 2]


def value_side(kv_ref, chunk):
    lanes = kv_ref.shape[4]
    return kv_ref[chunk].reshape(chunk_rows(kv_ref), lanes)[:, lanes // 2 // 128 * 128 :]


def bias_rows(bm_ref, head, chunk, rows):
    at = pl.multiple_of(BLOCK_PAD + chunk * rows, 128)
    return bm_ref[head if bm_ref.shape[0] > 1 else 0, pl.ds(at, rows), :].astype(jnp.float32)


def mix_part(q, kv_ref, bm_ref, o_ref, lse_ref, s_ref, ot_ref):
    chunks, rows = kv_ref.shape[0], chunk_rows(kv_ref)
    queries, width = q.shape
    heads = width // HD
    across = [slice(head * queries, (head + 1) * queries) for head in range(heads)]
    masked_q = [only_lanes(q, head * HD, HD) for head in range(heads)]

    def first(chunk, tops):
        keys = key_side(kv_ref, chunk)
        inside = pl.ds(pl.multiple_of(chunk * rows, rows), rows)
        new = []
        for head in range(heads):
            scores = nt(keys, masked_q[head]) + bias_rows(bm_ref, head, chunk, rows)
            s_ref[inside, across[head]] = scores
            new.append(jnp.maximum(tops[head], jnp.max(scores, axis=0, keepdims=True)))
        return tuple(new)

    tops = lax.fori_loop(0, chunks, first, (jnp.full((1, queries), NEGATIVE, jnp.float32),) * heads)

    def second(chunk, carried):
        values = value_side(kv_ref, chunk)
        inside = pl.ds(pl.multiple_of(chunk * rows, rows), rows)
        lead = values.shape[1] - width
        values_t = low(nt(identity(values.shape[1]), values))
        new = []
        for head in range(heads):
            total, mixed = carried[head]
            weights = jnp.exp(s_ref[inside, across[head]] - tops[head])
            mixed = mixed + nn(values_t[lead + head * HD : lead + (head + 1) * HD], low(weights))
            new.append((total + jnp.sum(weights, axis=0, keepdims=True), mixed))
        return tuple(new)

    start = (jnp.zeros((1, queries), jnp.float32), jnp.zeros((HD, queries), jnp.float32))
    done = lax.fori_loop(0, chunks, second, (start,) * heads)
    for head in range(heads):
        total, mixed = done[head]
        lse_ref[:, across[head]] = tops[head] + jnp.log(total)
        ot_ref[head * HD : (head + 1) * HD, :] = low(mixed / total)
    o_ref[...] = low(nt(identity(queries), ot_ref[...]))


def keys_send(place, kv_ref, base, sent, got):
    mine = kv_ref.at[:, place.core, place.part]
    pending = [
        send(mine, mine, sent.at[base, step], got.at[base, step], place.at_plane(place.plane(step)))
        for step in range(1, place.parts)
    ]
    pending.append(send(mine, mine, sent.at[base + 1, 0], got.at[base + 1, 0], place.sibling()))
    return pending


def keys_relay(place, kv_ref, base, sent, got):
    pending = []
    for step in range(1, place.parts):
        source = place.plane_behind(step)
        slot = kv_ref.at[:, place.core, source]
        arrived(slot, sent.at[base, step], got.at[base, step], place.at_plane(source))
        pending.append(send(slot, slot, sent.at[base + 1, step], got.at[base + 1, step], place.sibling()))
    return pending


def keys_wait(place, kv_ref, base, sent, got):
    for step in range(place.parts):
        slot = kv_ref.at[:, 1 - place.core, place.plane_behind(step)]
        arrived(slot, sent.at[base + 1, step], got.at[base + 1, step], place.sibling())


def mix_back_part(place, q, do, o, kv_ref, lse_ref, bm_ref, dkv_ref, ds_ref):
    chunks, cores, parts, block, lanes = kv_ref.shape
    rows = chunk_rows(kv_ref)
    queries, width = q.shape
    heads = width // HD
    strip = block + 2 * BLOCK_PAD
    first_value = width // 128 * 128
    lead = width - first_value
    do_wide = jnp.concatenate([jnp.zeros((queries, lead), do.dtype), do], axis=1) if lead else do
    across = [slice(head * queries, (head + 1) * queries) for head in range(heads)]
    masked_q = [only_lanes(q, head * HD, HD) for head in range(heads)]
    masked_do = [only_lanes(do_wide, lead + head * HD, HD) for head in range(heads)]
    q_wide = masked_q
    if lead:
        none = jnp.zeros((queries, lead), q.dtype)
        q_wide = [jnp.concatenate([one, none], axis=1) for one in masked_q]
    of_head = lax.broadcasted_iota(jnp.int32, (8, width), 1) // HD
    of_row = lax.broadcasted_iota(jnp.int32, (8, width), 0)
    inners = lax.dot_general(
        jnp.where(of_head == of_row, 1.0, 0.0), do.astype(jnp.float32) * o.astype(jnp.float32),
        (((1,), (1,)), ((), ())), precision=HIGHEST, preferred_element_type=jnp.float32,
    )
    nothing = jnp.zeros((1, queries), jnp.float32)
    if ds_ref is not None:
        empty = jnp.zeros((BLOCK_PAD, heads * queries), jnp.bfloat16)
        ds_ref[0:BLOCK_PAD, :] = empty
        ds_ref[BLOCK_PAD + chunks * rows :, :] = empty
        of_lane = lax.broadcasted_iota(jnp.int32, (1, queries), 1) // block
        lane_start = ((cores * of_lane + place.core) * parts + place.part) * block

    def chunk_step(chunk, carried):
        at = pl.multiple_of(chunk * rows, rows)
        keys, values = key_side(kv_ref, chunk), value_side(kv_ref, chunk)
        keys_t = low(nt(identity(width), keys))
        new, dk, dv = [], None, None
        for head in range(heads):
            left, right, back = carried[head]
            scores = nt(keys, masked_q[head]) + bias_rows(bm_ref, head, chunk, rows)
            p = jnp.exp(scores - lse_ref[:, across[head]])
            dp = nt(values, masked_do[head])
            ds = low(p * (dp - inners[head : head + 1, :]))
            if ds_ref is not None:
                ds_ref[pl.ds(pl.multiple_of(BLOCK_PAD + at, 128), rows), across[head]] = ds
                wide = ds.astype(jnp.float32)
                places = lax.broadcasted_iota(jnp.int32, wide.shape, 0) + (at + BLOCK_PAD)
                left = left + jnp.sum(jnp.where(places < lane_start, wide, 0.0), axis=0, keepdims=True)
                right = right + jnp.sum(jnp.where(places >= lane_start + strip, wide, 0.0), axis=0, keepdims=True)
            back = back + nn(keys_t[head * HD : (head + 1) * HD], ds)
            new.append((left, right, back))
            more_k, more_v = nn(ds, q_wide[head]), nn(low(p), masked_do[head])
            dk, dv = (more_k, more_v) if dk is None else (dk + more_k, dv + more_v)
        if lead:
            shared = dk[:, first_value:] + dv[:, : 2 * lead]
            both = jnp.concatenate([dk[:, :first_value], shared, dv[:, 2 * lead :]], axis=1)
        else:
            both = jnp.concatenate([dk, dv], axis=1)
        dkv_ref[chunk] = low(both).reshape(dkv_ref.shape[1:])
        return tuple(new)

    start = (nothing, nothing, jnp.zeros((HD, queries), jnp.float32))
    done = lax.fori_loop(0, chunks, chunk_step, (start,) * heads)
    return [one[2] for one in done], [one[:2] for one in done]


def table_grads(place, block, done, ds_ref, ahead_ref, rel_ref):
    queries = done[0][0].shape[1]
    width = ahead_ref.shape[1]
    strip = block + 2 * BLOCK_PAD
    rows = lax.broadcasted_iota(jnp.int32, (block, block), 0)
    cols = lax.broadcasted_iota(jnp.int32, (block, block), 1)
    backwards = jnp.where(rows + cols == block - 1, 1.0, 0.0)
    at = lax.broadcasted_iota(jnp.int32, (1, width), 1)
    sums = []
    for head, (left, right) in enumerate(done):
        total = jnp.zeros((strip, block), jnp.float32)
        for number in range(queries // block):
            low_at = head * queries + number * block
            near = pl.ds(place.first_token(number, block), strip)
            total = total + ds_ref[near, low_at : low_at + block].astype(jnp.float32)
        turned = lax.dot_general(
            backwards, total, (((1,), (1,)), ((), ())), precision=HIGHEST, preferred_element_type=jnp.float32
        )
        turned = jnp.concatenate([turned, jnp.zeros((block, width - strip), jnp.float32)], axis=1)
        by_distance = jnp.sum(pltpu.roll(turned, 0, 1, stride=1, stride_axis=0), axis=0, keepdims=True)
        left, right = (jnp.sum(side, axis=1, keepdims=True) for side in (left, right))
        sums.append(by_distance + jnp.where(at == 0, left, 0.0) + jnp.where(at == width - 2, right, 0.0))
    sums = jnp.concatenate(sums + [jnp.zeros((8 - len(sums), width), jnp.float32)], axis=0)
    by_bucket = lax.dot_general(
        sums, ahead_ref[...], (((1,), (1,)), ((), ())), precision=HIGHEST, preferred_element_type=jnp.float32
    )
    head_rows = lax.broadcasted_iota(jnp.int32, (8, 128), 0)
    head_lanes = lax.broadcasted_iota(jnp.int32, (8, 128), 1)
    lanes_of = (head_lanes == head_rows + place.group * len(done)) & (head_rows < len(done))
    rel_ref[...] = lax.dot_general(
        by_bucket, jnp.where(lanes_of, 1.0, 0.0), (((0,), (0,)), ((), ())), precision=HIGHEST, preferred_element_type=jnp.float32
    )


class AttendBack:
    OPERANDS = 10

    def __init__(self, place, ins, grads, dkv, scratch, cross, which=None):
        self.place, self.cross = place, cross
        self.x, self.n, self.q, self.kv, self.o, self.lse, self.w, self.wo, self.bm, other = ins
        self.source, self.ahead = (other, None) if cross else (self.n, other.at[which])
        self.dwkv, self.dwq, self.dwo = grads
        self.dkv, self.sib, self.zout, self.zin, self.d_buf, self.pn, self.rn, self.dq = [dkv] + scratch[:7]
        scratch = scratch[7:]
        self.pm, self.rm = (scratch.pop(0), scratch.pop(0)) if cross else (None, None)
        self.ds = None if cross else scratch.pop(0)
        self.sent, self.got = scratch
        self.kv_width = self.kv.shape[4]
        self.pending = []

    def begin(self, dy):
        self.d_buf[self.place.group] = low(dy)
        self.pending += spread_start(self.place, self.d_buf, self.sent.at[0], self.got.at[0])

    def arrive(self):
        spread_wait(self.place, self.d_buf, self.sent.at[0], self.got.at[0])

    def compute(self):
        place, sent, got = self.place, self.sent, self.got
        do = low(nt(all_rows(self.d_buf), self.wo[...]))
        back, self.edges = mix_back_part(
            place, self.q[...], do, self.o[...], self.kv, self.lse, self.bm, self.dkv, self.ds
        )
        self.halves = send(self.dkv.at[:, 1 - place.core], self.sib, sent.at[1, 0], got.at[1, 0], place.sibling())
        self.dq[...] = low(nt(identity(self.q.shape[0]), low(jnp.concatenate(back, axis=0))))
        if self.cross:
            share = nt(self.dq[...], self.w[:, self.kv_width :])
            self.pending += collect_start(place, share, self.pn, self.rn, sent.at[3], got.at[3])

    def exchange(self):
        place, sent, got = self.place, self.sent, self.got
        arrived(self.sib, sent.at[1, 0], got.at[1, 0], place.sibling())
        for step in list(range(1, place.parts)) + [0]:
            to = place.plane(step)
            self.zout[to] = low(self.dkv[:, place.core, to].astype(jnp.float32) + self.sib[:, to].astype(jnp.float32))
            if step:
                self.pending.append(
                    send(self.zout.at[to], self.zin.at[place.part], sent.at[2, step], got.at[2, step], place.at_plane(to))
                )

        self.halves.wait_send()

    def by_rows(self, grad):
        return low(grad).reshape(self.dwq.shape[:3] + grad.shape[1:])

    def query_grads(self, rel):
        self.dwo[...] = low(tn(self.o[...], all_rows(self.d_buf))).reshape(self.dwo.shape)
        self.dwq[...] = self.by_rows(tn(self.n[...], self.dq[...]))
        if not self.cross:
            table_grads(self.place, self.x.shape[0], self.edges, self.ds, self.ahead, rel)

    def keys(self):
        place, sent, got = self.place, self.sent, self.got
        total = self.zout[place.part].astype(jnp.float32)
        for step in range(1, place.parts):
            source = place.plane_behind(step)
            arrived(self.zin.at[source], sent.at[2, step], got.at[2, step], place.at_plane(source))
            total = total + self.zin[source].astype(jnp.float32)
        self.dkv_own = low(total).reshape(self.q.shape[0], self.kv_width)
        share = nt(self.dkv_own, self.w[:, : self.kv_width])
        if self.cross:
            self.pending += collect_start(place, share, self.pm, self.rm, sent.at[4], got.at[4])
        else:
            share = share + nt(self.dq[...], self.w[:, self.kv_width :])
            self.pending += collect_start(place, share, self.pn, self.rn, sent.at[3], got.at[3])

    def key_grads(self):
        self.dwkv[...] = self.by_rows(tn(self.source[...], self.dkv_own))

    def source_grad(self):
        return collect_wait(self.place, self.pm, self.rm, self.sent.at[4], self.got.at[4])

    def normed_grad(self):
        return collect_wait(self.place, self.pn, self.rn, self.sent.at[3], self.got.at[3])

    def wait(self):
        for copy in self.pending:
            copy.wait_send()


def attend_back_scratch(sizes, block, model, width, cross):
    groups, cores, parts = sizes
    tokens = groups * block
    turned, buffer = (parts, groups, block, 2 * width), (groups, block, model)
    shapes = [(groups, parts, block, 2 * width), turned, turned, buffer, buffer, buffer, (tokens, width)]
    if cross:
        shapes += [buffer, buffer]
    else:
        shapes.append((cores * parts * tokens + 2 * BLOCK_PAD, width // HD * tokens))
    return [pltpu.VMEM(shape, jnp.bfloat16) for shape in shapes] + [DMA((5, max(groups, parts)))] * 2


class Taker:
    def __init__(self, refs):
        self.refs = list(refs)

    def __call__(self, count):
        taken, self.refs = self.refs[:count], self.refs[count:]
        return taken


def decoder_back_kernel(sizes, streams, gain_at, plans, *refs):
    give_a, give_b, give_c, fold, cross_scratch, self_scratch = plans
    dec1, dec2, dec3, enc2, final = gain_at
    take = Taker(refs)
    gains, cx, dec_cot, dec_gu, dec_down = take(5)
    cross_ins, self_ins = take(AttendBack.OPERANDS), take(AttendBack.OPERANDS)
    ex, enc_out, enc_cot, en2, gu, down = take(6)
    dec_out, dec_in_grad, grad_ex, dg_d1, dg_d2, dg_d3, dg_e2, dg_ef, rel_d, dw_d, dwo_d = take(11)
    totals, c_outs = take(len(fold.outs)), take(len(give_c.outs))
    dw_c, dwo_c, dgu, ddown, dgu_a, ddown_a, dkv, grad_cx, grad_dx = take(9)
    n_buf, d_buf, py, ry, f_buf, pf, rf, f_sent, f_got = take(9)
    place = Place(*sizes)
    kv_width = cross_ins[3].shape[4]
    cross = AttendBack(place, cross_ins, (dw_c.at[:, :, :, :kv_width], dw_c.at[:, :, :, kv_width:], dwo_c), dkv, take(len(cross_scratch)), True)
    own = AttendBack(place, self_ins, (dw_d.at[:, :, :, :kv_width], dw_d.at[:, :, :, kv_width:], dwo_d), dkv, take(len(self_scratch)), False, 1)
    a_outs, b_outs = take(len(give_a.outs)), take(len(give_b.outs))
    give_a.bind([dgu_a, ddown_a], a_outs, take(len(give_a.scratch)))
    fold.bind(a_outs + b_outs, totals, take(len(fold.scratch)))
    of_a, of_b = fold.of(0, len(a_outs)), fold.of(len(a_outs), len(fold.outs))
    give_b.bind([dw_c, dwo_c], b_outs, take(len(give_b.scratch)))
    give_c.bind([dgu, ddown], c_outs, take(len(give_c.scratch)))
    pn, rn = own.pn, own.rn
    place.greet(planes=True)
    d_buf[place.group] = dec_cot[...]
    pending = spread_start(place, d_buf, f_sent.at[2], f_got.at[2])
    n_buf[place.group] = low(rms_norm(cx[...], gains[dec3]))
    pending += spread_start(place, n_buf, f_sent.at[3], f_got.at[3])
    spread_wait(place, d_buf, f_sent.at[2], f_got.at[2])
    spread_wait(place, n_buf, f_sent.at[3], f_got.at[3])
    n, dyb = all_rows(n_buf), all_rows(d_buf)
    h, dgu_value = feed_back_part(n, dyb, dec_gu, dec_down)
    leaving = collect_start(place, nt(dgu_value, dec_gu[...]), pn, rn, f_sent.at[4], f_got.at[4])
    dgu_a[...] = low(tn(n, dgu_value)).reshape(dgu_a.shape)
    ddown_a[...] = low(tn(h, dyb)).reshape(ddown_a.shape)
    dn = collect_wait(place, pn, rn, f_sent.at[4], f_got.at[4])
    for copy in leaving:
        copy.wait_send()
    back, dg = norm_back(cx[...], gains[dec3], dn)
    dg_d3[...] = dg
    grad_cx[...] = dec_cot[...].astype(jnp.float32) + back
    cross.begin(grad_cx[...])
    pending += collect_start(place, nn(h, dec_down[...]), py, ry, f_sent.at[5], f_got.at[5])
    give_a.begin(place)
    give_a.middle(place)
    streams.need(5, 15)
    cross.arrive()
    cross.compute()
    give_a.end(place)
    cross.exchange()
    fold.start(place, of_a)
    back, dg = norm_back(cross.x[...].astype(jnp.float32), gains[dec2], cross.normed_grad())
    dg_d2[...] = dg
    grad_dx[...] = grad_cx[...] + back
    own.begin(grad_dx[...])
    streams.need(15, 25)
    dec_out[...] = cx[...] + collect_wait(place, py, ry, f_sent.at[5], f_got.at[5])
    own.arrive()
    own.compute()
    fold.serve(place, 2, 0)
    cross.keys()
    own.exchange()
    fold.serve(place, 2, 1)
    cross.query_grads(None)
    cross.key_grads()
    give_b.begin(place)
    streams.need(25, 31)
    back, dg = norm_back(enc_out[...], gains[final], cross.source_grad())
    dg_ef[...] = dg
    dy = enc_cot[...].astype(jnp.float32) + back
    f_buf[place.group] = low(dy)
    pending += spread_start(place, f_buf, f_sent.at[0], f_got.at[0])
    give_b.middle(place)
    own.query_grads(rel_d)
    fold.serve(place, 3, 2)
    spread_wait(place, f_buf, f_sent.at[0], f_got.at[0])
    n, dyb = en2[...], all_rows(f_buf)
    h, dgu_value = feed_back_part(n, dyb, gu, down)
    pending += collect_start(place, nt(dgu_value, gu[...]), pf, rf, f_sent.at[1], f_got.at[1])
    dgu[...] = low(tn(n, dgu_value)).reshape(dgu.shape)
    ddown[...] = low(tn(h, dyb)).reshape(ddown.shape)
    give_b.end(place)
    fold.start(place, of_b)
    give_c.begin(place)
    fold.serve(place, 3, 3)
    dn = collect_wait(place, pf, rf, f_sent.at[1], f_got.at[1])
    back, dg = norm_back(ex[...], gains[enc2], dn)
    dg_e2[...] = dg
    grad_ex[...] = dy + back
    give_c.middle(place)
    fold.serve(place, 4, 3)
    own.keys()
    own.key_grads()
    fold.finish(place, 3)
    back, dg = norm_back(own.x[...].astype(jnp.float32), gains[dec1], own.normed_grad())
    dg_d1[...] = dg
    dec_in_grad[...] = grad_dx[...] + back
    give_c.end(place)
    fold.end(place)
    cross.wait()
    own.wait()
    for copy in pending:
        copy.wait_send()


def encoder_back_kernel(sizes, streams, gain_at, plans, *refs):
    give_d, give_q, give_e, fold, before, scratch = plans
    take = Taker(refs)
    gains, grad_ex = take(2)
    ins = take(AttendBack.OPERANDS)
    dg_d1, dg_d2, dg_d3, dg_e2, dg_ef, rel_d = take(6)
    ready, d_ins = take(before), take(give_d.cols + give_d.rows)
    (enc_in_grad,) = take(1)
    totals = take(len(fold.outs))
    dwkv_e, dwq_e, dwo_e, small, dkv, rel_e = take(6)
    place = Place(*sizes)
    own = AttendBack(place, ins, (dwkv_e, dwq_e, dwo_e), dkv, take(len(scratch)), False, 0)
    d_outs, q_outs, e_outs = take(len(give_d.outs)), take(len(give_q.outs)), take(len(give_e.outs))
    give_d.bind(d_ins, d_outs, take(len(give_d.scratch)))
    give_q.bind([dwq_e, dwo_e], q_outs, take(len(give_q.scratch)))
    give_e.bind([dwkv_e, small], e_outs, take(len(give_e.scratch)))
    fold.bind(ready + d_outs + q_outs + e_outs, totals, take(len(fold.scratch)))
    of_c = fold.of(0, before)
    of_d, of_q, of_e = (
        fold.of(first, last) for first, last in ((before, before + 2), (before + 2, before + 4), (before + 4, len(fold.outs)))
    )
    place.greet(planes=True)
    own.begin(grad_ex[...])
    fold.start(place, of_c)
    give_d.begin(place)
    give_d.middle(place)
    streams.need(2, 12)
    own.arrive()
    fold.serve(place, 2, 0)
    own.compute()
    fold.serve(place, 3, 2)
    own.exchange()
    give_d.end(place)
    fold.start(place, of_d)
    fold.serve(place, 2, 2)
    own.query_grads(rel_e)
    give_q.begin(place)
    fold.serve(place, 2, 2)
    own.keys()
    give_q.middle(place)
    fold.serve(place, len(of_c) - 9, 3)
    own.key_grads()
    dn = own.normed_grad()
    give_q.end(place)
    fold.start(place, of_q)
    back, dg_e1 = norm_back(own.x[...].astype(jnp.float32), gains[gain_at], dn)
    enc_in_grad[...] = grad_ex[...] + back
    devices = place.groups * place.cores
    share = dg_e1.shape[1] // devices
    small[...] = jnp.zeros_like(small)
    all_gains = jnp.concatenate([dg_e1, dg_e2[...], dg_ef[...], dg_d1[...], dg_d2[...], dg_d3[...]], axis=0)
    count = all_gains.shape[0]
    each = rel_e.shape[0] // devices
    tables = [rel_e[...].reshape(devices, each, 128), rel_d[...].reshape(devices, each, 128)]
    for device in range(devices):
        piece = jnp.concatenate([all_gains[:, device * share : (device + 1) * share], jnp.zeros((count, 128 - share), jnp.float32)], axis=1)
        rows = jnp.concatenate([piece, tables[0][device], tables[1][device]], axis=0)
        rows = jnp.concatenate([rows, jnp.zeros((16 - rows.shape[0], 128), jnp.float32)], axis=0)
        small[device // place.cores, device % place.cores] = low(rows)
    give_e.begin(place)
    fold.serve(place, 2, len(of_c) - 9)
    give_e.middle(place)
    fold.serve(place, len(of_d) - 2, 2)
    give_e.end(place)
    fold.start(place, of_e)
    fold.finish(place, 3)
    fold.end(place)
    own.wait()


class Streams:
    def __init__(self, fetches, stores):
        self.fetches, self.stores = fetches, stores
        self.stored = []

    def begin(self):
        for copy in self.fetches.values():
            copy.start()

    def need(self, first, last):
        for index in [i for i in self.fetches if first <= i < last]:
            self.fetches.pop(index).wait()

    def store(self, *indices):
        for index in indices:
            if index in self.stores:
                copy = self.stores.pop(index)
                copy.start()
                self.stored.append(copy)

    def end(self):
        self.need(0, 1 << 20)
        self.store(*sorted(self.stores))
        for copy in self.stored:
            copy.wait()


LARGE = 300_000


def size_of(shape, dtype):
    return math.prod(shape) * jnp.dtype(dtype).itemsize


def fused(sizes, collective_id, kernel, operands, outs, scratch, fetched=(0, 0), stored=False, large=LARGE):
    late = [i for i, w in enumerate(operands) if fetched[0] <= i < fetched[1] and size_of(w.shape, w.dtype) > large]
    early = [i for i, (shape, dtype) in enumerate(outs) if stored and size_of(shape, dtype) > large]
    held = [pltpu.VMEM(operands[i].shape, operands[i].dtype) for i in late]
    held += [pltpu.VMEM(*outs[i]) for i in early]
    sems = [DMA((max(1, len(late)),)), DMA((max(1, len(early)),))]

    def body(*refs):
        take = Taker(refs)
        ins, results, own = take(len(operands)), take(len(outs)), take(len(scratch))
        late_refs, early_refs = take(len(late)), take(len(early))
        late_sem, early_sem = take(2)
        fetches, stores = {}, {}
        for number, index in enumerate(late):
            fetches[index] = pltpu.make_async_copy(ins[index], late_refs[number], late_sem.at[number])
            ins[index] = late_refs[number]
        for number, index in enumerate(early):
            stores[index] = pltpu.make_async_copy(early_refs[number], results[index], early_sem.at[number])
            results[index] = early_refs[number]
        streams = Streams(fetches, stores)
        streams.begin()
        kernel(sizes, streams, *ins, *results, *own)
        streams.end()

    return pl.pallas_call(
        body,
        out_shape=tuple(jax.ShapeDtypeStruct(shape, dtype) for shape, dtype in outs),
        in_specs=[ANYWHERE if i in late else IN_VMEM for i in range(len(operands))],
        out_specs=tuple(ANYWHERE if i in early else IN_VMEM for i in range(len(outs))),
        scratch_shapes=list(scratch) + held + sems,
        compiler_params=pltpu.CompilerParams(
            collective_id=collective_id, has_side_effects=collective_id is not None, vmem_limit_bytes=VMEM_BYTES
        ),
        cost_estimate=pl.CostEstimate(flops=20_000_000_000, bytes_accessed=10_000_000, transcendentals=0),
    )(*operands)


def kept_operands(x, kept, w, wo, ahead):
    _, n, q, kv, o, lse, bm, memory = kept
    return [x, n, q, kv, o, lse, w, wo, bm, memory if ahead is None else ahead]


def buffers_of(shapes):
    return [pltpu.VMEM(shape, jnp.bfloat16) for shape in shapes]


def decoder_back(sizes, collective_id, gains, gain_at, last, cross, own, feed):
    groups, cores, parts = sizes
    f32, bf16 = jnp.float32, jnp.bfloat16
    block, model = last[0].shape
    share = model // (groups * cores)
    width = cross[3].shape[0]
    kv = cross[1][3].shape
    hidden = feed[5].shape[0]
    attention = [(groups, cores, share, 3 * width)], [(cores, width // cores, model)]
    feeds = [(groups, cores, share, 2 * hidden)], [(cores, hidden // cores, model)]
    give_a, give_b, give_c = GiveRows(sizes, *feeds), GiveRows(sizes, *attention), GiveRows(sizes, *feeds)
    fold = FoldPlanes([jax.ShapeDtypeStruct(shape, dtype) for shape, dtype in give_a.outs + give_b.outs], True)
    cross_scratch = attend_back_scratch(sizes, block, model, width, True)
    self_scratch = attend_back_scratch(sizes, block, model, width, False)
    plans = (give_a, give_b, give_c, fold, cross_scratch, self_scratch)
    operands = [gains, *last] + kept_operands(*cross) + kept_operands(*own) + list(feed)
    token, gain = ((block, model), f32), ((1, model), f32)
    outs = [token, token, token, gain, gain, gain, gain, gain, ((own[4].shape[1], 128), f32)]
    outs += [(attention[0][0], bf16), (attention[1][0], bf16)] + fold.outs + give_c.outs
    buffer = (groups, block, model)
    scratch = buffers_of(attention[0] + attention[1] + (feeds[0] + feeds[1]) * 2 + [kv]) + [pltpu.VMEM((block, model), f32)] * 2
    scratch += buffers_of([buffer] * 7) + [DMA((6, groups))] * 2 + cross_scratch + self_scratch
    scratch += buffers_of([shape for shape, _ in give_a.outs + give_b.outs])
    scratch += give_a.scratch + fold.scratch + give_b.scratch + give_c.scratch
    got = Taker(fused(sizes, collective_id, lambda s, t, *refs: decoder_back_kernel(s, t, gain_at, plans, *refs), operands, outs, scratch, (5, 31)))
    first = got(9)
    return first, got(2), got(len(give_a.outs)), got(len(give_b.outs)), got(len(give_c.outs))


def encoder_back(sizes, collective_id, gains, gain_at, grad_ex, own, small_grads, ready, grads_d):
    groups, cores, parts = sizes
    f32 = jnp.float32
    block, model = grad_ex.shape
    share = model // (groups * cores)
    width = own[3].shape[0]
    kv = own[1][3].shape
    give_d = GiveRows.__new__(GiveRows)
    give_d = GiveRows(sizes, [grads_d[0].shape], [grads_d[1].shape])
    keys, queries = (groups, cores, share, 2 * width), (groups, cores, share, width)
    table, projection = (groups, cores, 16, 128), (cores, width // cores, model)
    give_q, give_e = GiveRows(sizes, [queries], [projection]), GiveRows(sizes, [keys, table], [])
    all_outs = [jax.ShapeDtypeStruct(shape, dtype) for shape, dtype in give_d.outs + give_q.outs + give_e.outs]
    fold = FoldPlanes(list(ready) + all_outs)
    scratch = attend_back_scratch(sizes, block, model, width, False)
    plans = (give_d, give_q, give_e, fold, len(ready), scratch)
    operands = [gains, grad_ex] + kept_operands(*own) + list(small_grads) + list(ready) + list(grads_d)
    buffers = buffers_of([keys, queries, projection, table, kv]) + [pltpu.VMEM((own[4].shape[1], 128), f32)] + scratch
    buffers += buffers_of([shape for shape, _ in give_d.outs + give_q.outs + give_e.outs])
    buffers += give_d.scratch + give_q.scratch + give_e.scratch + fold.scratch
    outs = [((block, model), f32)] + fold.outs
    got = Taker(fused(sizes, collective_id, lambda s, t, *refs: encoder_back_kernel(s, t, gain_at, plans, *refs), operands, outs, buffers, (2, 12)))
    return got(1)[0], got(len(ready)), got(2), got(4)


def unpack_kernel(sizes, streams, kinds, *refs):
    take = Taker(refs)
    ins, at = take(len(kinds)), 0
    for index, (ref, pieces) in enumerate(zip(ins, kinds)):
        streams.need(index, index + 1)
        results = take(max(1, pieces))
        if pieces < 0:
            results[0][...] = ref[...]
        elif pieces == 0:
            results[0][...] = ref[0].astype(jnp.float32)
        else:
            value = ref[...].astype(jnp.float32)
            each = value.shape[2] // pieces
            for piece, out in enumerate(results):
                out[...] = jnp.concatenate([one[:, piece * each : (piece + 1) * each] for one in value], axis=1)
        streams.store(*range(at, at + len(results)))
        at += len(results)


def unpack(sizes, arrays, kinds):
    outs = []
    for array, pieces in zip(arrays, kinds):
        if pieces < 0:
            outs.append((array.shape, array.dtype))
        elif pieces == 0:
            outs.append((array.shape[1:], jnp.float32))
        for _ in range(pieces):
            outs.append(((array.shape[1], array.shape[0] * array.shape[2] // pieces), jnp.float32))
    return fused(
        sizes, None, lambda s, t, *refs: unpack_kernel(s, t, kinds, *refs), arrays, outs, [], (0, len(arrays)), True, 1
    )


class AttendForward:
    def __init__(self, place, outs, bufs, sems, base):
        self.place, self.base = place, base
        self.x, self.n, self.q, self.kv, self.o, self.lse, self.bm = outs
        self.p_buf, self.r_buf = bufs
        self.sent, self.got = sems

    def keys(self, kv):
        kv_ref = self.kv
        kv_ref[:, self.place.core, self.place.part] = kv.reshape(kv_ref.shape[0], kv_ref.shape[3], kv_ref.shape[4])

    def send(self):
        return keys_send(self.place, self.kv, self.base, self.sent, self.got)

    def gather(self):
        pending = keys_relay(self.place, self.kv, self.base, self.sent, self.got)
        keys_wait(self.place, self.kv, self.base, self.sent, self.got)
        return pending

    def mix(self, wo, s_ref, ot_ref):
        place, base = self.place, self.base
        mix_part(self.q[...], self.kv, self.bm, self.o, self.lse, s_ref, ot_ref)
        share = nn(self.o[...], wo)
        return collect_start(place, share, self.p_buf, self.r_buf, self.sent.at[base + 2], self.got.at[base + 2])

    def add(self, x):
        total = collect_wait(self.place, self.p_buf, self.r_buf, self.sent.at[self.base + 2], self.got.at[self.base + 2])
        self.x[...] = x + total


def pack_columns(pack, refs):
    groups = pack.shape[0]
    for group in range(groups):
        parts = [ref[:, group * (ref.shape[1] // groups) : (group + 1) * (ref.shape[1] // groups)] for ref in refs]
        pack[group] = jnp.concatenate([part.astype(jnp.float32) for part in parts], axis=1).astype(pack.dtype)


def flat(ref):
    rows = math.prod(ref.shape[:-1])
    return ref[...].reshape(rows, ref.shape[-1])


def forward_kernel(sizes, streams, counts, recuts, *refs):
    enc_first, dec_first, later, last = recuts
    gain_count, each = counts
    take = Taker(refs)
    enc_in, dec_in, small, enc_ids, dec_ids, buckets = take(6)
    enc_w, dec_w, cross_w, enc_gate_up, dec_gate_up = take(3), take(3), take(3), take(2), take(2)
    enc_wo_own, dec_wo_own, cross_wo_own, enc_wd_own, dec_wd_own = take(5)
    gains, enc_kvq, dec_kvq, enc_gu, cross_kvq, dec_gu, enc_wo, dec_wo, enc_wd, cross_wo, dec_wd = take(11)
    enc_outs, dec_outs, cross_outs = take(7), take(7), take(7)
    memory_all, enc_out, en2, ahead = take(4)
    small_pack, enc_pack, dec_pack, cross_pack, enc_gu_pack, dec_gu_pack, small_all, rels = take(8)
    s_ref, ot_ref = take(2)
    x_e, x_d, n_buf, d_buf, m_buf, f_p, f_r = take(7)
    bufs = [take(2) for _ in range(3)]
    sent, got = take(2)
    enc_first.bind([small_pack, enc_pack, enc_wo_own], [small_all, enc_kvq, enc_wo], take(len(enc_first.scratch)))
    dec_first.bind([dec_pack, dec_wo_own], [dec_kvq, dec_wo], take(len(dec_first.scratch)))
    later.bind(
        [enc_gu_pack, cross_pack, enc_wd_own, cross_wo_own], [enc_gu, cross_kvq, enc_wd, cross_wo], take(len(later.scratch))
    )
    last.bind([dec_gu_pack, dec_wd_own], [dec_gu, dec_wd], take(len(last.scratch)))
    place = Place(*sizes)
    enc, dec, cross = [
        AttendForward(place, outs, bufs[i], (sent, got), 6 + 3 * i) for i, outs in enumerate((enc_outs, dec_outs, cross_outs))
    ]
    for group in range(place.groups):
        small_pack[group] = small[...]
    pack_columns(enc_pack, enc_w)
    place.greet(planes=True)
    x_e[place.group] = enc_in[...]
    x_d[place.group] = dec_in[...]
    enc_first.begin(place)
    pending = spread_start(place, x_e, sent.at[0], got.at[0])
    pack_columns(dec_pack, dec_w)
    dec_first.begin(place)
    pending += spread_start(place, x_d, sent.at[1], got.at[1])
    pack_columns(enc_gu_pack, enc_gate_up)
    pack_columns(cross_pack, cross_w)
    pack_columns(dec_gu_pack, dec_gate_up)
    enc_first.middle(place)
    enc_first.end(place)

    devices = place.groups * place.cores
    share = enc_in.shape[1] // devices
    rows, model = small.shape[0], enc_in.shape[1]
    lane = lax.broadcasted_iota(jnp.int32, (128, model), 0)
    column = lax.broadcasted_iota(jnp.int32, (128, model), 1)
    bucket = lax.broadcasted_iota(jnp.int32, (devices * each, rows), 0)
    row = lax.broadcasted_iota(jnp.int32, (devices * each, rows), 1)
    every_gain, tables = 0.0, [0.0, 0.0]
    for device in range(devices):
        table = small_all[device // place.cores, device % place.cores]
        to_column = (column == lane + device * share) & (lane < share)
        every_gain = every_gain + nn(table, low(jnp.where(to_column, 1.0, 0.0)))
        for index in range(2):
            from_row = row == bucket - device * each + gain_count + index * each
            from_row = from_row & (bucket // each == device)
            tables[index] = tables[index] + nn(low(jnp.where(from_row, 1.0, 0.0)), table)
    for index in range(gain_count):
        gains[index] = every_gain[index : index + 1, :]
    for index in range(2):
        rels[index] = low(tables[index])

    def project(one, x_buf, gain_at, w, number):
        spread_wait(place, x_buf, sent.at[number], got.at[number])
        kv_width = one.kv.shape[4]
        n = low(rms_norm(all_rows(x_buf).astype(jnp.float32), gains[gain_at]))
        one.n[...] = n
        both = low(nn(n, flat(w)))
        one.keys(both[:, :kv_width])
        one.q[...] = both[:, kv_width:]

    project(enc, x_e, 0, enc_kvq, 0)
    pending += enc.send()
    dec_first.middle(place)
    dec_first.end(place)
    project(dec, x_d, 3, dec_kvq, 1)
    later.begin(place)
    block = enc_in.shape[0]
    reach, width = buckets.shape[1] // 2, ahead.shape[2]
    turns = []
    for index in range(2):
        row, count = buckets[index : index + 1, :], ahead.shape[1]
        ahead[index] = bucket_onehot(row, width, count, lambda column: column - (block - 1))
        turns.append(low(bucket_onehot(row, width, count, lambda column: 2 * reach + block - 1 - column)))
    bias_mask(place, block, False, rels.at[0], turns[0], enc_ids, enc_ids, enc.bm)
    streams.store(1, 2, 12, 19, 17)
    bias_mask(place, block, True, rels.at[1], turns[1], dec_ids, dec_ids, dec.bm)
    streams.store(24)
    pending += enc.gather()
    pending += dec.send()
    pending += enc.mix(flat(enc_wo), s_ref, ot_ref)
    streams.store(14)
    bias_mask(place, block, False, None, None, enc_ids, dec_ids, cross.bm)
    streams.store(31)
    enc.add(enc_in[...].astype(jnp.float32))
    ex = enc.x[...]
    n_buf[place.group] = low(rms_norm(ex, gains[1]))
    pending += spread_start(place, n_buf, sent.at[2], got.at[2])
    later.middle(place)
    later.end(place)
    streams.store(3, 4, 8)
    spread_wait(place, n_buf, sent.at[2], got.at[2])
    en2[...] = all_rows(n_buf)
    w_down = flat(enc_wd)
    hidden = w_down.shape[0]
    gu = nn(en2[...], flat(enc_gu))
    h = low(gelu_and_slope(gu[:, :hidden])[0] * gu[:, hidden:])
    pending += collect_start(place, nn(h, w_down), f_p, f_r, sent.at[5], got.at[5])
    enc_out[...] = ex + collect_wait(place, f_p, f_r, sent.at[5], got.at[5])
    m_buf[place.group] = low(rms_norm(enc_out[...], gains[2]))
    pending += spread_start(place, m_buf, sent.at[4], got.at[4])
    kv_width = cross.kv.shape[4]
    model = enc_in.shape[1]
    spread_wait(place, m_buf, sent.at[4], got.at[4])
    memory_all[...] = all_rows(m_buf)
    cross.keys(low(nn(memory_all[...], cross_kvq[:, :, :, :kv_width].reshape(model, kv_width))))
    pending += cross.send()
    pending += dec.gather()
    pending += dec.mix(flat(dec_wo), s_ref, ot_ref)
    streams.store(21)
    dec.add(dec_in[...].astype(jnp.float32))
    d_buf[place.group] = low(rms_norm(dec.x[...], gains[4]))
    pending += spread_start(place, d_buf, sent.at[3], got.at[3])
    last.begin(place)
    spread_wait(place, d_buf, sent.at[3], got.at[3])
    cross.n[...] = all_rows(d_buf)
    cross.q[...] = low(nn(cross.n[...], cross_kvq[:, :, :, kv_width:].reshape(model, kv_width // 2)))
    pending += cross.gather()
    pending += cross.mix(flat(cross_wo), s_ref, ot_ref)
    streams.store(28, 26, 32, 34)
    last.middle(place)
    cross.add(dec.x[...])
    last.end(place)
    for copy in pending:
        copy.wait_send()


def forward(sizes, collective_id, enc_in, dec_in, small, counts, ids, buckets, weights):
    groups, cores, parts = sizes
    f32, bf16 = jnp.float32, jnp.bfloat16
    block, model = enc_in.shape
    attention, feeds, rows = weights[:3], weights[3:5], weights[5]
    share = attention[0][0].shape[0]
    width = rows[0].shape[0] * cores
    tokens = groups * block
    keys = cores * parts * tokens
    heads = width // HD
    kvq, gu = (groups, share, 3 * width), (groups, share, 2 * feeds[0][0].shape[1] // groups)
    wo, wd = rows[0].shape, rows[3].shape
    small_shape = (groups,) + small.shape
    recuts = (
        Recut(sizes, [small_shape, kvq], [wo]), Recut(sizes, [kvq], [wo]), Recut(sizes, [gu, kvq], [wd, wo]), Recut(sizes, [gu], [wd])
    )

    def both(shape):
        return ((groups, cores) + shape[1:], bf16)

    def pair(shape):
        return ((cores,) + shape, bf16)

    token = ((block, model), f32)
    outs = [((counts[0], 1, model), f32), both(kvq), both(kvq), both(gu), both(kvq), both(gu)]
    outs += [pair(wo), pair(wo), pair(wd), pair(wo), pair(wd)]
    for number in range(3):
        outs += [
            token, ((tokens, model), bf16), ((tokens, width), bf16), ((groups, cores, parts, block, 2 * width), bf16),
            ((tokens, width), bf16), ((1, heads * tokens), f32),
            ((1 if number == 2 else heads, keys + 2 * BLOCK_PAD, tokens), bf16),
        ]
    bucket_count = groups * cores * counts[1]
    outs += [((tokens, model), bf16), token, ((tokens, model), bf16), ((2, bucket_count, buckets.shape[1] - 1 + 2 * block), f32)]
    buffer = (groups, block, model)
    scratch = buffers_of([small_shape, kvq, kvq, kvq, gu, gu, both(small_shape)[0], (2, bucket_count, 128)])
    scratch += [pltpu.VMEM((keys, heads * tokens), f32)] + buffers_of([(width, tokens)] + [buffer] * 13)
    scratch += [DMA((15, max(groups, parts)))] * 2 + [s for one in recuts for s in one.scratch]
    operands = [enc_in, dec_in, small, *ids, buckets] + [w for each in attention for w in each]
    operands += [w for each in feeds for w in each] + list(rows)
    got = Taker(
        fused(sizes, collective_id, lambda s, t, *refs: forward_kernel(s, t, counts, recuts, *refs), operands, outs, scratch, stored=True)
    )
    gains = got(1)[0]
    flat_weights = [w.reshape(-1, w.shape[-1]) for w in got(10)]
    enc_kept, dec_kept, cross_kept = got(7), got(7), got(7)
    memory_all, enc_out, en2, ahead = got(4)
    return gains, flat_weights, (*enc_kept, None), (*dec_kept, None), (*cross_kept, memory_all), enc_out, en2, ahead


def fast_device(
    enc_in, dec_in, enc_cot, dec_cot, enc_segments, dec_segments, buckets,
    enc_norm1, enc_query, enc_key, enc_value, enc_proj, enc_rel, enc_norm2, enc_gate, enc_up, enc_down, enc_final,
    dec_norm1, dec_query, dec_key, dec_value, dec_proj, dec_rel, dec_norm2, cross_query, cross_key, cross_value, cross_proj,
    dec_norm3, dec_gate, dec_up, dec_down,
):
    groups, cores, parts = sizes = lax.axis_size(HG), lax.axis_size(CORE), lax.axis_size(SP)
    block, model = enc_in.shape
    devices = groups * cores
    share = model // devices
    bf16, f32 = jnp.bfloat16, jnp.float32

    rel_len = enc_rel.shape[0]
    all_gains = jnp.stack([enc_norm1, enc_norm2, enc_final, dec_norm1, dec_norm2, dec_norm3])
    all_rels = jnp.concatenate([enc_rel, dec_rel]).reshape(-1, HEADS)
    small = jnp.concatenate([jnp.pad(w, ((0, 0), (0, 128 - w.shape[1]))) for w in (all_gains, all_rels)])
    each = all_rels.shape[0] // 2
    small = jnp.pad(small, ((0, 16 - small.shape[0]), (0, 0)))

    gains, weights, enc_kept, dec_kept, cross_kept, enc_out, en2, ahead = forward(
        sizes, 1, enc_in, dec_in, small, (6, each), (enc_segments[None, :], dec_segments[None, :]), buckets,
        (
            (enc_key, enc_value, enc_query), (dec_key, dec_value, dec_query), (cross_key, cross_value, cross_query),
            (enc_gate, enc_up), (dec_gate, dec_up), (enc_proj, dec_proj, cross_proj, enc_down, dec_down),
        ),
    )
    enc_kvq, dec_kvq, enc_gu, cross_kvq, dec_gu, enc_wo, dec_wo, enc_wd, cross_wo, dec_wd = weights
    ex, dx, cx = enc_kept[0], dec_kept[0], cross_kept[0]

    (dec_out, dec_in_grad, grad_ex, dg_d1, dg_d2, dg_d3, dg_e2, dg_ef, rel_d), grads_d, sum_a, sum_b, rows_c = decoder_back(
        sizes, 2, gains, (3, 4, 5, 1, 2), (cx, dec_cot, dec_gu, dec_wd),
        (dx, cross_kept, cross_kvq, cross_wo, None), (dec_in, dec_kept, dec_kvq, dec_wo, ahead),
        (ex, enc_out, enc_cot, en2, enc_gu, enc_wd),
    )
    enc_in_grad, sum_c, sum_d, sum_e = encoder_back(
        sizes, 3, gains, 0, grad_ex, (enc_in, enc_kept, enc_kvq, enc_wo, ahead),
        (dg_d1, dg_d2, dg_d3, dg_e2, dg_ef, rel_d), rows_c, grads_d,
    )

    dgu_rows, d_wd = sum_a
    cross_rows, c_wo = sum_b
    egu_rows, e_wd = sum_c
    dkvq_rows, d_wo = sum_d
    eq_rows, e_wo, ekv_rows, small_rows = sum_e
    (
        enc_out, dec_out, enc_in_grad, dec_in_grad, e_wk, e_wv, e_wq, e_wg, e_wu, d_wk, d_wv, d_wq, c_wk, c_wv, c_wq, d_wg, d_wu, d_wd, c_wo, e_wd, d_wo, e_wo
    ) = unpack(
        sizes,
        [enc_out, dec_out, enc_in_grad, dec_in_grad, ekv_rows, eq_rows, egu_rows, dkvq_rows, cross_rows, dgu_rows, d_wd, c_wo, e_wd, d_wo, e_wo],
        (-1, -1, -1, -1, 2, 1, 2, 3, 3, 2, 0, 0, 0, 0, 0),
    )
    own = jnp.sum(small_rows.astype(f32), axis=0)
    s = [own[i, :share] for i in range(6)]
    e_rel, d_rel = [own[6 + i * each : 6 + (i + 1) * each, :HEADS].reshape(rel_len) for i in range(2)]
    return (
        enc_out, dec_out, enc_in_grad, dec_in_grad,
        s[0], e_wq, e_wk, e_wv, e_wo, e_rel, s[1], e_wg, e_wu, e_wd, s[2],
        s[3], d_wq, d_wk, d_wv, d_wo, d_rel, s[4], c_wq, c_wk, c_wv, c_wo, s[5], d_wg, d_wu, d_wd,
    )


def general_plan(mesh):
    placed = (
        P(("ctx", "sp"), None),
        P(("ctx", "sp"), None),
        P(("ctx", "sp"), None),
        P(("ctx", "sp"), None),
        P(),
        P(),
        P(),
        P("ctx"),
        P("ctx", None),
        P("ctx", None),
        P("ctx", None),
        P("ctx", None),
        P("ctx"),
        P("ctx"),
        P("ctx", None),
        P("ctx", None),
        P("ctx", None),
        P("ctx"),
        P("ctx"),
        P("ctx", None),
        P("ctx", None),
        P("ctx", None),
        P("ctx", None),
        P("ctx"),
        P("ctx"),
        P("ctx", None),
        P("ctx", None),
        P("ctx", None),
        P("ctx", None),
        P("ctx"),
        P("ctx", None),
        P("ctx", None),
        P("ctx", None),
    )
    return jax.shard_map(
        per_device,
        mesh=mesh,
        in_specs=placed,
        out_specs=(
            P(("ctx", "sp"), None),
            P(("ctx", "sp"), None),
            P(("ctx", "sp"), None),
            P(("ctx", "sp"), None),
            P("ctx"),
            P("ctx", None),
            P("ctx", None),
            P("ctx", None),
            P("ctx", None),
            P("ctx"),
            P("ctx"),
            P("ctx", None),
            P("ctx", None),
            P("ctx", None),
            P("ctx"),
            P("ctx"),
            P("ctx", None),
            P("ctx", None),
            P("ctx", None),
            P("ctx", None),
            P("ctx"),
            P("ctx"),
            P("ctx", None),
            P("ctx", None),
            P("ctx", None),
            P("ctx", None),
            P("ctx"),
            P("ctx", None),
            P("ctx", None),
            P("ctx", None),
        ),
        check_vma=False,
    )


def split_plan(mesh, groups):
    cut = Mesh(np.asarray(mesh.devices).reshape(groups, 2, mesh.shape["sp"]), (HG, CORE, SP))
    tokens, rows, gain, same = P((HG, CORE, SP), None), P((HG, CORE), None), P((HG, CORE)), P()
    attention = (gain, rows, rows, rows, rows, gain)
    feed = (gain, rows, rows, rows)
    weights = attention + feed + (gain,) + attention + (gain, rows, rows, rows, rows) + feed
    return jax.shard_map(
        fast_device,
        mesh=cut,
        in_specs=(tokens,) * 4 + (same,) * 3 + weights,
        out_specs=(tokens,) * 4 + weights,
        check_vma=False,
    )


def solution(mesh):
    groups, odd = divmod(mesh.shape["ctx"], 2)
    if odd or HEADS % groups or mesh.shape["sp"] != 4:
        return general_plan(mesh)
    return split_plan(mesh, groups)
```
